32 devices in a mesh: seq: 4 (over x, core), fsdp: 8 (over z, y).
Axes of the slice: x: 2, y: 2, z: 4, core: 2. Of those that a mesh axis runs over, the one named last changes fastest.
Arguments:
- tokens: bfloat16 [8, 2048, 1024], P('fsdp', 'seq'), may hold values from -6 to 6
- lengths: int32 [8], P('fsdp'), may hold values from 512 to 2048, as said below
- state_init: bfloat16 [8, 512, 1024], P('fsdp', None, 'seq'), may hold values from -6 to 6
- w_qkv: bfloat16 [1024, 3072], P('fsdp'), may hold values from -0.1875 to 0.1875
- w_out: bfloat16 [1024, 1024], P('fsdp'), may hold values from -1 to 1
- w_up: bfloat16 [1024, 4096], P('fsdp'), may hold values from -0.1875 to 0.1875
- w_down: bfloat16 [4096, 1024], P('fsdp'), may hold values from -0.09375 to 0.09375
- norm_attn: bfloat16 [1024], P('fsdp'), may hold values from 0.099609375 to 1.8984375
- norm_mlp: bfloat16 [1024], P('fsdp'), may hold values from 0.099609375 to 1.8984375
- rel_bias: float32 [8, 32], P('seq'), may hold values from -4 to 4
- state_query: bfloat16 [8, 128, 128], P('seq'), may hold values from -0.5 to 0.5
- gate_bias: float32 [8, 128], P('seq'), may hold values from -1 to 4
- out_grad: bfloat16 [8, 2048, 1024], P('fsdp', 'seq'), may hold values from -6 to 6
- state_grad: bfloat16 [8, 512, 1024], P('fsdp', None, 'seq'), may hold values from -6 to 6
Outputs:
- output: bfloat16 [8, 2048, 1024], P('fsdp', 'seq')
- final_state: float32 [8, 512, 1024], P('fsdp', None, 'seq')
- tokens_grad: float32 [8, 2048, 1024], P('fsdp', 'seq')
- w_qkv_grad: float32 [1024, 3072], P(('seq', 'fsdp'))
- w_out_grad: float32 [1024, 1024], P(('seq', 'fsdp'))
- w_up_grad: float32 [1024, 4096], P(('seq', 'fsdp'))
- w_down_grad: float32 [4096, 1024], P(('seq', 'fsdp'))
- norm_attn_grad: float32 [1024], P(('seq', 'fsdp'))
- norm_mlp_grad: float32 [1024], P(('seq', 'fsdp'))
- rel_bias_grad: float32 [8, 32], P('seq')
- state_query_grad: float32 [8, 128, 128], P('seq')
- gate_bias_grad: float32 [8, 128], P('seq')
The draws below stay inside these ranges and needn't reach their ends.
Inputs may be any that keep to these rules, and one draw needn't show every extreme that they name: `lengths`: used positions of each slot; some slot is full, with 2048.
All inputs are finite; a program needn't handle non-finite values.
Results may differ from the reference program's by a relative error of at most 0.018.
Values may be sent and summed in bfloat16 or wider, within the bound.
A program may use at most 256 MiB of HBM per device.

```python
import jax
import jax.numpy as jnp
from jax import lax

D = 1024
H = 8
DH = 128
FF = 4096
WINDOW_LENGTH = 512
STATE_VECTORS = 512
SLOT = 2048
SLOTS = 8


def draw_lengths(key, part):
    key_lengths, key_full = jax.random.split(key)
    drawn_lengths = jax.random.randint(key_lengths, (SLOTS,), SLOT // 4, SLOT + 1, dtype=jnp.int32)
    full_slot = jax.random.randint(key_full, (), 0, SLOTS, dtype=jnp.int32)
    return jnp.where(jnp.arange(SLOTS, dtype=jnp.int32) == full_slot, SLOT, drawn_lengths).astype(jnp.int32)


def levels(own_key, dims, shards, smallest, top_value):
    level, own = 1.0, jax.random.fold_in(own_key, 6)
    for axis_at, shards_of in shards:
        heights = jnp.exp(jax.random.uniform(jax.random.fold_in(own, axis_at), (shards_of,), jnp.float32, smallest / len(shards), top_value / len(shards)))
        level = level * jnp.repeat(heights, dims[axis_at] // shards_of).reshape([-1 if axis == axis_at else 1 for axis in range(len(dims))])
    return level


def scatter_about(own_key, extent, deviation, reach, cuts=(), kind=jnp.bfloat16):
    loudness = levels(own_key, extent, cuts, -0.22, 0.18) if cuts else 1.0
    result = jax.random.normal(own_key, extent, jnp.float32) * deviation * loudness
    return jnp.minimum(jnp.maximum(result, -reach), reach).astype(kind)


def setup_inputs(seed: int = 0) -> dict:
    keys = jax.random.split(jax.random.key(seed), 15)
    tokens = scatter_about(keys[0], (SLOTS, SLOT, D), 1.0, 6.0, ((0, 8), (1, 4)))
    lengths = draw_lengths(jax.random.fold_in(keys[14], 71), 0)
    state_init = scatter_about(keys[2], (SLOTS, STATE_VECTORS, D), 1.0, 6.0, ((0, 8), (2, 4)))
    w_qkv = scatter_about(keys[3], (D, 3 * D), D ** -0.5, 0.1875, ((0, 8),))
    w_out = scatter_about(keys[4], (D, D), (D // 32) ** -0.5, 1.0, ((0, 8),))
    w_up = scatter_about(keys[5], (D, FF), D ** -0.5, 0.1875, ((0, 8),))
    w_down = scatter_about(keys[6], (FF, D), FF ** -0.5, 0.09375, ((0, 8),))
    norm_attn = jnp.clip(1.0 + 0.18 * jax.random.normal(keys[7], (D,), jnp.float32), 0.099609375, 1.8984375).astype(jnp.bfloat16)
    norm_mlp = jnp.clip(1.0 + 0.18 * jax.random.normal(keys[8], (D,), jnp.float32), 0.099609375, 1.8984375).astype(jnp.bfloat16)
    rel_bias = scatter_about(keys[9], (H, 32), 1.0, 4.0, ((0, 4),), jnp.float32)
    state_query = scatter_about(keys[10], (H, DH, DH), DH ** -0.5, 0.5, ((0, 4),))
    gate_bias = jnp.clip(-1.0 + 5.0 * jax.random.uniform(keys[11], (H, DH), jnp.float32) ** levels(keys[11], (H, DH), ((0, 4),), -0.2, 0.2), -1.0, 4.0)
    out_grad = scatter_about(keys[12], (SLOTS, SLOT, D), 1.0, 6.0, ((0, 8), (1, 4)))
    state_grad = scatter_about(keys[13], (SLOTS, STATE_VECTORS, D), 1.0, 6.0, ((0, 8), (2, 4)))
    return {"tokens": tokens, "lengths": lengths, "state_init": state_init, "w_qkv": w_qkv, "w_out": w_out, "w_up": w_up, "w_down": w_down, "norm_attn": norm_attn, "norm_mlp": norm_mlp, "rel_bias": rel_bias, "state_query": state_query, "gate_bias": gate_bias, "out_grad": out_grad, "state_grad": state_grad}


EPSILON = 1e-06
BUCKET_EDGES = (19, 21, 24, 27, 31, 35, 40, 46, 52, 59, 67, 77, 87, 99, 113)

@jax.custom_vjp
def lowered_input(v):
    return lax.optimization_barrier(v.astype(jnp.bfloat16)).astype(jnp.float32)

@jax.custom_vjp
def lowered_backward(v):
    return v

def low_keep(v):
    return (lowered_input(v), None)

def low_pass(kept, grad):
    return (grad,)

def back_keep(v):
    return (v, None)

def back_low(kept, grad):
    return (lowered_input(grad),)
lowered_input.defvjp(low_keep, low_pass)
lowered_backward.defvjp(back_keep, back_low)

def matmul(left, right):
    return jnp.dot(left, right, precision=lax.Precision.HIGHEST, preferred_element_type=jnp.float32)

def contract_product(form, left, right):
    return jnp.einsum(form, left, right, precision=lax.Precision.HIGHEST)

def rms_norm(values, gain):
    return values * lax.rsqrt(lax.optimization_barrier(jnp.mean(values * values, axis=-1, keepdims=True)) + EPSILON) * gain

def softmax_rows(scores):
    row_max = lax.optimization_barrier(jnp.max(scores, axis=-1, keepdims=True))
    expanded = jnp.exp(scores - row_max)
    return expanded / lax.optimization_barrier(jnp.sum(expanded, axis=-1, keepdims=True))

def smooth_gate(values):
    return jax.nn.gelu(values, approximate=False)

def bucket_table():
    row_index = jnp.arange(WINDOW_LENGTH, dtype=jnp.int32)[:, None]
    col_index = jnp.arange(2 * WINDOW_LENGTH, dtype=jnp.int32)[None, :]
    distance = row_index + WINDOW_LENGTH - col_index
    clipped = jnp.clip(distance, 0, WINDOW_LENGTH)
    bucket_edges = jnp.array(BUCKET_EDGES, dtype=jnp.int32)
    bucket = jnp.minimum(clipped, 16) + lax.optimization_barrier(jnp.sum((clipped[:, :, None] >= bucket_edges).astype(jnp.int32), axis=-1))
    window = (distance >= 0) & (distance < WINDOW_LENGTH)
    return (bucket, window)

def block_step(memory, inputs, query_weight, forget, bias_window, window, length, score_scale):
    query_rows, current_key, current_value, key_prev, value_prev, start = inputs
    key_ctx = jnp.concatenate([key_prev, current_key], axis=0)
    context_value = jnp.concatenate([value_prev, current_value], axis=0)
    key_pos = start - WINDOW_LENGTH + jnp.arange(2 * WINDOW_LENGTH, dtype=jnp.int32)
    key_live = (key_pos >= 0) & (key_pos < length)
    allowed = window & key_live[None, :]
    lowered_memory = lowered_input(memory)
    score_ctx = contract_product('qhd,khd->hqk', query_rows, key_ctx) * score_scale + bias_window
    score_ctx = jnp.where(allowed[None], score_ctx, -jnp.inf)
    memory_scores = contract_product('rub,yub->ury', query_rows, lowered_memory) * score_scale
    scores = lowered_backward(jnp.concatenate([score_ctx, memory_scores], axis=-1))
    probabilities = lowered_input(softmax_rows(scores))
    attended_output = contract_product('zvx,xzs->vzs', probabilities[:, :, :2 * WINDOW_LENGTH], context_value) + contract_product('rnf,fro->nro', probabilities[:, :, 2 * WINDOW_LENGTH:], lowered_memory)
    state_query_rows = lowered_backward(lowered_input(contract_product('czy,zyg->czg', lowered_memory, query_weight)))
    self_scores = contract_product('rtf,jtf->trj', state_query_rows, lowered_memory) * score_scale
    cross_scores = contract_product('ecw,ycw->cey', state_query_rows, current_key) * score_scale
    cross_scores = jnp.where(key_live[WINDOW_LENGTH:][None, None, :], cross_scores, -jnp.inf)
    state_probabilities = lowered_input(softmax_rows(lowered_backward(jnp.concatenate([self_scores, cross_scores], axis=-1))))
    state_update = lowered_backward(contract_product('rle,erv->lrv', state_probabilities[:, :, :STATE_VECTORS], lowered_memory) + contract_product('owg,goa->woa', state_probabilities[:, :, STATE_VECTORS:], current_value))
    live_flag = start < length
    new_memory = jnp.where(live_flag, forget * memory + (1.0 - forget) * state_update, memory)
    return (new_memory, attended_output)

def slot_forward(tokens_slot, length, memory_init, w_qkv, w_out, w_up, w_down, gain_attn, gain_mlp, rel_bias, state_query, gate_bias):
    blocks = SLOT // WINDOW_LENGTH
    positions = jnp.arange(SLOT, dtype=jnp.int32)
    row_live = (positions < length).astype(jnp.float32)[:, None]
    normed = lowered_input(rms_norm(tokens_slot, gain_attn))
    projected = lowered_backward(lowered_input(matmul(normed, w_qkv))).reshape(SLOT, 3, H, DH)
    query_rows = projected[:, 0].reshape(blocks, WINDOW_LENGTH, H, DH)
    keys_all = projected[:, 1].reshape(blocks, WINDOW_LENGTH, H, DH)
    values_all = projected[:, 2].reshape(blocks, WINDOW_LENGTH, H, DH)
    zero_block = jnp.zeros((1, WINDOW_LENGTH, H, DH), jnp.float32)
    key_prev = jnp.concatenate([zero_block, keys_all[:-1]], axis=0)
    value_prev = jnp.concatenate([zero_block, values_all[:-1]], axis=0)
    bucket, window = bucket_table()
    bias_window = rel_bias[:, bucket]
    forget = jax.nn.sigmoid(gate_bias)
    starts = jnp.arange(blocks, dtype=jnp.int32) * WINDOW_LENGTH
    memory = memory_init.reshape(STATE_VECTORS, H, DH)

    def scan_step(carry, inputs):
        return block_step(carry, inputs, state_query, forget, bias_window, window, length, DH ** (-0.5))
    final_memory, attended_output = lax.scan(jax.checkpoint(scan_step), memory, (query_rows, keys_all, values_all, key_prev, value_prev, starts))
    attended_rows = lowered_backward(lowered_input(attended_output.reshape(SLOT, H * DH)))
    branch = lowered_backward(matmul(attended_rows, w_out))
    mid = tokens_slot + branch
    normed_mid = lowered_input(rms_norm(mid, gain_mlp))
    hidden_pre = lowered_backward(matmul(normed_mid, w_up))
    hidden = lowered_input(smooth_gate(hidden_pre))
    mlp_out = lowered_backward(matmul(hidden, w_down))
    return (row_live * (mid + mlp_out), final_memory.reshape(STATE_VECTORS, H * DH))

def reference(tokens, lengths, state_init, w_qkv, w_out, w_up, w_down, norm_attn, norm_mlp, rel_bias, state_query, gate_bias, out_grad, state_grad):
    memory_init = state_init.astype(jnp.float32)

    def whole(tokens_all, w_qkv_f, w_out_f, w_up_f, w_down_f, gain_attn, gain_mlp, bias_table, query_weight, gate_logit):

        def per_slot(inputs):
            tokens_slot, length, memory_slot = inputs
            return slot_forward(tokens_slot, length, memory_slot, w_qkv_f, w_out_f, w_up_f, w_down_f, gain_attn, gain_mlp, bias_table, query_weight, gate_logit)
        return lax.map(jax.checkpoint(per_slot), (tokens_all, lengths, memory_init))
    primal, pull = jax.vjp(whole, tokens.astype(jnp.float32), w_qkv.astype(jnp.float32), w_out.astype(jnp.float32), w_up.astype(jnp.float32), w_down.astype(jnp.float32), norm_attn.astype(jnp.float32), norm_mlp.astype(jnp.float32), rel_bias.astype(jnp.float32), state_query.astype(jnp.float32), gate_bias.astype(jnp.float32))
    grads = pull((out_grad.astype(jnp.float32), state_grad.astype(jnp.float32)))
    return (primal[0].astype(jnp.bfloat16), primal[1], grads[0], grads[1], grads[2], grads[3], grads[4], grads[5], grads[6], grads[7], grads[8], grads[9])
```

```python
import functools
import math

import jax
import jax.numpy as jnp
import numpy as np
from jax import lax
from jax.experimental import pallas as pl
from jax.experimental.pallas import tpu as pltpu
from jax.sharding import PartitionSpec as P

H = 8
DH = 128
BLOCK = 512
STATE_VECTORS = 512
QTILE = 256
SPAN = BLOCK + QTILE

EPSILON = 1e-06
BUCKET_EDGES = (19, 21, 24, 27, 31, 35, 40, 46, 52, 59, 67, 77, 87, 99, 113)
BUCKETS = 32
LOG2E = math.log2(math.e)
SCALE = DH ** (-0.5)
NEAR = 384

f32 = jnp.float32
bf16 = jnp.bfloat16


def bucket_of(distance):
    return np.minimum(distance, 16) + (distance[..., None] >= np.array(BUCKET_EDGES)).sum(-1)


def tile_distance():
    rows = np.arange(QTILE)[:, None]
    cols = np.arange(SPAN)[None, :]
    return rows + BLOCK - cols


def tile_bias(table):
    distance = jnp.arange(QTILE, dtype=jnp.int32)[:, None] + BLOCK - jnp.arange(SPAN, dtype=jnp.int32)[None, :]
    clipped = jnp.clip(distance, 0, BLOCK)
    edges = jnp.array(BUCKET_EDGES, dtype=jnp.int32)
    bucket = jnp.minimum(clipped, 16) + jnp.sum((clipped[:, :, None] >= edges).astype(jnp.int32), axis=-1)
    total = jnp.zeros((table.shape[0],) + bucket.shape, f32)
    for bucket_id in range(BUCKETS):
        total = jnp.where((bucket == bucket_id)[None], table[:, bucket_id][:, None, None], total)
    window = (distance >= 0) & (distance < BLOCK)
    return jnp.where(window[None], total * LOG2E, -jnp.inf)


def dot(a, b):
    return jnp.dot(a, b, preferred_element_type=f32)


def dot_t(a, b):
    return lax.dot_general(a, b, (((1,), (1,)), ((), ())), preferred_element_type=f32)


def t_dot(a, b):
    return lax.dot_general(a, b, (((0,), (0,)), ((), ())), preferred_element_type=f32)


def to_row(column):
    wide = jnp.broadcast_to(column, (column.shape[0], 128))
    return wide.T[0:1, :]


def context_pieces(tile):
    start = tile * QTILE
    pieces = []
    if start < BLOCK:
        pieces.append((0, start, BLOCK, 0))
    pieces.append((1, 0, start + QTILE, BLOCK - start))
    return pieces


def softmax_parts(scores):
    top = functools.reduce(jnp.maximum, [jnp.max(s, axis=-1, keepdims=True) for s in scores])
    raised = [jnp.exp2(s - top) for s in scores]
    total = functools.reduce(jnp.add, [jnp.sum(e, axis=-1, keepdims=True) for e in raised])
    return raised, total, top + jnp.log2(total)


def attend_kernel(
    heads,
    length_ref,
    cur_ref,
    prev_ref,
    init_ref,
    query_ref,
    forget_ref,
    bias_ref,
    att_ref,
    final_ref,
    mem_ref,
    upd_ref,
    lse_ref,
    slse_ref,
    memory_ref,
):
    block = pl.program_id(0)
    length = length_ref[0]
    width = heads * DH
    scale2 = SCALE * LOG2E

    @pl.when(block == 0)
    def _():
        memory_ref[...] = init_ref[...].astype(f32)

    live_block = block * BLOCK < length
    for head in range(heads):
        own = slice(head * DH, (head + 1) * DH)
        memory = memory_ref[:, own]
        low = memory.astype(bf16)
        mem_ref[0, :, own] = memory
        refs = (prev_ref, cur_ref)
        key_cols = slice(width + head * DH, width + (head + 1) * DH)
        value_cols = slice(2 * width + head * DH, 2 * width + (head + 1) * DH)
        for tile in range(BLOCK // QTILE):
            rows = slice(tile * QTILE, (tile + 1) * QTILE)
            query = cur_ref[rows, own]
            scores, values = [], []
            for which, lo, hi, col in context_pieces(tile):
                s = dot_t(query, refs[which][lo:hi, key_cols])
                position = (block - 1 + which) * BLOCK + lo + lax.broadcasted_iota(jnp.int32, (1, hi - lo), 1)
                live = (position >= 0) & (position < length)
                s = s * scale2 + bias_ref[head, :, col : col + hi - lo]
                scores.append(jnp.where(live, s, -jnp.inf))
                values.append(refs[which][lo:hi, value_cols])
            scores.append(dot_t(query, low) * scale2)
            values.append(low)
            raised, total, lse = softmax_parts(scores)
            out = functools.reduce(jnp.add, [dot(e.astype(bf16), v) for e, v in zip(raised, values)])
            att_ref[rows, own] = (out / total).astype(bf16)
            lse_ref[head : head + 1, rows] = to_row(lse)
        own_key = cur_ref[:, key_cols]
        own_value = cur_ref[:, value_cols]
        squeries = dot(low, query_ref[head]).astype(bf16)
        position = block * BLOCK + lax.broadcasted_iota(jnp.int32, (1, BLOCK), 1)
        for tile in range(STATE_VECTORS // QTILE):
            rows = slice(tile * QTILE, (tile + 1) * QTILE)
            squery = squeries[rows]
            scores = [
                dot_t(squery, low) * scale2,
                jnp.where(position < length, dot_t(squery, own_key) * scale2, -jnp.inf),
            ]
            raised, total, lse = softmax_parts(scores)
            update = dot(raised[0].astype(bf16), low) + dot(raised[1].astype(bf16), own_value)
            update = update / total
            upd_ref[0, rows, own] = update
            slse_ref[head : head + 1, rows] = to_row(lse)
            forget = forget_ref[:, own]
            old = memory[rows]
            memory_ref[rows, own] = jnp.where(live_block, forget * old + (1.0 - forget) * update, old)
    final_ref[...] = memory_ref[...]


def attend(qkv, init, length, state_query, forget, bias, heads):
    rows, width3 = qkv.shape
    width = heads * DH
    blocks = rows // BLOCK
    return pl.pallas_call(
        functools.partial(attend_kernel, heads),
        grid=(blocks,),
        out_shape=(
            jax.ShapeDtypeStruct((rows, width), bf16),
            jax.ShapeDtypeStruct((STATE_VECTORS, width), f32),
            jax.ShapeDtypeStruct((blocks, STATE_VECTORS, width), f32),
            jax.ShapeDtypeStruct((blocks, STATE_VECTORS, width), f32),
            jax.ShapeDtypeStruct((heads, rows), f32),
            jax.ShapeDtypeStruct((heads, blocks * STATE_VECTORS), f32),
        ),
        in_specs=[
            pl.BlockSpec(memory_space=pltpu.SMEM),
            pl.BlockSpec((BLOCK, width3), lambda b: (b, 0)),
            pl.BlockSpec((BLOCK, width3), lambda b: (jnp.maximum(b - 1, 0), 0)),
            pl.BlockSpec((STATE_VECTORS, width), lambda b: (0, 0)),
            pl.BlockSpec((heads, DH, DH), lambda b: (0, 0, 0)),
            pl.BlockSpec((1, width), lambda b: (0, 0)),
            pl.BlockSpec((heads, QTILE, SPAN), lambda b: (0, 0, 0)),
        ],
        out_specs=(
            pl.BlockSpec((BLOCK, width), lambda b: (b, 0)),
            pl.BlockSpec((STATE_VECTORS, width), lambda b: (0, 0)),
            pl.BlockSpec((1, STATE_VECTORS, width), lambda b: (b, 0, 0)),
            pl.BlockSpec((1, STATE_VECTORS, width), lambda b: (b, 0, 0)),
            pl.BlockSpec((heads, BLOCK), lambda b: (0, b)),
            pl.BlockSpec((heads, STATE_VECTORS), lambda b: (0, b)),
        ),
        scratch_shapes=[pltpu.VMEM((STATE_VECTORS, width), f32)],
        compiler_params=pltpu.CompilerParams(vmem_limit_bytes=40 << 20),
        cost_estimate=pl.CostEstimate(
            flops=blocks * heads * 512 * 2400 * 128 * 4, bytes_accessed=16 << 20, transcendentals=10 << 20
        ),
        name="attend",
    )(length, qkv, qkv, init, state_query, forget, bias)


def attend_back_kernel(
    heads,
    blocks,
    length_ref,
    cur_ref,
    prev_ref,
    dout_ref,
    out_ref,
    mem_ref,
    upd_ref,
    lse_ref,
    slse_ref,
    sgrad_ref,
    query_ref,
    forget_ref,
    bias_ref,
    dqkv_ref,
    dquery_ref,
    dforget_ref,
    near_ref,
    far_ref,
    dmem_ref,
    dnext_ref,
    dctx_ref,
):
    step = pl.program_id(0)
    block = blocks - 1 - step
    length = length_ref[0]
    width = heads * DH
    scale2 = SCALE * LOG2E

    @pl.when(step == 0)
    def _():
        dmem_ref[...] = sgrad_ref[...].astype(f32)
        dnext_ref[...] = jnp.zeros_like(dnext_ref)
        dquery_ref[...] = jnp.zeros_like(dquery_ref)
        dforget_ref[...] = jnp.zeros_like(dforget_ref)
        near_ref[...] = jnp.zeros_like(near_ref)
        far_ref[...] = jnp.zeros_like(far_ref)

    live_block = block * BLOCK < length
    refs = (prev_ref, cur_ref)
    for head in range(heads):
        own = slice(head * DH, (head + 1) * DH)
        key_cols = slice(width + head * DH, width + (head + 1) * DH)
        value_cols = slice(2 * width + head * DH, 2 * width + (head + 1) * DH)
        memory = mem_ref[0, :, own]
        update = upd_ref[0, :, own]
        low = memory.astype(bf16)
        forget = forget_ref[:, own]
        dmem = dmem_ref[:, own]
        dupd = jnp.where(live_block, (1.0 - forget) * dmem, 0.0).astype(bf16)
        moved = jnp.where(live_block, dmem * (memory - update), 0.0)
        dforget_ref[:, own] += jnp.sum(moved, axis=0, keepdims=True)
        dmem_new = jnp.where(live_block, forget * dmem, dmem)
        own_key = cur_ref[:, key_cols]
        own_value = cur_ref[:, value_cols]
        squeries = dot(low, query_ref[head]).astype(bf16)
        sdelta = jnp.sum((dupd.astype(f32) * update).T, axis=0, keepdims=True)
        slse = slse_ref[head : head + 1, :]
        dsquery = jnp.zeros((STATE_VECTORS, DH), f32)
        dkey = []
        dvalue = []
        for part in range(2 * STATE_VECTORS // QTILE):
            own_part = part >= STATE_VECTORS // QTILE
            lo = (part % (STATE_VECTORS // QTILE)) * QTILE
            keys = (own_key if own_part else low)[lo : lo + QTILE]
            values = (own_value if own_part else low)[lo : lo + QTILE]
            s = dot_t(keys, squeries) * scale2 - slse
            if own_part:
                position = block * BLOCK + lo + lax.broadcasted_iota(jnp.int32, (QTILE, 1), 0)
                s = jnp.where(position < length, s, -jnp.inf)
            p = jnp.exp2(s)
            dp = dot_t(values, dupd)
            ds = (p * (dp - sdelta)).astype(bf16)
            dvalue.append(dot(p.astype(bf16), dupd))
            dkey.append(dot(ds, squeries))
            dsquery += t_dot(ds, keys)
        half = STATE_VECTORS // QTILE
        dlow = [dvalue[i] + dkey[i] * SCALE for i in range(half)]
        dctx_ref[0, 0:BLOCK] = jnp.zeros((BLOCK, DH), f32)
        dctx_ref[1, 0:BLOCK] = jnp.zeros((BLOCK, DH), f32)
        for i in range(half):
            rows = slice(BLOCK + i * QTILE, BLOCK + (i + 1) * QTILE)
            old = slice(i * QTILE, (i + 1) * QTILE)
            dctx_ref[0, rows] = dkey[half + i] * SCALE + dnext_ref[0, old, own]
            dctx_ref[1, rows] = dvalue[half + i] + dnext_ref[1, old, own]
        dsq = (dsquery * SCALE).astype(bf16)
        dquery_ref[head] += t_dot(low, dsq)
        dmem_ref[:, own] = dmem_new + dot_t(dsq, query_ref[head])
        for tile in range(BLOCK // QTILE):
            rows = slice(tile * QTILE, (tile + 1) * QTILE)
            query = cur_ref[rows, own]
            dout = dout_ref[rows, own]
            lse = lse_ref[head : head + 1, rows]
            delta = jnp.sum((dout.astype(f32) * out_ref[rows, own].astype(f32)).T, axis=0, keepdims=True)
            dq = jnp.zeros((QTILE, DH), f32)
            for which, lo, hi, col in context_pieces(tile):
                for at in range(lo, hi, QTILE):
                    keys = refs[which][at : at + QTILE, key_cols]
                    values = refs[which][at : at + QTILE, value_cols]
                    band = col + at - lo
                    position = (block - 1 + which) * BLOCK + at + lax.broadcasted_iota(jnp.int32, (QTILE, 1), 0)
                    live = (position >= 0) & (position < length)
                    s = dot_t(keys, query) * scale2 + bias_ref[head, band : band + QTILE, :] - lse
                    p = jnp.exp2(jnp.where(live, s, -jnp.inf))
                    dp = dot_t(values, dout)
                    ds = (p * (dp - delta)).astype(bf16)
                    wide = ds.astype(f32)
                    if band + QTILE <= SPAN - NEAR:
                        far_ref[head] += functools.reduce(jnp.add, [wide[i : i + 8] for i in range(0, QTILE, 8)])
                    else:
                        edge = max(SPAN - NEAR - band, 0)
                        if edge:
                            far_ref[head] += functools.reduce(jnp.add, [wide[i : i + 8] for i in range(0, edge, 8)])
                        at_near = band + edge - (SPAN - NEAR)
                        near_ref[head, at_near : at_near + QTILE - edge] += wide[edge:]
                    into = slice(which * BLOCK + at, which * BLOCK + at + QTILE)
                    dctx_ref[1, into] += dot(p.astype(bf16), dout)
                    dctx_ref[0, into] += dot(ds, query) * SCALE
                    dq += t_dot(ds, keys)
            for part in range(half):
                keys = low[part * QTILE : (part + 1) * QTILE]
                s = dot_t(keys, query) * scale2 - lse
                p = jnp.exp2(s)
                dp = dot_t(keys, dout)
                ds = (p * (dp - delta)).astype(bf16)
                dlow[part] += dot(p.astype(bf16), dout) + dot(ds, query) * SCALE
                dq += t_dot(ds, keys)
            dqkv_ref[rows, own] = (dq * SCALE).astype(bf16)
        for part in range(half):
            dmem_ref[part * QTILE : (part + 1) * QTILE, own] += dlow[part]
        dnext_ref[0, :, own] = dctx_ref[0, 0:BLOCK]
        dnext_ref[1, :, own] = dctx_ref[1, 0:BLOCK]
        dqkv_ref[:, key_cols] = dctx_ref[0, BLOCK:].astype(bf16)
        dqkv_ref[:, value_cols] = dctx_ref[1, BLOCK:].astype(bf16)


def attend_back(qkv, dout, out, mem, upd, lse, slse, sgrad, length, state_query, forget, bias_t, heads):
    rows, width3 = qkv.shape
    width = heads * DH
    blocks = rows // BLOCK
    last = blocks - 1
    return pl.pallas_call(
        functools.partial(attend_back_kernel, heads, blocks),
        grid=(blocks,),
        out_shape=(
            jax.ShapeDtypeStruct((rows, width3), bf16),
            jax.ShapeDtypeStruct((heads, DH, DH), f32),
            jax.ShapeDtypeStruct((1, width), f32),
            jax.ShapeDtypeStruct((heads, NEAR, QTILE), f32),
            jax.ShapeDtypeStruct((heads, 8, QTILE), f32),
        ),
        in_specs=[
            pl.BlockSpec(memory_space=pltpu.SMEM),
            pl.BlockSpec((BLOCK, width3), lambda b: (last - b, 0)),
            pl.BlockSpec((BLOCK, width3), lambda b: (jnp.maximum(last - b - 1, 0), 0)),
            pl.BlockSpec((BLOCK, width), lambda b: (last - b, 0)),
            pl.BlockSpec((BLOCK, width), lambda b: (last - b, 0)),
            pl.BlockSpec((1, STATE_VECTORS, width), lambda b: (last - b, 0, 0)),
            pl.BlockSpec((1, STATE_VECTORS, width), lambda b: (last - b, 0, 0)),
            pl.BlockSpec((heads, BLOCK), lambda b: (0, last - b)),
            pl.BlockSpec((heads, STATE_VECTORS), lambda b: (0, last - b)),
            pl.BlockSpec((STATE_VECTORS, width), lambda b: (0, 0)),
            pl.BlockSpec((heads, DH, DH), lambda b: (0, 0, 0)),
            pl.BlockSpec((1, width), lambda b: (0, 0)),
            pl.BlockSpec((heads, SPAN, QTILE), lambda b: (0, 0, 0)),
        ],
        out_specs=(
            pl.BlockSpec((BLOCK, width3), lambda b: (last - b, 0)),
            pl.BlockSpec((heads, DH, DH), lambda b: (0, 0, 0)),
            pl.BlockSpec((1, width), lambda b: (0, 0)),
            pl.BlockSpec((heads, NEAR, QTILE), lambda b: (0, 0, 0)),
            pl.BlockSpec((heads, 8, QTILE), lambda b: (0, 0, 0)),
        ),
        scratch_shapes=[
            pltpu.VMEM((STATE_VECTORS, width), f32),
            pltpu.VMEM((2, BLOCK, width), f32),
            pltpu.VMEM((2, 2 * BLOCK, DH), f32),
        ],
        compiler_params=pltpu.CompilerParams(vmem_limit_bytes=40 << 20),
        cost_estimate=pl.CostEstimate(
            flops=blocks * heads * 512 * 2400 * 128 * 10, bytes_accessed=20 << 20, transcendentals=10 << 20
        ),
        name="attend_back",
    )(length, qkv, qkv, dout, out, mem, upd, lse, slse, sgrad, state_query, forget, bias_t)


def bias_table_grad(near, far):
    distance = tile_distance().T[SPAN - NEAR :]
    bucket = np.where((distance >= 0) & (distance < BLOCK), bucket_of(np.clip(distance, 0, BLOCK)), BUCKETS)
    bucket = jnp.asarray(bucket.astype(np.int32))
    columns = [jnp.sum(jnp.where((bucket == i)[None], near, 0.0), axis=(1, 2)) for i in range(BUCKETS)]
    columns[-1] = columns[-1] + jnp.sum(far, axis=(1, 2))
    return jnp.stack(columns, axis=1)


def inverse_rms(values):
    return lax.rsqrt(jnp.mean(values * values, axis=-1, keepdims=True) + EPSILON)


def norm_back(values, gain, rho, grad):
    scaled = gain * grad
    mean = jnp.mean(values * scaled, axis=-1, keepdims=True)
    return rho * scaled - values * (rho * rho * rho * mean), jnp.sum(grad * values * rho, axis=0)


def body(
    tokens,
    lengths,
    state_init,
    w_qkv,
    w_out,
    w_up,
    w_down,
    norm_attn,
    norm_mlp,
    rel_bias,
    state_query,
    gate_bias,
    out_grad,
    state_grad,
):
    seq_count = lax.axis_size("seq")
    fsdp_count = lax.axis_size("fsdp")
    seq_at = lax.axis_index("seq")
    heads = H // seq_count
    width = heads * DH
    tok_rows, dim = tokens.shape[1:]
    rows = tok_rows * seq_count
    hidden_all = w_up.shape[1]
    share = hidden_all // (seq_count * fsdp_count)

    all_tokens = lax.all_gather(tokens[0], "seq", axis=0, tiled=True)
    own_qkv = lax.dynamic_slice_in_dim(
        w_qkv.reshape(w_qkv.shape[0], 3, seq_count, width), seq_at, 1, axis=2
    ).reshape(w_qkv.shape[0], 3 * width)
    qkv_w = lax.all_gather(own_qkv, "fsdp", axis=0, tiled=True)
    gains = lax.all_gather(jnp.stack([norm_attn, norm_mlp]), "fsdp", axis=1, tiled=True).astype(f32)
    gain_attn, gain_mlp = gains[0], gains[1]
    own_up = lax.dynamic_slice_in_dim(
        w_up.reshape(w_up.shape[0], fsdp_count, seq_count, share), seq_at, 1, axis=2
    ).reshape(w_up.shape[0], fsdp_count * share)
    own_down = lax.dynamic_slice_in_dim(w_down, seq_at * share, share, axis=0)
    up_w = lax.all_gather(own_up, "fsdp", axis=0, tiled=True)
    down_w = lax.all_gather(own_down, "fsdp", axis=0, tiled=True)
    out_w = lax.all_gather(w_out, "fsdp", axis=0, tiled=True)
    all_grad = lax.all_gather(out_grad[0], "seq", axis=0, tiled=True)

    bias = tile_bias(rel_bias)
    bias_t = jnp.swapaxes(bias, 1, 2)
    forget = jax.nn.sigmoid(gate_bias)
    forget_row = forget.reshape(1, width)

    inputs = all_tokens.astype(f32)
    normed = (inputs * inverse_rms(inputs) * gain_attn).astype(bf16)
    qkv = dot(normed, qkv_w).astype(bf16)
    attended, final_memory, mem, upd, lse, slse = attend(
        qkv, state_init[0], lengths, state_query, forget_row, bias, heads
    )

    all_attended = lax.all_gather(attended, "seq", axis=1, tiled=True)
    mid = inputs + dot(all_attended, out_w)
    rho_mid = inverse_rms(mid)
    normed_mid = (mid * rho_mid * gain_mlp).astype(bf16)
    live = (jnp.arange(rows, dtype=jnp.int32) < lengths[0]).astype(bf16)[:, None]
    grad_low = all_grad * live
    pre = dot(normed_mid, up_w)
    hidden, gelu_pull = jax.vjp(lambda v: jax.nn.gelu(v, approximate=False), pre)
    hidden = hidden.astype(bf16)
    dpre = gelu_pull(dot_t(grad_low, down_w))[0].astype(bf16)
    dnormed_mid = lax.psum_scatter(dot_t(dpre, up_w).astype(bf16), "seq", scatter_dimension=0, tiled=True)
    mlp_out = lax.psum_scatter(dot(hidden, down_w).astype(bf16), "seq", scatter_dimension=0, tiled=True)
    down_grad = t_dot(hidden, grad_low)
    up_grad = t_dot(normed_mid, dpre)

    here = seq_at * tok_rows
    mid_here = lax.dynamic_slice_in_dim(mid, here, tok_rows, axis=0)
    live_here = (here + jnp.arange(tok_rows, dtype=jnp.int32) < lengths[0]).astype(f32)[:, None]
    output = (live_here * (mid_here + mlp_out.astype(f32))).astype(bf16)[None]
    grad_here = out_grad[0].astype(f32) * live_here
    through, mlp_gain_grad = norm_back(mid_here, gain_mlp, inverse_rms(mid_here), dnormed_mid.astype(f32))
    dmid = grad_here + through
    dbranch = lax.all_gather(dmid.astype(bf16), "seq", axis=0, tiled=True)
    own_out = lax.dynamic_slice_in_dim(out_w, seq_at * width, width, axis=0)
    dattended = dot_t(dbranch, own_out).astype(bf16)
    out_w_grad = t_dot(attended, dbranch)

    dqkv, dquery, dforget, near, far = attend_back(
        qkv, dattended, attended, mem, upd, lse, slse, state_grad[0], lengths, state_query, forget_row, bias_t, heads
    )
    dnormed = lax.psum_scatter(dot_t(dqkv, qkv_w).astype(bf16), "seq", scatter_dimension=0, tiled=True)
    qkv_grad = t_dot(normed, dqkv)
    inputs_here = tokens[0].astype(f32)
    through, attn_gain_grad = norm_back(inputs_here, gain_attn, inverse_rms(inputs_here), dnormed.astype(f32))
    tokens_grad = (dmid + through)[None]

    grad_gate = dforget.reshape(heads, DH) * forget * (1.0 - forget)
    grad_table = bias_table_grad(near, far)
    small = jnp.concatenate(
        [dquery.reshape(-1), grad_gate.reshape(-1), grad_table.reshape(-1)]
    )
    small = lax.psum(small, "fsdp")
    cut = heads * DH * DH
    dquery = small[:cut].reshape(heads, DH, DH)
    grad_gate = small[cut : cut + heads * DH].reshape(heads, DH)
    grad_table = small[cut + heads * DH :].reshape(heads, BUCKETS)

    def spread(term):
        return lax.psum_scatter(term, "fsdp", scatter_dimension=0, tiled=True)

    def exchange(term):
        return lax.all_to_all(term, "seq", split_axis=0, concat_axis=0, tiled=True)

    qkv_part = exchange(qkv_grad.astype(bf16)).reshape(seq_count, dim // seq_count, 3, width)
    qkv_part = spread(jnp.transpose(qkv_part, (1, 2, 0, 3)).reshape(dim // seq_count, 3 * H * DH)).astype(f32)
    out_part = spread(out_w_grad.astype(bf16)).astype(f32)
    up_part = exchange(up_grad.astype(bf16)).reshape(seq_count, dim // seq_count, fsdp_count, share)
    up_part = spread(jnp.transpose(up_part, (1, 2, 0, 3)).reshape(dim // seq_count, hidden_all)).astype(f32)
    down_part = jnp.transpose(
        down_grad.astype(bf16).reshape(seq_count, fsdp_count // seq_count, share, dim), (0, 1, 2, 3)
    )
    down_part = lax.all_to_all(down_part, "seq", split_axis=0, concat_axis=0, tiled=True)
    down_part = jnp.swapaxes(down_part, 0, 1).reshape(seq_count * (fsdp_count // seq_count) * share, dim)
    down_part = spread(down_part).astype(f32)
    attn_gain_grad, mlp_gain_grad = jnp.split(
        lax.psum_scatter(
            jnp.stack([attn_gain_grad, mlp_gain_grad]), ("seq", "fsdp"), scatter_dimension=1, tiled=True
        ),
        2,
    )
    return (
        output,
        final_memory[None],
        tokens_grad,
        qkv_part,
        out_part,
        up_part,
        down_part,
        attn_gain_grad[0],
        mlp_gain_grad[0],
        grad_table,
        dquery,
        grad_gate,
    )


def solution(mesh):
    placed = (
        P("fsdp", "seq", None),
        P("fsdp"),
        P("fsdp", None, "seq"),
        P("fsdp", None),
        P("fsdp", None),
        P("fsdp", None),
        P("fsdp", None),
        P("fsdp"),
        P("fsdp"),
        P("seq", None),
        P("seq", None, None),
        P("seq", None),
        P("fsdp", "seq", None),
        P("fsdp", None, "seq"),
    )
    return jax.shard_map(
        body,
        mesh=mesh,
        in_specs=placed,
        out_specs=(
            P("fsdp", "seq", None),
            P("fsdp", None, "seq"),
            P("fsdp", "seq", None),
            P(("seq", "fsdp"), None),
            P(("seq", "fsdp"), None),
            P(("seq", "fsdp"), None),
            P(("seq", "fsdp"), None),
            P(("seq", "fsdp")),
            P(("seq", "fsdp")),
            P("seq", None),
            P("seq", None, None),
            P("seq", None),
        ),
        check_vma=False,
    )
```

```python
import functools
import math

import jax
import jax.numpy as jnp
import numpy as np
from jax import lax
from jax.experimental import pallas as pl
from jax.experimental.pallas import tpu as pltpu
from jax.sharding import PartitionSpec as P

H = 8
DH = 128
BLOCK = 512
STATE_VECTORS = 512
QTILE = 256
SPAN = BLOCK + QTILE

EPSILON = 1e-06
BUCKET_EDGES = (19, 21, 24, 27, 31, 35, 40, 46, 52, 59, 67, 77, 87, 99, 113)
BUCKETS = 32
LOG2E = math.log2(math.e)
SCALE = DH ** (-0.5)
NEAR = 384

f32 = jnp.float32
bf16 = jnp.bfloat16
MESH = pl.DeviceIdType.MESH


def bucket_of(distance):
    return np.minimum(distance, 16) + (distance[..., None] >= np.array(BUCKET_EDGES)).sum(-1)


def tile_distance():
    rows = np.arange(QTILE)[:, None]
    cols = np.arange(SPAN)[None, :]
    return rows + BLOCK - cols


def tile_bias(table):
    distance = jnp.arange(QTILE, dtype=jnp.int32)[:, None] + BLOCK - jnp.arange(SPAN, dtype=jnp.int32)[None, :]
    clipped = jnp.clip(distance, 0, BLOCK)
    edges = jnp.array(BUCKET_EDGES, dtype=jnp.int32)
    bucket = jnp.minimum(clipped, 16) + jnp.sum((clipped[:, :, None] >= edges).astype(jnp.int32), axis=-1)
    total = jnp.zeros((table.shape[0],) + bucket.shape, f32)
    for bucket_id in range(BUCKETS):
        total = jnp.where((bucket == bucket_id)[None], table[:, bucket_id][:, None, None], total)
    window = (distance >= 0) & (distance < BLOCK)
    return jnp.where(window[None], total * LOG2E, -jnp.inf)


def dot(a, b):
    return jnp.dot(a, b, preferred_element_type=f32)


def dot_t(a, b):
    return lax.dot_general(a, b, (((1,), (1,)), ((), ())), preferred_element_type=f32)


def t_dot(a, b):
    return lax.dot_general(a, b, (((0,), (0,)), ((), ())), preferred_element_type=f32)


def to_row(column):
    wide = jnp.broadcast_to(column, (column.shape[0], 128))
    return wide.T[0:1, :]


def context_pieces(tile):
    start = tile * QTILE
    pieces = []
    if start < BLOCK:
        pieces.append((0, start, BLOCK, 0))
    pieces.append((1, 0, start + QTILE, BLOCK - start))
    return pieces


def softmax_parts(scores):
    top = functools.reduce(jnp.maximum, [jnp.max(s, axis=-1, keepdims=True) for s in scores])
    raised = [jnp.exp2(s - top) for s in scores]
    total = functools.reduce(jnp.add, [jnp.sum(e, axis=-1, keepdims=True) for e in raised])
    return raised, total, top + jnp.log2(total)


def attend_kernel(
    heads,
    length_ref,
    order_ref,
    cur_ref,
    prev_ref,
    init_ref,
    query_ref,
    forget_ref,
    bias_ref,
    att_ref,
    final_ref,
    mem_ref,
    upd_ref,
    lse_ref,
    slse_ref,
    memory_ref,
):
    block = pl.program_id(0)
    length = length_ref[0]
    width = heads * DH
    scale2 = SCALE * LOG2E

    @pl.when(block == 0)
    def _():
        memory_ref[...] = init_ref[...].astype(f32)

    live_block = block * BLOCK < length
    for head in range(heads):
        own = slice(head * DH, (head + 1) * DH)
        memory = memory_ref[:, own]
        low = memory.astype(bf16)
        mem_ref[0, :, own] = memory
        refs = (prev_ref, cur_ref)
        key_cols = slice(width + head * DH, width + (head + 1) * DH)
        value_cols = slice(2 * width + head * DH, 2 * width + (head + 1) * DH)
        for tile in range(BLOCK // QTILE):
            rows = slice(tile * QTILE, (tile + 1) * QTILE)
            query = cur_ref[rows, own]
            scores, values = [], []
            for which, lo, hi, col in context_pieces(tile):
                s = dot_t(query, refs[which][lo:hi, key_cols])
                position = (block - 1 + which) * BLOCK + lo + lax.broadcasted_iota(jnp.int32, (1, hi - lo), 1)
                live = (position >= 0) & (position < length)
                s = s * scale2 + bias_ref[head, :, col : col + hi - lo]
                scores.append(jnp.where(live, s, -jnp.inf))
                values.append(refs[which][lo:hi, value_cols])
            scores.append(dot_t(query, low) * scale2)
            values.append(low)
            raised, total, lse = softmax_parts(scores)
            out = functools.reduce(jnp.add, [dot(e.astype(bf16), v) for e, v in zip(raised, values)])
            att_ref[rows, own] = (out / total).astype(bf16)
            lse_ref[head : head + 1, rows] = to_row(lse)
        own_key = cur_ref[:, key_cols]
        own_value = cur_ref[:, value_cols]
        squeries = dot(low, query_ref[head]).astype(bf16)
        position = block * BLOCK + lax.broadcasted_iota(jnp.int32, (1, BLOCK), 1)
        for tile in range(STATE_VECTORS // QTILE):
            rows = slice(tile * QTILE, (tile + 1) * QTILE)
            squery = squeries[rows]
            scores = [
                dot_t(squery, low) * scale2,
                jnp.where(position < length, dot_t(squery, own_key) * scale2, -jnp.inf),
            ]
            raised, total, lse = softmax_parts(scores)
            update = dot(raised[0].astype(bf16), low) + dot(raised[1].astype(bf16), own_value)
            update = update / total
            upd_ref[0, rows, own] = update
            slse_ref[head : head + 1, rows] = to_row(lse)
            forget = forget_ref[:, own]
            old = memory[rows]
            memory_ref[rows, own] = jnp.where(live_block, forget * old + (1.0 - forget) * update, old)
    final_ref[...] = memory_ref[...]


def attend(qkv, init, length, state_query, forget, bias, heads, order):
    rows, width3 = qkv.shape
    width = heads * DH
    blocks = rows // BLOCK
    return pl.pallas_call(
        functools.partial(attend_kernel, heads),
        out_shape=(
            jax.ShapeDtypeStruct((rows, width), bf16),
            jax.ShapeDtypeStruct((STATE_VECTORS, width), f32),
            jax.ShapeDtypeStruct((blocks, STATE_VECTORS, width), f32),
            jax.ShapeDtypeStruct((blocks, STATE_VECTORS, width), f32),
            jax.ShapeDtypeStruct((heads, rows), f32),
            jax.ShapeDtypeStruct((heads, blocks * STATE_VECTORS), f32),
        ),
        grid_spec=pltpu.PrefetchScalarGridSpec(
            num_scalar_prefetch=2,
            grid=(blocks,),
            in_specs=[
                pl.BlockSpec((BLOCK, width3), lambda b, _, at: (at[b], 0)),
                pl.BlockSpec((BLOCK, width3), lambda b, _, at: (at[jnp.maximum(b - 1, 0)], 0)),
                pl.BlockSpec((STATE_VECTORS, width), lambda b, _, at: (0, 0)),
                pl.BlockSpec((heads, DH, DH), lambda b, _, at: (0, 0, 0)),
                pl.BlockSpec((1, width), lambda b, _, at: (0, 0)),
                pl.BlockSpec((heads, QTILE, SPAN), lambda b, _, at: (0, 0, 0)),
            ],
            out_specs=(
                pl.BlockSpec((BLOCK, width), lambda b, _, at: (at[b], 0)),
                pl.BlockSpec((STATE_VECTORS, width), lambda b, _, at: (0, 0)),
                pl.BlockSpec((1, STATE_VECTORS, width), lambda b, _, at: (b, 0, 0)),
                pl.BlockSpec((1, STATE_VECTORS, width), lambda b, _, at: (b, 0, 0)),
                pl.BlockSpec((heads, BLOCK), lambda b, _, at: (0, b)),
                pl.BlockSpec((heads, STATE_VECTORS), lambda b, _, at: (0, b)),
            ),
            scratch_shapes=[pltpu.VMEM((STATE_VECTORS, width), f32)],
        ),
        compiler_params=pltpu.CompilerParams(vmem_limit_bytes=40 << 20),
        cost_estimate=pl.CostEstimate(
            flops=blocks * heads * 512 * 2400 * 128 * 4, bytes_accessed=16 << 20, transcendentals=10 << 20
        ),
        name="attend",
    )(length, order, qkv, qkv, init, state_query, forget, bias)


def attend_back_kernel(
    heads,
    blocks,
    length_ref,
    order_ref,
    cur_ref,
    prev_ref,
    dout_ref,
    out_ref,
    mem_ref,
    upd_ref,
    lse_ref,
    slse_ref,
    sgrad_ref,
    query_ref,
    forget_ref,
    bias_ref,
    dqkv_ref,
    dquery_ref,
    dforget_ref,
    near_ref,
    far_ref,
    dmem_ref,
    dnext_ref,
    dctx_ref,
):
    step = pl.program_id(0)
    block = blocks - 1 - step
    length = length_ref[0]
    width = heads * DH
    scale2 = SCALE * LOG2E

    @pl.when(step == 0)
    def _():
        dmem_ref[...] = sgrad_ref[...].astype(f32)
        dnext_ref[...] = jnp.zeros_like(dnext_ref)
        dquery_ref[...] = jnp.zeros_like(dquery_ref)
        dforget_ref[...] = jnp.zeros_like(dforget_ref)
        near_ref[...] = jnp.zeros_like(near_ref)
        far_ref[...] = jnp.zeros_like(far_ref)

    live_block = block * BLOCK < length
    refs = (prev_ref, cur_ref)
    for head in range(heads):
        own = slice(head * DH, (head + 1) * DH)
        key_cols = slice(width + head * DH, width + (head + 1) * DH)
        value_cols = slice(2 * width + head * DH, 2 * width + (head + 1) * DH)
        memory = mem_ref[0, :, own]
        update = upd_ref[0, :, own]
        low = memory.astype(bf16)
        forget = forget_ref[:, own]
        dmem = dmem_ref[:, own]
        dupd = jnp.where(live_block, (1.0 - forget) * dmem, 0.0).astype(bf16)
        moved = jnp.where(live_block, dmem * (memory - update), 0.0)
        dforget_ref[:, own] += jnp.sum(moved, axis=0, keepdims=True)
        dmem_new = jnp.where(live_block, forget * dmem, dmem)
        own_key = cur_ref[:, key_cols]
        own_value = cur_ref[:, value_cols]
        squeries = dot(low, query_ref[head]).astype(bf16)
        sdelta = jnp.sum((dupd.astype(f32) * update).T, axis=0, keepdims=True)
        slse = slse_ref[head : head + 1, :]
        dsquery = jnp.zeros((STATE_VECTORS, DH), f32)
        dkey = []
        dvalue = []
        for part in range(2 * STATE_VECTORS // QTILE):
            own_part = part >= STATE_VECTORS // QTILE
            lo = (part % (STATE_VECTORS // QTILE)) * QTILE
            keys = (own_key if own_part else low)[lo : lo + QTILE]
            values = (own_value if own_part else low)[lo : lo + QTILE]
            s = dot_t(keys, squeries) * scale2 - slse
            if own_part:
                position = block * BLOCK + lo + lax.broadcasted_iota(jnp.int32, (QTILE, 1), 0)
                s = jnp.where(position < length, s, -jnp.inf)
            p = jnp.exp2(s)
            dp = dot_t(values, dupd)
            ds = (p * (dp - sdelta)).astype(bf16)
            dvalue.append(dot(p.astype(bf16), dupd))
            dkey.append(dot(ds, squeries))
            dsquery += t_dot(ds, keys)
        half = STATE_VECTORS // QTILE
        dlow = [dvalue[i] + dkey[i] * SCALE for i in range(half)]
        dctx_ref[0, 0:BLOCK] = jnp.zeros((BLOCK, DH), f32)
        dctx_ref[1, 0:BLOCK] = jnp.zeros((BLOCK, DH), f32)
        for i in range(half):
            rows = slice(BLOCK + i * QTILE, BLOCK + (i + 1) * QTILE)
            old = slice(i * QTILE, (i + 1) * QTILE)
            dctx_ref[0, rows] = dkey[half + i] * SCALE + dnext_ref[0, old, own]
            dctx_ref[1, rows] = dvalue[half + i] + dnext_ref[1, old, own]
        dsq = (dsquery * SCALE).astype(bf16)
        dquery_ref[head] += t_dot(low, dsq)
        dmem_ref[:, own] = dmem_new + dot_t(dsq, query_ref[head])
        for tile in range(BLOCK // QTILE):
            rows = slice(tile * QTILE, (tile + 1) * QTILE)
            query = cur_ref[rows, own]
            dout = dout_ref[rows, own]
            lse = lse_ref[head : head + 1, rows]
            delta = jnp.sum((dout.astype(f32) * out_ref[rows, own].astype(f32)).T, axis=0, keepdims=True)
            dq = jnp.zeros((QTILE, DH), f32)
            for which, lo, hi, col in context_pieces(tile):
                for at in range(lo, hi, QTILE):
                    keys = refs[which][at : at + QTILE, key_cols]
                    values = refs[which][at : at + QTILE, value_cols]
                    band = col + at - lo
                    position = (block - 1 + which) * BLOCK + at + lax.broadcasted_iota(jnp.int32, (QTILE, 1), 0)
                    live = (position >= 0) & (position < length)
                    s = dot_t(keys, query) * scale2 + bias_ref[head, band : band + QTILE, :] - lse
                    p = jnp.exp2(jnp.where(live, s, -jnp.inf))
                    dp = dot_t(values, dout)
                    ds = (p * (dp - delta)).astype(bf16)
                    wide = ds.astype(f32)
                    if band + QTILE <= SPAN - NEAR:
                        far_ref[head] += functools.reduce(jnp.add, [wide[i : i + 8] for i in range(0, QTILE, 8)])
                    else:
                        edge = max(SPAN - NEAR - band, 0)
                        if edge:
                            far_ref[head] += functools.reduce(jnp.add, [wide[i : i + 8] for i in range(0, edge, 8)])
                        at_near = band + edge - (SPAN - NEAR)
                        near_ref[head, at_near : at_near + QTILE - edge] += wide[edge:]
                    into = slice(which * BLOCK + at, which * BLOCK + at + QTILE)
                    dctx_ref[1, into] += dot(p.astype(bf16), dout)
                    dctx_ref[0, into] += dot(ds, query) * SCALE
                    dq += t_dot(ds, keys)
            for part in range(half):
                keys = low[part * QTILE : (part + 1) * QTILE]
                s = dot_t(keys, query) * scale2 - lse
                p = jnp.exp2(s)
                dp = dot_t(keys, dout)
                ds = (p * (dp - delta)).astype(bf16)
                dlow[part] += dot(p.astype(bf16), dout) + dot(ds, query) * SCALE
                dq += t_dot(ds, keys)
            dqkv_ref[rows, own] = (dq * SCALE).astype(bf16)
        for part in range(half):
            dmem_ref[part * QTILE : (part + 1) * QTILE, own] += dlow[part]
        dnext_ref[0, :, own] = dctx_ref[0, 0:BLOCK]
        dnext_ref[1, :, own] = dctx_ref[1, 0:BLOCK]
        dqkv_ref[:, key_cols] = dctx_ref[0, BLOCK:].astype(bf16)
        dqkv_ref[:, value_cols] = dctx_ref[1, BLOCK:].astype(bf16)


def attend_back(qkv, dout, out, mem, upd, lse, slse, sgrad, length, state_query, forget, bias_t, heads, order):
    rows, width3 = qkv.shape
    width = heads * DH
    blocks = rows // BLOCK
    last = blocks - 1
    return pl.pallas_call(
        functools.partial(attend_back_kernel, heads, blocks),
        out_shape=(
            jax.ShapeDtypeStruct((rows, width3), bf16),
            jax.ShapeDtypeStruct((heads, DH, DH), f32),
            jax.ShapeDtypeStruct((1, width), f32),
            jax.ShapeDtypeStruct((heads, NEAR, QTILE), f32),
            jax.ShapeDtypeStruct((heads, 8, QTILE), f32),
        ),
        grid_spec=pltpu.PrefetchScalarGridSpec(
            num_scalar_prefetch=2,
            grid=(blocks,),
            in_specs=[
                pl.BlockSpec((BLOCK, width3), lambda b, _, at: (at[last - b], 0)),
                pl.BlockSpec((BLOCK, width3), lambda b, _, at: (at[jnp.maximum(last - b - 1, 0)], 0)),
                pl.BlockSpec((BLOCK, width), lambda b, _, at: (at[last - b], 0)),
                pl.BlockSpec((BLOCK, width), lambda b, _, at: (at[last - b], 0)),
                pl.BlockSpec((1, STATE_VECTORS, width), lambda b, _, at: (last - b, 0, 0)),
                pl.BlockSpec((1, STATE_VECTORS, width), lambda b, _, at: (last - b, 0, 0)),
                pl.BlockSpec((heads, BLOCK), lambda b, _, at: (0, last - b)),
                pl.BlockSpec((heads, STATE_VECTORS), lambda b, _, at: (0, last - b)),
                pl.BlockSpec((STATE_VECTORS, width), lambda b, _, at: (0, 0)),
                pl.BlockSpec((heads, DH, DH), lambda b, _, at: (0, 0, 0)),
                pl.BlockSpec((1, width), lambda b, _, at: (0, 0)),
                pl.BlockSpec((heads, SPAN, QTILE), lambda b, _, at: (0, 0, 0)),
            ],
            out_specs=(
                pl.BlockSpec((BLOCK, width3), lambda b, _, at: (at[last - b], 0)),
                pl.BlockSpec((heads, DH, DH), lambda b, _, at: (0, 0, 0)),
                pl.BlockSpec((1, width), lambda b, _, at: (0, 0)),
                pl.BlockSpec((heads, NEAR, QTILE), lambda b, _, at: (0, 0, 0)),
                pl.BlockSpec((heads, 8, QTILE), lambda b, _, at: (0, 0, 0)),
            ),
            scratch_shapes=[
                pltpu.VMEM((STATE_VECTORS, width), f32),
                pltpu.VMEM((2, BLOCK, width), f32),
                pltpu.VMEM((2, 2 * BLOCK, DH), f32),
            ],
        ),
        compiler_params=pltpu.CompilerParams(vmem_limit_bytes=40 << 20),
        cost_estimate=pl.CostEstimate(
            flops=blocks * heads * 512 * 2400 * 128 * 10, bytes_accessed=20 << 20, transcendentals=10 << 20
        ),
        name="attend_back",
    )(length, order, qkv, qkv, dout, out, mem, upd, lse, slse, sgrad, state_query, forget, bias_t)


def gather_kernel(seq, hi, lo, tok_ref, w_ref, gain_ref, toks_ref, ws_ref, gains_ref, here_sem, seq_send, seq_recv, far_send, far_recv, lo_send, lo_recv):
    me = lax.axis_index("seq")
    f = lax.axis_index("fsdp")
    z, y = f // lo, f % lo
    pairs = ((w_ref, ws_ref), (gain_ref, gains_ref))

    barrier = pltpu.get_barrier_semaphore()
    greeted = 0
    bit = 1
    while bit < seq:
        pl.semaphore_signal(barrier, inc=1, device_id={"seq": me ^ bit}, device_id_type=MESH)
        greeted += 1
        bit *= 2
    for target in (lax.rem(z + 1, hi) * lo + y, lax.rem(z + hi - 1, hi) * lo + y):
        pl.semaphore_signal(barrier, inc=1, device_id={"fsdp": target}, device_id_type=MESH)
        greeted += 1
    pl.semaphore_signal(barrier, inc=1, device_id={"fsdp": z * lo + 1 - y}, device_id_type=MESH)
    greeted += 1
    pl.semaphore_wait(barrier, greeted)

    own_copies = [pltpu.make_async_copy(tok_ref, toks_ref.at[0], here_sem.at[0])]
    own_copies += [pltpu.make_async_copy(a, b.at[f], here_sem.at[1 + i]) for i, (a, b) in enumerate(pairs)]
    for c in own_copies:
        c.start()

    def seq_copy(source, slot, bit):
        src = tok_ref if source == 0 else toks_ref.at[source]
        return pltpu.make_async_remote_copy(
            src_ref=src, dst_ref=toks_ref.at[slot], send_sem=seq_send.at[slot], recv_sem=seq_recv.at[slot],
            device_id={"seq": me ^ bit}, device_id_type=MESH,
        )

    def fsdp_copy(i, origin, own, target, send, recv):
        src, out = pairs[i]
        return pltpu.make_async_remote_copy(
            src_ref=src if own else out.at[origin], dst_ref=out.at[origin], send_sem=send, recv_sem=recv,
            device_id={"fsdp": target}, device_id_type=MESH,
        )

    def right(i, t):
        return fsdp_copy(i, (z - t) * lo + y, t == 0, (z + 1) * lo + y, far_send.at[i, 0, t], far_recv.at[i, 0, t])

    def left(i, t):
        return fsdp_copy(i, (z + t) * lo + y, t == 0, (z - 1) * lo + y, far_send.at[i, 1, t], far_recv.at[i, 1, t])

    def across(i, d):
        return fsdp_copy(i, (z + d) * lo + y, d == 0, z * lo + 1 - y, lo_send.at[i, d + hi - 1], lo_recv.at[i, d + hi - 1])

    both = range(len(pairs))
    seq_sends = []
    bits = []
    bit = seq // 2
    while bit > 1:
        bits.append(bit)
        bit //= 2
    have = [0]
    if bits:
        seq_sends.append(seq_copy(0, bits[0], bits[0]))
        seq_sends[-1].start()
    if seq > 1:
        seq_sends.append(seq_copy(0, 1, 1))
        seq_sends[-1].start()
    for i in both:
        pl.when(z + 1 < hi)(right(i, 0).start)
        pl.when(z >= 1)(left(i, 0).start)
        across(i, 0).start()
    for t in range(hi - 1):
        for i in both:
            @pl.when(z - 1 - t >= 0)
            def _():
                fsdp_copy(i, (z - 1 - t) * lo + y, False, f, far_send.at[i, 0, t], far_recv.at[i, 0, t]).wait_recv()
                across(i, -1 - t).start()
                if t + 1 < hi - 1:
                    pl.when(z + 1 < hi)(right(i, t + 1).start)

            @pl.when(z + 1 + t < hi)
            def _():
                fsdp_copy(i, (z + 1 + t) * lo + y, False, f, far_send.at[i, 1, t], far_recv.at[i, 1, t]).wait_recv()
                across(i, 1 + t).start()
                if t + 1 < hi - 1:
                    pl.when(z >= 1)(left(i, t + 1).start)
    for n, bit in enumerate(bits):
        if n:
            for j in have:
                seq_sends.append(seq_copy(j, j ^ bit, bit))
                seq_sends[-1].start()
        for j in list(have):
            seq_copy(0, j ^ bit, bit).wait_recv()
            seq_sends.append(seq_copy(j ^ bit, j ^ bit ^ 1, 1))
            seq_sends[-1].start()
        have += [j ^ bit for j in have]
    for j in have if seq > 1 else []:
        seq_copy(0, j ^ 1, 1).wait_recv()
    for i in both:
        for d in range(1 - hi, hi):
            @pl.when((z + d >= 0) & (z + d < hi))
            def _():
                fsdp_copy(i, (z + d) * lo + 1 - y, False, f, lo_send.at[i, d + hi - 1], lo_recv.at[i, d + hi - 1]).wait_recv()
                across(i, d).wait_send()
        for t in range(hi - 1):
            @pl.when((z + 1 < hi) & (z - t >= 0))
            def _():
                right(i, t).wait_send()

            @pl.when((z >= 1) & (z + t < hi))
            def _():
                left(i, t).wait_send()
    for c in seq_sends:
        c.wait_send()
    for c in own_copies:
        c.wait()


def gather_start(tokens, weights, gains, seq, fsdp):
    lo = 2
    hi = fsdp // lo
    anywhere = pl.BlockSpec(memory_space=pl.ANY)
    return pl.pallas_call(
        functools.partial(gather_kernel, seq, hi, lo),
        out_shape=(
            jax.ShapeDtypeStruct((seq,) + tokens.shape, tokens.dtype),
            jax.ShapeDtypeStruct((fsdp,) + weights.shape, weights.dtype),
            jax.ShapeDtypeStruct((fsdp,) + gains.shape, gains.dtype),
        ),
        in_specs=[anywhere] * 3,
        out_specs=(anywhere,) * 3,
        scratch_shapes=[
            pltpu.SemaphoreType.DMA((3,)),
            pltpu.SemaphoreType.DMA((seq,)),
            pltpu.SemaphoreType.DMA((seq,)),
            pltpu.SemaphoreType.DMA((2, 2, hi)),
            pltpu.SemaphoreType.DMA((2, 2, hi)),
            pltpu.SemaphoreType.DMA((2, 2 * hi)),
            pltpu.SemaphoreType.DMA((2, 2 * hi)),
        ],
        compiler_params=pltpu.CompilerParams(collective_id=0, has_side_effects=True),
        name="gather_start",
    )(tokens, weights, gains)


def swap(value, bit):
    count = lax.axis_size("seq")
    return lax.ppermute(value, "seq", [(i, i ^ bit) for i in range(count)])


def seq_bits():
    count = lax.axis_size("seq")
    return [1 << i for i in reversed(range(1, count.bit_length() - 1))]


def seq_gather(value):
    chunks = {0: value}
    for bit in seq_bits():
        for j in list(chunks):
            chunks[j ^ bit] = swap(chunks[j], bit)
    for j in list(chunks):
        chunks[j ^ 1] = swap(chunks[j], 1)
    return [chunks[j] for j in range(len(chunks))]


def seq_reduce(parts):
    count = len(parts)
    parts = dict(enumerate(parts))
    for j in range(count - 2, -1, -2):
        parts[j] = parts[j].astype(f32) + swap(parts.pop(j ^ 1).astype(bf16), 1).astype(f32)
    for bit in reversed(seq_bits()):
        keep = [j for j in parts if not j & bit]
        for j in sorted(keep, reverse=True):
            parts[j] = parts[j] + swap(parts.pop(j ^ bit).astype(bf16), bit).astype(f32)
    return parts[0]


def bias_table_grad(near, far):
    distance = tile_distance().T[SPAN - NEAR :]
    bucket = np.where((distance >= 0) & (distance < BLOCK), bucket_of(np.clip(distance, 0, BLOCK)), BUCKETS)
    bucket = jnp.asarray(bucket.astype(np.int32))
    columns = [jnp.sum(jnp.where((bucket == i)[None], near, 0.0), axis=(1, 2)) for i in range(BUCKETS)]
    columns[-1] = columns[-1] + jnp.sum(far, axis=(1, 2))
    return jnp.stack(columns, axis=1)


def inverse_rms(values):
    return lax.rsqrt(jnp.mean(values * values, axis=-1, keepdims=True) + EPSILON)


def norm_back(values, gain, rho, grad):
    scaled = gain * grad
    mean = jnp.mean(values * scaled, axis=-1, keepdims=True)
    return rho * scaled - values * (rho * rho * rho * mean), jnp.sum(grad * values * rho, axis=0)


def body(
    tokens,
    lengths,
    state_init,
    w_qkv,
    w_out,
    w_up,
    w_down,
    norm_attn,
    norm_mlp,
    rel_bias,
    state_query,
    gate_bias,
    out_grad,
    state_grad,
):
    seq_count = lax.axis_size("seq")
    fsdp_count = lax.axis_size("fsdp")
    seq_at = lax.axis_index("seq")
    heads = H // seq_count
    width = heads * DH
    tok_rows, dim = tokens.shape[1:]
    rows = tok_rows * seq_count
    hidden_all = w_up.shape[1]
    share = hidden_all // (seq_count * fsdp_count)

    own_qkv = lax.dynamic_slice_in_dim(
        w_qkv.reshape(w_qkv.shape[0], 3, seq_count, width), seq_at, 1, axis=2
    ).reshape(w_qkv.shape[0], 3 * width)
    own_up = lax.dynamic_slice_in_dim(
        w_up.reshape(w_up.shape[0], fsdp_count, seq_count, share), seq_at, 1, axis=2
    ).reshape(w_up.shape[0], fsdp_count * share)
    own_down = lax.dynamic_slice_in_dim(w_down, seq_at * share, share, axis=0)
    out_w = lax.all_gather(w_out, "fsdp", axis=0, tiled=True)
    up_w = lax.all_gather(own_up, "fsdp", axis=0, tiled=True)
    down_w = lax.all_gather(own_down, "fsdp", axis=0, tiled=True)
    all_tokens, qkv_w, gains = gather_start(
        tokens[0], own_qkv, jnp.stack([norm_attn, norm_mlp]), seq_count, fsdp_count
    )
    qkv_w = qkv_w.reshape(dim, 3 * width)
    gains = jnp.swapaxes(gains, 0, 1).reshape(2, dim).astype(f32)
    gain_attn, gain_mlp = gains[0], gains[1]
    all_grad = jnp.concatenate(seq_gather(out_grad[0]), axis=0)

    bias = tile_bias(rel_bias)
    bias_t = jnp.swapaxes(bias, 1, 2)
    forget = jax.nn.sigmoid(gate_bias)
    forget_row = forget.reshape(1, width)
    chunk_ids = jnp.arange(seq_count, dtype=jnp.int32)
    order = chunk_ids ^ seq_at

    inputs = all_tokens.reshape(rows, dim).astype(f32)
    normed = (inputs * inverse_rms(inputs) * gain_attn).astype(bf16)
    qkv = dot(normed, qkv_w).astype(bf16)
    attended, final_memory, mem, upd, lse, slse = attend(
        qkv, state_init[0], lengths, state_query, forget_row, bias, heads, order
    )

    from_heads = seq_gather(attended)
    columns = []
    for k in range(seq_count):
        blocks = from_heads[k].reshape(seq_count, tok_rows, width)
        columns.append(jnp.concatenate([blocks[j ^ k] for j in range(seq_count)], axis=0))
    all_attended = jnp.concatenate(columns, axis=1)
    out_w = out_w.reshape(seq_count, width, dim)
    own_out = lax.dynamic_slice_in_dim(out_w, seq_at, 1, axis=0)[0]
    out_w = jnp.concatenate(
        [lax.dynamic_slice_in_dim(out_w, seq_at ^ k, 1, axis=0)[0] for k in range(seq_count)], axis=0
    )
    mid = inputs + dot(all_attended, out_w)
    rho_mid = inverse_rms(mid)
    normed_mid = (mid * rho_mid * gain_mlp).astype(bf16)
    positions = (order[:, None] * tok_rows + jnp.arange(tok_rows, dtype=jnp.int32)).reshape(rows)
    live = (positions < lengths[0]).astype(bf16)[:, None]
    grad_low = all_grad * live
    pre = dot(normed_mid, up_w)
    hidden, gelu_pull = jax.vjp(lambda v: jax.nn.gelu(v, approximate=False), pre)
    hidden = hidden.astype(bf16)
    dpre = gelu_pull(dot_t(grad_low, down_w))[0].astype(bf16)

    def chunk(value, j):
        return value[j * tok_rows : (j + 1) * tok_rows]

    dnormed_mid = seq_reduce([dot_t(chunk(dpre, j), up_w) for j in range(seq_count)])
    down_grad = t_dot(hidden, grad_low)
    up_grad = t_dot(normed_mid, dpre)
    mlp_out = seq_reduce([dot(chunk(hidden, j), down_w) for j in range(seq_count)])

    mid_here = chunk(mid, 0)
    live_here = chunk(live, 0).astype(f32)
    output = (live_here * (mid_here + mlp_out)).astype(bf16)[None]
    grad_here = out_grad[0].astype(f32) * live_here
    through, mlp_gain_grad = norm_back(mid_here, gain_mlp, inverse_rms(mid_here), dnormed_mid)
    dmid = grad_here + through
    dbranch = jnp.concatenate(seq_gather(dmid.astype(bf16)), axis=0)
    dattended = dot_t(dbranch, own_out).astype(bf16)
    out_w_grad = t_dot(attended, dbranch)

    dqkv, dquery, dforget, near, far = attend_back(
        qkv, dattended, attended, mem, upd, lse, slse, state_grad[0], lengths, state_query, forget_row, bias_t, heads, order
    )
    dnormed = seq_reduce([dot_t(chunk(dqkv, j), qkv_w) for j in range(seq_count)])
    qkv_grad = t_dot(normed, dqkv)
    inputs_here = tokens[0].astype(f32)
    through, attn_gain_grad = norm_back(inputs_here, gain_attn, inverse_rms(inputs_here), dnormed)
    tokens_grad = (dmid + through)[None]

    grad_gate = dforget.reshape(heads, DH) * forget * (1.0 - forget)
    grad_table = bias_table_grad(near, far)
    small = jnp.concatenate(
        [dquery.reshape(-1), grad_gate.reshape(-1), grad_table.reshape(-1)]
    )
    small = lax.psum(small, "fsdp")
    cut = heads * DH * DH
    dquery = small[:cut].reshape(heads, DH, DH)
    grad_gate = small[cut : cut + heads * DH].reshape(heads, DH)
    grad_table = small[cut + heads * DH :].reshape(heads, BUCKETS)

    def spread(term):
        return lax.psum_scatter(term.astype(bf16), "fsdp", scatter_dimension=0, tiled=True)

    def exchange(term):
        return lax.all_to_all(term, "seq", split_axis=0, concat_axis=0, tiled=True).astype(f32)

    piece = dim // (seq_count * fsdp_count)

    def by_rows(grad):
        columns = grad.shape[1]
        grad = jnp.swapaxes(grad.reshape(seq_count, fsdp_count, piece, columns), 0, 1)
        return spread(grad.reshape(dim, columns)).reshape(seq_count, piece, columns)

    up_part = exchange(by_rows(up_grad)).reshape(seq_count, piece, fsdp_count, share)
    up_part = jnp.transpose(up_part, (1, 2, 0, 3)).reshape(piece, hidden_all)
    out_part = spread(out_w_grad).astype(f32)
    span = fsdp_count // seq_count
    down_low = down_grad.astype(bf16).reshape(seq_count, span, share, dim)
    moved = [lax.dynamic_slice_in_dim(down_low, seq_at, 1, axis=0)]
    for k in range(1, seq_count):
        moved.append(swap(lax.dynamic_slice_in_dim(down_low, seq_at ^ k, 1, axis=0), k))
    moved = jnp.concatenate(moved, axis=0)
    moved = [lax.dynamic_slice_in_dim(moved, seq_at ^ k, 1, axis=0) for k in range(seq_count)]
    down_part = jnp.swapaxes(jnp.concatenate(moved, axis=0), 0, 1).reshape(fsdp_count * share, dim)
    down_part = spread(down_part).astype(f32)
    qkv_part = exchange(by_rows(qkv_grad)).reshape(seq_count, piece, 3, width)
    qkv_part = jnp.transpose(qkv_part, (1, 2, 0, 3)).reshape(piece, 3 * H * DH)
    attn_gain_grad, mlp_gain_grad = jnp.split(
        lax.psum_scatter(
            jnp.stack([attn_gain_grad, mlp_gain_grad]), ("seq", "fsdp"), scatter_dimension=1, tiled=True
        ),
        2,
    )
    return (
        output,
        final_memory[None],
        tokens_grad,
        qkv_part,
        out_part,
        up_part,
        down_part,
        attn_gain_grad[0],
        mlp_gain_grad[0],
        grad_table,
        dquery,
        grad_gate,
    )


def solution(mesh):
    placed = (
        P("fsdp", "seq", None),
        P("fsdp"),
        P("fsdp", None, "seq"),
        P("fsdp", None),
        P("fsdp", None),
        P("fsdp", None),
        P("fsdp", None),
        P("fsdp"),
        P("fsdp"),
        P("seq", None),
        P("seq", None, None),
        P("seq", None),
        P("fsdp", "seq", None),
        P("fsdp", None, "seq"),
    )
    return jax.shard_map(
        body,
        mesh=mesh,
        in_specs=placed,
        out_specs=(
            P("fsdp", "seq", None),
            P("fsdp", None, "seq"),
            P("fsdp", "seq", None),
            P(("seq", "fsdp"), None),
            P(("seq", "fsdp"), None),
            P(("seq", "fsdp"), None),
            P(("seq", "fsdp"), None),
            P(("seq", "fsdp")),
            P(("seq", "fsdp")),
            P("seq", None),
            P("seq", None, None),
            P("seq", None),
        ),
        check_vma=False,
    )
```

```python
import functools
import math

import jax
import jax.numpy as jnp
import numpy as np
from jax import lax
from jax.experimental import pallas as pl
from jax.experimental.pallas import tpu as pltpu
from jax.sharding import PartitionSpec as P

H = 8
DH = 128
BLOCK = 512
STATE_VECTORS = 512
QTILE = 256
SPAN = BLOCK + QTILE

EPSILON = 1e-06
BUCKET_EDGES = (19, 21, 24, 27, 31, 35, 40, 46, 52, 59, 67, 77, 87, 99, 113)
BUCKETS = 32
LOG2E = math.log2(math.e)
SCALE = DH ** (-0.5)
NEAR = 384

f32 = jnp.float32
bf16 = jnp.bfloat16
MESH = pl.DeviceIdType.MESH


def bucket_of(distance):
    return np.minimum(distance, 16) + (distance[..., None] >= np.array(BUCKET_EDGES)).sum(-1)


def tile_distance():
    rows = np.arange(QTILE)[:, None]
    cols = np.arange(SPAN)[None, :]
    return rows + BLOCK - cols


def tile_bias(table):
    distance = jnp.arange(QTILE, dtype=jnp.int32)[:, None] + BLOCK - jnp.arange(SPAN, dtype=jnp.int32)[None, :]
    clipped = jnp.clip(distance, 0, BLOCK)
    edges = jnp.array(BUCKET_EDGES, dtype=jnp.int32)
    bucket = jnp.minimum(clipped, 16) + jnp.sum((clipped[:, :, None] >= edges).astype(jnp.int32), axis=-1)
    total = jnp.zeros((table.shape[0],) + bucket.shape, f32)
    for bucket_id in range(BUCKETS):
        total = jnp.where((bucket == bucket_id)[None], table[:, bucket_id][:, None, None], total)
    window = (distance >= 0) & (distance < BLOCK)
    return jnp.where(window[None], total * LOG2E, -jnp.inf)


def dot(a, b):
    return jnp.dot(a, b, preferred_element_type=f32)


def dot_t(a, b):
    return lax.dot_general(a, b, (((1,), (1,)), ((), ())), preferred_element_type=f32)


def t_dot(a, b):
    return lax.dot_general(a, b, (((0,), (0,)), ((), ())), preferred_element_type=f32)


def to_row(column):
    wide = jnp.broadcast_to(column, (column.shape[0], 128))
    return wide.T[0:1, :]


def context_pieces(tile):
    start = tile * QTILE
    pieces = []
    if start < BLOCK:
        pieces.append((0, start, BLOCK, 0))
    pieces.append((1, 0, start + QTILE, BLOCK - start))
    return pieces


def softmax_parts(scores):
    top = functools.reduce(jnp.maximum, [jnp.max(s, axis=-1, keepdims=True) for s in scores])
    raised = [jnp.exp2(s - top) for s in scores]
    total = functools.reduce(jnp.add, [jnp.sum(e, axis=-1, keepdims=True) for e in raised])
    return raised, total, top + jnp.log2(total)


def attend_kernel(
    heads,
    length_ref,
    order_ref,
    cur_ref,
    prev_ref,
    init_ref,
    query_ref,
    forget_ref,
    bias_ref,
    att_ref,
    final_ref,
    mem_ref,
    upd_ref,
    lse_ref,
    slse_ref,
    memory_ref,
):
    block = pl.program_id(0)
    length = length_ref[0]
    width = heads * DH
    scale2 = SCALE * LOG2E

    @pl.when(block == 0)
    def _():
        memory_ref[...] = init_ref[...].astype(f32)

    live_block = block * BLOCK < length
    for head in range(heads):
        own = slice(head * DH, (head + 1) * DH)
        memory = memory_ref[:, own]
        low = memory.astype(bf16)
        mem_ref[0, :, own] = memory
        refs = (prev_ref, cur_ref)
        key_cols = slice(width + head * DH, width + (head + 1) * DH)
        value_cols = slice(2 * width + head * DH, 2 * width + (head + 1) * DH)
        for tile in range(BLOCK // QTILE):
            rows = slice(tile * QTILE, (tile + 1) * QTILE)
            query = cur_ref[rows, own]
            scores, values = [], []
            for which, lo, hi, col in context_pieces(tile):
                s = dot_t(query, refs[which][lo:hi, key_cols])
                position = (block - 1 + which) * BLOCK + lo + lax.broadcasted_iota(jnp.int32, (1, hi - lo), 1)
                live = (position >= 0) & (position < length)
                s = s * scale2 + bias_ref[head, :, col : col + hi - lo]
                scores.append(jnp.where(live, s, -jnp.inf))
                values.append(refs[which][lo:hi, value_cols])
            scores.append(dot_t(query, low) * scale2)
            values.append(low)
            raised, total, lse = softmax_parts(scores)
            out = functools.reduce(jnp.add, [dot(e.astype(bf16), v) for e, v in zip(raised, values)])
            att_ref[rows, own] = (out / total).astype(bf16)
            lse_ref[head : head + 1, rows] = to_row(lse)
        own_key = cur_ref[:, key_cols]
        own_value = cur_ref[:, value_cols]
        squeries = dot(low, query_ref[head]).astype(bf16)
        position = block * BLOCK + lax.broadcasted_iota(jnp.int32, (1, BLOCK), 1)
        for tile in range(STATE_VECTORS // QTILE):
            rows = slice(tile * QTILE, (tile + 1) * QTILE)
            squery = squeries[rows]
            scores = [
                dot_t(squery, low) * scale2,
                jnp.where(position < length, dot_t(squery, own_key) * scale2, -jnp.inf),
            ]
            raised, total, lse = softmax_parts(scores)
            update = dot(raised[0].astype(bf16), low) + dot(raised[1].astype(bf16), own_value)
            update = update / total
            upd_ref[0, rows, own] = update
            slse_ref[head : head + 1, rows] = to_row(lse)
            forget = forget_ref[:, own]
            old = memory[rows]
            memory_ref[rows, own] = jnp.where(live_block, forget * old + (1.0 - forget) * update, old)
    final_ref[...] = memory_ref[...]


def attend(qkv, init, length, state_query, forget, bias, heads, order):
    rows, width3 = qkv.shape
    width = heads * DH
    blocks = rows // BLOCK
    return pl.pallas_call(
        functools.partial(attend_kernel, heads),
        out_shape=(
            jax.ShapeDtypeStruct((rows, width), bf16),
            jax.ShapeDtypeStruct((STATE_VECTORS, width), f32),
            jax.ShapeDtypeStruct((blocks, STATE_VECTORS, width), f32),
            jax.ShapeDtypeStruct((blocks, STATE_VECTORS, width), f32),
            jax.ShapeDtypeStruct((heads, rows), f32),
            jax.ShapeDtypeStruct((heads, blocks * STATE_VECTORS), f32),
        ),
        grid_spec=pltpu.PrefetchScalarGridSpec(
            num_scalar_prefetch=2,
            grid=(blocks,),
            in_specs=[
                pl.BlockSpec((BLOCK, width3), lambda b, _, at: (at[b], 0)),
                pl.BlockSpec((BLOCK, width3), lambda b, _, at: (at[jnp.maximum(b - 1, 0)], 0)),
                pl.BlockSpec((STATE_VECTORS, width), lambda b, _, at: (0, 0)),
                pl.BlockSpec((heads, DH, DH), lambda b, _, at: (0, 0, 0)),
                pl.BlockSpec((1, width), lambda b, _, at: (0, 0)),
                pl.BlockSpec((heads, QTILE, SPAN), lambda b, _, at: (0, 0, 0)),
            ],
            out_specs=(
                pl.BlockSpec((BLOCK, width), lambda b, _, at: (at[b], 0)),
                pl.BlockSpec((STATE_VECTORS, width), lambda b, _, at: (0, 0)),
                pl.BlockSpec((1, STATE_VECTORS, width), lambda b, _, at: (b, 0, 0)),
                pl.BlockSpec((1, STATE_VECTORS, width), lambda b, _, at: (b, 0, 0)),
                pl.BlockSpec((heads, BLOCK), lambda b, _, at: (0, b)),
                pl.BlockSpec((heads, STATE_VECTORS), lambda b, _, at: (0, b)),
            ),
            scratch_shapes=[pltpu.VMEM((STATE_VECTORS, width), f32)],
        ),
        compiler_params=pltpu.CompilerParams(vmem_limit_bytes=40 << 20),
        cost_estimate=pl.CostEstimate(
            flops=blocks * heads * 512 * 2400 * 128 * 4, bytes_accessed=16 << 20, transcendentals=10 << 20
        ),
        name="attend",
    )(length, order, qkv, qkv, init, state_query, forget, bias)


def attend_back_kernel(
    heads,
    blocks,
    length_ref,
    order_ref,
    cur_ref,
    prev_ref,
    dout_ref,
    out_ref,
    mem_ref,
    upd_ref,
    lse_ref,
    slse_ref,
    sgrad_ref,
    query_ref,
    forget_ref,
    bias_ref,
    dqkv_ref,
    dquery_ref,
    dforget_ref,
    near_ref,
    far_ref,
    dmem_ref,
    dnext_ref,
    dctx_ref,
):
    step = pl.program_id(0)
    block = blocks - 1 - step
    length = length_ref[0]
    width = heads * DH
    scale2 = SCALE * LOG2E

    @pl.when(step == 0)
    def _():
        dmem_ref[...] = sgrad_ref[...].astype(f32)
        dnext_ref[...] = jnp.zeros_like(dnext_ref)
        dquery_ref[...] = jnp.zeros_like(dquery_ref)
        dforget_ref[...] = jnp.zeros_like(dforget_ref)
        near_ref[...] = jnp.zeros_like(near_ref)
        far_ref[...] = jnp.zeros_like(far_ref)

    live_block = block * BLOCK < length
    refs = (prev_ref, cur_ref)
    for head in range(heads):
        own = slice(head * DH, (head + 1) * DH)
        key_cols = slice(width + head * DH, width + (head + 1) * DH)
        value_cols = slice(2 * width + head * DH, 2 * width + (head + 1) * DH)
        memory = mem_ref[0, :, own]
        update = upd_ref[0, :, own]
        low = memory.astype(bf16)
        forget = forget_ref[:, own]
        dmem = dmem_ref[:, own]
        dupd = jnp.where(live_block, (1.0 - forget) * dmem, 0.0).astype(bf16)
        moved = jnp.where(live_block, dmem * (memory - update), 0.0)
        dforget_ref[:, own] += jnp.sum(moved, axis=0, keepdims=True)
        dmem_new = jnp.where(live_block, forget * dmem, dmem)
        own_key = cur_ref[:, key_cols]
        own_value = cur_ref[:, value_cols]
        squeries = dot(low, query_ref[head]).astype(bf16)
        sdelta = jnp.sum((dupd.astype(f32) * update).T, axis=0, keepdims=True)
        slse = slse_ref[head : head + 1, :]
        dsquery = jnp.zeros((STATE_VECTORS, DH), f32)
        dkey = []
        dvalue = []
        for part in range(2 * STATE_VECTORS // QTILE):
            own_part = part >= STATE_VECTORS // QTILE
            lo = (part % (STATE_VECTORS // QTILE)) * QTILE
            keys = (own_key if own_part else low)[lo : lo + QTILE]
            values = (own_value if own_part else low)[lo : lo + QTILE]
            s = dot_t(keys, squeries) * scale2 - slse
            if own_part:
                position = block * BLOCK + lo + lax.broadcasted_iota(jnp.int32, (QTILE, 1), 0)
                s = jnp.where(position < length, s, -jnp.inf)
            p = jnp.exp2(s)
            dp = dot_t(values, dupd)
            ds = (p * (dp - sdelta)).astype(bf16)
            dvalue.append(dot(p.astype(bf16), dupd))
            dkey.append(dot(ds, squeries))
            dsquery += t_dot(ds, keys)
        half = STATE_VECTORS // QTILE
        dlow = [dvalue[i] + dkey[i] * SCALE for i in range(half)]
        dctx_ref[0, 0:BLOCK] = jnp.zeros((BLOCK, DH), f32)
        dctx_ref[1, 0:BLOCK] = jnp.zeros((BLOCK, DH), f32)
        for i in range(half):
            rows = slice(BLOCK + i * QTILE, BLOCK + (i + 1) * QTILE)
            old = slice(i * QTILE, (i + 1) * QTILE)
            dctx_ref[0, rows] = dkey[half + i] * SCALE + dnext_ref[0, old, own]
            dctx_ref[1, rows] = dvalue[half + i] + dnext_ref[1, old, own]
        dsq = (dsquery * SCALE).astype(bf16)
        dquery_ref[head] += t_dot(low, dsq)
        dmem_ref[:, own] = dmem_new + dot_t(dsq, query_ref[head])
        for tile in range(BLOCK // QTILE):
            rows = slice(tile * QTILE, (tile + 1) * QTILE)
            query = cur_ref[rows, own]
            dout = dout_ref[rows, own]
            lse = lse_ref[head : head + 1, rows]
            delta = jnp.sum((dout.astype(f32) * out_ref[rows, own].astype(f32)).T, axis=0, keepdims=True)
            dq = jnp.zeros((QTILE, DH), f32)
            for which, lo, hi, col in context_pieces(tile):
                for at in range(lo, hi, QTILE):
                    keys = refs[which][at : at + QTILE, key_cols]
                    values = refs[which][at : at + QTILE, value_cols]
                    band = col + at - lo
                    position = (block - 1 + which) * BLOCK + at + lax.broadcasted_iota(jnp.int32, (QTILE, 1), 0)
                    live = (position >= 0) & (position < length)
                    s = dot_t(keys, query) * scale2 + bias_ref[head, band : band + QTILE, :] - lse
                    p = jnp.exp2(jnp.where(live, s, -jnp.inf))
                    dp = dot_t(values, dout)
                    ds = (p * (dp - delta)).astype(bf16)
                    wide = ds.astype(f32)
                    if band + QTILE <= SPAN - NEAR:
                        far_ref[head] += functools.reduce(jnp.add, [wide[i : i + 8] for i in range(0, QTILE, 8)])
                    else:
                        edge = max(SPAN - NEAR - band, 0)
                        if edge:
                            far_ref[head] += functools.reduce(jnp.add, [wide[i : i + 8] for i in range(0, edge, 8)])
                        at_near = band + edge - (SPAN - NEAR)
                        near_ref[head, at_near : at_near + QTILE - edge] += wide[edge:]
                    into = slice(which * BLOCK + at, which * BLOCK + at + QTILE)
                    dctx_ref[1, into] += dot(p.astype(bf16), dout)
                    dctx_ref[0, into] += dot(ds, query) * SCALE
                    dq += t_dot(ds, keys)
            for part in range(half):
                keys = low[part * QTILE : (part + 1) * QTILE]
                s = dot_t(keys, query) * scale2 - lse
                p = jnp.exp2(s)
                dp = dot_t(keys, dout)
                ds = (p * (dp - delta)).astype(bf16)
                dlow[part] += dot(p.astype(bf16), dout) + dot(ds, query) * SCALE
                dq += t_dot(ds, keys)
            dqkv_ref[rows, own] = (dq * SCALE).astype(bf16)
        for part in range(half):
            dmem_ref[part * QTILE : (part + 1) * QTILE, own] += dlow[part]
        dnext_ref[0, :, own] = dctx_ref[0, 0:BLOCK]
        dnext_ref[1, :, own] = dctx_ref[1, 0:BLOCK]
        dqkv_ref[:, key_cols] = dctx_ref[0, BLOCK:].astype(bf16)
        dqkv_ref[:, value_cols] = dctx_ref[1, BLOCK:].astype(bf16)


def attend_back(qkv, dout, out, mem, upd, lse, slse, sgrad, length, state_query, forget, bias_t, heads, order):
    rows, width3 = qkv.shape
    width = heads * DH
    blocks = rows // BLOCK
    last = blocks - 1
    return pl.pallas_call(
        functools.partial(attend_back_kernel, heads, blocks),
        out_shape=(
            jax.ShapeDtypeStruct((rows, width3), bf16),
            jax.ShapeDtypeStruct((heads, DH, DH), f32),
            jax.ShapeDtypeStruct((1, width), f32),
            jax.ShapeDtypeStruct((heads, NEAR, QTILE), f32),
            jax.ShapeDtypeStruct((heads, 8, QTILE), f32),
        ),
        grid_spec=pltpu.PrefetchScalarGridSpec(
            num_scalar_prefetch=2,
            grid=(blocks,),
            in_specs=[
                pl.BlockSpec((BLOCK, width3), lambda b, _, at: (at[last - b], 0)),
                pl.BlockSpec((BLOCK, width3), lambda b, _, at: (at[jnp.maximum(last - b - 1, 0)], 0)),
                pl.BlockSpec((BLOCK, width), lambda b, _, at: (at[last - b], 0)),
                pl.BlockSpec((BLOCK, width), lambda b, _, at: (at[last - b], 0)),
                pl.BlockSpec((1, STATE_VECTORS, width), lambda b, _, at: (last - b, 0, 0)),
                pl.BlockSpec((1, STATE_VECTORS, width), lambda b, _, at: (last - b, 0, 0)),
                pl.BlockSpec((heads, BLOCK), lambda b, _, at: (0, last - b)),
                pl.BlockSpec((heads, STATE_VECTORS), lambda b, _, at: (0, last - b)),
                pl.BlockSpec((STATE_VECTORS, width), lambda b, _, at: (0, 0)),
                pl.BlockSpec((heads, DH, DH), lambda b, _, at: (0, 0, 0)),
                pl.BlockSpec((1, width), lambda b, _, at: (0, 0)),
                pl.BlockSpec((heads, SPAN, QTILE), lambda b, _, at: (0, 0, 0)),
            ],
            out_specs=(
                pl.BlockSpec((BLOCK, width3), lambda b, _, at: (at[last - b], 0)),
                pl.BlockSpec((heads, DH, DH), lambda b, _, at: (0, 0, 0)),
                pl.BlockSpec((1, width), lambda b, _, at: (0, 0)),
                pl.BlockSpec((heads, NEAR, QTILE), lambda b, _, at: (0, 0, 0)),
                pl.BlockSpec((heads, 8, QTILE), lambda b, _, at: (0, 0, 0)),
            ),
            scratch_shapes=[
                pltpu.VMEM((STATE_VECTORS, width), f32),
                pltpu.VMEM((2, BLOCK, width), f32),
                pltpu.VMEM((2, 2 * BLOCK, DH), f32),
            ],
        ),
        compiler_params=pltpu.CompilerParams(vmem_limit_bytes=40 << 20),
        cost_estimate=pl.CostEstimate(
            flops=blocks * heads * 512 * 2400 * 128 * 10, bytes_accessed=20 << 20, transcendentals=10 << 20
        ),
        name="attend_back",
    )(length, order, qkv, qkv, dout, out, mem, upd, lse, slse, sgrad, state_query, forget, bias_t)


def gather_kernel(seq, hi, lo, tok_ref, w_ref, gain_ref, out_ref, toks_ref, ws_ref, gains_ref, outs_ref, here_sem, seq_send, seq_recv, far_send, far_recv, lo_send, lo_recv):
    me = lax.axis_index("seq")
    f = lax.axis_index("fsdp")
    z, y = f // lo, f % lo
    pairs = ((w_ref, ws_ref), (gain_ref, gains_ref), (out_ref, outs_ref))

    barrier = pltpu.get_barrier_semaphore()
    greeted = 0
    bit = 1
    while bit < seq:
        pl.semaphore_signal(barrier, inc=1, device_id={"seq": me ^ bit}, device_id_type=MESH)
        greeted += 1
        bit *= 2
    for target in (lax.rem(z + 1, hi) * lo + y, lax.rem(z + hi - 1, hi) * lo + y):
        pl.semaphore_signal(barrier, inc=1, device_id={"fsdp": target}, device_id_type=MESH)
        greeted += 1
    pl.semaphore_signal(barrier, inc=1, device_id={"fsdp": z * lo + 1 - y}, device_id_type=MESH)
    greeted += 1
    pl.semaphore_wait(barrier, greeted)

    own_copies = [pltpu.make_async_copy(tok_ref, toks_ref.at[0], here_sem.at[0])]
    own_copies += [pltpu.make_async_copy(a, b.at[f], here_sem.at[1 + i]) for i, (a, b) in enumerate(pairs)]
    for c in own_copies:
        c.start()

    def seq_copy(source, slot, bit):
        src = tok_ref if source == 0 else toks_ref.at[source]
        return pltpu.make_async_remote_copy(
            src_ref=src, dst_ref=toks_ref.at[slot], send_sem=seq_send.at[slot], recv_sem=seq_recv.at[slot],
            device_id={"seq": me ^ bit}, device_id_type=MESH,
        )

    def fsdp_copy(i, origin, own, target, send, recv):
        src, out = pairs[i]
        return pltpu.make_async_remote_copy(
            src_ref=src if own else out.at[origin], dst_ref=out.at[origin], send_sem=send, recv_sem=recv,
            device_id={"fsdp": target}, device_id_type=MESH,
        )

    def right(i, t):
        return fsdp_copy(i, (z - t) * lo + y, t == 0, (z + 1) * lo + y, far_send.at[i, 0, t], far_recv.at[i, 0, t])

    def left(i, t):
        return fsdp_copy(i, (z + t) * lo + y, t == 0, (z - 1) * lo + y, far_send.at[i, 1, t], far_recv.at[i, 1, t])

    def across(i, d):
        return fsdp_copy(i, (z + d) * lo + y, d == 0, z * lo + 1 - y, lo_send.at[i, d + hi - 1], lo_recv.at[i, d + hi - 1])

    both = range(len(pairs))
    seq_sends = []
    bits = []
    bit = seq // 2
    while bit > 1:
        bits.append(bit)
        bit //= 2
    have = [0]
    if bits:
        seq_sends.append(seq_copy(0, bits[0], bits[0]))
        seq_sends[-1].start()
    if seq > 1:
        seq_sends.append(seq_copy(0, 1, 1))
        seq_sends[-1].start()
    for i in both:
        pl.when(z + 1 < hi)(right(i, 0).start)
        pl.when(z >= 1)(left(i, 0).start)
        across(i, 0).start()
    for t in range(hi - 1):
        for i in both:
            @pl.when(z - 1 - t >= 0)
            def _():
                fsdp_copy(i, (z - 1 - t) * lo + y, False, f, far_send.at[i, 0, t], far_recv.at[i, 0, t]).wait_recv()
                across(i, -1 - t).start()
                if t + 1 < hi - 1:
                    pl.when(z + 1 < hi)(right(i, t + 1).start)

            @pl.when(z + 1 + t < hi)
            def _():
                fsdp_copy(i, (z + 1 + t) * lo + y, False, f, far_send.at[i, 1, t], far_recv.at[i, 1, t]).wait_recv()
                across(i, 1 + t).start()
                if t + 1 < hi - 1:
                    pl.when(z >= 1)(left(i, t + 1).start)
    for n, bit in enumerate(bits):
        if n:
            for j in have:
                seq_sends.append(seq_copy(j, j ^ bit, bit))
                seq_sends[-1].start()
        for j in list(have):
            seq_copy(0, j ^ bit, bit).wait_recv()
            seq_sends.append(seq_copy(j ^ bit, j ^ bit ^ 1, 1))
            seq_sends[-1].start()
        have += [j ^ bit for j in have]
    for j in have if seq > 1 else []:
        seq_copy(0, j ^ 1, 1).wait_recv()
    for i in both:
        for d in range(1 - hi, hi):
            @pl.when((z + d >= 0) & (z + d < hi))
            def _():
                fsdp_copy(i, (z + d) * lo + 1 - y, False, f, lo_send.at[i, d + hi - 1], lo_recv.at[i, d + hi - 1]).wait_recv()
                across(i, d).wait_send()
        for t in range(hi - 1):
            @pl.when((z + 1 < hi) & (z - t >= 0))
            def _():
                right(i, t).wait_send()

            @pl.when((z >= 1) & (z + t < hi))
            def _():
                left(i, t).wait_send()
    for c in seq_sends:
        c.wait_send()
    for c in own_copies:
        c.wait()


def gather_start(tokens, weights, seq, fsdp):
    lo = 2
    hi = fsdp // lo
    count = len(weights)
    anywhere = pl.BlockSpec(memory_space=pl.ANY)
    dma = pltpu.SemaphoreType.DMA
    return pl.pallas_call(
        functools.partial(gather_kernel, seq, hi, lo),
        out_shape=(jax.ShapeDtypeStruct((seq,) + tokens.shape, tokens.dtype),)
        + tuple(jax.ShapeDtypeStruct((fsdp,) + w.shape, w.dtype) for w in weights),
        in_specs=[anywhere] * (1 + count),
        out_specs=(anywhere,) * (1 + count),
        scratch_shapes=[
            dma((1 + count,)),
            dma((seq,)),
            dma((seq,)),
            dma((count, 2, hi)),
            dma((count, 2, hi)),
            dma((count, 2 * hi)),
            dma((count, 2 * hi)),
        ],
        compiler_params=pltpu.CompilerParams(collective_id=0, has_side_effects=True),
        name="gather_start",
    )(tokens, *weights)


def finish_kernel(
    seq,
    hi,
    lo,
    chunks,
    dn_ref,
    gq_ref,
    gu_ref,
    gd_ref,
    go_ref,
    small_ref,
    mlp_gain_ref,
    tok_ref,
    dmid_ref,
    gain_ref,
    tg_ref,
    rq_ref,
    ru_ref,
    rd_ref,
    ro_ref,
    ssum_ref,
    gsum_ref,
    dn_own,
    dn_in,
    dn_low,
    dn_acc,
    tq,
    tu,
    td,
    to,
    yq,
    yu,
    yd,
    yo,
    lq,
    lu,
    ld,
    lq_r,
    lu_r,
    ld_r,
    lo_l,
    lo_r,
    xq,
    xu,
    sy,
    sz,
    gains,
    gy,
    gz,
    gs,
    load_sem,
    dn_send,
    dn_recv,
    y_send,
    y_recv,
    z_send,
    z_recv,
    x_send,
    x_recv,
    s_send,
    s_recv,
    g_send,
    g_recv,
):
    me = lax.axis_index("seq")
    f = lax.axis_index("fsdp")
    z, y = f // lo, f % lo
    peer = z * lo + 1 - y
    grads = (gq_ref, gu_ref, gd_ref, go_ref)
    totals = (tq, tu, td, to)
    from_y = (yq, yu, yd, yo)
    from_z = ((lq, lq_r), (lu, lu_r), (ld, ld_r), (lo_l, lo_r))
    tensors = range(4)
    rows = dn_ref.shape[1] // chunks

    barrier = pltpu.get_barrier_semaphore()
    for k in range(1, seq):
        pl.semaphore_signal(barrier, inc=1, device_id={"seq": me ^ k}, device_id_type=MESH)
    for k in range(1, hi):
        pl.semaphore_signal(barrier, inc=1, device_id={"fsdp": lax.rem(z + k, hi) * lo + y}, device_id_type=MESH)
    pl.semaphore_signal(barrier, inc=1, device_id={"fsdp": peer}, device_id_type=MESH)
    pl.semaphore_wait(barrier, seq + hi - 1)

    def block(i, target):
        return grads[i].at[:, target] if i < 2 else grads[i].at[target]

    def remote(src, dst, send, recv, axis, target):
        return pltpu.make_async_remote_copy(
            src_ref=src, dst_ref=dst, send_sem=send, recv_sem=recv, device_id={axis: target}, device_id_type=MESH
        )

    evens = list(range(0, seq, 2))
    loads = [pltpu.make_async_copy(dn_ref.at[j], dn_own.at[j // 2], load_sem.at[0, j // 2]) for j in evens]
    for c in loads:
        c.start()

    levels = []
    active = list(range(seq))
    bit = 1
    slot = 0
    while bit < seq:
        keep = [j for j in active if not j & bit]
        levels.append((bit, keep, {j: slot + n for n, j in enumerate(keep)}))
        slot += len(keep)
        active = keep
        bit *= 2
    order = sorted(evens, reverse=True)

    def piece_rows(c):
        return pl.ds(c * rows, rows)

    def dn_copy(level, j, c):
        bit, _, slots = levels[level]
        src = dn_ref.at[j ^ bit, piece_rows(c)] if level == 0 else dn_low.at[(j ^ bit) // 2, piece_rows(c)]
        return remote(
            src, dn_in.at[slots[j], piece_rows(c)], dn_send.at[slots[j], c], dn_recv.at[slots[j], c], "seq", me ^ bit
        )

    for c in range(chunks):
        for j in order[:1]:
            dn_copy(0, j, c).start()
    y_copies = {}
    for i in tensors:
        for d in range(hi):
            y_copies[i, d] = remote(
                block(i, d * lo + 1 - y), from_y[i].at[d], y_send.at[i, d], y_recv.at[i, d], "fsdp", peer
            )
    grad_loads = {}
    for i in tensors:
        for d in range(hi):
            grad_loads[i, d] = pltpu.make_async_copy(block(i, d * lo + y), totals[i].at[d], load_sem.at[1 + i, d])
    small_y = remote(small_ref, sy, s_send.at[0], s_recv.at[0], "fsdp", peer)
    small_y.start()
    for d in range(hi):
        y_copies[0, d].start()
        grad_loads[0, d].start()
    for j in order[1:]:
        for c in range(chunks):
            dn_copy(0, j, c).start()
    for i in tensors[1:]:
        for d in range(hi):
            y_copies[i, d].start()
            grad_loads[i, d].start()
    for c in loads:
        c.wait()
    for level, (bit, keep, slots) in enumerate(levels):
        later = levels[level + 1 :]
        for j in sorted(keep, reverse=True):
            for c in range(chunks):
                if level == len(levels) - 1:
                    continue
                dn_copy(level, j, c).wait_recv()
                at = piece_rows(c)
                own = dn_own[j // 2, at].astype(f32) if level == 0 else dn_low[j // 2, at].astype(f32)
                if j == 0:
                    own = own if level == 0 else dn_acc[at]
                    dn_acc[at] = own + dn_in[slots[j], at].astype(f32)
                else:
                    dn_low[j // 2, at] = (own + dn_in[slots[j], at].astype(f32)).astype(bf16)
                    nxt = later[0]
                    if j & nxt[0]:
                        dn_copy(level + 1, j ^ nxt[0], c).start()

    small_y.wait_recv()
    sz[z] = small_ref[...] + sy[...]
    small_z = []
    for k in range(1, hi):
        target = lax.rem(z + k, hi)
        small_z.append(remote(sz.at[z], sz.at[z], s_send.at[k], s_recv.at[k], "fsdp", target * lo + y))
        small_z[-1].start()

    def reduce_tensor(i):
        total = totals[i]
        for d in range(hi):
            grad_loads[i, d].wait()
            y_copies[i, d].wait_recv()
            total[d] = (total[d].astype(f32) + from_y[i][d].astype(f32)).astype(bf16)
        from_right, from_left = from_z[i]
        for t in range(hi - 1):
            d = t - (hi - 1 - z)
            m = hi - 1 - (t - z)

            @pl.when((d >= 0) & (d < z))
            def _():
                at = jnp.clip(d, 0, hi - 1)
                remote(
                    total.at[at], from_right.at[t], z_send.at[i, 0, t], z_recv.at[i, 0, t], "fsdp", (z - 1) * lo + y
                ).start()

            @pl.when((m > z) & (m < hi))
            def _():
                at = jnp.clip(m, 0, hi - 1)
                remote(
                    total.at[at], from_left.at[t], z_send.at[i, 1, t], z_recv.at[i, 1, t], "fsdp", (z + 1) * lo + y
                ).start()

            dr = t - (hi - 2 - z)

            @pl.when((z + 1 < hi) & (dr >= 0))
            def _():
                at = jnp.clip(dr, 0, hi - 1)
                remote(
                    total.at[at], from_right.at[t], z_send.at[i, 0, t], z_recv.at[i, 0, t], "fsdp", f
                ).wait_recv()
                total[at] = (total[at].astype(f32) + from_right[t].astype(f32)).astype(bf16)

            ml = hi - 1 - (t - (z - 1))

            @pl.when((z > 0) & (ml < hi))
            def _():
                at = jnp.clip(ml, 0, hi - 1)
                remote(
                    total.at[at], from_left.at[t], z_send.at[i, 1, t], z_recv.at[i, 1, t], "fsdp", f
                ).wait_recv()
                total[at] = (total[at].astype(f32) + from_left[t].astype(f32)).astype(bf16)

    exchanged = (xq, xu)
    results = (rq_ref, ru_ref, rd_ref, ro_ref)

    def exchange(i):
        for k in range(1, seq):
            remote(
                totals[i].at[z, me ^ k], exchanged[i].at[me], x_send.at[i, k], x_recv.at[i, k], "seq", me ^ k
            ).start()

    reduce_tensor(0)
    exchange(0)

    if levels:
        bit, keep, slots = levels[-1]
    gain = gain_ref[...]
    part = jnp.zeros((8, gain.shape[1]), f32)
    for c in range(chunks):
        at = piece_rows(c)
        if levels:
            dn_copy(len(levels) - 1, 0, c).wait_recv()
        if len(levels) > 1:
            dn = dn_acc[at]
        else:
            dn = dn_own[0, at].astype(f32)
        if levels:
            dn = dn + dn_in[slots[0], at].astype(f32)
        x = tok_ref[at].astype(f32)
        rho = lax.rsqrt(jnp.mean(x * x, axis=-1, keepdims=True) + EPSILON)
        scaled = gain * dn
        mean = jnp.mean(x * scaled, axis=-1, keepdims=True)
        tg_ref[at] = dmid_ref[at] + rho * scaled - x * (rho * rho * rho * mean)
        prod = dn * x * rho
        part += functools.reduce(jnp.add, [prod[n : n + 8] for n in range(0, rows, 8)])
    gains[0:8] = mlp_gain_ref[...]
    gains[8:16] = part
    gain_y = remote(gains, gy, g_send.at[0], g_recv.at[0], "fsdp", peer)
    gain_y.start()
    reduce_tensor(1)
    exchange(1)
    gain_y.wait_recv()
    gz[z] = gains[...] + gy[...]
    gain_z = []
    for k in range(1, hi):
        target = lax.rem(z + k, hi)
        gain_z.append(remote(gz.at[z], gz.at[z], g_send.at[k], g_recv.at[k], "fsdp", target * lo + y))
        gain_z[-1].start()
    reduce_tensor(2)
    for k in range(1, hi):
        source = lax.rem(z + hi - k, hi)
        remote(gz.at[source], gz.at[source], g_send.at[k], g_recv.at[k], "fsdp", f).wait_recv()
        remote(sz.at[source], sz.at[source], s_send.at[k], s_recv.at[k], "fsdp", f).wait_recv()
    gs[me] = functools.reduce(jnp.add, [gz[d] for d in range(hi)])
    gain_x = []
    for k in range(1, seq):
        gain_x.append(remote(gs.at[me], gs.at[me], g_send.at[hi + k], g_recv.at[hi + k], "seq", me ^ k))
        gain_x[-1].start()
    ssum_ref[...] = functools.reduce(jnp.add, [sz[d] for d in range(hi)])
    reduce_tensor(3)
    rd_ref[...] = td[z].astype(f32)
    ro_ref[...] = to[z].astype(f32)
    for i in range(2):
        for k in range(1, seq):
            remote(
                totals[i].at[z, me], exchanged[i].at[me ^ k], x_send.at[i, k], x_recv.at[i, k], "seq", me
            ).wait_recv()
        exchanged[i][me] = totals[i][z, me]
        for k in range(seq):
            results[i][k] = exchanged[i][k].astype(f32)
    for k in range(1, seq):
        remote(gs.at[me ^ k], gs.at[me ^ k], g_send.at[hi + k], g_recv.at[hi + k], "seq", me).wait_recv()
    gsum_ref[...] = functools.reduce(jnp.add, [gs[k] for k in range(seq)])

    for level, (bit, keep, slots) in enumerate(levels):
        for j in keep:
            for c in range(chunks):
                dn_copy(level, j, c).wait_send()
    for i in tensors:
        for d in range(hi):
            y_copies[i, d].wait_send()
        for t in range(hi - 1):
            d = t - (hi - 1 - z)
            m = hi - 1 - (t - z)

            @pl.when((d >= 0) & (d < z))
            def _():
                remote(
                    totals[i].at[0], from_z[i][0].at[t], z_send.at[i, 0, t], z_recv.at[i, 0, t], "fsdp", f
                ).wait_send()

            @pl.when((m > z) & (m < hi))
            def _():
                remote(
                    totals[i].at[0], from_z[i][1].at[t], z_send.at[i, 1, t], z_recv.at[i, 1, t], "fsdp", f
                ).wait_send()
    for i in range(2):
        for k in range(1, seq):
            remote(
                totals[i].at[z, me], exchanged[i].at[me], x_send.at[i, k], x_recv.at[i, k], "seq", me
            ).wait_send()
    for c in [small_y, gain_y] + small_z + gain_z + gain_x:
        c.wait_send()


def finish(dn, gq, gu, gd, go, small, mlp_gain, tok, dmid, gain, seq, fsdp):
    lo = 2
    hi = fsdp // lo
    chunks = 4
    anywhere = pl.BlockSpec(memory_space=pl.ANY)
    vmem = pl.BlockSpec(memory_space=pltpu.VMEM)
    block_q = (seq,) + gq.shape[2:]
    block_u = (seq,) + gu.shape[2:]
    block_d = gd.shape[1:]
    block_o = go.shape[1:]
    blocks = (block_q, block_u, block_d, block_o)
    tok_rows, dim = tok.shape
    sides = max(hi - 1, 1)

    def buf(lead, shape, kind=bf16):
        return pltpu.VMEM((lead,) + tuple(shape), kind)

    scratch = [
        buf(max(seq // 2, 1), (tok_rows, dim)),
        buf(max(seq - 1, 1), (tok_rows, dim)),
        buf(max(seq // 2, 1), (tok_rows, dim)),
        pltpu.VMEM((tok_rows, dim), f32),
    ]
    scratch += [buf(hi, b) for b in blocks]
    scratch += [buf(hi, b) for b in blocks]
    scratch += [buf(sides, b) for b in (block_q, block_u, block_d)] * 2
    scratch += [buf(sides, block_o), buf(sides, block_o)]
    scratch += [pltpu.VMEM(block_q, bf16), pltpu.VMEM(block_u, bf16)]
    scratch += [
        pltpu.VMEM(small.shape, f32),
        buf(hi, small.shape, f32),
        pltpu.VMEM((16, dim), f32),
        pltpu.VMEM((16, dim), f32),
        buf(hi, (16, dim), f32),
        buf(seq, (16, dim), f32),
    ]
    dma = pltpu.SemaphoreType.DMA
    scratch += [
        dma((5, max(hi, seq))),
        dma((seq, chunks)),
        dma((seq, chunks)),
        dma((4, hi)),
        dma((4, hi)),
        dma((4, 2, hi)),
        dma((4, 2, hi)),
        dma((2, seq)),
        dma((2, seq)),
        dma((hi,)),
        dma((hi,)),
        dma((hi + seq,)),
        dma((hi + seq,)),
    ]
    return pl.pallas_call(
        functools.partial(finish_kernel, seq, hi, lo, chunks),
        out_shape=(
            jax.ShapeDtypeStruct((tok_rows, dim), f32),
            jax.ShapeDtypeStruct(block_q, f32),
            jax.ShapeDtypeStruct(block_u, f32),
            jax.ShapeDtypeStruct(block_d, f32),
            jax.ShapeDtypeStruct(block_o, f32),
            jax.ShapeDtypeStruct(small.shape, f32),
            jax.ShapeDtypeStruct((16, dim), f32),
        ),
        in_specs=[anywhere] * 5 + [vmem] * 5,
        out_specs=(vmem,) * 7,
        scratch_shapes=scratch,
        compiler_params=pltpu.CompilerParams(
            collective_id=1, has_side_effects=True, vmem_limit_bytes=56 << 20
        ),
        name="finish",
    )(dn, gq, gu, gd, go, small, mlp_gain, tok, dmid, gain)


def swap(value, bit):
    count = lax.axis_size("seq")
    return lax.ppermute(value, "seq", [(i, i ^ bit) for i in range(count)])


def seq_bits():
    count = lax.axis_size("seq")
    return [1 << i for i in reversed(range(1, count.bit_length() - 1))]


def seq_gather(value):
    chunks = {0: value}
    for bit in seq_bits():
        for j in list(chunks):
            chunks[j ^ bit] = swap(chunks[j], bit)
    for j in list(chunks):
        chunks[j ^ 1] = swap(chunks[j], 1)
    return [chunks[j] for j in range(len(chunks))]


def seq_reduce(parts):
    count = len(parts)
    parts = dict(enumerate(parts))
    for j in range(count - 2, -1, -2):
        parts[j] = parts[j].astype(f32) + swap(parts.pop(j ^ 1).astype(bf16), 1).astype(f32)
    for bit in reversed(seq_bits()):
        keep = [j for j in parts if not j & bit]
        for j in sorted(keep, reverse=True):
            parts[j] = parts[j] + swap(parts.pop(j ^ bit).astype(bf16), bit).astype(f32)
    return parts[0]


def bias_table_grad(near, far):
    distance = tile_distance().T[SPAN - NEAR :]
    bucket = np.where((distance >= 0) & (distance < BLOCK), bucket_of(np.clip(distance, 0, BLOCK)), BUCKETS)
    bucket = jnp.asarray(bucket.astype(np.int32))
    columns = [jnp.sum(jnp.where((bucket == i)[None], near, 0.0), axis=(1, 2)) for i in range(BUCKETS)]
    columns[-1] = columns[-1] + jnp.sum(far, axis=(1, 2))
    return jnp.stack(columns, axis=1)


def inverse_rms(values):
    return lax.rsqrt(jnp.mean(values * values, axis=-1, keepdims=True) + EPSILON)


def norm_back(values, gain, rho, grad):
    scaled = gain * grad
    mean = jnp.mean(values * scaled, axis=-1, keepdims=True)
    gain_grad = (grad * values * rho).reshape(-1, 8, values.shape[1])
    return rho * scaled - values * (rho * rho * rho * mean), jnp.sum(gain_grad, axis=0)


def body(
    tokens,
    lengths,
    state_init,
    w_qkv,
    w_out,
    w_up,
    w_down,
    norm_attn,
    norm_mlp,
    rel_bias,
    state_query,
    gate_bias,
    out_grad,
    state_grad,
):
    seq_count = lax.axis_size("seq")
    fsdp_count = lax.axis_size("fsdp")
    seq_at = lax.axis_index("seq")
    heads = H // seq_count
    width = heads * DH
    tok_rows, dim = tokens.shape[1:]
    rows = tok_rows * seq_count
    hidden_all = w_up.shape[1]
    share = hidden_all // (seq_count * fsdp_count)

    own_qkv = lax.dynamic_slice_in_dim(
        w_qkv.reshape(w_qkv.shape[0], 3, seq_count, width), seq_at, 1, axis=2
    ).reshape(w_qkv.shape[0], 3 * width)
    own_up = lax.dynamic_slice_in_dim(w_up, seq_at * (hidden_all // seq_count), hidden_all // seq_count, axis=1)
    own_down = lax.dynamic_slice_in_dim(w_down, seq_at * share, share, axis=0)
    down_w = lax.all_gather(own_down, "fsdp", axis=0, tiled=True)
    up_w = lax.all_gather(own_up, "fsdp", axis=0, tiled=True)
    all_tokens, qkv_w, gains, out_w = gather_start(
        tokens[0], (own_qkv, jnp.stack([norm_attn, norm_mlp]), w_out), seq_count, fsdp_count
    )
    qkv_w = qkv_w.reshape(dim, 3 * width)
    gains = jnp.swapaxes(gains, 0, 1).reshape(2, dim).astype(f32)
    gain_attn, gain_mlp = gains[0], gains[1]
    span = fsdp_count // seq_count
    down_w = down_w.reshape(seq_count, span, share, dim)
    moved = [lax.dynamic_slice_in_dim(down_w, seq_at, 1, axis=0)]
    for k in range(1, seq_count):
        moved.append(swap(lax.dynamic_slice_in_dim(down_w, seq_at ^ k, 1, axis=0), k))
    moved = jnp.concatenate(moved, axis=0)
    moved = [lax.dynamic_slice_in_dim(moved, seq_at ^ k, 1, axis=0) for k in range(seq_count)]
    down_w = jnp.swapaxes(jnp.concatenate(moved, axis=0), 0, 1).reshape(fsdp_count * share, dim)
    all_grad = jnp.concatenate(seq_gather(out_grad[0]), axis=0)

    bias = tile_bias(rel_bias)
    bias_t = jnp.swapaxes(bias, 1, 2)
    forget = jax.nn.sigmoid(gate_bias)
    forget_row = forget.reshape(1, width)
    chunk_ids = jnp.arange(seq_count, dtype=jnp.int32)
    order = chunk_ids ^ seq_at

    inputs = all_tokens.reshape(rows, dim).astype(f32)
    normed = (inputs * inverse_rms(inputs) * gain_attn).astype(bf16)
    qkv = dot(normed, qkv_w).astype(bf16)
    attended, final_memory, mem, upd, lse, slse = attend(
        qkv, state_init[0], lengths, state_query, forget_row, bias, heads, order
    )

    from_heads = seq_gather(attended)
    columns = []
    for k in range(seq_count):
        blocks = from_heads[k].reshape(seq_count, tok_rows, width)
        columns.append(jnp.concatenate([blocks[j ^ k] for j in range(seq_count)], axis=0))
    all_attended = jnp.concatenate(columns, axis=1)
    out_w = out_w.reshape(seq_count, width, dim)
    own_out = lax.dynamic_slice_in_dim(out_w, seq_at, 1, axis=0)[0]
    out_w = jnp.concatenate(
        [lax.dynamic_slice_in_dim(out_w, seq_at ^ k, 1, axis=0)[0] for k in range(seq_count)], axis=0
    )
    mid = inputs + dot(all_attended, out_w)
    rho_mid = inverse_rms(mid)
    normed_mid = (mid * rho_mid * gain_mlp).astype(bf16)
    positions = (order[:, None] * tok_rows + jnp.arange(tok_rows, dtype=jnp.int32)).reshape(rows)
    live = (positions < lengths[0]).astype(bf16)[:, None]
    grad_low = all_grad * live
    pre = dot(normed_mid, up_w)
    hidden, gelu_pull = jax.vjp(lambda v: jax.nn.gelu(v, approximate=False), pre)
    hidden = hidden.astype(bf16)
    dpre = gelu_pull(dot_t(grad_low, down_w))[0].astype(bf16)

    def chunk(value, j):
        return value[j * tok_rows : (j + 1) * tok_rows]

    dnormed_mid = seq_reduce([dot_t(chunk(dpre, j), up_w) for j in range(seq_count)])
    down_grad = t_dot(hidden, grad_low)
    up_grad = t_dot(normed_mid, dpre)
    mlp_out = seq_reduce([dot(chunk(hidden, j), down_w) for j in range(seq_count)])

    mid_here = chunk(mid, 0)
    live_here = chunk(live, 0).astype(f32)
    output = (live_here * (mid_here + mlp_out)).astype(bf16)[None]
    grad_here = out_grad[0].astype(f32) * live_here
    through, mlp_gain_grad = norm_back(mid_here, gain_mlp, inverse_rms(mid_here), dnormed_mid)
    dmid = grad_here + through
    dbranch = jnp.concatenate(seq_gather(dmid.astype(bf16)), axis=0)
    dattended = dot_t(dbranch, own_out).astype(bf16)
    out_w_grad = t_dot(attended, dbranch)

    dqkv, dquery, dforget, near, far = attend_back(
        qkv, dattended, attended, mem, upd, lse, slse, state_grad[0], lengths, state_query, forget_row, bias_t, heads, order
    )
    dnormed = dot_t(dqkv, qkv_w).astype(bf16).reshape(seq_count, tok_rows, dim)
    piece = dim // (seq_count * fsdp_count)
    qkv_grad = t_dot(normed, dqkv).astype(bf16).reshape(seq_count, fsdp_count, piece, 3 * width)
    up_grad = up_grad.astype(bf16).reshape(seq_count, fsdp_count, piece, hidden_all // seq_count)
    down_grad = down_grad.astype(bf16).reshape(fsdp_count, share, dim)
    out_w_grad = out_w_grad.astype(bf16).reshape(fsdp_count, piece, dim)
    grad_gate = dforget.reshape(heads, DH) * forget * (1.0 - forget)
    grad_table = jnp.pad(bias_table_grad(near, far), ((0, 0), (0, DH - BUCKETS)))
    cut = heads * DH
    small = jnp.concatenate([dquery.reshape(cut, DH), grad_gate, grad_table], axis=0)
    small = jnp.pad(small, ((0, -small.shape[0] % 8), (0, 0)))
    tokens_grad, qkv_part, up_part, down_part, out_part, small, gain_sums = finish(
        dnormed,
        qkv_grad,
        up_grad,
        down_grad,
        out_w_grad,
        small,
        mlp_gain_grad,
        tokens[0],
        dmid,
        gain_attn.reshape(1, dim),
        seq_count,
        fsdp_count,
    )
    tokens_grad = tokens_grad[None]
    dquery = small[:cut].reshape(heads, DH, DH)
    grad_gate = small[cut : cut + heads]
    grad_table = small[cut + heads : cut + 2 * heads, :BUCKETS]
    up_part = jnp.swapaxes(up_part, 0, 1).reshape(piece, hidden_all)
    qkv_part = qkv_part.reshape(seq_count, piece, 3, width)
    qkv_part = jnp.transpose(qkv_part, (1, 2, 0, 3)).reshape(piece, 3 * H * DH)
    gain_sums = jnp.sum(gain_sums.reshape(2, 8, seq_count * fsdp_count, piece), axis=1)
    mine = seq_at * fsdp_count + lax.axis_index("fsdp")
    gain_sums = lax.dynamic_slice_in_dim(gain_sums, mine, 1, axis=1)[:, 0]
    mlp_gain_grad, attn_gain_grad = gain_sums[0], gain_sums[1]
    return (
        output,
        final_memory[None],
        tokens_grad,
        qkv_part,
        out_part,
        up_part,
        down_part,
        attn_gain_grad,
        mlp_gain_grad,
        grad_table,
        dquery,
        grad_gate,
    )


def solution(mesh):
    placed = (
        P("fsdp", "seq", None),
        P("fsdp"),
        P("fsdp", None, "seq"),
        P("fsdp", None),
        P("fsdp", None),
        P("fsdp", None),
        P("fsdp", None),
        P("fsdp"),
        P("fsdp"),
        P("seq", None),
        P("seq", None, None),
        P("seq", None),
        P("fsdp", "seq", None),
        P("fsdp", None, "seq"),
    )
    return jax.shard_map(
        body,
        mesh=mesh,
        in_specs=placed,
        out_specs=(
            P("fsdp", "seq", None),
            P("fsdp", None, "seq"),
            P("fsdp", "seq", None),
            P(("seq", "fsdp"), None),
            P(("seq", "fsdp"), None),
            P(("seq", "fsdp"), None),
            P(("seq", "fsdp"), None),
            P(("seq", "fsdp")),
            P(("seq", "fsdp")),
            P("seq", None),
            P("seq", None, None),
            P("seq", None),
        ),
        check_vma=False,
    )
```

```python
import functools
import math

import jax
import jax.numpy as jnp
import numpy as np
from jax import lax
from jax.experimental import pallas as pl
from jax.experimental.pallas import tpu as pltpu
from jax.sharding import PartitionSpec as P

H = 8
DH = 128
BLOCK = 512
STATE_VECTORS = 512
QTILE = 256
SPAN = BLOCK + QTILE

EPSILON = 1e-06
BUCKET_EDGES = (19, 21, 24, 27, 31, 35, 40, 46, 52, 59, 67, 77, 87, 99, 113)
BUCKETS = 32
LOG2E = math.log2(math.e)
SCALE = DH ** (-0.5)
NEAR = 384

f32 = jnp.float32
bf16 = jnp.bfloat16
MESH = pl.DeviceIdType.MESH


def bucket_of(distance):
    return np.minimum(distance, 16) + (distance[..., None] >= np.array(BUCKET_EDGES)).sum(-1)


def tile_distance():
    rows = np.arange(QTILE)[:, None]
    cols = np.arange(SPAN)[None, :]
    return rows + BLOCK - cols


def bias_vector(table):
    distance = BLOCK - np.arange(2 * BLOCK)
    inside = (distance >= 0) & (distance < BLOCK)
    bucket = jnp.asarray(np.where(inside, bucket_of(np.clip(distance, 0, BLOCK)), BUCKETS).astype(np.int32))
    total = jnp.full((table.shape[0], 2 * BLOCK), -jnp.inf, f32)
    for i in range(BUCKETS):
        total = jnp.where((bucket == i)[None], table[:, i : i + 1] * LOG2E, total)
    return total


def tile_bias(vector_ref, head):
    wide = jnp.broadcast_to(vector_ref[head : head + 1, :], (QTILE, 2 * BLOCK))
    return pltpu.roll(wide, 0, 1, stride=1, stride_axis=0)[:, :SPAN]


def dot(a, b):
    return jnp.dot(a, b, preferred_element_type=f32)


def dot_t(a, b):
    return lax.dot_general(a, b, (((1,), (1,)), ((), ())), preferred_element_type=f32)


def t_dot(a, b):
    return lax.dot_general(a, b, (((0,), (0,)), ((), ())), preferred_element_type=f32)


def to_row(column):
    wide = jnp.broadcast_to(column, (column.shape[0], 128))
    return wide.T[0:1, :]


def context_pieces(tile):
    start = tile * QTILE
    pieces = []
    if start < BLOCK:
        pieces.append((0, start, BLOCK, 0))
    pieces.append((1, 0, start + QTILE, BLOCK - start))
    return pieces


def softmax_parts(scores):
    top = functools.reduce(jnp.maximum, [jnp.max(s, axis=-1, keepdims=True) for s in scores])
    raised = [jnp.exp2(s - top) for s in scores]
    total = functools.reduce(jnp.add, [jnp.sum(e, axis=-1, keepdims=True) for e in raised])
    return raised, total, top + jnp.log2(total)


def attend_kernel(
    heads,
    length_ref,
    order_ref,
    cur_ref,
    prev_ref,
    init_ref,
    query_ref,
    forget_ref,
    vector_ref,
    att_ref,
    final_ref,
    mem_ref,
    upd_ref,
    lse_ref,
    slse_ref,
    memory_ref,
    bias_ref,
):
    block = pl.program_id(0)
    length = length_ref[0]
    width = heads * DH
    scale2 = SCALE * LOG2E

    @pl.when(block == 0)
    def _():
        memory_ref[...] = init_ref[...].astype(f32)
        for head in range(heads):
            bias_ref[head] = tile_bias(vector_ref, head)

    live_block = block * BLOCK < length
    for head in range(heads):
        own = slice(head * DH, (head + 1) * DH)
        memory = memory_ref[:, own]
        low = memory.astype(bf16)
        mem_ref[0, :, own] = memory
        refs = (prev_ref, cur_ref)
        key_cols = slice(width + head * DH, width + (head + 1) * DH)
        value_cols = slice(2 * width + head * DH, 2 * width + (head + 1) * DH)
        for tile in range(BLOCK // QTILE):
            rows = slice(tile * QTILE, (tile + 1) * QTILE)
            query = cur_ref[rows, own]
            scores, values = [], []
            for which, lo, hi, col in context_pieces(tile):
                s = dot_t(query, refs[which][lo:hi, key_cols])
                position = (block - 1 + which) * BLOCK + lo + lax.broadcasted_iota(jnp.int32, (1, hi - lo), 1)
                live = (position >= 0) & (position < length)
                s = s * scale2 + bias_ref[head, :, col : col + hi - lo]
                scores.append(jnp.where(live, s, -jnp.inf))
                values.append(refs[which][lo:hi, value_cols])
            scores.append(dot_t(query, low) * scale2)
            values.append(low)
            raised, total, lse = softmax_parts(scores)
            out = functools.reduce(jnp.add, [dot(e.astype(bf16), v) for e, v in zip(raised, values)])
            att_ref[rows, own] = (out / total).astype(bf16)
            lse_ref[head : head + 1, rows] = to_row(lse)
        own_key = cur_ref[:, key_cols]
        own_value = cur_ref[:, value_cols]
        squeries = dot(low, query_ref[head]).astype(bf16)
        position = block * BLOCK + lax.broadcasted_iota(jnp.int32, (1, BLOCK), 1)
        for tile in range(STATE_VECTORS // QTILE):
            rows = slice(tile * QTILE, (tile + 1) * QTILE)
            squery = squeries[rows]
            scores = [
                dot_t(squery, low) * scale2,
                jnp.where(position < length, dot_t(squery, own_key) * scale2, -jnp.inf),
            ]
            raised, total, lse = softmax_parts(scores)
            update = dot(raised[0].astype(bf16), low) + dot(raised[1].astype(bf16), own_value)
            update = update / total
            upd_ref[0, rows, own] = update
            slse_ref[head : head + 1, rows] = to_row(lse)
            forget = forget_ref[:, own]
            old = memory[rows]
            memory_ref[rows, own] = jnp.where(live_block, forget * old + (1.0 - forget) * update, old)
    final_ref[...] = memory_ref[...]


def attend(qkv, init, length, state_query, forget, bias, heads, order):
    rows, width3 = qkv.shape
    width = heads * DH
    blocks = rows // BLOCK
    return pl.pallas_call(
        functools.partial(attend_kernel, heads),
        out_shape=(
            jax.ShapeDtypeStruct((rows, width), bf16),
            jax.ShapeDtypeStruct((STATE_VECTORS, width), f32),
            jax.ShapeDtypeStruct((blocks, STATE_VECTORS, width), f32),
            jax.ShapeDtypeStruct((blocks, STATE_VECTORS, width), f32),
            jax.ShapeDtypeStruct((heads, rows), f32),
            jax.ShapeDtypeStruct((heads, blocks * STATE_VECTORS), f32),
        ),
        grid_spec=pltpu.PrefetchScalarGridSpec(
            num_scalar_prefetch=2,
            grid=(blocks,),
            in_specs=[
                pl.BlockSpec((BLOCK, width3), lambda b, _, at: (at[b], 0)),
                pl.BlockSpec((BLOCK, width3), lambda b, _, at: (at[jnp.maximum(b - 1, 0)], 0)),
                pl.BlockSpec((STATE_VECTORS, width), lambda b, _, at: (0, 0)),
                pl.BlockSpec((heads, DH, DH), lambda b, _, at: (0, 0, 0)),
                pl.BlockSpec((1, width), lambda b, _, at: (0, 0)),
                pl.BlockSpec((heads, 2 * BLOCK), lambda b, _, at: (0, 0)),
            ],
            out_specs=(
                pl.BlockSpec((BLOCK, width), lambda b, _, at: (at[b], 0)),
                pl.BlockSpec((STATE_VECTORS, width), lambda b, _, at: (0, 0)),
                pl.BlockSpec((1, STATE_VECTORS, width), lambda b, _, at: (b, 0, 0)),
                pl.BlockSpec((1, STATE_VECTORS, width), lambda b, _, at: (b, 0, 0)),
                pl.BlockSpec((heads, BLOCK), lambda b, _, at: (0, b)),
                pl.BlockSpec((heads, STATE_VECTORS), lambda b, _, at: (0, b)),
            ),
            scratch_shapes=[pltpu.VMEM((STATE_VECTORS, width), f32), pltpu.VMEM((heads, QTILE, SPAN), f32)],
        ),
        compiler_params=pltpu.CompilerParams(vmem_limit_bytes=40 << 20),
        cost_estimate=pl.CostEstimate(
            flops=blocks * heads * 512 * 2400 * 128 * 4, bytes_accessed=16 << 20, transcendentals=10 << 20
        ),
        name="attend",
    )(length, order, qkv, qkv, init, state_query, forget, bias)


def attend_back_kernel(
    heads,
    blocks,
    length_ref,
    order_ref,
    cur_ref,
    prev_ref,
    dout_ref,
    out_ref,
    mem_ref,
    upd_ref,
    lse_ref,
    slse_ref,
    sgrad_ref,
    query_ref,
    forget_ref,
    vector_ref,
    dqkv_ref,
    dquery_ref,
    dforget_ref,
    near_ref,
    far_ref,
    dmem_ref,
    dnext_ref,
    dctx_ref,
    bias_ref,
):
    step = pl.program_id(0)
    block = blocks - 1 - step
    length = length_ref[0]
    width = heads * DH
    scale2 = SCALE * LOG2E

    @pl.when(step == 0)
    def _():
        dmem_ref[...] = sgrad_ref[...].astype(f32)
        dnext_ref[...] = jnp.zeros_like(dnext_ref)
        dquery_ref[...] = jnp.zeros_like(dquery_ref)
        dforget_ref[...] = jnp.zeros_like(dforget_ref)
        near_ref[...] = jnp.zeros_like(near_ref)
        far_ref[...] = jnp.zeros_like(far_ref)
        for head in range(heads):
            bias_ref[head] = tile_bias(vector_ref, head).T

    live_block = block * BLOCK < length
    refs = (prev_ref, cur_ref)
    for head in range(heads):
        own = slice(head * DH, (head + 1) * DH)
        key_cols = slice(width + head * DH, width + (head + 1) * DH)
        value_cols = slice(2 * width + head * DH, 2 * width + (head + 1) * DH)
        memory = mem_ref[0, :, own]
        update = upd_ref[0, :, own]
        low = memory.astype(bf16)
        forget = forget_ref[:, own]
        dmem = dmem_ref[:, own]
        dupd = jnp.where(live_block, (1.0 - forget) * dmem, 0.0).astype(bf16)
        moved = jnp.where(live_block, dmem * (memory - update), 0.0)
        dforget_ref[:, own] += jnp.sum(moved, axis=0, keepdims=True)
        dmem_new = jnp.where(live_block, forget * dmem, dmem)
        own_key = cur_ref[:, key_cols]
        own_value = cur_ref[:, value_cols]
        squeries = dot(low, query_ref[head]).astype(bf16)
        sdelta = jnp.sum((dupd.astype(f32) * update).T, axis=0, keepdims=True)
        slse = slse_ref[head : head + 1, :]
        dsquery = jnp.zeros((STATE_VECTORS, DH), f32)
        dkey = []
        dvalue = []
        for part in range(2 * STATE_VECTORS // QTILE):
            own_part = part >= STATE_VECTORS // QTILE
            lo = (part % (STATE_VECTORS // QTILE)) * QTILE
            keys = (own_key if own_part else low)[lo : lo + QTILE]
            values = (own_value if own_part else low)[lo : lo + QTILE]
            s = dot_t(keys, squeries) * scale2 - slse
            if own_part:
                position = block * BLOCK + lo + lax.broadcasted_iota(jnp.int32, (QTILE, 1), 0)
                s = jnp.where(position < length, s, -jnp.inf)
            p = jnp.exp2(s)
            dp = dot_t(values, dupd)
            ds = (p * (dp - sdelta)).astype(bf16)
            dvalue.append(dot(p.astype(bf16), dupd))
            dkey.append(dot(ds, squeries))
            dsquery += t_dot(ds, keys)
        half = STATE_VECTORS // QTILE
        dlow = [dvalue[i] + dkey[i] * SCALE for i in range(half)]
        dctx_ref[0, 0:BLOCK] = jnp.zeros((BLOCK, DH), f32)
        dctx_ref[1, 0:BLOCK] = jnp.zeros((BLOCK, DH), f32)
        for i in range(half):
            rows = slice(BLOCK + i * QTILE, BLOCK + (i + 1) * QTILE)
            old = slice(i * QTILE, (i + 1) * QTILE)
            dctx_ref[0, rows] = dkey[half + i] * SCALE + dnext_ref[0, old, own]
            dctx_ref[1, rows] = dvalue[half + i] + dnext_ref[1, old, own]
        dsq = (dsquery * SCALE).astype(bf16)
        dquery_ref[head] += t_dot(low, dsq)
        dmem_ref[:, own] = dmem_new + dot_t(dsq, query_ref[head])
        for tile in range(BLOCK // QTILE):
            rows = slice(tile * QTILE, (tile + 1) * QTILE)
            query = cur_ref[rows, own]
            dout = dout_ref[rows, own]
            lse = lse_ref[head : head + 1, rows]
            delta = jnp.sum((dout.astype(f32) * out_ref[rows, own].astype(f32)).T, axis=0, keepdims=True)
            dq = jnp.zeros((QTILE, DH), f32)
            for which, lo, hi, col in context_pieces(tile):
                for at in range(lo, hi, QTILE):
                    keys = refs[which][at : at + QTILE, key_cols]
                    values = refs[which][at : at + QTILE, value_cols]
                    band = col + at - lo
                    position = (block - 1 + which) * BLOCK + at + lax.broadcasted_iota(jnp.int32, (QTILE, 1), 0)
                    live = (position >= 0) & (position < length)
                    s = dot_t(keys, query) * scale2 + bias_ref[head, band : band + QTILE, :] - lse
                    p = jnp.exp2(jnp.where(live, s, -jnp.inf))
                    dp = dot_t(values, dout)
                    ds = (p * (dp - delta)).astype(bf16)
                    wide = ds.astype(f32)
                    if band + QTILE <= SPAN - NEAR:
                        far_ref[head] += functools.reduce(jnp.add, [wide[i : i + 8] for i in range(0, QTILE, 8)])
                    else:
                        edge = max(SPAN - NEAR - band, 0)
                        if edge:
                            far_ref[head] += functools.reduce(jnp.add, [wide[i : i + 8] for i in range(0, edge, 8)])
                        at_near = band + edge - (SPAN - NEAR)
                        near_ref[head, at_near : at_near + QTILE - edge] += wide[edge:]
                    into = slice(which * BLOCK + at, which * BLOCK + at + QTILE)
                    dctx_ref[1, into] += dot(p.astype(bf16), dout)
                    dctx_ref[0, into] += dot(ds, query) * SCALE
                    dq += t_dot(ds, keys)
            for part in range(half):
                keys = low[part * QTILE : (part + 1) * QTILE]
                s = dot_t(keys, query) * scale2 - lse
                p = jnp.exp2(s)
                dp = dot_t(keys, dout)
                ds = (p * (dp - delta)).astype(bf16)
                dlow[part] += dot(p.astype(bf16), dout) + dot(ds, query) * SCALE
                dq += t_dot(ds, keys)
            dqkv_ref[rows, own] = (dq * SCALE).astype(bf16)
        for part in range(half):
            dmem_ref[part * QTILE : (part + 1) * QTILE, own] += dlow[part]
        dnext_ref[0, :, own] = dctx_ref[0, 0:BLOCK]
        dnext_ref[1, :, own] = dctx_ref[1, 0:BLOCK]
        dqkv_ref[:, key_cols] = dctx_ref[0, BLOCK:].astype(bf16)
        dqkv_ref[:, value_cols] = dctx_ref[1, BLOCK:].astype(bf16)


def attend_back(qkv, dout, out, mem, upd, lse, slse, sgrad, length, state_query, forget, bias, heads, order):
    rows, width3 = qkv.shape
    width = heads * DH
    blocks = rows // BLOCK
    last = blocks - 1
    return pl.pallas_call(
        functools.partial(attend_back_kernel, heads, blocks),
        out_shape=(
            jax.ShapeDtypeStruct((rows, width3), bf16),
            jax.ShapeDtypeStruct((heads, DH, DH), f32),
            jax.ShapeDtypeStruct((1, width), f32),
            jax.ShapeDtypeStruct((heads, NEAR, QTILE), f32),
            jax.ShapeDtypeStruct((heads, 8, QTILE), f32),
        ),
        grid_spec=pltpu.PrefetchScalarGridSpec(
            num_scalar_prefetch=2,
            grid=(blocks,),
            in_specs=[
                pl.BlockSpec((BLOCK, width3), lambda b, _, at: (at[last - b], 0)),
                pl.BlockSpec((BLOCK, width3), lambda b, _, at: (at[jnp.maximum(last - b - 1, 0)], 0)),
                pl.BlockSpec((BLOCK, width), lambda b, _, at: (at[last - b], 0)),
                pl.BlockSpec((BLOCK, width), lambda b, _, at: (at[last - b], 0)),
                pl.BlockSpec((1, STATE_VECTORS, width), lambda b, _, at: (last - b, 0, 0)),
                pl.BlockSpec((1, STATE_VECTORS, width), lambda b, _, at: (last - b, 0, 0)),
                pl.BlockSpec((heads, BLOCK), lambda b, _, at: (0, last - b)),
                pl.BlockSpec((heads, STATE_VECTORS), lambda b, _, at: (0, last - b)),
                pl.BlockSpec((STATE_VECTORS, width), lambda b, _, at: (0, 0)),
                pl.BlockSpec((heads, DH, DH), lambda b, _, at: (0, 0, 0)),
                pl.BlockSpec((1, width), lambda b, _, at: (0, 0)),
                pl.BlockSpec((heads, 2 * BLOCK), lambda b, _, at: (0, 0)),
            ],
            out_specs=(
                pl.BlockSpec((BLOCK, width3), lambda b, _, at: (at[last - b], 0)),
                pl.BlockSpec((heads, DH, DH), lambda b, _, at: (0, 0, 0)),
                pl.BlockSpec((1, width), lambda b, _, at: (0, 0)),
                pl.BlockSpec((heads, NEAR, QTILE), lambda b, _, at: (0, 0, 0)),
                pl.BlockSpec((heads, 8, QTILE), lambda b, _, at: (0, 0, 0)),
            ),
            scratch_shapes=[
                pltpu.VMEM((STATE_VECTORS, width), f32),
                pltpu.VMEM((2, BLOCK, width), f32),
                pltpu.VMEM((2, 2 * BLOCK, DH), f32),
                pltpu.VMEM((heads, SPAN, QTILE), f32),
            ],
        ),
        compiler_params=pltpu.CompilerParams(vmem_limit_bytes=40 << 20),
        cost_estimate=pl.CostEstimate(
            flops=blocks * heads * 512 * 2400 * 128 * 10, bytes_accessed=20 << 20, transcendentals=10 << 20
        ),
        name="attend_back",
    )(length, order, qkv, qkv, dout, out, mem, upd, lse, slse, sgrad, state_query, forget, bias)


def gather_kernel(seq, hi, lo, tok_ref, w_ref, gain_ref, out_ref, toks_ref, ws_ref, gains_ref, outs_ref, here_sem, seq_send, seq_recv, far_send, far_recv, lo_send, lo_recv):
    me = lax.axis_index("seq")
    f = lax.axis_index("fsdp")
    z, y = f // lo, f % lo
    pairs = ((w_ref, ws_ref), (gain_ref, gains_ref), (out_ref, outs_ref))

    barrier = pltpu.get_barrier_semaphore()
    greeted = 0
    bit = 1
    while bit < seq:
        pl.semaphore_signal(barrier, inc=1, device_id={"seq": me ^ bit}, device_id_type=MESH)
        greeted += 1
        bit *= 2
    for target in (lax.rem(z + 1, hi) * lo + y, lax.rem(z + hi - 1, hi) * lo + y):
        pl.semaphore_signal(barrier, inc=1, device_id={"fsdp": target}, device_id_type=MESH)
        greeted += 1
    pl.semaphore_signal(barrier, inc=1, device_id={"fsdp": z * lo + 1 - y}, device_id_type=MESH)
    greeted += 1
    pl.semaphore_wait(barrier, greeted)

    own_copies = [pltpu.make_async_copy(tok_ref, toks_ref.at[0], here_sem.at[0])]
    own_copies += [pltpu.make_async_copy(a, b.at[f], here_sem.at[1 + i]) for i, (a, b) in enumerate(pairs)]
    for c in own_copies:
        c.start()

    def seq_copy(source, slot, bit):
        src = tok_ref if source == 0 else toks_ref.at[source]
        return pltpu.make_async_remote_copy(
            src_ref=src, dst_ref=toks_ref.at[slot], send_sem=seq_send.at[slot], recv_sem=seq_recv.at[slot],
            device_id={"seq": me ^ bit}, device_id_type=MESH,
        )

    def fsdp_copy(i, origin, own, target, send, recv):
        src, out = pairs[i]
        return pltpu.make_async_remote_copy(
            src_ref=src if own else out.at[origin], dst_ref=out.at[origin], send_sem=send, recv_sem=recv,
            device_id={"fsdp": target}, device_id_type=MESH,
        )

    def right(i, t):
        return fsdp_copy(i, (z - t) * lo + y, t == 0, (z + 1) * lo + y, far_send.at[i, 0, t], far_recv.at[i, 0, t])

    def left(i, t):
        return fsdp_copy(i, (z + t) * lo + y, t == 0, (z - 1) * lo + y, far_send.at[i, 1, t], far_recv.at[i, 1, t])

    def across(i, d):
        return fsdp_copy(i, (z + d) * lo + y, d == 0, z * lo + 1 - y, lo_send.at[i, d + hi - 1], lo_recv.at[i, d + hi - 1])

    both = range(len(pairs))
    seq_sends = []
    bits = []
    bit = seq // 2
    while bit > 1:
        bits.append(bit)
        bit //= 2
    have = [0]
    if bits:
        seq_sends.append(seq_copy(0, bits[0], bits[0]))
        seq_sends[-1].start()
    if seq > 1:
        seq_sends.append(seq_copy(0, 1, 1))
        seq_sends[-1].start()
    for i in both:
        pl.when(z + 1 < hi)(right(i, 0).start)
        pl.when(z >= 1)(left(i, 0).start)
        across(i, 0).start()
    for t in range(hi - 1):
        for i in both:
            @pl.when(z - 1 - t >= 0)
            def _():
                fsdp_copy(i, (z - 1 - t) * lo + y, False, f, far_send.at[i, 0, t], far_recv.at[i, 0, t]).wait_recv()
                across(i, -1 - t).start()
                if t + 1 < hi - 1:
                    pl.when(z + 1 < hi)(right(i, t + 1).start)

            @pl.when(z + 1 + t < hi)
            def _():
                fsdp_copy(i, (z + 1 + t) * lo + y, False, f, far_send.at[i, 1, t], far_recv.at[i, 1, t]).wait_recv()
                across(i, 1 + t).start()
                if t + 1 < hi - 1:
                    pl.when(z >= 1)(left(i, t + 1).start)
    for n, bit in enumerate(bits):
        if n:
            for j in have:
                seq_sends.append(seq_copy(j, j ^ bit, bit))
                seq_sends[-1].start()
        for j in list(have):
            seq_copy(0, j ^ bit, bit).wait_recv()
            seq_sends.append(seq_copy(j ^ bit, j ^ bit ^ 1, 1))
            seq_sends[-1].start()
        have += [j ^ bit for j in have]
    for j in have if seq > 1 else []:
        seq_copy(0, j ^ 1, 1).wait_recv()
    for i in both:
        for d in range(1 - hi, hi):
            @pl.when((z + d >= 0) & (z + d < hi))
            def _():
                fsdp_copy(i, (z + d) * lo + 1 - y, False, f, lo_send.at[i, d + hi - 1], lo_recv.at[i, d + hi - 1]).wait_recv()
                across(i, d).wait_send()
        for t in range(hi - 1):
            @pl.when((z + 1 < hi) & (z - t >= 0))
            def _():
                right(i, t).wait_send()

            @pl.when((z >= 1) & (z + t < hi))
            def _():
                left(i, t).wait_send()
    for c in seq_sends:
        c.wait_send()
    for c in own_copies:
        c.wait()


def gather_start(tokens, weights, seq, fsdp):
    lo = 2
    hi = fsdp // lo
    count = len(weights)
    anywhere = pl.BlockSpec(memory_space=pl.ANY)
    dma = pltpu.SemaphoreType.DMA
    return pl.pallas_call(
        functools.partial(gather_kernel, seq, hi, lo),
        out_shape=(jax.ShapeDtypeStruct((seq,) + tokens.shape, tokens.dtype),)
        + tuple(jax.ShapeDtypeStruct((fsdp,) + w.shape, w.dtype) for w in weights),
        in_specs=[anywhere] * (1 + count),
        out_specs=(anywhere,) * (1 + count),
        scratch_shapes=[
            dma((1 + count,)),
            dma((seq,)),
            dma((seq,)),
            dma((count, 2, hi)),
            dma((count, 2, hi)),
            dma((count, 2 * hi)),
            dma((count, 2 * hi)),
        ],
        compiler_params=pltpu.CompilerParams(collective_id=0, has_side_effects=True),
        name="gather_start",
    )(tokens, *weights)


def finish_kernel(
    seq,
    hi,
    lo,
    chunks,
    dn_ref,
    gq_ref,
    gu_ref,
    gd_ref,
    go_ref,
    small_ref,
    mlp_gain_ref,
    tok_ref,
    dmid_ref,
    gain_ref,
    tg_ref,
    rq_ref,
    ru_ref,
    rd_ref,
    ro_ref,
    ssum_ref,
    gsum_ref,
    dn_own,
    dn_in,
    dn_low,
    dn_acc,
    tq,
    tu,
    td,
    to,
    yq,
    yu,
    yd,
    yo,
    lq,
    lu,
    ld,
    lq_r,
    lu_r,
    ld_r,
    lo_l,
    lo_r,
    xq,
    xu,
    sy,
    sz,
    gains,
    gy,
    gz,
    gs,
    load_sem,
    dn_send,
    dn_recv,
    y_send,
    y_recv,
    z_send,
    z_recv,
    x_send,
    x_recv,
    s_send,
    s_recv,
    g_send,
    g_recv,
):
    me = lax.axis_index("seq")
    f = lax.axis_index("fsdp")
    z, y = f // lo, f % lo
    peer = z * lo + 1 - y
    grads = (gq_ref, gu_ref, gd_ref, go_ref)
    totals = (tq, tu, td, to)
    from_y = (yq, yu, yd, yo)
    from_z = ((lq, lq_r), (lu, lu_r), (ld, ld_r), (lo_l, lo_r))
    tensors = range(4)
    rows = dn_ref.shape[1] // chunks

    barrier = pltpu.get_barrier_semaphore()
    for k in range(1, seq):
        pl.semaphore_signal(barrier, inc=1, device_id={"seq": me ^ k}, device_id_type=MESH)
    for k in range(1, hi):
        pl.semaphore_signal(barrier, inc=1, device_id={"fsdp": lax.rem(z + k, hi) * lo + y}, device_id_type=MESH)
    pl.semaphore_signal(barrier, inc=1, device_id={"fsdp": peer}, device_id_type=MESH)
    pl.semaphore_wait(barrier, seq + hi - 1)

    def block(i, target):
        return grads[i].at[:, target] if i < 2 else grads[i].at[target]

    def remote(src, dst, send, recv, axis, target):
        return pltpu.make_async_remote_copy(
            src_ref=src, dst_ref=dst, send_sem=send, recv_sem=recv, device_id={axis: target}, device_id_type=MESH
        )

    evens = list(range(0, seq, 2))
    loads = [pltpu.make_async_copy(dn_ref.at[j], dn_own.at[j // 2], load_sem.at[0, j // 2]) for j in evens]
    for c in loads:
        c.start()

    levels = []
    active = list(range(seq))
    bit = 1
    slot = 0
    while bit < seq:
        keep = [j for j in active if not j & bit]
        levels.append((bit, keep, {j: slot + n for n, j in enumerate(keep)}))
        slot += len(keep)
        active = keep
        bit *= 2
    order = sorted(evens, reverse=True)

    def piece_rows(c):
        return pl.ds(c * rows, rows)

    def dn_copy(level, j, c):
        bit, _, slots = levels[level]
        src = dn_ref.at[j ^ bit, piece_rows(c)] if level == 0 else dn_low.at[(j ^ bit) // 2, piece_rows(c)]
        return remote(
            src, dn_in.at[slots[j], piece_rows(c)], dn_send.at[slots[j], c], dn_recv.at[slots[j], c], "seq", me ^ bit
        )

    for c in range(chunks):
        for j in order[:1]:
            dn_copy(0, j, c).start()
    y_copies = {}
    for i in tensors:
        for d in range(hi):
            y_copies[i, d] = remote(
                block(i, d * lo + 1 - y), from_y[i].at[d], y_send.at[i, d], y_recv.at[i, d], "fsdp", peer
            )
    grad_loads = {}
    for i in tensors:
        for d in range(hi):
            grad_loads[i, d] = pltpu.make_async_copy(block(i, d * lo + y), totals[i].at[d], load_sem.at[1 + i, d])
    small_y = remote(small_ref, sy, s_send.at[0], s_recv.at[0], "fsdp", peer)
    small_y.start()
    for d in range(hi):
        y_copies[0, d].start()
        grad_loads[0, d].start()
    for j in order[1:]:
        for c in range(chunks):
            dn_copy(0, j, c).start()
    for i in tensors[1:]:
        for d in range(hi):
            y_copies[i, d].start()
            grad_loads[i, d].start()
    for c in loads:
        c.wait()
    for level, (bit, keep, slots) in enumerate(levels):
        later = levels[level + 1 :]
        for j in sorted(keep, reverse=True):
            for c in range(chunks):
                if level == len(levels) - 1:
                    continue
                dn_copy(level, j, c).wait_recv()
                at = piece_rows(c)
                own = dn_own[j // 2, at].astype(f32) if level == 0 else dn_low[j // 2, at].astype(f32)
                if j == 0:
                    own = own if level == 0 else dn_acc[at]
                    dn_acc[at] = own + dn_in[slots[j], at].astype(f32)
                else:
                    dn_low[j // 2, at] = (own + dn_in[slots[j], at].astype(f32)).astype(bf16)
                    nxt = later[0]
                    if j & nxt[0]:
                        dn_copy(level + 1, j ^ nxt[0], c).start()

    small_y.wait_recv()
    sz[z] = small_ref[...] + sy[...]
    small_z = []
    for k in range(1, hi):
        target = lax.rem(z + k, hi)
        small_z.append(remote(sz.at[z], sz.at[z], s_send.at[k], s_recv.at[k], "fsdp", target * lo + y))
        small_z[-1].start()

    def reduce_tensor(i):
        total = totals[i]
        for d in range(hi):
            grad_loads[i, d].wait()
            y_copies[i, d].wait_recv()
            total[d] = (total[d].astype(f32) + from_y[i][d].astype(f32)).astype(bf16)
        from_right, from_left = from_z[i]
        for t in range(hi - 1):
            d = t - (hi - 1 - z)
            m = hi - 1 - (t - z)

            @pl.when((d >= 0) & (d < z))
            def _():
                at = jnp.clip(d, 0, hi - 1)
                remote(
                    total.at[at], from_right.at[t], z_send.at[i, 0, t], z_recv.at[i, 0, t], "fsdp", (z - 1) * lo + y
                ).start()

            @pl.when((m > z) & (m < hi))
            def _():
                at = jnp.clip(m, 0, hi - 1)
                remote(
                    total.at[at], from_left.at[t], z_send.at[i, 1, t], z_recv.at[i, 1, t], "fsdp", (z + 1) * lo + y
                ).start()

            dr = t - (hi - 2 - z)

            @pl.when((z + 1 < hi) & (dr >= 0))
            def _():
                at = jnp.clip(dr, 0, hi - 1)
                remote(
                    total.at[at], from_right.at[t], z_send.at[i, 0, t], z_recv.at[i, 0, t], "fsdp", f
                ).wait_recv()
                total[at] = (total[at].astype(f32) + from_right[t].astype(f32)).astype(bf16)

            ml = hi - 1 - (t - (z - 1))

            @pl.when((z > 0) & (ml < hi))
            def _():
                at = jnp.clip(ml, 0, hi - 1)
                remote(
                    total.at[at], from_left.at[t], z_send.at[i, 1, t], z_recv.at[i, 1, t], "fsdp", f
                ).wait_recv()
                total[at] = (total[at].astype(f32) + from_left[t].astype(f32)).astype(bf16)

    exchanged = (xq, xu)
    results = (rq_ref, ru_ref, rd_ref, ro_ref)

    def exchange(i):
        for k in range(1, seq):
            remote(
                totals[i].at[z, me ^ k], exchanged[i].at[me], x_send.at[i, k], x_recv.at[i, k], "seq", me ^ k
            ).start()

    reduce_tensor(0)
    exchange(0)

    if levels:
        bit, keep, slots = levels[-1]
    gain = gain_ref[...]
    part = jnp.zeros((8, gain.shape[1]), f32)
    for c in range(chunks):
        at = piece_rows(c)
        if levels:
            dn_copy(len(levels) - 1, 0, c).wait_recv()
        if len(levels) > 1:
            dn = dn_acc[at]
        else:
            dn = dn_own[0, at].astype(f32)
        if levels:
            dn = dn + dn_in[slots[0], at].astype(f32)
        x = tok_ref[at].astype(f32)
        rho = lax.rsqrt(jnp.mean(x * x, axis=-1, keepdims=True) + EPSILON)
        scaled = gain * dn
        mean = jnp.mean(x * scaled, axis=-1, keepdims=True)
        tg_ref[at] = dmid_ref[at] + rho * scaled - x * (rho * rho * rho * mean)
        prod = dn * x * rho
        part += functools.reduce(jnp.add, [prod[n : n + 8] for n in range(0, rows, 8)])
    gains[0:8] = mlp_gain_ref[...]
    gains[8:16] = part
    gain_y = remote(gains, gy, g_send.at[0], g_recv.at[0], "fsdp", peer)
    gain_y.start()
    reduce_tensor(1)
    exchange(1)
    gain_y.wait_recv()
    gz[z] = gains[...] + gy[...]
    gain_z = []
    for k in range(1, hi):
        target = lax.rem(z + k, hi)
        gain_z.append(remote(gz.at[z], gz.at[z], g_send.at[k], g_recv.at[k], "fsdp", target * lo + y))
        gain_z[-1].start()
    reduce_tensor(2)
    for k in range(1, hi):
        source = lax.rem(z + hi - k, hi)
        remote(gz.at[source], gz.at[source], g_send.at[k], g_recv.at[k], "fsdp", f).wait_recv()
        remote(sz.at[source], sz.at[source], s_send.at[k], s_recv.at[k], "fsdp", f).wait_recv()
    gs[me] = functools.reduce(jnp.add, [gz[d] for d in range(hi)])
    gain_x = []
    for k in range(1, seq):
        gain_x.append(remote(gs.at[me], gs.at[me], g_send.at[hi + k], g_recv.at[hi + k], "seq", me ^ k))
        gain_x[-1].start()
    ssum_ref[...] = functools.reduce(jnp.add, [sz[d] for d in range(hi)])
    reduce_tensor(3)
    rd_ref[...] = td[z].astype(f32)
    ro_ref[...] = to[z].astype(f32)
    for i in range(2):
        for k in range(1, seq):
            remote(
                totals[i].at[z, me], exchanged[i].at[me ^ k], x_send.at[i, k], x_recv.at[i, k], "seq", me
            ).wait_recv()
        exchanged[i][me] = totals[i][z, me]
        for k in range(seq):
            results[i][k] = exchanged[i][k].astype(f32)
    for k in range(1, seq):
        remote(gs.at[me ^ k], gs.at[me ^ k], g_send.at[hi + k], g_recv.at[hi + k], "seq", me).wait_recv()
    gsum_ref[...] = functools.reduce(jnp.add, [gs[k] for k in range(seq)])

    for level, (bit, keep, slots) in enumerate(levels):
        for j in keep:
            for c in range(chunks):
                dn_copy(level, j, c).wait_send()
    for i in tensors:
        for d in range(hi):
            y_copies[i, d].wait_send()
        for t in range(hi - 1):
            d = t - (hi - 1 - z)
            m = hi - 1 - (t - z)

            @pl.when((d >= 0) & (d < z))
            def _():
                remote(
                    totals[i].at[0], from_z[i][0].at[t], z_send.at[i, 0, t], z_recv.at[i, 0, t], "fsdp", f
                ).wait_send()

            @pl.when((m > z) & (m < hi))
            def _():
                remote(
                    totals[i].at[0], from_z[i][1].at[t], z_send.at[i, 1, t], z_recv.at[i, 1, t], "fsdp", f
                ).wait_send()
    for i in range(2):
        for k in range(1, seq):
            remote(
                totals[i].at[z, me], exchanged[i].at[me], x_send.at[i, k], x_recv.at[i, k], "seq", me
            ).wait_send()
    for c in [small_y, gain_y] + small_z + gain_z + gain_x:
        c.wait_send()


def finish(dn, gq, gu, gd, go, small, mlp_gain, tok, dmid, gain, seq, fsdp):
    lo = 2
    hi = fsdp // lo
    chunks = 4
    anywhere = pl.BlockSpec(memory_space=pl.ANY)
    vmem = pl.BlockSpec(memory_space=pltpu.VMEM)
    block_q = (seq,) + gq.shape[2:]
    block_u = (seq,) + gu.shape[2:]
    block_d = gd.shape[1:]
    block_o = go.shape[1:]
    blocks = (block_q, block_u, block_d, block_o)
    tok_rows, dim = tok.shape
    sides = max(hi - 1, 1)

    def buf(lead, shape, kind=bf16):
        return pltpu.VMEM((lead,) + tuple(shape), kind)

    scratch = [
        buf(max(seq // 2, 1), (tok_rows, dim)),
        buf(max(seq - 1, 1), (tok_rows, dim)),
        buf(max(seq // 2, 1), (tok_rows, dim)),
        pltpu.VMEM((tok_rows, dim), f32),
    ]
    scratch += [buf(hi, b) for b in blocks]
    scratch += [buf(hi, b) for b in blocks]
    scratch += [buf(sides, b) for b in (block_q, block_u, block_d)] * 2
    scratch += [buf(sides, block_o), buf(sides, block_o)]
    scratch += [pltpu.VMEM(block_q, bf16), pltpu.VMEM(block_u, bf16)]
    scratch += [
        pltpu.VMEM(small.shape, f32),
        buf(hi, small.shape, f32),
        pltpu.VMEM((16, dim), f32),
        pltpu.VMEM((16, dim), f32),
        buf(hi, (16, dim), f32),
        buf(seq, (16, dim), f32),
    ]
    dma = pltpu.SemaphoreType.DMA
    scratch += [
        dma((5, max(hi, seq))),
        dma((seq, chunks)),
        dma((seq, chunks)),
        dma((4, hi)),
        dma((4, hi)),
        dma((4, 2, hi)),
        dma((4, 2, hi)),
        dma((2, seq)),
        dma((2, seq)),
        dma((hi,)),
        dma((hi,)),
        dma((hi + seq,)),
        dma((hi + seq,)),
    ]
    return pl.pallas_call(
        functools.partial(finish_kernel, seq, hi, lo, chunks),
        out_shape=(
            jax.ShapeDtypeStruct((tok_rows, dim), f32),
            jax.ShapeDtypeStruct(block_q, f32),
            jax.ShapeDtypeStruct(block_u, f32),
            jax.ShapeDtypeStruct(block_d, f32),
            jax.ShapeDtypeStruct(block_o, f32),
            jax.ShapeDtypeStruct(small.shape, f32),
            jax.ShapeDtypeStruct((16, dim), f32),
        ),
        in_specs=[anywhere] * 5 + [vmem] * 5,
        out_specs=(vmem,) * 7,
        scratch_shapes=scratch,
        compiler_params=pltpu.CompilerParams(
            collective_id=1, has_side_effects=True, vmem_limit_bytes=56 << 20
        ),
        name="finish",
    )(dn, gq, gu, gd, go, small, mlp_gain, tok, dmid, gain)


GELU_P = 0.24
GELU_C = (
    0.08951261885080208,
    0.15562094398234086,
    -0.15437154502074169,
    0.6261054138112487,
    -0.6465313024138201,
    0.5547927291245551,
    -0.125128858665134,
)


def gelu_parts(x):
    size = jnp.abs(x)
    t = 1.0 / (1.0 + GELU_P * size)
    poly = GELU_C[-1] * t
    for c in GELU_C[-2::-1]:
        poly = (poly + c) * t
    bell = jnp.exp2(x * x * (-0.5 * LOG2E))
    tail = poly * bell
    cdf = jnp.where(x < 0.0, tail, 1.0 - tail)
    return x * cdf, cdf + x * bell * (1.0 / math.sqrt(2.0 * math.pi))


def mlp_kernel(seq, sub, length_ref, *refs):
    refs = list(refs)

    def take(count):
        taken = refs[:count]
        del refs[:count]
        return taken

    att_refs = take(seq)
    (tok_ref,) = take(1)
    grad_refs = take(seq)
    wo_ref, wu_ref, wd_ref, gain_ref = take(4)
    mid_ref, dmid_ref, gsum_ref, db_ref, mo_ref, ug_ref, dg_ref = take(7)
    att_buf, tok_buf, gm, nm, hid, dpre, low, into, acc = take(9)
    dbv = low.at[0]
    depth = att_buf.shape[0]
    load_sem, gm_sem, dn_send, dn_recv, db_send, db_recv, mo_sem, own_sem = take(8)

    me = lax.axis_index("seq")
    length = length_ref[0]
    dim = wo_ref.shape[0]
    width = dim // seq
    rows = tok_ref.shape[1]
    share = wu_ref.shape[1]
    bits = [1 << i for i in range(seq.bit_length() - 1)]

    barrier = pltpu.get_barrier_semaphore()
    for bit in bits:
        pl.semaphore_signal(barrier, inc=1, device_id={"seq": me ^ bit}, device_id_type=MESH)
    pl.semaphore_wait(barrier, len(bits))

    order = list(reversed(range(seq)))
    gm_loads = {j: pltpu.make_async_copy(grad_refs[j], gm.at[pl.ds(j * rows, rows)], gm_sem.at[j]) for j in order}

    def chunk_loads(n):
        j, slot = order[n], n % depth
        copies = [
            pltpu.make_async_copy(
                att_refs[k].at[pl.ds((j ^ k) * rows, rows)], att_buf.at[slot, k], load_sem.at[slot, k]
            )
            for k in range(seq)
        ]
        copies.append(pltpu.make_async_copy(tok_ref.at[j], tok_buf.at[slot], load_sem.at[slot, seq]))
        return copies

    for c in chunk_loads(0):
        c.start()
    for j in order:
        gm_loads[j].start()

    slots = {}
    for bit in bits:
        for j in range(0, seq, 2 * bit):
            slots[bit, j] = len(slots)

    def dn_copy(bit, j):
        slot = slots[bit, j]
        return pltpu.make_async_remote_copy(
            src_ref=low.at[j ^ bit],
            dst_ref=into.at[slot],
            send_sem=dn_send.at[slot],
            recv_sem=dn_recv.at[slot],
            device_id={"seq": me ^ bit},
            device_id_type=MESH,
        )

    gain = gain_ref[...]
    for n, j in enumerate(order):
        slot = n % depth
        if depth == 1 and n:
            for c in chunk_loads(n):
                c.start()
        for c in chunk_loads(n):
            c.wait()
        if depth == 2 and n + 1 < seq:
            for c in chunk_loads(n + 1):
                c.start()
        gm_loads[j].wait()
        base = (j ^ me) * rows

        @pl.loop(0, rows // sub)
        def _(s):
            at = pl.ds(pl.multiple_of(s * sub, sub), sub)
            here = pl.ds(pl.multiple_of(j * rows + s * sub, sub), sub)
            position = base + s * sub + lax.broadcasted_iota(jnp.int32, (sub, 1), 0)
            live = jnp.where(position < length, 1.0, 0.0)
            masked = (gm[here].astype(f32) * live).astype(bf16)
            gm[here] = masked
            mid = tok_buf[slot, at].astype(f32)
            for k in range(seq):
                own = pl.ds(pl.multiple_of((me ^ k) * width, width), width)
                mid = mid + dot(att_buf[slot, k, at], wo_ref[own])
            rho = lax.rsqrt(jnp.mean(mid * mid, axis=-1, keepdims=True) + EPSILON)
            normed = (mid * rho * gain).astype(bf16)
            nm[here] = normed
            if j == 0:
                mid_ref[at] = mid
            for c in range(0, share, 256):
                cols = slice(c, c + 256)
                value, slope = gelu_parts(dot(normed, wu_ref[:, cols]))
                hid[here, cols] = value.astype(bf16)
                dpre[here, cols] = (dot_t(masked, wd_ref[cols]) * slope).astype(bf16)
            part = dot_t(dpre[here], wu_ref[...])
            if j % 2:
                low[j, at] = part.astype(bf16)
            else:
                acc[at] = part

        if j % 2:
            dn_copy(1, j ^ 1).start()
        elif j:
            for bit in bits:
                if j & bit:
                    low[j] = acc[...].astype(bf16)
                    dn_copy(bit, j ^ bit).start()
                    break
                dn_copy(bit, j).wait_recv()
                acc[...] += into[slots[bit, j]].astype(f32)

    for c in range(0, dim, 256):
        ug_ref[c : c + 256] = t_dot(nm[:, c : c + 256], dpre[...]).astype(bf16)

    for bit in bits:
        dn_copy(bit, 0).wait_recv()
    step = 128
    part = jnp.zeros((8, dim), f32)
    for r in range(0, rows, step):
        at = slice(r, r + step)
        dn = acc[at]
        for bit in bits:
            dn = dn + into[slots[bit, 0], at].astype(f32)
        mid = mid_ref[at]
        rho = lax.rsqrt(jnp.mean(mid * mid, axis=-1, keepdims=True) + EPSILON)
        scaled = gain * dn
        mean = jnp.mean(mid * scaled, axis=-1, keepdims=True)
        dmid = gm[at].astype(f32) + rho * scaled - mid * (rho * rho * rho * mean)
        dmid_ref[at] = dmid
        dbv[at] = dmid.astype(bf16)
        prod = dn * mid * rho
        part += functools.reduce(jnp.add, [prod[i : i + 8] for i in range(0, step, 8)])
    gsum_ref[...] = part

    def db_copy(source, target, bit):
        return pltpu.make_async_remote_copy(
            src_ref=db_ref.at[source] if source else dbv,
            dst_ref=db_ref.at[target],
            send_sem=db_send.at[target],
            recv_sem=db_recv.at[target],
            device_id={"seq": me ^ bit},
            device_id_type=MESH,
        )

    own_copy = pltpu.make_async_copy(dbv, db_ref.at[0], own_sem)
    own_copy.start()
    sends = []
    high = [bit for bit in reversed(bits) if bit > 1]

    def send(source, target, bit):
        sends.append(db_copy(source, target, bit))
        sends[-1].start()

    if high:
        send(0, high[0], high[0])
    if seq > 1:
        send(0, 1, 1)
    for c in range(0, share, 256):
        dg_ref[c : c + 256] = t_dot(hid[:, c : c + 256], gm[...]).astype(bf16)
    mo_copies = []
    for j in range(seq):
        at = slice(j * rows, (j + 1) * rows)
        nm[at] = dot(hid[at], wd_ref[...]).astype(bf16)
        mo_copies.append(pltpu.make_async_copy(nm.at[pl.ds(j * rows, rows)], mo_ref.at[j], mo_sem.at[j]))
        mo_copies[-1].start()
    have = [0]
    for n, bit in enumerate(high):
        if n:
            for j in have:
                send(j, j ^ bit, bit)
        for j in have:
            db_copy(0, j ^ bit, bit).wait_recv()
            send(j ^ bit, j ^ bit ^ 1, 1)
        have += [j ^ bit for j in have]
    if seq > 1:
        for j in have:
            db_copy(0, j ^ 1, 1).wait_recv()
    for c in sends:
        c.wait_send()
    own_copy.wait()
    for c in mo_copies:
        c.wait()
    for bit in bits:
        for j in range(0, seq, 2 * bit):
            dn_copy(bit, j).wait_send()


def mlp(length, atts, tok, grads, wo, wu, wd, gain):
    seq, rows, dim = tok.shape
    share = wu.shape[1]
    sub = 256
    depth = 2 if seq <= 4 else 1
    anywhere = pl.BlockSpec(memory_space=pl.ANY)
    vmem = pl.BlockSpec(memory_space=pltpu.VMEM)
    dma = pltpu.SemaphoreType.DMA
    return pl.pallas_call(
        functools.partial(mlp_kernel, seq, sub),
        out_shape=(
            jax.ShapeDtypeStruct((rows, dim), f32),
            jax.ShapeDtypeStruct((rows, dim), f32),
            jax.ShapeDtypeStruct((8, dim), f32),
            jax.ShapeDtypeStruct((seq, rows, dim), bf16),
            jax.ShapeDtypeStruct((seq, rows, dim), bf16),
            jax.ShapeDtypeStruct((dim, share), bf16),
            jax.ShapeDtypeStruct((share, dim), bf16),
        ),
        in_specs=[pl.BlockSpec(memory_space=pltpu.SMEM)] + [anywhere] * (2 * seq + 1) + [vmem] * 4,
        out_specs=(vmem, vmem, vmem, anywhere, anywhere, vmem, vmem),
        scratch_shapes=[
            pltpu.VMEM((depth, seq, rows, dim // seq), bf16),
            pltpu.VMEM((depth, rows, dim), bf16),
            pltpu.VMEM((seq * rows, dim), bf16),
            pltpu.VMEM((seq * rows, dim), bf16),
            pltpu.VMEM((seq * rows, share), bf16),
            pltpu.VMEM((seq * rows, share), bf16),
            pltpu.VMEM((seq, rows, dim), bf16),
            pltpu.VMEM((max(seq - 1, 1), rows, dim), bf16),
            pltpu.VMEM((rows, dim), f32),
            dma((2, seq + 1)),
            dma((seq,)),
            dma((seq,)),
            dma((seq,)),
            dma((seq,)),
            dma((seq,)),
            dma((seq,)),
            dma,
        ],
        compiler_params=pltpu.CompilerParams(collective_id=2, has_side_effects=True, vmem_limit_bytes=60 << 20),
        cost_estimate=pl.CostEstimate(
            flops=2 * rows * seq * dim * (dim + 6 * share), bytes_accessed=32 << 20, transcendentals=rows * seq * share
        ),
        name="mlp",
    )(length, *atts, tok, *grads, wo, wu, wd, gain)


def swap(value, bit):
    count = lax.axis_size("seq")
    return lax.ppermute(value, "seq", [(i, i ^ bit) for i in range(count)])


def seq_bits():
    count = lax.axis_size("seq")
    return [1 << i for i in reversed(range(1, count.bit_length() - 1))]


def seq_gather(value):
    chunks = {0: value}
    for bit in seq_bits():
        for j in list(chunks):
            chunks[j ^ bit] = swap(chunks[j], bit)
    for j in list(chunks):
        chunks[j ^ 1] = swap(chunks[j], 1)
    return [chunks[j] for j in range(len(chunks))]


def seq_reduce(parts):
    count = len(parts)
    parts = dict(enumerate(parts))
    for j in range(count - 2, -1, -2):
        parts[j] = parts[j].astype(f32) + swap(parts.pop(j ^ 1).astype(bf16), 1).astype(f32)
    for bit in reversed(seq_bits()):
        keep = [j for j in parts if not j & bit]
        for j in sorted(keep, reverse=True):
            parts[j] = parts[j] + swap(parts.pop(j ^ bit).astype(bf16), bit).astype(f32)
    return parts[0]


def bias_table_grad(near, far):
    distance = tile_distance().T[SPAN - NEAR :]
    bucket = np.where((distance >= 0) & (distance < BLOCK), bucket_of(np.clip(distance, 0, BLOCK)), BUCKETS)
    bucket = jnp.asarray(bucket.astype(np.int32))
    columns = [jnp.sum(jnp.where((bucket == i)[None], near, 0.0), axis=(1, 2)) for i in range(BUCKETS)]
    columns[-1] = columns[-1] + jnp.sum(far, axis=(1, 2))
    return jnp.stack(columns, axis=1)


def inverse_rms(values):
    return lax.rsqrt(jnp.mean(values * values, axis=-1, keepdims=True) + EPSILON)


def norm_back(values, gain, rho, grad):
    scaled = gain * grad
    mean = jnp.mean(values * scaled, axis=-1, keepdims=True)
    gain_grad = (grad * values * rho).reshape(-1, 8, values.shape[1])
    return rho * scaled - values * (rho * rho * rho * mean), jnp.sum(gain_grad, axis=0)


def body(
    tokens,
    lengths,
    state_init,
    w_qkv,
    w_out,
    w_up,
    w_down,
    norm_attn,
    norm_mlp,
    rel_bias,
    state_query,
    gate_bias,
    out_grad,
    state_grad,
):
    seq_count = lax.axis_size("seq")
    fsdp_count = lax.axis_size("fsdp")
    seq_at = lax.axis_index("seq")
    heads = H // seq_count
    width = heads * DH
    tok_rows, dim = tokens.shape[1:]
    rows = tok_rows * seq_count
    hidden_all = w_up.shape[1]
    share = hidden_all // (seq_count * fsdp_count)

    own_qkv = lax.dynamic_slice_in_dim(
        w_qkv.reshape(w_qkv.shape[0], 3, seq_count, width), seq_at, 1, axis=2
    ).reshape(w_qkv.shape[0], 3 * width)
    own_up = lax.dynamic_slice_in_dim(w_up, seq_at * (hidden_all // seq_count), hidden_all // seq_count, axis=1)
    own_down = lax.dynamic_slice_in_dim(w_down, seq_at * share, share, axis=0)
    down_w = lax.all_gather(own_down, "fsdp", axis=0, tiled=True)
    up_w = lax.all_gather(own_up, "fsdp", axis=0, tiled=True)
    all_tokens, qkv_w, gains, out_w = gather_start(
        tokens[0], (own_qkv, jnp.stack([norm_attn, norm_mlp]), w_out), seq_count, fsdp_count
    )
    qkv_w = qkv_w.reshape(dim, 3 * width)
    gains = jnp.swapaxes(gains, 0, 1).reshape(2, dim).astype(f32)
    gain_attn, gain_mlp = gains[0], gains[1]
    span = fsdp_count // seq_count
    down_w = down_w.reshape(seq_count, span, share, dim)
    moved = [lax.dynamic_slice_in_dim(down_w, seq_at, 1, axis=0)]
    for k in range(1, seq_count):
        moved.append(swap(lax.dynamic_slice_in_dim(down_w, seq_at ^ k, 1, axis=0), k))
    moved = jnp.concatenate(moved, axis=0)
    moved = [lax.dynamic_slice_in_dim(moved, seq_at ^ k, 1, axis=0) for k in range(seq_count)]
    down_w = jnp.swapaxes(jnp.concatenate(moved, axis=0), 0, 1).reshape(fsdp_count * share, dim)
    all_grad = seq_gather(out_grad[0])

    bias = bias_vector(rel_bias)
    forget = jax.nn.sigmoid(gate_bias)
    forget_row = forget.reshape(1, width)
    chunk_ids = jnp.arange(seq_count, dtype=jnp.int32)
    order = chunk_ids ^ seq_at

    inputs = all_tokens.reshape(rows, dim).astype(f32)
    normed = (inputs * inverse_rms(inputs) * gain_attn).astype(bf16)
    qkv = dot(normed, qkv_w).astype(bf16)
    attended, final_memory, mem, upd, lse, slse = attend(
        qkv, state_init[0], lengths, state_query, forget_row, bias, heads, order
    )

    out_w = out_w.reshape(dim, dim)
    own_out = lax.dynamic_slice_in_dim(out_w, seq_at * width, width, axis=0)
    mid_here, dmid, mlp_gain_grad, dbranch, mlp_parts, up_grad, down_grad = mlp(
        lengths, seq_gather(attended), all_tokens, all_grad, out_w, up_w, down_w, gain_mlp.reshape(1, dim)
    )
    dbranch = dbranch.reshape(rows, dim)
    dattended = dot_t(dbranch, own_out).astype(bf16)
    out_w_grad = t_dot(attended, dbranch)

    dqkv, dquery, dforget, near, far = attend_back(
        qkv, dattended, attended, mem, upd, lse, slse, state_grad[0], lengths, state_query, forget_row, bias, heads, order
    )
    mlp_parts, dqkv = lax.optimization_barrier((mlp_parts, dqkv))
    mlp_out = seq_reduce([mlp_parts[j] for j in range(seq_count)])
    live_here = (seq_at * tok_rows + jnp.arange(tok_rows, dtype=jnp.int32) < lengths[0]).astype(f32)[:, None]
    output = (live_here * (mid_here + mlp_out)).astype(bf16)[None]
    dnormed = dot_t(dqkv, qkv_w).astype(bf16).reshape(seq_count, tok_rows, dim)
    piece = dim // (seq_count * fsdp_count)
    qkv_grad = t_dot(normed, dqkv).astype(bf16).reshape(seq_count, fsdp_count, piece, 3 * width)
    up_grad = up_grad.reshape(seq_count, fsdp_count, piece, hidden_all // seq_count)
    down_grad = down_grad.reshape(fsdp_count, share, dim)
    out_w_grad = out_w_grad.astype(bf16).reshape(fsdp_count, piece, dim)
    grad_gate = dforget.reshape(heads, DH) * forget * (1.0 - forget)
    grad_table = jnp.pad(bias_table_grad(near, far), ((0, 0), (0, DH - BUCKETS)))
    cut = heads * DH
    small = jnp.concatenate([dquery.reshape(cut, DH), grad_gate, grad_table], axis=0)
    small = jnp.pad(small, ((0, -small.shape[0] % 8), (0, 0)))
    tokens_grad, qkv_part, up_part, down_part, out_part, small, gain_sums = finish(
        dnormed,
        qkv_grad,
        up_grad,
        down_grad,
        out_w_grad,
        small,
        mlp_gain_grad,
        tokens[0],
        dmid,
        gain_attn.reshape(1, dim),
        seq_count,
        fsdp_count,
    )
    tokens_grad = tokens_grad[None]
    dquery = small[:cut].reshape(heads, DH, DH)
    grad_gate = small[cut : cut + heads]
    grad_table = small[cut + heads : cut + 2 * heads, :BUCKETS]
    up_part = jnp.swapaxes(up_part, 0, 1).reshape(piece, hidden_all)
    qkv_part = qkv_part.reshape(seq_count, piece, 3, width)
    qkv_part = jnp.transpose(qkv_part, (1, 2, 0, 3)).reshape(piece, 3 * H * DH)
    gain_sums = jnp.sum(gain_sums.reshape(2, 8, seq_count * fsdp_count, piece), axis=1)
    mine = seq_at * fsdp_count + lax.axis_index("fsdp")
    gain_sums = lax.dynamic_slice_in_dim(gain_sums, mine, 1, axis=1)[:, 0]
    mlp_gain_grad, attn_gain_grad = gain_sums[0], gain_sums[1]
    return (
        output,
        final_memory[None],
        tokens_grad,
        qkv_part,
        out_part,
        up_part,
        down_part,
        attn_gain_grad,
        mlp_gain_grad,
        grad_table,
        dquery,
        grad_gate,
    )


def solution(mesh):
    placed = (
        P("fsdp", "seq", None),
        P("fsdp"),
        P("fsdp", None, "seq"),
        P("fsdp", None),
        P("fsdp", None),
        P("fsdp", None),
        P("fsdp", None),
        P("fsdp"),
        P("fsdp"),
        P("seq", None),
        P("seq", None, None),
        P("seq", None),
        P("fsdp", "seq", None),
        P("fsdp", None, "seq"),
    )
    return jax.shard_map(
        body,
        mesh=mesh,
        in_specs=placed,
        out_specs=(
            P("fsdp", "seq", None),
            P("fsdp", None, "seq"),
            P("fsdp", "seq", None),
            P(("seq", "fsdp"), None),
            P(("seq", "fsdp"), None),
            P(("seq", "fsdp"), None),
            P(("seq", "fsdp"), None),
            P(("seq", "fsdp")),
            P(("seq", "fsdp")),
            P("seq", None),
            P("seq", None, None),
            P("seq", None),
        ),
        check_vma=False,
    )
```

```python
import functools
import math

import jax
import jax.numpy as jnp
import numpy as np
from jax import lax
from jax.experimental import pallas as pl
from jax.experimental.pallas import tpu as pltpu
from jax.sharding import PartitionSpec as P

H = 8
DH = 128
BLOCK = 512
STATE_VECTORS = 512
QTILE = 256
SPAN = BLOCK + QTILE

EPSILON = 1e-06
BUCKET_EDGES = (19, 21, 24, 27, 31, 35, 40, 46, 52, 59, 67, 77, 87, 99, 113)
BUCKETS = 32
LOG2E = math.log2(math.e)
SCALE = DH ** (-0.5)
NEAR = 384

f32 = jnp.float32
bf16 = jnp.bfloat16
MESH = pl.DeviceIdType.MESH


def bucket_of(distance):
    return np.minimum(distance, 16) + (distance[..., None] >= np.array(BUCKET_EDGES)).sum(-1)


def tile_distance():
    rows = np.arange(QTILE)[:, None]
    cols = np.arange(SPAN)[None, :]
    return rows + BLOCK - cols


def bias_vector(table):
    distance = BLOCK - np.arange(2 * BLOCK)
    inside = (distance >= 0) & (distance < BLOCK)
    bucket = jnp.asarray(np.where(inside, bucket_of(np.clip(distance, 0, BLOCK)), BUCKETS).astype(np.int32))
    total = jnp.full((table.shape[0], 2 * BLOCK), -jnp.inf, f32)
    for i in range(BUCKETS):
        total = jnp.where((bucket == i)[None], table[:, i : i + 1] * LOG2E, total)
    return total


def tile_bias(vector_ref, head):
    wide = jnp.broadcast_to(vector_ref[head : head + 1, :], (QTILE, 2 * BLOCK))
    return pltpu.roll(wide, 0, 1, stride=1, stride_axis=0)[:, :SPAN]


def dot(a, b):
    return jnp.dot(a, b, preferred_element_type=f32)


def dot_t(a, b):
    return lax.dot_general(a, b, (((1,), (1,)), ((), ())), preferred_element_type=f32)


def t_dot(a, b):
    return lax.dot_general(a, b, (((0,), (0,)), ((), ())), preferred_element_type=f32)


def to_row(column):
    wide = jnp.broadcast_to(column, (column.shape[0], 128))
    return wide.T[0:1, :]


def context_pieces(tile):
    start = tile * QTILE
    pieces = []
    if start < BLOCK:
        pieces.append((0, start, BLOCK, 0))
    pieces.append((1, 0, start + QTILE, BLOCK - start))
    return pieces


def softmax_parts(scores):
    top = functools.reduce(jnp.maximum, [jnp.max(s, axis=-1, keepdims=True) for s in scores])
    raised = [jnp.exp2(s - top) for s in scores]
    total = functools.reduce(jnp.add, [jnp.sum(e, axis=-1, keepdims=True) for e in raised])
    return raised, total, top + jnp.log2(total)


def line_gather(hi, lo, slot, count, z_send, z_recv, y_send, y_recv):
    f = lax.axis_index("fsdp")
    z, y = f // lo, f % lo

    def copy(i, origin, target, send, recv):
        ref = slot(i, origin)
        return pltpu.make_async_remote_copy(
            src_ref=ref, dst_ref=ref, send_sem=send, recv_sem=recv, device_id={"fsdp": target}, device_id_type=MESH
        )

    def right(i, t):
        return copy(i, (z - t) * lo + y, (z + 1) * lo + y, z_send.at[i, 0, t], z_recv.at[i, 0, t])

    def left(i, t):
        return copy(i, (z + t) * lo + y, (z - 1) * lo + y, z_send.at[i, 1, t], z_recv.at[i, 1, t])

    def across(i, d):
        return copy(i, (z + d) * lo + y, z * lo + 1 - y, y_send.at[i, d + hi - 1], y_recv.at[i, d + hi - 1])

    def start(i):
        pl.when(z + 1 < hi)(lambda: right(i, 0).start())
        pl.when(z >= 1)(lambda: left(i, 0).start())
        across(i, 0).start()

    def step(i, t):
        @pl.when(z - 1 - t >= 0)
        def _():
            copy(i, (z - 1 - t) * lo + y, f, z_send.at[i, 0, t], z_recv.at[i, 0, t]).wait_recv()
            if t + 1 < hi - 1:
                pl.when(z + 1 < hi)(lambda: right(i, t + 1).start())
            across(i, -1 - t).start()

        @pl.when(z + 1 + t < hi)
        def _():
            copy(i, (z + 1 + t) * lo + y, f, z_send.at[i, 1, t], z_recv.at[i, 1, t]).wait_recv()
            if t + 1 < hi - 1:
                pl.when(z >= 1)(lambda: left(i, t + 1).start())
            across(i, 1 + t).start()

    def arrive(i):
        for d in range(1 - hi, hi):

            @pl.when((z + d >= 0) & (z + d < hi))
            def _():
                copy(
                    i, (z + d) * lo + 1 - y, f, y_send.at[i, d + hi - 1], y_recv.at[i, d + hi - 1]
                ).wait_recv()

    def drain(i):
        for d in range(1 - hi, hi):

            @pl.when((z + d >= 0) & (z + d < hi))
            def _():
                across(i, d).wait_send()

        for t in range(hi - 1):

            @pl.when((z + 1 < hi) & (z - t >= 0))
            def _():
                right(i, t).wait_send()

            @pl.when((z >= 1) & (z + t < hi))
            def _():
                left(i, t).wait_send()

    return start, step, arrive, drain


def line_sems(count, hi):
    dma = pltpu.SemaphoreType.DMA
    return [dma((count, 2, hi)), dma((count, 2, hi)), dma((count, 2 * hi)), dma((count, 2 * hi))]


def greet(seq_targets, hi, lo):
    me = lax.axis_index("seq")
    f = lax.axis_index("fsdp")
    z, y = f // lo, f % lo
    barrier = pltpu.get_barrier_semaphore()
    for k in seq_targets:
        pl.semaphore_signal(barrier, inc=1, device_id={"seq": me ^ k}, device_id_type=MESH)
    near = (lax.rem(z + 1, hi) * lo + y, lax.rem(z + hi - 1, hi) * lo + y, z * lo + 1 - y)
    for target in near:
        pl.semaphore_signal(barrier, inc=1, device_id={"fsdp": target}, device_id_type=MESH)
    pl.semaphore_wait(barrier, len(seq_targets) + len(near))


def attend_kernel(
    heads,
    seq,
    hi,
    lo,
    length_ref,
    qkv_ref,
    init_ref,
    query_ref,
    forget_ref,
    vector_ref,
    own_out_ref,
    own_down_ref,
    att_ref,
    others_ref,
    outs_ref,
    downs_ref,
    final_ref,
    mem_ref,
    upd_ref,
    lse_ref,
    slse_ref,
    memory_ref,
    bias_ref,
    own_sem,
    att_send,
    att_recv,
    out_send,
    out_recv,
    z_send,
    z_recv,
    y_send,
    y_recv,
):
    me = lax.axis_index("seq")
    f = lax.axis_index("fsdp")
    length = length_ref[0]
    width = heads * DH
    scale2 = SCALE * LOG2E
    blocks = seq
    bits = [1 << i for i in range(seq.bit_length() - 1)]
    greet(bits, hi, lo)

    own_copies = [
        pltpu.make_async_copy(own_down_ref, downs_ref.at[f], own_sem.at[0]),
        pltpu.make_async_copy(own_out_ref, outs_ref.at[:, me], own_sem.at[1]),
    ]
    for c in own_copies:
        c.start()

    def lowest(k):
        return k & -k

    def out_copy(k):
        return pltpu.make_async_remote_copy(
            src_ref=outs_ref.at[:, me ^ k ^ lowest(k)],
            dst_ref=outs_ref.at[:, me ^ k ^ lowest(k)],
            send_sem=out_send.at[k],
            recv_sem=out_recv.at[k],
            device_id={"seq": me ^ lowest(k)},
            device_id_type=MESH,
        )

    def out_arrival(k):
        return pltpu.make_async_remote_copy(
            src_ref=outs_ref.at[:, me ^ k],
            dst_ref=outs_ref.at[:, me ^ k],
            send_sem=out_send.at[k],
            recv_sem=out_recv.at[k],
            device_id={"seq": me},
            device_id_type=MESH,
        )

    def att_copy(k, b):
        bit = lowest(k)
        came = k ^ bit
        here = pl.ds(pl.multiple_of((b ^ me) * BLOCK, BLOCK), BLOCK)
        there = pl.ds(pl.multiple_of((b ^ me ^ bit) * BLOCK, BLOCK), BLOCK)
        src = others_ref.at[came, here] if came else att_ref.at[here]
        return pltpu.make_async_remote_copy(
            src_ref=src,
            dst_ref=others_ref.at[k, there],
            send_sem=att_send.at[k, b],
            recv_sem=att_recv.at[k, b],
            device_id={"seq": me ^ bit},
            device_id_type=MESH,
        )

    def att_arrival(k, b):
        here = pl.ds(pl.multiple_of((b ^ me) * BLOCK, BLOCK), BLOCK)
        return pltpu.make_async_remote_copy(
            src_ref=others_ref.at[k, here],
            dst_ref=others_ref.at[k, here],
            send_sem=att_send.at[k, b],
            recv_sem=att_recv.at[k, b],
            device_id={"seq": me},
            device_id_type=MESH,
        )

    passing = sorted([k for k in range(2, seq, 2)], key=lambda k: (bin(k).count("1"), -k))

    def onward(k, send):
        for bit in reversed(bits):
            if bit < lowest(k):
                send(k | bit)

    start, step, arrive, drain = line_gather(
        hi, lo, lambda i, origin: downs_ref.at[origin], 1, z_send, z_recv, y_send, y_recv
    )

    memory_ref[...] = init_ref[...].astype(f32)
    for head in range(heads):
        bias_ref[head] = tile_bias(vector_ref, head)
    for c in own_copies:
        c.wait()
    start(0)
    for bit in reversed(bits):
        out_copy(bit).start()

    @pl.loop(0, blocks)
    def _(block):
        cur_at = pl.multiple_of((block ^ me) * BLOCK, BLOCK)
        prev_at = pl.multiple_of((jnp.maximum(block - 1, 0) ^ me) * BLOCK, BLOCK)
        cur_ref = qkv_ref.at[pl.ds(cur_at, BLOCK)]
        prev_ref = qkv_ref.at[pl.ds(prev_at, BLOCK)]
        for t in range(min(hi - 1, blocks - 1)):
            pl.when(block == t + 1)(lambda t=t: step(0, t))

        live_block = block * BLOCK < length
        for head in range(heads):
            own = slice(head * DH, (head + 1) * DH)
            memory = memory_ref[:, own]
            low = memory.astype(bf16)
            mem_ref[block, :, own] = memory
            refs = (prev_ref, cur_ref)
            key_cols = slice(width + head * DH, width + (head + 1) * DH)
            value_cols = slice(2 * width + head * DH, 2 * width + (head + 1) * DH)
            for tile in range(BLOCK // QTILE):
                rows = slice(tile * QTILE, (tile + 1) * QTILE)
                query = cur_ref[rows, own]
                scores, values = [], []
                for which, at, end, col in context_pieces(tile):
                    s = dot_t(query, refs[which][at:end, key_cols])
                    position = (block - 1 + which) * BLOCK + at + lax.broadcasted_iota(jnp.int32, (1, end - at), 1)
                    live = (position >= 0) & (position < length)
                    s = s * scale2 + bias_ref[head, :, col : col + end - at]
                    scores.append(jnp.where(live, s, -jnp.inf))
                    values.append(refs[which][at:end, value_cols])
                scores.append(dot_t(query, low) * scale2)
                values.append(low)
                raised, total, lse = softmax_parts(scores)
                out = functools.reduce(jnp.add, [dot(e.astype(bf16), v) for e, v in zip(raised, values)])
                att_ref[pl.ds(cur_at + tile * QTILE, QTILE), own] = (out / total).astype(bf16)
                lse_ref[head : head + 1, pl.ds(pl.multiple_of(block * BLOCK, BLOCK) + tile * QTILE, QTILE)] = to_row(lse)
            own_key = cur_ref[:, key_cols]
            own_value = cur_ref[:, value_cols]
            squeries = dot(low, query_ref[head]).astype(bf16)
            position = block * BLOCK + lax.broadcasted_iota(jnp.int32, (1, BLOCK), 1)
            for tile in range(STATE_VECTORS // QTILE):
                rows = slice(tile * QTILE, (tile + 1) * QTILE)
                squery = squeries[rows]
                scores = [
                    dot_t(squery, low) * scale2,
                    jnp.where(position < length, dot_t(squery, own_key) * scale2, -jnp.inf),
                ]
                raised, total, lse = softmax_parts(scores)
                update = dot(raised[0].astype(bf16), low) + dot(raised[1].astype(bf16), own_value)
                update = update / total
                upd_ref[block, rows, own] = update
                slse_ref[head : head + 1, pl.ds(pl.multiple_of(block * BLOCK, BLOCK) + tile * QTILE, QTILE)] = to_row(
                    lse
                )
                forget = forget_ref[:, own]
                old = memory[rows]
                memory_ref[rows, own] = jnp.where(live_block, forget * old + (1.0 - forget) * update, old)

        for bit in reversed(bits):
            att_copy(bit, block).start()

        @pl.when(block == 0)
        def _():
            for k in passing:
                out_arrival(k).wait_recv()
                onward(k, lambda target: out_copy(target).start())

        @pl.when(block >= 1)
        def _():
            for k in passing:
                att_arrival(k, block - 1).wait_recv()
                onward(k, lambda target: att_copy(target, block - 1).start())

    final_ref[...] = memory_ref[...]
    for t in range(min(hi - 1, blocks - 1), hi - 1):
        step(0, t)
    for k in passing:
        att_arrival(k, blocks - 1).wait_recv()
        onward(k, lambda target: att_copy(target, blocks - 1).start())
    arrive(0)
    for k in range(1, seq, 2):
        out_arrival(k).wait_recv()
        for b in range(blocks):
            att_arrival(k, b).wait_recv()
    drain(0)
    for k in range(1, seq):
        out_copy(k).wait_send()
        for b in range(blocks):
            att_copy(k, b).wait_send()


def attend(qkv, init, length, state_query, forget, bias, own_out, own_down, heads, seq, fsdp):
    rows, width3 = qkv.shape
    width = heads * DH
    blocks = rows // BLOCK
    lo = 2
    hi = fsdp // lo
    dim = own_down.shape[1]
    anywhere = pl.BlockSpec(memory_space=pl.ANY)
    vmem = pl.BlockSpec(memory_space=pltpu.VMEM)
    dma = pltpu.SemaphoreType.DMA
    return pl.pallas_call(
        functools.partial(attend_kernel, heads, seq, hi, lo),
        out_shape=(
            jax.ShapeDtypeStruct((rows, width), bf16),
            jax.ShapeDtypeStruct((seq, rows, width), bf16),
            jax.ShapeDtypeStruct((fsdp, seq) + own_out.shape[1:], bf16),
            jax.ShapeDtypeStruct((fsdp,) + own_down.shape, bf16),
            jax.ShapeDtypeStruct((STATE_VECTORS, width), f32),
            jax.ShapeDtypeStruct((blocks, STATE_VECTORS, width), f32),
            jax.ShapeDtypeStruct((blocks, STATE_VECTORS, width), f32),
            jax.ShapeDtypeStruct((heads, rows), f32),
            jax.ShapeDtypeStruct((heads, blocks * STATE_VECTORS), f32),
        ),
        in_specs=[pl.BlockSpec(memory_space=pltpu.SMEM)] + [vmem] * 5 + [anywhere] * 2,
        out_specs=(vmem, anywhere, anywhere, anywhere, vmem, vmem, vmem, vmem, vmem),
        scratch_shapes=[
            pltpu.VMEM((STATE_VECTORS, width), f32),
            pltpu.VMEM((heads, QTILE, SPAN), f32),
            dma((2,)),
            dma((seq, blocks)),
            dma((seq, blocks)),
            dma((seq,)),
            dma((seq,)),
        ]
        + line_sems(1, hi),
        compiler_params=pltpu.CompilerParams(collective_id=3, has_side_effects=True, vmem_limit_bytes=40 << 20),
        cost_estimate=pl.CostEstimate(
            flops=blocks * heads * 512 * 2400 * 128 * 4, bytes_accessed=16 << 20, transcendentals=10 << 20
        ),
        name="attend",
    )(length, qkv, init, state_query, forget, bias, own_out, own_down)


def attend_back_kernel(
    heads,
    blocks,
    length_ref,
    order_ref,
    cur_ref,
    prev_ref,
    dout_ref,
    out_ref,
    mem_ref,
    upd_ref,
    lse_ref,
    slse_ref,
    sgrad_ref,
    query_ref,
    forget_ref,
    vector_ref,
    dqkv_ref,
    dquery_ref,
    dforget_ref,
    near_ref,
    far_ref,
    dmem_ref,
    dnext_ref,
    dctx_ref,
    bias_ref,
):
    step = pl.program_id(0)
    block = blocks - 1 - step
    length = length_ref[0]
    width = heads * DH
    scale2 = SCALE * LOG2E

    @pl.when(step == 0)
    def _():
        dmem_ref[...] = sgrad_ref[...].astype(f32)
        dnext_ref[...] = jnp.zeros_like(dnext_ref)
        dquery_ref[...] = jnp.zeros_like(dquery_ref)
        dforget_ref[...] = jnp.zeros_like(dforget_ref)
        near_ref[...] = jnp.zeros_like(near_ref)
        far_ref[...] = jnp.zeros_like(far_ref)
        for head in range(heads):
            bias_ref[head] = tile_bias(vector_ref, head).T

    live_block = block * BLOCK < length
    refs = (prev_ref, cur_ref)
    for head in range(heads):
        own = slice(head * DH, (head + 1) * DH)
        key_cols = slice(width + head * DH, width + (head + 1) * DH)
        value_cols = slice(2 * width + head * DH, 2 * width + (head + 1) * DH)
        memory = mem_ref[0, :, own]
        update = upd_ref[0, :, own]
        low = memory.astype(bf16)
        forget = forget_ref[:, own]
        dmem = dmem_ref[:, own]
        dupd = jnp.where(live_block, (1.0 - forget) * dmem, 0.0).astype(bf16)
        moved = jnp.where(live_block, dmem * (memory - update), 0.0)
        dforget_ref[:, own] += jnp.sum(moved, axis=0, keepdims=True)
        dmem_new = jnp.where(live_block, forget * dmem, dmem)
        own_key = cur_ref[:, key_cols]
        own_value = cur_ref[:, value_cols]
        squeries = dot(low, query_ref[head]).astype(bf16)
        sdelta = jnp.sum((dupd.astype(f32) * update).T, axis=0, keepdims=True)
        slse = slse_ref[head : head + 1, :]
        dsquery = jnp.zeros((STATE_VECTORS, DH), f32)
        dkey = []
        dvalue = []
        for part in range(2 * STATE_VECTORS // QTILE):
            own_part = part >= STATE_VECTORS // QTILE
            lo = (part % (STATE_VECTORS // QTILE)) * QTILE
            keys = (own_key if own_part else low)[lo : lo + QTILE]
            values = (own_value if own_part else low)[lo : lo + QTILE]
            s = dot_t(keys, squeries) * scale2 - slse
            if own_part:
                position = block * BLOCK + lo + lax.broadcasted_iota(jnp.int32, (QTILE, 1), 0)
                s = jnp.where(position < length, s, -jnp.inf)
            p = jnp.exp2(s)
            dp = dot_t(values, dupd)
            ds = (p * (dp - sdelta)).astype(bf16)
            dvalue.append(dot(p.astype(bf16), dupd))
            dkey.append(dot(ds, squeries))
            dsquery += t_dot(ds, keys)
        half = STATE_VECTORS // QTILE
        dlow = [dvalue[i] + dkey[i] * SCALE for i in range(half)]
        dctx_ref[0, 0:BLOCK] = jnp.zeros((BLOCK, DH), f32)
        dctx_ref[1, 0:BLOCK] = jnp.zeros((BLOCK, DH), f32)
        for i in range(half):
            rows = slice(BLOCK + i * QTILE, BLOCK + (i + 1) * QTILE)
            old = slice(i * QTILE, (i + 1) * QTILE)
            dctx_ref[0, rows] = dkey[half + i] * SCALE + dnext_ref[0, old, own]
            dctx_ref[1, rows] = dvalue[half + i] + dnext_ref[1, old, own]
        dsq = (dsquery * SCALE).astype(bf16)
        dquery_ref[head] += t_dot(low, dsq)
        dmem_ref[:, own] = dmem_new + dot_t(dsq, query_ref[head])
        for tile in range(BLOCK // QTILE):
            rows = slice(tile * QTILE, (tile + 1) * QTILE)
            query = cur_ref[rows, own]
            dout = dout_ref[rows, own]
            lse = lse_ref[head : head + 1, rows]
            delta = jnp.sum((dout.astype(f32) * out_ref[rows, own].astype(f32)).T, axis=0, keepdims=True)
            dq = jnp.zeros((QTILE, DH), f32)
            for which, lo, hi, col in context_pieces(tile):
                for at in range(lo, hi, QTILE):
                    keys = refs[which][at : at + QTILE, key_cols]
                    values = refs[which][at : at + QTILE, value_cols]
                    band = col + at - lo
                    position = (block - 1 + which) * BLOCK + at + lax.broadcasted_iota(jnp.int32, (QTILE, 1), 0)
                    live = (position >= 0) & (position < length)
                    s = dot_t(keys, query) * scale2 + bias_ref[head, band : band + QTILE, :] - lse
                    p = jnp.exp2(jnp.where(live, s, -jnp.inf))
                    dp = dot_t(values, dout)
                    ds = (p * (dp - delta)).astype(bf16)
                    wide = ds.astype(f32)
                    if band + QTILE <= SPAN - NEAR:
                        far_ref[head] += functools.reduce(jnp.add, [wide[i : i + 8] for i in range(0, QTILE, 8)])
                    else:
                        edge = max(SPAN - NEAR - band, 0)
                        if edge:
                            far_ref[head] += functools.reduce(jnp.add, [wide[i : i + 8] for i in range(0, edge, 8)])
                        at_near = band + edge - (SPAN - NEAR)
                        near_ref[head, at_near : at_near + QTILE - edge] += wide[edge:]
                    into = slice(which * BLOCK + at, which * BLOCK + at + QTILE)
                    dctx_ref[1, into] += dot(p.astype(bf16), dout)
                    dctx_ref[0, into] += dot(ds, query) * SCALE
                    dq += t_dot(ds, keys)
            for part in range(half):
                keys = low[part * QTILE : (part + 1) * QTILE]
                s = dot_t(keys, query) * scale2 - lse
                p = jnp.exp2(s)
                dp = dot_t(keys, dout)
                ds = (p * (dp - delta)).astype(bf16)
                dlow[part] += dot(p.astype(bf16), dout) + dot(ds, query) * SCALE
                dq += t_dot(ds, keys)
            dqkv_ref[rows, own] = (dq * SCALE).astype(bf16)
        for part in range(half):
            dmem_ref[part * QTILE : (part + 1) * QTILE, own] += dlow[part]
        dnext_ref[0, :, own] = dctx_ref[0, 0:BLOCK]
        dnext_ref[1, :, own] = dctx_ref[1, 0:BLOCK]
        dqkv_ref[:, key_cols] = dctx_ref[0, BLOCK:].astype(bf16)
        dqkv_ref[:, value_cols] = dctx_ref[1, BLOCK:].astype(bf16)


def attend_back(qkv, dout, out, mem, upd, lse, slse, sgrad, length, state_query, forget, bias, heads, order):
    rows, width3 = qkv.shape
    width = heads * DH
    blocks = rows // BLOCK
    last = blocks - 1
    return pl.pallas_call(
        functools.partial(attend_back_kernel, heads, blocks),
        out_shape=(
            jax.ShapeDtypeStruct((rows, width3), bf16),
            jax.ShapeDtypeStruct((heads, DH, DH), f32),
            jax.ShapeDtypeStruct((1, width), f32),
            jax.ShapeDtypeStruct((heads, NEAR, QTILE), f32),
            jax.ShapeDtypeStruct((heads, 8, QTILE), f32),
        ),
        grid_spec=pltpu.PrefetchScalarGridSpec(
            num_scalar_prefetch=2,
            grid=(blocks,),
            in_specs=[
                pl.BlockSpec((BLOCK, width3), lambda b, _, at: (at[last - b], 0)),
                pl.BlockSpec((BLOCK, width3), lambda b, _, at: (at[jnp.maximum(last - b - 1, 0)], 0)),
                pl.BlockSpec((BLOCK, width), lambda b, _, at: (at[last - b], 0)),
                pl.BlockSpec((BLOCK, width), lambda b, _, at: (at[last - b], 0)),
                pl.BlockSpec((1, STATE_VECTORS, width), lambda b, _, at: (last - b, 0, 0)),
                pl.BlockSpec((1, STATE_VECTORS, width), lambda b, _, at: (last - b, 0, 0)),
                pl.BlockSpec((heads, BLOCK), lambda b, _, at: (0, last - b)),
                pl.BlockSpec((heads, STATE_VECTORS), lambda b, _, at: (0, last - b)),
                pl.BlockSpec((STATE_VECTORS, width), lambda b, _, at: (0, 0)),
                pl.BlockSpec((heads, DH, DH), lambda b, _, at: (0, 0, 0)),
                pl.BlockSpec((1, width), lambda b, _, at: (0, 0)),
                pl.BlockSpec((heads, 2 * BLOCK), lambda b, _, at: (0, 0)),
            ],
            out_specs=(
                pl.BlockSpec((BLOCK, width3), lambda b, _, at: (at[last - b], 0)),
                pl.BlockSpec((heads, DH, DH), lambda b, _, at: (0, 0, 0)),
                pl.BlockSpec((1, width), lambda b, _, at: (0, 0)),
                pl.BlockSpec((heads, NEAR, QTILE), lambda b, _, at: (0, 0, 0)),
                pl.BlockSpec((heads, 8, QTILE), lambda b, _, at: (0, 0, 0)),
            ),
            scratch_shapes=[
                pltpu.VMEM((STATE_VECTORS, width), f32),
                pltpu.VMEM((2, BLOCK, width), f32),
                pltpu.VMEM((2, 2 * BLOCK, DH), f32),
                pltpu.VMEM((heads, SPAN, QTILE), f32),
            ],
        ),
        compiler_params=pltpu.CompilerParams(vmem_limit_bytes=40 << 20),
        cost_estimate=pl.CostEstimate(
            flops=blocks * heads * 512 * 2400 * 128 * 10, bytes_accessed=20 << 20, transcendentals=10 << 20
        ),
        name="attend_back",
    )(length, order, qkv, qkv, dout, out, mem, upd, lse, slse, sgrad, state_query, forget, bias)


def gather_kernel(
    seq,
    hi,
    lo,
    tok_ref,
    grad_ref,
    wq_ref,
    ga_ref,
    gm_ref,
    wo_ref,
    wu_ref,
    toks_ref,
    grads_ref,
    wqs_ref,
    gas_ref,
    gms_ref,
    wos_ref,
    wus_ref,
    own_sem,
    seq_send,
    seq_recv,
    z_send,
    z_recv,
    y_send,
    y_recv,
):
    me = lax.axis_index("seq")
    f = lax.axis_index("fsdp")
    fsdp = hi * lo
    bits = [1 << i for i in range(seq.bit_length() - 1)]
    greet(bits, hi, lo)

    pairs = ((tok_ref, toks_ref), (grad_ref, grads_ref))

    def seq_copy(i, source, slot, bit):
        src, out = pairs[i]
        return pltpu.make_async_remote_copy(
            src_ref=out.at[source] if source else src,
            dst_ref=out.at[slot],
            send_sem=seq_send.at[i, slot],
            recv_sem=seq_recv.at[i, slot],
            device_id={"seq": me ^ bit},
            device_id_type=MESH,
        )

    sends = []

    def send(i, source, slot, bit):
        sends.append(seq_copy(i, source, slot, bit))
        sends[-1].start()

    high = [bit for bit in reversed(bits) if bit > 1]
    if high:
        send(0, 0, high[0], high[0])
    if seq > 1:
        send(0, 0, 1, 1)

    width = wqs_ref.shape[2] // 3
    share = wus_ref.shape[2] // fsdp
    every = wq_ref.shape[1] // 3
    piece = wos_ref.shape[1]
    copies = [[], [], [], [], []]

    def local(i, src, dst):
        copies[i].append(pltpu.make_async_copy(src, dst, own_sem.at[i, len(copies[i])]))
        copies[i][-1].start()

    for c in range(3):
        cols = pl.ds(pl.multiple_of(c * every + me * width, width), width)
        local(0, wq_ref.at[:, cols], wqs_ref.at[f, :, pl.ds(c * width, width)])
    local(1, ga_ref, gas_ref.at[f])
    local(2, gm_ref, gms_ref.at[f])
    local(3, wo_ref.at[me], wos_ref.at[f])
    if wu_ref.shape[1] == wus_ref.shape[2]:
        local(4, wu_ref, wus_ref.at[f])
    else:
        for c in range(fsdp):
            cols = pl.ds(pl.multiple_of((c * seq + me) * share, share), share)
            local(4, wu_ref.at[:, cols], wus_ref.at[f, :, pl.ds(c * share, share)])
    own_rows = [
        pltpu.make_async_copy(src, out.at[0], own_sem.at[5, i]) for i, (src, out) in enumerate(pairs)
    ]
    for c in own_rows:
        c.start()
    outs = (wqs_ref, gas_ref, gms_ref, wos_ref, wus_ref)
    start, step, arrive, drain = line_gather(
        hi, lo, lambda i, origin: outs[i].at[origin], len(outs), z_send, z_recv, y_send, y_recv
    )
    for i in range(len(outs)):
        for c in copies[i]:
            c.wait()
        start(i)
    if high:
        send(1, 0, high[0], high[0])
    if seq > 1:
        send(1, 0, 1, 1)
    for t in range(hi - 1):
        for i in range(len(outs)):
            step(i, t)
    for i in range(len(pairs)):
        have = [0]
        for n, bit in enumerate(high):
            if n:
                for j in have:
                    send(i, j, j ^ bit, bit)
            for j in have:
                seq_copy(i, 0, j ^ bit, bit).wait_recv()
                send(i, j ^ bit, j ^ bit ^ 1, 1)
            have += [j ^ bit for j in have]
        if seq > 1:
            for j in have:
                seq_copy(i, 0, j ^ 1, 1).wait_recv()
    for i in range(len(outs)):
        arrive(i)
    for i in range(len(outs)):
        drain(i)
    for c in sends:
        c.wait_send()
    for c in own_rows:
        c.wait()


def gather_start(tokens, grads, w_qkv, gain_a, gain_m, w_out, w_up, seq, fsdp):
    lo = 2
    hi = fsdp // lo
    dim_rows, hidden = w_up.shape
    share = hidden // (seq * fsdp)
    if share % 128:
        w_up = lax.dynamic_slice_in_dim(w_up.reshape(dim_rows, fsdp, seq, share), lax.axis_index("seq"), 1, axis=2)
        w_up = w_up.reshape(dim_rows, fsdp * share)
    anywhere = pl.BlockSpec(memory_space=pl.ANY)
    dma = pltpu.SemaphoreType.DMA
    shapes = (
        (seq,) + tokens.shape,
        (seq,) + grads.shape,
        (fsdp, dim_rows, w_qkv.shape[1] // seq),
        (fsdp,) + gain_a.shape,
        (fsdp,) + gain_m.shape,
        (fsdp,) + w_out.shape[1:],
        (fsdp, dim_rows, hidden // seq),
    )
    return pl.pallas_call(
        functools.partial(gather_kernel, seq, hi, lo),
        out_shape=tuple(jax.ShapeDtypeStruct(shape, bf16) for shape in shapes),
        in_specs=[anywhere] * 7,
        out_specs=(anywhere,) * 7,
        scratch_shapes=[dma((6, max(fsdp, 3))), dma((2, seq)), dma((2, seq))] + line_sems(5, hi),
        compiler_params=pltpu.CompilerParams(collective_id=0, has_side_effects=True),
        name="gather_start",
    )(tokens, grads, w_qkv, gain_a, gain_m, w_out, w_up)


def finish_kernel(
    seq,
    hi,
    lo,
    chunks,
    dn_ref,
    gq_ref,
    gu_ref,
    gd_ref,
    go_ref,
    small_ref,
    mlp_gain_ref,
    tok_ref,
    dmid_ref,
    gain_ref,
    tg_ref,
    rq_ref,
    ru_ref,
    rd_ref,
    ro_ref,
    ssum_ref,
    gsum_ref,
    dn_own,
    dn_in,
    dn_low,
    dn_acc,
    tq,
    tu,
    td,
    to,
    yq,
    yu,
    yd,
    yo,
    lq,
    lu,
    ld,
    lq_r,
    lu_r,
    ld_r,
    lo_l,
    lo_r,
    xq,
    xu,
    sy,
    sz,
    gains,
    gy,
    gz,
    gs,
    load_sem,
    dn_send,
    dn_recv,
    y_send,
    y_recv,
    z_send,
    z_recv,
    x_send,
    x_recv,
    s_send,
    s_recv,
    g_send,
    g_recv,
):
    me = lax.axis_index("seq")
    f = lax.axis_index("fsdp")
    z, y = f // lo, f % lo
    peer = z * lo + 1 - y
    grads = (gq_ref, gu_ref, gd_ref, go_ref)
    totals = (tq, tu, td, to)
    from_y = (yq, yu, yd, yo)
    from_z = ((lq, lq_r), (lu, lu_r), (ld, ld_r), (lo_l, lo_r))
    tensors = range(4)
    rows = dn_ref.shape[1] // chunks

    barrier = pltpu.get_barrier_semaphore()
    for k in range(1, seq):
        pl.semaphore_signal(barrier, inc=1, device_id={"seq": me ^ k}, device_id_type=MESH)
    for k in range(1, hi):
        pl.semaphore_signal(barrier, inc=1, device_id={"fsdp": lax.rem(z + k, hi) * lo + y}, device_id_type=MESH)
    pl.semaphore_signal(barrier, inc=1, device_id={"fsdp": peer}, device_id_type=MESH)
    pl.semaphore_wait(barrier, seq + hi - 1)

    def block(i, target):
        return grads[i].at[:, target] if i < 2 else grads[i].at[target]

    def remote(src, dst, send, recv, axis, target):
        return pltpu.make_async_remote_copy(
            src_ref=src, dst_ref=dst, send_sem=send, recv_sem=recv, device_id={axis: target}, device_id_type=MESH
        )

    evens = list(range(0, seq, 2))
    loads = [pltpu.make_async_copy(dn_ref.at[j], dn_own.at[j // 2], load_sem.at[0, j // 2]) for j in evens]
    for c in loads:
        c.start()

    levels = []
    active = list(range(seq))
    bit = 1
    slot = 0
    while bit < seq:
        keep = [j for j in active if not j & bit]
        levels.append((bit, keep, {j: slot + n for n, j in enumerate(keep)}))
        slot += len(keep)
        active = keep
        bit *= 2
    order = sorted(evens, reverse=True)

    def piece_rows(c):
        return pl.ds(c * rows, rows)

    def dn_copy(level, j, c):
        bit, _, slots = levels[level]
        src = dn_ref.at[j ^ bit, piece_rows(c)] if level == 0 else dn_low.at[(j ^ bit) // 2, piece_rows(c)]
        return remote(
            src, dn_in.at[slots[j], piece_rows(c)], dn_send.at[slots[j], c], dn_recv.at[slots[j], c], "seq", me ^ bit
        )

    for c in range(chunks):
        for j in order[:1]:
            dn_copy(0, j, c).start()
    y_copies = {}
    for i in tensors:
        for d in range(hi):
            y_copies[i, d] = remote(
                block(i, d * lo + 1 - y), from_y[i].at[d], y_send.at[i, d], y_recv.at[i, d], "fsdp", peer
            )
    grad_loads = {}
    for i in tensors:
        for d in range(hi):
            grad_loads[i, d] = pltpu.make_async_copy(block(i, d * lo + y), totals[i].at[d], load_sem.at[1 + i, d])
    small_y = remote(small_ref, sy, s_send.at[0], s_recv.at[0], "fsdp", peer)
    small_y.start()
    for d in range(hi):
        y_copies[0, d].start()
        grad_loads[0, d].start()
    for j in order[1:]:
        for c in range(chunks):
            dn_copy(0, j, c).start()
    for i in tensors[1:]:
        for d in range(hi):
            y_copies[i, d].start()
            grad_loads[i, d].start()
    for c in loads:
        c.wait()
    for level, (bit, keep, slots) in enumerate(levels):
        later = levels[level + 1 :]
        for j in sorted(keep, reverse=True):
            for c in range(chunks):
                if level == len(levels) - 1:
                    continue
                dn_copy(level, j, c).wait_recv()
                at = piece_rows(c)
                own = dn_own[j // 2, at].astype(f32) if level == 0 else dn_low[j // 2, at].astype(f32)
                if j == 0:
                    own = own if level == 0 else dn_acc[at]
                    dn_acc[at] = own + dn_in[slots[j], at].astype(f32)
                else:
                    dn_low[j // 2, at] = (own + dn_in[slots[j], at].astype(f32)).astype(bf16)
                    nxt = later[0]
                    if j & nxt[0]:
                        dn_copy(level + 1, j ^ nxt[0], c).start()

    small_y.wait_recv()
    sz[z] = small_ref[...] + sy[...]
    small_z = []
    for k in range(1, hi):
        target = lax.rem(z + k, hi)
        small_z.append(remote(sz.at[z], sz.at[z], s_send.at[k], s_recv.at[k], "fsdp", target * lo + y))
        small_z[-1].start()

    def reduce_tensor(i):
        total = totals[i]
        for d in range(hi):
            grad_loads[i, d].wait()
            y_copies[i, d].wait_recv()
            total[d] = (total[d].astype(f32) + from_y[i][d].astype(f32)).astype(bf16)
        from_right, from_left = from_z[i]
        for t in range(hi - 1):
            d = t - (hi - 1 - z)
            m = hi - 1 - (t - z)

            @pl.when((d >= 0) & (d < z))
            def _():
                at = jnp.clip(d, 0, hi - 1)
                remote(
                    total.at[at], from_right.at[t], z_send.at[i, 0, t], z_recv.at[i, 0, t], "fsdp", (z - 1) * lo + y
                ).start()

            @pl.when((m > z) & (m < hi))
            def _():
                at = jnp.clip(m, 0, hi - 1)
                remote(
                    total.at[at], from_left.at[t], z_send.at[i, 1, t], z_recv.at[i, 1, t], "fsdp", (z + 1) * lo + y
                ).start()

            dr = t - (hi - 2 - z)

            @pl.when((z + 1 < hi) & (dr >= 0))
            def _():
                at = jnp.clip(dr, 0, hi - 1)
                remote(
                    total.at[at], from_right.at[t], z_send.at[i, 0, t], z_recv.at[i, 0, t], "fsdp", f
                ).wait_recv()
                total[at] = (total[at].astype(f32) + from_right[t].astype(f32)).astype(bf16)

            ml = hi - 1 - (t - (z - 1))

            @pl.when((z > 0) & (ml < hi))
            def _():
                at = jnp.clip(ml, 0, hi - 1)
                remote(
                    total.at[at], from_left.at[t], z_send.at[i, 1, t], z_recv.at[i, 1, t], "fsdp", f
                ).wait_recv()
                total[at] = (total[at].astype(f32) + from_left[t].astype(f32)).astype(bf16)

    exchanged = (xq, xu)
    results = (rq_ref, ru_ref, rd_ref, ro_ref)

    def exchange(i):
        for k in range(1, seq):
            remote(
                totals[i].at[z, me ^ k], exchanged[i].at[me], x_send.at[i, k], x_recv.at[i, k], "seq", me ^ k
            ).start()

    reduce_tensor(0)
    exchange(0)

    if levels:
        bit, keep, slots = levels[-1]
    gain = gain_ref[...]
    part = jnp.zeros((8, gain.shape[1]), f32)
    for c in range(chunks):
        at = piece_rows(c)
        if levels:
            dn_copy(len(levels) - 1, 0, c).wait_recv()
        if len(levels) > 1:
            dn = dn_acc[at]
        else:
            dn = dn_own[0, at].astype(f32)
        if levels:
            dn = dn + dn_in[slots[0], at].astype(f32)
        x = tok_ref[at].astype(f32)
        rho = lax.rsqrt(jnp.mean(x * x, axis=-1, keepdims=True) + EPSILON)
        scaled = gain * dn
        mean = jnp.mean(x * scaled, axis=-1, keepdims=True)
        tg_ref[at] = dmid_ref[at] + rho * scaled - x * (rho * rho * rho * mean)
        prod = dn * x * rho
        part += functools.reduce(jnp.add, [prod[n : n + 8] for n in range(0, rows, 8)])
    gains[0:8] = mlp_gain_ref[...]
    gains[8:16] = part
    gain_y = remote(gains, gy, g_send.at[0], g_recv.at[0], "fsdp", peer)
    gain_y.start()
    reduce_tensor(1)
    exchange(1)
    gain_y.wait_recv()
    gz[z] = gains[...] + gy[...]
    gain_z = []
    for k in range(1, hi):
        target = lax.rem(z + k, hi)
        gain_z.append(remote(gz.at[z], gz.at[z], g_send.at[k], g_recv.at[k], "fsdp", target * lo + y))
        gain_z[-1].start()
    reduce_tensor(2)
    for k in range(1, hi):
        source = lax.rem(z + hi - k, hi)
        remote(gz.at[source], gz.at[source], g_send.at[k], g_recv.at[k], "fsdp", f).wait_recv()
        remote(sz.at[source], sz.at[source], s_send.at[k], s_recv.at[k], "fsdp", f).wait_recv()
    gs[me] = functools.reduce(jnp.add, [gz[d] for d in range(hi)])
    gain_x = []
    for k in range(1, seq):
        gain_x.append(remote(gs.at[me], gs.at[me], g_send.at[hi + k], g_recv.at[hi + k], "seq", me ^ k))
        gain_x[-1].start()
    ssum_ref[...] = functools.reduce(jnp.add, [sz[d] for d in range(hi)])
    reduce_tensor(3)
    rd_ref[...] = td[z].astype(f32)
    ro_ref[...] = to[z].astype(f32)
    for i in range(2):
        for k in range(1, seq):
            remote(
                totals[i].at[z, me], exchanged[i].at[me ^ k], x_send.at[i, k], x_recv.at[i, k], "seq", me
            ).wait_recv()
        exchanged[i][me] = totals[i][z, me]
        for k in range(seq):
            results[i][k] = exchanged[i][k].astype(f32)
    for k in range(1, seq):
        remote(gs.at[me ^ k], gs.at[me ^ k], g_send.at[hi + k], g_recv.at[hi + k], "seq", me).wait_recv()
    gsum_ref[...] = functools.reduce(jnp.add, [gs[k] for k in range(seq)])

    for level, (bit, keep, slots) in enumerate(levels):
        for j in keep:
            for c in range(chunks):
                dn_copy(level, j, c).wait_send()
    for i in tensors:
        for d in range(hi):
            y_copies[i, d].wait_send()
        for t in range(hi - 1):
            d = t - (hi - 1 - z)
            m = hi - 1 - (t - z)

            @pl.when((d >= 0) & (d < z))
            def _():
                remote(
                    totals[i].at[0], from_z[i][0].at[t], z_send.at[i, 0, t], z_recv.at[i, 0, t], "fsdp", f
                ).wait_send()

            @pl.when((m > z) & (m < hi))
            def _():
                remote(
                    totals[i].at[0], from_z[i][1].at[t], z_send.at[i, 1, t], z_recv.at[i, 1, t], "fsdp", f
                ).wait_send()
    for i in range(2):
        for k in range(1, seq):
            remote(
                totals[i].at[z, me], exchanged[i].at[me], x_send.at[i, k], x_recv.at[i, k], "seq", me
            ).wait_send()
    for c in [small_y, gain_y] + small_z + gain_z + gain_x:
        c.wait_send()


def finish(dn, gq, gu, gd, go, small, mlp_gain, tok, dmid, gain, seq, fsdp):
    lo = 2
    hi = fsdp // lo
    chunks = 4
    anywhere = pl.BlockSpec(memory_space=pl.ANY)
    vmem = pl.BlockSpec(memory_space=pltpu.VMEM)
    block_q = (seq,) + gq.shape[2:]
    block_u = (seq,) + gu.shape[2:]
    block_d = gd.shape[1:]
    block_o = go.shape[1:]
    blocks = (block_q, block_u, block_d, block_o)
    tok_rows, dim = tok.shape
    sides = max(hi - 1, 1)

    def buf(lead, shape, kind=bf16):
        return pltpu.VMEM((lead,) + tuple(shape), kind)

    scratch = [
        buf(max(seq // 2, 1), (tok_rows, dim)),
        buf(max(seq - 1, 1), (tok_rows, dim)),
        buf(max(seq // 2, 1), (tok_rows, dim)),
        pltpu.VMEM((tok_rows, dim), f32),
    ]
    scratch += [buf(hi, b) for b in blocks]
    scratch += [buf(hi, b) for b in blocks]
    scratch += [buf(sides, b) for b in (block_q, block_u, block_d)] * 2
    scratch += [buf(sides, block_o), buf(sides, block_o)]
    scratch += [pltpu.VMEM(block_q, bf16), pltpu.VMEM(block_u, bf16)]
    scratch += [
        pltpu.VMEM(small.shape, f32),
        buf(hi, small.shape, f32),
        pltpu.VMEM((16, dim), f32),
        pltpu.VMEM((16, dim), f32),
        buf(hi, (16, dim), f32),
        buf(seq, (16, dim), f32),
    ]
    dma = pltpu.SemaphoreType.DMA
    scratch += [
        dma((5, max(hi, seq))),
        dma((seq, chunks)),
        dma((seq, chunks)),
        dma((4, hi)),
        dma((4, hi)),
        dma((4, 2, hi)),
        dma((4, 2, hi)),
        dma((2, seq)),
        dma((2, seq)),
        dma((hi,)),
        dma((hi,)),
        dma((hi + seq,)),
        dma((hi + seq,)),
    ]
    return pl.pallas_call(
        functools.partial(finish_kernel, seq, hi, lo, chunks),
        out_shape=(
            jax.ShapeDtypeStruct((tok_rows, dim), f32),
            jax.ShapeDtypeStruct(block_q, f32),
            jax.ShapeDtypeStruct(block_u, f32),
            jax.ShapeDtypeStruct(block_d, f32),
            jax.ShapeDtypeStruct(block_o, f32),
            jax.ShapeDtypeStruct(small.shape, f32),
            jax.ShapeDtypeStruct((16, dim), f32),
        ),
        in_specs=[anywhere] * 5 + [vmem] * 5,
        out_specs=(vmem,) * 7,
        scratch_shapes=scratch,
        compiler_params=pltpu.CompilerParams(
            collective_id=1, has_side_effects=True, vmem_limit_bytes=56 << 20
        ),
        name="finish",
    )(dn, gq, gu, gd, go, small, mlp_gain, tok, dmid, gain)


GELU_P = 0.24
GELU_C = (
    0.08951261885080208,
    0.15562094398234086,
    -0.15437154502074169,
    0.6261054138112487,
    -0.6465313024138201,
    0.5547927291245551,
    -0.125128858665134,
)


def gelu_parts(x):
    size = jnp.abs(x)
    t = 1.0 / (1.0 + GELU_P * size)
    poly = GELU_C[-1] * t
    for c in GELU_C[-2::-1]:
        poly = (poly + c) * t
    bell = jnp.exp2(x * x * (-0.5 * LOG2E))
    tail = poly * bell
    cdf = jnp.where(x < 0.0, tail, 1.0 - tail)
    return x * cdf, cdf + x * bell * (1.0 / math.sqrt(2.0 * math.pi))


def mlp_kernel(seq, sub, length_ref, *refs):
    refs = list(refs)

    def take(count):
        taken = refs[:count]
        del refs[:count]
        return taken

    own_ref, others_ref, tok_ref, grads_ref = take(4)
    att_refs = [own_ref] + [others_ref.at[k] for k in range(1, seq)]
    grad_refs = [grads_ref.at[j] for j in range(seq)]
    wo_ref, wu_ref, wd_ref, gain_ref = take(4)
    mid_ref, dmid_ref, gsum_ref, db_ref, mo_ref, ug_ref, dg_ref = take(7)
    att_buf, tok_buf, gm, nm, hid, dpre, low, into, acc = take(9)
    dbv = low.at[0]
    depth = att_buf.shape[0]
    load_sem, gm_sem, dn_send, dn_recv, db_send, db_recv, mo_sem, own_sem = take(8)

    me = lax.axis_index("seq")
    length = length_ref[0]
    dim = wo_ref.shape[0]
    width = dim // seq
    rows = tok_ref.shape[1]
    share = wu_ref.shape[1]
    bits = [1 << i for i in range(seq.bit_length() - 1)]

    barrier = pltpu.get_barrier_semaphore()
    for bit in bits:
        pl.semaphore_signal(barrier, inc=1, device_id={"seq": me ^ bit}, device_id_type=MESH)
    pl.semaphore_wait(barrier, len(bits))

    order = list(reversed(range(seq)))
    gm_loads = {j: pltpu.make_async_copy(grad_refs[j], gm.at[pl.ds(j * rows, rows)], gm_sem.at[j]) for j in order}

    def chunk_loads(n):
        j, slot = order[n], n % depth
        copies = [
            pltpu.make_async_copy(
                att_refs[k].at[pl.ds(j * rows, rows)], att_buf.at[slot, k], load_sem.at[slot, k]
            )
            for k in range(seq)
        ]
        copies.append(pltpu.make_async_copy(tok_ref.at[j], tok_buf.at[slot], load_sem.at[slot, seq]))
        return copies

    for c in chunk_loads(0):
        c.start()
    for j in order:
        gm_loads[j].start()

    slots = {}
    for bit in bits:
        for j in range(0, seq, 2 * bit):
            slots[bit, j] = len(slots)

    def dn_copy(bit, j):
        slot = slots[bit, j]
        return pltpu.make_async_remote_copy(
            src_ref=low.at[j ^ bit],
            dst_ref=into.at[slot],
            send_sem=dn_send.at[slot],
            recv_sem=dn_recv.at[slot],
            device_id={"seq": me ^ bit},
            device_id_type=MESH,
        )

    gain = gain_ref[...]
    for n, j in enumerate(order):
        slot = n % depth
        if depth == 1 and n:
            for c in chunk_loads(n):
                c.start()
        for c in chunk_loads(n):
            c.wait()
        if depth == 2 and n + 1 < seq:
            for c in chunk_loads(n + 1):
                c.start()
        gm_loads[j].wait()
        base = (j ^ me) * rows

        @pl.loop(0, rows // sub)
        def _(s):
            at = pl.ds(pl.multiple_of(s * sub, sub), sub)
            here = pl.ds(pl.multiple_of(j * rows + s * sub, sub), sub)
            position = base + s * sub + lax.broadcasted_iota(jnp.int32, (sub, 1), 0)
            live = jnp.where(position < length, 1.0, 0.0)
            masked = (gm[here].astype(f32) * live).astype(bf16)
            gm[here] = masked
            mid = tok_buf[slot, at].astype(f32)
            for k in range(seq):
                own = pl.ds(pl.multiple_of((me ^ k) * width, width), width)
                mid = mid + dot(att_buf[slot, k, at], wo_ref[own])
            rho = lax.rsqrt(jnp.mean(mid * mid, axis=-1, keepdims=True) + EPSILON)
            normed = (mid * rho * gain).astype(bf16)
            nm[here] = normed
            if j == 0:
                mid_ref[at] = mid
            for c in range(0, share, 256):
                cols = slice(c, c + 256)
                value, slope = gelu_parts(dot(normed, wu_ref[:, cols]))
                hid[here, cols] = value.astype(bf16)
                dpre[here, cols] = (dot_t(masked, wd_ref[cols]) * slope).astype(bf16)
            part = dot_t(dpre[here], wu_ref[...])
            if j % 2:
                low[j, at] = part.astype(bf16)
            else:
                acc[at] = part

        if j % 2:
            dn_copy(1, j ^ 1).start()
        elif j:
            for bit in bits:
                if j & bit:
                    low[j] = acc[...].astype(bf16)
                    dn_copy(bit, j ^ bit).start()
                    break
                dn_copy(bit, j).wait_recv()
                acc[...] += into[slots[bit, j]].astype(f32)

    for c in range(0, dim, 256):
        ug_ref[c : c + 256] = t_dot(nm[:, c : c + 256], dpre[...]).astype(bf16)

    for bit in bits:
        dn_copy(bit, 0).wait_recv()
    step = 128
    part = jnp.zeros((8, dim), f32)
    for r in range(0, rows, step):
        at = slice(r, r + step)
        dn = acc[at]
        for bit in bits:
            dn = dn + into[slots[bit, 0], at].astype(f32)
        mid = mid_ref[at]
        rho = lax.rsqrt(jnp.mean(mid * mid, axis=-1, keepdims=True) + EPSILON)
        scaled = gain * dn
        mean = jnp.mean(mid * scaled, axis=-1, keepdims=True)
        dmid = gm[at].astype(f32) + rho * scaled - mid * (rho * rho * rho * mean)
        dmid_ref[at] = dmid
        dbv[at] = dmid.astype(bf16)
        prod = dn * mid * rho
        part += functools.reduce(jnp.add, [prod[i : i + 8] for i in range(0, step, 8)])
    gsum_ref[...] = part

    def db_copy(source, target, bit):
        return pltpu.make_async_remote_copy(
            src_ref=db_ref.at[source] if source else dbv,
            dst_ref=db_ref.at[target],
            send_sem=db_send.at[target],
            recv_sem=db_recv.at[target],
            device_id={"seq": me ^ bit},
            device_id_type=MESH,
        )

    own_copy = pltpu.make_async_copy(dbv, db_ref.at[0], own_sem)
    own_copy.start()
    sends = []
    high = [bit for bit in reversed(bits) if bit > 1]

    def send(source, target, bit):
        sends.append(db_copy(source, target, bit))
        sends[-1].start()

    if high:
        send(0, high[0], high[0])
    if seq > 1:
        send(0, 1, 1)
    for c in range(0, share, 256):
        dg_ref[c : c + 256] = t_dot(hid[:, c : c + 256], gm[...]).astype(bf16)
    mo_copies = []
    for j in range(seq):
        at = slice(j * rows, (j + 1) * rows)
        nm[at] = dot(hid[at], wd_ref[...]).astype(bf16)
        mo_copies.append(pltpu.make_async_copy(nm.at[pl.ds(j * rows, rows)], mo_ref.at[j], mo_sem.at[j]))
        mo_copies[-1].start()
    have = [0]
    for n, bit in enumerate(high):
        if n:
            for j in have:
                send(j, j ^ bit, bit)
        for j in have:
            db_copy(0, j ^ bit, bit).wait_recv()
            send(j ^ bit, j ^ bit ^ 1, 1)
        have += [j ^ bit for j in have]
    if seq > 1:
        for j in have:
            db_copy(0, j ^ 1, 1).wait_recv()
    for c in sends:
        c.wait_send()
    own_copy.wait()
    for c in mo_copies:
        c.wait()
    for bit in bits:
        for j in range(0, seq, 2 * bit):
            dn_copy(bit, j).wait_send()


def mlp(length, own, others, tok, grads, wo, wu, wd, gain):
    seq, rows, dim = tok.shape
    share = wu.shape[1]
    sub = 256
    depth = 2 if seq <= 4 else 1
    anywhere = pl.BlockSpec(memory_space=pl.ANY)
    vmem = pl.BlockSpec(memory_space=pltpu.VMEM)
    dma = pltpu.SemaphoreType.DMA
    return pl.pallas_call(
        functools.partial(mlp_kernel, seq, sub),
        out_shape=(
            jax.ShapeDtypeStruct((rows, dim), f32),
            jax.ShapeDtypeStruct((rows, dim), f32),
            jax.ShapeDtypeStruct((8, dim), f32),
            jax.ShapeDtypeStruct((seq, rows, dim), bf16),
            jax.ShapeDtypeStruct((seq, rows, dim), bf16),
            jax.ShapeDtypeStruct((dim, share), bf16),
            jax.ShapeDtypeStruct((share, dim), bf16),
        ),
        in_specs=[pl.BlockSpec(memory_space=pltpu.SMEM)] + [anywhere] * 4 + [vmem] * 4,
        out_specs=(vmem, vmem, vmem, anywhere, anywhere, vmem, vmem),
        scratch_shapes=[
            pltpu.VMEM((depth, seq, rows, dim // seq), bf16),
            pltpu.VMEM((depth, rows, dim), bf16),
            pltpu.VMEM((seq * rows, dim), bf16),
            pltpu.VMEM((seq * rows, dim), bf16),
            pltpu.VMEM((seq * rows, share), bf16),
            pltpu.VMEM((seq * rows, share), bf16),
            pltpu.VMEM((seq, rows, dim), bf16),
            pltpu.VMEM((max(seq - 1, 1), rows, dim), bf16),
            pltpu.VMEM((rows, dim), f32),
            dma((2, seq + 1)),
            dma((seq,)),
            dma((seq,)),
            dma((seq,)),
            dma((seq,)),
            dma((seq,)),
            dma((seq,)),
            dma,
        ],
        compiler_params=pltpu.CompilerParams(collective_id=2, has_side_effects=True, vmem_limit_bytes=60 << 20),
        cost_estimate=pl.CostEstimate(
            flops=2 * rows * seq * dim * (dim + 6 * share), bytes_accessed=32 << 20, transcendentals=rows * seq * share
        ),
        name="mlp",
    )(length, own, others, tok, grads, wo, wu, wd, gain)


def swap(value, bit):
    count = lax.axis_size("seq")
    return lax.ppermute(value, "seq", [(i, i ^ bit) for i in range(count)])


def seq_bits():
    count = lax.axis_size("seq")
    return [1 << i for i in reversed(range(1, count.bit_length() - 1))]


def seq_gather(value):
    chunks = {0: value}
    for bit in seq_bits():
        for j in list(chunks):
            chunks[j ^ bit] = swap(chunks[j], bit)
    for j in list(chunks):
        chunks[j ^ 1] = swap(chunks[j], 1)
    return [chunks[j] for j in range(len(chunks))]


def seq_reduce(parts):
    count = len(parts)
    parts = dict(enumerate(parts))
    for j in range(count - 2, -1, -2):
        parts[j] = parts[j].astype(f32) + swap(parts.pop(j ^ 1).astype(bf16), 1).astype(f32)
    for bit in reversed(seq_bits()):
        keep = [j for j in parts if not j & bit]
        for j in sorted(keep, reverse=True):
            parts[j] = parts[j] + swap(parts.pop(j ^ bit).astype(bf16), bit).astype(f32)
    return parts[0]


def bias_table_grad(near, far):
    distance = tile_distance().T[SPAN - NEAR :]
    bucket = np.where((distance >= 0) & (distance < BLOCK), bucket_of(np.clip(distance, 0, BLOCK)), BUCKETS)
    bucket = jnp.asarray(bucket.astype(np.int32))
    columns = [jnp.sum(jnp.where((bucket == i)[None], near, 0.0), axis=(1, 2)) for i in range(BUCKETS)]
    columns[-1] = columns[-1] + jnp.sum(far, axis=(1, 2))
    return jnp.stack(columns, axis=1)


def inverse_rms(values):
    return lax.rsqrt(jnp.mean(values * values, axis=-1, keepdims=True) + EPSILON)


def norm_back(values, gain, rho, grad):
    scaled = gain * grad
    mean = jnp.mean(values * scaled, axis=-1, keepdims=True)
    gain_grad = (grad * values * rho).reshape(-1, 8, values.shape[1])
    return rho * scaled - values * (rho * rho * rho * mean), jnp.sum(gain_grad, axis=0)


def body(
    tokens,
    lengths,
    state_init,
    w_qkv,
    w_out,
    w_up,
    w_down,
    norm_attn,
    norm_mlp,
    rel_bias,
    state_query,
    gate_bias,
    out_grad,
    state_grad,
):
    seq_count = lax.axis_size("seq")
    fsdp_count = lax.axis_size("fsdp")
    seq_at = lax.axis_index("seq")
    heads = H // seq_count
    width = heads * DH
    tok_rows, dim = tokens.shape[1:]
    rows = tok_rows * seq_count
    hidden_all = w_up.shape[1]
    share = hidden_all // (seq_count * fsdp_count)

    piece = dim // (seq_count * fsdp_count)
    all_tokens, all_grad, qkv_w, gain_attn, gain_mlp, own_out, up_w = gather_start(
        tokens[0],
        out_grad[0],
        w_qkv,
        norm_attn.reshape(1, -1),
        norm_mlp.reshape(1, -1),
        w_out.reshape(seq_count, piece, dim),
        w_up,
        seq_count,
        fsdp_count,
    )
    qkv_w = qkv_w.reshape(dim, 3 * width)
    up_w = up_w.reshape(dim, hidden_all // seq_count)
    gain_attn = gain_attn.reshape(dim).astype(f32)
    gain_mlp = gain_mlp.reshape(dim).astype(f32)
    own_down = lax.dynamic_slice_in_dim(w_down, seq_at * share, share, axis=0)

    bias = bias_vector(rel_bias)
    forget = jax.nn.sigmoid(gate_bias)
    forget_row = forget.reshape(1, width)
    chunk_ids = jnp.arange(seq_count, dtype=jnp.int32)
    order = chunk_ids ^ seq_at

    inputs = all_tokens.reshape(rows, dim).astype(f32)
    normed = (inputs * inverse_rms(inputs) * gain_attn).astype(bf16)
    qkv = dot(normed, qkv_w).astype(bf16)
    attended, others, out_w, down_w, final_memory, mem, upd, lse, slse = attend(
        qkv,
        state_init[0],
        lengths,
        state_query,
        forget_row,
        bias,
        own_out,
        own_down,
        heads,
        seq_count,
        fsdp_count,
    )
    out_w = out_w.reshape(dim, dim)
    down_w = down_w.reshape(fsdp_count * share, dim)
    own_out = lax.dynamic_slice_in_dim(out_w, seq_at * width, width, axis=0)
    mid_here, dmid, mlp_gain_grad, dbranch, mlp_parts, up_grad, down_grad = mlp(
        lengths, attended, others, all_tokens, all_grad, out_w, up_w, down_w, gain_mlp.reshape(1, dim)
    )
    dbranch = dbranch.reshape(rows, dim)
    dattended = dot_t(dbranch, own_out).astype(bf16)
    out_w_grad = t_dot(attended, dbranch)

    dqkv, dquery, dforget, near, far = attend_back(
        qkv, dattended, attended, mem, upd, lse, slse, state_grad[0], lengths, state_query, forget_row, bias, heads, order
    )
    mlp_parts, dqkv = lax.optimization_barrier((mlp_parts, dqkv))
    mlp_out = seq_reduce([mlp_parts[j] for j in range(seq_count)])
    live_here = (seq_at * tok_rows + jnp.arange(tok_rows, dtype=jnp.int32) < lengths[0]).astype(f32)[:, None]
    output = (live_here * (mid_here + mlp_out)).astype(bf16)[None]
    dnormed = dot_t(dqkv, qkv_w).astype(bf16).reshape(seq_count, tok_rows, dim)
    qkv_grad = t_dot(normed, dqkv).astype(bf16).reshape(seq_count, fsdp_count, piece, 3 * width)
    up_grad = up_grad.reshape(seq_count, fsdp_count, piece, hidden_all // seq_count)
    span = fsdp_count // seq_count
    down_grad = down_grad.reshape(seq_count, span, share, dim)
    moved = [lax.dynamic_slice_in_dim(down_grad, seq_at, 1, axis=0)]
    for k in range(1, seq_count):
        moved.append(swap(lax.dynamic_slice_in_dim(down_grad, seq_at ^ k, 1, axis=0), k))
    moved = lax.optimization_barrier(jnp.concatenate(moved, axis=0))
    moved = [lax.dynamic_slice_in_dim(moved, seq_at ^ k, 1, axis=0) for k in range(seq_count)]
    down_grad = jnp.swapaxes(jnp.concatenate(moved, axis=0), 0, 1).reshape(fsdp_count, share, dim)
    out_w_grad = out_w_grad.astype(bf16).reshape(fsdp_count, piece, dim)
    grad_gate = dforget.reshape(heads, DH) * forget * (1.0 - forget)
    grad_table = jnp.pad(bias_table_grad(near, far), ((0, 0), (0, DH - BUCKETS)))
    cut = heads * DH
    small = jnp.concatenate([dquery.reshape(cut, DH), grad_gate, grad_table], axis=0)
    small = jnp.pad(small, ((0, -small.shape[0] % 8), (0, 0)))
    tokens_grad, qkv_part, up_part, down_part, out_part, small, gain_sums = finish(
        dnormed,
        qkv_grad,
        up_grad,
        down_grad,
        out_w_grad,
        small,
        mlp_gain_grad,
        tokens[0],
        dmid,
        gain_attn.reshape(1, dim),
        seq_count,
        fsdp_count,
    )
    tokens_grad = tokens_grad[None]
    dquery = small[:cut].reshape(heads, DH, DH)
    grad_gate = small[cut : cut + heads]
    grad_table = small[cut + heads : cut + 2 * heads, :BUCKETS]
    up_part = up_part.reshape(seq_count, piece, fsdp_count, share)
    up_part = jnp.transpose(up_part, (1, 2, 0, 3)).reshape(piece, hidden_all)
    qkv_part = qkv_part.reshape(seq_count, piece, 3, width)
    qkv_part = jnp.transpose(qkv_part, (1, 2, 0, 3)).reshape(piece, 3 * H * DH)
    gain_sums = jnp.sum(gain_sums.reshape(2, 8, seq_count * fsdp_count, piece), axis=1)
    mine = seq_at * fsdp_count + lax.axis_index("fsdp")
    gain_sums = lax.dynamic_slice_in_dim(gain_sums, mine, 1, axis=1)[:, 0]
    mlp_gain_grad, attn_gain_grad = gain_sums[0], gain_sums[1]
    return (
        output,
        final_memory[None],
        tokens_grad,
        qkv_part,
        out_part,
        up_part,
        down_part,
        attn_gain_grad,
        mlp_gain_grad,
        grad_table,
        dquery,
        grad_gate,
    )


def solution(mesh):
    placed = (
        P("fsdp", "seq", None),
        P("fsdp"),
        P("fsdp", None, "seq"),
        P("fsdp", None),
        P("fsdp", None),
        P("fsdp", None),
        P("fsdp", None),
        P("fsdp"),
        P("fsdp"),
        P("seq", None),
        P("seq", None, None),
        P("seq", None),
        P("fsdp", "seq", None),
        P("fsdp", None, "seq"),
    )
    return jax.shard_map(
        body,
        mesh=mesh,
        in_specs=placed,
        out_specs=(
            P("fsdp", "seq", None),
            P("fsdp", None, "seq"),
            P("fsdp", "seq", None),
            P(("seq", "fsdp"), None),
            P(("seq", "fsdp"), None),
            P(("seq", "fsdp"), None),
            P(("seq", "fsdp"), None),
            P(("seq", "fsdp")),
            P(("seq", "fsdp")),
            P("seq", None),
            P("seq", None, None),
            P("seq", None),
        ),
        check_vma=False,
    )
```

```python
import functools
import math

import jax
import jax.numpy as jnp
import numpy as np
from jax import lax
from jax.experimental import pallas as pl
from jax.experimental.pallas import tpu as pltpu
from jax.sharding import PartitionSpec as P

H = 8
DH = 128
BLOCK = 512
STATE_VECTORS = 512
QTILE = 256
SPAN = BLOCK + QTILE

EPSILON = 1e-06
BUCKET_EDGES = (19, 21, 24, 27, 31, 35, 40, 46, 52, 59, 67, 77, 87, 99, 113)
BUCKETS = 32
LOG2E = math.log2(math.e)
SCALE = DH ** (-0.5)
NEAR = 384

f32 = jnp.float32
bf16 = jnp.bfloat16
MESH = pl.DeviceIdType.MESH


def bucket_of(distance):
    return np.minimum(distance, 16) + (distance[..., None] >= np.array(BUCKET_EDGES)).sum(-1)


def tile_distance():
    rows = np.arange(QTILE)[:, None]
    cols = np.arange(SPAN)[None, :]
    return rows + BLOCK - cols


def bias_vector(table):
    distance = BLOCK - np.arange(2 * BLOCK)
    inside = (distance >= 0) & (distance < BLOCK)
    bucket = jnp.asarray(np.where(inside, bucket_of(np.clip(distance, 0, BLOCK)), BUCKETS).astype(np.int32))
    total = jnp.full((table.shape[0], 2 * BLOCK), -jnp.inf, f32)
    for i in range(BUCKETS):
        total = jnp.where((bucket == i)[None], table[:, i : i + 1] * LOG2E, total)
    return total


def tile_bias(vector_ref, head):
    wide = jnp.broadcast_to(vector_ref[head : head + 1, :], (QTILE, 2 * BLOCK))
    return pltpu.roll(wide, 0, 1, stride=1, stride_axis=0)[:, :SPAN]


def dot(a, b):
    return jnp.dot(a, b, preferred_element_type=f32)


def dot_t(a, b):
    return lax.dot_general(a, b, (((1,), (1,)), ((), ())), preferred_element_type=f32)


def t_dot(a, b):
    return lax.dot_general(a, b, (((0,), (0,)), ((), ())), preferred_element_type=f32)


def to_row(column):
    wide = jnp.broadcast_to(column, (column.shape[0], 128))
    return wide.T[0:1, :]


def context_pieces(tile):
    start = tile * QTILE
    pieces = []
    if start < BLOCK:
        pieces.append((0, start, BLOCK, 0))
    pieces.append((1, 0, start + QTILE, BLOCK - start))
    return pieces


def softmax_parts(scores):
    top = functools.reduce(jnp.maximum, [jnp.max(s, axis=-1, keepdims=True) for s in scores])
    raised = [jnp.exp2(s - top) for s in scores]
    total = functools.reduce(jnp.add, [jnp.sum(e, axis=-1, keepdims=True) for e in raised])
    return raised, total, top + jnp.log2(total)


def line_gather(hi, lo, slot, own, z_send, z_recv, y_send, y_recv):
    f = lax.axis_index("fsdp")
    z, y = f // lo, f % lo

    def copy(i, origin, target, send, recv, first=False):
        ref = slot(i, origin)
        return pltpu.make_async_remote_copy(
            src_ref=own(i) if first else ref,
            dst_ref=ref,
            send_sem=send,
            recv_sem=recv,
            device_id={"fsdp": target},
            device_id_type=MESH,
        )

    def right(i, t):
        return copy(i, (z - t) * lo + y, (z + 1) * lo + y, z_send.at[i, 0, t], z_recv.at[i, 0, t], t == 0)

    def left(i, t):
        return copy(i, (z + t) * lo + y, (z - 1) * lo + y, z_send.at[i, 1, t], z_recv.at[i, 1, t], t == 0)

    def across(i, d):
        return copy(
            i, (z + d) * lo + y, z * lo + 1 - y, y_send.at[i, d + hi - 1], y_recv.at[i, d + hi - 1], d == 0
        )

    def start(i):
        pl.when(z + 1 < hi)(lambda: right(i, 0).start())
        pl.when(z >= 1)(lambda: left(i, 0).start())
        across(i, 0).start()

    def step(i, t):
        @pl.when(z - 1 - t >= 0)
        def _():
            copy(i, (z - 1 - t) * lo + y, f, z_send.at[i, 0, t], z_recv.at[i, 0, t]).wait_recv()
            if t + 1 < hi - 1:
                pl.when(z + 1 < hi)(lambda: right(i, t + 1).start())
            across(i, -1 - t).start()

        @pl.when(z + 1 + t < hi)
        def _():
            copy(i, (z + 1 + t) * lo + y, f, z_send.at[i, 1, t], z_recv.at[i, 1, t]).wait_recv()
            if t + 1 < hi - 1:
                pl.when(z >= 1)(lambda: left(i, t + 1).start())
            across(i, 1 + t).start()

    def arrive(i):
        for d in range(1 - hi, hi):

            @pl.when((z + d >= 0) & (z + d < hi))
            def _():
                copy(
                    i, (z + d) * lo + 1 - y, f, y_send.at[i, d + hi - 1], y_recv.at[i, d + hi - 1]
                ).wait_recv()

    def drain(i):
        for d in range(1 - hi, hi):

            @pl.when((z + d >= 0) & (z + d < hi))
            def _():
                across(i, d).wait_send()

        for t in range(hi - 1):

            @pl.when((z + 1 < hi) & (z - t >= 0))
            def _():
                right(i, t).wait_send()

            @pl.when((z >= 1) & (z + t < hi))
            def _():
                left(i, t).wait_send()

    return start, step, arrive, drain


def line_sems(count, hi):
    dma = pltpu.SemaphoreType.DMA
    return [dma((count, 2, hi)), dma((count, 2, hi)), dma((count, 2 * hi)), dma((count, 2 * hi))]


def greet(seq_targets, hi, lo):
    me = lax.axis_index("seq")
    f = lax.axis_index("fsdp")
    z, y = f // lo, f % lo
    barrier = pltpu.get_barrier_semaphore()
    for k in seq_targets:
        pl.semaphore_signal(barrier, inc=1, device_id={"seq": me ^ k}, device_id_type=MESH)
    near = (lax.rem(z + 1, hi) * lo + y, lax.rem(z + hi - 1, hi) * lo + y, z * lo + 1 - y)
    for target in near:
        pl.semaphore_signal(barrier, inc=1, device_id={"fsdp": target}, device_id_type=MESH)
    pl.semaphore_wait(barrier, len(seq_targets) + len(near))


def attend_kernel(
    heads,
    seq,
    hi,
    lo,
    length_ref,
    qkv_ref,
    init_ref,
    query_ref,
    forget_ref,
    vector_ref,
    own_out_ref,
    own_down_ref,
    att_ref,
    others_ref,
    outs_ref,
    downs_ref,
    final_ref,
    mem_ref,
    upd_ref,
    lse_ref,
    slse_ref,
    memory_ref,
    bias_ref,
    own_sem,
    att_send,
    att_recv,
    out_send,
    out_recv,
    z_send,
    z_recv,
    y_send,
    y_recv,
):
    me = lax.axis_index("seq")
    f = lax.axis_index("fsdp")
    length = length_ref[0]
    width = heads * DH
    scale2 = SCALE * LOG2E
    blocks = seq
    bits = [1 << i for i in range(seq.bit_length() - 1)]
    greet(bits, hi, lo)

    own_copies = [
        pltpu.make_async_copy(own_down_ref, downs_ref.at[f], own_sem.at[0]),
        pltpu.make_async_copy(own_out_ref, outs_ref.at[:, me], own_sem.at[1]),
    ]
    for c in own_copies:
        c.start()

    def lowest(k):
        return k & -k

    def out_copy(k):
        return pltpu.make_async_remote_copy(
            src_ref=outs_ref.at[:, me ^ k ^ lowest(k)] if k ^ lowest(k) else own_out_ref,
            dst_ref=outs_ref.at[:, me ^ k ^ lowest(k)],
            send_sem=out_send.at[k],
            recv_sem=out_recv.at[k],
            device_id={"seq": me ^ lowest(k)},
            device_id_type=MESH,
        )

    def out_arrival(k):
        return pltpu.make_async_remote_copy(
            src_ref=outs_ref.at[:, me ^ k],
            dst_ref=outs_ref.at[:, me ^ k],
            send_sem=out_send.at[k],
            recv_sem=out_recv.at[k],
            device_id={"seq": me},
            device_id_type=MESH,
        )

    def att_copy(k, b):
        bit = lowest(k)
        came = k ^ bit
        here = pl.ds(pl.multiple_of((b ^ me) * BLOCK, BLOCK), BLOCK)
        there = pl.ds(pl.multiple_of((b ^ me ^ bit) * BLOCK, BLOCK), BLOCK)
        src = others_ref.at[came, here] if came else att_ref.at[here]
        return pltpu.make_async_remote_copy(
            src_ref=src,
            dst_ref=others_ref.at[k, there],
            send_sem=att_send.at[k, b],
            recv_sem=att_recv.at[k, b],
            device_id={"seq": me ^ bit},
            device_id_type=MESH,
        )

    def att_arrival(k, b):
        here = pl.ds(pl.multiple_of((b ^ me) * BLOCK, BLOCK), BLOCK)
        return pltpu.make_async_remote_copy(
            src_ref=others_ref.at[k, here],
            dst_ref=others_ref.at[k, here],
            send_sem=att_send.at[k, b],
            recv_sem=att_recv.at[k, b],
            device_id={"seq": me},
            device_id_type=MESH,
        )

    passing = sorted([k for k in range(2, seq, 2)], key=lambda k: (bin(k).count("1"), -k))

    def onward(k, send):
        for bit in reversed(bits):
            if bit < lowest(k):
                send(k | bit)

    start, step, arrive, drain = line_gather(
        hi, lo, lambda i, origin: downs_ref.at[origin], lambda i: own_down_ref, z_send, z_recv, y_send, y_recv
    )

    start(0)
    for bit in reversed(bits):
        out_copy(bit).start()
    memory_ref[...] = init_ref[...].astype(f32)
    for head in range(heads):
        bias_ref[head] = tile_bias(vector_ref, head)

    @pl.loop(0, blocks)
    def _(block):
        cur_at = pl.multiple_of((block ^ me) * BLOCK, BLOCK)
        prev_at = pl.multiple_of((jnp.maximum(block - 1, 0) ^ me) * BLOCK, BLOCK)
        cur_ref = qkv_ref.at[pl.ds(cur_at, BLOCK)]
        prev_ref = qkv_ref.at[pl.ds(prev_at, BLOCK)]
        for t in range(min(hi - 1, blocks - 1)):
            pl.when(block == t + 1)(lambda t=t: step(0, t))

        live_block = block * BLOCK < length
        for head in range(heads):
            own = slice(head * DH, (head + 1) * DH)
            memory = memory_ref[:, own]
            low = memory.astype(bf16)
            mem_ref[block, :, own] = memory
            refs = (prev_ref, cur_ref)
            key_cols = slice(width + head * DH, width + (head + 1) * DH)
            value_cols = slice(2 * width + head * DH, 2 * width + (head + 1) * DH)
            for tile in range(BLOCK // QTILE):
                rows = slice(tile * QTILE, (tile + 1) * QTILE)
                query = cur_ref[rows, own]
                scores, values = [], []
                for which, at, end, col in context_pieces(tile):
                    s = dot_t(query, refs[which][at:end, key_cols])
                    position = (block - 1 + which) * BLOCK + at + lax.broadcasted_iota(jnp.int32, (1, end - at), 1)
                    live = (position >= 0) & (position < length)
                    s = s * scale2 + bias_ref[head, :, col : col + end - at]
                    scores.append(jnp.where(live, s, -jnp.inf))
                    values.append(refs[which][at:end, value_cols])
                scores.append(dot_t(query, low) * scale2)
                values.append(low)
                raised, total, lse = softmax_parts(scores)
                out = functools.reduce(jnp.add, [dot(e.astype(bf16), v) for e, v in zip(raised, values)])
                att_ref[pl.ds(cur_at + tile * QTILE, QTILE), own] = (out / total).astype(bf16)
                lse_ref[head : head + 1, pl.ds(pl.multiple_of(block * BLOCK, BLOCK) + tile * QTILE, QTILE)] = to_row(lse)
            own_key = cur_ref[:, key_cols]
            own_value = cur_ref[:, value_cols]
            squeries = dot(low, query_ref[head]).astype(bf16)
            position = block * BLOCK + lax.broadcasted_iota(jnp.int32, (1, BLOCK), 1)
            for tile in range(STATE_VECTORS // QTILE):
                rows = slice(tile * QTILE, (tile + 1) * QTILE)
                squery = squeries[rows]
                scores = [
                    dot_t(squery, low) * scale2,
                    jnp.where(position < length, dot_t(squery, own_key) * scale2, -jnp.inf),
                ]
                raised, total, lse = softmax_parts(scores)
                update = dot(raised[0].astype(bf16), low) + dot(raised[1].astype(bf16), own_value)
                update = update / total
                upd_ref[block, rows, own] = update
                slse_ref[head : head + 1, pl.ds(pl.multiple_of(block * BLOCK, BLOCK) + tile * QTILE, QTILE)] = to_row(
                    lse
                )
                forget = forget_ref[:, own]
                old = memory[rows]
                memory_ref[rows, own] = jnp.where(live_block, forget * old + (1.0 - forget) * update, old)

        for bit in reversed(bits):
            att_copy(bit, block).start()

        @pl.when(block == 0)
        def _():
            for k in passing:
                out_arrival(k).wait_recv()
                onward(k, lambda target: out_copy(target).start())

        @pl.when(block >= 1)
        def _():
            for k in passing:
                att_arrival(k, block - 1).wait_recv()
                onward(k, lambda target: att_copy(target, block - 1).start())

    final_ref[...] = memory_ref[...]
    for t in range(min(hi - 1, blocks - 1), hi - 1):
        step(0, t)
    for k in passing:
        att_arrival(k, blocks - 1).wait_recv()
        onward(k, lambda target: att_copy(target, blocks - 1).start())
    arrive(0)
    for k in range(1, seq, 2):
        out_arrival(k).wait_recv()
        for b in range(blocks):
            att_arrival(k, b).wait_recv()
    for c in own_copies:
        c.wait()
    drain(0)
    for k in range(1, seq):
        out_copy(k).wait_send()
        for b in range(blocks):
            att_copy(k, b).wait_send()


def attend(qkv, init, length, state_query, forget, bias, own_out, own_down, heads, seq, fsdp):
    rows, width3 = qkv.shape
    width = heads * DH
    blocks = rows // BLOCK
    lo = 2
    hi = fsdp // lo
    dim = own_down.shape[1]
    anywhere = pl.BlockSpec(memory_space=pl.ANY)
    vmem = pl.BlockSpec(memory_space=pltpu.VMEM)
    dma = pltpu.SemaphoreType.DMA
    return pl.pallas_call(
        functools.partial(attend_kernel, heads, seq, hi, lo),
        out_shape=(
            jax.ShapeDtypeStruct((rows, width), bf16),
            jax.ShapeDtypeStruct((seq, rows, width), bf16),
            jax.ShapeDtypeStruct((fsdp, seq) + own_out.shape[1:], bf16),
            jax.ShapeDtypeStruct((fsdp,) + own_down.shape, bf16),
            jax.ShapeDtypeStruct((STATE_VECTORS, width), f32),
            jax.ShapeDtypeStruct((blocks, STATE_VECTORS, width), f32),
            jax.ShapeDtypeStruct((blocks, STATE_VECTORS, width), f32),
            jax.ShapeDtypeStruct((heads, rows), f32),
            jax.ShapeDtypeStruct((heads, blocks * STATE_VECTORS), f32),
        ),
        in_specs=[pl.BlockSpec(memory_space=pltpu.SMEM)] + [vmem] * 7,
        out_specs=(vmem, anywhere, anywhere, anywhere, vmem, vmem, vmem, vmem, vmem),
        scratch_shapes=[
            pltpu.VMEM((STATE_VECTORS, width), f32),
            pltpu.VMEM((heads, QTILE, SPAN), f32),
            dma((2,)),
            dma((seq, blocks)),
            dma((seq, blocks)),
            dma((seq,)),
            dma((seq,)),
        ]
        + line_sems(1, hi),
        compiler_params=pltpu.CompilerParams(collective_id=3, has_side_effects=True, vmem_limit_bytes=40 << 20),
        cost_estimate=pl.CostEstimate(
            flops=blocks * heads * 512 * 2400 * 128 * 4, bytes_accessed=16 << 20, transcendentals=10 << 20
        ),
        name="attend",
    )(length, qkv, init, state_query, forget, bias, own_out, own_down)


def attend_back_kernel(
    heads,
    blocks,
    length_ref,
    order_ref,
    cur_ref,
    prev_ref,
    dout_ref,
    out_ref,
    mem_ref,
    upd_ref,
    lse_ref,
    slse_ref,
    sgrad_ref,
    query_ref,
    forget_ref,
    vector_ref,
    dqkv_ref,
    dquery_ref,
    dforget_ref,
    near_ref,
    far_ref,
    dmem_ref,
    dnext_ref,
    dctx_ref,
    bias_ref,
):
    step = pl.program_id(0)
    block = blocks - 1 - step
    length = length_ref[0]
    width = heads * DH
    scale2 = SCALE * LOG2E

    @pl.when(step == 0)
    def _():
        dmem_ref[...] = sgrad_ref[...].astype(f32)
        dnext_ref[...] = jnp.zeros_like(dnext_ref)
        dquery_ref[...] = jnp.zeros_like(dquery_ref)
        dforget_ref[...] = jnp.zeros_like(dforget_ref)
        near_ref[...] = jnp.zeros_like(near_ref)
        far_ref[...] = jnp.zeros_like(far_ref)
        for head in range(heads):
            bias_ref[head] = tile_bias(vector_ref, head).T

    live_block = block * BLOCK < length
    refs = (prev_ref, cur_ref)
    for head in range(heads):
        own = slice(head * DH, (head + 1) * DH)
        key_cols = slice(width + head * DH, width + (head + 1) * DH)
        value_cols = slice(2 * width + head * DH, 2 * width + (head + 1) * DH)
        memory = mem_ref[0, :, own]
        update = upd_ref[0, :, own]
        low = memory.astype(bf16)
        forget = forget_ref[:, own]
        dmem = dmem_ref[:, own]
        dupd = jnp.where(live_block, (1.0 - forget) * dmem, 0.0).astype(bf16)
        moved = jnp.where(live_block, dmem * (memory - update), 0.0)
        dforget_ref[:, own] += jnp.sum(moved, axis=0, keepdims=True)
        dmem_new = jnp.where(live_block, forget * dmem, dmem)
        own_key = cur_ref[:, key_cols]
        own_value = cur_ref[:, value_cols]
        squeries = dot(low, query_ref[head]).astype(bf16)
        sdelta = jnp.sum((dupd.astype(f32) * update).T, axis=0, keepdims=True)
        slse = slse_ref[head : head + 1, :]
        dsquery = jnp.zeros((STATE_VECTORS, DH), f32)
        dkey = []
        dvalue = []
        for part in range(2 * STATE_VECTORS // QTILE):
            own_part = part >= STATE_VECTORS // QTILE
            lo = (part % (STATE_VECTORS // QTILE)) * QTILE
            keys = (own_key if own_part else low)[lo : lo + QTILE]
            values = (own_value if own_part else low)[lo : lo + QTILE]
            s = dot_t(keys, squeries) * scale2 - slse
            if own_part:
                position = block * BLOCK + lo + lax.broadcasted_iota(jnp.int32, (QTILE, 1), 0)
                s = jnp.where(position < length, s, -jnp.inf)
            p = jnp.exp2(s)
            dp = dot_t(values, dupd)
            ds = (p * (dp - sdelta)).astype(bf16)
            dvalue.append(dot(p.astype(bf16), dupd))
            dkey.append(dot(ds, squeries))
            dsquery += t_dot(ds, keys)
        half = STATE_VECTORS // QTILE
        dlow = [dvalue[i] + dkey[i] * SCALE for i in range(half)]
        dctx_ref[0, 0:BLOCK] = jnp.zeros((BLOCK, DH), f32)
        dctx_ref[1, 0:BLOCK] = jnp.zeros((BLOCK, DH), f32)
        for i in range(half):
            rows = slice(BLOCK + i * QTILE, BLOCK + (i + 1) * QTILE)
            old = slice(i * QTILE, (i + 1) * QTILE)
            dctx_ref[0, rows] = dkey[half + i] * SCALE + dnext_ref[0, old, own]
            dctx_ref[1, rows] = dvalue[half + i] + dnext_ref[1, old, own]
        dsq = (dsquery * SCALE).astype(bf16)
        dquery_ref[head] += t_dot(low, dsq)
        dmem_ref[:, own] = dmem_new + dot_t(dsq, query_ref[head])
        for tile in range(BLOCK // QTILE):
            rows = slice(tile * QTILE, (tile + 1) * QTILE)
            query = cur_ref[rows, own]
            dout = dout_ref[rows, own]
            lse = lse_ref[head : head + 1, rows]
            delta = jnp.sum((dout.astype(f32) * out_ref[rows, own].astype(f32)).T, axis=0, keepdims=True)
            dq = jnp.zeros((QTILE, DH), f32)
            for which, lo, hi, col in context_pieces(tile):
                for at in range(lo, hi, QTILE):
                    keys = refs[which][at : at + QTILE, key_cols]
                    values = refs[which][at : at + QTILE, value_cols]
                    band = col + at - lo
                    position = (block - 1 + which) * BLOCK + at + lax.broadcasted_iota(jnp.int32, (QTILE, 1), 0)
                    live = (position >= 0) & (position < length)
                    s = dot_t(keys, query) * scale2 + bias_ref[head, band : band + QTILE, :] - lse
                    p = jnp.exp2(jnp.where(live, s, -jnp.inf))
                    dp = dot_t(values, dout)
                    ds = (p * (dp - delta)).astype(bf16)
                    wide = ds.astype(f32)
                    if band + QTILE <= SPAN - NEAR:
                        far_ref[head] += functools.reduce(jnp.add, [wide[i : i + 8] for i in range(0, QTILE, 8)])
                    else:
                        edge = max(SPAN - NEAR - band, 0)
                        if edge:
                            far_ref[head] += functools.reduce(jnp.add, [wide[i : i + 8] for i in range(0, edge, 8)])
                        at_near = band + edge - (SPAN - NEAR)
                        near_ref[head, at_near : at_near + QTILE - edge] += wide[edge:]
                    into = slice(which * BLOCK + at, which * BLOCK + at + QTILE)
                    dctx_ref[1, into] += dot(p.astype(bf16), dout)
                    dctx_ref[0, into] += dot(ds, query) * SCALE
                    dq += t_dot(ds, keys)
            for part in range(half):
                keys = low[part * QTILE : (part + 1) * QTILE]
                s = dot_t(keys, query) * scale2 - lse
                p = jnp.exp2(s)
                dp = dot_t(keys, dout)
                ds = (p * (dp - delta)).astype(bf16)
                dlow[part] += dot(p.astype(bf16), dout) + dot(ds, query) * SCALE
                dq += t_dot(ds, keys)
            dqkv_ref[rows, own] = (dq * SCALE).astype(bf16)
        for part in range(half):
            dmem_ref[part * QTILE : (part + 1) * QTILE, own] += dlow[part]
        dnext_ref[0, :, own] = dctx_ref[0, 0:BLOCK]
        dnext_ref[1, :, own] = dctx_ref[1, 0:BLOCK]
        dqkv_ref[:, key_cols] = dctx_ref[0, BLOCK:].astype(bf16)
        dqkv_ref[:, value_cols] = dctx_ref[1, BLOCK:].astype(bf16)


def attend_back(qkv, dout, out, mem, upd, lse, slse, sgrad, length, state_query, forget, bias, heads, order):
    rows, width3 = qkv.shape
    width = heads * DH
    blocks = rows // BLOCK
    last = blocks - 1
    return pl.pallas_call(
        functools.partial(attend_back_kernel, heads, blocks),
        out_shape=(
            jax.ShapeDtypeStruct((rows, width3), bf16),
            jax.ShapeDtypeStruct((heads, DH, DH), f32),
            jax.ShapeDtypeStruct((1, width), f32),
            jax.ShapeDtypeStruct((heads, NEAR, QTILE), f32),
            jax.ShapeDtypeStruct((heads, 8, QTILE), f32),
        ),
        grid_spec=pltpu.PrefetchScalarGridSpec(
            num_scalar_prefetch=2,
            grid=(blocks,),
            in_specs=[
                pl.BlockSpec((BLOCK, width3), lambda b, _, at: (at[last - b], 0)),
                pl.BlockSpec((BLOCK, width3), lambda b, _, at: (at[jnp.maximum(last - b - 1, 0)], 0)),
                pl.BlockSpec((BLOCK, width), lambda b, _, at: (at[last - b], 0)),
                pl.BlockSpec((BLOCK, width), lambda b, _, at: (at[last - b], 0)),
                pl.BlockSpec((1, STATE_VECTORS, width), lambda b, _, at: (last - b, 0, 0)),
                pl.BlockSpec((1, STATE_VECTORS, width), lambda b, _, at: (last - b, 0, 0)),
                pl.BlockSpec((heads, BLOCK), lambda b, _, at: (0, last - b)),
                pl.BlockSpec((heads, STATE_VECTORS), lambda b, _, at: (0, last - b)),
                pl.BlockSpec((STATE_VECTORS, width), lambda b, _, at: (0, 0)),
                pl.BlockSpec((heads, DH, DH), lambda b, _, at: (0, 0, 0)),
                pl.BlockSpec((1, width), lambda b, _, at: (0, 0)),
                pl.BlockSpec((heads, 2 * BLOCK), lambda b, _, at: (0, 0)),
            ],
            out_specs=(
                pl.BlockSpec((BLOCK, width3), lambda b, _, at: (at[last - b], 0)),
                pl.BlockSpec((heads, DH, DH), lambda b, _, at: (0, 0, 0)),
                pl.BlockSpec((1, width), lambda b, _, at: (0, 0)),
                pl.BlockSpec((heads, NEAR, QTILE), lambda b, _, at: (0, 0, 0)),
                pl.BlockSpec((heads, 8, QTILE), lambda b, _, at: (0, 0, 0)),
            ),
            scratch_shapes=[
                pltpu.VMEM((STATE_VECTORS, width), f32),
                pltpu.VMEM((2, BLOCK, width), f32),
                pltpu.VMEM((2, 2 * BLOCK, DH), f32),
                pltpu.VMEM((heads, SPAN, QTILE), f32),
            ],
        ),
        compiler_params=pltpu.CompilerParams(vmem_limit_bytes=40 << 20),
        cost_estimate=pl.CostEstimate(
            flops=blocks * heads * 512 * 2400 * 128 * 10, bytes_accessed=20 << 20, transcendentals=10 << 20
        ),
        name="attend_back",
    )(length, order, qkv, qkv, dout, out, mem, upd, lse, slse, sgrad, state_query, forget, bias)


def gather_kernel(
    seq,
    hi,
    lo,
    tok_ref,
    grad_ref,
    wq_ref,
    ga_ref,
    gm_ref,
    wo_ref,
    wu_ref,
    toks_ref,
    grads_ref,
    wqs_ref,
    gas_ref,
    gms_ref,
    wos_ref,
    wus_ref,
    *rest,
):
    own_bufs = rest[:7]
    own_sem, store_sem, seq_send, seq_recv, z_send, z_recv, y_send, y_recv = rest[7:]
    me = lax.axis_index("seq")
    f = lax.axis_index("fsdp")
    fsdp = hi * lo
    bits = [1 << i for i in range(seq.bit_length() - 1)]
    greet(bits, hi, lo)

    pairs = ((tok_ref, toks_ref), (grad_ref, grads_ref))

    def seq_copy(i, source, slot, bit):
        src, out = pairs[i]
        return pltpu.make_async_remote_copy(
            src_ref=out.at[source] if source else src,
            dst_ref=out.at[slot],
            send_sem=seq_send.at[i, slot],
            recv_sem=seq_recv.at[i, slot],
            device_id={"seq": me ^ bit},
            device_id_type=MESH,
        )

    sends = []

    def send(i, source, slot, bit):
        sends.append(seq_copy(i, source, slot, bit))
        sends[-1].start()

    high = [bit for bit in reversed(bits) if bit > 1]
    if high:
        send(0, 0, high[0], high[0])
    if seq > 1:
        send(0, 0, 1, 1)

    width = wqs_ref.shape[2] // 3
    share = wus_ref.shape[2] // fsdp
    every = wq_ref.shape[1] // 3
    loads = [[] for _ in own_bufs]

    def load(i, src, dst):
        loads[i].append(pltpu.make_async_copy(src, dst, own_sem.at[i, len(loads[i])]))
        loads[i][-1].start()

    wq_buf, ga_buf, gm_buf, wo_buf, wu_buf, tok_buf, grad_buf = own_bufs
    for c in range(3):
        cols = pl.ds(pl.multiple_of(c * every + me * width, width), width)
        load(0, wq_ref.at[:, cols], wq_buf.at[:, pl.ds(c * width, width)])
    load(1, ga_ref, ga_buf)
    load(2, gm_ref, gm_buf)
    load(3, wo_ref.at[me], wo_buf)
    if wu_ref.shape[1] == wus_ref.shape[2]:
        load(4, wu_ref, wu_buf)
    else:
        for c in range(fsdp):
            cols = pl.ds(pl.multiple_of((c * seq + me) * share, share), share)
            load(4, wu_ref.at[:, cols], wu_buf.at[:, pl.ds(c * share, share)])
    load(5, tok_ref, tok_buf)
    load(6, grad_ref, grad_buf)
    outs = (wqs_ref, gas_ref, gms_ref, wos_ref, wus_ref)
    start, step, arrive, drain = line_gather(
        hi, lo, lambda i, origin: outs[i].at[origin], lambda i: own_bufs[i], z_send, z_recv, y_send, y_recv
    )
    own_stores = []
    for i in range(len(own_bufs)):
        for c in loads[i]:
            c.wait()
        if i < len(outs):
            start(i)
        target = outs[i].at[f] if i < len(outs) else pairs[i - len(outs)][1].at[0]
        own_stores.append(pltpu.make_async_copy(own_bufs[i], target, store_sem.at[i]))
        own_stores[-1].start()
    if high:
        send(1, 0, high[0], high[0])
    if seq > 1:
        send(1, 0, 1, 1)
    for t in range(hi - 1):
        for i in range(len(outs)):
            step(i, t)
    for i in range(len(pairs)):
        have = [0]
        for n, bit in enumerate(high):
            if n:
                for j in have:
                    send(i, j, j ^ bit, bit)
            for j in have:
                seq_copy(i, 0, j ^ bit, bit).wait_recv()
                send(i, j ^ bit, j ^ bit ^ 1, 1)
            have += [j ^ bit for j in have]
        if seq > 1:
            for j in have:
                seq_copy(i, 0, j ^ 1, 1).wait_recv()
    for i in range(len(outs)):
        arrive(i)
    for i in range(len(outs)):
        drain(i)
    for c in sends:
        c.wait_send()
    for c in own_stores:
        c.wait()


def gather_start(tokens, grads, w_qkv, gain_a, gain_m, w_out, w_up, seq, fsdp):
    lo = 2
    hi = fsdp // lo
    dim_rows, hidden = w_up.shape
    share = hidden // (seq * fsdp)
    if share % 128:
        w_up = lax.dynamic_slice_in_dim(w_up.reshape(dim_rows, fsdp, seq, share), lax.axis_index("seq"), 1, axis=2)
        w_up = w_up.reshape(dim_rows, fsdp * share)
    anywhere = pl.BlockSpec(memory_space=pl.ANY)
    dma = pltpu.SemaphoreType.DMA
    shapes = (
        (seq,) + tokens.shape,
        (seq,) + grads.shape,
        (fsdp, dim_rows, w_qkv.shape[1] // seq),
        (fsdp,) + gain_a.shape,
        (fsdp,) + gain_m.shape,
        (fsdp,) + w_out.shape[1:],
        (fsdp, dim_rows, hidden // seq),
    )
    return pl.pallas_call(
        functools.partial(gather_kernel, seq, hi, lo),
        out_shape=tuple(jax.ShapeDtypeStruct(shape, bf16) for shape in shapes),
        in_specs=[anywhere] * 7,
        out_specs=(anywhere,) * 7,
        scratch_shapes=[pltpu.VMEM(shape[1:], bf16) for shape in shapes[2:] + shapes[:2]]
        + [dma((7, max(fsdp, 3))), dma((7,)), dma((2, seq)), dma((2, seq))]
        + line_sems(5, hi),
        compiler_params=pltpu.CompilerParams(collective_id=0, has_side_effects=True),
        name="gather_start",
    )(tokens, grads, w_qkv, gain_a, gain_m, w_out, w_up)


def finish_kernel(
    seq,
    hi,
    lo,
    chunks,
    dn_ref,
    gq_ref,
    gu_ref,
    gd_ref,
    go_ref,
    small_ref,
    mlp_gain_ref,
    tok_ref,
    dmid_ref,
    gain_ref,
    tg_ref,
    rq_ref,
    ru_ref,
    rd_ref,
    ro_ref,
    ssum_ref,
    gsum_ref,
    dn_own,
    dn_in,
    dn_low,
    dn_acc,
    tq,
    tu,
    td,
    to,
    yq,
    yu,
    yd,
    yo,
    lq,
    lu,
    ld,
    lq_r,
    lu_r,
    ld_r,
    lo_l,
    lo_r,
    xq,
    xu,
    sy,
    sz,
    gains,
    gy,
    gz,
    gs,
    load_sem,
    dn_send,
    dn_recv,
    y_send,
    y_recv,
    z_send,
    z_recv,
    x_send,
    x_recv,
    s_send,
    s_recv,
    g_send,
    g_recv,
):
    me = lax.axis_index("seq")
    f = lax.axis_index("fsdp")
    z, y = f // lo, f % lo
    peer = z * lo + 1 - y
    grads = (gq_ref, gu_ref, gd_ref, go_ref)
    totals = (tq, tu, td, to)
    from_y = (yq, yu, yd, yo)
    from_z = ((lq, lq_r), (lu, lu_r), (ld, ld_r), (lo_l, lo_r))
    tensors = range(4)
    rows = dn_ref.shape[1] // chunks

    barrier = pltpu.get_barrier_semaphore()
    for k in range(1, seq):
        pl.semaphore_signal(barrier, inc=1, device_id={"seq": me ^ k}, device_id_type=MESH)
    for k in range(1, hi):
        pl.semaphore_signal(barrier, inc=1, device_id={"fsdp": lax.rem(z + k, hi) * lo + y}, device_id_type=MESH)
    pl.semaphore_signal(barrier, inc=1, device_id={"fsdp": peer}, device_id_type=MESH)
    pl.semaphore_wait(barrier, seq + hi - 1)

    def block(i, target):
        return grads[i].at[:, target] if i < 2 else grads[i].at[target]

    def remote(src, dst, send, recv, axis, target):
        return pltpu.make_async_remote_copy(
            src_ref=src, dst_ref=dst, send_sem=send, recv_sem=recv, device_id={axis: target}, device_id_type=MESH
        )

    evens = list(range(0, seq, 2))
    loads = [pltpu.make_async_copy(dn_ref.at[j], dn_own.at[j // 2], load_sem.at[0, j // 2]) for j in evens]
    for c in loads:
        c.start()

    levels = []
    active = list(range(seq))
    bit = 1
    slot = 0
    while bit < seq:
        keep = [j for j in active if not j & bit]
        levels.append((bit, keep, {j: slot + n for n, j in enumerate(keep)}))
        slot += len(keep)
        active = keep
        bit *= 2
    order = sorted(evens, reverse=True)

    def piece_rows(c):
        return pl.ds(c * rows, rows)

    def dn_copy(level, j, c):
        bit, _, slots = levels[level]
        src = dn_ref.at[j ^ bit, piece_rows(c)] if level == 0 else dn_low.at[(j ^ bit) // 2, piece_rows(c)]
        return remote(
            src, dn_in.at[slots[j], piece_rows(c)], dn_send.at[slots[j], c], dn_recv.at[slots[j], c], "seq", me ^ bit
        )

    for c in range(chunks):
        for j in order[:1]:
            dn_copy(0, j, c).start()
    y_copies = {}
    for i in tensors:
        for d in range(hi):
            y_copies[i, d] = remote(
                block(i, d * lo + 1 - y), from_y[i].at[d], y_send.at[i, d], y_recv.at[i, d], "fsdp", peer
            )
    grad_loads = {}
    for i in tensors:
        for d in range(hi):
            grad_loads[i, d] = pltpu.make_async_copy(block(i, d * lo + y), totals[i].at[d], load_sem.at[1 + i, d])
    small_y = remote(small_ref, sy, s_send.at[0], s_recv.at[0], "fsdp", peer)
    small_y.start()
    for d in range(hi):
        y_copies[0, d].start()
        grad_loads[0, d].start()
    for j in order[1:]:
        for c in range(chunks):
            dn_copy(0, j, c).start()
    for i in tensors[1:]:
        for d in range(hi):
            y_copies[i, d].start()
            grad_loads[i, d].start()
    for c in loads:
        c.wait()
    for level, (bit, keep, slots) in enumerate(levels):
        later = levels[level + 1 :]
        for j in sorted(keep, reverse=True):
            for c in range(chunks):
                if level == len(levels) - 1:
                    continue
                dn_copy(level, j, c).wait_recv()
                at = piece_rows(c)
                own = dn_own[j // 2, at].astype(f32) if level == 0 else dn_low[j // 2, at].astype(f32)
                if j == 0:
                    own = own if level == 0 else dn_acc[at]
                    dn_acc[at] = own + dn_in[slots[j], at].astype(f32)
                else:
                    dn_low[j // 2, at] = (own + dn_in[slots[j], at].astype(f32)).astype(bf16)
                    nxt = later[0]
                    if j & nxt[0]:
                        dn_copy(level + 1, j ^ nxt[0], c).start()

    small_y.wait_recv()
    sz[z] = small_ref[...] + sy[...]
    small_z = []
    for k in range(1, hi):
        target = lax.rem(z + k, hi)
        small_z.append(remote(sz.at[z], sz.at[z], s_send.at[k], s_recv.at[k], "fsdp", target * lo + y))
        small_z[-1].start()

    def reduce_tensor(i):
        total = totals[i]
        for d in range(hi):
            grad_loads[i, d].wait()
            y_copies[i, d].wait_recv()
            total[d] = (total[d].astype(f32) + from_y[i][d].astype(f32)).astype(bf16)
        from_right, from_left = from_z[i]
        for t in range(hi - 1):
            d = t - (hi - 1 - z)
            m = hi - 1 - (t - z)

            @pl.when((d >= 0) & (d < z))
            def _():
                at = jnp.clip(d, 0, hi - 1)
                remote(
                    total.at[at], from_right.at[t], z_send.at[i, 0, t], z_recv.at[i, 0, t], "fsdp", (z - 1) * lo + y
                ).start()

            @pl.when((m > z) & (m < hi))
            def _():
                at = jnp.clip(m, 0, hi - 1)
                remote(
                    total.at[at], from_left.at[t], z_send.at[i, 1, t], z_recv.at[i, 1, t], "fsdp", (z + 1) * lo + y
                ).start()

            dr = t - (hi - 2 - z)

            @pl.when((z + 1 < hi) & (dr >= 0))
            def _():
                at = jnp.clip(dr, 0, hi - 1)
                remote(
                    total.at[at], from_right.at[t], z_send.at[i, 0, t], z_recv.at[i, 0, t], "fsdp", f
                ).wait_recv()
                total[at] = (total[at].astype(f32) + from_right[t].astype(f32)).astype(bf16)

            ml = hi - 1 - (t - (z - 1))

            @pl.when((z > 0) & (ml < hi))
            def _():
                at = jnp.clip(ml, 0, hi - 1)
                remote(
                    total.at[at], from_left.at[t], z_send.at[i, 1, t], z_recv.at[i, 1, t], "fsdp", f
                ).wait_recv()
                total[at] = (total[at].astype(f32) + from_left[t].astype(f32)).astype(bf16)

    exchanged = (xq, xu)
    results = (rq_ref, ru_ref, rd_ref, ro_ref)

    def exchange(i):
        for k in range(1, seq):
            remote(
                totals[i].at[z, me ^ k], exchanged[i].at[me], x_send.at[i, k], x_recv.at[i, k], "seq", me ^ k
            ).start()

    reduce_tensor(0)
    exchange(0)

    if levels:
        bit, keep, slots = levels[-1]
    gain = gain_ref[...]
    part = jnp.zeros((8, gain.shape[1]), f32)
    for c in range(chunks):
        at = piece_rows(c)
        if levels:
            dn_copy(len(levels) - 1, 0, c).wait_recv()
        if len(levels) > 1:
            dn = dn_acc[at]
        else:
            dn = dn_own[0, at].astype(f32)
        if levels:
            dn = dn + dn_in[slots[0], at].astype(f32)
        x = tok_ref[at].astype(f32)
        rho = lax.rsqrt(jnp.mean(x * x, axis=-1, keepdims=True) + EPSILON)
        scaled = gain * dn
        mean = jnp.mean(x * scaled, axis=-1, keepdims=True)
        tg_ref[at] = dmid_ref[at] + rho * scaled - x * (rho * rho * rho * mean)
        prod = dn * x * rho
        part += functools.reduce(jnp.add, [prod[n : n + 8] for n in range(0, rows, 8)])
    gains[0:8] = mlp_gain_ref[...]
    gains[8:16] = part
    gain_y = remote(gains, gy, g_send.at[0], g_recv.at[0], "fsdp", peer)
    gain_y.start()
    reduce_tensor(1)
    exchange(1)
    gain_y.wait_recv()
    gz[z] = gains[...] + gy[...]
    gain_z = []
    for k in range(1, hi):
        target = lax.rem(z + k, hi)
        gain_z.append(remote(gz.at[z], gz.at[z], g_send.at[k], g_recv.at[k], "fsdp", target * lo + y))
        gain_z[-1].start()
    reduce_tensor(2)
    for k in range(1, hi):
        source = lax.rem(z + hi - k, hi)
        remote(gz.at[source], gz.at[source], g_send.at[k], g_recv.at[k], "fsdp", f).wait_recv()
        remote(sz.at[source], sz.at[source], s_send.at[k], s_recv.at[k], "fsdp", f).wait_recv()
    gs[me] = functools.reduce(jnp.add, [gz[d] for d in range(hi)])
    gain_x = []
    for k in range(1, seq):
        gain_x.append(remote(gs.at[me], gs.at[me], g_send.at[hi + k], g_recv.at[hi + k], "seq", me ^ k))
        gain_x[-1].start()
    ssum_ref[...] = functools.reduce(jnp.add, [sz[d] for d in range(hi)])
    reduce_tensor(3)
    rd_ref[...] = td[z].astype(f32)
    ro_ref[...] = to[z].astype(f32)
    for i in range(2):
        for k in range(1, seq):
            remote(
                totals[i].at[z, me], exchanged[i].at[me ^ k], x_send.at[i, k], x_recv.at[i, k], "seq", me
            ).wait_recv()
        exchanged[i][me] = totals[i][z, me]
        for k in range(seq):
            results[i][k] = exchanged[i][k].astype(f32)
    for k in range(1, seq):
        remote(gs.at[me ^ k], gs.at[me ^ k], g_send.at[hi + k], g_recv.at[hi + k], "seq", me).wait_recv()
    gsum_ref[...] = functools.reduce(jnp.add, [gs[k] for k in range(seq)])

    for level, (bit, keep, slots) in enumerate(levels):
        for j in keep:
            for c in range(chunks):
                dn_copy(level, j, c).wait_send()
    for i in tensors:
        for d in range(hi):
            y_copies[i, d].wait_send()
        for t in range(hi - 1):
            d = t - (hi - 1 - z)
            m = hi - 1 - (t - z)

            @pl.when((d >= 0) & (d < z))
            def _():
                remote(
                    totals[i].at[0], from_z[i][0].at[t], z_send.at[i, 0, t], z_recv.at[i, 0, t], "fsdp", f
                ).wait_send()

            @pl.when((m > z) & (m < hi))
            def _():
                remote(
                    totals[i].at[0], from_z[i][1].at[t], z_send.at[i, 1, t], z_recv.at[i, 1, t], "fsdp", f
                ).wait_send()
    for i in range(2):
        for k in range(1, seq):
            remote(
                totals[i].at[z, me], exchanged[i].at[me], x_send.at[i, k], x_recv.at[i, k], "seq", me
            ).wait_send()
    for c in [small_y, gain_y] + small_z + gain_z + gain_x:
        c.wait_send()


def finish(dn, gq, gu, gd, go, small, mlp_gain, tok, dmid, gain, seq, fsdp):
    lo = 2
    hi = fsdp // lo
    chunks = 4
    anywhere = pl.BlockSpec(memory_space=pl.ANY)
    vmem = pl.BlockSpec(memory_space=pltpu.VMEM)
    block_q = (seq,) + gq.shape[2:]
    block_u = (seq,) + gu.shape[2:]
    block_d = gd.shape[1:]
    block_o = go.shape[1:]
    blocks = (block_q, block_u, block_d, block_o)
    tok_rows, dim = tok.shape
    sides = max(hi - 1, 1)

    def buf(lead, shape, kind=bf16):
        return pltpu.VMEM((lead,) + tuple(shape), kind)

    scratch = [
        buf(max(seq // 2, 1), (tok_rows, dim)),
        buf(max(seq - 1, 1), (tok_rows, dim)),
        buf(max(seq // 2, 1), (tok_rows, dim)),
        pltpu.VMEM((tok_rows, dim), f32),
    ]
    scratch += [buf(hi, b) for b in blocks]
    scratch += [buf(hi, b) for b in blocks]
    scratch += [buf(sides, b) for b in (block_q, block_u, block_d)] * 2
    scratch += [buf(sides, block_o), buf(sides, block_o)]
    scratch += [pltpu.VMEM(block_q, bf16), pltpu.VMEM(block_u, bf16)]
    scratch += [
        pltpu.VMEM(small.shape, f32),
        buf(hi, small.shape, f32),
        pltpu.VMEM((16, dim), f32),
        pltpu.VMEM((16, dim), f32),
        buf(hi, (16, dim), f32),
        buf(seq, (16, dim), f32),
    ]
    dma = pltpu.SemaphoreType.DMA
    scratch += [
        dma((5, max(hi, seq))),
        dma((seq, chunks)),
        dma((seq, chunks)),
        dma((4, hi)),
        dma((4, hi)),
        dma((4, 2, hi)),
        dma((4, 2, hi)),
        dma((2, seq)),
        dma((2, seq)),
        dma((hi,)),
        dma((hi,)),
        dma((hi + seq,)),
        dma((hi + seq,)),
    ]
    return pl.pallas_call(
        functools.partial(finish_kernel, seq, hi, lo, chunks),
        out_shape=(
            jax.ShapeDtypeStruct((tok_rows, dim), f32),
            jax.ShapeDtypeStruct(block_q, f32),
            jax.ShapeDtypeStruct(block_u, f32),
            jax.ShapeDtypeStruct(block_d, f32),
            jax.ShapeDtypeStruct(block_o, f32),
            jax.ShapeDtypeStruct(small.shape, f32),
            jax.ShapeDtypeStruct((16, dim), f32),
        ),
        in_specs=[anywhere] * 5 + [vmem] * 5,
        out_specs=(vmem,) * 7,
        scratch_shapes=scratch,
        compiler_params=pltpu.CompilerParams(
            collective_id=1, has_side_effects=True, vmem_limit_bytes=56 << 20
        ),
        name="finish",
    )(dn, gq, gu, gd, go, small, mlp_gain, tok, dmid, gain)


GELU_P = 0.24
GELU_C = (
    0.08951261885080208,
    0.15562094398234086,
    -0.15437154502074169,
    0.6261054138112487,
    -0.6465313024138201,
    0.5547927291245551,
    -0.125128858665134,
)


def gelu_parts(x):
    size = jnp.abs(x)
    t = 1.0 / (1.0 + GELU_P * size)
    poly = GELU_C[-1] * t
    for c in GELU_C[-2::-1]:
        poly = (poly + c) * t
    bell = jnp.exp2(x * x * (-0.5 * LOG2E))
    tail = poly * bell
    cdf = jnp.where(x < 0.0, tail, 1.0 - tail)
    return x * cdf, cdf + x * bell * (1.0 / math.sqrt(2.0 * math.pi))


def mlp_kernel(seq, sub, length_ref, *refs):
    refs = list(refs)

    def take(count):
        taken = refs[:count]
        del refs[:count]
        return taken

    own_ref, others_ref, tok_ref, grads_ref = take(4)
    att_refs = [own_ref] + [others_ref.at[k] for k in range(1, seq)]
    grad_refs = [grads_ref.at[j] for j in range(seq)]
    wo_ref, wu_ref, wd_ref, gain_ref = take(4)
    mid_ref, dmid_ref, gsum_ref, db_ref, mo_ref, ug_ref, dg_ref = take(7)
    att_buf, tok_buf, gm, nm, hid, dpre, low, into, acc = take(9)
    dbv = low.at[0]
    depth = att_buf.shape[0]
    load_sem, gm_sem, dn_send, dn_recv, db_send, db_recv, mo_sem, own_sem = take(8)

    me = lax.axis_index("seq")
    length = length_ref[0]
    dim = wo_ref.shape[0]
    width = dim // seq
    rows = tok_ref.shape[1]
    share = wu_ref.shape[1]
    bits = [1 << i for i in range(seq.bit_length() - 1)]

    barrier = pltpu.get_barrier_semaphore()
    for bit in bits:
        pl.semaphore_signal(barrier, inc=1, device_id={"seq": me ^ bit}, device_id_type=MESH)
    pl.semaphore_wait(barrier, len(bits))

    order = list(reversed(range(seq)))
    gm_loads = {j: pltpu.make_async_copy(grad_refs[j], gm.at[pl.ds(j * rows, rows)], gm_sem.at[j]) for j in order}

    def chunk_loads(n):
        j, slot = order[n], n % depth
        copies = [
            pltpu.make_async_copy(
                att_refs[k].at[pl.ds(j * rows, rows)], att_buf.at[slot, k], load_sem.at[slot, k]
            )
            for k in range(seq)
        ]
        copies.append(pltpu.make_async_copy(tok_ref.at[j], tok_buf.at[slot], load_sem.at[slot, seq]))
        return copies

    for c in chunk_loads(0):
        c.start()
    for j in order:
        gm_loads[j].start()

    slots = {}
    for bit in bits:
        for j in range(0, seq, 2 * bit):
            slots[bit, j] = len(slots)

    def dn_copy(bit, j):
        slot = slots[bit, j]
        return pltpu.make_async_remote_copy(
            src_ref=low.at[j ^ bit],
            dst_ref=into.at[slot],
            send_sem=dn_send.at[slot],
            recv_sem=dn_recv.at[slot],
            device_id={"seq": me ^ bit},
            device_id_type=MESH,
        )

    gain = gain_ref[...]
    for n, j in enumerate(order):
        slot = n % depth
        if depth == 1 and n:
            for c in chunk_loads(n):
                c.start()
        for c in chunk_loads(n):
            c.wait()
        if depth == 2 and n + 1 < seq:
            for c in chunk_loads(n + 1):
                c.start()
        gm_loads[j].wait()
        base = (j ^ me) * rows

        @pl.loop(0, rows // sub)
        def _(s):
            at = pl.ds(pl.multiple_of(s * sub, sub), sub)
            here = pl.ds(pl.multiple_of(j * rows + s * sub, sub), sub)
            position = base + s * sub + lax.broadcasted_iota(jnp.int32, (sub, 1), 0)
            live = jnp.where(position < length, 1.0, 0.0)
            masked = (gm[here].astype(f32) * live).astype(bf16)
            gm[here] = masked
            mid = tok_buf[slot, at].astype(f32)
            for k in range(seq):
                own = pl.ds(pl.multiple_of((me ^ k) * width, width), width)
                mid = mid + dot(att_buf[slot, k, at], wo_ref[own])
            rho = lax.rsqrt(jnp.mean(mid * mid, axis=-1, keepdims=True) + EPSILON)
            normed = (mid * rho * gain).astype(bf16)
            nm[here] = normed
            if j == 0:
                mid_ref[at] = mid
            for c in range(0, share, 256):
                cols = slice(c, c + 256)
                value, slope = gelu_parts(dot(normed, wu_ref[:, cols]))
                hid[here, cols] = value.astype(bf16)
                dpre[here, cols] = (dot_t(masked, wd_ref[cols]) * slope).astype(bf16)
            part = dot_t(dpre[here], wu_ref[...])
            if j % 2:
                low[j, at] = part.astype(bf16)
            else:
                acc[at] = part

        if j % 2:
            dn_copy(1, j ^ 1).start()
        elif j:
            for bit in bits:
                if j & bit:
                    low[j] = acc[...].astype(bf16)
                    dn_copy(bit, j ^ bit).start()
                    break
                dn_copy(bit, j).wait_recv()
                acc[...] += into[slots[bit, j]].astype(f32)

    for c in range(0, dim, 256):
        ug_ref[c : c + 256] = t_dot(nm[:, c : c + 256], dpre[...]).astype(bf16)

    for bit in bits:
        dn_copy(bit, 0).wait_recv()
    step = 128
    part = jnp.zeros((8, dim), f32)
    for r in range(0, rows, step):
        at = slice(r, r + step)
        dn = acc[at]
        for bit in bits:
            dn = dn + into[slots[bit, 0], at].astype(f32)
        mid = mid_ref[at]
        rho = lax.rsqrt(jnp.mean(mid * mid, axis=-1, keepdims=True) + EPSILON)
        scaled = gain * dn
        mean = jnp.mean(mid * scaled, axis=-1, keepdims=True)
        dmid = gm[at].astype(f32) + rho * scaled - mid * (rho * rho * rho * mean)
        dmid_ref[at] = dmid
        dbv[at] = dmid.astype(bf16)
        prod = dn * mid * rho
        part += functools.reduce(jnp.add, [prod[i : i + 8] for i in range(0, step, 8)])
    gsum_ref[...] = part

    def db_copy(source, target, bit):
        return pltpu.make_async_remote_copy(
            src_ref=db_ref.at[source] if source else dbv,
            dst_ref=db_ref.at[target],
            send_sem=db_send.at[target],
            recv_sem=db_recv.at[target],
            device_id={"seq": me ^ bit},
            device_id_type=MESH,
        )

    own_copy = pltpu.make_async_copy(dbv, db_ref.at[0], own_sem)
    own_copy.start()
    sends = []
    high = [bit for bit in reversed(bits) if bit > 1]

    def send(source, target, bit):
        sends.append(db_copy(source, target, bit))
        sends[-1].start()

    if high:
        send(0, high[0], high[0])
    if seq > 1:
        send(0, 1, 1)
    for c in range(0, share, 256):
        dg_ref[c : c + 256] = t_dot(hid[:, c : c + 256], gm[...]).astype(bf16)
    mo_copies = []
    for j in range(seq):
        at = slice(j * rows, (j + 1) * rows)
        nm[at] = dot(hid[at], wd_ref[...]).astype(bf16)
        mo_copies.append(pltpu.make_async_copy(nm.at[pl.ds(j * rows, rows)], mo_ref.at[j], mo_sem.at[j]))
        mo_copies[-1].start()
    have = [0]
    for n, bit in enumerate(high):
        if n:
            for j in have:
                send(j, j ^ bit, bit)
        for j in have:
            db_copy(0, j ^ bit, bit).wait_recv()
            send(j ^ bit, j ^ bit ^ 1, 1)
        have += [j ^ bit for j in have]
    if seq > 1:
        for j in have:
            db_copy(0, j ^ 1, 1).wait_recv()
    for c in sends:
        c.wait_send()
    own_copy.wait()
    for c in mo_copies:
        c.wait()
    for bit in bits:
        for j in range(0, seq, 2 * bit):
            dn_copy(bit, j).wait_send()


def mlp(length, own, others, tok, grads, wo, wu, wd, gain):
    seq, rows, dim = tok.shape
    share = wu.shape[1]
    sub = 256
    depth = 2 if seq <= 4 else 1
    anywhere = pl.BlockSpec(memory_space=pl.ANY)
    vmem = pl.BlockSpec(memory_space=pltpu.VMEM)
    dma = pltpu.SemaphoreType.DMA
    return pl.pallas_call(
        functools.partial(mlp_kernel, seq, sub),
        out_shape=(
            jax.ShapeDtypeStruct((rows, dim), f32),
            jax.ShapeDtypeStruct((rows, dim), f32),
            jax.ShapeDtypeStruct((8, dim), f32),
            jax.ShapeDtypeStruct((seq, rows, dim), bf16),
            jax.ShapeDtypeStruct((seq, rows, dim), bf16),
            jax.ShapeDtypeStruct((dim, share), bf16),
            jax.ShapeDtypeStruct((share, dim), bf16),
        ),
        in_specs=[pl.BlockSpec(memory_space=pltpu.SMEM)] + [anywhere] * 4 + [vmem] * 4,
        out_specs=(vmem, vmem, vmem, anywhere, anywhere, vmem, vmem),
        scratch_shapes=[
            pltpu.VMEM((depth, seq, rows, dim // seq), bf16),
            pltpu.VMEM((depth, rows, dim), bf16),
            pltpu.VMEM((seq * rows, dim), bf16),
            pltpu.VMEM((seq * rows, dim), bf16),
            pltpu.VMEM((seq * rows, share), bf16),
            pltpu.VMEM((seq * rows, share), bf16),
            pltpu.VMEM((seq, rows, dim), bf16),
            pltpu.VMEM((max(seq - 1, 1), rows, dim), bf16),
            pltpu.VMEM((rows, dim), f32),
            dma((2, seq + 1)),
            dma((seq,)),
            dma((seq,)),
            dma((seq,)),
            dma((seq,)),
            dma((seq,)),
            dma((seq,)),
            dma,
        ],
        compiler_params=pltpu.CompilerParams(collective_id=2, has_side_effects=True, vmem_limit_bytes=60 << 20),
        cost_estimate=pl.CostEstimate(
            flops=2 * rows * seq * dim * (dim + 6 * share), bytes_accessed=32 << 20, transcendentals=rows * seq * share
        ),
        name="mlp",
    )(length, own, others, tok, grads, wo, wu, wd, gain)


def swap(value, bit):
    count = lax.axis_size("seq")
    return lax.ppermute(value, "seq", [(i, i ^ bit) for i in range(count)])


def seq_bits():
    count = lax.axis_size("seq")
    return [1 << i for i in reversed(range(1, count.bit_length() - 1))]


def seq_gather(value):
    chunks = {0: value}
    for bit in seq_bits():
        for j in list(chunks):
            chunks[j ^ bit] = swap(chunks[j], bit)
    for j in list(chunks):
        chunks[j ^ 1] = swap(chunks[j], 1)
    return [chunks[j] for j in range(len(chunks))]


def seq_reduce(parts):
    count = len(parts)
    parts = dict(enumerate(parts))
    for j in range(count - 2, -1, -2):
        parts[j] = parts[j].astype(f32) + swap(parts.pop(j ^ 1).astype(bf16), 1).astype(f32)
    for bit in reversed(seq_bits()):
        keep = [j for j in parts if not j & bit]
        for j in sorted(keep, reverse=True):
            parts[j] = parts[j] + swap(parts.pop(j ^ bit).astype(bf16), bit).astype(f32)
    return parts[0]


def bias_table_grad(near, far):
    distance = tile_distance().T[SPAN - NEAR :]
    bucket = np.where((distance >= 0) & (distance < BLOCK), bucket_of(np.clip(distance, 0, BLOCK)), BUCKETS)
    bucket = jnp.asarray(bucket.astype(np.int32))
    columns = [jnp.sum(jnp.where((bucket == i)[None], near, 0.0), axis=(1, 2)) for i in range(BUCKETS)]
    columns[-1] = columns[-1] + jnp.sum(far, axis=(1, 2))
    return jnp.stack(columns, axis=1)


def inverse_rms(values):
    return lax.rsqrt(jnp.mean(values * values, axis=-1, keepdims=True) + EPSILON)


def norm_back(values, gain, rho, grad):
    scaled = gain * grad
    mean = jnp.mean(values * scaled, axis=-1, keepdims=True)
    gain_grad = (grad * values * rho).reshape(-1, 8, values.shape[1])
    return rho * scaled - values * (rho * rho * rho * mean), jnp.sum(gain_grad, axis=0)


def body(
    tokens,
    lengths,
    state_init,
    w_qkv,
    w_out,
    w_up,
    w_down,
    norm_attn,
    norm_mlp,
    rel_bias,
    state_query,
    gate_bias,
    out_grad,
    state_grad,
):
    seq_count = lax.axis_size("seq")
    fsdp_count = lax.axis_size("fsdp")
    seq_at = lax.axis_index("seq")
    heads = H // seq_count
    width = heads * DH
    tok_rows, dim = tokens.shape[1:]
    rows = tok_rows * seq_count
    hidden_all = w_up.shape[1]
    share = hidden_all // (seq_count * fsdp_count)

    piece = dim // (seq_count * fsdp_count)
    all_tokens, all_grad, qkv_w, gain_attn, gain_mlp, own_out, up_w = gather_start(
        tokens[0],
        out_grad[0],
        w_qkv,
        norm_attn.reshape(1, -1),
        norm_mlp.reshape(1, -1),
        w_out.reshape(seq_count, piece, dim),
        w_up,
        seq_count,
        fsdp_count,
    )
    qkv_w = qkv_w.reshape(dim, 3 * width)
    up_w = up_w.reshape(dim, hidden_all // seq_count)
    gain_attn = gain_attn.reshape(dim).astype(f32)
    gain_mlp = gain_mlp.reshape(dim).astype(f32)
    own_down = lax.dynamic_slice_in_dim(w_down, seq_at * share, share, axis=0)

    bias = bias_vector(rel_bias)
    forget = jax.nn.sigmoid(gate_bias)
    forget_row = forget.reshape(1, width)
    chunk_ids = jnp.arange(seq_count, dtype=jnp.int32)
    order = chunk_ids ^ seq_at

    inputs = all_tokens.reshape(rows, dim).astype(f32)
    normed = (inputs * inverse_rms(inputs) * gain_attn).astype(bf16)
    qkv = dot(normed, qkv_w).astype(bf16)
    attended, others, out_w, down_w, final_memory, mem, upd, lse, slse = attend(
        qkv,
        state_init[0],
        lengths,
        state_query,
        forget_row,
        bias,
        own_out,
        own_down,
        heads,
        seq_count,
        fsdp_count,
    )
    out_w = out_w.reshape(dim, dim)
    down_w = down_w.reshape(fsdp_count * share, dim)
    own_out = lax.dynamic_slice_in_dim(out_w, seq_at * width, width, axis=0)
    mid_here, dmid, mlp_gain_grad, dbranch, mlp_parts, up_grad, down_grad = mlp(
        lengths, attended, others, all_tokens, all_grad, out_w, up_w, down_w, gain_mlp.reshape(1, dim)
    )
    dbranch = dbranch.reshape(rows, dim)
    dattended = dot_t(dbranch, own_out).astype(bf16)
    out_w_grad = t_dot(attended, dbranch)

    dqkv, dquery, dforget, near, far = attend_back(
        qkv, dattended, attended, mem, upd, lse, slse, state_grad[0], lengths, state_query, forget_row, bias, heads, order
    )
    mlp_parts, dqkv = lax.optimization_barrier((mlp_parts, dqkv))
    mlp_out = seq_reduce([mlp_parts[j] for j in range(seq_count)])
    live_here = (seq_at * tok_rows + jnp.arange(tok_rows, dtype=jnp.int32) < lengths[0]).astype(f32)[:, None]
    output = (live_here * (mid_here + mlp_out)).astype(bf16)[None]
    dnormed = dot_t(dqkv, qkv_w).astype(bf16).reshape(seq_count, tok_rows, dim)
    qkv_grad = t_dot(normed, dqkv).astype(bf16).reshape(seq_count, fsdp_count, piece, 3 * width)
    up_grad = up_grad.reshape(seq_count, fsdp_count, piece, hidden_all // seq_count)
    span = fsdp_count // seq_count
    down_grad = down_grad.reshape(seq_count, span, share, dim)
    moved = [lax.dynamic_slice_in_dim(down_grad, seq_at, 1, axis=0)]
    for k in range(1, seq_count):
        moved.append(swap(lax.dynamic_slice_in_dim(down_grad, seq_at ^ k, 1, axis=0), k))
    moved = lax.optimization_barrier(jnp.concatenate(moved, axis=0))
    moved = [lax.dynamic_slice_in_dim(moved, seq_at ^ k, 1, axis=0) for k in range(seq_count)]
    down_grad = jnp.swapaxes(jnp.concatenate(moved, axis=0), 0, 1).reshape(fsdp_count, share, dim)
    out_w_grad = out_w_grad.astype(bf16).reshape(fsdp_count, piece, dim)
    grad_gate = dforget.reshape(heads, DH) * forget * (1.0 - forget)
    grad_table = jnp.pad(bias_table_grad(near, far), ((0, 0), (0, DH - BUCKETS)))
    cut = heads * DH
    small = jnp.concatenate([dquery.reshape(cut, DH), grad_gate, grad_table], axis=0)
    small = jnp.pad(small, ((0, -small.shape[0] % 8), (0, 0)))
    tokens_grad, qkv_part, up_part, down_part, out_part, small, gain_sums = finish(
        dnormed,
        qkv_grad,
        up_grad,
        down_grad,
        out_w_grad,
        small,
        mlp_gain_grad,
        tokens[0],
        dmid,
        gain_attn.reshape(1, dim),
        seq_count,
        fsdp_count,
    )
    tokens_grad = tokens_grad[None]
    dquery = small[:cut].reshape(heads, DH, DH)
    grad_gate = small[cut : cut + heads]
    grad_table = small[cut + heads : cut + 2 * heads, :BUCKETS]
    up_part = up_part.reshape(seq_count, piece, fsdp_count, share)
    up_part = jnp.transpose(up_part, (1, 2, 0, 3)).reshape(piece, hidden_all)
    qkv_part = qkv_part.reshape(seq_count, piece, 3, width)
    qkv_part = jnp.transpose(qkv_part, (1, 2, 0, 3)).reshape(piece, 3 * H * DH)
    gain_sums = jnp.sum(gain_sums.reshape(2, 8, seq_count * fsdp_count, piece), axis=1)
    mine = seq_at * fsdp_count + lax.axis_index("fsdp")
    gain_sums = lax.dynamic_slice_in_dim(gain_sums, mine, 1, axis=1)[:, 0]
    mlp_gain_grad, attn_gain_grad = gain_sums[0], gain_sums[1]
    return (
        output,
        final_memory[None],
        tokens_grad,
        qkv_part,
        out_part,
        up_part,
        down_part,
        attn_gain_grad,
        mlp_gain_grad,
        grad_table,
        dquery,
        grad_gate,
    )


def solution(mesh):
    placed = (
        P("fsdp", "seq", None),
        P("fsdp"),
        P("fsdp", None, "seq"),
        P("fsdp", None),
        P("fsdp", None),
        P("fsdp", None),
        P("fsdp", None),
        P("fsdp"),
        P("fsdp"),
        P("seq", None),
        P("seq", None, None),
        P("seq", None),
        P("fsdp", "seq", None),
        P("fsdp", None, "seq"),
    )
    return jax.shard_map(
        body,
        mesh=mesh,
        in_specs=placed,
        out_specs=(
            P("fsdp", "seq", None),
            P("fsdp", None, "seq"),
            P("fsdp", "seq", None),
            P(("seq", "fsdp"), None),
            P(("seq", "fsdp"), None),
            P(("seq", "fsdp"), None),
            P(("seq", "fsdp"), None),
            P(("seq", "fsdp")),
            P(("seq", "fsdp")),
            P("seq", None),
            P("seq", None, None),
            P("seq", None),
        ),
        check_vma=False,
    )
```

```python
import functools
import math

import jax
import jax.numpy as jnp
import numpy as np
from jax import lax
from jax.experimental import pallas as pl
from jax.experimental.pallas import tpu as pltpu
from jax.sharding import PartitionSpec as P

H = 8
DH = 128
BLOCK = 512
STATE_VECTORS = 512
QTILE = 256
SPAN = BLOCK + QTILE

EPSILON = 1e-06
BUCKET_EDGES = (19, 21, 24, 27, 31, 35, 40, 46, 52, 59, 67, 77, 87, 99, 113)
BUCKETS = 32
LOG2E = math.log2(math.e)
SCALE = DH ** (-0.5)
NEAR = 384

f32 = jnp.float32
bf16 = jnp.bfloat16
MESH = pl.DeviceIdType.MESH


def bucket_of(distance):
    return np.minimum(distance, 16) + (distance[..., None] >= np.array(BUCKET_EDGES)).sum(-1)


def tile_distance():
    rows = np.arange(QTILE)[:, None]
    cols = np.arange(SPAN)[None, :]
    return rows + BLOCK - cols


def bias_vector(table):
    distance = BLOCK - np.arange(2 * BLOCK)
    inside = (distance >= 0) & (distance < BLOCK)
    bucket = jnp.asarray(np.where(inside, bucket_of(np.clip(distance, 0, BLOCK)), BUCKETS).astype(np.int32))
    total = jnp.full((table.shape[0], 2 * BLOCK), -jnp.inf, f32)
    for i in range(BUCKETS):
        total = jnp.where((bucket == i)[None], table[:, i : i + 1] * LOG2E, total)
    return total


def tile_bias(vector_ref, head):
    wide = jnp.broadcast_to(vector_ref[head : head + 1, :], (QTILE, 2 * BLOCK))
    return pltpu.roll(wide, 0, 1, stride=1, stride_axis=0)[:, :SPAN]


def dot(a, b):
    return jnp.dot(a, b, preferred_element_type=f32)


def dot_t(a, b):
    return lax.dot_general(a, b, (((1,), (1,)), ((), ())), preferred_element_type=f32)


def t_dot(a, b):
    return lax.dot_general(a, b, (((0,), (0,)), ((), ())), preferred_element_type=f32)


def to_row(column):
    wide = jnp.broadcast_to(column, (column.shape[0], 128))
    return wide.T[0:1, :]


def context_pieces(tile):
    start = tile * QTILE
    pieces = []
    if start < BLOCK:
        pieces.append((0, start, BLOCK, 0))
    pieces.append((1, 0, start + QTILE, BLOCK - start))
    return pieces


def softmax_parts(scores):
    top = functools.reduce(jnp.maximum, [jnp.max(s, axis=-1, keepdims=True) for s in scores])
    raised = [jnp.exp2(s - top) for s in scores]
    total = functools.reduce(jnp.add, [jnp.sum(e, axis=-1, keepdims=True) for e in raised])
    return raised, total, top + jnp.log2(total)


def line_gather(hi, lo, slot, own, z_send, z_recv, y_send, y_recv):
    f = lax.axis_index("fsdp")
    z, y = f // lo, f % lo

    def copy(i, origin, target, send, recv, first=False):
        ref = slot(i, origin)
        return pltpu.make_async_remote_copy(
            src_ref=own(i) if first else ref,
            dst_ref=ref,
            send_sem=send,
            recv_sem=recv,
            device_id={"fsdp": target},
            device_id_type=MESH,
        )

    def right(i, t):
        return copy(i, (z - t) * lo + y, (z + 1) * lo + y, z_send.at[i, 0, t], z_recv.at[i, 0, t], t == 0)

    def left(i, t):
        return copy(i, (z + t) * lo + y, (z - 1) * lo + y, z_send.at[i, 1, t], z_recv.at[i, 1, t], t == 0)

    def across(i, d):
        return copy(
            i, (z + d) * lo + y, z * lo + 1 - y, y_send.at[i, d + hi - 1], y_recv.at[i, d + hi - 1], d == 0
        )

    def start(i):
        pl.when(z + 1 < hi)(lambda: right(i, 0).start())
        pl.when(z >= 1)(lambda: left(i, 0).start())
        across(i, 0).start()

    def step(i, t):
        @pl.when(z - 1 - t >= 0)
        def _():
            copy(i, (z - 1 - t) * lo + y, f, z_send.at[i, 0, t], z_recv.at[i, 0, t]).wait_recv()
            if t + 1 < hi - 1:
                pl.when(z + 1 < hi)(lambda: right(i, t + 1).start())
            across(i, -1 - t).start()

        @pl.when(z + 1 + t < hi)
        def _():
            copy(i, (z + 1 + t) * lo + y, f, z_send.at[i, 1, t], z_recv.at[i, 1, t]).wait_recv()
            if t + 1 < hi - 1:
                pl.when(z >= 1)(lambda: left(i, t + 1).start())
            across(i, 1 + t).start()

    def arrive(i):
        for d in range(1 - hi, hi):

            @pl.when((z + d >= 0) & (z + d < hi))
            def _():
                copy(
                    i, (z + d) * lo + 1 - y, f, y_send.at[i, d + hi - 1], y_recv.at[i, d + hi - 1]
                ).wait_recv()

    def drain(i):
        for d in range(1 - hi, hi):

            @pl.when((z + d >= 0) & (z + d < hi))
            def _():
                across(i, d).wait_send()

        for t in range(hi - 1):

            @pl.when((z + 1 < hi) & (z - t >= 0))
            def _():
                right(i, t).wait_send()

            @pl.when((z >= 1) & (z + t < hi))
            def _():
                left(i, t).wait_send()

    return start, step, arrive, drain


def line_sems(count, hi):
    dma = pltpu.SemaphoreType.DMA
    return [dma((count, 2, hi)), dma((count, 2, hi)), dma((count, 2 * hi)), dma((count, 2 * hi))]


def greet(seq_targets, hi, lo):
    me = lax.axis_index("seq")
    f = lax.axis_index("fsdp")
    z, y = f // lo, f % lo
    barrier = pltpu.get_barrier_semaphore()
    for k in seq_targets:
        pl.semaphore_signal(barrier, inc=1, device_id={"seq": me ^ k}, device_id_type=MESH)
    near = (lax.rem(z + 1, hi) * lo + y, lax.rem(z + hi - 1, hi) * lo + y, z * lo + 1 - y)
    for target in near:
        pl.semaphore_signal(barrier, inc=1, device_id={"fsdp": target}, device_id_type=MESH)
    pl.semaphore_wait(barrier, len(seq_targets) + len(near))


def attend_kernel(
    heads,
    seq,
    hi,
    lo,
    length_ref,
    qkv_ref,
    init_ref,
    query_ref,
    forget_ref,
    vector_ref,
    own_out_ref,
    own_down_ref,
    att_ref,
    others_ref,
    outs_ref,
    downs_ref,
    final_ref,
    mem_ref,
    upd_ref,
    lse_ref,
    slse_ref,
    memory_ref,
    bias_ref,
    own_sem,
    att_send,
    att_recv,
    out_send,
    out_recv,
    z_send,
    z_recv,
    y_send,
    y_recv,
):
    me = lax.axis_index("seq")
    f = lax.axis_index("fsdp")
    length = length_ref[0]
    width = heads * DH
    scale2 = SCALE * LOG2E
    blocks = seq
    bits = [1 << i for i in range(seq.bit_length() - 1)]
    greet(bits, hi, lo)

    own_copies = [
        pltpu.make_async_copy(own_down_ref, downs_ref.at[f], own_sem.at[0]),
        pltpu.make_async_copy(own_out_ref, outs_ref.at[:, me], own_sem.at[1]),
    ]
    for c in own_copies:
        c.start()

    def lowest(k):
        return k & -k

    def out_copy(k):
        return pltpu.make_async_remote_copy(
            src_ref=outs_ref.at[:, me ^ k ^ lowest(k)] if k ^ lowest(k) else own_out_ref,
            dst_ref=outs_ref.at[:, me ^ k ^ lowest(k)],
            send_sem=out_send.at[k],
            recv_sem=out_recv.at[k],
            device_id={"seq": me ^ lowest(k)},
            device_id_type=MESH,
        )

    def out_arrival(k):
        return pltpu.make_async_remote_copy(
            src_ref=outs_ref.at[:, me ^ k],
            dst_ref=outs_ref.at[:, me ^ k],
            send_sem=out_send.at[k],
            recv_sem=out_recv.at[k],
            device_id={"seq": me},
            device_id_type=MESH,
        )

    def att_copy(k, b):
        bit = lowest(k)
        came = k ^ bit
        here = pl.ds(pl.multiple_of((b ^ me) * BLOCK, BLOCK), BLOCK)
        there = pl.ds(pl.multiple_of((b ^ me ^ bit) * BLOCK, BLOCK), BLOCK)
        src = others_ref.at[came, here] if came else att_ref.at[here]
        return pltpu.make_async_remote_copy(
            src_ref=src,
            dst_ref=others_ref.at[k, there],
            send_sem=att_send.at[k, b],
            recv_sem=att_recv.at[k, b],
            device_id={"seq": me ^ bit},
            device_id_type=MESH,
        )

    def att_arrival(k, b):
        here = pl.ds(pl.multiple_of((b ^ me) * BLOCK, BLOCK), BLOCK)
        return pltpu.make_async_remote_copy(
            src_ref=others_ref.at[k, here],
            dst_ref=others_ref.at[k, here],
            send_sem=att_send.at[k, b],
            recv_sem=att_recv.at[k, b],
            device_id={"seq": me},
            device_id_type=MESH,
        )

    passing = sorted([k for k in range(2, seq, 2)], key=lambda k: (bin(k).count("1"), -k))

    def onward(k, send):
        for bit in reversed(bits):
            if bit < lowest(k):
                send(k | bit)

    start, step, arrive, drain = line_gather(
        hi, lo, lambda i, origin: downs_ref.at[origin], lambda i: own_down_ref, z_send, z_recv, y_send, y_recv
    )

    start(0)
    for bit in reversed(bits):
        out_copy(bit).start()
    memory_ref[...] = init_ref[...].astype(f32)
    for head in range(heads):
        bias_ref[head] = tile_bias(vector_ref, head)

    @pl.loop(0, blocks)
    def _(block):
        cur_at = pl.multiple_of((block ^ me) * BLOCK, BLOCK)
        prev_at = pl.multiple_of((jnp.maximum(block - 1, 0) ^ me) * BLOCK, BLOCK)
        cur_ref = qkv_ref.at[pl.ds(cur_at, BLOCK)]
        prev_ref = qkv_ref.at[pl.ds(prev_at, BLOCK)]
        for t in range(min(hi - 1, blocks - 1)):
            pl.when(block == t + 1)(lambda t=t: step(0, t))

        live_block = block * BLOCK < length
        for head in range(heads):
            own = slice(head * DH, (head + 1) * DH)
            memory = memory_ref[:, own]
            low = memory.astype(bf16)
            mem_ref[block, :, own] = memory
            refs = (prev_ref, cur_ref)
            key_cols = slice(width + head * DH, width + (head + 1) * DH)
            value_cols = slice(2 * width + head * DH, 2 * width + (head + 1) * DH)
            for tile in range(BLOCK // QTILE):
                rows = slice(tile * QTILE, (tile + 1) * QTILE)
                query = cur_ref[rows, own]
                scores, values = [], []
                for which, at, end, col in context_pieces(tile):
                    s = dot_t(query, refs[which][at:end, key_cols])
                    position = (block - 1 + which) * BLOCK + at + lax.broadcasted_iota(jnp.int32, (1, end - at), 1)
                    live = (position >= 0) & (position < length)
                    s = s * scale2 + bias_ref[head, :, col : col + end - at]
                    scores.append(jnp.where(live, s, -jnp.inf))
                    values.append(refs[which][at:end, value_cols])
                scores.append(dot_t(query, low) * scale2)
                values.append(low)
                raised, total, lse = softmax_parts(scores)
                out = functools.reduce(jnp.add, [dot(e.astype(bf16), v) for e, v in zip(raised, values)])
                att_ref[pl.ds(cur_at + tile * QTILE, QTILE), own] = (out / total).astype(bf16)
                lse_ref[head : head + 1, pl.ds(pl.multiple_of(block * BLOCK, BLOCK) + tile * QTILE, QTILE)] = to_row(lse)
            own_key = cur_ref[:, key_cols]
            own_value = cur_ref[:, value_cols]
            squeries = dot(low, query_ref[head]).astype(bf16)
            position = block * BLOCK + lax.broadcasted_iota(jnp.int32, (1, BLOCK), 1)
            for tile in range(STATE_VECTORS // QTILE):
                rows = slice(tile * QTILE, (tile + 1) * QTILE)
                squery = squeries[rows]
                scores = [
                    dot_t(squery, low) * scale2,
                    jnp.where(position < length, dot_t(squery, own_key) * scale2, -jnp.inf),
                ]
                raised, total, lse = softmax_parts(scores)
                update = dot(raised[0].astype(bf16), low) + dot(raised[1].astype(bf16), own_value)
                update = update / total
                upd_ref[block, rows, own] = update
                slse_ref[head : head + 1, pl.ds(pl.multiple_of(block * BLOCK, BLOCK) + tile * QTILE, QTILE)] = to_row(
                    lse
                )
                forget = forget_ref[:, own]
                old = memory[rows]
                memory_ref[rows, own] = jnp.where(live_block, forget * old + (1.0 - forget) * update, old)

        for bit in reversed(bits):
            att_copy(bit, block).start()

        @pl.when(block == 0)
        def _():
            for k in passing:
                out_arrival(k).wait_recv()
                onward(k, lambda target: out_copy(target).start())

        @pl.when(block >= 1)
        def _():
            for k in passing:
                att_arrival(k, block - 1).wait_recv()
                onward(k, lambda target: att_copy(target, block - 1).start())

    final_ref[...] = memory_ref[...]
    for t in range(min(hi - 1, blocks - 1), hi - 1):
        step(0, t)
    for k in passing:
        att_arrival(k, blocks - 1).wait_recv()
        onward(k, lambda target: att_copy(target, blocks - 1).start())
    arrive(0)
    for k in range(1, seq, 2):
        out_arrival(k).wait_recv()
        for b in range(blocks):
            att_arrival(k, b).wait_recv()
    for c in own_copies:
        c.wait()
    drain(0)
    for k in range(1, seq):
        out_copy(k).wait_send()
        for b in range(blocks):
            att_copy(k, b).wait_send()


def attend(qkv, init, length, state_query, forget, bias, own_out, own_down, heads, seq, fsdp):
    rows, width3 = qkv.shape
    width = heads * DH
    blocks = rows // BLOCK
    lo = 2
    hi = fsdp // lo
    dim = own_down.shape[1]
    anywhere = pl.BlockSpec(memory_space=pl.ANY)
    vmem = pl.BlockSpec(memory_space=pltpu.VMEM)
    dma = pltpu.SemaphoreType.DMA
    return pl.pallas_call(
        functools.partial(attend_kernel, heads, seq, hi, lo),
        out_shape=(
            jax.ShapeDtypeStruct((rows, width), bf16),
            jax.ShapeDtypeStruct((seq, rows, width), bf16),
            jax.ShapeDtypeStruct((fsdp, seq) + own_out.shape[1:], bf16),
            jax.ShapeDtypeStruct((fsdp,) + own_down.shape, bf16),
            jax.ShapeDtypeStruct((STATE_VECTORS, width), f32),
            jax.ShapeDtypeStruct((blocks, STATE_VECTORS, width), f32),
            jax.ShapeDtypeStruct((blocks, STATE_VECTORS, width), f32),
            jax.ShapeDtypeStruct((heads, rows), f32),
            jax.ShapeDtypeStruct((heads, blocks * STATE_VECTORS), f32),
        ),
        in_specs=[pl.BlockSpec(memory_space=pltpu.SMEM)] + [vmem] * 7,
        out_specs=(vmem, anywhere, anywhere, anywhere, vmem, vmem, vmem, vmem, vmem),
        scratch_shapes=[
            pltpu.VMEM((STATE_VECTORS, width), f32),
            pltpu.VMEM((heads, QTILE, SPAN), f32),
            dma((2,)),
            dma((seq, blocks)),
            dma((seq, blocks)),
            dma((seq,)),
            dma((seq,)),
        ]
        + line_sems(1, hi),
        compiler_params=pltpu.CompilerParams(collective_id=3, has_side_effects=True, vmem_limit_bytes=40 << 20),
        cost_estimate=pl.CostEstimate(
            flops=blocks * heads * 512 * 2400 * 128 * 4, bytes_accessed=16 << 20, transcendentals=10 << 20
        ),
        name="attend",
    )(length, qkv, init, state_query, forget, bias, own_out, own_down)


def line_reduce(hi, lo, block, total, from_y, from_z, z_send, z_recv, y_send, y_recv):
    f = lax.axis_index("fsdp")
    z, y = f // lo, f % lo

    def remote(src, dst, send, recv, target):
        return pltpu.make_async_remote_copy(
            src_ref=src, dst_ref=dst, send_sem=send, recv_sem=recv, device_id={"fsdp": target}, device_id_type=MESH
        )

    def across(i, d):
        return remote(
            block(i, d * lo + 1 - y), from_y[i].at[d], y_send.at[i, d], y_recv.at[i, d], z * lo + 1 - y
        )

    def start(i):
        for d in range(hi):
            across(i, d).start()

    def combine(i):
        for d in range(hi):
            across(i, d).wait_recv()
            own = block(i, d * lo + y)
            total[i][d] = (own[...].astype(f32) + from_y[i][d].astype(f32)).astype(bf16)

    def hop(i, side, t, at, target):
        return remote(
            total[i].at[jnp.clip(at, 0, hi - 1)],
            from_z[i].at[side, t],
            z_send.at[i, side, t],
            z_recv.at[i, side, t],
            target,
        )

    def sending(t):
        d = t - (hi - 1 - z)
        m = hi - 1 - (t - z)
        return ((0, d, (d >= 0) & (d < z), z - 1), (1, m, (m > z) & (m < hi), z + 1))

    def zsend(i, t):
        for side, at, cond, target in sending(t):
            pl.when(cond)(lambda: hop(i, side, t, at, target * lo + y).start())

    def zrecv(i, t):
        d = t - (hi - 2 - z)
        m = hi - 1 - (t - (z - 1))
        for side, at, cond in ((0, d, (z + 1 < hi) & (d >= 0)), (1, m, (z > 0) & (m < hi))):

            @pl.when(cond)
            def _():
                hop(i, side, t, at, f).wait_recv()
                slot = jnp.clip(at, 0, hi - 1)
                total[i][slot] = (total[i][slot].astype(f32) + from_z[i][side, t].astype(f32)).astype(bf16)

    def drain_y(i):
        for d in range(hi):
            across(i, d).wait_send()

    def drain_z(i):
        for t in range(hi - 1):
            for side, at, cond, target in sending(t):
                pl.when(cond)(lambda: hop(i, side, t, at, f).wait_send())

    return start, combine, zsend, zrecv, drain_y, drain_z


def seq_levels(seq):
    bits = [1 << i for i in range(seq.bit_length() - 1)]
    slots = {}
    for bit in bits:
        for j in range(0, seq, 2 * bit):
            slots[bit, j] = len(slots)
    return bits, slots


def diagonal_sums(tile):
    rows, lanes = tile.shape
    wide = jnp.concatenate([tile, jnp.zeros((rows, lanes), f32)], axis=1)
    row = lax.broadcasted_iota(jnp.int32, wide.shape, 0)
    bit = 1
    while bit < rows:
        wide = jnp.where((row & bit) != 0, pltpu.roll(wide, 2 * lanes - bit, 1), wide)
        bit *= 2
    return jnp.sum(wide, axis=0, keepdims=True)


def attend_back_kernel(heads, seq, hi, lo, inside, length_ref, *refs):
    refs = list(refs)

    def take(count):
        taken = refs[:count]
        del refs[:count]
        return taken

    qkv_ref, db_ref, wout_ref, att_ref, mem_ref, upd_ref, lse_ref, slse_ref = take(8)
    sgrad_ref, query_ref, forget_ref, vector_ref, up_ref, down_ref, mo_ref, mid_ref = take(8)
    ow_in = None if inside else take(1)[0]
    dqkv_ref, small_ref, upart_ref, dtotal_ref, opart_ref, output_ref = take(6)
    dmem_ref, dnext_ref, dctx_ref, bias_ref, near_ref, far_ref, dout_ref, ow_buf = take(8)
    moved, to, tu, yo, yu, yd, zo, zu, xu, mo_low, mo_in = take(11)
    z_send, z_recv, y_send, y_recv, m_send, m_recv, e_send, e_recv, x_send, x_recv = take(10)
    ow_ref = ow_buf if inside else ow_in

    me = lax.axis_index("seq")
    f = lax.axis_index("fsdp")
    z, y = f // lo, f % lo
    blocks = seq
    length = length_ref[0]
    width = heads * DH
    scale2 = SCALE * LOG2E
    tok_rows = mid_ref.shape[0]
    share = dtotal_ref.shape[1]
    bits, slots = seq_levels(seq)
    greet(list(range(1, seq)), hi, lo)

    def mo_copy(bit, j):
        slot = slots[bit, j]
        return pltpu.make_async_remote_copy(
            src_ref=mo_ref.at[j ^ bit] if bit == 1 else mo_low.at[(j ^ bit) // 2],
            dst_ref=mo_in.at[slot],
            send_sem=m_send.at[slot],
            recv_sem=m_recv.at[slot],
            device_id={"seq": me ^ bit},
            device_id_type=MESH,
        )

    def move_copy(k):
        return pltpu.make_async_remote_copy(
            src_ref=down_ref.at[me ^ k],
            dst_ref=moved.at[me],
            send_sem=e_send.at[k],
            recv_sem=e_recv.at[k],
            device_id={"seq": me ^ k},
            device_id_type=MESH,
        )

    def move_arrival(k):
        return pltpu.make_async_remote_copy(
            src_ref=down_ref.at[me],
            dst_ref=moved.at[me ^ k],
            send_sem=e_send.at[k],
            recv_sem=e_recv.at[k],
            device_id={"seq": me},
            device_id_type=MESH,
        )

    def block_of(i, target):
        if i == 0:
            return ow_ref.at[target]
        if i == 1:
            return up_ref.at[:, target]
        return moved.at[target % seq, pl.ds(pl.multiple_of((target // seq) * share, share), share)]

    start, combine, zsend, zrecv, drain_y, drain_z = line_reduce(
        hi, lo, block_of, (to, tu, dtotal_ref), (yo, yu, yd), (zo, zu), z_send, z_recv, y_send, y_recv
    )

    def exchange(k, sending):
        return pltpu.make_async_remote_copy(
            src_ref=tu.at[z, me ^ k] if sending else tu.at[z, me],
            dst_ref=xu.at[me] if sending else xu.at[me ^ k],
            send_sem=x_send.at[k],
            recv_sem=x_recv.at[k],
            device_id={"seq": me ^ k if sending else me},
            device_id_type=MESH,
        )

    for j in range(seq - 1, 0, -2):
        mo_copy(1, j ^ 1).start()
    for k in reversed(range(1, seq)):
        move_copy(k).start()
    moved[me] = down_ref[me]
    if inside:
        full = t_dot(att_ref[...], db_ref[...]).astype(bf16)
        ow_buf[...] = full.reshape(ow_buf.shape)
    start(0)
    start(1)

    dmem_ref[...] = sgrad_ref[...].astype(f32)
    dnext_ref[...] = jnp.zeros_like(dnext_ref)
    small_ref[...] = jnp.zeros_like(small_ref)
    near_ref[...] = jnp.zeros_like(near_ref)
    far_ref[...] = jnp.zeros_like(far_ref)
    for head in range(heads):
        bias_ref[head] = tile_bias(vector_ref, head).T

    def mo_step(j):
        for bit in bits:
            if j & bit:
                mo_copy(bit, j ^ bit).start()
                break
            mo_copy(bit, j).wait_recv()
            own = mo_ref[j] if bit == 1 else mo_low[j // 2]
            mo_low[j // 2] = (own.astype(f32) + mo_in[slots[bit, j]].astype(f32)).astype(bf16)

    def down_ready():
        for k in range(1, seq):
            move_arrival(k).wait_recv()
        start(2)

    def up_done():
        for k in range(1, seq):
            exchange(k, True).start()

    jobs = [lambda j=j: mo_step(j) for j in range(seq - 2, 0, -2)]
    jobs.append(lambda: (combine(0), zsend(0, 0)))
    for t in range(hi - 2):
        jobs.append(lambda t=t: (zrecv(0, t), zsend(0, t + 1)))
    jobs.append(lambda: (zrecv(0, hi - 2), down_ready()))
    jobs.append(lambda: (combine(1), zsend(1, 0)))
    for t in range(hi - 2):
        jobs.append(lambda t=t: (zrecv(1, t), zsend(1, t + 1)))
    jobs.append(lambda: (zrecv(1, hi - 2), up_done()))
    points = blocks * heads - 1

    dq_row = heads * DH

    @pl.loop(0, blocks)
    def _(step):
        block = blocks - 1 - step
        cur_at = pl.multiple_of((block ^ me) * BLOCK, BLOCK)
        prev_at = pl.multiple_of((jnp.maximum(block - 1, 0) ^ me) * BLOCK, BLOCK)
        base = pl.multiple_of(block * BLOCK, BLOCK)
        cur_ref = qkv_ref.at[pl.ds(cur_at, BLOCK)]
        prev_ref = qkv_ref.at[pl.ds(prev_at, BLOCK)]
        live_block = block * BLOCK < length
        refs = (prev_ref, cur_ref)
        dout_ref[...] = dot_t(db_ref[pl.ds(cur_at, BLOCK)], wout_ref[...]).astype(bf16)
        for head in range(heads):
            for n, job in enumerate(jobs[:points]):
                if (n + 1) % heads == head:
                    pl.when(step == (n + 1) // heads)(lambda job=job: (job(), None)[1])
            own = slice(head * DH, (head + 1) * DH)
            key_cols = slice(width + head * DH, width + (head + 1) * DH)
            value_cols = slice(2 * width + head * DH, 2 * width + (head + 1) * DH)
            memory = mem_ref[block, :, own]
            update = upd_ref[block, :, own]
            low = memory.astype(bf16)
            forget = forget_ref[:, own]
            dmem = dmem_ref[:, own]
            dupd = jnp.where(live_block, (1.0 - forget) * dmem, 0.0).astype(bf16)
            gone = jnp.where(live_block, dmem * (memory - update), 0.0)
            small_ref[dq_row + head : dq_row + head + 1, :] += jnp.sum(gone, axis=0, keepdims=True)
            dmem_new = jnp.where(live_block, forget * dmem, dmem)
            own_key = cur_ref[:, key_cols]
            own_value = cur_ref[:, value_cols]
            squeries = dot(low, query_ref[head]).astype(bf16)
            sdelta = jnp.sum((dupd.astype(f32) * update).T, axis=0, keepdims=True)
            slse = slse_ref[head : head + 1, pl.ds(base, BLOCK)]
            dsquery = jnp.zeros((STATE_VECTORS, DH), f32)
            dkey = []
            dvalue = []
            for part in range(2 * STATE_VECTORS // QTILE):
                own_part = part >= STATE_VECTORS // QTILE
                at = (part % (STATE_VECTORS // QTILE)) * QTILE
                keys = (own_key if own_part else low)[at : at + QTILE]
                values = (own_value if own_part else low)[at : at + QTILE]
                s = dot_t(keys, squeries) * scale2 - slse
                if own_part:
                    position = block * BLOCK + at + lax.broadcasted_iota(jnp.int32, (QTILE, 1), 0)
                    s = jnp.where(position < length, s, -jnp.inf)
                p = jnp.exp2(s)
                dp = dot_t(values, dupd)
                ds = (p * (dp - sdelta)).astype(bf16)
                dvalue.append(dot(p.astype(bf16), dupd))
                dkey.append(dot(ds, squeries))
                dsquery += t_dot(ds, keys)
            half = STATE_VECTORS // QTILE
            dlow = [dvalue[i] + dkey[i] * SCALE for i in range(half)]
            dctx_ref[0, 0:BLOCK] = jnp.zeros((BLOCK, DH), f32)
            dctx_ref[1, 0:BLOCK] = jnp.zeros((BLOCK, DH), f32)
            for i in range(half):
                rows = slice(BLOCK + i * QTILE, BLOCK + (i + 1) * QTILE)
                old = slice(i * QTILE, (i + 1) * QTILE)
                dctx_ref[0, rows] = dkey[half + i] * SCALE + dnext_ref[0, old, own]
                dctx_ref[1, rows] = dvalue[half + i] + dnext_ref[1, old, own]
            dsq = (dsquery * SCALE).astype(bf16)
            small_ref[head * DH : (head + 1) * DH, :] += t_dot(low, dsq)
            dmem_ref[:, own] = dmem_new + dot_t(dsq, query_ref[head])
            for tile in range(BLOCK // QTILE):
                rows = slice(tile * QTILE, (tile + 1) * QTILE)
                here = pl.ds(cur_at + tile * QTILE, QTILE)
                query = cur_ref[rows, own]
                dout = dout_ref[rows, own]
                lse = lse_ref[head : head + 1, pl.ds(base + tile * QTILE, QTILE)]
                delta = jnp.sum((dout.astype(f32) * att_ref[here, own].astype(f32)).T, axis=0, keepdims=True)
                dq = jnp.zeros((QTILE, DH), f32)
                for which, first, end, col in context_pieces(tile):
                    for at in range(first, end, QTILE):
                        keys = refs[which][at : at + QTILE, key_cols]
                        values = refs[which][at : at + QTILE, value_cols]
                        band = col + at - first
                        position = (block - 1 + which) * BLOCK + at + lax.broadcasted_iota(jnp.int32, (QTILE, 1), 0)
                        live = (position >= 0) & (position < length)
                        s = dot_t(keys, query) * scale2 + bias_ref[head, band : band + QTILE, :] - lse
                        p = jnp.exp2(jnp.where(live, s, -jnp.inf))
                        dp = dot_t(values, dout)
                        ds = (p * (dp - delta)).astype(bf16)
                        wide = ds.astype(f32)
                        edge = min(max(SPAN - NEAR - band, 0), QTILE)
                        if edge:
                            far_ref[head] += functools.reduce(jnp.add, [wide[i : i + 8] for i in range(0, edge, 8)])
                        if edge < QTILE:
                            at_near = band + edge - (SPAN - NEAR)
                            near_ref[head, at_near : at_near + QTILE - edge] += wide[edge:]
                        into = slice(which * BLOCK + at, which * BLOCK + at + QTILE)
                        dctx_ref[1, into] += dot(p.astype(bf16), dout)
                        dctx_ref[0, into] += dot(ds, query) * SCALE
                        dq += t_dot(ds, keys)
                for part in range(half):
                    keys = low[part * QTILE : (part + 1) * QTILE]
                    s = dot_t(keys, query) * scale2 - lse
                    p = jnp.exp2(s)
                    dp = dot_t(keys, dout)
                    ds = (p * (dp - delta)).astype(bf16)
                    dlow[part] += dot(p.astype(bf16), dout) + dot(ds, query) * SCALE
                    dq += t_dot(ds, keys)
                dqkv_ref[here, own] = (dq * SCALE).astype(bf16)
            for part in range(half):
                dmem_ref[part * QTILE : (part + 1) * QTILE, own] += dlow[part]
            dnext_ref[0, :, own] = dctx_ref[0, 0:BLOCK]
            dnext_ref[1, :, own] = dctx_ref[1, 0:BLOCK]
            dqkv_ref[pl.ds(cur_at, BLOCK), key_cols] = dctx_ref[0, BLOCK:].astype(bf16)
            dqkv_ref[pl.ds(cur_at, BLOCK), value_cols] = dctx_ref[1, BLOCK:].astype(bf16)

    for job in jobs[points:]:
        job()
    near_row = dq_row + heads
    far_row = near_row + heads * (2 * QTILE // DH)
    for head in range(heads):
        sums = diagonal_sums(near_ref[head])
        for i in range(2 * QTILE // DH):
            row = near_row + head * (2 * QTILE // DH) + i
            small_ref[row : row + 1, :] = sums[:, i * DH : (i + 1) * DH]
        total = jnp.sum(far_ref[head], axis=0, keepdims=True)
        for i in range(QTILE // DH):
            row = far_row + head * (QTILE // DH) + i
            small_ref[row : row + 1, :] = total[:, i * DH : (i + 1) * DH]
    for bit in bits:
        mo_copy(bit, 0).wait_recv()
    step = 128
    for r in range(0, tok_rows, step):
        at = slice(r, r + step)
        value = mid_ref[at] + mo_ref[0, at].astype(f32)
        for bit in bits:
            value = value + mo_in[slots[bit, 0], at].astype(f32)
        position = me * tok_rows + r + lax.broadcasted_iota(jnp.int32, (step, 1), 0)
        output_ref[at] = (value * jnp.where(position < length, 1.0, 0.0)).astype(bf16)
    combine(2)
    opart_ref[...] = to[z].astype(f32)
    for k in range(1, seq):
        exchange(k, False).wait_recv()
    xu[me] = tu[z, me]
    write_parts(upart_ref, xu, seq, share)
    for i in range(3):
        drain_y(i)
    for i in range(2):
        drain_z(i)
    for bit in bits:
        for j in range(0, seq, 2 * bit):
            mo_copy(bit, j).wait_send()
    for k in range(1, seq):
        move_copy(k).wait_send()
        exchange(k, True).wait_send()


def write_parts(out_ref, pieces, seq, unit):
    if len(out_ref.shape) == 3:
        out_ref[...] = pieces[...].astype(f32)
        return
    count = pieces.shape[2] // unit
    for k in range(seq):
        for c in range(count):
            at = (c * seq + k) * unit
            out_ref[:, at : at + unit] = pieces[k, :, c * unit : (c + 1) * unit].astype(f32)


def attend_back(
    qkv, db, wout, att, mem, upd, lse, slse, sgrad, length, state_query, forget, bias, up, down, mo, mid, seq, fsdp
):
    rows, width3 = qkv.shape
    width = width3 // 3
    heads = width // DH
    dim = db.shape[1]
    lo = 2
    hi = fsdp // lo
    piece = up.shape[2]
    hidden = up.shape[3]
    share = hidden // fsdp
    tok_rows = mid.shape[0]
    inside = piece % 16 == 0
    blocks = (piece, dim), (seq, piece, hidden), (share, dim)
    small_rows = heads * (DH + 1 + 3 * QTILE // DH)
    small_rows += -small_rows % 8
    vmem = pl.BlockSpec(memory_space=pltpu.VMEM)
    dma = pltpu.SemaphoreType.DMA

    def buf(*shape):
        return pltpu.VMEM(shape, bf16)

    extra = []
    if not inside:
        extra.append(t_dot(att, db).astype(bf16).reshape(fsdp, piece, dim))
    upart = (piece, hidden * seq) if share % 128 == 0 else (seq, piece, hidden)
    return pl.pallas_call(
        functools.partial(attend_back_kernel, heads, seq, hi, lo, inside),
        out_shape=(
            jax.ShapeDtypeStruct((rows, width3), bf16),
            jax.ShapeDtypeStruct((small_rows, DH), f32),
            jax.ShapeDtypeStruct(upart, f32),
            jax.ShapeDtypeStruct((hi, share, dim), bf16),
            jax.ShapeDtypeStruct((piece, dim), f32),
            jax.ShapeDtypeStruct((tok_rows, dim), bf16),
        ),
        in_specs=[pl.BlockSpec(memory_space=pltpu.SMEM)] + [vmem] * (16 + len(extra)),
        out_specs=(vmem,) * 6,
        scratch_shapes=[
            pltpu.VMEM((STATE_VECTORS, width), f32),
            pltpu.VMEM((2, BLOCK, width), f32),
            pltpu.VMEM((2, 2 * BLOCK, DH), f32),
            pltpu.VMEM((heads, SPAN, QTILE), f32),
            pltpu.VMEM((heads, NEAR, QTILE), f32),
            pltpu.VMEM((heads, 8, QTILE), f32),
            buf(BLOCK, width),
            buf(fsdp, piece, dim),
            buf(*down.shape),
            buf(hi, *blocks[0]),
            buf(hi, *blocks[1]),
            buf(hi, *blocks[0]),
            buf(hi, *blocks[1]),
            buf(hi, *blocks[2]),
            buf(2, max(hi - 1, 1), *blocks[0]),
            buf(2, max(hi - 1, 1), *blocks[1]),
            buf(*blocks[1]),
            buf(max(seq // 2, 1), tok_rows, dim),
            buf(max(seq - 1, 1), tok_rows, dim),
            dma((2, 2, hi)),
            dma((2, 2, hi)),
            dma((3, hi)),
            dma((3, hi)),
            dma((seq,)),
            dma((seq,)),
            dma((seq,)),
            dma((seq,)),
            dma((seq,)),
            dma((seq,)),
        ],
        compiler_params=pltpu.CompilerParams(collective_id=4, has_side_effects=True, vmem_limit_bytes=60 << 20),
        cost_estimate=pl.CostEstimate(
            flops=seq * heads * 512 * 2400 * 128 * 10, bytes_accessed=20 << 20, transcendentals=10 << 20
        ),
        name="attend_back",
    )(
        length, qkv, db, wout, att, mem, upd, lse, slse, sgrad, state_query, forget, bias, up, down, mo, mid, *extra
    )


def gather_kernel(
    seq,
    hi,
    lo,
    tok_ref,
    grad_ref,
    wq_ref,
    ga_ref,
    gm_ref,
    wo_ref,
    wu_ref,
    toks_ref,
    grads_ref,
    wqs_ref,
    gas_ref,
    gms_ref,
    wos_ref,
    wus_ref,
    *rest,
):
    own_bufs = rest[:7]
    own_sem, store_sem, seq_send, seq_recv, z_send, z_recv, y_send, y_recv = rest[7:]
    me = lax.axis_index("seq")
    f = lax.axis_index("fsdp")
    fsdp = hi * lo
    bits = [1 << i for i in range(seq.bit_length() - 1)]
    greet(bits, hi, lo)

    pairs = ((tok_ref, toks_ref), (grad_ref, grads_ref))

    def seq_copy(i, source, slot, bit):
        src, out = pairs[i]
        return pltpu.make_async_remote_copy(
            src_ref=out.at[source] if source else src,
            dst_ref=out.at[slot],
            send_sem=seq_send.at[i, slot],
            recv_sem=seq_recv.at[i, slot],
            device_id={"seq": me ^ bit},
            device_id_type=MESH,
        )

    sends = []

    def send(i, source, slot, bit):
        sends.append(seq_copy(i, source, slot, bit))
        sends[-1].start()

    high = [bit for bit in reversed(bits) if bit > 1]
    if high:
        send(0, 0, high[0], high[0])
    if seq > 1:
        send(0, 0, 1, 1)

    width = wqs_ref.shape[2] // 3
    share = wus_ref.shape[2] // fsdp
    every = wq_ref.shape[1] // 3
    loads = [[] for _ in own_bufs]

    def load(i, src, dst):
        loads[i].append(pltpu.make_async_copy(src, dst, own_sem.at[i, len(loads[i])]))
        loads[i][-1].start()

    wq_buf, ga_buf, gm_buf, wo_buf, wu_buf, tok_buf, grad_buf = own_bufs
    for c in range(3):
        cols = pl.ds(pl.multiple_of(c * every + me * width, width), width)
        load(0, wq_ref.at[:, cols], wq_buf.at[:, pl.ds(c * width, width)])
    load(1, ga_ref, ga_buf)
    load(2, gm_ref, gm_buf)
    load(3, wo_ref.at[me], wo_buf)
    if wu_ref.shape[1] == wus_ref.shape[2]:
        load(4, wu_ref, wu_buf)
    else:
        for c in range(fsdp):
            cols = pl.ds(pl.multiple_of((c * seq + me) * share, share), share)
            load(4, wu_ref.at[:, cols], wu_buf.at[:, pl.ds(c * share, share)])
    load(5, tok_ref, tok_buf)
    load(6, grad_ref, grad_buf)
    outs = (wqs_ref, gas_ref, gms_ref, wos_ref, wus_ref)
    start, step, arrive, drain = line_gather(
        hi, lo, lambda i, origin: outs[i].at[origin], lambda i: own_bufs[i], z_send, z_recv, y_send, y_recv
    )
    own_stores = []
    for i in range(len(own_bufs)):
        for c in loads[i]:
            c.wait()
        if i < len(outs):
            start(i)
        target = outs[i].at[f] if i < len(outs) else pairs[i - len(outs)][1].at[0]
        own_stores.append(pltpu.make_async_copy(own_bufs[i], target, store_sem.at[i]))
        own_stores[-1].start()
    if high:
        send(1, 0, high[0], high[0])
    if seq > 1:
        send(1, 0, 1, 1)
    for t in range(hi - 1):
        for i in range(len(outs)):
            step(i, t)
    for i in range(len(pairs)):
        have = [0]
        for n, bit in enumerate(high):
            if n:
                for j in have:
                    send(i, j, j ^ bit, bit)
            for j in have:
                seq_copy(i, 0, j ^ bit, bit).wait_recv()
                send(i, j ^ bit, j ^ bit ^ 1, 1)
            have += [j ^ bit for j in have]
        if seq > 1:
            for j in have:
                seq_copy(i, 0, j ^ 1, 1).wait_recv()
    for i in range(len(outs)):
        arrive(i)
    for i in range(len(outs)):
        drain(i)
    for c in sends:
        c.wait_send()
    for c in own_stores:
        c.wait()


def gather_start(tokens, grads, w_qkv, gain_a, gain_m, w_out, w_up, seq, fsdp):
    lo = 2
    hi = fsdp // lo
    dim_rows, hidden = w_up.shape
    share = hidden // (seq * fsdp)
    if share % 128:
        w_up = lax.dynamic_slice_in_dim(w_up.reshape(dim_rows, fsdp, seq, share), lax.axis_index("seq"), 1, axis=2)
        w_up = w_up.reshape(dim_rows, fsdp * share)
    anywhere = pl.BlockSpec(memory_space=pl.ANY)
    dma = pltpu.SemaphoreType.DMA
    shapes = (
        (seq,) + tokens.shape,
        (seq,) + grads.shape,
        (fsdp, dim_rows, w_qkv.shape[1] // seq),
        (fsdp,) + gain_a.shape,
        (fsdp,) + gain_m.shape,
        (fsdp,) + w_out.shape[1:],
        (fsdp, dim_rows, hidden // seq),
    )
    return pl.pallas_call(
        functools.partial(gather_kernel, seq, hi, lo),
        out_shape=tuple(jax.ShapeDtypeStruct(shape, bf16) for shape in shapes),
        in_specs=[anywhere] * 7,
        out_specs=(anywhere,) * 7,
        scratch_shapes=[pltpu.VMEM(shape[1:], bf16) for shape in shapes[2:] + shapes[:2]]
        + [dma((7, max(fsdp, 3))), dma((7,)), dma((2, seq)), dma((2, seq))]
        + line_sems(5, hi),
        compiler_params=pltpu.CompilerParams(collective_id=0, has_side_effects=True),
        name="gather_start",
    )(tokens, grads, w_qkv, gain_a, gain_m, w_out, w_up)


def finish_kernel(seq, hi, lo, inside, *refs):
    refs = list(refs)

    def take(count):
        taken = refs[:count]
        del refs[:count]
        return taken

    dqkv_ref, wqkv_ref, normed_ref, down_ref, small_ref, mlp_gain_ref, tok_ref, dmid_ref, gain_ref = take(9)
    gq_in = None if inside else take(1)[0]
    tg_ref, rq_ref, rd_ref, ssum_ref, gsum_ref = take(5)
    low, into, acc, gq_buf, tq, td, yq, zq, zd, xq, sy, sz, gains, gy, gz, gs = take(16)
    dn_send, dn_recv, z_send, z_recv, y_send, y_recv, x_send, x_recv, s_send, s_recv, g_send, g_recv = take(12)
    gq_ref = gq_buf if inside else gq_in

    me = lax.axis_index("seq")
    f = lax.axis_index("fsdp")
    z, y = f // lo, f % lo
    peer = z * lo + 1 - y
    rows, dim = tok_ref.shape
    width = xq.shape[2] // 3
    bits, slots = seq_levels(seq)

    barrier = pltpu.get_barrier_semaphore()
    for k in range(1, seq):
        pl.semaphore_signal(barrier, inc=1, device_id={"seq": me ^ k}, device_id_type=MESH)
    for k in range(1, hi):
        pl.semaphore_signal(barrier, inc=1, device_id={"fsdp": lax.rem(z + k, hi) * lo + y}, device_id_type=MESH)
    pl.semaphore_signal(barrier, inc=1, device_id={"fsdp": peer}, device_id_type=MESH)
    pl.semaphore_wait(barrier, seq + hi - 1)

    def remote(src, dst, send, recv, axis, target):
        return pltpu.make_async_remote_copy(
            src_ref=src, dst_ref=dst, send_sem=send, recv_sem=recv, device_id={axis: target}, device_id_type=MESH
        )

    def dn_copy(bit, j):
        slot = slots[bit, j]
        return remote(low.at[j ^ bit], into.at[slot], dn_send.at[slot], dn_recv.at[slot], "seq", me ^ bit)

    start, combine, zsend, zrecv, drain_y, drain_z = line_reduce(
        hi,
        lo,
        lambda i, target: gq_ref.at[:, target],
        (tq, td),
        (yq,),
        (zq, zd),
        z_send,
        z_recv,
        y_send,
        y_recv,
    )

    def exchange(k, sending):
        return remote(
            tq.at[z, me ^ k] if sending else tq.at[z, me],
            xq.at[me] if sending else xq.at[me ^ k],
            x_send.at[k],
            x_recv.at[k],
            "seq",
            me ^ k if sending else me,
        )

    small_y = remote(small_ref, sy, s_send.at[0], s_recv.at[0], "fsdp", peer)
    small_y.start()
    td[...] = down_ref[...]
    zsend(1, 0)
    if not inside:
        start(0)

    def dn_part(j):
        part = dot_t(dqkv_ref[j * rows : (j + 1) * rows], wqkv_ref[...])
        if j % 2:
            low[j] = part.astype(bf16)
            dn_copy(1, j ^ 1).start()
        else:
            acc[...] = part

    def dn_sum(j):
        for bit in bits:
            if j & bit:
                low[j] = acc[...].astype(bf16)
                dn_copy(bit, j ^ bit).start()
                break
            dn_copy(bit, j).wait_recv()
            acc[...] += into[slots[bit, j]].astype(f32)

    for j in reversed(range(2, seq)):
        dn_part(j)
        if j % 2 == 0:
            dn_sum(j)
    if inside:
        for k in range(seq):
            cols = slice(k * (dim // seq), (k + 1) * (dim // seq))
            part = t_dot(normed_ref[:, cols], dqkv_ref[...]).astype(bf16)
            gq_buf[k] = part.reshape(gq_buf.shape[1:])
        start(0)
    small_y.wait_recv()
    sz[z] = small_ref[...] + sy[...]
    small_z = []
    for k in range(1, hi):
        small_z.append(
            remote(sz.at[z], sz.at[z], s_send.at[k], s_recv.at[k], "fsdp", lax.rem(z + k, hi) * lo + y)
        )
        small_z[-1].start()
    for t in range(hi - 1):
        zrecv(1, t)
        if t + 1 < hi - 1:
            zsend(1, t + 1)
        if t == 0:
            for j in reversed(range(min(2, seq))):
                dn_part(j)
    rd_ref[...] = td[z].astype(f32)

    for bit in bits:
        dn_copy(bit, 0).wait_recv()
    gain = gain_ref[...]
    part = jnp.zeros((8, dim), f32)
    step = 128
    for r in range(0, rows, step):
        at = slice(r, r + step)
        dn = acc[at]
        for bit in bits:
            dn = dn + into[slots[bit, 0], at].astype(f32)
        x = tok_ref[at].astype(f32)
        rho = lax.rsqrt(jnp.mean(x * x, axis=-1, keepdims=True) + EPSILON)
        scaled = gain * dn
        mean = jnp.mean(x * scaled, axis=-1, keepdims=True)
        tg_ref[at] = dmid_ref[at] + rho * scaled - x * (rho * rho * rho * mean)
        prod = dn * x * rho
        part += functools.reduce(jnp.add, [prod[n : n + 8] for n in range(0, step, 8)])
    gains[0:8] = mlp_gain_ref[...]
    gains[8:16] = part
    gain_y = remote(gains, gy, g_send.at[0], g_recv.at[0], "fsdp", peer)
    gain_y.start()
    combine(0)
    zsend(0, 0)
    gain_y.wait_recv()
    gz[z] = gains[...] + gy[...]
    gain_z = []
    for k in range(1, hi):
        gain_z.append(
            remote(gz.at[z], gz.at[z], g_send.at[k], g_recv.at[k], "fsdp", lax.rem(z + k, hi) * lo + y)
        )
        gain_z[-1].start()
    for t in range(hi - 1):
        zrecv(0, t)
        if t + 1 < hi - 1:
            zsend(0, t + 1)
    for k in range(1, seq):
        exchange(k, True).start()
    for k in range(1, hi):
        source = lax.rem(z + hi - k, hi)
        remote(gz.at[source], gz.at[source], g_send.at[k], g_recv.at[k], "fsdp", f).wait_recv()
        remote(sz.at[source], sz.at[source], s_send.at[k], s_recv.at[k], "fsdp", f).wait_recv()
    gs[me] = functools.reduce(jnp.add, [gz[d] for d in range(hi)])
    gain_x = []
    for k in range(1, seq):
        gain_x.append(remote(gs.at[me], gs.at[me], g_send.at[hi + k], g_recv.at[hi + k], "seq", me ^ k))
        gain_x[-1].start()
    ssum_ref[...] = functools.reduce(jnp.add, [sz[d] for d in range(hi)])
    xq[me] = tq[z, me]
    for k in range(1, seq):
        exchange(k, False).wait_recv()
    write_parts(rq_ref, xq, seq, width)
    for k in range(1, seq):
        remote(gs.at[me ^ k], gs.at[me ^ k], g_send.at[hi + k], g_recv.at[hi + k], "seq", me).wait_recv()
    gsum_ref[...] = functools.reduce(jnp.add, [gs[k] for k in range(seq)])

    for bit in bits:
        for j in range(0, seq, 2 * bit):
            dn_copy(bit, j).wait_send()
    drain_y(0)
    for i in range(2):
        drain_z(i)
    for k in range(1, seq):
        exchange(k, True).wait_send()
    for c in [small_y, gain_y] + small_z + gain_z + gain_x:
        c.wait_send()


def finish(dqkv, wqkv, normed, down, small, mlp_gain, tok, dmid, gain, seq, fsdp):
    lo = 2
    hi = fsdp // lo
    rows, dim = tok.shape
    width3 = dqkv.shape[1]
    piece = dim // (seq * fsdp)
    inside = piece % 16 == 0
    vmem = pl.BlockSpec(memory_space=pltpu.VMEM)
    dma = pltpu.SemaphoreType.DMA

    def buf(*shape):
        return pltpu.VMEM(shape, bf16)

    extra = []
    if not inside:
        extra.append(t_dot(normed, dqkv).astype(bf16).reshape(seq, fsdp, piece, width3))
    scratch = [
        buf(seq, rows, dim),
        buf(max(seq - 1, 1), rows, dim),
        pltpu.VMEM((rows, dim), f32),
        buf(seq, fsdp, piece, width3) if inside else buf(16, 128),
        buf(hi, seq, piece, width3),
        buf(*down.shape),
        buf(hi, seq, piece, width3),
        buf(2, max(hi - 1, 1), seq, piece, width3),
        buf(2, max(hi - 1, 1), *down.shape[1:]),
        buf(seq, piece, width3),
        pltpu.VMEM(small.shape, f32),
        pltpu.VMEM((hi,) + small.shape, f32),
        pltpu.VMEM((16, dim), f32),
        pltpu.VMEM((16, dim), f32),
        pltpu.VMEM((hi, 16, dim), f32),
        pltpu.VMEM((seq, 16, dim), f32),
        dma((seq,)),
        dma((seq,)),
        dma((2, 2, hi)),
        dma((2, 2, hi)),
        dma((1, hi)),
        dma((1, hi)),
        dma((seq,)),
        dma((seq,)),
        dma((hi,)),
        dma((hi,)),
        dma((hi + seq,)),
        dma((hi + seq,)),
    ]
    return pl.pallas_call(
        functools.partial(finish_kernel, seq, hi, lo, inside),
        out_shape=(
            jax.ShapeDtypeStruct((rows, dim), f32),
            jax.ShapeDtypeStruct((piece, seq * width3), f32),
            jax.ShapeDtypeStruct(down.shape[1:], f32),
            jax.ShapeDtypeStruct(small.shape, f32),
            jax.ShapeDtypeStruct((16, dim), f32),
        ),
        in_specs=[vmem] * (9 + len(extra)),
        out_specs=(vmem,) * 5,
        scratch_shapes=scratch,
        compiler_params=pltpu.CompilerParams(
            collective_id=1, has_side_effects=True, vmem_limit_bytes=60 << 20
        ),
        name="finish",
    )(dqkv, wqkv, normed, down, small, mlp_gain, tok, dmid, gain, *extra)


GELU_P = 0.24
GELU_C = (
    0.08951261885080208,
    0.15562094398234086,
    -0.15437154502074169,
    0.6261054138112487,
    -0.6465313024138201,
    0.5547927291245551,
    -0.125128858665134,
)


def gelu_parts(x):
    size = jnp.abs(x)
    t = 1.0 / (1.0 + GELU_P * size)
    poly = GELU_C[-1] * t
    for c in GELU_C[-2::-1]:
        poly = (poly + c) * t
    bell = jnp.exp2(x * x * (-0.5 * LOG2E))
    tail = poly * bell
    cdf = jnp.where(x < 0.0, tail, 1.0 - tail)
    return x * cdf, cdf + x * bell * (1.0 / math.sqrt(2.0 * math.pi))


def mlp_kernel(seq, sub, length_ref, *refs):
    refs = list(refs)

    def take(count):
        taken = refs[:count]
        del refs[:count]
        return taken

    own_ref, others_ref, tok_ref, grads_ref = take(4)
    att_refs = [own_ref] + [others_ref.at[k] for k in range(1, seq)]
    grad_refs = [grads_ref.at[j] for j in range(seq)]
    wo_ref, wu_ref, wd_ref, gain_ref = take(4)
    mid_ref, dmid_ref, gsum_ref, db_ref, mo_ref, ug_ref, dg_ref = take(7)
    att_buf, tok_buf, gm, nm, hid, dpre, low, into, acc = take(9)
    dbv = low.at[0]
    depth = att_buf.shape[0]
    load_sem, gm_sem, dn_send, dn_recv, db_send, db_recv, mo_sem, own_sem = take(8)

    me = lax.axis_index("seq")
    length = length_ref[0]
    dim = wo_ref.shape[0]
    width = dim // seq
    rows = tok_ref.shape[1]
    share = wu_ref.shape[1]
    bits = [1 << i for i in range(seq.bit_length() - 1)]

    barrier = pltpu.get_barrier_semaphore()
    for bit in bits:
        pl.semaphore_signal(barrier, inc=1, device_id={"seq": me ^ bit}, device_id_type=MESH)
    pl.semaphore_wait(barrier, len(bits))

    order = list(reversed(range(seq)))
    gm_loads = {j: pltpu.make_async_copy(grad_refs[j], gm.at[pl.ds(j * rows, rows)], gm_sem.at[j]) for j in order}

    def chunk_loads(n):
        j, slot = order[n], n % depth
        copies = [
            pltpu.make_async_copy(
                att_refs[k].at[pl.ds(j * rows, rows)], att_buf.at[slot, k], load_sem.at[slot, k]
            )
            for k in range(seq)
        ]
        copies.append(pltpu.make_async_copy(tok_ref.at[j], tok_buf.at[slot], load_sem.at[slot, seq]))
        return copies

    for c in chunk_loads(0):
        c.start()
    for j in order:
        gm_loads[j].start()

    slots = {}
    for bit in bits:
        for j in range(0, seq, 2 * bit):
            slots[bit, j] = len(slots)

    def dn_copy(bit, j):
        slot = slots[bit, j]
        return pltpu.make_async_remote_copy(
            src_ref=low.at[j ^ bit],
            dst_ref=into.at[slot],
            send_sem=dn_send.at[slot],
            recv_sem=dn_recv.at[slot],
            device_id={"seq": me ^ bit},
            device_id_type=MESH,
        )

    gain = gain_ref[...]
    for n, j in enumerate(order):
        slot = n % depth
        if depth == 1 and n:
            for c in chunk_loads(n):
                c.start()
        for c in chunk_loads(n):
            c.wait()
        if depth == 2 and n + 1 < seq:
            for c in chunk_loads(n + 1):
                c.start()
        gm_loads[j].wait()
        base = (j ^ me) * rows

        @pl.loop(0, rows // sub)
        def _(s):
            at = pl.ds(pl.multiple_of(s * sub, sub), sub)
            here = pl.ds(pl.multiple_of(j * rows + s * sub, sub), sub)
            position = base + s * sub + lax.broadcasted_iota(jnp.int32, (sub, 1), 0)
            live = jnp.where(position < length, 1.0, 0.0)
            masked = (gm[here].astype(f32) * live).astype(bf16)
            gm[here] = masked
            mid = tok_buf[slot, at].astype(f32)
            for k in range(seq):
                own = pl.ds(pl.multiple_of((me ^ k) * width, width), width)
                mid = mid + dot(att_buf[slot, k, at], wo_ref[own])
            rho = lax.rsqrt(jnp.mean(mid * mid, axis=-1, keepdims=True) + EPSILON)
            normed = (mid * rho * gain).astype(bf16)
            nm[here] = normed
            if j == 0:
                mid_ref[at] = mid
            for c in range(0, share, 256):
                cols = slice(c, c + 256)
                value, slope = gelu_parts(dot(normed, wu_ref[:, cols]))
                hid[here, cols] = value.astype(bf16)
                dpre[here, cols] = (dot_t(masked, wd_ref[cols]) * slope).astype(bf16)
            part = dot_t(dpre[here], wu_ref[...])
            if j % 2:
                low[j, at] = part.astype(bf16)
            else:
                acc[at] = part

        if j % 2:
            dn_copy(1, j ^ 1).start()
        elif j:
            for bit in bits:
                if j & bit:
                    low[j] = acc[...].astype(bf16)
                    dn_copy(bit, j ^ bit).start()
                    break
                dn_copy(bit, j).wait_recv()
                acc[...] += into[slots[bit, j]].astype(f32)

    for c in range(0, dim, 256):
        ug_ref[c : c + 256] = t_dot(nm[:, c : c + 256], dpre[...]).astype(bf16)

    for bit in bits:
        dn_copy(bit, 0).wait_recv()
    step = 128
    part = jnp.zeros((8, dim), f32)
    for r in range(0, rows, step):
        at = slice(r, r + step)
        dn = acc[at]
        for bit in bits:
            dn = dn + into[slots[bit, 0], at].astype(f32)
        mid = mid_ref[at]
        rho = lax.rsqrt(jnp.mean(mid * mid, axis=-1, keepdims=True) + EPSILON)
        scaled = gain * dn
        mean = jnp.mean(mid * scaled, axis=-1, keepdims=True)
        dmid = gm[at].astype(f32) + rho * scaled - mid * (rho * rho * rho * mean)
        dmid_ref[at] = dmid
        dbv[at] = dmid.astype(bf16)
        prod = dn * mid * rho
        part += functools.reduce(jnp.add, [prod[i : i + 8] for i in range(0, step, 8)])
    gsum_ref[...] = part

    def db_copy(source, target, bit):
        return pltpu.make_async_remote_copy(
            src_ref=db_ref.at[source] if source else dbv,
            dst_ref=db_ref.at[target],
            send_sem=db_send.at[target],
            recv_sem=db_recv.at[target],
            device_id={"seq": me ^ bit},
            device_id_type=MESH,
        )

    own_copy = pltpu.make_async_copy(dbv, db_ref.at[0], own_sem)
    own_copy.start()
    sends = []
    high = [bit for bit in reversed(bits) if bit > 1]

    def send(source, target, bit):
        sends.append(db_copy(source, target, bit))
        sends[-1].start()

    if high:
        send(0, high[0], high[0])
    if seq > 1:
        send(0, 1, 1)
    for c in range(0, share, 256):
        dg_ref[c : c + 256] = t_dot(hid[:, c : c + 256], gm[...]).astype(bf16)
    mo_copies = []
    for j in range(seq):
        at = slice(j * rows, (j + 1) * rows)
        nm[at] = dot(hid[at], wd_ref[...]).astype(bf16)
        mo_copies.append(pltpu.make_async_copy(nm.at[pl.ds(j * rows, rows)], mo_ref.at[j], mo_sem.at[j]))
        mo_copies[-1].start()
    have = [0]
    for n, bit in enumerate(high):
        if n:
            for j in have:
                send(j, j ^ bit, bit)
        for j in have:
            db_copy(0, j ^ bit, bit).wait_recv()
            send(j ^ bit, j ^ bit ^ 1, 1)
        have += [j ^ bit for j in have]
    if seq > 1:
        for j in have:
            db_copy(0, j ^ 1, 1).wait_recv()
    for c in sends:
        c.wait_send()
    own_copy.wait()
    for c in mo_copies:
        c.wait()
    for bit in bits:
        for j in range(0, seq, 2 * bit):
            dn_copy(bit, j).wait_send()


def mlp(length, own, others, tok, grads, wo, wu, wd, gain):
    seq, rows, dim = tok.shape
    share = wu.shape[1]
    sub = 256
    depth = 2 if seq <= 4 else 1
    anywhere = pl.BlockSpec(memory_space=pl.ANY)
    vmem = pl.BlockSpec(memory_space=pltpu.VMEM)
    dma = pltpu.SemaphoreType.DMA
    return pl.pallas_call(
        functools.partial(mlp_kernel, seq, sub),
        out_shape=(
            jax.ShapeDtypeStruct((rows, dim), f32),
            jax.ShapeDtypeStruct((rows, dim), f32),
            jax.ShapeDtypeStruct((8, dim), f32),
            jax.ShapeDtypeStruct((seq, rows, dim), bf16),
            jax.ShapeDtypeStruct((seq, rows, dim), bf16),
            jax.ShapeDtypeStruct((dim, share), bf16),
            jax.ShapeDtypeStruct((share, dim), bf16),
        ),
        in_specs=[pl.BlockSpec(memory_space=pltpu.SMEM)] + [anywhere] * 4 + [vmem] * 4,
        out_specs=(vmem, vmem, vmem, anywhere, anywhere, vmem, vmem),
        scratch_shapes=[
            pltpu.VMEM((depth, seq, rows, dim // seq), bf16),
            pltpu.VMEM((depth, rows, dim), bf16),
            pltpu.VMEM((seq * rows, dim), bf16),
            pltpu.VMEM((seq * rows, dim), bf16),
            pltpu.VMEM((seq * rows, share), bf16),
            pltpu.VMEM((seq * rows, share), bf16),
            pltpu.VMEM((seq, rows, dim), bf16),
            pltpu.VMEM((max(seq - 1, 1), rows, dim), bf16),
            pltpu.VMEM((rows, dim), f32),
            dma((2, seq + 1)),
            dma((seq,)),
            dma((seq,)),
            dma((seq,)),
            dma((seq,)),
            dma((seq,)),
            dma((seq,)),
            dma,
        ],
        compiler_params=pltpu.CompilerParams(collective_id=2, has_side_effects=True, vmem_limit_bytes=60 << 20),
        cost_estimate=pl.CostEstimate(
            flops=2 * rows * seq * dim * (dim + 6 * share), bytes_accessed=32 << 20, transcendentals=rows * seq * share
        ),
        name="mlp",
    )(length, own, others, tok, grads, wo, wu, wd, gain)


def bias_table_grad(near, far):
    lane = np.arange(2 * QTILE)
    distance = np.where(lane < QTILE, lane, lane - 2 * QTILE) + NEAR - QTILE
    inside = (distance >= 0) & (distance < BLOCK)
    bucket = np.where(inside, bucket_of(np.clip(distance, 0, BLOCK)), BUCKETS)
    bucket = jnp.asarray(bucket.astype(np.int32))
    columns = [jnp.sum(jnp.where((bucket == i)[None], near, 0.0), axis=1) for i in range(BUCKETS)]
    columns[-1] = columns[-1] + jnp.sum(far, axis=1)
    return jnp.stack(columns, axis=1)


def inverse_rms(values):
    return lax.rsqrt(jnp.mean(values * values, axis=-1, keepdims=True) + EPSILON)


def norm_back(values, gain, rho, grad):
    scaled = gain * grad
    mean = jnp.mean(values * scaled, axis=-1, keepdims=True)
    gain_grad = (grad * values * rho).reshape(-1, 8, values.shape[1])
    return rho * scaled - values * (rho * rho * rho * mean), jnp.sum(gain_grad, axis=0)


def body(
    tokens,
    lengths,
    state_init,
    w_qkv,
    w_out,
    w_up,
    w_down,
    norm_attn,
    norm_mlp,
    rel_bias,
    state_query,
    gate_bias,
    out_grad,
    state_grad,
):
    seq_count = lax.axis_size("seq")
    fsdp_count = lax.axis_size("fsdp")
    seq_at = lax.axis_index("seq")
    heads = H // seq_count
    width = heads * DH
    tok_rows, dim = tokens.shape[1:]
    rows = tok_rows * seq_count
    hidden_all = w_up.shape[1]
    share = hidden_all // (seq_count * fsdp_count)

    piece = dim // (seq_count * fsdp_count)
    all_tokens, all_grad, qkv_w, gain_attn, gain_mlp, own_out, up_w = gather_start(
        tokens[0],
        out_grad[0],
        w_qkv,
        norm_attn.reshape(1, -1),
        norm_mlp.reshape(1, -1),
        w_out.reshape(seq_count, piece, dim),
        w_up,
        seq_count,
        fsdp_count,
    )
    qkv_w = qkv_w.reshape(dim, 3 * width)
    up_w = up_w.reshape(dim, hidden_all // seq_count)
    gain_attn = gain_attn.reshape(dim).astype(f32)
    gain_mlp = gain_mlp.reshape(dim).astype(f32)
    own_down = lax.dynamic_slice_in_dim(w_down, seq_at * share, share, axis=0)

    bias = bias_vector(rel_bias)
    forget = jax.nn.sigmoid(gate_bias)
    forget_row = forget.reshape(1, width)

    inputs = all_tokens.reshape(rows, dim).astype(f32)
    normed = (inputs * inverse_rms(inputs) * gain_attn).astype(bf16)
    qkv = dot(normed, qkv_w).astype(bf16)
    attended, others, out_w, down_w, final_memory, mem, upd, lse, slse = attend(
        qkv,
        state_init[0],
        lengths,
        state_query,
        forget_row,
        bias,
        own_out,
        own_down,
        heads,
        seq_count,
        fsdp_count,
    )
    out_w = out_w.reshape(dim, dim)
    down_w = down_w.reshape(fsdp_count * share, dim)
    own_out = lax.dynamic_slice_in_dim(out_w, seq_at * width, width, axis=0)
    mid_here, dmid, mlp_gain_grad, dbranch, mlp_parts, up_grad, down_grad = mlp(
        lengths, attended, others, all_tokens, all_grad, out_w, up_w, down_w, gain_mlp.reshape(1, dim)
    )
    span = fsdp_count // seq_count
    dqkv, small, up_part, down_total, out_part, output = attend_back(
        qkv,
        dbranch.reshape(rows, dim),
        own_out,
        attended,
        mem,
        upd,
        lse,
        slse,
        state_grad[0],
        lengths,
        state_query,
        forget_row,
        bias,
        up_grad.reshape(seq_count, fsdp_count, piece, hidden_all // seq_count),
        down_grad.reshape(seq_count, span * share, dim),
        mlp_parts,
        mid_here,
        seq_count,
        fsdp_count,
    )
    tokens_grad, qkv_part, down_part, small, gain_sums = finish(
        dqkv,
        qkv_w,
        normed,
        down_total,
        small,
        mlp_gain_grad,
        tokens[0],
        dmid,
        gain_attn.reshape(1, dim),
        seq_count,
        fsdp_count,
    )
    output = output[None]
    tokens_grad = tokens_grad[None]
    cut = heads * DH
    near_rows, far_rows = 2 * QTILE // DH, QTILE // DH
    dquery = small[:cut].reshape(heads, DH, DH)
    grad_gate = small[cut : cut + heads] * forget * (1.0 - forget)
    at = cut + heads
    near = small[at : at + heads * near_rows].reshape(heads, near_rows * DH)
    at += heads * near_rows
    far = small[at : at + heads * far_rows].reshape(heads, far_rows * DH)
    grad_table = bias_table_grad(near, far)
    if up_part.ndim == 3:
        up_part = up_part.reshape(seq_count, piece, fsdp_count, share)
        up_part = jnp.transpose(up_part, (1, 2, 0, 3)).reshape(piece, hidden_all)
    gain_sums = jnp.sum(gain_sums.reshape(2, 8, seq_count * fsdp_count, piece), axis=1)
    mine = seq_at * fsdp_count + lax.axis_index("fsdp")
    gain_sums = lax.dynamic_slice_in_dim(gain_sums, mine, 1, axis=1)[:, 0]
    mlp_gain_grad, attn_gain_grad = gain_sums[0], gain_sums[1]
    return (
        output,
        final_memory[None],
        tokens_grad,
        qkv_part,
        out_part,
        up_part,
        down_part,
        attn_gain_grad,
        mlp_gain_grad,
        grad_table,
        dquery,
        grad_gate,
    )


def solution(mesh):
    placed = (
        P("fsdp", "seq", None),
        P("fsdp"),
        P("fsdp", None, "seq"),
        P("fsdp", None),
        P("fsdp", None),
        P("fsdp", None),
        P("fsdp", None),
        P("fsdp"),
        P("fsdp"),
        P("seq", None),
        P("seq", None, None),
        P("seq", None),
        P("fsdp", "seq", None),
        P("fsdp", None, "seq"),
    )
    return jax.shard_map(
        body,
        mesh=mesh,
        in_specs=placed,
        out_specs=(
            P("fsdp", "seq", None),
            P("fsdp", None, "seq"),
            P("fsdp", "seq", None),
            P(("seq", "fsdp"), None),
            P(("seq", "fsdp"), None),
            P(("seq", "fsdp"), None),
            P(("seq", "fsdp"), None),
            P(("seq", "fsdp")),
            P(("seq", "fsdp")),
            P("seq", None),
            P("seq", None, None),
            P("seq", None),
        ),
        check_vma=False,
    )
```

```python
import functools
import math

import jax
import jax.numpy as jnp
import numpy as np
from jax import lax
from jax.experimental import pallas as pl
from jax.experimental.pallas import tpu as pltpu
from jax.sharding import PartitionSpec as P

H = 8
DH = 128
BLOCK = 512
STATE_VECTORS = 512
QTILE = 256
SPAN = BLOCK + QTILE

EPSILON = 1e-06
BUCKET_EDGES = (19, 21, 24, 27, 31, 35, 40, 46, 52, 59, 67, 77, 87, 99, 113)
BUCKETS = 32
LOG2E = math.log2(math.e)
SCALE = DH ** (-0.5)
NEAR = 384

f32 = jnp.float32
bf16 = jnp.bfloat16
MESH = pl.DeviceIdType.MESH


def bucket_of(distance):
    return np.minimum(distance, 16) + (distance[..., None] >= np.array(BUCKET_EDGES)).sum(-1)


def tile_distance():
    rows = np.arange(QTILE)[:, None]
    cols = np.arange(SPAN)[None, :]
    return rows + BLOCK - cols


def bias_vector(table):
    distance = BLOCK - np.arange(2 * BLOCK)
    inside = (distance >= 0) & (distance < BLOCK)
    bucket = jnp.asarray(np.where(inside, bucket_of(np.clip(distance, 0, BLOCK)), BUCKETS).astype(np.int32))
    total = jnp.full((table.shape[0], 2 * BLOCK), -jnp.inf, f32)
    for i in range(BUCKETS):
        total = jnp.where((bucket == i)[None], table[:, i : i + 1] * LOG2E, total)
    return total


def tile_bias(vector_ref, head):
    wide = jnp.broadcast_to(vector_ref[head : head + 1, :], (QTILE, 2 * BLOCK))
    return pltpu.roll(wide, 0, 1, stride=1, stride_axis=0)[:, :SPAN]


def dot(a, b):
    return jnp.dot(a, b, preferred_element_type=f32)


def dot_t(a, b):
    return lax.dot_general(a, b, (((1,), (1,)), ((), ())), preferred_element_type=f32)


def t_dot(a, b):
    return lax.dot_general(a, b, (((0,), (0,)), ((), ())), preferred_element_type=f32)


def to_row(column):
    wide = jnp.broadcast_to(column, (column.shape[0], 128))
    return wide.T[0:1, :]


def context_pieces(tile):
    start = tile * QTILE
    pieces = []
    if start < BLOCK:
        pieces.append((0, start, BLOCK, 0))
    pieces.append((1, 0, start + QTILE, BLOCK - start))
    return pieces


def softmax_parts(scores):
    top = functools.reduce(jnp.maximum, [jnp.max(s, axis=-1, keepdims=True) for s in scores])
    raised = [jnp.exp2(s - top) for s in scores]
    total = functools.reduce(jnp.add, [jnp.sum(e, axis=-1, keepdims=True) for e in raised])
    return raised, total, top + jnp.log2(total)


def line_gather(hi, lo, slot, own, z_send, z_recv, y_send, y_recv):
    f = lax.axis_index("fsdp")
    z, y = f // lo, f % lo

    def copy(i, origin, target, send, recv, first=False):
        ref = slot(i, origin)
        return pltpu.make_async_remote_copy(
            src_ref=own(i) if first else ref,
            dst_ref=ref,
            send_sem=send,
            recv_sem=recv,
            device_id={"fsdp": target},
            device_id_type=MESH,
        )

    def right(i, t):
        return copy(i, (z - t) * lo + y, (z + 1) * lo + y, z_send.at[i, 0, t], z_recv.at[i, 0, t], t == 0)

    def left(i, t):
        return copy(i, (z + t) * lo + y, (z - 1) * lo + y, z_send.at[i, 1, t], z_recv.at[i, 1, t], t == 0)

    def across(i, d):
        return copy(
            i, (z + d) * lo + y, z * lo + 1 - y, y_send.at[i, d + hi - 1], y_recv.at[i, d + hi - 1], d == 0
        )

    def start(i):
        pl.when(z + 1 < hi)(lambda: right(i, 0).start())
        pl.when(z >= 1)(lambda: left(i, 0).start())
        across(i, 0).start()

    def step(i, t):
        @pl.when(z - 1 - t >= 0)
        def _():
            copy(i, (z - 1 - t) * lo + y, f, z_send.at[i, 0, t], z_recv.at[i, 0, t]).wait_recv()
            if t + 1 < hi - 1:
                pl.when(z + 1 < hi)(lambda: right(i, t + 1).start())
            across(i, -1 - t).start()

        @pl.when(z + 1 + t < hi)
        def _():
            copy(i, (z + 1 + t) * lo + y, f, z_send.at[i, 1, t], z_recv.at[i, 1, t]).wait_recv()
            if t + 1 < hi - 1:
                pl.when(z >= 1)(lambda: left(i, t + 1).start())
            across(i, 1 + t).start()

    def arrive(i):
        for d in range(1 - hi, hi):

            @pl.when((z + d >= 0) & (z + d < hi))
            def _():
                copy(
                    i, (z + d) * lo + 1 - y, f, y_send.at[i, d + hi - 1], y_recv.at[i, d + hi - 1]
                ).wait_recv()

    def drain(i):
        for d in range(1 - hi, hi):

            @pl.when((z + d >= 0) & (z + d < hi))
            def _():
                across(i, d).wait_send()

        for t in range(hi - 1):

            @pl.when((z + 1 < hi) & (z - t >= 0))
            def _():
                right(i, t).wait_send()

            @pl.when((z >= 1) & (z + t < hi))
            def _():
                left(i, t).wait_send()

    return start, step, arrive, drain


def line_sems(count, hi):
    dma = pltpu.SemaphoreType.DMA
    return [dma((count, 2, hi)), dma((count, 2, hi)), dma((count, 2 * hi)), dma((count, 2 * hi))]


def greet(seq_targets, hi, lo):
    me = lax.axis_index("seq")
    f = lax.axis_index("fsdp")
    z, y = f // lo, f % lo
    barrier = pltpu.get_barrier_semaphore()
    for k in seq_targets:
        pl.semaphore_signal(barrier, inc=1, device_id={"seq": me ^ k}, device_id_type=MESH)
    near = (lax.rem(z + 1, hi) * lo + y, lax.rem(z + hi - 1, hi) * lo + y, z * lo + 1 - y)
    for target in near:
        pl.semaphore_signal(barrier, inc=1, device_id={"fsdp": target}, device_id_type=MESH)
    pl.semaphore_wait(barrier, len(seq_targets) + len(near))


def attend_kernel(
    heads,
    seq,
    hi,
    lo,
    length_ref,
    qkv_ref,
    init_ref,
    query_ref,
    forget_ref,
    vector_ref,
    own_out_ref,
    own_down_ref,
    att_ref,
    others_ref,
    outs_ref,
    downs_ref,
    final_ref,
    mem_ref,
    upd_ref,
    lse_ref,
    slse_ref,
    memory_ref,
    bias_ref,
    own_sem,
    att_send,
    att_recv,
    out_send,
    out_recv,
    z_send,
    z_recv,
    y_send,
    y_recv,
):
    me = lax.axis_index("seq")
    f = lax.axis_index("fsdp")
    length = length_ref[0]
    width = heads * DH
    scale2 = SCALE * LOG2E
    blocks = seq
    bits = [1 << i for i in range(seq.bit_length() - 1)]
    greet(bits, hi, lo)

    own_copies = [
        pltpu.make_async_copy(own_down_ref, downs_ref.at[f], own_sem.at[0]),
        pltpu.make_async_copy(own_out_ref, outs_ref.at[:, me % 2], own_sem.at[1]),
    ]
    for c in own_copies:
        c.start()

    def lowest(k):
        return k & -k

    def out_copy(sending):
        half = me % 2 if sending else 1 - me % 2
        return pltpu.make_async_remote_copy(
            src_ref=own_out_ref,
            dst_ref=outs_ref.at[:, half],
            send_sem=out_send,
            recv_sem=out_recv,
            device_id={"seq": me ^ 1},
            device_id_type=MESH,
        )

    def att_copy(k, b):
        bit = lowest(k)
        came = k ^ bit
        here = pl.ds(pl.multiple_of((b ^ me) * BLOCK, BLOCK), BLOCK)
        there = pl.ds(pl.multiple_of((b ^ me ^ bit) * BLOCK, BLOCK), BLOCK)
        src = others_ref.at[came, here] if came else att_ref.at[here]
        return pltpu.make_async_remote_copy(
            src_ref=src,
            dst_ref=others_ref.at[k, there],
            send_sem=att_send.at[k, b],
            recv_sem=att_recv.at[k, b],
            device_id={"seq": me ^ bit},
            device_id_type=MESH,
        )

    def att_arrival(k, b):
        here = pl.ds(pl.multiple_of((b ^ me) * BLOCK, BLOCK), BLOCK)
        return pltpu.make_async_remote_copy(
            src_ref=others_ref.at[k, here],
            dst_ref=others_ref.at[k, here],
            send_sem=att_send.at[k, b],
            recv_sem=att_recv.at[k, b],
            device_id={"seq": me},
            device_id_type=MESH,
        )

    passing = sorted([k for k in range(2, seq, 2)], key=lambda k: (bin(k).count("1"), -k))

    def onward(k, send):
        for bit in reversed(bits):
            if bit < lowest(k):
                send(k | bit)

    start, step, arrive, drain = line_gather(
        hi, lo, lambda i, origin: downs_ref.at[origin], lambda i: own_down_ref, z_send, z_recv, y_send, y_recv
    )

    start(0)
    out_copy(True).start()
    memory_ref[...] = init_ref[...].astype(f32)
    for head in range(heads):
        bias_ref[head] = tile_bias(vector_ref, head)

    @pl.loop(0, blocks)
    def _(block):
        cur_at = pl.multiple_of((block ^ me) * BLOCK, BLOCK)
        prev_at = pl.multiple_of((jnp.maximum(block - 1, 0) ^ me) * BLOCK, BLOCK)
        cur_ref = qkv_ref.at[pl.ds(cur_at, BLOCK)]
        prev_ref = qkv_ref.at[pl.ds(prev_at, BLOCK)]
        for t in range(min(hi - 1, blocks - 1)):
            pl.when(block == t + 1)(lambda t=t: step(0, t))

        live_block = block * BLOCK < length
        for head in range(heads):
            own = slice(head * DH, (head + 1) * DH)
            memory = memory_ref[:, own]
            low = memory.astype(bf16)
            mem_ref[block, :, own] = memory
            refs = (prev_ref, cur_ref)
            key_cols = slice(width + head * DH, width + (head + 1) * DH)
            value_cols = slice(2 * width + head * DH, 2 * width + (head + 1) * DH)
            for tile in range(BLOCK // QTILE):
                rows = slice(tile * QTILE, (tile + 1) * QTILE)
                query = cur_ref[rows, own]
                scores, values = [], []
                for which, at, end, col in context_pieces(tile):
                    s = dot_t(query, refs[which][at:end, key_cols])
                    position = (block - 1 + which) * BLOCK + at + lax.broadcasted_iota(jnp.int32, (1, end - at), 1)
                    live = (position >= 0) & (position < length)
                    s = s * scale2 + bias_ref[head, :, col : col + end - at]
                    scores.append(jnp.where(live, s, -jnp.inf))
                    values.append(refs[which][at:end, value_cols])
                scores.append(dot_t(query, low) * scale2)
                values.append(low)
                raised, total, lse = softmax_parts(scores)
                out = functools.reduce(jnp.add, [dot(e.astype(bf16), v) for e, v in zip(raised, values)])
                att_ref[pl.ds(cur_at + tile * QTILE, QTILE), own] = (out / total).astype(bf16)
                lse_ref[head : head + 1, pl.ds(pl.multiple_of(block * BLOCK, BLOCK) + tile * QTILE, QTILE)] = to_row(lse)
            own_key = cur_ref[:, key_cols]
            own_value = cur_ref[:, value_cols]
            squeries = dot(low, query_ref[head]).astype(bf16)
            position = block * BLOCK + lax.broadcasted_iota(jnp.int32, (1, BLOCK), 1)
            for tile in range(STATE_VECTORS // QTILE):
                rows = slice(tile * QTILE, (tile + 1) * QTILE)
                squery = squeries[rows]
                scores = [
                    dot_t(squery, low) * scale2,
                    jnp.where(position < length, dot_t(squery, own_key) * scale2, -jnp.inf),
                ]
                raised, total, lse = softmax_parts(scores)
                update = dot(raised[0].astype(bf16), low) + dot(raised[1].astype(bf16), own_value)
                update = update / total
                upd_ref[block, rows, own] = update
                slse_ref[head : head + 1, pl.ds(pl.multiple_of(block * BLOCK, BLOCK) + tile * QTILE, QTILE)] = to_row(
                    lse
                )
                forget = forget_ref[:, own]
                old = memory[rows]
                memory_ref[rows, own] = jnp.where(live_block, forget * old + (1.0 - forget) * update, old)

        for bit in reversed(bits):
            att_copy(bit, block).start()

        @pl.when(block >= 1)
        def _():
            for k in passing:
                att_arrival(k, block - 1).wait_recv()
                onward(k, lambda target: att_copy(target, block - 1).start())

    final_ref[...] = memory_ref[...]
    for t in range(min(hi - 1, blocks - 1), hi - 1):
        step(0, t)
    for k in passing:
        att_arrival(k, blocks - 1).wait_recv()
        onward(k, lambda target: att_copy(target, blocks - 1).start())
    arrive(0)
    out_copy(False).wait_recv()
    for k in range(1, seq, 2):
        for b in range(blocks):
            att_arrival(k, b).wait_recv()
    for c in own_copies:
        c.wait()
    drain(0)
    out_copy(True).wait_send()
    for k in range(1, seq):
        for b in range(blocks):
            att_copy(k, b).wait_send()


def attend(qkv, init, length, state_query, forget, bias, own_out, own_down, heads, seq, fsdp):
    rows, width3 = qkv.shape
    width = heads * DH
    blocks = rows // BLOCK
    lo = 2
    hi = fsdp // lo
    dim = own_down.shape[1]
    anywhere = pl.BlockSpec(memory_space=pl.ANY)
    vmem = pl.BlockSpec(memory_space=pltpu.VMEM)
    dma = pltpu.SemaphoreType.DMA
    return pl.pallas_call(
        functools.partial(attend_kernel, heads, seq, hi, lo),
        out_shape=(
            jax.ShapeDtypeStruct((rows, width), bf16),
            jax.ShapeDtypeStruct((seq, rows, width), bf16),
            jax.ShapeDtypeStruct((fsdp, 2) + own_out.shape[1:], bf16),
            jax.ShapeDtypeStruct((fsdp,) + own_down.shape, bf16),
            jax.ShapeDtypeStruct((STATE_VECTORS, width), f32),
            jax.ShapeDtypeStruct((blocks, STATE_VECTORS, width), f32),
            jax.ShapeDtypeStruct((blocks, STATE_VECTORS, width), f32),
            jax.ShapeDtypeStruct((heads, rows), f32),
            jax.ShapeDtypeStruct((heads, blocks * STATE_VECTORS), f32),
        ),
        in_specs=[pl.BlockSpec(memory_space=pltpu.SMEM)] + [vmem] * 7,
        out_specs=(vmem, anywhere, anywhere, anywhere, vmem, vmem, vmem, vmem, vmem),
        scratch_shapes=[
            pltpu.VMEM((STATE_VECTORS, width), f32),
            pltpu.VMEM((heads, QTILE, SPAN), f32),
            dma((2,)),
            dma((seq, blocks)),
            dma((seq, blocks)),
            dma,
            dma,
        ]
        + line_sems(1, hi),
        compiler_params=pltpu.CompilerParams(collective_id=3, has_side_effects=True, vmem_limit_bytes=40 << 20),
        cost_estimate=pl.CostEstimate(
            flops=blocks * heads * 512 * 2400 * 128 * 4, bytes_accessed=16 << 20, transcendentals=10 << 20
        ),
        name="attend",
    )(length, qkv, init, state_query, forget, bias, own_out, own_down)


def line_reduce(hi, lo, block, total, from_y, from_z, z_send, z_recv, y_send, y_recv, loads=None):
    loads = loads or {}
    f = lax.axis_index("fsdp")
    z, y = f // lo, f % lo

    def remote(src, dst, send, recv, target):
        return pltpu.make_async_remote_copy(
            src_ref=src, dst_ref=dst, send_sem=send, recv_sem=recv, device_id={"fsdp": target}, device_id_type=MESH
        )

    def across(i, d):
        return remote(
            block(i, d * lo + 1 - y), from_y[i].at[d], y_send.at[i, d], y_recv.at[i, d], z * lo + 1 - y
        )

    def start(i):
        for d in range(hi):
            across(i, d).start()

    def combine(i):
        for d in range(hi):
            across(i, d).wait_recv()
            if i in loads:
                loads[i][d].wait()
                own = total[i].at[d]
            else:
                own = block(i, d * lo + y)
            total[i][d] = (own[...].astype(f32) + from_y[i][d].astype(f32)).astype(bf16)

    def hop(i, side, t, at, target):
        return remote(
            total[i].at[jnp.clip(at, 0, hi - 1)],
            from_z[i].at[side, t],
            z_send.at[i, side, t],
            z_recv.at[i, side, t],
            target,
        )

    def sending(t):
        d = t - (hi - 1 - z)
        m = hi - 1 - (t - z)
        return ((0, d, (d >= 0) & (d < z), z - 1), (1, m, (m > z) & (m < hi), z + 1))

    def zsend(i, t):
        for side, at, cond, target in sending(t):
            pl.when(cond)(lambda: hop(i, side, t, at, target * lo + y).start())

    def zrecv(i, t):
        d = t - (hi - 2 - z)
        m = hi - 1 - (t - (z - 1))
        for side, at, cond in ((0, d, (z + 1 < hi) & (d >= 0)), (1, m, (z > 0) & (m < hi))):

            @pl.when(cond)
            def _():
                hop(i, side, t, at, f).wait_recv()
                slot = jnp.clip(at, 0, hi - 1)
                total[i][slot] = (total[i][slot].astype(f32) + from_z[i][side, t].astype(f32)).astype(bf16)

    def drain_y(i):
        for d in range(hi):
            across(i, d).wait_send()

    def drain_z(i):
        for t in range(hi - 1):
            for side, at, cond, target in sending(t):
                pl.when(cond)(lambda: hop(i, side, t, at, f).wait_send())

    return start, combine, zsend, zrecv, drain_y, drain_z


def seq_levels(seq):
    bits = [1 << i for i in range(seq.bit_length() - 1)]
    slots = {}
    for bit in bits:
        for j in range(0, seq, 2 * bit):
            slots[bit, j] = len(slots)
    return bits, slots


def diagonal_sums(tile):
    rows, lanes = tile.shape
    wide = jnp.concatenate([tile, jnp.zeros((rows, lanes), f32)], axis=1)
    row = lax.broadcasted_iota(jnp.int32, wide.shape, 0)
    bit = 1
    while bit < rows:
        wide = jnp.where((row & bit) != 0, pltpu.roll(wide, 2 * lanes - bit, 1), wide)
        bit *= 2
    return jnp.sum(wide, axis=0, keepdims=True)


def attend_back_kernel(heads, seq, hi, lo, inside, length_ref, *refs):
    refs = list(refs)

    def take(count):
        taken = refs[:count]
        del refs[:count]
        return taken

    qkv_hbm, db_hbm, wout_ref, att_hbm, mem_hbm, upd_hbm, lse_ref, slse_ref = take(8)
    sgrad_ref, query_ref, forget_ref, vector_ref, up_ref, down_ref, mo_ref, mid_hbm = take(8)
    ow_in = None if inside else take(1)[0]
    dqkv_out, small_ref, upart_ref, dtotal_ref, opart_ref, output_ref = take(6)
    qkv_ref, db_ref, att_ref, mem_ref, upd_ref, mid_ref, dqkv_ref = take(7)
    dmem_ref, dnext_ref, dctx_ref, bias_ref, near_ref, far_ref, dout_ref, ow_buf = take(8)
    moved, to, tu, yo, yu, yd, zo, zu, xu, mo_low, mo_in = take(11)
    z_send, z_recv, y_send, y_recv, m_send, m_recv, e_send, e_recv, x_send, x_recv = take(10)
    load_sem, block_sem, up_sem, mo_sem, out_sem = take(5)
    ow_ref = ow_buf if inside else ow_in

    me = lax.axis_index("seq")
    f = lax.axis_index("fsdp")
    z, y = f // lo, f % lo
    blocks = seq
    length = length_ref[0]
    width = heads * DH
    scale2 = SCALE * LOG2E
    tok_rows = mid_ref.shape[0]
    share = dtotal_ref.shape[1]
    bits, slots = seq_levels(seq)

    def chunk_at(block):
        return pl.ds(pl.multiple_of((block ^ me) * BLOCK, BLOCK), BLOCK)

    def block_loads(block):
        at = chunk_at(block)
        pairs = (
            (qkv_hbm.at[at], qkv_ref.at[at]),
            (mem_hbm.at[block], mem_ref.at[block]),
            (upd_hbm.at[block], upd_ref.at[block]),
        )
        return [pltpu.make_async_copy(a, b, block_sem.at[i, block]) for i, (a, b) in enumerate(pairs)]

    loads = [
        pltpu.make_async_copy(att_hbm, att_ref, load_sem.at[0]),
        pltpu.make_async_copy(db_hbm, db_ref, load_sem.at[1]),
        pltpu.make_async_copy(down_ref.at[me], moved.at[me], load_sem.at[2]),
        pltpu.make_async_copy(mid_hbm, mid_ref, load_sem.at[3]),
    ]
    up_loads = [pltpu.make_async_copy(up_ref.at[:, d * lo + y], tu.at[d], up_sem.at[d]) for d in range(hi)]
    mo_loads = [pltpu.make_async_copy(mo_ref.at[j], mo_low.at[j // 2], mo_sem.at[j // 2]) for j in range(0, seq, 2)]
    for c in loads[:2] + block_loads(blocks - 1) + mo_loads + up_loads:
        c.start()
    for b in reversed(range(blocks - 1)):
        for c in block_loads(b):
            c.start()
    for c in loads[2:]:
        c.start()
    greet(list(range(1, seq)), hi, lo)

    def mo_copy(bit, j):
        slot = slots[bit, j]
        return pltpu.make_async_remote_copy(
            src_ref=mo_ref.at[j ^ bit] if bit == 1 else mo_low.at[(j ^ bit) // 2],
            dst_ref=mo_in.at[slot],
            send_sem=m_send.at[slot],
            recv_sem=m_recv.at[slot],
            device_id={"seq": me ^ bit},
            device_id_type=MESH,
        )

    def move_copy(k):
        return pltpu.make_async_remote_copy(
            src_ref=down_ref.at[me ^ k],
            dst_ref=moved.at[me],
            send_sem=e_send.at[k],
            recv_sem=e_recv.at[k],
            device_id={"seq": me ^ k},
            device_id_type=MESH,
        )

    def move_arrival(k):
        return pltpu.make_async_remote_copy(
            src_ref=down_ref.at[me],
            dst_ref=moved.at[me ^ k],
            send_sem=e_send.at[k],
            recv_sem=e_recv.at[k],
            device_id={"seq": me},
            device_id_type=MESH,
        )

    def block_of(i, target):
        if i == 0:
            return ow_ref.at[target]
        if i == 1:
            return up_ref.at[:, target]
        return moved.at[target % seq, pl.ds(pl.multiple_of((target // seq) * share, share), share)]

    start, combine, zsend, zrecv, drain_y, drain_z = line_reduce(
        hi,
        lo,
        block_of,
        (to, tu, dtotal_ref),
        (yo, yu, yd),
        (zo, zu),
        z_send,
        z_recv,
        y_send,
        y_recv,
        {1: up_loads},
    )

    def exchange(k, sending):
        return pltpu.make_async_remote_copy(
            src_ref=tu.at[z, me ^ k] if sending else tu.at[z, me],
            dst_ref=xu.at[me] if sending else xu.at[me ^ k],
            send_sem=x_send.at[k],
            recv_sem=x_recv.at[k],
            device_id={"seq": me ^ k if sending else me},
            device_id_type=MESH,
        )

    start(1)
    for j in range(seq - 1, 0, -2):
        mo_copy(1, j ^ 1).start()
    for k in reversed(range(1, seq)):
        move_copy(k).start()
    dmem_ref[...] = sgrad_ref[...].astype(f32)
    dnext_ref[...] = jnp.zeros_like(dnext_ref)
    small_ref[...] = jnp.zeros_like(small_ref)
    near_ref[...] = jnp.zeros_like(near_ref)
    far_ref[...] = jnp.zeros_like(far_ref)
    for head in range(heads):
        bias_ref[head] = tile_bias(vector_ref, head).T
    for c in loads[:2]:
        c.wait()
    if inside:
        full = t_dot(att_ref[...], db_ref[...]).astype(bf16)
        ow_buf[...] = full.reshape(ow_buf.shape)
    start(0)

    def mo_step(j):
        mo_loads[j // 2].wait()
        for bit in bits:
            if j & bit:
                mo_copy(bit, j ^ bit).start()
                break
            mo_copy(bit, j).wait_recv()
            own = mo_low[j // 2].astype(f32)
            mo_low[j // 2] = (own + mo_in[slots[bit, j]].astype(f32)).astype(bf16)

    def down_ready():
        for k in range(1, seq):
            move_arrival(k).wait_recv()
        loads[2].wait()
        start(2)

    def up_done():
        for k in range(1, seq):
            exchange(k, True).start()

    jobs = [lambda j=j: mo_step(j) for j in range(seq - 2, 0, -2)]
    jobs += [lambda: None, lambda: None]
    jobs.append(lambda: down_ready())
    jobs.append(lambda: (combine(1), zsend(1, 0), combine(0), zsend(0, 0)))
    for t in range(hi - 2):
        jobs.append(lambda t=t: (zrecv(1, t), zsend(1, t + 1), zrecv(0, t), zsend(0, t + 1)))
    jobs.append(lambda: (zrecv(1, hi - 2), up_done(), zrecv(0, hi - 2)))
    points = blocks * heads - 1

    dq_row = heads * DH
    block_loads(blocks - 1)[0].wait()

    @pl.loop(0, blocks)
    def _(step):
        block = blocks - 1 - step
        pl.when(block >= 1)(lambda: block_loads(jnp.maximum(block - 1, 0))[0].wait())
        for c in block_loads(block)[1:]:
            c.wait()
        cur_at = pl.multiple_of((block ^ me) * BLOCK, BLOCK)
        prev_at = pl.multiple_of((jnp.maximum(block - 1, 0) ^ me) * BLOCK, BLOCK)
        base = pl.multiple_of(block * BLOCK, BLOCK)
        cur_ref = qkv_ref.at[pl.ds(cur_at, BLOCK)]
        prev_ref = qkv_ref.at[pl.ds(prev_at, BLOCK)]
        live_block = block * BLOCK < length
        refs = (prev_ref, cur_ref)
        dout_ref[...] = dot_t(db_ref[pl.ds(cur_at, BLOCK)], wout_ref[...]).astype(bf16)
        for head in range(heads):
            for n, job in enumerate(jobs[:points]):
                if (n + 1) % heads == head:
                    pl.when(step == (n + 1) // heads)(lambda job=job: (job(), None)[1])
            own = slice(head * DH, (head + 1) * DH)
            key_cols = slice(width + head * DH, width + (head + 1) * DH)
            value_cols = slice(2 * width + head * DH, 2 * width + (head + 1) * DH)
            memory = mem_ref[block, :, own]
            update = upd_ref[block, :, own]
            low = memory.astype(bf16)
            forget = forget_ref[:, own]
            dmem = dmem_ref[:, own]
            dupd = jnp.where(live_block, (1.0 - forget) * dmem, 0.0).astype(bf16)
            gone = jnp.where(live_block, dmem * (memory - update), 0.0)
            small_ref[dq_row + head : dq_row + head + 1, :] += jnp.sum(gone, axis=0, keepdims=True)
            dmem_new = jnp.where(live_block, forget * dmem, dmem)
            own_key = cur_ref[:, key_cols]
            own_value = cur_ref[:, value_cols]
            squeries = dot(low, query_ref[head]).astype(bf16)
            sdelta = jnp.sum((dupd.astype(f32) * update).T, axis=0, keepdims=True)
            slse = slse_ref[head : head + 1, pl.ds(base, BLOCK)]
            dsquery = jnp.zeros((STATE_VECTORS, DH), f32)
            dkey = []
            dvalue = []
            for part in range(2 * STATE_VECTORS // QTILE):
                own_part = part >= STATE_VECTORS // QTILE
                at = (part % (STATE_VECTORS // QTILE)) * QTILE
                keys = (own_key if own_part else low)[at : at + QTILE]
                values = (own_value if own_part else low)[at : at + QTILE]
                s = dot_t(keys, squeries) * scale2 - slse
                if own_part:
                    position = block * BLOCK + at + lax.broadcasted_iota(jnp.int32, (QTILE, 1), 0)
                    s = jnp.where(position < length, s, -jnp.inf)
                p = jnp.exp2(s)
                dp = dot_t(values, dupd)
                ds = (p * (dp - sdelta)).astype(bf16)
                dvalue.append(dot(p.astype(bf16), dupd))
                dkey.append(dot(ds, squeries))
                dsquery += t_dot(ds, keys)
            half = STATE_VECTORS // QTILE
            dlow = [dvalue[i] + dkey[i] * SCALE for i in range(half)]
            dctx_ref[0, 0:BLOCK] = jnp.zeros((BLOCK, DH), f32)
            dctx_ref[1, 0:BLOCK] = jnp.zeros((BLOCK, DH), f32)
            for i in range(half):
                rows = slice(BLOCK + i * QTILE, BLOCK + (i + 1) * QTILE)
                old = slice(i * QTILE, (i + 1) * QTILE)
                dctx_ref[0, rows] = dkey[half + i] * SCALE + dnext_ref[0, old, own]
                dctx_ref[1, rows] = dvalue[half + i] + dnext_ref[1, old, own]
            dsq = (dsquery * SCALE).astype(bf16)
            small_ref[head * DH : (head + 1) * DH, :] += t_dot(low, dsq)
            dmem_ref[:, own] = dmem_new + dot_t(dsq, query_ref[head])
            for tile in range(BLOCK // QTILE):
                rows = slice(tile * QTILE, (tile + 1) * QTILE)
                here = pl.ds(cur_at + tile * QTILE, QTILE)
                query = cur_ref[rows, own]
                dout = dout_ref[rows, own]
                lse = lse_ref[head : head + 1, pl.ds(base + tile * QTILE, QTILE)]
                delta = jnp.sum((dout.astype(f32) * att_ref[here, own].astype(f32)).T, axis=0, keepdims=True)
                dq = jnp.zeros((QTILE, DH), f32)
                for which, first, end, col in context_pieces(tile):
                    for at in range(first, end, QTILE):
                        keys = refs[which][at : at + QTILE, key_cols]
                        values = refs[which][at : at + QTILE, value_cols]
                        band = col + at - first
                        position = (block - 1 + which) * BLOCK + at + lax.broadcasted_iota(jnp.int32, (QTILE, 1), 0)
                        live = (position >= 0) & (position < length)
                        s = dot_t(keys, query) * scale2 + bias_ref[head, band : band + QTILE, :] - lse
                        p = jnp.exp2(jnp.where(live, s, -jnp.inf))
                        dp = dot_t(values, dout)
                        ds = (p * (dp - delta)).astype(bf16)
                        wide = ds.astype(f32)
                        edge = min(max(SPAN - NEAR - band, 0), QTILE)
                        if edge:
                            far_ref[head] += functools.reduce(jnp.add, [wide[i : i + 8] for i in range(0, edge, 8)])
                        if edge < QTILE:
                            at_near = band + edge - (SPAN - NEAR)
                            near_ref[head, at_near : at_near + QTILE - edge] += wide[edge:]
                        into = slice(which * BLOCK + at, which * BLOCK + at + QTILE)
                        dctx_ref[1, into] += dot(p.astype(bf16), dout)
                        dctx_ref[0, into] += dot(ds, query) * SCALE
                        dq += t_dot(ds, keys)
                for part in range(half):
                    keys = low[part * QTILE : (part + 1) * QTILE]
                    s = dot_t(keys, query) * scale2 - lse
                    p = jnp.exp2(s)
                    dp = dot_t(keys, dout)
                    ds = (p * (dp - delta)).astype(bf16)
                    dlow[part] += dot(p.astype(bf16), dout) + dot(ds, query) * SCALE
                    dq += t_dot(ds, keys)
                dqkv_ref[here, own] = (dq * SCALE).astype(bf16)
            for part in range(half):
                dmem_ref[part * QTILE : (part + 1) * QTILE, own] += dlow[part]
            dnext_ref[0, :, own] = dctx_ref[0, 0:BLOCK]
            dnext_ref[1, :, own] = dctx_ref[1, 0:BLOCK]
            dqkv_ref[pl.ds(cur_at, BLOCK), key_cols] = dctx_ref[0, BLOCK:].astype(bf16)
            dqkv_ref[pl.ds(cur_at, BLOCK), value_cols] = dctx_ref[1, BLOCK:].astype(bf16)

    dqkv_store = pltpu.make_async_copy(dqkv_ref, dqkv_out, out_sem)
    dqkv_store.start()
    for job in jobs[points:]:
        job()
    member = bucket_members()
    lane = lax.broadcasted_iota(jnp.int32, (1, DH), 1)
    for head in range(heads):
        sums = jnp.broadcast_to(diagonal_sums(near_ref[head]), (8, 2 * QTILE))
        table = jnp.dot(sums, member, precision=lax.Precision.HIGHEST, preferred_element_type=f32)[0:1]
        total = jnp.sum(jnp.sum(far_ref[head], axis=0, keepdims=True), axis=1, keepdims=True)
        row = dq_row + heads + head
        small_ref[row : row + 1, :] = table + jnp.where(lane == BUCKETS - 1, total, 0.0)
        row = dq_row + head
        forget = forget_ref[:, head * DH : (head + 1) * DH]
        small_ref[row : row + 1, :] = small_ref[row : row + 1, :] * forget * (1.0 - forget)
    loads[3].wait()
    mo_loads[0].wait()
    for bit in bits:
        mo_copy(bit, 0).wait_recv()
    step = 128
    for r in range(0, tok_rows, step):
        at = slice(r, r + step)
        value = mid_ref[at] + mo_low[0, at].astype(f32)
        for bit in bits:
            value = value + mo_in[slots[bit, 0], at].astype(f32)
        position = me * tok_rows + r + lax.broadcasted_iota(jnp.int32, (step, 1), 0)
        output_ref[at] = (value * jnp.where(position < length, 1.0, 0.0)).astype(bf16)
    combine(2)
    opart_ref[...] = to[z].astype(f32)
    for k in range(1, seq):
        exchange(k, False).wait_recv()
    xu[me] = tu[z, me]
    write_parts(upart_ref, xu, seq, share)
    for i in range(3):
        drain_y(i)
    for i in range(2):
        drain_z(i)
    for bit in bits:
        for j in range(0, seq, 2 * bit):
            mo_copy(bit, j).wait_send()
    for k in range(1, seq):
        move_copy(k).wait_send()
        exchange(k, True).wait_send()
    dqkv_store.wait()


def bucket_members():
    shape = (2 * QTILE, DH)
    row = lax.broadcasted_iota(jnp.int32, shape, 0)
    lane = lax.broadcasted_iota(jnp.int32, shape, 1)
    distance = jnp.where(row < QTILE, row, row - 2 * QTILE) + NEAR - QTILE
    bucket = jnp.minimum(distance, 16)
    for edge in BUCKET_EDGES:
        bucket = bucket + jnp.where(distance >= edge, 1, 0)
    inside = (distance >= 0) & (distance < BLOCK) & (bucket == lane)
    return jnp.where(inside, 1.0, 0.0)


def write_parts(out_ref, pieces, seq, unit):
    if len(out_ref.shape) == 3:
        out_ref[...] = pieces[...].astype(f32)
        return
    count = pieces.shape[2] // unit
    for k in range(seq):
        for c in range(count):
            at = (c * seq + k) * unit
            out_ref[:, at : at + unit] = pieces[k, :, c * unit : (c + 1) * unit].astype(f32)


def attend_back(
    qkv, db, wout, att, mem, upd, lse, slse, sgrad, length, state_query, forget, bias, up, down, mo, mid, seq, fsdp
):
    rows, width3 = qkv.shape
    width = width3 // 3
    heads = width // DH
    dim = db.shape[1]
    lo = 2
    hi = fsdp // lo
    piece = up.shape[2]
    hidden = up.shape[3]
    share = hidden // fsdp
    tok_rows = mid.shape[0]
    inside = piece % 16 == 0
    blocks = (piece, dim), (seq, piece, hidden), (share, dim)
    small_rows = heads * (DH + 2)
    small_rows += -small_rows % 8
    vmem = pl.BlockSpec(memory_space=pltpu.VMEM)
    anywhere = pl.BlockSpec(memory_space=pl.ANY)
    dma = pltpu.SemaphoreType.DMA

    def buf(*shape):
        return pltpu.VMEM(shape, bf16)

    extra = []
    if not inside:
        extra.append(t_dot(att, db).astype(bf16).reshape(fsdp, piece, dim))
    upart = (piece, hidden * seq) if share % 128 == 0 else (seq, piece, hidden)
    return pl.pallas_call(
        functools.partial(attend_back_kernel, heads, seq, hi, lo, inside),
        out_shape=(
            jax.ShapeDtypeStruct((rows, width3), bf16),
            jax.ShapeDtypeStruct((small_rows, DH), f32),
            jax.ShapeDtypeStruct(upart, f32),
            jax.ShapeDtypeStruct((hi, share, dim), bf16),
            jax.ShapeDtypeStruct((piece, dim), f32),
            jax.ShapeDtypeStruct((tok_rows, dim), bf16),
        ),
        in_specs=[pl.BlockSpec(memory_space=pltpu.SMEM), anywhere, anywhere, vmem]
        + [anywhere] * 3
        + [vmem] * 6
        + [anywhere] * 4
        + [vmem] * len(extra),
        out_specs=(anywhere,) + (vmem,) * 5,
        scratch_shapes=[
            buf(rows, width3),
            buf(rows, dim),
            buf(rows, width),
            pltpu.VMEM(mem.shape, f32),
            pltpu.VMEM(upd.shape, f32),
            pltpu.VMEM((tok_rows, dim), f32),
            buf(rows, width3),
            pltpu.VMEM((STATE_VECTORS, width), f32),
            pltpu.VMEM((2, BLOCK, width), f32),
            pltpu.VMEM((2, 2 * BLOCK, DH), f32),
            pltpu.VMEM((heads, SPAN, QTILE), f32),
            pltpu.VMEM((heads, NEAR, QTILE), f32),
            pltpu.VMEM((heads, 8, QTILE), f32),
            buf(BLOCK, width),
            buf(fsdp, piece, dim),
            buf(*down.shape),
            buf(hi, *blocks[0]),
            buf(hi, *blocks[1]),
            buf(hi, *blocks[0]),
            buf(hi, *blocks[1]),
            buf(hi, *blocks[2]),
            buf(2, max(hi - 1, 1), *blocks[0]),
            buf(2, max(hi - 1, 1), *blocks[1]),
            buf(*blocks[1]),
            buf(max(seq // 2, 1), tok_rows, dim),
            buf(max(seq - 1, 1), tok_rows, dim),
            dma((2, 2, hi)),
            dma((2, 2, hi)),
            dma((3, hi)),
            dma((3, hi)),
            dma((seq,)),
            dma((seq,)),
            dma((seq,)),
            dma((seq,)),
            dma((seq,)),
            dma((seq,)),
            dma((4,)),
            dma((3, seq)),
            dma((hi,)),
            dma((seq,)),
            dma,
        ],
        compiler_params=pltpu.CompilerParams(collective_id=4, has_side_effects=True, vmem_limit_bytes=62 << 20),
        cost_estimate=pl.CostEstimate(
            flops=seq * heads * 512 * 2400 * 128 * 10, bytes_accessed=20 << 20, transcendentals=10 << 20
        ),
        name="attend_back",
    )(
        length, qkv, db, wout, att, mem, upd, lse, slse, sgrad, state_query, forget, bias, up, down, mo, mid, *extra
    )


def gather_kernel(
    seq,
    hi,
    lo,
    tok_ref,
    grad_ref,
    wq_ref,
    ga_ref,
    gm_ref,
    wo_ref,
    wu_ref,
    toks_ref,
    grads_ref,
    wqs_ref,
    gas_ref,
    gms_ref,
    wos_ref,
    wus_ref,
    *rest,
):
    own_bufs = rest[:7]
    own_sem, store_sem, seq_send, seq_recv, z_send, z_recv, y_send, y_recv = rest[7:]
    me = lax.axis_index("seq")
    f = lax.axis_index("fsdp")
    fsdp = hi * lo
    bits = [1 << i for i in range(seq.bit_length() - 1)]
    greet(bits, hi, lo)

    pairs = ((tok_ref, toks_ref), (grad_ref, grads_ref))

    def seq_copy(i, source, slot, bit):
        src, out = pairs[i]
        return pltpu.make_async_remote_copy(
            src_ref=out.at[source] if source else src,
            dst_ref=out.at[slot],
            send_sem=seq_send.at[i, slot],
            recv_sem=seq_recv.at[i, slot],
            device_id={"seq": me ^ bit},
            device_id_type=MESH,
        )

    sends = []

    def send(i, source, slot, bit):
        sends.append(seq_copy(i, source, slot, bit))
        sends[-1].start()

    high = [bit for bit in reversed(bits) if bit > 1]
    if high:
        send(0, 0, high[0], high[0])
    if seq > 1:
        send(0, 0, 1, 1)

    width = wqs_ref.shape[2] // 3
    share = wus_ref.shape[2] // fsdp
    every = wq_ref.shape[1] // 3
    loads = [[] for _ in own_bufs]

    def load(i, src, dst):
        loads[i].append(pltpu.make_async_copy(src, dst, own_sem.at[i, len(loads[i])]))
        loads[i][-1].start()

    wq_buf, ga_buf, gm_buf, wo_buf, wu_buf, tok_buf, grad_buf = own_bufs
    for c in range(3):
        cols = pl.ds(pl.multiple_of(c * every + me * width, width), width)
        load(0, wq_ref.at[:, cols], wq_buf.at[:, pl.ds(c * width, width)])
    load(1, ga_ref, ga_buf)
    load(2, gm_ref, gm_buf)
    load(3, wo_ref.at[me % 2], wo_buf)
    if wu_ref.shape[1] == wus_ref.shape[2]:
        load(4, wu_ref, wu_buf)
    else:
        for c in range(fsdp):
            cols = pl.ds(pl.multiple_of((c * seq + me) * share, share), share)
            load(4, wu_ref.at[:, cols], wu_buf.at[:, pl.ds(c * share, share)])
    load(5, tok_ref, tok_buf)
    load(6, grad_ref, grad_buf)
    outs = (wqs_ref, gas_ref, gms_ref, wos_ref, wus_ref)
    start, step, arrive, drain = line_gather(
        hi, lo, lambda i, origin: outs[i].at[origin], lambda i: own_bufs[i], z_send, z_recv, y_send, y_recv
    )
    own_stores = []
    for i in range(len(own_bufs)):
        for c in loads[i]:
            c.wait()
        if i < len(outs):
            start(i)
        target = outs[i].at[f] if i < len(outs) else pairs[i - len(outs)][1].at[0]
        own_stores.append(pltpu.make_async_copy(own_bufs[i], target, store_sem.at[i]))
        own_stores[-1].start()
    if high:
        send(1, 0, high[0], high[0])
    if seq > 1:
        send(1, 0, 1, 1)
    for t in range(hi - 1):
        for i in range(len(outs)):
            step(i, t)
    for i in range(len(pairs)):
        have = [0]
        for n, bit in enumerate(high):
            if n:
                for j in have:
                    send(i, j, j ^ bit, bit)
            for j in have:
                seq_copy(i, 0, j ^ bit, bit).wait_recv()
                send(i, j ^ bit, j ^ bit ^ 1, 1)
            have += [j ^ bit for j in have]
        if seq > 1:
            for j in have:
                seq_copy(i, 0, j ^ 1, 1).wait_recv()
    for i in range(len(outs)):
        arrive(i)
    for i in range(len(outs)):
        drain(i)
    for c in sends:
        c.wait_send()
    for c in own_stores:
        c.wait()


def gather_start(tokens, grads, w_qkv, gain_a, gain_m, w_out, w_up, seq, fsdp):
    lo = 2
    hi = fsdp // lo
    dim_rows, hidden = w_up.shape
    share = hidden // (seq * fsdp)
    if share % 128:
        w_up = lax.dynamic_slice_in_dim(w_up.reshape(dim_rows, fsdp, seq, share), lax.axis_index("seq"), 1, axis=2)
        w_up = w_up.reshape(dim_rows, fsdp * share)
    anywhere = pl.BlockSpec(memory_space=pl.ANY)
    dma = pltpu.SemaphoreType.DMA
    shapes = (
        (seq,) + tokens.shape,
        (seq,) + grads.shape,
        (fsdp, dim_rows, w_qkv.shape[1] // seq),
        (fsdp,) + gain_a.shape,
        (fsdp,) + gain_m.shape,
        (fsdp,) + w_out.shape[1:],
        (fsdp, dim_rows, hidden // seq),
    )
    return pl.pallas_call(
        functools.partial(gather_kernel, seq, hi, lo),
        out_shape=tuple(jax.ShapeDtypeStruct(shape, bf16) for shape in shapes),
        in_specs=[anywhere] * 7,
        out_specs=(anywhere,) * 7,
        scratch_shapes=[pltpu.VMEM(shape[1:], bf16) for shape in shapes[2:] + shapes[:2]]
        + [dma((7, max(fsdp, 3))), dma((7,)), dma((2, seq)), dma((2, seq))]
        + line_sems(5, hi),
        compiler_params=pltpu.CompilerParams(collective_id=0, has_side_effects=True),
        name="gather_start",
    )(tokens, grads, w_qkv, gain_a, gain_m, w_out, w_up)


def finish_kernel(seq, hi, lo, inside, *refs):
    refs = list(refs)

    def take(count):
        taken = refs[:count]
        del refs[:count]
        return taken

    dqkv_hbm, wqkv_hbm, normed_hbm, down_ref, small_ref, mlp_gain_ref, tok_hbm, dmid_hbm, gain_ref = take(9)
    gq_in = None if inside else take(1)[0]
    tg_ref, rq_ref, rd_ref, dquery_ref, gate_ref, table_ref, again_ref, mgain_ref = take(8)
    dqkv_ref, wqkv_ref, normed_ref, tok_ref, dmid_ref = take(5)
    low, into, acc, gq_buf, tq, td, yq, zq, zd, xq, sy, sz, gains, gy, gz, gs = take(16)
    dn_send, dn_recv, z_send, z_recv, y_send, y_recv, x_send, x_recv, s_send, s_recv, g_send, g_recv = take(12)
    load_sem, dqkv_sem, tg_sem = take(3)
    gq_ref = gq_buf if inside else gq_in

    me = lax.axis_index("seq")
    f = lax.axis_index("fsdp")
    z, y = f // lo, f % lo
    peer = z * lo + 1 - y
    rows, dim = tok_ref.shape
    width = xq.shape[2] // 3
    bits, slots = seq_levels(seq)

    loads = [
        pltpu.make_async_copy(src, dst, load_sem.at[i])
        for i, (src, dst) in enumerate(
            (
                (wqkv_hbm, wqkv_ref),
                (down_ref, td),
                (normed_hbm, normed_ref),
                (tok_hbm, tok_ref),
                (dmid_hbm, dmid_ref),
            )
        )
    ]
    dqkv_loads = {
        j: pltpu.make_async_copy(
            dqkv_hbm.at[pl.ds(j * rows, rows)], dqkv_ref.at[pl.ds(j * rows, rows)], dqkv_sem.at[j]
        )
        for j in range(seq)
    }
    loads[0].start()
    for j in reversed(range(seq)):
        dqkv_loads[j].start()
    for c in loads[1:]:
        c.start()

    barrier = pltpu.get_barrier_semaphore()
    for k in range(1, seq):
        pl.semaphore_signal(barrier, inc=1, device_id={"seq": me ^ k}, device_id_type=MESH)
    for k in range(1, hi):
        pl.semaphore_signal(barrier, inc=1, device_id={"fsdp": lax.rem(z + k, hi) * lo + y}, device_id_type=MESH)
    pl.semaphore_signal(barrier, inc=1, device_id={"fsdp": peer}, device_id_type=MESH)
    pl.semaphore_wait(barrier, seq + hi - 1)

    def remote(src, dst, send, recv, axis, target):
        return pltpu.make_async_remote_copy(
            src_ref=src, dst_ref=dst, send_sem=send, recv_sem=recv, device_id={axis: target}, device_id_type=MESH
        )

    def dn_copy(bit, j):
        slot = slots[bit, j]
        return remote(low.at[j ^ bit], into.at[slot], dn_send.at[slot], dn_recv.at[slot], "seq", me ^ bit)

    start, combine, zsend, zrecv, drain_y, drain_z = line_reduce(
        hi,
        lo,
        lambda i, target: gq_ref.at[:, target],
        (tq, td),
        (yq,),
        (zq, zd),
        z_send,
        z_recv,
        y_send,
        y_recv,
    )

    def exchange(k, sending):
        return remote(
            tq.at[z, me ^ k] if sending else tq.at[z, me],
            xq.at[me] if sending else xq.at[me ^ k],
            x_send.at[k],
            x_recv.at[k],
            "seq",
            me ^ k if sending else me,
        )

    small_y = remote(small_ref, sy, s_send.at[0], s_recv.at[0], "fsdp", peer)
    small_y.start()
    loads[0].wait()
    if not inside:
        start(0)

    def dn_part(j):
        part = dot_t(dqkv_ref[j * rows : (j + 1) * rows], wqkv_ref[...])
        if j % 2:
            low[j] = part.astype(bf16)
            dn_copy(1, j ^ 1).start()
        else:
            acc[...] = part

    def dn_sum(j):
        for bit in bits:
            if j & bit:
                low[j] = acc[...].astype(bf16)
                dn_copy(bit, j ^ bit).start()
                break
            dn_copy(bit, j).wait_recv()
            acc[...] += into[slots[bit, j]].astype(f32)

    for j in reversed(range(2, seq)):
        dqkv_loads[j].wait()
        dn_part(j)
        if j == seq - 1:
            loads[1].wait()
            zsend(1, 0)
        if j % 2 == 0:
            dn_sum(j)
    for j in range(min(2, seq)):
        dqkv_loads[j].wait()
    loads[2].wait()
    if inside:
        for k in range(seq):
            cols = slice(k * (dim // seq), (k + 1) * (dim // seq))
            part = t_dot(normed_ref[:, cols], dqkv_ref[...]).astype(bf16)
            gq_buf[k] = part.reshape(gq_buf.shape[1:])
        start(0)
    small_y.wait_recv()
    sz[z] = small_ref[...] + sy[...]
    small_z = []
    for k in range(1, hi):
        small_z.append(
            remote(sz.at[z], sz.at[z], s_send.at[k], s_recv.at[k], "fsdp", lax.rem(z + k, hi) * lo + y)
        )
        small_z[-1].start()
    for j in reversed(range(min(2, seq))):
        dn_part(j)
    for t in range(hi - 1):
        zrecv(1, t)
        if t + 1 < hi - 1:
            zsend(1, t + 1)
    rd_ref[...] = td[z].astype(f32)
    for c in loads[3:]:
        c.wait()
    combine(0)
    zsend(0, 0)
    for bit in bits:
        dn_copy(bit, 0).wait_recv()
    gain = gain_ref[...]
    part = jnp.zeros((8, dim), f32)
    step = 128
    for r in range(0, rows, step):
        at = slice(r, r + step)
        dn = acc[at]
        for bit in bits:
            dn = dn + into[slots[bit, 0], at].astype(f32)
        x = tok_ref[at].astype(f32)
        rho = lax.rsqrt(jnp.mean(x * x, axis=-1, keepdims=True) + EPSILON)
        scaled = gain * dn
        mean = jnp.mean(x * scaled, axis=-1, keepdims=True)
        dmid_ref[at] += rho * scaled - x * (rho * rho * rho * mean)
        prod = dn * x * rho
        part += functools.reduce(jnp.add, [prod[n : n + 8] for n in range(0, step, 8)])
    tg_store = pltpu.make_async_copy(dmid_ref, tg_ref, tg_sem)
    tg_store.start()
    gains[0:8] = mlp_gain_ref[...]
    gains[8:16] = part
    gain_y = remote(gains, gy, g_send.at[0], g_recv.at[0], "fsdp", peer)
    gain_y.start()
    zrecv(0, 0)
    if hi > 2:
        zsend(0, 1)
    gain_y.wait_recv()
    gz[z] = gains[...] + gy[...]
    gain_z = []
    for k in range(1, hi):
        gain_z.append(
            remote(gz.at[z], gz.at[z], g_send.at[k], g_recv.at[k], "fsdp", lax.rem(z + k, hi) * lo + y)
        )
        gain_z[-1].start()
    for t in range(1, hi - 1):
        zrecv(0, t)
        if t + 1 < hi - 1:
            zsend(0, t + 1)
    for k in range(1, seq):
        exchange(k, True).start()
    for k in range(1, hi):
        source = lax.rem(z + hi - k, hi)
        remote(gz.at[source], gz.at[source], g_send.at[k], g_recv.at[k], "fsdp", f).wait_recv()
        remote(sz.at[source], sz.at[source], s_send.at[k], s_recv.at[k], "fsdp", f).wait_recv()
    gs[me] = functools.reduce(jnp.add, [gz[d] for d in range(hi)])
    gain_x = []
    for k in range(1, seq):
        gain_x.append(remote(gs.at[me], gs.at[me], g_send.at[hi + k], g_recv.at[hi + k], "seq", me ^ k))
        gain_x[-1].start()
    total = functools.reduce(jnp.add, [sz[d] for d in range(hi)])
    cut, heads = dquery_ref.shape[0], gate_ref.shape[0]
    dquery_ref[...] = total[:cut]
    gate_ref[...] = total[cut : cut + heads]
    table_ref[...] = total[cut + heads : cut + 2 * heads, :BUCKETS]
    xq[me] = tq[z, me]
    for k in range(1, seq):
        exchange(k, False).wait_recv()
    write_parts(rq_ref, xq, seq, width)
    for k in range(1, seq):
        remote(gs.at[me ^ k], gs.at[me ^ k], g_send.at[hi + k], g_recv.at[hi + k], "seq", me).wait_recv()
    total = functools.reduce(jnp.add, [gs[k] for k in range(seq)])
    piece = again_ref.shape[1]
    total = pltpu.roll(total, lax.rem(dim - (me * hi * lo + f) * piece, dim), 1)[:, :DH]
    mgain_ref[...] = jnp.sum(total[0:8], axis=0, keepdims=True)[:, :piece]
    again_ref[...] = jnp.sum(total[8:16], axis=0, keepdims=True)[:, :piece]

    for bit in bits:
        for j in range(0, seq, 2 * bit):
            dn_copy(bit, j).wait_send()
    drain_y(0)
    for i in range(2):
        drain_z(i)
    for k in range(1, seq):
        exchange(k, True).wait_send()
    for c in [small_y, gain_y] + small_z + gain_z + gain_x:
        c.wait_send()
    tg_store.wait()


def finish(dqkv, wqkv, normed, down, small, mlp_gain, tok, dmid, gain, seq, fsdp):
    lo = 2
    hi = fsdp // lo
    rows, dim = tok.shape
    width3 = dqkv.shape[1]
    piece = dim // (seq * fsdp)
    inside = piece % 16 == 0
    heads = width3 // (3 * DH)
    vmem = pl.BlockSpec(memory_space=pltpu.VMEM)
    anywhere = pl.BlockSpec(memory_space=pl.ANY)
    dma = pltpu.SemaphoreType.DMA

    def buf(*shape):
        return pltpu.VMEM(shape, bf16)

    extra = []
    if not inside:
        extra.append(t_dot(normed, dqkv).astype(bf16).reshape(seq, fsdp, piece, width3))
    scratch = [
        buf(*dqkv.shape),
        buf(*wqkv.shape),
        buf(*normed.shape),
        buf(rows, dim),
        pltpu.VMEM((rows, dim), f32),
        buf(seq, rows, dim),
        buf(max(seq - 1, 1), rows, dim),
        pltpu.VMEM((rows, dim), f32),
        buf(seq, fsdp, piece, width3) if inside else buf(16, 128),
        buf(hi, seq, piece, width3),
        buf(*down.shape),
        buf(hi, seq, piece, width3),
        buf(2, max(hi - 1, 1), seq, piece, width3),
        buf(2, max(hi - 1, 1), *down.shape[1:]),
        buf(seq, piece, width3),
        pltpu.VMEM(small.shape, f32),
        pltpu.VMEM((hi,) + small.shape, f32),
        pltpu.VMEM((16, dim), f32),
        pltpu.VMEM((16, dim), f32),
        pltpu.VMEM((hi, 16, dim), f32),
        pltpu.VMEM((seq, 16, dim), f32),
        dma((seq,)),
        dma((seq,)),
        dma((2, 2, hi)),
        dma((2, 2, hi)),
        dma((1, hi)),
        dma((1, hi)),
        dma((seq,)),
        dma((seq,)),
        dma((hi,)),
        dma((hi,)),
        dma((hi + seq,)),
        dma((hi + seq,)),
        dma((5,)),
        dma((seq,)),
        dma,
    ]
    return pl.pallas_call(
        functools.partial(finish_kernel, seq, hi, lo, inside),
        out_shape=(
            jax.ShapeDtypeStruct((rows, dim), f32),
            jax.ShapeDtypeStruct((piece, seq * width3), f32),
            jax.ShapeDtypeStruct(down.shape[1:], f32),
            jax.ShapeDtypeStruct((heads * DH, DH), f32),
            jax.ShapeDtypeStruct((heads, DH), f32),
            jax.ShapeDtypeStruct((heads, BUCKETS), f32),
            jax.ShapeDtypeStruct((1, piece), f32),
            jax.ShapeDtypeStruct((1, piece), f32),
        ),
        in_specs=[anywhere] * 4 + [vmem] * 2 + [anywhere] * 2 + [vmem] * (1 + len(extra)),
        out_specs=(anywhere,) + (vmem,) * 7,
        scratch_shapes=scratch,
        compiler_params=pltpu.CompilerParams(
            collective_id=1, has_side_effects=True, vmem_limit_bytes=60 << 20
        ),
        name="finish",
    )(dqkv, wqkv, normed, down, small, mlp_gain, tok, dmid, gain, *extra)


GELU_P = 0.24
GELU_C = (
    0.08951261885080208,
    0.15562094398234086,
    -0.15437154502074169,
    0.6261054138112487,
    -0.6465313024138201,
    0.5547927291245551,
    -0.125128858665134,
)


def gelu_parts(x):
    size = jnp.abs(x)
    t = 1.0 / (1.0 + GELU_P * size)
    poly = GELU_C[-1] * t
    for c in GELU_C[-2::-1]:
        poly = (poly + c) * t
    bell = jnp.exp2(x * x * (-0.5 * LOG2E))
    tail = poly * bell
    cdf = jnp.where(x < 0.0, tail, 1.0 - tail)
    return x * cdf, cdf + x * bell * (1.0 / math.sqrt(2.0 * math.pi))


def mlp_kernel(seq, sub, length_ref, *refs):
    refs = list(refs)

    def take(count):
        taken = refs[:count]
        del refs[:count]
        return taken

    own_ref, others_ref, tok_ref, grads_ref, wo_hbm, wu_hbm, wd_hbm, gain_ref = take(8)
    mid_out, dmid_out, gsum_ref, db_ref, mo_ref, ug_out, dg_out = take(7)
    att_refs = [own_ref] + [others_ref.at[k] for k in range(1, seq)]
    att_buf, tok_buf, wo_ref, wu_ref, wd_ref, gm, nm, hid, dpre, low, into, acc, mid_ref, ug_ref, dg_ref = take(15)
    load_sem, w_sem, gm_sem, dn_send, dn_recv, db_send, db_recv, mo_sem, own_sem = take(9)
    dbv = low.at[0]
    depth = att_buf.shape[0]

    me = lax.axis_index("seq")
    length = length_ref[0]
    dim = wo_ref.shape[0]
    width = dim // seq
    rows = tok_ref.shape[1]
    share = wu_ref.shape[1]
    subs = rows // sub
    bits, slots = seq_levels(seq)
    order = list(reversed(range(seq)))

    def chunk_loads(j):
        slot = j % depth
        copies = [
            pltpu.make_async_copy(att_refs[k].at[pl.ds(j * rows, rows)], att_buf.at[slot, k], load_sem.at[slot, k])
            for k in range(seq)
        ]
        copies.append(pltpu.make_async_copy(tok_ref.at[j], tok_buf.at[slot], load_sem.at[slot, seq]))
        return copies

    gm_loads = {
        j: pltpu.make_async_copy(grads_ref.at[j], gm.at[pl.ds(j * rows, rows)], gm_sem.at[j]) for j in order
    }
    weights = [
        pltpu.make_async_copy(src, dst, w_sem.at[i])
        for i, (src, dst) in enumerate(((wo_hbm, wo_ref), (wu_hbm, wu_ref), (wd_hbm, wd_ref)))
    ]
    for c in chunk_loads(order[0]) + weights[:1] + (chunk_loads(order[1]) if seq > 1 else []) + weights[1:]:
        c.start()
    for j in order:
        gm_loads[j].start()
    if depth == seq:
        for j in order[2:]:
            for c in chunk_loads(j):
                c.start()

    barrier = pltpu.get_barrier_semaphore()
    for bit in bits:
        pl.semaphore_signal(barrier, inc=1, device_id={"seq": me ^ bit}, device_id_type=MESH)
    pl.semaphore_wait(barrier, len(bits))

    def dn_copy(bit, j, s):
        slot = slots[bit, j]
        at = pl.ds(pl.multiple_of(s * sub, sub), sub)
        return pltpu.make_async_remote_copy(
            src_ref=low.at[j ^ bit, at],
            dst_ref=into.at[slot, at],
            send_sem=dn_send.at[slot, s],
            recv_sem=dn_recv.at[slot, s],
            device_id={"seq": me ^ bit},
            device_id_type=MESH,
        )

    gain = gain_ref[...]

    def forward(j, s):
        slot = j % depth
        at = pl.ds(pl.multiple_of(s * sub, sub), sub)
        here = pl.ds(pl.multiple_of(j * rows + s * sub, sub), sub)
        position = (j ^ me) * rows + s * sub + lax.broadcasted_iota(jnp.int32, (sub, 1), 0)
        live = jnp.where(position < length, 1.0, 0.0)
        masked = (gm[here].astype(f32) * live).astype(bf16)
        gm[here] = masked
        mid = tok_buf[slot, at].astype(f32)
        for k in range(seq):
            own = pl.ds(pl.multiple_of((me ^ k) * width, width), width)
            mid = mid + dot(att_buf[slot, k, at], wo_ref[own])
        rho = lax.rsqrt(jnp.mean(mid * mid, axis=-1, keepdims=True) + EPSILON)
        normed = (mid * rho * gain).astype(bf16)
        nm[here] = normed
        if j == 0:
            mid_ref[at] = mid
        for c in range(0, share, 256):
            cols = slice(c, c + 256)
            value, slope = gelu_parts(dot(normed, wu_ref[:, cols]))
            hid[here, cols] = value.astype(bf16)
            dpre[here, cols] = (dot_t(masked, wd_ref[cols]) * slope).astype(bf16)
        part = dot_t(dpre[here], wu_ref[...])
        if j % 2:
            low[j, at] = part.astype(bf16)
            dn_copy(1, j ^ 1, s).start()
        else:
            acc[at] = part

    def settle(j, s):
        at = pl.ds(pl.multiple_of(s * sub, sub), sub)
        for bit in bits:
            if j & bit:
                low[j, at] = acc[at].astype(bf16)
                dn_copy(bit, j ^ bit, s).start()
                break
            dn_copy(bit, j, s).wait_recv()
            acc[at] += into[slots[bit, j], at].astype(f32)

    for c in weights:
        c.wait()
    for n in range(0, seq, 2):
        pair = order[n : n + 2]
        if n and depth < seq:
            for j in pair:
                for c in chunk_loads(j):
                    c.start()
        for j in pair:
            for c in chunk_loads(j):
                c.wait()
            gm_loads[j].wait()

        @pl.loop(0, subs)
        def _(s):
            for j in pair:
                forward(j, s)
            if pair[-1]:
                settle(pair[-1], s)

    stores = [pltpu.make_async_copy(mid_ref, mid_out, own_sem.at[1])]
    stores[0].start()
    for c in range(0, dim, 256):
        ug_ref[c : c + 256] = t_dot(nm[:, c : c + 256], dpre[...]).astype(bf16)
    stores.append(pltpu.make_async_copy(ug_ref, ug_out, own_sem.at[2]))
    stores[-1].start()

    def db_copy(source, target, bit, s):
        at = pl.ds(s * sub, sub)
        return pltpu.make_async_remote_copy(
            src_ref=db_ref.at[source, at] if source else dbv.at[at],
            dst_ref=db_ref.at[target, at],
            send_sem=db_send.at[target, s],
            recv_sem=db_recv.at[target, s],
            device_id={"seq": me ^ bit},
            device_id_type=MESH,
        )

    sends = []
    high = [bit for bit in reversed(bits) if bit > 1]

    def send(source, target, bit, s):
        sends.append(db_copy(source, target, bit, s))
        sends[-1].start()

    step = 128
    part = jnp.zeros((8, dim), f32)
    for s in range(subs):
        for bit in bits:
            dn_copy(bit, 0, s).wait_recv()
        for r in range(s * sub, (s + 1) * sub, step):
            at = slice(r, r + step)
            dn = acc[at]
            for bit in bits:
                dn = dn + into[slots[bit, 0], at].astype(f32)
            mid = mid_ref[at]
            rho = lax.rsqrt(jnp.mean(mid * mid, axis=-1, keepdims=True) + EPSILON)
            scaled = gain * dn
            mean = jnp.mean(mid * scaled, axis=-1, keepdims=True)
            dmid = gm[at].astype(f32) + rho * scaled - mid * (rho * rho * rho * mean)
            acc[at] = dmid
            dbv[at] = dmid.astype(bf16)
            prod = dn * mid * rho
            part += functools.reduce(jnp.add, [prod[i : i + 8] for i in range(0, step, 8)])
        if high:
            send(0, high[0], high[0], s)
        if seq > 1:
            send(0, 1, 1, s)
    gsum_ref[...] = part
    stores.append(pltpu.make_async_copy(dbv, db_ref.at[0], own_sem.at[0]))
    stores[-1].start()
    stores.append(pltpu.make_async_copy(acc, dmid_out, own_sem.at[3]))
    stores[-1].start()
    for c in range(0, share, 256):
        dg_ref[c : c + 256] = t_dot(hid[:, c : c + 256], gm[...]).astype(bf16)
    stores.append(pltpu.make_async_copy(dg_ref, dg_out, own_sem.at[4]))
    stores[-1].start()
    for j in range(seq):
        at = slice(j * rows, (j + 1) * rows)
        nm[at] = dot(hid[at], wd_ref[...]).astype(bf16)
        stores.append(pltpu.make_async_copy(nm.at[pl.ds(j * rows, rows)], mo_ref.at[j], mo_sem.at[j]))
        stores[-1].start()
    have = [0]
    for n, bit in enumerate(high):
        if n:
            for j in have:
                for s in range(subs):
                    send(j, j ^ bit, bit, s)
        for j in have:
            for s in range(subs):
                db_copy(0, j ^ bit, bit, s).wait_recv()
                send(j ^ bit, j ^ bit ^ 1, 1, s)
        have += [j ^ bit for j in have]
    if seq > 1:
        for j in have:
            for s in range(subs):
                db_copy(0, j ^ 1, 1, s).wait_recv()
    for c in sends:
        c.wait_send()
    for c in stores:
        c.wait()
    for bit in bits:
        for j in range(0, seq, 2 * bit):
            for s in range(subs):
                dn_copy(bit, j, s).wait_send()


def mlp(length, own, others, tok, grads, wo, wu, wd, gain):
    seq, rows, dim = tok.shape
    share = wu.shape[1]
    sub = 256
    depth = seq if seq <= 4 else 2
    anywhere = pl.BlockSpec(memory_space=pl.ANY)
    vmem = pl.BlockSpec(memory_space=pltpu.VMEM)
    dma = pltpu.SemaphoreType.DMA

    def buf(*shape):
        return pltpu.VMEM(shape, bf16)

    return pl.pallas_call(
        functools.partial(mlp_kernel, seq, sub),
        out_shape=(
            jax.ShapeDtypeStruct((rows, dim), f32),
            jax.ShapeDtypeStruct((rows, dim), f32),
            jax.ShapeDtypeStruct((8, dim), f32),
            jax.ShapeDtypeStruct((seq, rows, dim), bf16),
            jax.ShapeDtypeStruct((seq, rows, dim), bf16),
            jax.ShapeDtypeStruct((dim, share), bf16),
            jax.ShapeDtypeStruct((share, dim), bf16),
        ),
        in_specs=[pl.BlockSpec(memory_space=pltpu.SMEM)] + [anywhere] * 7 + [vmem],
        out_specs=(anywhere, anywhere, vmem, anywhere, anywhere, anywhere, anywhere),
        scratch_shapes=[
            buf(depth, seq, rows, dim // seq),
            buf(depth, rows, dim),
            buf(dim, dim),
            buf(dim, share),
            buf(share, dim),
            buf(seq * rows, dim),
            buf(seq * rows, dim),
            buf(seq * rows, share),
            buf(seq * rows, share),
            buf(seq, rows, dim),
            buf(max(seq - 1, 1), rows, dim),
            pltpu.VMEM((rows, dim), f32),
            pltpu.VMEM((rows, dim), f32),
            buf(dim, share),
            buf(share, dim),
            dma((depth, seq + 1)),
            dma((3,)),
            dma((seq,)),
            dma((seq, rows // sub)),
            dma((seq, rows // sub)),
            dma((seq, rows // sub)),
            dma((seq, rows // sub)),
            dma((seq,)),
            dma((5,)),
        ],
        compiler_params=pltpu.CompilerParams(collective_id=2, has_side_effects=True, vmem_limit_bytes=62 << 20),
        cost_estimate=pl.CostEstimate(
            flops=2 * rows * seq * dim * (dim + 6 * share), bytes_accessed=32 << 20, transcendentals=rows * seq * share
        ),
        name="mlp",
    )(length, own, others, tok, grads, wo, wu, wd, gain)


def inverse_rms(values):
    return lax.rsqrt(jnp.mean(values * values, axis=-1, keepdims=True) + EPSILON)


def norm_back(values, gain, rho, grad):
    scaled = gain * grad
    mean = jnp.mean(values * scaled, axis=-1, keepdims=True)
    gain_grad = (grad * values * rho).reshape(-1, 8, values.shape[1])
    return rho * scaled - values * (rho * rho * rho * mean), jnp.sum(gain_grad, axis=0)


def body(
    tokens,
    lengths,
    state_init,
    w_qkv,
    w_out,
    w_up,
    w_down,
    norm_attn,
    norm_mlp,
    rel_bias,
    state_query,
    gate_bias,
    out_grad,
    state_grad,
):
    seq_count = lax.axis_size("seq")
    fsdp_count = lax.axis_size("fsdp")
    seq_at = lax.axis_index("seq")
    heads = H // seq_count
    width = heads * DH
    tok_rows, dim = tokens.shape[1:]
    rows = tok_rows * seq_count
    hidden_all = w_up.shape[1]
    share = hidden_all // (seq_count * fsdp_count)

    piece = dim // (seq_count * fsdp_count)
    all_tokens, all_grad, qkv_w, gain_attn, gain_mlp, own_out, up_w = gather_start(
        tokens[0],
        out_grad[0],
        w_qkv,
        norm_attn.reshape(1, -1),
        norm_mlp.reshape(1, -1),
        w_out.reshape(2, w_out.shape[0] // 2, dim),
        w_up,
        seq_count,
        fsdp_count,
    )
    qkv_w = qkv_w.reshape(dim, 3 * width)
    up_w = up_w.reshape(dim, hidden_all // seq_count)
    gain_attn = gain_attn.reshape(dim).astype(f32)
    gain_mlp = gain_mlp.reshape(dim).astype(f32)
    own_down = lax.dynamic_slice_in_dim(w_down, seq_at * share, share, axis=0)

    bias = bias_vector(rel_bias)
    forget = jax.nn.sigmoid(gate_bias)
    forget_row = forget.reshape(1, width)

    inputs = all_tokens.reshape(rows, dim).astype(f32)
    normed = (inputs * inverse_rms(inputs) * gain_attn).astype(bf16)
    qkv = dot(normed, qkv_w).astype(bf16)
    attended, others, out_w, down_w, final_memory, mem, upd, lse, slse = attend(
        qkv,
        state_init[0],
        lengths,
        state_query,
        forget_row,
        bias,
        own_out,
        own_down,
        heads,
        seq_count,
        fsdp_count,
    )
    out_w = out_w.reshape(dim, dim)
    down_w = down_w.reshape(fsdp_count * share, dim)
    own_out = lax.dynamic_slice_in_dim(out_w, seq_at * width, width, axis=0)
    mid_here, dmid, mlp_gain_grad, dbranch, mlp_parts, up_grad, down_grad = mlp(
        lengths, attended, others, all_tokens, all_grad, out_w, up_w, down_w, gain_mlp.reshape(1, dim)
    )
    span = fsdp_count // seq_count
    dqkv, small, up_part, down_total, out_part, output = attend_back(
        qkv,
        dbranch.reshape(rows, dim),
        own_out,
        attended,
        mem,
        upd,
        lse,
        slse,
        state_grad[0],
        lengths,
        state_query,
        forget_row,
        bias,
        up_grad.reshape(seq_count, fsdp_count, piece, hidden_all // seq_count),
        down_grad.reshape(seq_count, span * share, dim),
        mlp_parts,
        mid_here,
        seq_count,
        fsdp_count,
    )
    tokens_grad, qkv_part, down_part, dquery, grad_gate, grad_table, attn_gain_grad, mlp_gain_grad = finish(
        dqkv,
        qkv_w,
        normed,
        down_total,
        small,
        mlp_gain_grad,
        tokens[0],
        dmid,
        gain_attn.reshape(1, dim),
        seq_count,
        fsdp_count,
    )
    output = output[None]
    tokens_grad = tokens_grad[None]
    dquery = dquery.reshape(heads, DH, DH)
    attn_gain_grad = attn_gain_grad.reshape(piece)
    mlp_gain_grad = mlp_gain_grad.reshape(piece)
    if up_part.ndim == 3:
        up_part = up_part.reshape(seq_count, piece, fsdp_count, share)
        up_part = jnp.transpose(up_part, (1, 2, 0, 3)).reshape(piece, hidden_all)
    return (
        output,
        final_memory[None],
        tokens_grad,
        qkv_part,
        out_part,
        up_part,
        down_part,
        attn_gain_grad,
        mlp_gain_grad,
        grad_table,
        dquery,
        grad_gate,
    )


def solution(mesh):
    placed = (
        P("fsdp", "seq", None),
        P("fsdp"),
        P("fsdp", None, "seq"),
        P("fsdp", None),
        P("fsdp", None),
        P("fsdp", None),
        P("fsdp", None),
        P("fsdp"),
        P("fsdp"),
        P("seq", None),
        P("seq", None, None),
        P("seq", None),
        P("fsdp", "seq", None),
        P("fsdp", None, "seq"),
    )
    return jax.shard_map(
        body,
        mesh=mesh,
        in_specs=placed,
        out_specs=(
            P("fsdp", "seq", None),
            P("fsdp", None, "seq"),
            P("fsdp", "seq", None),
            P(("seq", "fsdp"), None),
            P(("seq", "fsdp"), None),
            P(("seq", "fsdp"), None),
            P(("seq", "fsdp"), None),
            P(("seq", "fsdp")),
            P(("seq", "fsdp")),
            P("seq", None),
            P("seq", None, None),
            P("seq", None),
        ),
        check_vma=False,
    )
```

```python
import functools
import math

import jax
import jax.numpy as jnp
import numpy as np
from jax import lax
from jax.experimental import pallas as pl
from jax.experimental.pallas import tpu as pltpu
from jax.sharding import PartitionSpec as P

H = 8
DH = 128
BLOCK = 512
STATE_VECTORS = 512
QTILE = 256
SPAN = BLOCK + QTILE

EPSILON = 1e-06
BUCKET_EDGES = (19, 21, 24, 27, 31, 35, 40, 46, 52, 59, 67, 77, 87, 99, 113)
BUCKETS = 32
LOG2E = math.log2(math.e)
SCALE = DH ** (-0.5)
NEAR = 384

f32 = jnp.float32
bf16 = jnp.bfloat16
MESH = pl.DeviceIdType.MESH


def bucket_of(distance):
    return np.minimum(distance, 16) + (distance[..., None] >= np.array(BUCKET_EDGES)).sum(-1)


def tile_distance():
    rows = np.arange(QTILE)[:, None]
    cols = np.arange(SPAN)[None, :]
    return rows + BLOCK - cols


def bias_vector(table):
    distance = BLOCK - np.arange(2 * BLOCK)
    inside = (distance >= 0) & (distance < BLOCK)
    bucket = jnp.asarray(np.where(inside, bucket_of(np.clip(distance, 0, BLOCK)), BUCKETS).astype(np.int32))
    total = jnp.full((table.shape[0], 2 * BLOCK), -jnp.inf, f32)
    for i in range(BUCKETS):
        total = jnp.where((bucket == i)[None], table[:, i : i + 1] * LOG2E, total)
    return total


def tile_bias(vector_ref, head):
    wide = jnp.broadcast_to(vector_ref[head : head + 1, :], (QTILE, 2 * BLOCK))
    return pltpu.roll(wide, 0, 1, stride=1, stride_axis=0)[:, :SPAN]


def dot(a, b):
    return jnp.dot(a, b, preferred_element_type=f32)


def dot_t(a, b):
    return lax.dot_general(a, b, (((1,), (1,)), ((), ())), preferred_element_type=f32)


def t_dot(a, b):
    return lax.dot_general(a, b, (((0,), (0,)), ((), ())), preferred_element_type=f32)


def to_row(column):
    wide = jnp.broadcast_to(column, (column.shape[0], 128))
    return wide.T[0:1, :]


def context_pieces(tile):
    start = tile * QTILE
    pieces = []
    if start < BLOCK:
        pieces.append((0, start, BLOCK, 0))
    pieces.append((1, 0, start + QTILE, BLOCK - start))
    return pieces


def softmax_parts(scores):
    top = functools.reduce(jnp.maximum, [jnp.max(s, axis=-1, keepdims=True) for s in scores])
    raised = [jnp.exp2(s - top) for s in scores]
    total = functools.reduce(jnp.add, [jnp.sum(e, axis=-1, keepdims=True) for e in raised])
    return raised, total, top + jnp.log2(total)


def line_gather(hi, lo, slot, own, z_send, z_recv, y_send, y_recv):
    f = lax.axis_index("fsdp")
    z, y = f // lo, f % lo

    def copy(i, origin, target, send, recv, first=False):
        ref = slot(i, origin)
        return pltpu.make_async_remote_copy(
            src_ref=own(i) if first else ref,
            dst_ref=ref,
            send_sem=send,
            recv_sem=recv,
            device_id={"fsdp": target},
            device_id_type=MESH,
        )

    def right(i, t):
        return copy(i, (z - t) * lo + y, (z + 1) * lo + y, z_send.at[i, 0, t], z_recv.at[i, 0, t], t == 0)

    def left(i, t):
        return copy(i, (z + t) * lo + y, (z - 1) * lo + y, z_send.at[i, 1, t], z_recv.at[i, 1, t], t == 0)

    def across(i, d):
        return copy(
            i, (z + d) * lo + y, z * lo + 1 - y, y_send.at[i, d + hi - 1], y_recv.at[i, d + hi - 1], d == 0
        )

    def start(i):
        pl.when(z + 1 < hi)(lambda: right(i, 0).start())
        pl.when(z >= 1)(lambda: left(i, 0).start())
        across(i, 0).start()

    def step(i, t):
        @pl.when(z - 1 - t >= 0)
        def _():
            copy(i, (z - 1 - t) * lo + y, f, z_send.at[i, 0, t], z_recv.at[i, 0, t]).wait_recv()
            if t + 1 < hi - 1:
                pl.when(z + 1 < hi)(lambda: right(i, t + 1).start())
            across(i, -1 - t).start()

        @pl.when(z + 1 + t < hi)
        def _():
            copy(i, (z + 1 + t) * lo + y, f, z_send.at[i, 1, t], z_recv.at[i, 1, t]).wait_recv()
            if t + 1 < hi - 1:
                pl.when(z >= 1)(lambda: left(i, t + 1).start())
            across(i, 1 + t).start()

    def arrive(i):
        for d in range(1 - hi, hi):

            @pl.when((z + d >= 0) & (z + d < hi))
            def _():
                copy(
                    i, (z + d) * lo + 1 - y, f, y_send.at[i, d + hi - 1], y_recv.at[i, d + hi - 1]
                ).wait_recv()

    def drain(i):
        for d in range(1 - hi, hi):

            @pl.when((z + d >= 0) & (z + d < hi))
            def _():
                across(i, d).wait_send()

        for t in range(hi - 1):

            @pl.when((z + 1 < hi) & (z - t >= 0))
            def _():
                right(i, t).wait_send()

            @pl.when((z >= 1) & (z + t < hi))
            def _():
                left(i, t).wait_send()

    return start, step, arrive, drain


def line_sems(count, hi):
    dma = pltpu.SemaphoreType.DMA
    return [dma((count, 2, hi)), dma((count, 2, hi)), dma((count, 2 * hi)), dma((count, 2 * hi))]


def greet(seq_targets, hi, lo):
    me = lax.axis_index("seq")
    f = lax.axis_index("fsdp")
    z, y = f // lo, f % lo
    barrier = pltpu.get_barrier_semaphore()
    for k in seq_targets:
        pl.semaphore_signal(barrier, inc=1, device_id={"seq": me ^ k}, device_id_type=MESH)
    near = (lax.rem(z + 1, hi) * lo + y, lax.rem(z + hi - 1, hi) * lo + y, z * lo + 1 - y)
    for target in near:
        pl.semaphore_signal(barrier, inc=1, device_id={"fsdp": target}, device_id_type=MESH)
    pl.semaphore_wait(barrier, len(seq_targets) + len(near))


def attend_kernel(
    heads,
    seq,
    hi,
    lo,
    length_ref,
    qkv_ref,
    init_ref,
    query_ref,
    forget_ref,
    vector_ref,
    own_out_ref,
    down_hbm,
    att_out,
    others_ref,
    outs_ref,
    downs_ref,
    final_ref,
    mem_out,
    upd_out,
    lse_ref,
    slse_ref,
    memory_ref,
    bias_ref,
    att_ref,
    mem_ref,
    upd_ref,
    down_ref,
    store_sem,
    own_sem,
    att_send,
    att_recv,
    out_send,
    out_recv,
    z_send,
    z_recv,
    y_send,
    y_recv,
):
    me = lax.axis_index("seq")
    f = lax.axis_index("fsdp")
    length = length_ref[0]
    width = heads * DH
    scale2 = SCALE * LOG2E
    blocks = seq
    bits = [1 << i for i in range(seq.bit_length() - 1)]
    z, y = f // lo, f % lo
    parts = 4
    held = down_ref.shape[0]
    part_rows = held // parts
    planes = downs_ref.shape[0] // (held * lo)
    down_load = pltpu.make_async_copy(down_hbm, down_ref, own_sem.at[0])
    down_load.start()
    greet(bits, hi, lo)

    own_copies = [pltpu.make_async_copy(own_out_ref, outs_ref.at[:, me % 2], own_sem.at[1])]
    own_copies[0].start()

    def down_rows(q, column, c):
        return pl.ds(pl.multiple_of((q * lo + column) * held + c * part_rows, part_rows), part_rows)

    def down_copy(q, c, target, send, recv, own):
        at = down_rows(q, y, c)
        own_at = pl.ds(pl.multiple_of(c * part_rows, part_rows), part_rows)
        return pltpu.make_async_remote_copy(
            src_ref=down_ref.at[own_at] if own else downs_ref.at[at],
            dst_ref=downs_ref.at[at],
            send_sem=send,
            recv_sem=recv,
            device_id={"fsdp": target},
            device_id_type=MESH,
        )

    def down_sends(q, c, own):
        plane = me * planes + q
        rightward = (z + 1 < hi) & (z >= plane)
        leftward = (z >= 1) & (z <= plane)
        return (
            (rightward, down_copy(q, c, (z + 1) * lo + y, z_send.at[q, 0, c], z_recv.at[q, c], own)),
            (leftward, down_copy(q, c, (z - 1) * lo + y, z_send.at[q, 1, c], z_recv.at[q, c], own)),
            (z >= 0, down_copy(q, c, z * lo + 1 - y, y_send.at[q, c], y_recv.at[q, c], own)),
        )

    def down_start(q):
        @pl.when(z == me * planes + q)
        def _():
            for c in range(parts):
                for cond, copy in down_sends(q, c, True):
                    pl.when(cond)(copy.start)

    def down_step(q, point):
        far = jnp.abs(z - (me * planes + q))
        c = point - far + 1

        @pl.when((far >= 1) & (c >= 0) & (c < parts))
        def _():
            down_copy(q, c, f, z_send.at[q, 0, c], z_recv.at[q, c], False).wait_recv()
            for cond, copy in down_sends(q, c, False):
                pl.when(cond)(copy.start)

    def down_arrive(q):
        for c in range(parts):
            pltpu.make_async_remote_copy(
                src_ref=downs_ref.at[down_rows(q, 1 - y, c)],
                dst_ref=downs_ref.at[down_rows(q, 1 - y, c)],
                send_sem=y_send.at[q, c],
                recv_sem=y_recv.at[q, c],
                device_id={"fsdp": f},
                device_id_type=MESH,
            ).wait_recv()

    def down_drain(q):
        for c in range(parts):
            for cond, copy in down_sends(q, c, False):
                pl.when(cond)(copy.wait_send)

    def down_store(q):
        at = pl.ds(pl.multiple_of((q * lo + y) * held, held), held)
        return pltpu.make_async_copy(down_ref, downs_ref.at[at], own_sem.at[2])

    def lowest(k):
        return k & -k

    def out_copy(sending):
        half = me % 2 if sending else 1 - me % 2
        return pltpu.make_async_remote_copy(
            src_ref=own_out_ref,
            dst_ref=outs_ref.at[:, half],
            send_sem=out_send,
            recv_sem=out_recv,
            device_id={"seq": me ^ 1},
            device_id_type=MESH,
        )

    def att_copy(k, b):
        bit = lowest(k)
        came = k ^ bit
        here = pl.ds(pl.multiple_of((b ^ me) * BLOCK, BLOCK), BLOCK)
        there = pl.ds(pl.multiple_of((b ^ me ^ bit) * BLOCK, BLOCK), BLOCK)
        src = others_ref.at[came, here] if came else att_ref.at[here]
        return pltpu.make_async_remote_copy(
            src_ref=src,
            dst_ref=others_ref.at[k, there],
            send_sem=att_send.at[k, b],
            recv_sem=att_recv.at[k, b],
            device_id={"seq": me ^ bit},
            device_id_type=MESH,
        )

    def att_arrival(k, b):
        here = pl.ds(pl.multiple_of((b ^ me) * BLOCK, BLOCK), BLOCK)
        return pltpu.make_async_remote_copy(
            src_ref=others_ref.at[k, here],
            dst_ref=others_ref.at[k, here],
            send_sem=att_send.at[k, b],
            recv_sem=att_recv.at[k, b],
            device_id={"seq": me},
            device_id_type=MESH,
        )

    passing = sorted([k for k in range(2, seq, 2)], key=lambda k: (bin(k).count("1"), -k))

    def onward(k, send):
        for bit in reversed(bits):
            if bit < lowest(k):
                send(k | bit)

    down_load.wait()
    for q in range(planes):
        down_start(q)
        pl.when(z == me * planes + q)(lambda: down_store(q).start())
    out_copy(True).start()
    memory_ref[...] = init_ref[...].astype(f32)
    for head in range(heads):
        bias_ref[head] = tile_bias(vector_ref, head)

    def block_stores(block):
        at = pl.ds(pl.multiple_of((block ^ me) * BLOCK, BLOCK), BLOCK)
        pairs = (
            (att_ref.at[at], att_out.at[at]),
            (mem_ref.at[block], mem_out.at[block]),
            (upd_ref.at[block], upd_out.at[block]),
        )
        return [pltpu.make_async_copy(a, b, store_sem.at[i, block]) for i, (a, b) in enumerate(pairs)]

    @pl.loop(0, blocks)
    def _(block):
        cur_at = pl.multiple_of((block ^ me) * BLOCK, BLOCK)
        prev_at = pl.multiple_of((jnp.maximum(block - 1, 0) ^ me) * BLOCK, BLOCK)
        cur_ref = qkv_ref.at[pl.ds(cur_at, BLOCK)]
        prev_ref = qkv_ref.at[pl.ds(prev_at, BLOCK)]
        live_block = block * BLOCK < length
        for head in range(heads):
            for q in range(planes):
                pl.when(block * heads + head >= 1)(lambda: down_step(q, block * heads + head - 1))
            own = slice(head * DH, (head + 1) * DH)
            memory = memory_ref[:, own]
            low = memory.astype(bf16)
            mem_ref[block, :, own] = memory
            refs = (prev_ref, cur_ref)
            key_cols = slice(width + head * DH, width + (head + 1) * DH)
            value_cols = slice(2 * width + head * DH, 2 * width + (head + 1) * DH)
            for tile in range(BLOCK // QTILE):
                rows = slice(tile * QTILE, (tile + 1) * QTILE)
                query = cur_ref[rows, own]
                scores, values = [], []
                for which, at, end, col in context_pieces(tile):
                    s = dot_t(query, refs[which][at:end, key_cols])
                    position = (block - 1 + which) * BLOCK + at + lax.broadcasted_iota(jnp.int32, (1, end - at), 1)
                    live = (position >= 0) & (position < length)
                    s = s * scale2 + bias_ref[head, :, col : col + end - at]
                    scores.append(jnp.where(live, s, -jnp.inf))
                    values.append(refs[which][at:end, value_cols])
                scores.append(dot_t(query, low) * scale2)
                values.append(low)
                raised, total, lse = softmax_parts(scores)
                out = functools.reduce(jnp.add, [dot(e.astype(bf16), v) for e, v in zip(raised, values)])
                att_ref[pl.ds(cur_at + tile * QTILE, QTILE), own] = (out / total).astype(bf16)
                lse_ref[head : head + 1, pl.ds(pl.multiple_of(block * BLOCK, BLOCK) + tile * QTILE, QTILE)] = to_row(lse)
            own_key = cur_ref[:, key_cols]
            own_value = cur_ref[:, value_cols]
            squeries = dot(low, query_ref[head]).astype(bf16)
            position = block * BLOCK + lax.broadcasted_iota(jnp.int32, (1, BLOCK), 1)
            for tile in range(STATE_VECTORS // QTILE):
                rows = slice(tile * QTILE, (tile + 1) * QTILE)
                squery = squeries[rows]
                scores = [
                    dot_t(squery, low) * scale2,
                    jnp.where(position < length, dot_t(squery, own_key) * scale2, -jnp.inf),
                ]
                raised, total, lse = softmax_parts(scores)
                update = dot(raised[0].astype(bf16), low) + dot(raised[1].astype(bf16), own_value)
                update = update / total
                upd_ref[block, rows, own] = update
                slse_ref[head : head + 1, pl.ds(pl.multiple_of(block * BLOCK, BLOCK) + tile * QTILE, QTILE)] = to_row(
                    lse
                )
                forget = forget_ref[:, own]
                old = memory[rows]
                memory_ref[rows, own] = jnp.where(live_block, forget * old + (1.0 - forget) * update, old)

        for bit in reversed(bits):
            att_copy(bit, block).start()
        for c in block_stores(block):
            c.start()

        @pl.when(block >= 1)
        def _():
            for k in passing:
                att_arrival(k, block - 1).wait_recv()
                onward(k, lambda target: att_copy(target, block - 1).start())

    final_ref[...] = memory_ref[...]
    for point in range(blocks * heads - 1, parts + hi - 2):
        for q in range(planes):
            down_step(q, point)
    for k in passing:
        att_arrival(k, blocks - 1).wait_recv()
        onward(k, lambda target: att_copy(target, blocks - 1).start())
    for q in range(planes):
        down_arrive(q)
    out_copy(False).wait_recv()
    for k in range(1, seq, 2):
        for b in range(blocks):
            att_arrival(k, b).wait_recv()
    for c in own_copies:
        c.wait()
    for q in range(planes):
        down_drain(q)
        pl.when(z == me * planes + q)(lambda: down_store(q).wait())
    for b in range(blocks):
        for c in block_stores(b):
            c.wait()
    out_copy(True).wait_send()
    for k in range(1, seq):
        for b in range(blocks):
            att_copy(k, b).wait_send()


def attend(qkv, init, length, state_query, forget, bias, own_out, w_down, heads, seq, fsdp):
    rows, width3 = qkv.shape
    width = heads * DH
    blocks = rows // BLOCK
    lo = 2
    hi = fsdp // lo
    held, dim = w_down.shape
    planes = fsdp // (seq * lo)
    anywhere = pl.BlockSpec(memory_space=pl.ANY)
    vmem = pl.BlockSpec(memory_space=pltpu.VMEM)
    dma = pltpu.SemaphoreType.DMA
    return pl.pallas_call(
        functools.partial(attend_kernel, heads, seq, hi, lo),
        out_shape=(
            jax.ShapeDtypeStruct((rows, width), bf16),
            jax.ShapeDtypeStruct((seq, rows, width), bf16),
            jax.ShapeDtypeStruct((fsdp, 2) + own_out.shape[1:], bf16),
            jax.ShapeDtypeStruct((held * lo * planes, dim), bf16),
            jax.ShapeDtypeStruct((STATE_VECTORS, width), f32),
            jax.ShapeDtypeStruct((blocks, STATE_VECTORS, width), f32),
            jax.ShapeDtypeStruct((blocks, STATE_VECTORS, width), f32),
            jax.ShapeDtypeStruct((heads, rows), f32),
            jax.ShapeDtypeStruct((heads, blocks * STATE_VECTORS), f32),
        ),
        in_specs=[pl.BlockSpec(memory_space=pltpu.SMEM)] + [vmem] * 6 + [anywhere],
        out_specs=(anywhere, anywhere, anywhere, anywhere, vmem, anywhere, anywhere, vmem, vmem),
        scratch_shapes=[
            pltpu.VMEM((STATE_VECTORS, width), f32),
            pltpu.VMEM((heads, QTILE, SPAN), f32),
            pltpu.VMEM((rows, width), bf16),
            pltpu.VMEM((blocks, STATE_VECTORS, width), f32),
            pltpu.VMEM((blocks, STATE_VECTORS, width), f32),
            pltpu.VMEM((held, dim), bf16),
            dma((3, blocks)),
            dma((3,)),
            dma((seq, blocks)),
            dma((seq, blocks)),
            dma,
            dma,
            dma((planes, 2, 4)),
            dma((planes, 4)),
            dma((planes, 4)),
            dma((planes, 4)),
        ],
        compiler_params=pltpu.CompilerParams(collective_id=3, has_side_effects=True, vmem_limit_bytes=60 << 20),
        cost_estimate=pl.CostEstimate(
            flops=blocks * heads * 512 * 2400 * 128 * 4, bytes_accessed=16 << 20, transcendentals=10 << 20
        ),
        name="attend",
    )(length, qkv, init, state_query, forget, bias, own_out, w_down)


def line_reduce(hi, lo, block, total, from_y, from_z, z_send, z_recv, y_send, y_recv, loads=None):
    loads = loads or {}
    f = lax.axis_index("fsdp")
    z, y = f // lo, f % lo

    def remote(src, dst, send, recv, target):
        return pltpu.make_async_remote_copy(
            src_ref=src, dst_ref=dst, send_sem=send, recv_sem=recv, device_id={"fsdp": target}, device_id_type=MESH
        )

    def across(i, d):
        return remote(
            block(i, d * lo + 1 - y), from_y[i].at[d], y_send.at[i, d], y_recv.at[i, d], z * lo + 1 - y
        )

    def start(i):
        for d in range(hi):
            across(i, d).start()

    def combine(i):
        for d in range(hi):
            across(i, d).wait_recv()
            if i in loads:
                loads[i][d].wait()
                own = total[i].at[d]
            else:
                own = block(i, d * lo + y)
            total[i][d] = (own[...].astype(f32) + from_y[i][d].astype(f32)).astype(bf16)

    def hop(i, side, t, at, target):
        return remote(
            total[i].at[jnp.clip(at, 0, hi - 1)],
            from_z[i].at[side, t],
            z_send.at[i, side, t],
            z_recv.at[i, side, t],
            target,
        )

    def sending(t):
        d = t - (hi - 1 - z)
        m = hi - 1 - (t - z)
        return ((0, d, (d >= 0) & (d < z), z - 1), (1, m, (m > z) & (m < hi), z + 1))

    def zsend(i, t):
        for side, at, cond, target in sending(t):
            pl.when(cond)(lambda: hop(i, side, t, at, target * lo + y).start())

    def zrecv(i, t):
        d = t - (hi - 2 - z)
        m = hi - 1 - (t - (z - 1))
        for side, at, cond in ((0, d, (z + 1 < hi) & (d >= 0)), (1, m, (z > 0) & (m < hi))):

            @pl.when(cond)
            def _():
                hop(i, side, t, at, f).wait_recv()
                slot = jnp.clip(at, 0, hi - 1)
                total[i][slot] = (total[i][slot].astype(f32) + from_z[i][side, t].astype(f32)).astype(bf16)

    def drain_y(i):
        for d in range(hi):
            across(i, d).wait_send()

    def drain_z(i):
        for t in range(hi - 1):
            for side, at, cond, target in sending(t):
                pl.when(cond)(lambda: hop(i, side, t, at, f).wait_send())

    return start, combine, zsend, zrecv, drain_y, drain_z


def seq_levels(seq):
    bits = [1 << i for i in range(seq.bit_length() - 1)]
    slots = {}
    for bit in bits:
        for j in range(0, seq, 2 * bit):
            slots[bit, j] = len(slots)
    return bits, slots


def diagonal_sums(tile):
    rows, lanes = tile.shape
    wide = jnp.concatenate([tile, jnp.zeros((rows, lanes), f32)], axis=1)
    row = lax.broadcasted_iota(jnp.int32, wide.shape, 0)
    bit = 1
    while bit < rows:
        wide = jnp.where((row & bit) != 0, pltpu.roll(wide, 2 * lanes - bit, 1), wide)
        bit *= 2
    return jnp.sum(wide, axis=0, keepdims=True)


def attend_back_kernel(heads, seq, hi, lo, inside, length_ref, *refs):
    refs = list(refs)

    def take(count):
        taken = refs[:count]
        del refs[:count]
        return taken

    qkv_hbm, db_hbm, wout_ref, att_hbm, mem_hbm, upd_hbm, lse_ref, slse_ref = take(8)
    sgrad_ref, query_ref, forget_ref, vector_ref, up_ref, down_ref, mo_ref, mid_hbm = take(8)
    ow_in = None if inside else take(1)[0]
    dqkv_out, small_ref, upart_ref, dpart_ref, opart_ref, output_ref = take(6)
    qkv_ref, db_ref, att_ref, mem_ref, upd_ref, mid_ref, dqkv_ref = take(7)
    dmem_ref, dnext_ref, dctx_ref, bias_ref, near_ref, far_ref, dout_ref, ow_buf = take(8)
    to, tu, td, yo, yu, yd, zo, zu, zd, xu, mo_low, mo_in = take(12)
    z_send, z_recv, y_send, y_recv, m_send, m_recv, x_send, x_recv = take(8)
    load_sem, block_sem, up_sem, down_sem, mo_sem, out_sem = take(6)
    ow_ref = ow_buf if inside else ow_in

    me = lax.axis_index("seq")
    f = lax.axis_index("fsdp")
    z, y = f // lo, f % lo
    blocks = seq
    length = length_ref[0]
    width = heads * DH
    scale2 = SCALE * LOG2E
    tok_rows = mid_ref.shape[0]
    bits, slots = seq_levels(seq)

    def chunk_at(block):
        return pl.ds(pl.multiple_of((block ^ me) * BLOCK, BLOCK), BLOCK)

    def block_loads(block):
        at = chunk_at(block)
        pairs = (
            (qkv_hbm.at[at], qkv_ref.at[at]),
            (mem_hbm.at[block], mem_ref.at[block]),
            (upd_hbm.at[block], upd_ref.at[block]),
        )
        return [pltpu.make_async_copy(a, b, block_sem.at[i, block]) for i, (a, b) in enumerate(pairs)]

    loads = [
        pltpu.make_async_copy(att_hbm, att_ref, load_sem.at[0]),
        pltpu.make_async_copy(db_hbm, db_ref, load_sem.at[1]),
        pltpu.make_async_copy(mid_hbm, mid_ref, load_sem.at[2]),
    ]
    up_loads = [
        pltpu.make_async_copy(up_ref.at[d] if inside else up_ref.at[:, d * lo + y], tu.at[d], up_sem.at[d])
        for d in range(hi)
    ]
    down_loads = [pltpu.make_async_copy(down_ref.at[d * lo + y], td.at[d], down_sem.at[d]) for d in range(hi)]
    mo_loads = [pltpu.make_async_copy(mo_ref.at[j], mo_low.at[j // 2], mo_sem.at[j // 2]) for j in range(0, seq, 2)]
    for c in up_loads + loads[:2] + block_loads(blocks - 1) + mo_loads + down_loads:
        c.start()
    for b in reversed(range(blocks - 1)):
        for c in block_loads(b):
            c.start()
    for c in loads[2:]:
        c.start()
    greet(list(range(1, seq)), hi, lo)

    def mo_copy(bit, j):
        slot = slots[bit, j]
        return pltpu.make_async_remote_copy(
            src_ref=mo_ref.at[j ^ bit] if bit == 1 else mo_low.at[(j ^ bit) // 2],
            dst_ref=mo_in.at[slot],
            send_sem=m_send.at[slot],
            recv_sem=m_recv.at[slot],
            device_id={"seq": me ^ bit},
            device_id_type=MESH,
        )

    def block_of(i, target):
        if i == 0:
            return ow_ref.at[target]
        return up_ref.at[:, target] if i == 1 else down_ref.at[target]

    start, combine, zsend, zrecv, drain_y, drain_z = line_reduce(
        hi,
        lo,
        block_of,
        (to, tu, td),
        (yo, yu, yd),
        (zo, zu, zd),
        z_send,
        z_recv,
        y_send,
        y_recv,
        {1: up_loads, 2: down_loads},
    )

    def exchange(k, sending):
        return pltpu.make_async_remote_copy(
            src_ref=tu.at[z, me ^ k] if sending else tu.at[z, me],
            dst_ref=xu.at[me] if sending else xu.at[me ^ k],
            send_sem=x_send.at[k],
            recv_sem=x_recv.at[k],
            device_id={"seq": me ^ k if sending else me},
            device_id_type=MESH,
        )

    if not inside:
        start(1)
    start(2)
    for j in range(seq - 1, 0, -2):
        mo_copy(1, j ^ 1).start()
    if inside:
        for c in up_loads:
            c.wait()
        zsend(1, 0)
    dmem_ref[...] = sgrad_ref[...].astype(f32)
    dnext_ref[...] = jnp.zeros_like(dnext_ref)
    small_ref[...] = jnp.zeros_like(small_ref)
    near_ref[...] = jnp.zeros_like(near_ref)
    far_ref[...] = jnp.zeros_like(far_ref)
    for head in range(heads):
        bias_ref[head] = tile_bias(vector_ref, head).T
    for c in loads[:2]:
        c.wait()
    if inside:
        full = t_dot(att_ref[...], db_ref[...]).astype(bf16)
        ow_buf[...] = full.reshape(ow_buf.shape)
    start(0)

    def mo_step(j):
        mo_loads[j // 2].wait()
        for bit in bits:
            if j & bit:
                mo_copy(bit, j ^ bit).start()
                break
            mo_copy(bit, j).wait_recv()
            own = mo_low[j // 2].astype(f32)
            mo_low[j // 2] = (own + mo_in[slots[bit, j]].astype(f32)).astype(bf16)

    def up_done():
        for k in range(1, seq):
            exchange(k, True).start()

    jobs = [lambda j=j: mo_step(j) for j in range(seq - 2, 0, -2)]
    if not inside:
        jobs.append(lambda: (combine(1), zsend(1, 0)))
    jobs.append(lambda: (zrecv(1, 0), zsend(1, 1) if hi > 2 else None))
    for t in range(1, hi - 1):
        jobs.append(lambda t=t: (zrecv(1, t), zsend(1, t + 1) if t + 1 < hi - 1 else up_done()))
    jobs.append(lambda: (combine(2), zsend(2, 0), combine(0), zsend(0, 0)))
    for t in range(hi - 2):
        jobs.append(lambda t=t: (zrecv(2, t), zsend(2, t + 1), zrecv(0, t), zsend(0, t + 1)))
    jobs.append(lambda: (zrecv(2, hi - 2), zrecv(0, hi - 2)))
    points = blocks * heads - 1

    dq_row = heads * DH
    block_loads(blocks - 1)[0].wait()

    @pl.loop(0, blocks)
    def _(step):
        block = blocks - 1 - step
        pl.when(block >= 1)(lambda: block_loads(jnp.maximum(block - 1, 0))[0].wait())
        for c in block_loads(block)[1:]:
            c.wait()
        cur_at = pl.multiple_of((block ^ me) * BLOCK, BLOCK)
        prev_at = pl.multiple_of((jnp.maximum(block - 1, 0) ^ me) * BLOCK, BLOCK)
        base = pl.multiple_of(block * BLOCK, BLOCK)
        cur_ref = qkv_ref.at[pl.ds(cur_at, BLOCK)]
        prev_ref = qkv_ref.at[pl.ds(prev_at, BLOCK)]
        live_block = block * BLOCK < length
        refs = (prev_ref, cur_ref)
        dout_ref[...] = dot_t(db_ref[pl.ds(cur_at, BLOCK)], wout_ref[...]).astype(bf16)
        for head in range(heads):
            for n, job in enumerate(jobs[:points]):
                if (n + 1) % heads == head:
                    pl.when(step == (n + 1) // heads)(lambda job=job: (job(), None)[1])
            own = slice(head * DH, (head + 1) * DH)
            key_cols = slice(width + head * DH, width + (head + 1) * DH)
            value_cols = slice(2 * width + head * DH, 2 * width + (head + 1) * DH)
            memory = mem_ref[block, :, own]
            update = upd_ref[block, :, own]
            low = memory.astype(bf16)
            forget = forget_ref[:, own]
            dmem = dmem_ref[:, own]
            dupd = jnp.where(live_block, (1.0 - forget) * dmem, 0.0).astype(bf16)
            gone = jnp.where(live_block, dmem * (memory - update), 0.0)
            small_ref[dq_row + head : dq_row + head + 1, :] += jnp.sum(gone, axis=0, keepdims=True)
            dmem_new = jnp.where(live_block, forget * dmem, dmem)
            own_key = cur_ref[:, key_cols]
            own_value = cur_ref[:, value_cols]
            squeries = dot(low, query_ref[head]).astype(bf16)
            sdelta = jnp.sum((dupd.astype(f32) * update).T, axis=0, keepdims=True)
            slse = slse_ref[head : head + 1, pl.ds(base, BLOCK)]
            dsquery = jnp.zeros((STATE_VECTORS, DH), f32)
            dkey = []
            dvalue = []
            for part in range(2 * STATE_VECTORS // QTILE):
                own_part = part >= STATE_VECTORS // QTILE
                at = (part % (STATE_VECTORS // QTILE)) * QTILE
                keys = (own_key if own_part else low)[at : at + QTILE]
                values = (own_value if own_part else low)[at : at + QTILE]
                s = dot_t(keys, squeries) * scale2 - slse
                if own_part:
                    position = block * BLOCK + at + lax.broadcasted_iota(jnp.int32, (QTILE, 1), 0)
                    s = jnp.where(position < length, s, -jnp.inf)
                p = jnp.exp2(s)
                dp = dot_t(values, dupd)
                ds = (p * (dp - sdelta)).astype(bf16)
                dvalue.append(dot(p.astype(bf16), dupd))
                dkey.append(dot(ds, squeries))
                dsquery += t_dot(ds, keys)
            half = STATE_VECTORS // QTILE
            dlow = [dvalue[i] + dkey[i] * SCALE for i in range(half)]
            dctx_ref[0, 0:BLOCK] = jnp.zeros((BLOCK, DH), f32)
            dctx_ref[1, 0:BLOCK] = jnp.zeros((BLOCK, DH), f32)
            for i in range(half):
                rows = slice(BLOCK + i * QTILE, BLOCK + (i + 1) * QTILE)
                old = slice(i * QTILE, (i + 1) * QTILE)
                dctx_ref[0, rows] = dkey[half + i] * SCALE + dnext_ref[0, old, own]
                dctx_ref[1, rows] = dvalue[half + i] + dnext_ref[1, old, own]
            dsq = (dsquery * SCALE).astype(bf16)
            small_ref[head * DH : (head + 1) * DH, :] += t_dot(low, dsq)
            dmem_ref[:, own] = dmem_new + dot_t(dsq, query_ref[head])
            for tile in range(BLOCK // QTILE):
                rows = slice(tile * QTILE, (tile + 1) * QTILE)
                here = pl.ds(cur_at + tile * QTILE, QTILE)
                query = cur_ref[rows, own]
                dout = dout_ref[rows, own]
                lse = lse_ref[head : head + 1, pl.ds(base + tile * QTILE, QTILE)]
                delta = jnp.sum((dout.astype(f32) * att_ref[here, own].astype(f32)).T, axis=0, keepdims=True)
                dq = jnp.zeros((QTILE, DH), f32)
                for which, first, end, col in context_pieces(tile):
                    for at in range(first, end, QTILE):
                        keys = refs[which][at : at + QTILE, key_cols]
                        values = refs[which][at : at + QTILE, value_cols]
                        band = col + at - first
                        position = (block - 1 + which) * BLOCK + at + lax.broadcasted_iota(jnp.int32, (QTILE, 1), 0)
                        live = (position >= 0) & (position < length)
                        s = dot_t(keys, query) * scale2 + bias_ref[head, band : band + QTILE, :] - lse
                        p = jnp.exp2(jnp.where(live, s, -jnp.inf))
                        dp = dot_t(values, dout)
                        ds = (p * (dp - delta)).astype(bf16)
                        wide = ds.astype(f32)
                        edge = min(max(SPAN - NEAR - band, 0), QTILE)
                        if edge:
                            far_ref[head] += functools.reduce(jnp.add, [wide[i : i + 8] for i in range(0, edge, 8)])
                        if edge < QTILE:
                            at_near = band + edge - (SPAN - NEAR)
                            near_ref[head, at_near : at_near + QTILE - edge] += wide[edge:]
                        into = slice(which * BLOCK + at, which * BLOCK + at + QTILE)
                        dctx_ref[1, into] += dot(p.astype(bf16), dout)
                        dctx_ref[0, into] += dot(ds, query) * SCALE
                        dq += t_dot(ds, keys)
                for part in range(half):
                    keys = low[part * QTILE : (part + 1) * QTILE]
                    s = dot_t(keys, query) * scale2 - lse
                    p = jnp.exp2(s)
                    dp = dot_t(keys, dout)
                    ds = (p * (dp - delta)).astype(bf16)
                    dlow[part] += dot(p.astype(bf16), dout) + dot(ds, query) * SCALE
                    dq += t_dot(ds, keys)
                dqkv_ref[here, own] = (dq * SCALE).astype(bf16)
            for part in range(half):
                dmem_ref[part * QTILE : (part + 1) * QTILE, own] += dlow[part]
            dnext_ref[0, :, own] = dctx_ref[0, 0:BLOCK]
            dnext_ref[1, :, own] = dctx_ref[1, 0:BLOCK]
            dqkv_ref[pl.ds(cur_at, BLOCK), key_cols] = dctx_ref[0, BLOCK:].astype(bf16)
            dqkv_ref[pl.ds(cur_at, BLOCK), value_cols] = dctx_ref[1, BLOCK:].astype(bf16)

    dqkv_store = pltpu.make_async_copy(dqkv_ref, dqkv_out, out_sem)
    dqkv_store.start()
    for job in jobs[points:]:
        job()
    member = bucket_members()
    lane = lax.broadcasted_iota(jnp.int32, (1, DH), 1)
    for head in range(heads):
        sums = jnp.broadcast_to(diagonal_sums(near_ref[head]), (8, 2 * QTILE))
        table = jnp.dot(sums, member, precision=lax.Precision.HIGHEST, preferred_element_type=f32)[0:1]
        total = jnp.sum(jnp.sum(far_ref[head], axis=0, keepdims=True), axis=1, keepdims=True)
        row = dq_row + heads + head
        small_ref[row : row + 1, :] = table + jnp.where(lane == BUCKETS - 1, total, 0.0)
        row = dq_row + head
        forget = forget_ref[:, head * DH : (head + 1) * DH]
        small_ref[row : row + 1, :] = small_ref[row : row + 1, :] * forget * (1.0 - forget)
    loads[2].wait()
    mo_loads[0].wait()
    for bit in bits:
        mo_copy(bit, 0).wait_recv()
    step = 128
    for r in range(0, tok_rows, step):
        at = slice(r, r + step)
        value = mid_ref[at] + mo_low[0, at].astype(f32)
        for bit in bits:
            value = value + mo_in[slots[bit, 0], at].astype(f32)
        position = me * tok_rows + r + lax.broadcasted_iota(jnp.int32, (step, 1), 0)
        output_ref[at] = (value * jnp.where(position < length, 1.0, 0.0)).astype(bf16)
    opart_ref[...] = to[z].astype(f32)
    dpart_ref[...] = td[z].astype(f32)
    for k in range(1, seq):
        exchange(k, False).wait_recv()
    xu[me] = tu[z, me]
    write_parts(upart_ref, xu, seq, xu.shape[2])
    for i in (0, 2) if inside else (0, 1, 2):
        drain_y(i)
    for i in range(3):
        drain_z(i)
    for bit in bits:
        for j in range(0, seq, 2 * bit):
            mo_copy(bit, j).wait_send()
    for k in range(1, seq):
        exchange(k, True).wait_send()
    dqkv_store.wait()


def bucket_members():
    shape = (2 * QTILE, DH)
    row = lax.broadcasted_iota(jnp.int32, shape, 0)
    lane = lax.broadcasted_iota(jnp.int32, shape, 1)
    distance = jnp.where(row < QTILE, row, row - 2 * QTILE) + NEAR - QTILE
    bucket = jnp.minimum(distance, 16)
    for edge in BUCKET_EDGES:
        bucket = bucket + jnp.where(distance >= edge, 1, 0)
    inside = (distance >= 0) & (distance < BLOCK) & (bucket == lane)
    return jnp.where(inside, 1.0, 0.0)


def write_parts(out_ref, pieces, seq, unit):
    count = pieces.shape[2] // unit
    for k in range(seq):
        for c in range(count):
            at = (c * seq + k) * unit
            out_ref[:, at : at + unit] = pieces[k, :, c * unit : (c + 1) * unit].astype(f32)


def attend_back(
    qkv, db, wout, att, mem, upd, lse, slse, sgrad, length, state_query, forget, bias, up, down, mo, mid, seq, fsdp
):
    rows, width3 = qkv.shape
    width = width3 // 3
    heads = width // DH
    dim = db.shape[1]
    lo = 2
    hi = fsdp // lo
    piece, hidden = up.shape[2:]
    share = hidden // fsdp
    tok_rows = mid.shape[0]
    inside = piece % 16 == 0
    blocks = (piece, dim), (seq, piece, hidden), (share, dim)
    small_rows = heads * (DH + 2)
    small_rows += -small_rows % 8
    vmem = pl.BlockSpec(memory_space=pltpu.VMEM)
    anywhere = pl.BlockSpec(memory_space=pl.ANY)
    dma = pltpu.SemaphoreType.DMA

    def buf(*shape):
        return pltpu.VMEM(shape, bf16)

    extra = []
    if not inside:
        extra.append(t_dot(att, db).astype(bf16).reshape(fsdp, piece, dim))
    return pl.pallas_call(
        functools.partial(attend_back_kernel, heads, seq, hi, lo, inside),
        out_shape=(
            jax.ShapeDtypeStruct((rows, width3), bf16),
            jax.ShapeDtypeStruct((small_rows, DH), f32),
            jax.ShapeDtypeStruct((piece, hidden * seq), f32),
            jax.ShapeDtypeStruct((share, dim), f32),
            jax.ShapeDtypeStruct((piece, dim), f32),
            jax.ShapeDtypeStruct((tok_rows, dim), bf16),
        ),
        in_specs=[pl.BlockSpec(memory_space=pltpu.SMEM), anywhere, anywhere, vmem]
        + [anywhere] * 3
        + [vmem] * 6
        + [anywhere] * 4
        + [vmem] * len(extra),
        out_specs=(anywhere,) + (vmem,) * 5,
        scratch_shapes=[
            buf(rows, width3),
            buf(rows, dim),
            buf(rows, width),
            pltpu.VMEM(mem.shape, f32),
            pltpu.VMEM(upd.shape, f32),
            pltpu.VMEM((tok_rows, dim), f32),
            buf(rows, width3),
            pltpu.VMEM((STATE_VECTORS, width), f32),
            pltpu.VMEM((2, BLOCK, width), f32),
            pltpu.VMEM((2, 2 * BLOCK, DH), f32),
            pltpu.VMEM((heads, SPAN, QTILE), f32),
            pltpu.VMEM((heads, NEAR, QTILE), f32),
            pltpu.VMEM((heads, 8, QTILE), f32),
            buf(BLOCK, width),
            buf(fsdp, piece, dim),
            buf(hi, *blocks[0]),
            buf(hi, *blocks[1]),
            buf(hi, *blocks[2]),
            buf(hi, *blocks[0]),
            buf(16, 128) if inside else buf(hi, *blocks[1]),
            buf(hi, *blocks[2]),
            buf(2, max(hi - 1, 1), *blocks[0]),
            buf(2, max(hi - 1, 1), *blocks[1]),
            buf(2, max(hi - 1, 1), *blocks[2]),
            buf(*blocks[1]),
            buf(max(seq // 2, 1), tok_rows, dim),
            buf(max(seq - 1, 1), tok_rows, dim),
            dma((3, 2, hi)),
            dma((3, 2, hi)),
            dma((3, hi)),
            dma((3, hi)),
            dma((seq,)),
            dma((seq,)),
            dma((seq,)),
            dma((seq,)),
            dma((3,)),
            dma((3, seq)),
            dma((hi,)),
            dma((hi,)),
            dma((seq,)),
            dma,
        ],
        compiler_params=pltpu.CompilerParams(collective_id=4, has_side_effects=True, vmem_limit_bytes=62 << 20),
        cost_estimate=pl.CostEstimate(
            flops=seq * heads * 512 * 2400 * 128 * 10, bytes_accessed=20 << 20, transcendentals=10 << 20
        ),
        name="attend_back",
    )(
        length, qkv, db, wout, att, mem, upd, lse, slse, sgrad, state_query, forget, bias, up, down, mo, mid, *extra
    )


def gather_kernel(
    seq,
    hi,
    lo,
    tok_ref,
    grad_ref,
    wq_ref,
    ga_ref,
    gm_ref,
    wo_ref,
    wu_ref,
    toks_ref,
    grads_ref,
    wqs_ref,
    gas_ref,
    gms_ref,
    wos_ref,
    wus_ref,
    *rest,
):
    own_bufs = rest[:7]
    own_sem, store_sem, seq_send, seq_recv, z_send, z_recv, y_send, y_recv = rest[7:]
    me = lax.axis_index("seq")
    f = lax.axis_index("fsdp")
    fsdp = hi * lo
    bits = [1 << i for i in range(seq.bit_length() - 1)]
    greet(bits, hi, lo)

    pairs = ((tok_ref, toks_ref), (grad_ref, grads_ref))

    def seq_copy(i, source, slot, bit):
        src, out = pairs[i]
        return pltpu.make_async_remote_copy(
            src_ref=out.at[source] if source else src,
            dst_ref=out.at[slot],
            send_sem=seq_send.at[i, slot],
            recv_sem=seq_recv.at[i, slot],
            device_id={"seq": me ^ bit},
            device_id_type=MESH,
        )

    sends = []

    def send(i, source, slot, bit):
        sends.append(seq_copy(i, source, slot, bit))
        sends[-1].start()

    high = [bit for bit in reversed(bits) if bit > 1]
    if high:
        send(0, 0, high[0], high[0])
    if seq > 1:
        send(0, 0, 1, 1)

    width = wqs_ref.shape[2] // 3
    every = wq_ref.shape[1] // 3
    loads = [[] for _ in own_bufs]

    def load(i, src, dst):
        loads[i].append(pltpu.make_async_copy(src, dst, own_sem.at[i, len(loads[i])]))
        loads[i][-1].start()

    wq_buf, ga_buf, gm_buf, wo_buf, wu_buf, tok_buf, grad_buf = own_bufs
    for c in range(3):
        cols = pl.ds(pl.multiple_of(c * every + me * width, width), width)
        load(0, wq_ref.at[:, cols], wq_buf.at[:, pl.ds(c * width, width)])
    load(1, ga_ref, ga_buf)
    load(2, gm_ref, gm_buf)
    load(3, wo_ref.at[me % 2], wo_buf)
    hidden = wus_ref.shape[2]
    load(4, wu_ref.at[:, pl.ds(pl.multiple_of(me * hidden, hidden), hidden)], wu_buf)
    load(5, tok_ref, tok_buf)
    load(6, grad_ref, grad_buf)
    outs = (wqs_ref, gas_ref, gms_ref, wos_ref, wus_ref)
    start, step, arrive, drain = line_gather(
        hi, lo, lambda i, origin: outs[i].at[origin], lambda i: own_bufs[i], z_send, z_recv, y_send, y_recv
    )
    own_stores = []
    for i in range(len(own_bufs)):
        for c in loads[i]:
            c.wait()
        if i < len(outs):
            start(i)
        target = outs[i].at[f] if i < len(outs) else pairs[i - len(outs)][1].at[0]
        own_stores.append(pltpu.make_async_copy(own_bufs[i], target, store_sem.at[i]))
        own_stores[-1].start()
    if high:
        send(1, 0, high[0], high[0])
    if seq > 1:
        send(1, 0, 1, 1)
    for t in range(hi - 1):
        for i in range(len(outs)):
            step(i, t)
    for i in range(len(pairs)):
        have = [0]
        for n, bit in enumerate(high):
            if n:
                for j in have:
                    send(i, j, j ^ bit, bit)
            for j in have:
                seq_copy(i, 0, j ^ bit, bit).wait_recv()
                send(i, j ^ bit, j ^ bit ^ 1, 1)
            have += [j ^ bit for j in have]
        if seq > 1:
            for j in have:
                seq_copy(i, 0, j ^ 1, 1).wait_recv()
    for i in range(len(outs)):
        arrive(i)
    for i in range(len(outs)):
        drain(i)
    for c in sends:
        c.wait_send()
    for c in own_stores:
        c.wait()


def gather_start(tokens, grads, w_qkv, gain_a, gain_m, w_out, w_up, seq, fsdp):
    lo = 2
    hi = fsdp // lo
    dim_rows, hidden = w_up.shape
    anywhere = pl.BlockSpec(memory_space=pl.ANY)
    dma = pltpu.SemaphoreType.DMA
    shapes = (
        (seq,) + tokens.shape,
        (seq,) + grads.shape,
        (fsdp, dim_rows, w_qkv.shape[1] // seq),
        (fsdp,) + gain_a.shape,
        (fsdp,) + gain_m.shape,
        (fsdp,) + w_out.shape[1:],
        (fsdp, dim_rows, hidden // seq),
    )
    return pl.pallas_call(
        functools.partial(gather_kernel, seq, hi, lo),
        out_shape=tuple(jax.ShapeDtypeStruct(shape, bf16) for shape in shapes),
        in_specs=[anywhere] * 7,
        out_specs=(anywhere,) * 7,
        scratch_shapes=[pltpu.VMEM(shape[1:], bf16) for shape in shapes[2:] + shapes[:2]]
        + [dma((7, max(fsdp, 3))), dma((7,)), dma((2, seq)), dma((2, seq))]
        + line_sems(5, hi),
        compiler_params=pltpu.CompilerParams(collective_id=0, has_side_effects=True),
        name="gather_start",
    )(tokens, grads, w_qkv, gain_a, gain_m, w_out, w_up)


def finish_kernel(seq, hi, lo, inside, *refs):
    refs = list(refs)

    def take(count):
        taken = refs[:count]
        del refs[:count]
        return taken

    dqkv_hbm, wqkv_hbm, normed_hbm, small_ref, mlp_gain_ref, tok_hbm, dmid_hbm, gain_ref = take(8)
    gq_in = None if inside else take(1)[0]
    tg_ref, rq_ref, dquery_ref, gate_ref, table_ref, again_ref, mgain_ref = take(7)
    dqkv_ref, wqkv_ref, normed_ref, tok_ref, dmid_ref = take(5)
    low, into, acc, gq_buf, tq, yq, zq, xq, sy, sz, gains, gy, gz, gs = take(14)
    dn_send, dn_recv, z_send, z_recv, y_send, y_recv, x_send, x_recv, s_send, s_recv, g_send, g_recv = take(12)
    load_sem, dqkv_sem, tg_sem = take(3)
    gq_ref = gq_buf if inside else gq_in

    me = lax.axis_index("seq")
    f = lax.axis_index("fsdp")
    z, y = f // lo, f % lo
    peer = z * lo + 1 - y
    rows, dim = tok_ref.shape
    width = xq.shape[2] // 3
    bits, slots = seq_levels(seq)

    loads = [
        pltpu.make_async_copy(src, dst, load_sem.at[i])
        for i, (src, dst) in enumerate(
            (
                (wqkv_hbm, wqkv_ref),
                (normed_hbm, normed_ref),
                (tok_hbm, tok_ref),
                (dmid_hbm, dmid_ref),
            )
        )
    ]
    dqkv_loads = {
        j: pltpu.make_async_copy(
            dqkv_hbm.at[pl.ds(j * rows, rows)], dqkv_ref.at[pl.ds(j * rows, rows)], dqkv_sem.at[j]
        )
        for j in range(seq)
    }
    loads[0].start()
    for j in reversed(range(seq)):
        dqkv_loads[j].start()
    for c in loads[1:]:
        c.start()

    barrier = pltpu.get_barrier_semaphore()
    for k in range(1, seq):
        pl.semaphore_signal(barrier, inc=1, device_id={"seq": me ^ k}, device_id_type=MESH)
    for k in range(1, hi):
        pl.semaphore_signal(barrier, inc=1, device_id={"fsdp": lax.rem(z + k, hi) * lo + y}, device_id_type=MESH)
    pl.semaphore_signal(barrier, inc=1, device_id={"fsdp": peer}, device_id_type=MESH)
    pl.semaphore_wait(barrier, seq + hi - 1)

    def remote(src, dst, send, recv, axis, target):
        return pltpu.make_async_remote_copy(
            src_ref=src, dst_ref=dst, send_sem=send, recv_sem=recv, device_id={axis: target}, device_id_type=MESH
        )

    def dn_copy(bit, j):
        slot = slots[bit, j]
        return remote(low.at[j ^ bit], into.at[slot], dn_send.at[slot], dn_recv.at[slot], "seq", me ^ bit)

    start, combine, zsend, zrecv, drain_y, drain_z = line_reduce(
        hi,
        lo,
        lambda i, target: gq_ref.at[:, target],
        (tq,),
        (yq,),
        (zq,),
        z_send,
        z_recv,
        y_send,
        y_recv,
    )

    def exchange(k, sending):
        return remote(
            tq.at[z, me ^ k] if sending else tq.at[z, me],
            xq.at[me] if sending else xq.at[me ^ k],
            x_send.at[k],
            x_recv.at[k],
            "seq",
            me ^ k if sending else me,
        )

    small_y = remote(small_ref, sy, s_send.at[0], s_recv.at[0], "fsdp", peer)
    small_y.start()
    loads[0].wait()
    if not inside:
        start(0)

    def dn_part(j):
        part = dot_t(dqkv_ref[j * rows : (j + 1) * rows], wqkv_ref[...])
        if j % 2:
            low[j] = part.astype(bf16)
            dn_copy(1, j ^ 1).start()
        else:
            acc[...] = part

    def dn_sum(j):
        for bit in bits:
            if j & bit:
                low[j] = acc[...].astype(bf16)
                dn_copy(bit, j ^ bit).start()
                break
            dn_copy(bit, j).wait_recv()
            acc[...] += into[slots[bit, j]].astype(f32)

    for j in reversed(range(2, seq)):
        dqkv_loads[j].wait()
        dn_part(j)
        if j % 2 == 0:
            dn_sum(j)
    for j in range(min(2, seq)):
        dqkv_loads[j].wait()
    loads[1].wait()
    if inside:
        for k in range(seq):
            cols = slice(k * (dim // seq), (k + 1) * (dim // seq))
            part = t_dot(normed_ref[:, cols], dqkv_ref[...]).astype(bf16)
            gq_buf[k] = part.reshape(gq_buf.shape[1:])
        start(0)
    small_y.wait_recv()
    sz[z] = small_ref[...] + sy[...]
    small_z = []
    for k in range(1, hi):
        small_z.append(
            remote(sz.at[z], sz.at[z], s_send.at[k], s_recv.at[k], "fsdp", lax.rem(z + k, hi) * lo + y)
        )
        small_z[-1].start()
    for j in reversed(range(min(2, seq))):
        dn_part(j)
    for c in loads[2:]:
        c.wait()
    combine(0)
    zsend(0, 0)
    for bit in bits:
        dn_copy(bit, 0).wait_recv()
    gain = gain_ref[...]
    part = jnp.zeros((8, dim), f32)
    step = 128
    for r in range(0, rows, step):
        at = slice(r, r + step)
        dn = acc[at]
        for bit in bits:
            dn = dn + into[slots[bit, 0], at].astype(f32)
        x = tok_ref[at].astype(f32)
        rho = lax.rsqrt(jnp.mean(x * x, axis=-1, keepdims=True) + EPSILON)
        scaled = gain * dn
        mean = jnp.mean(x * scaled, axis=-1, keepdims=True)
        dmid_ref[at] += rho * scaled - x * (rho * rho * rho * mean)
        prod = dn * x * rho
        part += functools.reduce(jnp.add, [prod[n : n + 8] for n in range(0, step, 8)])
    tg_store = pltpu.make_async_copy(dmid_ref, tg_ref, tg_sem)
    tg_store.start()
    gains[0:8] = mlp_gain_ref[...]
    gains[8:16] = part
    gain_y = remote(gains, gy, g_send.at[0], g_recv.at[0], "fsdp", peer)
    gain_y.start()
    zrecv(0, 0)
    if hi > 2:
        zsend(0, 1)
    gain_y.wait_recv()
    gz[z] = gains[...] + gy[...]
    gain_z = []
    for k in range(1, hi):
        gain_z.append(
            remote(gz.at[z], gz.at[z], g_send.at[k], g_recv.at[k], "fsdp", lax.rem(z + k, hi) * lo + y)
        )
        gain_z[-1].start()
    for t in range(1, hi - 1):
        zrecv(0, t)
        if t + 1 < hi - 1:
            zsend(0, t + 1)
    for k in range(1, seq):
        exchange(k, True).start()
    for k in range(1, hi):
        source = lax.rem(z + hi - k, hi)
        remote(gz.at[source], gz.at[source], g_send.at[k], g_recv.at[k], "fsdp", f).wait_recv()
        remote(sz.at[source], sz.at[source], s_send.at[k], s_recv.at[k], "fsdp", f).wait_recv()
    gs[me] = functools.reduce(jnp.add, [gz[d] for d in range(hi)])
    gain_x = []
    for k in range(1, seq):
        gain_x.append(remote(gs.at[me], gs.at[me], g_send.at[hi + k], g_recv.at[hi + k], "seq", me ^ k))
        gain_x[-1].start()
    total = functools.reduce(jnp.add, [sz[d] for d in range(hi)])
    cut, heads = dquery_ref.shape[0], gate_ref.shape[0]
    dquery_ref[...] = total[:cut]
    gate_ref[...] = total[cut : cut + heads]
    table_ref[...] = total[cut + heads : cut + 2 * heads, :BUCKETS]
    xq[me] = tq[z, me]
    for k in range(1, seq):
        exchange(k, False).wait_recv()
    write_parts(rq_ref, xq, seq, width)
    for k in range(1, seq):
        remote(gs.at[me ^ k], gs.at[me ^ k], g_send.at[hi + k], g_recv.at[hi + k], "seq", me).wait_recv()
    total = functools.reduce(jnp.add, [gs[k] for k in range(seq)])
    piece = again_ref.shape[1]
    total = pltpu.roll(total, lax.rem(dim - (me * hi * lo + f) * piece, dim), 1)[:, :DH]
    mgain_ref[...] = jnp.sum(total[0:8], axis=0, keepdims=True)[:, :piece]
    again_ref[...] = jnp.sum(total[8:16], axis=0, keepdims=True)[:, :piece]

    for bit in bits:
        for j in range(0, seq, 2 * bit):
            dn_copy(bit, j).wait_send()
    drain_y(0)
    drain_z(0)
    for k in range(1, seq):
        exchange(k, True).wait_send()
    for c in [small_y, gain_y] + small_z + gain_z + gain_x:
        c.wait_send()
    tg_store.wait()


def finish(dqkv, wqkv, normed, small, mlp_gain, tok, dmid, gain, seq, fsdp):
    lo = 2
    hi = fsdp // lo
    rows, dim = tok.shape
    width3 = dqkv.shape[1]
    piece = dim // (seq * fsdp)
    inside = piece % 16 == 0
    heads = width3 // (3 * DH)
    vmem = pl.BlockSpec(memory_space=pltpu.VMEM)
    anywhere = pl.BlockSpec(memory_space=pl.ANY)
    dma = pltpu.SemaphoreType.DMA

    def buf(*shape):
        return pltpu.VMEM(shape, bf16)

    extra = []
    if not inside:
        extra.append(t_dot(normed, dqkv).astype(bf16).reshape(seq, fsdp, piece, width3))
    scratch = [
        buf(*dqkv.shape),
        buf(*wqkv.shape),
        buf(*normed.shape),
        buf(rows, dim),
        pltpu.VMEM((rows, dim), f32),
        buf(seq, rows, dim),
        buf(max(seq - 1, 1), rows, dim),
        pltpu.VMEM((rows, dim), f32),
        buf(seq, fsdp, piece, width3) if inside else buf(16, 128),
        buf(hi, seq, piece, width3),
        buf(hi, seq, piece, width3),
        buf(2, max(hi - 1, 1), seq, piece, width3),
        buf(seq, piece, width3),
        pltpu.VMEM(small.shape, f32),
        pltpu.VMEM((hi,) + small.shape, f32),
        pltpu.VMEM((16, dim), f32),
        pltpu.VMEM((16, dim), f32),
        pltpu.VMEM((hi, 16, dim), f32),
        pltpu.VMEM((seq, 16, dim), f32),
        dma((seq,)),
        dma((seq,)),
        dma((1, 2, hi)),
        dma((1, 2, hi)),
        dma((1, hi)),
        dma((1, hi)),
        dma((seq,)),
        dma((seq,)),
        dma((hi,)),
        dma((hi,)),
        dma((hi + seq,)),
        dma((hi + seq,)),
        dma((5,)),
        dma((seq,)),
        dma,
    ]
    return pl.pallas_call(
        functools.partial(finish_kernel, seq, hi, lo, inside),
        out_shape=(
            jax.ShapeDtypeStruct((rows, dim), f32),
            jax.ShapeDtypeStruct((piece, seq * width3), f32),
            jax.ShapeDtypeStruct((heads * DH, DH), f32),
            jax.ShapeDtypeStruct((heads, DH), f32),
            jax.ShapeDtypeStruct((heads, BUCKETS), f32),
            jax.ShapeDtypeStruct((1, piece), f32),
            jax.ShapeDtypeStruct((1, piece), f32),
        ),
        in_specs=[anywhere] * 3 + [vmem] * 2 + [anywhere] * 2 + [vmem] * (1 + len(extra)),
        out_specs=(anywhere,) + (vmem,) * 6,
        scratch_shapes=scratch,
        compiler_params=pltpu.CompilerParams(
            collective_id=1, has_side_effects=True, vmem_limit_bytes=60 << 20
        ),
        name="finish",
    )(dqkv, wqkv, normed, small, mlp_gain, tok, dmid, gain, *extra)


GELU_P = 0.24
GELU_C = (
    0.08951261885080208,
    0.15562094398234086,
    -0.15437154502074169,
    0.6261054138112487,
    -0.6465313024138201,
    0.5547927291245551,
    -0.125128858665134,
)


def gelu_parts(x):
    size = jnp.abs(x)
    t = 1.0 / (1.0 + GELU_P * size)
    poly = GELU_C[-1] * t
    for c in GELU_C[-2::-1]:
        poly = (poly + c) * t
    bell = jnp.exp2(x * x * (-0.5 * LOG2E))
    tail = poly * bell
    cdf = jnp.where(x < 0.0, tail, 1.0 - tail)
    return x * cdf, cdf + x * bell * (1.0 / math.sqrt(2.0 * math.pi))


def mlp_kernel(seq, hi, lo, sub, length_ref, *refs):
    refs = list(refs)

    def take(count):
        taken = refs[:count]
        del refs[:count]
        return taken

    own_ref, others_ref, tok_ref, grads_ref, wo_hbm, wu_hbm, wd_hbm, gain_ref = take(8)
    mid_out, dmid_out, gsum_ref, db_ref, mo_ref, ug_out, dg_out = take(7)
    staged = len(ug_out.shape) == 4
    att_refs = [own_ref] + [others_ref.at[k] for k in range(1, seq)]
    att_buf, tok_buf, wo_ref, wu_ref, wd_ref, gm, nm, hid, dpre, low, into, acc, mid_ref, ug_ref, dg_ref = take(15)
    load_sem, w_sem, gm_sem, dn_send, dn_recv, db_send, db_recv, mo_sem, own_sem = take(9)
    if staged:
        tu, yu, y_send, y_recv = take(4)
    dbv = low.at[0]
    depth = att_buf.shape[0]

    me = lax.axis_index("seq")
    length = length_ref[0]
    dim = wo_ref.shape[0]
    width = dim // seq
    rows = tok_ref.shape[1]
    share = wu_ref.shape[1]
    subs = rows // sub
    bits, slots = seq_levels(seq)
    order = list(reversed(range(seq)))

    def chunk_loads(j):
        slot = j % depth
        copies = [
            pltpu.make_async_copy(att_refs[k].at[pl.ds(j * rows, rows)], att_buf.at[slot, k], load_sem.at[slot, k])
            for k in range(seq)
        ]
        copies.append(pltpu.make_async_copy(tok_ref.at[j], tok_buf.at[slot], load_sem.at[slot, seq]))
        return copies

    gm_loads = {
        j: pltpu.make_async_copy(grads_ref.at[j], gm.at[pl.ds(j * rows, rows)], gm_sem.at[j]) for j in order
    }
    weights = [
        pltpu.make_async_copy(src, dst, w_sem.at[i])
        for i, (src, dst) in enumerate(((wo_hbm, wo_ref), (wu_hbm, wu_ref), (wd_hbm, wd_ref)))
    ]
    for c in chunk_loads(order[0]) + weights[:1] + (chunk_loads(order[1]) if seq > 1 else []) + weights[1:]:
        c.start()
    for j in order:
        gm_loads[j].start()
    if depth == seq:
        for j in order[2:]:
            for c in chunk_loads(j):
                c.start()

    greet(bits, hi, lo)

    def dn_copy(bit, j, s):
        slot = slots[bit, j]
        at = pl.ds(pl.multiple_of(s * sub, sub), sub)
        return pltpu.make_async_remote_copy(
            src_ref=low.at[j ^ bit, at],
            dst_ref=into.at[slot, at],
            send_sem=dn_send.at[slot, s],
            recv_sem=dn_recv.at[slot, s],
            device_id={"seq": me ^ bit},
            device_id_type=MESH,
        )

    gain = gain_ref[...]

    def forward(j, s):
        slot = j % depth
        at = pl.ds(pl.multiple_of(s * sub, sub), sub)
        here = pl.ds(pl.multiple_of(j * rows + s * sub, sub), sub)
        position = (j ^ me) * rows + s * sub + lax.broadcasted_iota(jnp.int32, (sub, 1), 0)
        live = jnp.where(position < length, 1.0, 0.0)
        masked = (gm[here].astype(f32) * live).astype(bf16)
        gm[here] = masked
        mid = tok_buf[slot, at].astype(f32)
        for k in range(seq):
            own = pl.ds(pl.multiple_of((me ^ k) * width, width), width)
            mid = mid + dot(att_buf[slot, k, at], wo_ref[own])
        rho = lax.rsqrt(jnp.mean(mid * mid, axis=-1, keepdims=True) + EPSILON)
        normed = (mid * rho * gain).astype(bf16)
        nm[here] = normed
        if j == 0:
            mid_ref[at] = mid
        for c in range(0, share, 256):
            cols = slice(c, c + 256)
            value, slope = gelu_parts(dot(normed, wu_ref[:, cols]))
            hid[here, cols] = value.astype(bf16)
            dpre[here, cols] = (dot_t(masked, wd_ref[cols]) * slope).astype(bf16)
        part = dot_t(dpre[here], wu_ref[...])
        if j % 2:
            low[j, at] = part.astype(bf16)
            dn_copy(1, j ^ 1, s).start()
        else:
            acc[at] = part

    def settle(j, s):
        at = pl.ds(pl.multiple_of(s * sub, sub), sub)
        for bit in bits:
            if j & bit:
                low[j, at] = acc[at].astype(bf16)
                dn_copy(bit, j ^ bit, s).start()
                break
            dn_copy(bit, j, s).wait_recv()
            acc[at] += into[slots[bit, j], at].astype(f32)

    for c in weights:
        c.wait()
    for n in range(0, seq, 2):
        pair = order[n : n + 2]
        if n and depth < seq:
            for j in pair:
                for c in chunk_loads(j):
                    c.start()
        for j in pair:
            for c in chunk_loads(j):
                c.wait()
            gm_loads[j].wait()

        @pl.loop(0, subs)
        def _(s):
            for j in pair:
                forward(j, s)
            if pair[-1]:
                settle(pair[-1], s)

    stores = [pltpu.make_async_copy(mid_ref, mid_out, own_sem.at[1])]
    stores[0].start()
    if staged:
        for k in range(seq):
            cols = slice(k * (dim // seq), (k + 1) * (dim // seq))
            ug_ref[k] = t_dot(nm[:, cols], dpre[...]).astype(bf16).reshape(ug_ref.shape[1:])
        start, combine, _, _, drain_y, _ = line_reduce(
            hi, lo, lambda i, target: ug_ref.at[:, target], (tu,), (yu,), (), None, None, y_send, y_recv
        )
        start(0)
    else:
        for c in range(0, dim, 256):
            ug_ref[c : c + 256] = t_dot(nm[:, c : c + 256], dpre[...]).astype(bf16)
        stores.append(pltpu.make_async_copy(ug_ref, ug_out, own_sem.at[2]))
        stores[-1].start()

    def db_copy(source, target, bit, s):
        at = pl.ds(s * sub, sub)
        return pltpu.make_async_remote_copy(
            src_ref=db_ref.at[source, at] if source else dbv.at[at],
            dst_ref=db_ref.at[target, at],
            send_sem=db_send.at[target, s],
            recv_sem=db_recv.at[target, s],
            device_id={"seq": me ^ bit},
            device_id_type=MESH,
        )

    sends = []
    high = [bit for bit in reversed(bits) if bit > 1]

    def send(source, target, bit, s):
        sends.append(db_copy(source, target, bit, s))
        sends[-1].start()

    step = 128
    part = jnp.zeros((8, dim), f32)
    for s in range(subs):
        for bit in bits:
            dn_copy(bit, 0, s).wait_recv()
        for r in range(s * sub, (s + 1) * sub, step):
            at = slice(r, r + step)
            dn = acc[at]
            for bit in bits:
                dn = dn + into[slots[bit, 0], at].astype(f32)
            mid = mid_ref[at]
            rho = lax.rsqrt(jnp.mean(mid * mid, axis=-1, keepdims=True) + EPSILON)
            scaled = gain * dn
            mean = jnp.mean(mid * scaled, axis=-1, keepdims=True)
            dmid = gm[at].astype(f32) + rho * scaled - mid * (rho * rho * rho * mean)
            acc[at] = dmid
            dbv[at] = dmid.astype(bf16)
            prod = dn * mid * rho
            part += functools.reduce(jnp.add, [prod[i : i + 8] for i in range(0, step, 8)])
        if high:
            send(0, high[0], high[0], s)
        if seq > 1:
            send(0, 1, 1, s)
    gsum_ref[...] = part
    stores.append(pltpu.make_async_copy(dbv, db_ref.at[0], own_sem.at[0]))
    stores[-1].start()
    stores.append(pltpu.make_async_copy(acc, dmid_out, own_sem.at[3]))
    stores[-1].start()
    for c in range(0, share, 256):
        dg_ref[c : c + 256] = t_dot(hid[:, c : c + 256], gm[...]).astype(bf16)
    stores.append(pltpu.make_async_copy(dg_ref, dg_out, own_sem.at[4]))
    stores[-1].start()
    for j in range(seq):
        at = slice(j * rows, (j + 1) * rows)
        nm[at] = dot(hid[at], wd_ref[...]).astype(bf16)
        stores.append(pltpu.make_async_copy(nm.at[pl.ds(j * rows, rows)], mo_ref.at[j], mo_sem.at[j]))
        stores[-1].start()
    have = [0]
    for n, bit in enumerate(high):
        if n:
            for j in have:
                for s in range(subs):
                    send(j, j ^ bit, bit, s)
        for j in have:
            for s in range(subs):
                db_copy(0, j ^ bit, bit, s).wait_recv()
                send(j ^ bit, j ^ bit ^ 1, 1, s)
        have += [j ^ bit for j in have]
    if seq > 1:
        for j in have:
            for s in range(subs):
                db_copy(0, j ^ 1, 1, s).wait_recv()
    if staged:
        combine(0)
        stores.append(pltpu.make_async_copy(tu, ug_out, own_sem.at[2]))
        stores[-1].start()
        drain_y(0)
    for c in sends:
        c.wait_send()
    for c in stores:
        c.wait()
    for bit in bits:
        for j in range(0, seq, 2 * bit):
            for s in range(subs):
                dn_copy(bit, j, s).wait_send()


def mlp(length, own, others, tok, grads, wo, wu, wd, gain, fsdp):
    seq, rows, dim = tok.shape
    share = wu.shape[1]
    lo = 2
    hi = fsdp // lo
    piece = dim // (seq * fsdp)
    staged = piece % 16 == 0
    up_shape = (hi, seq, piece, share) if staged else (dim, share)
    sub = 256
    depth = seq if seq <= 4 else 2
    anywhere = pl.BlockSpec(memory_space=pl.ANY)
    vmem = pl.BlockSpec(memory_space=pltpu.VMEM)
    dma = pltpu.SemaphoreType.DMA

    def buf(*shape):
        return pltpu.VMEM(shape, bf16)

    return pl.pallas_call(
        functools.partial(mlp_kernel, seq, hi, lo, sub),
        out_shape=(
            jax.ShapeDtypeStruct((rows, dim), f32),
            jax.ShapeDtypeStruct((rows, dim), f32),
            jax.ShapeDtypeStruct((8, dim), f32),
            jax.ShapeDtypeStruct((seq, rows, dim), bf16),
            jax.ShapeDtypeStruct((seq, rows, dim), bf16),
            jax.ShapeDtypeStruct(up_shape, bf16),
            jax.ShapeDtypeStruct((share, dim), bf16),
        ),
        in_specs=[pl.BlockSpec(memory_space=pltpu.SMEM)] + [anywhere] * 7 + [vmem],
        out_specs=(anywhere, anywhere, vmem, anywhere, anywhere, anywhere, anywhere),
        scratch_shapes=[
            buf(depth, seq, rows, dim // seq),
            buf(depth, rows, dim),
            buf(dim, dim),
            buf(dim, share),
            buf(share, dim),
            buf(seq * rows, dim),
            buf(seq * rows, dim),
            buf(seq * rows, share),
            buf(seq * rows, share),
            buf(seq, rows, dim),
            buf(max(seq - 1, 1), rows, dim),
            pltpu.VMEM((rows, dim), f32),
            pltpu.VMEM((rows, dim), f32),
            buf(seq, fsdp, piece, share) if staged else buf(dim, share),
            buf(share, dim),
            dma((depth, seq + 1)),
            dma((3,)),
            dma((seq,)),
            dma((seq, rows // sub)),
            dma((seq, rows // sub)),
            dma((seq, rows // sub)),
            dma((seq, rows // sub)),
            dma((seq,)),
            dma((5,)),
        ]
        + ([buf(*up_shape), buf(*up_shape), dma((1, hi)), dma((1, hi))] if staged else []),
        compiler_params=pltpu.CompilerParams(collective_id=2, has_side_effects=True, vmem_limit_bytes=62 << 20),
        cost_estimate=pl.CostEstimate(
            flops=2 * rows * seq * dim * (dim + 6 * share), bytes_accessed=32 << 20, transcendentals=rows * seq * share
        ),
        name="mlp",
    )(length, own, others, tok, grads, wo, wu, wd, gain)


def inverse_rms(values):
    return lax.rsqrt(jnp.mean(values * values, axis=-1, keepdims=True) + EPSILON)


def norm_back(values, gain, rho, grad):
    scaled = gain * grad
    mean = jnp.mean(values * scaled, axis=-1, keepdims=True)
    gain_grad = (grad * values * rho).reshape(-1, 8, values.shape[1])
    return rho * scaled - values * (rho * rho * rho * mean), jnp.sum(gain_grad, axis=0)


def body(
    tokens,
    lengths,
    state_init,
    w_qkv,
    w_out,
    w_up,
    w_down,
    norm_attn,
    norm_mlp,
    rel_bias,
    state_query,
    gate_bias,
    out_grad,
    state_grad,
):
    seq_count = lax.axis_size("seq")
    fsdp_count = lax.axis_size("fsdp")
    seq_at = lax.axis_index("seq")
    heads = H // seq_count
    width = heads * DH
    tok_rows, dim = tokens.shape[1:]
    rows = tok_rows * seq_count
    hidden_all = w_up.shape[1]
    share = hidden_all // (seq_count * fsdp_count)

    piece = dim // (seq_count * fsdp_count)
    all_tokens, all_grad, qkv_w, gain_attn, gain_mlp, own_out, up_w = gather_start(
        tokens[0],
        out_grad[0],
        w_qkv,
        norm_attn.reshape(1, -1),
        norm_mlp.reshape(1, -1),
        w_out.reshape(2, w_out.shape[0] // 2, dim),
        w_up,
        seq_count,
        fsdp_count,
    )
    qkv_w = qkv_w.reshape(dim, 3 * width)
    up_w = up_w.reshape(dim, hidden_all // seq_count)
    gain_attn = gain_attn.reshape(dim).astype(f32)
    gain_mlp = gain_mlp.reshape(dim).astype(f32)

    bias = bias_vector(rel_bias)
    forget = jax.nn.sigmoid(gate_bias)
    forget_row = forget.reshape(1, width)

    inputs = all_tokens.reshape(rows, dim).astype(f32)
    normed = (inputs * inverse_rms(inputs) * gain_attn).astype(bf16)
    qkv = dot(normed, qkv_w).astype(bf16)
    attended, others, out_w, down_w, final_memory, mem, upd, lse, slse = attend(
        qkv,
        state_init[0],
        lengths,
        state_query,
        forget_row,
        bias,
        own_out,
        w_down,
        heads,
        seq_count,
        fsdp_count,
    )
    out_w = out_w.reshape(dim, dim)
    own_out = lax.dynamic_slice_in_dim(out_w, seq_at * width, width, axis=0)
    mid_here, dmid, mlp_gain_grad, dbranch, mlp_parts, up_grad, down_grad = mlp(
        lengths, attended, others, all_tokens, all_grad, out_w, up_w, down_w, gain_mlp.reshape(1, dim), fsdp_count
    )
    if up_grad.ndim == 2:
        up_grad = up_grad.reshape(seq_count, fsdp_count, piece, hidden_all // seq_count)
    dqkv, small, up_part, down_part, out_part, output = attend_back(
        qkv,
        dbranch.reshape(rows, dim),
        own_out,
        attended,
        mem,
        upd,
        lse,
        slse,
        state_grad[0],
        lengths,
        state_query,
        forget_row,
        bias,
        up_grad,
        down_grad.reshape(fsdp_count, share, dim),
        mlp_parts,
        mid_here,
        seq_count,
        fsdp_count,
    )
    tokens_grad, qkv_part, dquery, grad_gate, grad_table, attn_gain_grad, mlp_gain_grad = finish(
        dqkv,
        qkv_w,
        normed,
        small,
        mlp_gain_grad,
        tokens[0],
        dmid,
        gain_attn.reshape(1, dim),
        seq_count,
        fsdp_count,
    )
    output = output[None]
    tokens_grad = tokens_grad[None]
    dquery = dquery.reshape(heads, DH, DH)
    attn_gain_grad = attn_gain_grad.reshape(piece)
    mlp_gain_grad = mlp_gain_grad.reshape(piece)
    return (
        output,
        final_memory[None],
        tokens_grad,
        qkv_part,
        out_part,
        up_part,
        down_part,
        attn_gain_grad,
        mlp_gain_grad,
        grad_table,
        dquery,
        grad_gate,
    )


def solution(mesh):
    placed = (
        P("fsdp", "seq", None),
        P("fsdp"),
        P("fsdp", None, "seq"),
        P("fsdp", None),
        P("fsdp", None),
        P("fsdp", None),
        P("fsdp", None),
        P("fsdp"),
        P("fsdp"),
        P("seq", None),
        P("seq", None, None),
        P("seq", None),
        P("fsdp", "seq", None),
        P("fsdp", None, "seq"),
    )
    return jax.shard_map(
        body,
        mesh=mesh,
        in_specs=placed,
        out_specs=(
            P("fsdp", "seq", None),
            P("fsdp", None, "seq"),
            P("fsdp", "seq", None),
            P(("seq", "fsdp"), None),
            P(("seq", "fsdp"), None),
            P(("seq", "fsdp"), None),
            P(("seq", "fsdp"), None),
            P(("seq", "fsdp")),
            P(("seq", "fsdp")),
            P("seq", None),
            P("seq", None, None),
            P("seq", None),
        ),
        check_vma=False,
    )
```

```python
import functools
import math

import jax
import jax.numpy as jnp
import numpy as np
from jax import lax
from jax.experimental import pallas as pl
from jax.experimental.pallas import tpu as pltpu
from jax.sharding import PartitionSpec as P

H = 8
DH = 128
BLOCK = 512
STATE_VECTORS = 512
QTILE = 256
SPAN = BLOCK + QTILE

EPSILON = 1e-06
BUCKET_EDGES = (19, 21, 24, 27, 31, 35, 40, 46, 52, 59, 67, 77, 87, 99, 113)
BUCKETS = 32
LOG2E = math.log2(math.e)
SCALE = DH ** (-0.5)
NEAR = 384

f32 = jnp.float32
bf16 = jnp.bfloat16
MESH = pl.DeviceIdType.MESH


def bucket_of(distance):
    return np.minimum(distance, 16) + (distance[..., None] >= np.array(BUCKET_EDGES)).sum(-1)


def tile_distance():
    rows = np.arange(QTILE)[:, None]
    cols = np.arange(SPAN)[None, :]
    return rows + BLOCK - cols


def bias_vector(table):
    distance = BLOCK - np.arange(2 * BLOCK)
    inside = (distance >= 0) & (distance < BLOCK)
    bucket = jnp.asarray(np.where(inside, bucket_of(np.clip(distance, 0, BLOCK)), BUCKETS).astype(np.int32))
    total = jnp.full((table.shape[0], 2 * BLOCK), -jnp.inf, f32)
    for i in range(BUCKETS):
        total = jnp.where((bucket == i)[None], table[:, i : i + 1] * LOG2E, total)
    return total


def tile_bias(vector_ref, head):
    wide = jnp.broadcast_to(vector_ref[head : head + 1, :], (QTILE, 2 * BLOCK))
    return pltpu.roll(wide, 0, 1, stride=1, stride_axis=0)[:, :SPAN]


def dot(a, b):
    return jnp.dot(a, b, preferred_element_type=f32)


def dot_t(a, b):
    return lax.dot_general(a, b, (((1,), (1,)), ((), ())), preferred_element_type=f32)


def t_dot(a, b):
    return lax.dot_general(a, b, (((0,), (0,)), ((), ())), preferred_element_type=f32)


def to_row(column):
    wide = jnp.broadcast_to(column, (column.shape[0], 128))
    return wide.T[0:1, :]


def context_pieces(tile):
    start = tile * QTILE
    pieces = []
    if start < BLOCK:
        pieces.append((0, start, BLOCK, 0))
    pieces.append((1, 0, start + QTILE, BLOCK - start))
    return pieces


def softmax_parts(scores):
    top = functools.reduce(jnp.maximum, [jnp.max(s, axis=-1, keepdims=True) for s in scores])
    raised = [jnp.exp2(s - top) for s in scores]
    total = functools.reduce(jnp.add, [jnp.sum(e, axis=-1, keepdims=True) for e in raised])
    return raised, total, top + jnp.log2(total)


def line_gather(hi, lo, slot, own, z_send, z_recv, y_send, y_recv):
    f = lax.axis_index("fsdp")
    z, y = f // lo, f % lo

    def copy(i, origin, target, send, recv, first=False):
        ref = slot(i, origin)
        return pltpu.make_async_remote_copy(
            src_ref=own(i) if first else ref,
            dst_ref=ref,
            send_sem=send,
            recv_sem=recv,
            device_id={"fsdp": target},
            device_id_type=MESH,
        )

    def right(i, t):
        return copy(i, (z - t) * lo + y, (z + 1) * lo + y, z_send.at[i, 0, t], z_recv.at[i, 0, t], t == 0)

    def left(i, t):
        return copy(i, (z + t) * lo + y, (z - 1) * lo + y, z_send.at[i, 1, t], z_recv.at[i, 1, t], t == 0)

    def across(i, d):
        return copy(
            i, (z + d) * lo + y, z * lo + 1 - y, y_send.at[i, d + hi - 1], y_recv.at[i, d + hi - 1], d == 0
        )

    def start(i):
        pl.when(z + 1 < hi)(lambda: right(i, 0).start())
        pl.when(z >= 1)(lambda: left(i, 0).start())
        across(i, 0).start()

    def step(i, t):
        @pl.when(z - 1 - t >= 0)
        def _():
            copy(i, (z - 1 - t) * lo + y, f, z_send.at[i, 0, t], z_recv.at[i, 0, t]).wait_recv()
            if t + 1 < hi - 1:
                pl.when(z + 1 < hi)(lambda: right(i, t + 1).start())
            across(i, -1 - t).start()

        @pl.when(z + 1 + t < hi)
        def _():
            copy(i, (z + 1 + t) * lo + y, f, z_send.at[i, 1, t], z_recv.at[i, 1, t]).wait_recv()
            if t + 1 < hi - 1:
                pl.when(z >= 1)(lambda: left(i, t + 1).start())
            across(i, 1 + t).start()

    def arrive(i):
        for d in range(1 - hi, hi):

            @pl.when((z + d >= 0) & (z + d < hi))
            def _():
                copy(
                    i, (z + d) * lo + 1 - y, f, y_send.at[i, d + hi - 1], y_recv.at[i, d + hi - 1]
                ).wait_recv()

    def drain(i):
        for d in range(1 - hi, hi):

            @pl.when((z + d >= 0) & (z + d < hi))
            def _():
                across(i, d).wait_send()

        for t in range(hi - 1):

            @pl.when((z + 1 < hi) & (z - t >= 0))
            def _():
                right(i, t).wait_send()

            @pl.when((z >= 1) & (z + t < hi))
            def _():
                left(i, t).wait_send()

    return start, step, arrive, drain


def line_sems(count, hi):
    dma = pltpu.SemaphoreType.DMA
    return [dma((count, 2, hi)), dma((count, 2, hi)), dma((count, 2 * hi)), dma((count, 2 * hi))]


def greet(seq_targets, hi, lo):
    me = lax.axis_index("seq")
    f = lax.axis_index("fsdp")
    z, y = f // lo, f % lo
    barrier = pltpu.get_barrier_semaphore()
    for k in seq_targets:
        pl.semaphore_signal(barrier, inc=1, device_id={"seq": me ^ k}, device_id_type=MESH)
    near = (lax.rem(z + 1, hi) * lo + y, lax.rem(z + hi - 1, hi) * lo + y, z * lo + 1 - y)
    for target in near:
        pl.semaphore_signal(barrier, inc=1, device_id={"fsdp": target}, device_id_type=MESH)
    pl.semaphore_wait(barrier, len(seq_targets) + len(near))


def attend_kernel(
    heads,
    seq,
    hi,
    lo,
    length_ref,
    qkv_ref,
    init_ref,
    query_ref,
    forget_ref,
    vector_ref,
    own_out_ref,
    own_down_ref,
    att_out,
    others_ref,
    outs_ref,
    downs_ref,
    final_ref,
    mem_out,
    upd_out,
    lse_ref,
    slse_ref,
    memory_ref,
    bias_ref,
    att_ref,
    mem_ref,
    upd_ref,
    store_sem,
    own_sem,
    att_send,
    att_recv,
    out_send,
    out_recv,
    z_send,
    z_recv,
    y_send,
    y_recv,
):
    me = lax.axis_index("seq")
    f = lax.axis_index("fsdp")
    length = length_ref[0]
    width = heads * DH
    scale2 = SCALE * LOG2E
    blocks = seq
    bits = [1 << i for i in range(seq.bit_length() - 1)]
    greet(bits, hi, lo)

    own_copies = [
        pltpu.make_async_copy(own_down_ref, downs_ref.at[f], own_sem.at[0]),
        pltpu.make_async_copy(own_out_ref, outs_ref.at[:, me % 2], own_sem.at[1]),
    ]
    for c in own_copies:
        c.start()

    def lowest(k):
        return k & -k

    def out_copy(sending):
        half = me % 2 if sending else 1 - me % 2
        return pltpu.make_async_remote_copy(
            src_ref=own_out_ref,
            dst_ref=outs_ref.at[:, half],
            send_sem=out_send,
            recv_sem=out_recv,
            device_id={"seq": me ^ 1},
            device_id_type=MESH,
        )

    def att_copy(k, b):
        bit = lowest(k)
        came = k ^ bit
        here = pl.ds(pl.multiple_of((b ^ me) * BLOCK, BLOCK), BLOCK)
        there = pl.ds(pl.multiple_of((b ^ me ^ bit) * BLOCK, BLOCK), BLOCK)
        src = others_ref.at[came, here] if came else att_ref.at[here]
        return pltpu.make_async_remote_copy(
            src_ref=src,
            dst_ref=others_ref.at[k, there],
            send_sem=att_send.at[k, b],
            recv_sem=att_recv.at[k, b],
            device_id={"seq": me ^ bit},
            device_id_type=MESH,
        )

    def att_arrival(k, b):
        here = pl.ds(pl.multiple_of((b ^ me) * BLOCK, BLOCK), BLOCK)
        return pltpu.make_async_remote_copy(
            src_ref=others_ref.at[k, here],
            dst_ref=others_ref.at[k, here],
            send_sem=att_send.at[k, b],
            recv_sem=att_recv.at[k, b],
            device_id={"seq": me},
            device_id_type=MESH,
        )

    passing = sorted([k for k in range(2, seq, 2)], key=lambda k: (bin(k).count("1"), -k))

    def onward(k, send):
        for bit in reversed(bits):
            if bit < lowest(k):
                send(k | bit)

    start, step, arrive, drain = line_gather(
        hi, lo, lambda i, origin: downs_ref.at[origin], lambda i: own_down_ref, z_send, z_recv, y_send, y_recv
    )

    start(0)
    out_copy(True).start()
    memory_ref[...] = init_ref[...].astype(f32)
    for head in range(heads):
        bias_ref[head] = tile_bias(vector_ref, head)

    def block_stores(block):
        at = pl.ds(pl.multiple_of((block ^ me) * BLOCK, BLOCK), BLOCK)
        pairs = (
            (att_ref.at[at], att_out.at[at]),
            (mem_ref.at[block], mem_out.at[block]),
            (upd_ref.at[block], upd_out.at[block]),
        )
        return [pltpu.make_async_copy(a, b, store_sem.at[i, block]) for i, (a, b) in enumerate(pairs)]

    @pl.loop(0, blocks)
    def _(block):
        cur_at = pl.multiple_of((block ^ me) * BLOCK, BLOCK)
        prev_at = pl.multiple_of((jnp.maximum(block - 1, 0) ^ me) * BLOCK, BLOCK)
        cur_ref = qkv_ref.at[pl.ds(cur_at, BLOCK)]
        prev_ref = qkv_ref.at[pl.ds(prev_at, BLOCK)]
        for t in range(min(hi - 1, blocks - 1)):
            pl.when(block == t + 1)(lambda t=t: step(0, t))

        live_block = block * BLOCK < length
        for head in range(heads):
            own = slice(head * DH, (head + 1) * DH)
            memory = memory_ref[:, own]
            low = memory.astype(bf16)
            mem_ref[block, :, own] = memory
            refs = (prev_ref, cur_ref)
            key_cols = slice(width + head * DH, width + (head + 1) * DH)
            value_cols = slice(2 * width + head * DH, 2 * width + (head + 1) * DH)
            for tile in range(BLOCK // QTILE):
                rows = slice(tile * QTILE, (tile + 1) * QTILE)
                query = cur_ref[rows, own]
                scores, values = [], []
                for which, at, end, col in context_pieces(tile):
                    s = dot_t(query, refs[which][at:end, key_cols])
                    position = (block - 1 + which) * BLOCK + at + lax.broadcasted_iota(jnp.int32, (1, end - at), 1)
                    live = (position >= 0) & (position < length)
                    s = s * scale2 + bias_ref[head, :, col : col + end - at]
                    scores.append(jnp.where(live, s, -jnp.inf))
                    values.append(refs[which][at:end, value_cols])
                scores.append(dot_t(query, low) * scale2)
                values.append(low)
                raised, total, lse = softmax_parts(scores)
                out = functools.reduce(jnp.add, [dot(e.astype(bf16), v) for e, v in zip(raised, values)])
                att_ref[pl.ds(cur_at + tile * QTILE, QTILE), own] = (out / total).astype(bf16)
                lse_ref[head : head + 1, pl.ds(pl.multiple_of(block * BLOCK, BLOCK) + tile * QTILE, QTILE)] = to_row(lse)
            own_key = cur_ref[:, key_cols]
            own_value = cur_ref[:, value_cols]
            squeries = dot(low, query_ref[head]).astype(bf16)
            position = block * BLOCK + lax.broadcasted_iota(jnp.int32, (1, BLOCK), 1)
            for tile in range(STATE_VECTORS // QTILE):
                rows = slice(tile * QTILE, (tile + 1) * QTILE)
                squery = squeries[rows]
                scores = [
                    dot_t(squery, low) * scale2,
                    jnp.where(position < length, dot_t(squery, own_key) * scale2, -jnp.inf),
                ]
                raised, total, lse = softmax_parts(scores)
                update = dot(raised[0].astype(bf16), low) + dot(raised[1].astype(bf16), own_value)
                update = update / total
                upd_ref[block, rows, own] = update
                slse_ref[head : head + 1, pl.ds(pl.multiple_of(block * BLOCK, BLOCK) + tile * QTILE, QTILE)] = to_row(
                    lse
                )
                forget = forget_ref[:, own]
                old = memory[rows]
                memory_ref[rows, own] = jnp.where(live_block, forget * old + (1.0 - forget) * update, old)

        for bit in reversed(bits):
            att_copy(bit, block).start()
        for c in block_stores(block):
            c.start()

        @pl.when(block >= 1)
        def _():
            for k in passing:
                att_arrival(k, block - 1).wait_recv()
                onward(k, lambda target: att_copy(target, block - 1).start())

    final_ref[...] = memory_ref[...]
    for t in range(min(hi - 1, blocks - 1), hi - 1):
        step(0, t)
    for k in passing:
        att_arrival(k, blocks - 1).wait_recv()
        onward(k, lambda target: att_copy(target, blocks - 1).start())
    arrive(0)
    out_copy(False).wait_recv()
    for k in range(1, seq, 2):
        for b in range(blocks):
            att_arrival(k, b).wait_recv()
    for c in own_copies:
        c.wait()
    drain(0)
    for b in range(blocks):
        for c in block_stores(b):
            c.wait()
    out_copy(True).wait_send()
    for k in range(1, seq):
        for b in range(blocks):
            att_copy(k, b).wait_send()


def attend(qkv, init, length, state_query, forget, bias, own_out, own_down, heads, seq, fsdp):
    rows, width3 = qkv.shape
    width = heads * DH
    blocks = rows // BLOCK
    lo = 2
    hi = fsdp // lo
    dim = own_down.shape[1]
    anywhere = pl.BlockSpec(memory_space=pl.ANY)
    vmem = pl.BlockSpec(memory_space=pltpu.VMEM)
    dma = pltpu.SemaphoreType.DMA
    return pl.pallas_call(
        functools.partial(attend_kernel, heads, seq, hi, lo),
        out_shape=(
            jax.ShapeDtypeStruct((rows, width), bf16),
            jax.ShapeDtypeStruct((seq, rows, width), bf16),
            jax.ShapeDtypeStruct((fsdp, 2) + own_out.shape[1:], bf16),
            jax.ShapeDtypeStruct((fsdp,) + own_down.shape, bf16),
            jax.ShapeDtypeStruct((STATE_VECTORS, width), f32),
            jax.ShapeDtypeStruct((blocks, STATE_VECTORS, width), f32),
            jax.ShapeDtypeStruct((blocks, STATE_VECTORS, width), f32),
            jax.ShapeDtypeStruct((heads, rows), f32),
            jax.ShapeDtypeStruct((heads, blocks * STATE_VECTORS), f32),
        ),
        in_specs=[pl.BlockSpec(memory_space=pltpu.SMEM)] + [vmem] * 7,
        out_specs=(anywhere, anywhere, anywhere, anywhere, vmem, anywhere, anywhere, vmem, vmem),
        scratch_shapes=[
            pltpu.VMEM((STATE_VECTORS, width), f32),
            pltpu.VMEM((heads, QTILE, SPAN), f32),
            pltpu.VMEM((rows, width), bf16),
            pltpu.VMEM((blocks, STATE_VECTORS, width), f32),
            pltpu.VMEM((blocks, STATE_VECTORS, width), f32),
            dma((3, blocks)),
            dma((2,)),
            dma((seq, blocks)),
            dma((seq, blocks)),
            dma,
            dma,
        ]
        + line_sems(1, hi),
        compiler_params=pltpu.CompilerParams(collective_id=3, has_side_effects=True, vmem_limit_bytes=60 << 20),
        cost_estimate=pl.CostEstimate(
            flops=blocks * heads * 512 * 2400 * 128 * 4, bytes_accessed=16 << 20, transcendentals=10 << 20
        ),
        name="attend",
    )(length, qkv, init, state_query, forget, bias, own_out, own_down)


def line_reduce(hi, lo, block, total, from_y, from_z, z_send, z_recv, y_send, y_recv, loads=None):
    loads = loads or {}
    f = lax.axis_index("fsdp")
    z, y = f // lo, f % lo

    def remote(src, dst, send, recv, target):
        return pltpu.make_async_remote_copy(
            src_ref=src, dst_ref=dst, send_sem=send, recv_sem=recv, device_id={"fsdp": target}, device_id_type=MESH
        )

    def across(i, d):
        return remote(
            block(i, d * lo + 1 - y), from_y[i].at[d], y_send.at[i, d], y_recv.at[i, d], z * lo + 1 - y
        )

    def start(i):
        for d in range(hi):
            across(i, d).start()

    def combine(i):
        for d in range(hi):
            across(i, d).wait_recv()
            if i in loads:
                loads[i][d].wait()
                own = total[i].at[d]
            else:
                own = block(i, d * lo + y)
            total[i][d] = (own[...].astype(f32) + from_y[i][d].astype(f32)).astype(bf16)

    def hop(i, side, t, at, target):
        return remote(
            total[i].at[jnp.clip(at, 0, hi - 1)],
            from_z[i].at[side, t],
            z_send.at[i, side, t],
            z_recv.at[i, side, t],
            target,
        )

    def sending(t):
        d = t - (hi - 1 - z)
        m = hi - 1 - (t - z)
        return ((0, d, (d >= 0) & (d < z), z - 1), (1, m, (m > z) & (m < hi), z + 1))

    def zsend(i, t):
        for side, at, cond, target in sending(t):
            pl.when(cond)(lambda: hop(i, side, t, at, target * lo + y).start())

    def zrecv(i, t):
        d = t - (hi - 2 - z)
        m = hi - 1 - (t - (z - 1))
        for side, at, cond in ((0, d, (z + 1 < hi) & (d >= 0)), (1, m, (z > 0) & (m < hi))):

            @pl.when(cond)
            def _():
                hop(i, side, t, at, f).wait_recv()
                slot = jnp.clip(at, 0, hi - 1)
                total[i][slot] = (total[i][slot].astype(f32) + from_z[i][side, t].astype(f32)).astype(bf16)

    def drain_y(i):
        for d in range(hi):
            across(i, d).wait_send()

    def drain_z(i):
        for t in range(hi - 1):
            for side, at, cond, target in sending(t):
                pl.when(cond)(lambda: hop(i, side, t, at, f).wait_send())

    return start, combine, zsend, zrecv, drain_y, drain_z


def seq_levels(seq):
    bits = [1 << i for i in range(seq.bit_length() - 1)]
    slots = {}
    for bit in bits:
        for j in range(0, seq, 2 * bit):
            slots[bit, j] = len(slots)
    return bits, slots


def diagonal_sums(tile):
    rows, lanes = tile.shape
    wide = jnp.concatenate([tile, jnp.zeros((rows, lanes), f32)], axis=1)
    row = lax.broadcasted_iota(jnp.int32, wide.shape, 0)
    bit = 1
    while bit < rows:
        wide = jnp.where((row & bit) != 0, pltpu.roll(wide, 2 * lanes - bit, 1), wide)
        bit *= 2
    return jnp.sum(wide, axis=0, keepdims=True)


def attend_back_kernel(heads, seq, hi, lo, inside, length_ref, *refs):
    refs = list(refs)

    def take(count):
        taken = refs[:count]
        del refs[:count]
        return taken

    qkv_hbm, db_hbm, wout_ref, att_hbm, mem_hbm, upd_hbm, lse_ref, slse_ref = take(8)
    sgrad_ref, query_ref, forget_ref, vector_ref, up_ref, down_ref, mo_ref, mid_hbm = take(8)
    ow_in = None if inside else take(1)[0]
    dqkv_out, small_ref, upart_ref, dtotal_ref, opart_ref, output_ref = take(6)
    qkv_ref, db_ref, att_ref, mem_ref, upd_ref, mid_ref, dqkv_ref = take(7)
    dmem_ref, dnext_ref, dctx_ref, bias_ref, near_ref, far_ref, dout_ref, ow_buf = take(8)
    moved, to, tu, yo, yu, yd, zo, zu, xu, mo_low, mo_in = take(11)
    z_send, z_recv, y_send, y_recv, m_send, m_recv, e_send, e_recv, x_send, x_recv = take(10)
    load_sem, block_sem, up_sem, mo_sem, out_sem = take(5)
    ow_ref = ow_buf if inside else ow_in

    me = lax.axis_index("seq")
    f = lax.axis_index("fsdp")
    z, y = f // lo, f % lo
    blocks = seq
    length = length_ref[0]
    width = heads * DH
    scale2 = SCALE * LOG2E
    tok_rows = mid_ref.shape[0]
    share = dtotal_ref.shape[1]
    bits, slots = seq_levels(seq)

    def chunk_at(block):
        return pl.ds(pl.multiple_of((block ^ me) * BLOCK, BLOCK), BLOCK)

    def block_loads(block):
        at = chunk_at(block)
        pairs = (
            (qkv_hbm.at[at], qkv_ref.at[at]),
            (mem_hbm.at[block], mem_ref.at[block]),
            (upd_hbm.at[block], upd_ref.at[block]),
        )
        return [pltpu.make_async_copy(a, b, block_sem.at[i, block]) for i, (a, b) in enumerate(pairs)]

    loads = [
        pltpu.make_async_copy(att_hbm, att_ref, load_sem.at[0]),
        pltpu.make_async_copy(db_hbm, db_ref, load_sem.at[1]),
        pltpu.make_async_copy(down_ref.at[me], moved.at[me], load_sem.at[2]),
        pltpu.make_async_copy(mid_hbm, mid_ref, load_sem.at[3]),
    ]
    up_loads = [
        pltpu.make_async_copy(up_ref.at[d] if inside else up_ref.at[:, d * lo + y], tu.at[d], up_sem.at[d])
        for d in range(hi)
    ]
    mo_loads = [pltpu.make_async_copy(mo_ref.at[j], mo_low.at[j // 2], mo_sem.at[j // 2]) for j in range(0, seq, 2)]
    for c in up_loads + loads[:2] + block_loads(blocks - 1) + mo_loads:
        c.start()
    for b in reversed(range(blocks - 1)):
        for c in block_loads(b):
            c.start()
    for c in loads[2:]:
        c.start()
    greet(list(range(1, seq)), hi, lo)

    def mo_copy(bit, j):
        slot = slots[bit, j]
        return pltpu.make_async_remote_copy(
            src_ref=mo_ref.at[j ^ bit] if bit == 1 else mo_low.at[(j ^ bit) // 2],
            dst_ref=mo_in.at[slot],
            send_sem=m_send.at[slot],
            recv_sem=m_recv.at[slot],
            device_id={"seq": me ^ bit},
            device_id_type=MESH,
        )

    def move_copy(k):
        return pltpu.make_async_remote_copy(
            src_ref=down_ref.at[me ^ k],
            dst_ref=moved.at[me],
            send_sem=e_send.at[k],
            recv_sem=e_recv.at[k],
            device_id={"seq": me ^ k},
            device_id_type=MESH,
        )

    def move_arrival(k):
        return pltpu.make_async_remote_copy(
            src_ref=down_ref.at[me],
            dst_ref=moved.at[me ^ k],
            send_sem=e_send.at[k],
            recv_sem=e_recv.at[k],
            device_id={"seq": me},
            device_id_type=MESH,
        )

    def block_of(i, target):
        if i == 0:
            return ow_ref.at[target]
        if i == 1:
            return up_ref.at[:, target]
        return moved.at[target % seq, pl.ds(pl.multiple_of((target // seq) * share, share), share)]

    start, combine, zsend, zrecv, drain_y, drain_z = line_reduce(
        hi,
        lo,
        block_of,
        (to, tu, dtotal_ref),
        (yo, yu, yd),
        (zo, zu),
        z_send,
        z_recv,
        y_send,
        y_recv,
        {1: up_loads},
    )

    def exchange(k, sending):
        return pltpu.make_async_remote_copy(
            src_ref=tu.at[z, me ^ k] if sending else tu.at[z, me],
            dst_ref=xu.at[me] if sending else xu.at[me ^ k],
            send_sem=x_send.at[k],
            recv_sem=x_recv.at[k],
            device_id={"seq": me ^ k if sending else me},
            device_id_type=MESH,
        )

    if not inside:
        start(1)
    for k in reversed(range(1, seq)):
        move_copy(k).start()
    for j in range(seq - 1, 0, -2):
        mo_copy(1, j ^ 1).start()
    if inside:
        for c in up_loads:
            c.wait()
        zsend(1, 0)
    dmem_ref[...] = sgrad_ref[...].astype(f32)
    dnext_ref[...] = jnp.zeros_like(dnext_ref)
    small_ref[...] = jnp.zeros_like(small_ref)
    near_ref[...] = jnp.zeros_like(near_ref)
    far_ref[...] = jnp.zeros_like(far_ref)
    for head in range(heads):
        bias_ref[head] = tile_bias(vector_ref, head).T
    for c in loads[:2]:
        c.wait()
    if inside:
        full = t_dot(att_ref[...], db_ref[...]).astype(bf16)
        ow_buf[...] = full.reshape(ow_buf.shape)
    start(0)

    def mo_step(j):
        mo_loads[j // 2].wait()
        for bit in bits:
            if j & bit:
                mo_copy(bit, j ^ bit).start()
                break
            mo_copy(bit, j).wait_recv()
            own = mo_low[j // 2].astype(f32)
            mo_low[j // 2] = (own + mo_in[slots[bit, j]].astype(f32)).astype(bf16)

    def down_ready():
        for k in range(1, seq):
            move_arrival(k).wait_recv()
        loads[2].wait()
        start(2)

    def up_done():
        for k in range(1, seq):
            exchange(k, True).start()

    def zstep(i, t):
        zrecv(i, t)
        if t + 1 < hi - 1:
            zsend(i, t + 1)

    jobs = [lambda j=j: mo_step(j) for j in range(seq - 2, 0, -2)]
    if not inside:
        jobs.append(lambda: (combine(1), zsend(1, 0)))
    jobs.append(lambda: (zstep(1, 0), combine(0), zsend(0, 0)))
    for t in range(1, hi - 1):
        jobs.append(lambda t=t: zstep(1, t))
        if t == 1:
            jobs.append(lambda: down_ready())
    jobs.append(lambda: up_done())
    jobs += [lambda t=t: zstep(0, t) for t in range(hi - 1)]
    points = blocks * heads - 1

    dq_row = heads * DH
    block_loads(blocks - 1)[0].wait()

    @pl.loop(0, blocks)
    def _(step):
        block = blocks - 1 - step
        pl.when(block >= 1)(lambda: block_loads(jnp.maximum(block - 1, 0))[0].wait())
        for c in block_loads(block)[1:]:
            c.wait()
        cur_at = pl.multiple_of((block ^ me) * BLOCK, BLOCK)
        prev_at = pl.multiple_of((jnp.maximum(block - 1, 0) ^ me) * BLOCK, BLOCK)
        base = pl.multiple_of(block * BLOCK, BLOCK)
        cur_ref = qkv_ref.at[pl.ds(cur_at, BLOCK)]
        prev_ref = qkv_ref.at[pl.ds(prev_at, BLOCK)]
        live_block = block * BLOCK < length
        refs = (prev_ref, cur_ref)
        dout_ref[...] = dot_t(db_ref[pl.ds(cur_at, BLOCK)], wout_ref[...]).astype(bf16)
        for head in range(heads):
            for n, job in enumerate(jobs[:points]):
                if (n + 1) % heads == head:
                    pl.when(step == (n + 1) // heads)(lambda job=job: (job(), None)[1])
            own = slice(head * DH, (head + 1) * DH)
            key_cols = slice(width + head * DH, width + (head + 1) * DH)
            value_cols = slice(2 * width + head * DH, 2 * width + (head + 1) * DH)
            memory = mem_ref[block, :, own]
            update = upd_ref[block, :, own]
            low = memory.astype(bf16)
            forget = forget_ref[:, own]
            dmem = dmem_ref[:, own]
            dupd = jnp.where(live_block, (1.0 - forget) * dmem, 0.0).astype(bf16)
            gone = jnp.where(live_block, dmem * (memory - update), 0.0)
            small_ref[dq_row + head : dq_row + head + 1, :] += jnp.sum(gone, axis=0, keepdims=True)
            dmem_new = jnp.where(live_block, forget * dmem, dmem)
            own_key = cur_ref[:, key_cols]
            own_value = cur_ref[:, value_cols]
            squeries = dot(low, query_ref[head]).astype(bf16)
            sdelta = jnp.sum((dupd.astype(f32) * update).T, axis=0, keepdims=True)
            slse = slse_ref[head : head + 1, pl.ds(base, BLOCK)]
            dsquery = jnp.zeros((STATE_VECTORS, DH), f32)
            dkey = []
            dvalue = []
            for part in range(2 * STATE_VECTORS // QTILE):
                own_part = part >= STATE_VECTORS // QTILE
                at = (part % (STATE_VECTORS // QTILE)) * QTILE
                keys = (own_key if own_part else low)[at : at + QTILE]
                values = (own_value if own_part else low)[at : at + QTILE]
                s = dot_t(keys, squeries) * scale2 - slse
                if own_part:
                    position = block * BLOCK + at + lax.broadcasted_iota(jnp.int32, (QTILE, 1), 0)
                    s = jnp.where(position < length, s, -jnp.inf)
                p = jnp.exp2(s)
                dp = dot_t(values, dupd)
                ds = (p * (dp - sdelta)).astype(bf16)
                dvalue.append(dot(p.astype(bf16), dupd))
                dkey.append(dot(ds, squeries))
                dsquery += t_dot(ds, keys)
            half = STATE_VECTORS // QTILE
            dlow = [dvalue[i] + dkey[i] * SCALE for i in range(half)]
            dctx_ref[0, 0:BLOCK] = jnp.zeros((BLOCK, DH), f32)
            dctx_ref[1, 0:BLOCK] = jnp.zeros((BLOCK, DH), f32)
            for i in range(half):
                rows = slice(BLOCK + i * QTILE, BLOCK + (i + 1) * QTILE)
                old = slice(i * QTILE, (i + 1) * QTILE)
                dctx_ref[0, rows] = dkey[half + i] * SCALE + dnext_ref[0, old, own]
                dctx_ref[1, rows] = dvalue[half + i] + dnext_ref[1, old, own]
            dsq = (dsquery * SCALE).astype(bf16)
            small_ref[head * DH : (head + 1) * DH, :] += t_dot(low, dsq)
            dmem_ref[:, own] = dmem_new + dot_t(dsq, query_ref[head])
            for tile in range(BLOCK // QTILE):
                rows = slice(tile * QTILE, (tile + 1) * QTILE)
                here = pl.ds(cur_at + tile * QTILE, QTILE)
                query = cur_ref[rows, own]
                dout = dout_ref[rows, own]
                lse = lse_ref[head : head + 1, pl.ds(base + tile * QTILE, QTILE)]
                delta = jnp.sum((dout.astype(f32) * att_ref[here, own].astype(f32)).T, axis=0, keepdims=True)
                dq = jnp.zeros((QTILE, DH), f32)
                for which, first, end, col in context_pieces(tile):
                    for at in range(first, end, QTILE):
                        keys = refs[which][at : at + QTILE, key_cols]
                        values = refs[which][at : at + QTILE, value_cols]
                        band = col + at - first
                        position = (block - 1 + which) * BLOCK + at + lax.broadcasted_iota(jnp.int32, (QTILE, 1), 0)
                        live = (position >= 0) & (position < length)
                        s = dot_t(keys, query) * scale2 + bias_ref[head, band : band + QTILE, :] - lse
                        p = jnp.exp2(jnp.where(live, s, -jnp.inf))
                        dp = dot_t(values, dout)
                        ds = (p * (dp - delta)).astype(bf16)
                        wide = ds.astype(f32)
                        edge = min(max(SPAN - NEAR - band, 0), QTILE)
                        if edge:
                            far_ref[head] += functools.reduce(jnp.add, [wide[i : i + 8] for i in range(0, edge, 8)])
                        if edge < QTILE:
                            at_near = band + edge - (SPAN - NEAR)
                            near_ref[head, at_near : at_near + QTILE - edge] += wide[edge:]
                        into = slice(which * BLOCK + at, which * BLOCK + at + QTILE)
                        dctx_ref[1, into] += dot(p.astype(bf16), dout)
                        dctx_ref[0, into] += dot(ds, query) * SCALE
                        dq += t_dot(ds, keys)
                for part in range(half):
                    keys = low[part * QTILE : (part + 1) * QTILE]
                    s = dot_t(keys, query) * scale2 - lse
                    p = jnp.exp2(s)
                    dp = dot_t(keys, dout)
                    ds = (p * (dp - delta)).astype(bf16)
                    dlow[part] += dot(p.astype(bf16), dout) + dot(ds, query) * SCALE
                    dq += t_dot(ds, keys)
                dqkv_ref[here, own] = (dq * SCALE).astype(bf16)
            for part in range(half):
                dmem_ref[part * QTILE : (part + 1) * QTILE, own] += dlow[part]
            dnext_ref[0, :, own] = dctx_ref[0, 0:BLOCK]
            dnext_ref[1, :, own] = dctx_ref[1, 0:BLOCK]
            dqkv_ref[pl.ds(cur_at, BLOCK), key_cols] = dctx_ref[0, BLOCK:].astype(bf16)
            dqkv_ref[pl.ds(cur_at, BLOCK), value_cols] = dctx_ref[1, BLOCK:].astype(bf16)

    dqkv_store = pltpu.make_async_copy(dqkv_ref, dqkv_out, out_sem)
    dqkv_store.start()
    for job in jobs[points:]:
        job()
    member = bucket_members()
    lane = lax.broadcasted_iota(jnp.int32, (1, DH), 1)
    for head in range(heads):
        sums = jnp.broadcast_to(diagonal_sums(near_ref[head]), (8, 2 * QTILE))
        table = jnp.dot(sums, member, precision=lax.Precision.HIGHEST, preferred_element_type=f32)[0:1]
        total = jnp.sum(jnp.sum(far_ref[head], axis=0, keepdims=True), axis=1, keepdims=True)
        row = dq_row + heads + head
        small_ref[row : row + 1, :] = table + jnp.where(lane == BUCKETS - 1, total, 0.0)
        row = dq_row + head
        forget = forget_ref[:, head * DH : (head + 1) * DH]
        small_ref[row : row + 1, :] = small_ref[row : row + 1, :] * forget * (1.0 - forget)
    loads[3].wait()
    mo_loads[0].wait()
    for bit in bits:
        mo_copy(bit, 0).wait_recv()
    step = 128
    for r in range(0, tok_rows, step):
        at = slice(r, r + step)
        value = mid_ref[at] + mo_low[0, at].astype(f32)
        for bit in bits:
            value = value + mo_in[slots[bit, 0], at].astype(f32)
        position = me * tok_rows + r + lax.broadcasted_iota(jnp.int32, (step, 1), 0)
        output_ref[at] = (value * jnp.where(position < length, 1.0, 0.0)).astype(bf16)
    combine(2)
    opart_ref[...] = to[z].astype(f32)
    for k in range(1, seq):
        exchange(k, False).wait_recv()
    xu[me] = tu[z, me]
    write_parts(upart_ref, xu, seq, share)
    for i in (0, 2) if inside else (0, 1, 2):
        drain_y(i)
    for i in range(2):
        drain_z(i)
    for bit in bits:
        for j in range(0, seq, 2 * bit):
            mo_copy(bit, j).wait_send()
    for k in range(1, seq):
        move_copy(k).wait_send()
        exchange(k, True).wait_send()
    dqkv_store.wait()


def bucket_members():
    shape = (2 * QTILE, DH)
    row = lax.broadcasted_iota(jnp.int32, shape, 0)
    lane = lax.broadcasted_iota(jnp.int32, shape, 1)
    distance = jnp.where(row < QTILE, row, row - 2 * QTILE) + NEAR - QTILE
    bucket = jnp.minimum(distance, 16)
    for edge in BUCKET_EDGES:
        bucket = bucket + jnp.where(distance >= edge, 1, 0)
    inside = (distance >= 0) & (distance < BLOCK) & (bucket == lane)
    return jnp.where(inside, 1.0, 0.0)


def write_parts(out_ref, pieces, seq, unit):
    if len(out_ref.shape) == 3:
        out_ref[...] = pieces[...].astype(f32)
        return
    count = pieces.shape[2] // unit
    for k in range(seq):
        for c in range(count):
            at = (c * seq + k) * unit
            out_ref[:, at : at + unit] = pieces[k, :, c * unit : (c + 1) * unit].astype(f32)


def attend_back(
    qkv, db, wout, att, mem, upd, lse, slse, sgrad, length, state_query, forget, bias, up, down, mo, mid, seq, fsdp
):
    rows, width3 = qkv.shape
    width = width3 // 3
    heads = width // DH
    dim = db.shape[1]
    lo = 2
    hi = fsdp // lo
    piece, hidden = up.shape[2:]
    share = hidden // fsdp
    tok_rows = mid.shape[0]
    inside = piece % 16 == 0
    blocks = (piece, dim), (seq, piece, hidden), (share, dim)
    small_rows = heads * (DH + 2)
    small_rows += -small_rows % 8
    vmem = pl.BlockSpec(memory_space=pltpu.VMEM)
    anywhere = pl.BlockSpec(memory_space=pl.ANY)
    dma = pltpu.SemaphoreType.DMA

    def buf(*shape):
        return pltpu.VMEM(shape, bf16)

    extra = []
    if not inside:
        extra.append(t_dot(att, db).astype(bf16).reshape(fsdp, piece, dim))
    upart = (piece, hidden * seq) if share % 128 == 0 else (seq, piece, hidden)
    return pl.pallas_call(
        functools.partial(attend_back_kernel, heads, seq, hi, lo, inside),
        out_shape=(
            jax.ShapeDtypeStruct((rows, width3), bf16),
            jax.ShapeDtypeStruct((small_rows, DH), f32),
            jax.ShapeDtypeStruct(upart, f32),
            jax.ShapeDtypeStruct((hi, share, dim), bf16),
            jax.ShapeDtypeStruct((piece, dim), f32),
            jax.ShapeDtypeStruct((tok_rows, dim), bf16),
        ),
        in_specs=[pl.BlockSpec(memory_space=pltpu.SMEM), anywhere, anywhere, vmem]
        + [anywhere] * 3
        + [vmem] * 6
        + [anywhere] * 4
        + [vmem] * len(extra),
        out_specs=(anywhere,) + (vmem,) * 5,
        scratch_shapes=[
            buf(rows, width3),
            buf(rows, dim),
            buf(rows, width),
            pltpu.VMEM(mem.shape, f32),
            pltpu.VMEM(upd.shape, f32),
            pltpu.VMEM((tok_rows, dim), f32),
            buf(rows, width3),
            pltpu.VMEM((STATE_VECTORS, width), f32),
            pltpu.VMEM((2, BLOCK, width), f32),
            pltpu.VMEM((2, 2 * BLOCK, DH), f32),
            pltpu.VMEM((heads, SPAN, QTILE), f32),
            pltpu.VMEM((heads, NEAR, QTILE), f32),
            pltpu.VMEM((heads, 8, QTILE), f32),
            buf(BLOCK, width),
            buf(fsdp, piece, dim),
            buf(*down.shape),
            buf(hi, *blocks[0]),
            buf(hi, *blocks[1]),
            buf(hi, *blocks[0]),
            buf(16, 128) if inside else buf(hi, *blocks[1]),
            buf(hi, *blocks[2]),
            buf(2, max(hi - 1, 1), *blocks[0]),
            buf(2, max(hi - 1, 1), *blocks[1]),
            buf(*blocks[1]),
            buf(max(seq // 2, 1), tok_rows, dim),
            buf(max(seq - 1, 1), tok_rows, dim),
            dma((2, 2, hi)),
            dma((2, 2, hi)),
            dma((3, hi)),
            dma((3, hi)),
            dma((seq,)),
            dma((seq,)),
            dma((seq,)),
            dma((seq,)),
            dma((seq,)),
            dma((seq,)),
            dma((4,)),
            dma((3, seq)),
            dma((hi,)),
            dma((seq,)),
            dma,
        ],
        compiler_params=pltpu.CompilerParams(collective_id=4, has_side_effects=True, vmem_limit_bytes=62 << 20),
        cost_estimate=pl.CostEstimate(
            flops=seq * heads * 512 * 2400 * 128 * 10, bytes_accessed=20 << 20, transcendentals=10 << 20
        ),
        name="attend_back",
    )(
        length, qkv, db, wout, att, mem, upd, lse, slse, sgrad, state_query, forget, bias, up, down, mo, mid, *extra
    )


def gather_kernel(
    seq,
    hi,
    lo,
    tok_ref,
    grad_ref,
    wq_ref,
    ga_ref,
    gm_ref,
    wo_ref,
    wu_ref,
    toks_ref,
    grads_ref,
    wqs_ref,
    gas_ref,
    gms_ref,
    wos_ref,
    wus_ref,
    *rest,
):
    own_bufs = rest[:7]
    own_sem, store_sem, seq_send, seq_recv, z_send, z_recv, y_send, y_recv = rest[7:]
    me = lax.axis_index("seq")
    f = lax.axis_index("fsdp")
    fsdp = hi * lo
    bits = [1 << i for i in range(seq.bit_length() - 1)]
    greet(bits, hi, lo)

    pairs = ((tok_ref, toks_ref), (grad_ref, grads_ref))

    def seq_copy(i, source, slot, bit):
        src, out = pairs[i]
        return pltpu.make_async_remote_copy(
            src_ref=out.at[source] if source else src,
            dst_ref=out.at[slot],
            send_sem=seq_send.at[i, slot],
            recv_sem=seq_recv.at[i, slot],
            device_id={"seq": me ^ bit},
            device_id_type=MESH,
        )

    sends = []

    def send(i, source, slot, bit):
        sends.append(seq_copy(i, source, slot, bit))
        sends[-1].start()

    high = [bit for bit in reversed(bits) if bit > 1]
    if high:
        send(0, 0, high[0], high[0])
    if seq > 1:
        send(0, 0, 1, 1)

    width = wqs_ref.shape[2] // 3
    share = wus_ref.shape[2] // fsdp
    every = wq_ref.shape[1] // 3
    loads = [[] for _ in own_bufs]

    def load(i, src, dst):
        loads[i].append(pltpu.make_async_copy(src, dst, own_sem.at[i, len(loads[i])]))
        loads[i][-1].start()

    wq_buf, ga_buf, gm_buf, wo_buf, wu_buf, tok_buf, grad_buf = own_bufs
    for c in range(3):
        cols = pl.ds(pl.multiple_of(c * every + me * width, width), width)
        load(0, wq_ref.at[:, cols], wq_buf.at[:, pl.ds(c * width, width)])
    load(1, ga_ref, ga_buf)
    load(2, gm_ref, gm_buf)
    load(3, wo_ref.at[me % 2], wo_buf)
    if wu_ref.shape[1] == wus_ref.shape[2]:
        load(4, wu_ref, wu_buf)
    else:
        for c in range(fsdp):
            cols = pl.ds(pl.multiple_of((c * seq + me) * share, share), share)
            load(4, wu_ref.at[:, cols], wu_buf.at[:, pl.ds(c * share, share)])
    load(5, tok_ref, tok_buf)
    load(6, grad_ref, grad_buf)
    outs = (wqs_ref, gas_ref, gms_ref, wos_ref, wus_ref)
    start, step, arrive, drain = line_gather(
        hi, lo, lambda i, origin: outs[i].at[origin], lambda i: own_bufs[i], z_send, z_recv, y_send, y_recv
    )
    own_stores = []
    for i in range(len(own_bufs)):
        for c in loads[i]:
            c.wait()
        if i < len(outs):
            start(i)
        target = outs[i].at[f] if i < len(outs) else pairs[i - len(outs)][1].at[0]
        own_stores.append(pltpu.make_async_copy(own_bufs[i], target, store_sem.at[i]))
        own_stores[-1].start()
    if high:
        send(1, 0, high[0], high[0])
    if seq > 1:
        send(1, 0, 1, 1)
    for t in range(hi - 1):
        for i in range(len(outs)):
            step(i, t)
    for i in range(len(pairs)):
        have = [0]
        for n, bit in enumerate(high):
            if n:
                for j in have:
                    send(i, j, j ^ bit, bit)
            for j in have:
                seq_copy(i, 0, j ^ bit, bit).wait_recv()
                send(i, j ^ bit, j ^ bit ^ 1, 1)
            have += [j ^ bit for j in have]
        if seq > 1:
            for j in have:
                seq_copy(i, 0, j ^ 1, 1).wait_recv()
    for i in range(len(outs)):
        arrive(i)
    for i in range(len(outs)):
        drain(i)
    for c in sends:
        c.wait_send()
    for c in own_stores:
        c.wait()


def gather_start(tokens, grads, w_qkv, gain_a, gain_m, w_out, w_up, seq, fsdp):
    lo = 2
    hi = fsdp // lo
    dim_rows, hidden = w_up.shape
    share = hidden // (seq * fsdp)
    if share % 128:
        w_up = lax.dynamic_slice_in_dim(w_up.reshape(dim_rows, fsdp, seq, share), lax.axis_index("seq"), 1, axis=2)
        w_up = w_up.reshape(dim_rows, fsdp * share)
    anywhere = pl.BlockSpec(memory_space=pl.ANY)
    dma = pltpu.SemaphoreType.DMA
    shapes = (
        (seq,) + tokens.shape,
        (seq,) + grads.shape,
        (fsdp, dim_rows, w_qkv.shape[1] // seq),
        (fsdp,) + gain_a.shape,
        (fsdp,) + gain_m.shape,
        (fsdp,) + w_out.shape[1:],
        (fsdp, dim_rows, hidden // seq),
    )
    return pl.pallas_call(
        functools.partial(gather_kernel, seq, hi, lo),
        out_shape=tuple(jax.ShapeDtypeStruct(shape, bf16) for shape in shapes),
        in_specs=[anywhere] * 7,
        out_specs=(anywhere,) * 7,
        scratch_shapes=[pltpu.VMEM(shape[1:], bf16) for shape in shapes[2:] + shapes[:2]]
        + [dma((7, max(fsdp, 3))), dma((7,)), dma((2, seq)), dma((2, seq))]
        + line_sems(5, hi),
        compiler_params=pltpu.CompilerParams(collective_id=0, has_side_effects=True),
        name="gather_start",
    )(tokens, grads, w_qkv, gain_a, gain_m, w_out, w_up)


def finish_kernel(seq, hi, lo, inside, *refs):
    refs = list(refs)

    def take(count):
        taken = refs[:count]
        del refs[:count]
        return taken

    dqkv_hbm, wqkv_hbm, normed_hbm, down_ref, small_ref, mlp_gain_ref, tok_hbm, dmid_hbm, gain_ref = take(9)
    gq_in = None if inside else take(1)[0]
    tg_ref, rq_ref, rd_ref, dquery_ref, gate_ref, table_ref, again_ref, mgain_ref = take(8)
    dqkv_ref, wqkv_ref, normed_ref, tok_ref, dmid_ref = take(5)
    low, into, acc, gq_buf, tq, td, yq, zq, zd, xq, sy, sz, gains, gy, gz, gs = take(16)
    dn_send, dn_recv, z_send, z_recv, y_send, y_recv, x_send, x_recv, s_send, s_recv, g_send, g_recv = take(12)
    load_sem, dqkv_sem, tg_sem = take(3)
    gq_ref = gq_buf if inside else gq_in

    me = lax.axis_index("seq")
    f = lax.axis_index("fsdp")
    z, y = f // lo, f % lo
    peer = z * lo + 1 - y
    rows, dim = tok_ref.shape
    width = xq.shape[2] // 3
    bits, slots = seq_levels(seq)

    loads = [
        pltpu.make_async_copy(src, dst, load_sem.at[i])
        for i, (src, dst) in enumerate(
            (
                (wqkv_hbm, wqkv_ref),
                (down_ref, td),
                (normed_hbm, normed_ref),
                (tok_hbm, tok_ref),
                (dmid_hbm, dmid_ref),
            )
        )
    ]
    dqkv_loads = {
        j: pltpu.make_async_copy(
            dqkv_hbm.at[pl.ds(j * rows, rows)], dqkv_ref.at[pl.ds(j * rows, rows)], dqkv_sem.at[j]
        )
        for j in range(seq)
    }
    loads[0].start()
    for j in reversed(range(seq)):
        dqkv_loads[j].start()
    for c in loads[1:]:
        c.start()

    barrier = pltpu.get_barrier_semaphore()
    for k in range(1, seq):
        pl.semaphore_signal(barrier, inc=1, device_id={"seq": me ^ k}, device_id_type=MESH)
    for k in range(1, hi):
        pl.semaphore_signal(barrier, inc=1, device_id={"fsdp": lax.rem(z + k, hi) * lo + y}, device_id_type=MESH)
    pl.semaphore_signal(barrier, inc=1, device_id={"fsdp": peer}, device_id_type=MESH)
    pl.semaphore_wait(barrier, seq + hi - 1)

    def remote(src, dst, send, recv, axis, target):
        return pltpu.make_async_remote_copy(
            src_ref=src, dst_ref=dst, send_sem=send, recv_sem=recv, device_id={axis: target}, device_id_type=MESH
        )

    def dn_copy(bit, j):
        slot = slots[bit, j]
        return remote(low.at[j ^ bit], into.at[slot], dn_send.at[slot], dn_recv.at[slot], "seq", me ^ bit)

    start, combine, zsend, zrecv, drain_y, drain_z = line_reduce(
        hi,
        lo,
        lambda i, target: gq_ref.at[:, target],
        (tq, td),
        (yq,),
        (zq, zd),
        z_send,
        z_recv,
        y_send,
        y_recv,
    )

    def exchange(k, sending):
        return remote(
            tq.at[z, me ^ k] if sending else tq.at[z, me],
            xq.at[me] if sending else xq.at[me ^ k],
            x_send.at[k],
            x_recv.at[k],
            "seq",
            me ^ k if sending else me,
        )

    small_y = remote(small_ref, sy, s_send.at[0], s_recv.at[0], "fsdp", peer)
    small_y.start()
    loads[0].wait()
    if not inside:
        start(0)

    def dn_part(j):
        part = dot_t(dqkv_ref[j * rows : (j + 1) * rows], wqkv_ref[...])
        if j % 2:
            low[j] = part.astype(bf16)
            dn_copy(1, j ^ 1).start()
        else:
            acc[...] = part

    def dn_sum(j):
        for bit in bits:
            if j & bit:
                low[j] = acc[...].astype(bf16)
                dn_copy(bit, j ^ bit).start()
                break
            dn_copy(bit, j).wait_recv()
            acc[...] += into[slots[bit, j]].astype(f32)

    for j in reversed(range(2, seq)):
        dqkv_loads[j].wait()
        dn_part(j)
        if j == seq - 1:
            loads[1].wait()
            zsend(1, 0)
        if j % 2 == 0:
            dn_sum(j)
    for j in range(min(2, seq)):
        dqkv_loads[j].wait()
    loads[2].wait()
    if inside:
        for k in range(seq):
            cols = slice(k * (dim // seq), (k + 1) * (dim // seq))
            part = t_dot(normed_ref[:, cols], dqkv_ref[...]).astype(bf16)
            gq_buf[k] = part.reshape(gq_buf.shape[1:])
        start(0)
    def zstep(i, t):
        if t < hi - 1:
            zrecv(i, t)
            if t + 1 < hi - 1:
                zsend(i, t + 1)

    zstep(1, 0)
    small_y.wait_recv()
    sz[z] = small_ref[...] + sy[...]
    small_z = []
    for k in range(1, hi):
        small_z.append(
            remote(sz.at[z], sz.at[z], s_send.at[k], s_recv.at[k], "fsdp", lax.rem(z + k, hi) * lo + y)
        )
        small_z[-1].start()
    for j in reversed(range(min(2, seq))):
        dn_part(j)
    zstep(1, 1)
    for c in loads[3:]:
        c.wait()
    combine(0)
    zsend(0, 0)
    zstep(1, 2)
    for t in range(3, hi - 1):
        zstep(1, t)
    for bit in bits:
        dn_copy(bit, 0).wait_recv()
    gain = gain_ref[...]
    part = jnp.zeros((8, dim), f32)
    step = 128
    for r in range(0, rows, step):
        at = slice(r, r + step)
        dn = acc[at]
        for bit in bits:
            dn = dn + into[slots[bit, 0], at].astype(f32)
        x = tok_ref[at].astype(f32)
        rho = lax.rsqrt(jnp.mean(x * x, axis=-1, keepdims=True) + EPSILON)
        scaled = gain * dn
        mean = jnp.mean(x * scaled, axis=-1, keepdims=True)
        dmid_ref[at] += rho * scaled - x * (rho * rho * rho * mean)
        prod = dn * x * rho
        part += functools.reduce(jnp.add, [prod[n : n + 8] for n in range(0, step, 8)])
    tg_store = pltpu.make_async_copy(dmid_ref, tg_ref, tg_sem)
    tg_store.start()
    gains[0:8] = mlp_gain_ref[...]
    gains[8:16] = part
    gain_y = remote(gains, gy, g_send.at[0], g_recv.at[0], "fsdp", peer)
    gain_y.start()
    zrecv(0, 0)
    if hi > 2:
        zsend(0, 1)
    gain_y.wait_recv()
    gz[z] = gains[...] + gy[...]
    gain_z = []
    for k in range(1, hi):
        gain_z.append(
            remote(gz.at[z], gz.at[z], g_send.at[k], g_recv.at[k], "fsdp", lax.rem(z + k, hi) * lo + y)
        )
        gain_z[-1].start()
    for t in range(1, hi - 1):
        zrecv(0, t)
        if t + 1 < hi - 1:
            zsend(0, t + 1)
    for k in range(1, seq):
        exchange(k, True).start()
    for k in range(1, hi):
        source = lax.rem(z + hi - k, hi)
        remote(gz.at[source], gz.at[source], g_send.at[k], g_recv.at[k], "fsdp", f).wait_recv()
        remote(sz.at[source], sz.at[source], s_send.at[k], s_recv.at[k], "fsdp", f).wait_recv()
    gs[me] = functools.reduce(jnp.add, [gz[d] for d in range(hi)])
    gain_x = []
    for k in range(1, seq):
        gain_x.append(remote(gs.at[me], gs.at[me], g_send.at[hi + k], g_recv.at[hi + k], "seq", me ^ k))
        gain_x[-1].start()
    rd_ref[...] = td[z].astype(f32)
    total = functools.reduce(jnp.add, [sz[d] for d in range(hi)])
    cut, heads = dquery_ref.shape[0], gate_ref.shape[0]
    dquery_ref[...] = total[:cut]
    gate_ref[...] = total[cut : cut + heads]
    table_ref[...] = total[cut + heads : cut + 2 * heads, :BUCKETS]
    xq[me] = tq[z, me]
    for k in range(1, seq):
        exchange(k, False).wait_recv()
    write_parts(rq_ref, xq, seq, width)
    for k in range(1, seq):
        remote(gs.at[me ^ k], gs.at[me ^ k], g_send.at[hi + k], g_recv.at[hi + k], "seq", me).wait_recv()
    total = functools.reduce(jnp.add, [gs[k] for k in range(seq)])
    piece = again_ref.shape[1]
    total = pltpu.roll(total, lax.rem(dim - (me * hi * lo + f) * piece, dim), 1)[:, :DH]
    mgain_ref[...] = jnp.sum(total[0:8], axis=0, keepdims=True)[:, :piece]
    again_ref[...] = jnp.sum(total[8:16], axis=0, keepdims=True)[:, :piece]

    for bit in bits:
        for j in range(0, seq, 2 * bit):
            dn_copy(bit, j).wait_send()
    drain_y(0)
    for i in range(2):
        drain_z(i)
    for k in range(1, seq):
        exchange(k, True).wait_send()
    for c in [small_y, gain_y] + small_z + gain_z + gain_x:
        c.wait_send()
    tg_store.wait()


def finish(dqkv, wqkv, normed, down, small, mlp_gain, tok, dmid, gain, seq, fsdp):
    lo = 2
    hi = fsdp // lo
    rows, dim = tok.shape
    width3 = dqkv.shape[1]
    piece = dim // (seq * fsdp)
    inside = piece % 16 == 0
    heads = width3 // (3 * DH)
    vmem = pl.BlockSpec(memory_space=pltpu.VMEM)
    anywhere = pl.BlockSpec(memory_space=pl.ANY)
    dma = pltpu.SemaphoreType.DMA

    def buf(*shape):
        return pltpu.VMEM(shape, bf16)

    extra = []
    if not inside:
        extra.append(t_dot(normed, dqkv).astype(bf16).reshape(seq, fsdp, piece, width3))
    scratch = [
        buf(*dqkv.shape),
        buf(*wqkv.shape),
        buf(*normed.shape),
        buf(rows, dim),
        pltpu.VMEM((rows, dim), f32),
        buf(seq, rows, dim),
        buf(max(seq - 1, 1), rows, dim),
        pltpu.VMEM((rows, dim), f32),
        buf(seq, fsdp, piece, width3) if inside else buf(16, 128),
        buf(hi, seq, piece, width3),
        buf(*down.shape),
        buf(hi, seq, piece, width3),
        buf(2, max(hi - 1, 1), seq, piece, width3),
        buf(2, max(hi - 1, 1), *down.shape[1:]),
        buf(seq, piece, width3),
        pltpu.VMEM(small.shape, f32),
        pltpu.VMEM((hi,) + small.shape, f32),
        pltpu.VMEM((16, dim), f32),
        pltpu.VMEM((16, dim), f32),
        pltpu.VMEM((hi, 16, dim), f32),
        pltpu.VMEM((seq, 16, dim), f32),
        dma((seq,)),
        dma((seq,)),
        dma((2, 2, hi)),
        dma((2, 2, hi)),
        dma((1, hi)),
        dma((1, hi)),
        dma((seq,)),
        dma((seq,)),
        dma((hi,)),
        dma((hi,)),
        dma((hi + seq,)),
        dma((hi + seq,)),
        dma((5,)),
        dma((seq,)),
        dma,
    ]
    return pl.pallas_call(
        functools.partial(finish_kernel, seq, hi, lo, inside),
        out_shape=(
            jax.ShapeDtypeStruct((rows, dim), f32),
            jax.ShapeDtypeStruct((piece, seq * width3), f32),
            jax.ShapeDtypeStruct(down.shape[1:], f32),
            jax.ShapeDtypeStruct((heads * DH, DH), f32),
            jax.ShapeDtypeStruct((heads, DH), f32),
            jax.ShapeDtypeStruct((heads, BUCKETS), f32),
            jax.ShapeDtypeStruct((1, piece), f32),
            jax.ShapeDtypeStruct((1, piece), f32),
        ),
        in_specs=[anywhere] * 4 + [vmem] * 2 + [anywhere] * 2 + [vmem] * (1 + len(extra)),
        out_specs=(anywhere,) + (vmem,) * 7,
        scratch_shapes=scratch,
        compiler_params=pltpu.CompilerParams(
            collective_id=1, has_side_effects=True, vmem_limit_bytes=60 << 20
        ),
        name="finish",
    )(dqkv, wqkv, normed, down, small, mlp_gain, tok, dmid, gain, *extra)


GELU_P = 0.24
GELU_C = (
    0.08951261885080208,
    0.15562094398234086,
    -0.15437154502074169,
    0.6261054138112487,
    -0.6465313024138201,
    0.5547927291245551,
    -0.125128858665134,
)


def gelu_parts(x):
    size = jnp.abs(x)
    t = 1.0 / (1.0 + GELU_P * size)
    poly = GELU_C[-1] * t
    for c in GELU_C[-2::-1]:
        poly = (poly + c) * t
    bell = jnp.exp2(x * x * (-0.5 * LOG2E))
    tail = poly * bell
    cdf = jnp.where(x < 0.0, tail, 1.0 - tail)
    return x * cdf, cdf + x * bell * (1.0 / math.sqrt(2.0 * math.pi))


def mlp_kernel(seq, hi, lo, sub, length_ref, *refs):
    refs = list(refs)

    def take(count):
        taken = refs[:count]
        del refs[:count]
        return taken

    own_ref, others_ref, tok_ref, grads_ref, wo_hbm, wu_hbm, wd_hbm, gain_ref = take(8)
    mid_out, dmid_out, gsum_ref, db_ref, mo_ref, ug_out, dg_out = take(7)
    staged = len(ug_out.shape) == 4
    att_refs = [own_ref] + [others_ref.at[k] for k in range(1, seq)]
    att_buf, tok_buf, wo_ref, wu_ref, wd_ref, gm, nm, hid, dpre, low, into, acc, mid_ref, ug_ref, dg_ref = take(15)
    load_sem, w_sem, gm_sem, dn_send, dn_recv, db_send, db_recv, mo_sem, own_sem = take(9)
    if staged:
        tu, yu, y_send, y_recv = take(4)
    dbv = low.at[0]
    depth = att_buf.shape[0]

    me = lax.axis_index("seq")
    length = length_ref[0]
    dim = wo_ref.shape[0]
    width = dim // seq
    rows = tok_ref.shape[1]
    share = wu_ref.shape[1]
    subs = rows // sub
    bits, slots = seq_levels(seq)
    order = list(reversed(range(seq)))

    def chunk_loads(j):
        slot = j % depth
        copies = [
            pltpu.make_async_copy(att_refs[k].at[pl.ds(j * rows, rows)], att_buf.at[slot, k], load_sem.at[slot, k])
            for k in range(seq)
        ]
        copies.append(pltpu.make_async_copy(tok_ref.at[j], tok_buf.at[slot], load_sem.at[slot, seq]))
        return copies

    gm_loads = {
        j: pltpu.make_async_copy(grads_ref.at[j], gm.at[pl.ds(j * rows, rows)], gm_sem.at[j]) for j in order
    }
    weights = [
        pltpu.make_async_copy(src, dst, w_sem.at[i])
        for i, (src, dst) in enumerate(((wo_hbm, wo_ref), (wu_hbm, wu_ref), (wd_hbm, wd_ref)))
    ]
    for c in chunk_loads(order[0]) + weights[:1] + (chunk_loads(order[1]) if seq > 1 else []) + weights[1:]:
        c.start()
    for j in order:
        gm_loads[j].start()
    if depth == seq:
        for j in order[2:]:
            for c in chunk_loads(j):
                c.start()

    greet(bits, hi, lo)

    def dn_copy(bit, j, s):
        slot = slots[bit, j]
        at = pl.ds(pl.multiple_of(s * sub, sub), sub)
        return pltpu.make_async_remote_copy(
            src_ref=low.at[j ^ bit, at],
            dst_ref=into.at[slot, at],
            send_sem=dn_send.at[slot, s],
            recv_sem=dn_recv.at[slot, s],
            device_id={"seq": me ^ bit},
            device_id_type=MESH,
        )

    gain = gain_ref[...]

    def forward(j, s):
        slot = j % depth
        at = pl.ds(pl.multiple_of(s * sub, sub), sub)
        here = pl.ds(pl.multiple_of(j * rows + s * sub, sub), sub)
        position = (j ^ me) * rows + s * sub + lax.broadcasted_iota(jnp.int32, (sub, 1), 0)
        live = jnp.where(position < length, 1.0, 0.0)
        masked = (gm[here].astype(f32) * live).astype(bf16)
        gm[here] = masked
        mid = tok_buf[slot, at].astype(f32)
        for k in range(seq):
            own = pl.ds(pl.multiple_of((me ^ k) * width, width), width)
            mid = mid + dot(att_buf[slot, k, at], wo_ref[own])
        rho = lax.rsqrt(jnp.mean(mid * mid, axis=-1, keepdims=True) + EPSILON)
        normed = (mid * rho * gain).astype(bf16)
        nm[here] = normed
        if j == 0:
            mid_ref[at] = mid
        for c in range(0, share, 256):
            cols = slice(c, c + 256)
            value, slope = gelu_parts(dot(normed, wu_ref[:, cols]))
            hid[here, cols] = value.astype(bf16)
            dpre[here, cols] = (dot_t(masked, wd_ref[cols]) * slope).astype(bf16)
        part = dot_t(dpre[here], wu_ref[...])
        if j % 2:
            low[j, at] = part.astype(bf16)
            dn_copy(1, j ^ 1, s).start()
        else:
            acc[at] = part

    def settle(j, s):
        at = pl.ds(pl.multiple_of(s * sub, sub), sub)
        for bit in bits:
            if j & bit:
                low[j, at] = acc[at].astype(bf16)
                dn_copy(bit, j ^ bit, s).start()
                break
            dn_copy(bit, j, s).wait_recv()
            acc[at] += into[slots[bit, j], at].astype(f32)

    for c in weights:
        c.wait()
    for n in range(0, seq, 2):
        pair = order[n : n + 2]
        if n and depth < seq:
            for j in pair:
                for c in chunk_loads(j):
                    c.start()
        for j in pair:
            for c in chunk_loads(j):
                c.wait()
            gm_loads[j].wait()

        @pl.loop(0, subs)
        def _(s):
            for j in pair:
                forward(j, s)
            if pair[-1]:
                settle(pair[-1], s)

    stores = [pltpu.make_async_copy(mid_ref, mid_out, own_sem.at[1])]
    stores[0].start()
    if staged:
        for k in range(seq):
            cols = slice(k * (dim // seq), (k + 1) * (dim // seq))
            ug_ref[k] = t_dot(nm[:, cols], dpre[...]).astype(bf16).reshape(ug_ref.shape[1:])
        start, combine, _, _, drain_y, _ = line_reduce(
            hi, lo, lambda i, target: ug_ref.at[:, target], (tu,), (yu,), (), None, None, y_send, y_recv
        )
        start(0)
    else:
        for c in range(0, dim, 256):
            ug_ref[c : c + 256] = t_dot(nm[:, c : c + 256], dpre[...]).astype(bf16)
        stores.append(pltpu.make_async_copy(ug_ref, ug_out, own_sem.at[2]))
        stores[-1].start()

    def db_copy(source, target, bit, s):
        at = pl.ds(s * sub, sub)
        return pltpu.make_async_remote_copy(
            src_ref=db_ref.at[source, at] if source else dbv.at[at],
            dst_ref=db_ref.at[target, at],
            send_sem=db_send.at[target, s],
            recv_sem=db_recv.at[target, s],
            device_id={"seq": me ^ bit},
            device_id_type=MESH,
        )

    sends = []
    high = [bit for bit in reversed(bits) if bit > 1]

    def send(source, target, bit, s):
        sends.append(db_copy(source, target, bit, s))
        sends[-1].start()

    step = 128
    part = jnp.zeros((8, dim), f32)
    for s in range(subs):
        for bit in bits:
            dn_copy(bit, 0, s).wait_recv()
        for r in range(s * sub, (s + 1) * sub, step):
            at = slice(r, r + step)
            dn = acc[at]
            for bit in bits:
                dn = dn + into[slots[bit, 0], at].astype(f32)
            mid = mid_ref[at]
            rho = lax.rsqrt(jnp.mean(mid * mid, axis=-1, keepdims=True) + EPSILON)
            scaled = gain * dn
            mean = jnp.mean(mid * scaled, axis=-1, keepdims=True)
            dmid = gm[at].astype(f32) + rho * scaled - mid * (rho * rho * rho * mean)
            acc[at] = dmid
            dbv[at] = dmid.astype(bf16)
            prod = dn * mid * rho
            part += functools.reduce(jnp.add, [prod[i : i + 8] for i in range(0, step, 8)])
        if high:
            send(0, high[0], high[0], s)
        if seq > 1:
            send(0, 1, 1, s)
    gsum_ref[...] = part
    stores.append(pltpu.make_async_copy(dbv, db_ref.at[0], own_sem.at[0]))
    stores[-1].start()
    stores.append(pltpu.make_async_copy(acc, dmid_out, own_sem.at[3]))
    stores[-1].start()
    for c in range(0, share, 256):
        dg_ref[c : c + 256] = t_dot(hid[:, c : c + 256], gm[...]).astype(bf16)
    stores.append(pltpu.make_async_copy(dg_ref, dg_out, own_sem.at[4]))
    stores[-1].start()
    for j in range(seq):
        at = slice(j * rows, (j + 1) * rows)
        nm[at] = dot(hid[at], wd_ref[...]).astype(bf16)
        stores.append(pltpu.make_async_copy(nm.at[pl.ds(j * rows, rows)], mo_ref.at[j], mo_sem.at[j]))
        stores[-1].start()
    have = [0]
    for n, bit in enumerate(high):
        if n:
            for j in have:
                for s in range(subs):
                    send(j, j ^ bit, bit, s)
        for j in have:
            for s in range(subs):
                db_copy(0, j ^ bit, bit, s).wait_recv()
                send(j ^ bit, j ^ bit ^ 1, 1, s)
        have += [j ^ bit for j in have]
    if seq > 1:
        for j in have:
            for s in range(subs):
                db_copy(0, j ^ 1, 1, s).wait_recv()
    if staged:
        combine(0)
        stores.append(pltpu.make_async_copy(tu, ug_out, own_sem.at[2]))
        stores[-1].start()
        drain_y(0)
    for c in sends:
        c.wait_send()
    for c in stores:
        c.wait()
    for bit in bits:
        for j in range(0, seq, 2 * bit):
            for s in range(subs):
                dn_copy(bit, j, s).wait_send()


def mlp(length, own, others, tok, grads, wo, wu, wd, gain, fsdp):
    seq, rows, dim = tok.shape
    share = wu.shape[1]
    lo = 2
    hi = fsdp // lo
    piece = dim // (seq * fsdp)
    staged = piece % 16 == 0
    up_shape = (hi, seq, piece, share) if staged else (dim, share)
    sub = 256
    depth = seq if seq <= 4 else 2
    anywhere = pl.BlockSpec(memory_space=pl.ANY)
    vmem = pl.BlockSpec(memory_space=pltpu.VMEM)
    dma = pltpu.SemaphoreType.DMA

    def buf(*shape):
        return pltpu.VMEM(shape, bf16)

    return pl.pallas_call(
        functools.partial(mlp_kernel, seq, hi, lo, sub),
        out_shape=(
            jax.ShapeDtypeStruct((rows, dim), f32),
            jax.ShapeDtypeStruct((rows, dim), f32),
            jax.ShapeDtypeStruct((8, dim), f32),
            jax.ShapeDtypeStruct((seq, rows, dim), bf16),
            jax.ShapeDtypeStruct((seq, rows, dim), bf16),
            jax.ShapeDtypeStruct(up_shape, bf16),
            jax.ShapeDtypeStruct((share, dim), bf16),
        ),
        in_specs=[pl.BlockSpec(memory_space=pltpu.SMEM)] + [anywhere] * 7 + [vmem],
        out_specs=(anywhere, anywhere, vmem, anywhere, anywhere, anywhere, anywhere),
        scratch_shapes=[
            buf(depth, seq, rows, dim // seq),
            buf(depth, rows, dim),
            buf(dim, dim),
            buf(dim, share),
            buf(share, dim),
            buf(seq * rows, dim),
            buf(seq * rows, dim),
            buf(seq * rows, share),
            buf(seq * rows, share),
            buf(seq, rows, dim),
            buf(max(seq - 1, 1), rows, dim),
            pltpu.VMEM((rows, dim), f32),
            pltpu.VMEM((rows, dim), f32),
            buf(seq, fsdp, piece, share) if staged else buf(dim, share),
            buf(share, dim),
            dma((depth, seq + 1)),
            dma((3,)),
            dma((seq,)),
            dma((seq, rows // sub)),
            dma((seq, rows // sub)),
            dma((seq, rows // sub)),
            dma((seq, rows // sub)),
            dma((seq,)),
            dma((5,)),
        ]
        + ([buf(*up_shape), buf(*up_shape), dma((1, hi)), dma((1, hi))] if staged else []),
        compiler_params=pltpu.CompilerParams(collective_id=2, has_side_effects=True, vmem_limit_bytes=62 << 20),
        cost_estimate=pl.CostEstimate(
            flops=2 * rows * seq * dim * (dim + 6 * share), bytes_accessed=32 << 20, transcendentals=rows * seq * share
        ),
        name="mlp",
    )(length, own, others, tok, grads, wo, wu, wd, gain)


def inverse_rms(values):
    return lax.rsqrt(jnp.mean(values * values, axis=-1, keepdims=True) + EPSILON)


def norm_back(values, gain, rho, grad):
    scaled = gain * grad
    mean = jnp.mean(values * scaled, axis=-1, keepdims=True)
    gain_grad = (grad * values * rho).reshape(-1, 8, values.shape[1])
    return rho * scaled - values * (rho * rho * rho * mean), jnp.sum(gain_grad, axis=0)


def body(
    tokens,
    lengths,
    state_init,
    w_qkv,
    w_out,
    w_up,
    w_down,
    norm_attn,
    norm_mlp,
    rel_bias,
    state_query,
    gate_bias,
    out_grad,
    state_grad,
):
    seq_count = lax.axis_size("seq")
    fsdp_count = lax.axis_size("fsdp")
    seq_at = lax.axis_index("seq")
    heads = H // seq_count
    width = heads * DH
    tok_rows, dim = tokens.shape[1:]
    rows = tok_rows * seq_count
    hidden_all = w_up.shape[1]
    share = hidden_all // (seq_count * fsdp_count)

    piece = dim // (seq_count * fsdp_count)
    all_tokens, all_grad, qkv_w, gain_attn, gain_mlp, own_out, up_w = gather_start(
        tokens[0],
        out_grad[0],
        w_qkv,
        norm_attn.reshape(1, -1),
        norm_mlp.reshape(1, -1),
        w_out.reshape(2, w_out.shape[0] // 2, dim),
        w_up,
        seq_count,
        fsdp_count,
    )
    qkv_w = qkv_w.reshape(dim, 3 * width)
    up_w = up_w.reshape(dim, hidden_all // seq_count)
    gain_attn = gain_attn.reshape(dim).astype(f32)
    gain_mlp = gain_mlp.reshape(dim).astype(f32)
    own_down = lax.dynamic_slice_in_dim(w_down, seq_at * share, share, axis=0)

    bias = bias_vector(rel_bias)
    forget = jax.nn.sigmoid(gate_bias)
    forget_row = forget.reshape(1, width)

    inputs = all_tokens.reshape(rows, dim).astype(f32)
    normed = (inputs * inverse_rms(inputs) * gain_attn).astype(bf16)
    qkv = dot(normed, qkv_w).astype(bf16)
    attended, others, out_w, down_w, final_memory, mem, upd, lse, slse = attend(
        qkv,
        state_init[0],
        lengths,
        state_query,
        forget_row,
        bias,
        own_out,
        own_down,
        heads,
        seq_count,
        fsdp_count,
    )
    out_w = out_w.reshape(dim, dim)
    down_w = down_w.reshape(fsdp_count * share, dim)
    own_out = lax.dynamic_slice_in_dim(out_w, seq_at * width, width, axis=0)
    mid_here, dmid, mlp_gain_grad, dbranch, mlp_parts, up_grad, down_grad = mlp(
        lengths, attended, others, all_tokens, all_grad, out_w, up_w, down_w, gain_mlp.reshape(1, dim), fsdp_count
    )
    span = fsdp_count // seq_count
    if up_grad.ndim == 2:
        up_grad = up_grad.reshape(seq_count, fsdp_count, piece, hidden_all // seq_count)
    dqkv, small, up_part, down_total, out_part, output = attend_back(
        qkv,
        dbranch.reshape(rows, dim),
        own_out,
        attended,
        mem,
        upd,
        lse,
        slse,
        state_grad[0],
        lengths,
        state_query,
        forget_row,
        bias,
        up_grad,
        down_grad.reshape(seq_count, span * share, dim),
        mlp_parts,
        mid_here,
        seq_count,
        fsdp_count,
    )
    tokens_grad, qkv_part, down_part, dquery, grad_gate, grad_table, attn_gain_grad, mlp_gain_grad = finish(
        dqkv,
        qkv_w,
        normed,
        down_total,
        small,
        mlp_gain_grad,
        tokens[0],
        dmid,
        gain_attn.reshape(1, dim),
        seq_count,
        fsdp_count,
    )
    output = output[None]
    tokens_grad = tokens_grad[None]
    dquery = dquery.reshape(heads, DH, DH)
    attn_gain_grad = attn_gain_grad.reshape(piece)
    mlp_gain_grad = mlp_gain_grad.reshape(piece)
    if up_part.ndim == 3:
        up_part = up_part.reshape(seq_count, piece, fsdp_count, share)
        up_part = jnp.transpose(up_part, (1, 2, 0, 3)).reshape(piece, hidden_all)
    return (
        output,
        final_memory[None],
        tokens_grad,
        qkv_part,
        out_part,
        up_part,
        down_part,
        attn_gain_grad,
        mlp_gain_grad,
        grad_table,
        dquery,
        grad_gate,
    )


def solution(mesh):
    placed = (
        P("fsdp", "seq", None),
        P("fsdp"),
        P("fsdp", None, "seq"),
        P("fsdp", None),
        P("fsdp", None),
        P("fsdp", None),
        P("fsdp", None),
        P("fsdp"),
        P("fsdp"),
        P("seq", None),
        P("seq", None, None),
        P("seq", None),
        P("fsdp", "seq", None),
        P("fsdp", None, "seq"),
    )
    return jax.shard_map(
        body,
        mesh=mesh,
        in_specs=placed,
        out_specs=(
            P("fsdp", "seq", None),
            P("fsdp", None, "seq"),
            P("fsdp", "seq", None),
            P(("seq", "fsdp"), None),
            P(("seq", "fsdp"), None),
            P(("seq", "fsdp"), None),
            P(("seq", "fsdp"), None),
            P(("seq", "fsdp")),
            P(("seq", "fsdp")),
            P("seq", None),
            P("seq", None, None),
            P("seq", None),
        ),
        check_vma=False,
    )
```

```python
import functools
import math

import jax
import jax.numpy as jnp
import numpy as np
from jax import lax
from jax.experimental import pallas as pl
from jax.experimental.pallas import tpu as pltpu
from jax.sharding import PartitionSpec as P

H = 8
DH = 128
BLOCK = 512
STATE_VECTORS = 512
QTILE = 256
SPAN = BLOCK + QTILE

EPSILON = 1e-06
BUCKET_EDGES = (19, 21, 24, 27, 31, 35, 40, 46, 52, 59, 67, 77, 87, 99, 113)
BUCKETS = 32
LOG2E = math.log2(math.e)
SCALE = DH ** (-0.5)
NEAR = 384

f32 = jnp.float32
bf16 = jnp.bfloat16
MESH = pl.DeviceIdType.MESH


def bucket_of(distance):
    return np.minimum(distance, 16) + (distance[..., None] >= np.array(BUCKET_EDGES)).sum(-1)


def tile_distance():
    rows = np.arange(QTILE)[:, None]
    cols = np.arange(SPAN)[None, :]
    return rows + BLOCK - cols


def bias_vector(table):
    distance = BLOCK - np.arange(2 * BLOCK)
    inside = (distance >= 0) & (distance < BLOCK)
    bucket = np.where(inside, bucket_of(np.clip(distance, 0, BLOCK)), BUCKETS)
    member = jnp.asarray((np.arange(BUCKETS)[:, None] == bucket[None]).astype(np.float32))
    total = jnp.dot(table, member, precision=lax.Precision.HIGHEST, preferred_element_type=f32)
    return jnp.where(jnp.asarray(inside)[None], total * LOG2E, -jnp.inf)


def tile_bias(vector_ref, head):
    wide = jnp.broadcast_to(vector_ref[head : head + 1, :], (QTILE, 2 * BLOCK))
    return pltpu.roll(wide, 0, 1, stride=1, stride_axis=0)[:, :SPAN]


def dot(a, b):
    return jnp.dot(a, b, preferred_element_type=f32)


def dot_t(a, b):
    return lax.dot_general(a, b, (((1,), (1,)), ((), ())), preferred_element_type=f32)


def t_dot(a, b):
    return lax.dot_general(a, b, (((0,), (0,)), ((), ())), preferred_element_type=f32)


def to_row(column):
    wide = jnp.broadcast_to(column, (column.shape[0], 128))
    return wide.T[0:1, :]


def context_pieces(tile):
    start = tile * QTILE
    pieces = []
    if start < BLOCK:
        pieces.append((0, start, BLOCK, 0))
    pieces.append((1, 0, start + QTILE, BLOCK - start))
    return pieces


def softmax_parts(scores):
    top = functools.reduce(jnp.maximum, [jnp.max(s, axis=-1, keepdims=True) for s in scores])
    raised = [jnp.exp2(s - top) for s in scores]
    total = functools.reduce(jnp.add, [jnp.sum(e, axis=-1, keepdims=True) for e in raised])
    return raised, total, top + jnp.log2(total)


def line_gather(hi, lo, slot, own, z_send, z_recv, y_send, y_recv):
    f = lax.axis_index("fsdp")
    z, y = f // lo, f % lo

    def copy(i, origin, target, send, recv, first=False):
        ref = slot(i, origin)
        return pltpu.make_async_remote_copy(
            src_ref=own(i) if first else ref,
            dst_ref=ref,
            send_sem=send,
            recv_sem=recv,
            device_id={"fsdp": target},
            device_id_type=MESH,
        )

    def right(i, t):
        return copy(i, (z - t) * lo + y, (z + 1) * lo + y, z_send.at[i, 0, t], z_recv.at[i, 0, t], t == 0)

    def left(i, t):
        return copy(i, (z + t) * lo + y, (z - 1) * lo + y, z_send.at[i, 1, t], z_recv.at[i, 1, t], t == 0)

    def across(i, d):
        return copy(
            i, (z + d) * lo + y, z * lo + 1 - y, y_send.at[i, d + hi - 1], y_recv.at[i, d + hi - 1], d == 0
        )

    def start(i):
        pl.when(z + 1 < hi)(lambda: right(i, 0).start())
        pl.when(z >= 1)(lambda: left(i, 0).start())
        across(i, 0).start()

    def step(i, t):
        @pl.when(z - 1 - t >= 0)
        def _():
            copy(i, (z - 1 - t) * lo + y, f, z_send.at[i, 0, t], z_recv.at[i, 0, t]).wait_recv()
            if t + 1 < hi - 1:
                pl.when(z + 1 < hi)(lambda: right(i, t + 1).start())
            across(i, -1 - t).start()

        @pl.when(z + 1 + t < hi)
        def _():
            copy(i, (z + 1 + t) * lo + y, f, z_send.at[i, 1, t], z_recv.at[i, 1, t]).wait_recv()
            if t + 1 < hi - 1:
                pl.when(z >= 1)(lambda: left(i, t + 1).start())
            across(i, 1 + t).start()

    def arrive(i):
        for d in range(1 - hi, hi):

            @pl.when((z + d >= 0) & (z + d < hi))
            def _():
                copy(
                    i, (z + d) * lo + 1 - y, f, y_send.at[i, d + hi - 1], y_recv.at[i, d + hi - 1]
                ).wait_recv()

    def drain(i):
        for d in range(1 - hi, hi):

            @pl.when((z + d >= 0) & (z + d < hi))
            def _():
                across(i, d).wait_send()

        for t in range(hi - 1):

            @pl.when((z + 1 < hi) & (z - t >= 0))
            def _():
                right(i, t).wait_send()

            @pl.when((z >= 1) & (z + t < hi))
            def _():
                left(i, t).wait_send()

    return start, step, arrive, drain


def line_sems(count, hi):
    dma = pltpu.SemaphoreType.DMA
    return [dma((count, 2, hi)), dma((count, 2, hi)), dma((count, 2 * hi)), dma((count, 2 * hi))]


def greet(seq_targets, hi, lo):
    me = lax.axis_index("seq")
    f = lax.axis_index("fsdp")
    z, y = f // lo, f % lo
    barrier = pltpu.get_barrier_semaphore()
    for k in seq_targets:
        pl.semaphore_signal(barrier, inc=1, device_id={"seq": me ^ k}, device_id_type=MESH)
    near = (lax.rem(z + 1, hi) * lo + y, lax.rem(z + hi - 1, hi) * lo + y, z * lo + 1 - y)
    for target in near:
        pl.semaphore_signal(barrier, inc=1, device_id={"fsdp": target}, device_id_type=MESH)
    pl.semaphore_wait(barrier, len(seq_targets) + len(near))


def attend_kernel(
    heads,
    seq,
    hi,
    lo,
    length_ref,
    qkv_ref,
    init_ref,
    query_ref,
    forget_ref,
    vector_ref,
    own_out_ref,
    own_down_ref,
    att_out,
    others_ref,
    outs_ref,
    downs_ref,
    final_ref,
    mem_out,
    upd_out,
    lse_ref,
    slse_ref,
    memory_ref,
    bias_ref,
    att_ref,
    mem_ref,
    upd_ref,
    store_sem,
    own_sem,
    att_send,
    att_recv,
    out_send,
    out_recv,
    z_send,
    z_recv,
    y_send,
    y_recv,
):
    me = lax.axis_index("seq")
    f = lax.axis_index("fsdp")
    length = length_ref[0]
    width = heads * DH
    scale2 = SCALE * LOG2E
    blocks = seq
    bits = [1 << i for i in range(seq.bit_length() - 1)]
    greet(bits, hi, lo)

    own_copies = [
        pltpu.make_async_copy(own_down_ref, downs_ref.at[f], own_sem.at[0]),
        pltpu.make_async_copy(own_out_ref, outs_ref.at[:, me % 2], own_sem.at[1]),
    ]
    for c in own_copies:
        c.start()

    def lowest(k):
        return k & -k

    def out_copy(sending):
        half = me % 2 if sending else 1 - me % 2
        return pltpu.make_async_remote_copy(
            src_ref=own_out_ref,
            dst_ref=outs_ref.at[:, half],
            send_sem=out_send,
            recv_sem=out_recv,
            device_id={"seq": me ^ 1},
            device_id_type=MESH,
        )

    def att_copy(k, b):
        bit = lowest(k)
        came = k ^ bit
        here = pl.ds(pl.multiple_of((b ^ me) * BLOCK, BLOCK), BLOCK)
        there = pl.ds(pl.multiple_of((b ^ me ^ bit) * BLOCK, BLOCK), BLOCK)
        src = others_ref.at[came, here] if came else att_ref.at[here]
        return pltpu.make_async_remote_copy(
            src_ref=src,
            dst_ref=others_ref.at[k, there],
            send_sem=att_send.at[k, b],
            recv_sem=att_recv.at[k, b],
            device_id={"seq": me ^ bit},
            device_id_type=MESH,
        )

    def att_arrival(k, b):
        here = pl.ds(pl.multiple_of((b ^ me) * BLOCK, BLOCK), BLOCK)
        return pltpu.make_async_remote_copy(
            src_ref=others_ref.at[k, here],
            dst_ref=others_ref.at[k, here],
            send_sem=att_send.at[k, b],
            recv_sem=att_recv.at[k, b],
            device_id={"seq": me},
            device_id_type=MESH,
        )

    passing = sorted([k for k in range(2, seq, 2)], key=lambda k: (bin(k).count("1"), -k))

    def onward(k, send):
        for bit in reversed(bits):
            if bit < lowest(k):
                send(k | bit)

    start, step, arrive, drain = line_gather(
        hi, lo, lambda i, origin: downs_ref.at[origin], lambda i: own_down_ref, z_send, z_recv, y_send, y_recv
    )

    start(0)
    out_copy(True).start()
    memory_ref[...] = init_ref[...].astype(f32)
    for head in range(heads):
        bias_ref[head] = tile_bias(vector_ref, head)

    def block_stores(block):
        at = pl.ds(pl.multiple_of((block ^ me) * BLOCK, BLOCK), BLOCK)
        pairs = (
            (att_ref.at[at], att_out.at[at]),
            (mem_ref.at[block], mem_out.at[block]),
            (upd_ref.at[block], upd_out.at[block]),
        )
        return [pltpu.make_async_copy(a, b, store_sem.at[i, block]) for i, (a, b) in enumerate(pairs)]

    @pl.loop(0, blocks)
    def _(block):
        cur_at = pl.multiple_of((block ^ me) * BLOCK, BLOCK)
        prev_at = pl.multiple_of((jnp.maximum(block - 1, 0) ^ me) * BLOCK, BLOCK)
        cur_ref = qkv_ref.at[pl.ds(cur_at, BLOCK)]
        prev_ref = qkv_ref.at[pl.ds(prev_at, BLOCK)]
        for t in range(min(hi - 1, blocks - 1)):
            pl.when(block == t + 1)(lambda t=t: step(0, t))

        live_block = block * BLOCK < length
        for head in range(heads):
            own = slice(head * DH, (head + 1) * DH)
            memory = memory_ref[:, own]
            low = memory.astype(bf16)
            mem_ref[block, :, own] = memory
            refs = (prev_ref, cur_ref)
            key_cols = slice(width + head * DH, width + (head + 1) * DH)
            value_cols = slice(2 * width + head * DH, 2 * width + (head + 1) * DH)
            for tile in range(BLOCK // QTILE):
                rows = slice(tile * QTILE, (tile + 1) * QTILE)
                query = cur_ref[rows, own]
                scores, values = [], []
                for which, at, end, col in context_pieces(tile):
                    s = dot_t(query, refs[which][at:end, key_cols])
                    position = (block - 1 + which) * BLOCK + at + lax.broadcasted_iota(jnp.int32, (1, end - at), 1)
                    live = (position >= 0) & (position < length)
                    s = s * scale2 + bias_ref[head, :, col : col + end - at]
                    scores.append(jnp.where(live, s, -jnp.inf))
                    values.append(refs[which][at:end, value_cols])
                scores.append(dot_t(query, low) * scale2)
                values.append(low)
                raised, total, lse = softmax_parts(scores)
                out = functools.reduce(jnp.add, [dot(e.astype(bf16), v) for e, v in zip(raised, values)])
                att_ref[pl.ds(cur_at + tile * QTILE, QTILE), own] = (out / total).astype(bf16)
                lse_ref[head : head + 1, pl.ds(pl.multiple_of(block * BLOCK, BLOCK) + tile * QTILE, QTILE)] = to_row(lse)
            own_key = cur_ref[:, key_cols]
            own_value = cur_ref[:, value_cols]
            squeries = dot(low, query_ref[head]).astype(bf16)
            position = block * BLOCK + lax.broadcasted_iota(jnp.int32, (1, BLOCK), 1)
            for tile in range(STATE_VECTORS // QTILE):
                rows = slice(tile * QTILE, (tile + 1) * QTILE)
                squery = squeries[rows]
                scores = [
                    dot_t(squery, low) * scale2,
                    jnp.where(position < length, dot_t(squery, own_key) * scale2, -jnp.inf),
                ]
                raised, total, lse = softmax_parts(scores)
                update = dot(raised[0].astype(bf16), low) + dot(raised[1].astype(bf16), own_value)
                update = update / total
                upd_ref[block, rows, own] = update
                slse_ref[head : head + 1, pl.ds(pl.multiple_of(block * BLOCK, BLOCK) + tile * QTILE, QTILE)] = to_row(
                    lse
                )
                forget = forget_ref[:, own]
                old = memory[rows]
                memory_ref[rows, own] = jnp.where(live_block, forget * old + (1.0 - forget) * update, old)

        for bit in reversed(bits):
            att_copy(bit, block).start()
        for c in block_stores(block):
            c.start()

        @pl.when(block >= 1)
        def _():
            for k in passing:
                att_arrival(k, block - 1).wait_recv()
                onward(k, lambda target: att_copy(target, block - 1).start())

    final_ref[...] = memory_ref[...]
    for t in range(min(hi - 1, blocks - 1), hi - 1):
        step(0, t)
    for k in passing:
        att_arrival(k, blocks - 1).wait_recv()
        onward(k, lambda target: att_copy(target, blocks - 1).start())
    arrive(0)
    out_copy(False).wait_recv()
    for k in range(1, seq, 2):
        for b in range(blocks):
            att_arrival(k, b).wait_recv()
    for c in own_copies:
        c.wait()
    drain(0)
    for b in range(blocks):
        for c in block_stores(b):
            c.wait()
    out_copy(True).wait_send()
    for k in range(1, seq):
        for b in range(blocks):
            att_copy(k, b).wait_send()


def attend(qkv, init, length, state_query, forget, bias, own_out, own_down, heads, seq, fsdp):
    rows, width3 = qkv.shape
    width = heads * DH
    blocks = rows // BLOCK
    lo = 2
    hi = fsdp // lo
    dim = own_down.shape[1]
    anywhere = pl.BlockSpec(memory_space=pl.ANY)
    vmem = pl.BlockSpec(memory_space=pltpu.VMEM)
    dma = pltpu.SemaphoreType.DMA
    return pl.pallas_call(
        functools.partial(attend_kernel, heads, seq, hi, lo),
        out_shape=(
            jax.ShapeDtypeStruct((rows, width), bf16),
            jax.ShapeDtypeStruct((seq, rows, width), bf16),
            jax.ShapeDtypeStruct((fsdp, 2) + own_out.shape[1:], bf16),
            jax.ShapeDtypeStruct((fsdp,) + own_down.shape, bf16),
            jax.ShapeDtypeStruct((STATE_VECTORS, width), f32),
            jax.ShapeDtypeStruct((blocks, STATE_VECTORS, width), f32),
            jax.ShapeDtypeStruct((blocks, STATE_VECTORS, width), f32),
            jax.ShapeDtypeStruct((heads, rows), f32),
            jax.ShapeDtypeStruct((heads, blocks * STATE_VECTORS), f32),
        ),
        in_specs=[pl.BlockSpec(memory_space=pltpu.SMEM)] + [vmem] * 7,
        out_specs=(anywhere, anywhere, anywhere, anywhere, vmem, anywhere, anywhere, vmem, vmem),
        scratch_shapes=[
            pltpu.VMEM((STATE_VECTORS, width), f32),
            pltpu.VMEM((heads, QTILE, SPAN), f32),
            pltpu.VMEM((rows, width), bf16),
            pltpu.VMEM((blocks, STATE_VECTORS, width), f32),
            pltpu.VMEM((blocks, STATE_VECTORS, width), f32),
            dma((3, blocks)),
            dma((2,)),
            dma((seq, blocks)),
            dma((seq, blocks)),
            dma,
            dma,
        ]
        + line_sems(1, hi),
        compiler_params=pltpu.CompilerParams(collective_id=3, has_side_effects=True, vmem_limit_bytes=60 << 20),
        cost_estimate=pl.CostEstimate(
            flops=blocks * heads * 512 * 2400 * 128 * 4, bytes_accessed=16 << 20, transcendentals=10 << 20
        ),
        name="attend",
    )(length, qkv, init, state_query, forget, bias, own_out, own_down)


def line_reduce(hi, lo, block, total, from_y, from_z, z_send, z_recv, y_send, y_recv, loads=None):
    loads = loads or {}
    f = lax.axis_index("fsdp")
    z, y = f // lo, f % lo

    def remote(src, dst, send, recv, target):
        return pltpu.make_async_remote_copy(
            src_ref=src, dst_ref=dst, send_sem=send, recv_sem=recv, device_id={"fsdp": target}, device_id_type=MESH
        )

    def across(i, d):
        return remote(
            block(i, d * lo + 1 - y), from_y[i].at[d], y_send.at[i, d], y_recv.at[i, d], z * lo + 1 - y
        )

    def start(i):
        for d in range(hi):
            across(i, d).start()

    def combine(i):
        for d in range(hi):
            across(i, d).wait_recv()
            if i in loads:
                loads[i][d].wait()
                own = total[i].at[d]
            else:
                own = block(i, d * lo + y)
            total[i][d] = (own[...].astype(f32) + from_y[i][d].astype(f32)).astype(bf16)

    def hop(i, side, t, at, target):
        return remote(
            total[i].at[jnp.clip(at, 0, hi - 1)],
            from_z[i].at[side, t],
            z_send.at[i, side, t],
            z_recv.at[i, side, t],
            target,
        )

    def sending(t):
        d = t - (hi - 1 - z)
        m = hi - 1 - (t - z)
        return ((0, d, (d >= 0) & (d < z), z - 1), (1, m, (m > z) & (m < hi), z + 1))

    def zsend(i, t):
        for side, at, cond, target in sending(t):
            pl.when(cond)(lambda: hop(i, side, t, at, target * lo + y).start())

    def zrecv(i, t):
        d = t - (hi - 2 - z)
        m = hi - 1 - (t - (z - 1))
        for side, at, cond in ((0, d, (z + 1 < hi) & (d >= 0)), (1, m, (z > 0) & (m < hi))):

            @pl.when(cond)
            def _():
                hop(i, side, t, at, f).wait_recv()
                slot = jnp.clip(at, 0, hi - 1)
                total[i][slot] = (total[i][slot].astype(f32) + from_z[i][side, t].astype(f32)).astype(bf16)

    def drain_y(i):
        for d in range(hi):
            across(i, d).wait_send()

    def drain_z(i):
        for t in range(hi - 1):
            for side, at, cond, target in sending(t):
                pl.when(cond)(lambda: hop(i, side, t, at, f).wait_send())

    return start, combine, zsend, zrecv, drain_y, drain_z


def seq_levels(seq):
    bits = [1 << i for i in range(seq.bit_length() - 1)]
    slots = {}
    for bit in bits:
        for j in range(0, seq, 2 * bit):
            slots[bit, j] = len(slots)
    return bits, slots


def diagonal_sums(tile):
    rows, lanes = tile.shape
    wide = jnp.concatenate([tile, jnp.zeros((rows, lanes), f32)], axis=1)
    row = lax.broadcasted_iota(jnp.int32, wide.shape, 0)
    bit = 1
    while bit < rows:
        wide = jnp.where((row & bit) != 0, pltpu.roll(wide, 2 * lanes - bit, 1), wide)
        bit *= 2
    return jnp.sum(wide, axis=0, keepdims=True)


def attend_back_kernel(heads, seq, hi, lo, inside, length_ref, *refs):
    refs = list(refs)

    def take(count):
        taken = refs[:count]
        del refs[:count]
        return taken

    qkv_hbm, db_hbm, wout_hbm, att_hbm, mem_hbm, upd_hbm, lse_ref, slse_ref = take(8)
    sgrad_ref, query_ref, forget_ref, vector_ref, up_ref, down_ref, mo_ref, mid_hbm = take(8)
    ow_in = None if inside else take(1)[0]
    dqkv_out, small_ref, upart_ref, dtotal_ref, opart_ref, output_ref = take(6)
    qkv_ref, db_ref, att_ref, mem_ref, upd_ref, mid_ref, dqkv_ref, wout_ref = take(8)
    dmem_ref, dnext_ref, dctx_ref, bias_ref, near_ref, far_ref, dout_ref, ow_buf = take(8)
    moved, to, tu, yo, yu, yd, zo, zu, xu, mo_low, mo_in = take(11)
    z_send, z_recv, y_send, y_recv, m_send, m_recv, e_send, e_recv, x_send, x_recv = take(10)
    load_sem, block_sem, up_sem, mo_sem, out_sem = take(5)
    ow_ref = ow_buf if inside else ow_in

    me = lax.axis_index("seq")
    f = lax.axis_index("fsdp")
    z, y = f // lo, f % lo
    blocks = seq
    length = length_ref[0]
    width = heads * DH
    scale2 = SCALE * LOG2E
    tok_rows = mid_ref.shape[0]
    share = dtotal_ref.shape[1]
    bits, slots = seq_levels(seq)

    def chunk_at(block):
        return pl.ds(pl.multiple_of((block ^ me) * BLOCK, BLOCK), BLOCK)

    def block_loads(block):
        at = chunk_at(block)
        pairs = (
            (qkv_hbm.at[at], qkv_ref.at[at]),
            (mem_hbm.at[block], mem_ref.at[block]),
            (upd_hbm.at[block], upd_ref.at[block]),
        )
        return [pltpu.make_async_copy(a, b, block_sem.at[i, block]) for i, (a, b) in enumerate(pairs)]

    loads = [
        pltpu.make_async_copy(att_hbm, att_ref, load_sem.at[0]),
        pltpu.make_async_copy(db_hbm, db_ref, load_sem.at[1]),
        pltpu.make_async_copy(down_ref.at[me], moved.at[me], load_sem.at[2]),
        pltpu.make_async_copy(mid_hbm, mid_ref, load_sem.at[3]),
        pltpu.make_async_copy(
            wout_hbm.at[pl.ds(pl.multiple_of(me * width, width), width)], wout_ref, load_sem.at[4]
        ),
    ]
    up_loads = [
        pltpu.make_async_copy(up_ref.at[d] if inside else up_ref.at[:, d * lo + y], tu.at[d], up_sem.at[d])
        for d in range(hi)
    ]
    mo_loads = [pltpu.make_async_copy(mo_ref.at[j], mo_low.at[j // 2], mo_sem.at[j // 2]) for j in range(0, seq, 2)]
    for c in up_loads + loads[:2] + loads[4:] + block_loads(blocks - 1) + mo_loads:
        c.start()
    for b in reversed(range(blocks - 1)):
        for c in block_loads(b):
            c.start()
    for c in loads[2:4]:
        c.start()
    greet(list(range(1, seq)), hi, lo)

    def mo_copy(bit, j):
        slot = slots[bit, j]
        return pltpu.make_async_remote_copy(
            src_ref=mo_ref.at[j ^ bit] if bit == 1 else mo_low.at[(j ^ bit) // 2],
            dst_ref=mo_in.at[slot],
            send_sem=m_send.at[slot],
            recv_sem=m_recv.at[slot],
            device_id={"seq": me ^ bit},
            device_id_type=MESH,
        )

    def move_copy(k):
        return pltpu.make_async_remote_copy(
            src_ref=down_ref.at[me ^ k],
            dst_ref=moved.at[me],
            send_sem=e_send.at[k],
            recv_sem=e_recv.at[k],
            device_id={"seq": me ^ k},
            device_id_type=MESH,
        )

    def move_arrival(k):
        return pltpu.make_async_remote_copy(
            src_ref=down_ref.at[me],
            dst_ref=moved.at[me ^ k],
            send_sem=e_send.at[k],
            recv_sem=e_recv.at[k],
            device_id={"seq": me},
            device_id_type=MESH,
        )

    def block_of(i, target):
        if i == 0:
            return ow_ref.at[target]
        if i == 1:
            return up_ref.at[:, target]
        return moved.at[target % seq, pl.ds(pl.multiple_of((target // seq) * share, share), share)]

    start, combine, zsend, zrecv, drain_y, drain_z = line_reduce(
        hi,
        lo,
        block_of,
        (to, tu, dtotal_ref),
        (yo, yu, yd),
        (zo, zu),
        z_send,
        z_recv,
        y_send,
        y_recv,
        {1: up_loads},
    )

    def exchange(k, sending):
        return pltpu.make_async_remote_copy(
            src_ref=tu.at[z, me ^ k] if sending else tu.at[z, me],
            dst_ref=xu.at[me] if sending else xu.at[me ^ k],
            send_sem=x_send.at[k],
            recv_sem=x_recv.at[k],
            device_id={"seq": me ^ k if sending else me},
            device_id_type=MESH,
        )

    if not inside:
        start(1)
    for k in reversed(range(1, seq)):
        move_copy(k).start()
    for j in range(seq - 1, 0, -2):
        mo_copy(1, j ^ 1).start()
    if inside:
        for c in up_loads:
            c.wait()
        zsend(1, 0)
    dmem_ref[...] = sgrad_ref[...].astype(f32)
    dnext_ref[...] = jnp.zeros_like(dnext_ref)
    small_ref[...] = jnp.zeros_like(small_ref)
    near_ref[...] = jnp.zeros_like(near_ref)
    far_ref[...] = jnp.zeros_like(far_ref)
    for head in range(heads):
        bias_ref[head] = tile_bias(vector_ref, head).T
    for c in loads[:2] + loads[4:]:
        c.wait()
    if inside:
        full = t_dot(att_ref[...], db_ref[...]).astype(bf16)
        ow_buf[...] = full.reshape(ow_buf.shape)
    start(0)

    def mo_step(j):
        mo_loads[j // 2].wait()
        for bit in bits:
            if j & bit:
                mo_copy(bit, j ^ bit).start()
                break
            mo_copy(bit, j).wait_recv()
            own = mo_low[j // 2].astype(f32)
            mo_low[j // 2] = (own + mo_in[slots[bit, j]].astype(f32)).astype(bf16)

    def down_ready():
        for k in range(1, seq):
            move_arrival(k).wait_recv()
        loads[2].wait()
        start(2)

    def up_done():
        for k in range(1, seq):
            exchange(k, True).start()

    def zstep(i, t):
        zrecv(i, t)
        if t + 1 < hi - 1:
            zsend(i, t + 1)

    jobs = [lambda j=j: mo_step(j) for j in range(seq - 2, 0, -2)]
    if not inside:
        jobs.append(lambda: (combine(1), zsend(1, 0)))
    jobs.append(lambda: (zstep(1, 0), combine(0), zsend(0, 0)))
    for t in range(1, hi - 1):
        jobs.append(lambda t=t: zstep(1, t))
        if t == 1:
            jobs.append(lambda: down_ready())
    jobs.append(lambda: up_done())
    jobs += [lambda t=t: zstep(0, t) for t in range(hi - 1)]
    points = blocks * heads - 1

    dq_row = heads * DH
    block_loads(blocks - 1)[0].wait()

    @pl.loop(0, blocks)
    def _(step):
        block = blocks - 1 - step
        pl.when(block >= 1)(lambda: block_loads(jnp.maximum(block - 1, 0))[0].wait())
        for c in block_loads(block)[1:]:
            c.wait()
        cur_at = pl.multiple_of((block ^ me) * BLOCK, BLOCK)
        prev_at = pl.multiple_of((jnp.maximum(block - 1, 0) ^ me) * BLOCK, BLOCK)
        base = pl.multiple_of(block * BLOCK, BLOCK)
        cur_ref = qkv_ref.at[pl.ds(cur_at, BLOCK)]
        prev_ref = qkv_ref.at[pl.ds(prev_at, BLOCK)]
        live_block = block * BLOCK < length
        refs = (prev_ref, cur_ref)
        dout_ref[...] = dot_t(db_ref[pl.ds(cur_at, BLOCK)], wout_ref[...]).astype(bf16)
        for head in range(heads):
            for n, job in enumerate(jobs[:points]):
                if (n + 1) % heads == head:
                    pl.when(step == (n + 1) // heads)(lambda job=job: (job(), None)[1])
            own = slice(head * DH, (head + 1) * DH)
            key_cols = slice(width + head * DH, width + (head + 1) * DH)
            value_cols = slice(2 * width + head * DH, 2 * width + (head + 1) * DH)
            memory = mem_ref[block, :, own]
            update = upd_ref[block, :, own]
            low = memory.astype(bf16)
            forget = forget_ref[:, own]
            dmem = dmem_ref[:, own]
            dupd = jnp.where(live_block, (1.0 - forget) * dmem, 0.0).astype(bf16)
            gone = jnp.where(live_block, dmem * (memory - update), 0.0)
            small_ref[dq_row + head : dq_row + head + 1, :] += jnp.sum(gone, axis=0, keepdims=True)
            dmem_new = jnp.where(live_block, forget * dmem, dmem)
            own_key = cur_ref[:, key_cols]
            own_value = cur_ref[:, value_cols]
            squeries = dot(low, query_ref[head]).astype(bf16)
            sdelta = jnp.sum((dupd.astype(f32) * update).T, axis=0, keepdims=True)
            slse = slse_ref[head : head + 1, pl.ds(base, BLOCK)]
            dsquery = jnp.zeros((STATE_VECTORS, DH), f32)
            dkey = []
            dvalue = []
            for part in range(2 * STATE_VECTORS // QTILE):
                own_part = part >= STATE_VECTORS // QTILE
                at = (part % (STATE_VECTORS // QTILE)) * QTILE
                keys = (own_key if own_part else low)[at : at + QTILE]
                values = (own_value if own_part else low)[at : at + QTILE]
                s = dot_t(keys, squeries) * scale2 - slse
                if own_part:
                    position = block * BLOCK + at + lax.broadcasted_iota(jnp.int32, (QTILE, 1), 0)
                    s = jnp.where(position < length, s, -jnp.inf)
                p = jnp.exp2(s)
                dp = dot_t(values, dupd)
                ds = (p * (dp - sdelta)).astype(bf16)
                dvalue.append(dot(p.astype(bf16), dupd))
                dkey.append(dot(ds, squeries))
                dsquery += t_dot(ds, keys)
            half = STATE_VECTORS // QTILE
            dlow = [dvalue[i] + dkey[i] * SCALE for i in range(half)]
            dctx_ref[0, 0:BLOCK] = jnp.zeros((BLOCK, DH), f32)
            dctx_ref[1, 0:BLOCK] = jnp.zeros((BLOCK, DH), f32)
            for i in range(half):
                rows = slice(BLOCK + i * QTILE, BLOCK + (i + 1) * QTILE)
                old = slice(i * QTILE, (i + 1) * QTILE)
                dctx_ref[0, rows] = dkey[half + i] * SCALE + dnext_ref[0, old, own]
                dctx_ref[1, rows] = dvalue[half + i] + dnext_ref[1, old, own]
            dsq = (dsquery * SCALE).astype(bf16)
            small_ref[head * DH : (head + 1) * DH, :] += t_dot(low, dsq)
            dmem_ref[:, own] = dmem_new + dot_t(dsq, query_ref[head])
            for tile in range(BLOCK // QTILE):
                rows = slice(tile * QTILE, (tile + 1) * QTILE)
                here = pl.ds(cur_at + tile * QTILE, QTILE)
                query = cur_ref[rows, own]
                dout = dout_ref[rows, own]
                lse = lse_ref[head : head + 1, pl.ds(base + tile * QTILE, QTILE)]
                delta = jnp.sum((dout.astype(f32) * att_ref[here, own].astype(f32)).T, axis=0, keepdims=True)
                dq = jnp.zeros((QTILE, DH), f32)
                for which, first, end, col in context_pieces(tile):
                    for at in range(first, end, QTILE):
                        keys = refs[which][at : at + QTILE, key_cols]
                        values = refs[which][at : at + QTILE, value_cols]
                        band = col + at - first
                        position = (block - 1 + which) * BLOCK + at + lax.broadcasted_iota(jnp.int32, (QTILE, 1), 0)
                        live = (position >= 0) & (position < length)
                        s = dot_t(keys, query) * scale2 + bias_ref[head, band : band + QTILE, :] - lse
                        p = jnp.exp2(jnp.where(live, s, -jnp.inf))
                        dp = dot_t(values, dout)
                        ds = (p * (dp - delta)).astype(bf16)
                        wide = ds.astype(f32)
                        edge = min(max(SPAN - NEAR - band, 0), QTILE)
                        if edge:
                            far_ref[head] += functools.reduce(jnp.add, [wide[i : i + 8] for i in range(0, edge, 8)])
                        if edge < QTILE:
                            at_near = band + edge - (SPAN - NEAR)
                            near_ref[head, at_near : at_near + QTILE - edge] += wide[edge:]
                        into = slice(which * BLOCK + at, which * BLOCK + at + QTILE)
                        dctx_ref[1, into] += dot(p.astype(bf16), dout)
                        dctx_ref[0, into] += dot(ds, query) * SCALE
                        dq += t_dot(ds, keys)
                for part in range(half):
                    keys = low[part * QTILE : (part + 1) * QTILE]
                    s = dot_t(keys, query) * scale2 - lse
                    p = jnp.exp2(s)
                    dp = dot_t(keys, dout)
                    ds = (p * (dp - delta)).astype(bf16)
                    dlow[part] += dot(p.astype(bf16), dout) + dot(ds, query) * SCALE
                    dq += t_dot(ds, keys)
                dqkv_ref[here, own] = (dq * SCALE).astype(bf16)
            for part in range(half):
                dmem_ref[part * QTILE : (part + 1) * QTILE, own] += dlow[part]
            dnext_ref[0, :, own] = dctx_ref[0, 0:BLOCK]
            dnext_ref[1, :, own] = dctx_ref[1, 0:BLOCK]
            dqkv_ref[pl.ds(cur_at, BLOCK), key_cols] = dctx_ref[0, BLOCK:].astype(bf16)
            dqkv_ref[pl.ds(cur_at, BLOCK), value_cols] = dctx_ref[1, BLOCK:].astype(bf16)

    dqkv_store = pltpu.make_async_copy(dqkv_ref, dqkv_out, out_sem)
    dqkv_store.start()
    for job in jobs[points:]:
        job()
    member = bucket_members()
    lane = lax.broadcasted_iota(jnp.int32, (1, DH), 1)
    for head in range(heads):
        sums = jnp.broadcast_to(diagonal_sums(near_ref[head]), (8, 2 * QTILE))
        table = jnp.dot(sums, member, precision=lax.Precision.HIGHEST, preferred_element_type=f32)[0:1]
        total = jnp.sum(jnp.sum(far_ref[head], axis=0, keepdims=True), axis=1, keepdims=True)
        row = dq_row + heads + head
        small_ref[row : row + 1, :] = table + jnp.where(lane == BUCKETS - 1, total, 0.0)
        row = dq_row + head
        forget = forget_ref[:, head * DH : (head + 1) * DH]
        small_ref[row : row + 1, :] = small_ref[row : row + 1, :] * forget * (1.0 - forget)
    loads[3].wait()
    mo_loads[0].wait()
    for bit in bits:
        mo_copy(bit, 0).wait_recv()
    step = 128
    for r in range(0, tok_rows, step):
        at = slice(r, r + step)
        value = mid_ref[at] + mo_low[0, at].astype(f32)
        for bit in bits:
            value = value + mo_in[slots[bit, 0], at].astype(f32)
        position = me * tok_rows + r + lax.broadcasted_iota(jnp.int32, (step, 1), 0)
        output_ref[at] = (value * jnp.where(position < length, 1.0, 0.0)).astype(bf16)
    combine(2)
    opart_ref[...] = to[z].astype(f32)
    for k in range(1, seq):
        exchange(k, False).wait_recv()
    xu[me] = tu[z, me]
    write_parts(upart_ref, xu, seq, share)
    for i in (0, 2) if inside else (0, 1, 2):
        drain_y(i)
    for i in range(2):
        drain_z(i)
    for bit in bits:
        for j in range(0, seq, 2 * bit):
            mo_copy(bit, j).wait_send()
    for k in range(1, seq):
        move_copy(k).wait_send()
        exchange(k, True).wait_send()
    dqkv_store.wait()


def bucket_members():
    shape = (2 * QTILE, DH)
    row = lax.broadcasted_iota(jnp.int32, shape, 0)
    lane = lax.broadcasted_iota(jnp.int32, shape, 1)
    distance = jnp.where(row < QTILE, row, row - 2 * QTILE) + NEAR - QTILE
    bucket = jnp.minimum(distance, 16)
    for edge in BUCKET_EDGES:
        bucket = bucket + jnp.where(distance >= edge, 1, 0)
    inside = (distance >= 0) & (distance < BLOCK) & (bucket == lane)
    return jnp.where(inside, 1.0, 0.0)


def write_parts(out_ref, pieces, seq, unit):
    if len(out_ref.shape) == 3:
        out_ref[...] = pieces[...].astype(f32)
        return
    count = pieces.shape[2] // unit
    for k in range(seq):
        for c in range(count):
            at = (c * seq + k) * unit
            out_ref[:, at : at + unit] = pieces[k, :, c * unit : (c + 1) * unit].astype(f32)


def attend_back(
    qkv, db, wout, att, mem, upd, lse, slse, sgrad, length, state_query, forget, bias, up, down, mo, mid, seq, fsdp
):
    rows, width3 = qkv.shape
    width = width3 // 3
    heads = width // DH
    dim = db.shape[1]
    lo = 2
    hi = fsdp // lo
    piece, hidden = up.shape[2:]
    share = hidden // fsdp
    tok_rows = mid.shape[0]
    inside = piece % 16 == 0
    blocks = (piece, dim), (seq, piece, hidden), (share, dim)
    small_rows = heads * (DH + 2)
    small_rows += -small_rows % 8
    vmem = pl.BlockSpec(memory_space=pltpu.VMEM)
    anywhere = pl.BlockSpec(memory_space=pl.ANY)
    dma = pltpu.SemaphoreType.DMA

    def buf(*shape):
        return pltpu.VMEM(shape, bf16)

    extra = []
    if not inside:
        extra.append(t_dot(att, db).astype(bf16).reshape(fsdp, piece, dim))
    upart = (piece, hidden * seq) if share % 128 == 0 else (seq, piece, hidden)
    return pl.pallas_call(
        functools.partial(attend_back_kernel, heads, seq, hi, lo, inside),
        out_shape=(
            jax.ShapeDtypeStruct((rows, width3), bf16),
            jax.ShapeDtypeStruct((small_rows, DH), f32),
            jax.ShapeDtypeStruct(upart, f32),
            jax.ShapeDtypeStruct((hi, share, dim), bf16),
            jax.ShapeDtypeStruct((piece, dim), f32),
            jax.ShapeDtypeStruct((tok_rows, dim), bf16),
        ),
        in_specs=[pl.BlockSpec(memory_space=pltpu.SMEM), anywhere, anywhere, anywhere]
        + [anywhere] * 3
        + [vmem] * 6
        + [anywhere] * 4
        + [vmem] * len(extra),
        out_specs=(anywhere,) + (vmem,) * 5,
        scratch_shapes=[
            buf(rows, width3),
            buf(rows, dim),
            buf(rows, width),
            pltpu.VMEM(mem.shape, f32),
            pltpu.VMEM(upd.shape, f32),
            pltpu.VMEM((tok_rows, dim), f32),
            buf(rows, width3),
            buf(width, dim),
            pltpu.VMEM((STATE_VECTORS, width), f32),
            pltpu.VMEM((2, BLOCK, width), f32),
            pltpu.VMEM((2, 2 * BLOCK, DH), f32),
            pltpu.VMEM((heads, SPAN, QTILE), f32),
            pltpu.VMEM((heads, NEAR, QTILE), f32),
            pltpu.VMEM((heads, 8, QTILE), f32),
            buf(BLOCK, width),
            buf(fsdp, piece, dim),
            buf(*down.shape),
            buf(hi, *blocks[0]),
            buf(hi, *blocks[1]),
            buf(hi, *blocks[0]),
            buf(16, 128) if inside else buf(hi, *blocks[1]),
            buf(hi, *blocks[2]),
            buf(2, max(hi - 1, 1), *blocks[0]),
            buf(2, max(hi - 1, 1), *blocks[1]),
            buf(*blocks[1]),
            buf(max(seq // 2, 1), tok_rows, dim),
            buf(max(seq - 1, 1), tok_rows, dim),
            dma((2, 2, hi)),
            dma((2, 2, hi)),
            dma((3, hi)),
            dma((3, hi)),
            dma((seq,)),
            dma((seq,)),
            dma((seq,)),
            dma((seq,)),
            dma((seq,)),
            dma((seq,)),
            dma((5,)),
            dma((3, seq)),
            dma((hi,)),
            dma((seq,)),
            dma,
        ],
        compiler_params=pltpu.CompilerParams(collective_id=4, has_side_effects=True, vmem_limit_bytes=62 << 20),
        cost_estimate=pl.CostEstimate(
            flops=seq * heads * 512 * 2400 * 128 * 10, bytes_accessed=20 << 20, transcendentals=10 << 20
        ),
        name="attend_back",
    )(
        length, qkv, db, wout, att, mem, upd, lse, slse, sgrad, state_query, forget, bias, up, down, mo, mid, *extra
    )


def gather_kernel(seq, hi, lo, *refs):
    refs = list(refs)

    def take(count):
        taken = refs[:count]
        del refs[:count]
        return taken

    tok_ref, grad_ref, wq_ref, ga_ref, gm_ref, wo_ref, wu_ref = take(7)
    toks_ref, grads_ref, wqs_ref, gas_ref, gms_ref, wos_ref, wus_ref, normed_ref, qkv_ref = take(9)
    toks_full, grad_buf, wq_full, ga_full, gm_full, wo_buf, wu_buf, normed_buf, qkv_buf = take(9)
    own_sem, store_sem, seq_send, seq_recv, chunk_sem, z_send, z_recv, y_send, y_recv = take(9)

    me = lax.axis_index("seq")
    f = lax.axis_index("fsdp")
    fsdp = hi * lo
    bits = [1 << i for i in range(seq.bit_length() - 1)]
    high = [bit for bit in reversed(bits) if bit > 1]
    rows, dim = tok_ref.shape
    width = wq_full.shape[2] // 3
    share = wus_ref.shape[2] // fsdp
    every = wq_ref.shape[1] // 3
    loads = [[] for _ in range(7)]

    def load(i, src, dst):
        loads[i].append(pltpu.make_async_copy(src, dst, own_sem.at[i, len(loads[i])]))
        loads[i][-1].start()

    for c in range(3):
        cols = pl.ds(pl.multiple_of(c * every + me * width, width), width)
        load(0, wq_ref.at[:, cols], wq_full.at[f, :, pl.ds(c * width, width)])
    load(1, ga_ref, ga_full.at[f])
    load(2, gm_ref, gm_full.at[f])
    load(3, wo_ref.at[me % 2], wo_buf)
    if wu_ref.shape[1] == wus_ref.shape[2]:
        load(4, wu_ref, wu_buf)
    else:
        for c in range(fsdp):
            cols = pl.ds(pl.multiple_of((c * seq + me) * share, share), share)
            load(4, wu_ref.at[:, cols], wu_buf.at[:, pl.ds(c * share, share)])
    load(5, tok_ref, toks_full.at[0])
    load(6, grad_ref, grad_buf)
    greet(bits, hi, lo)

    pairs = ((tok_ref, toks_full), (grad_ref, grads_ref))

    def seq_copy(i, source, slot, bit):
        src, out = pairs[i]
        return pltpu.make_async_remote_copy(
            src_ref=out.at[source] if source else src,
            dst_ref=out.at[slot],
            send_sem=seq_send.at[i, slot],
            recv_sem=seq_recv.at[i, slot],
            device_id={"seq": me ^ bit},
            device_id_type=MESH,
        )

    sends = []

    def send(i, source, slot, bit):
        sends.append(seq_copy(i, source, slot, bit))
        sends[-1].start()

    fulls = (wq_full, ga_full, gm_full, wos_ref, wus_ref)
    bufs = (None, None, None, wo_buf, wu_buf)
    start, step, arrive, drain = line_gather(
        hi,
        lo,
        lambda i, origin: fulls[i].at[origin],
        lambda i: fulls[i].at[f] if i < 3 else bufs[i],
        z_send,
        z_recv,
        y_send,
        y_recv,
    )
    first, later = (0, 1, 2), (3, 4)
    if high:
        send(0, 0, high[0], high[0])
    if seq > 1:
        send(0, 0, 1, 1)
    for i in first:
        for c in loads[i]:
            c.wait()
        start(i)
    if high:
        send(1, 0, high[0], high[0])
    if seq > 1:
        send(1, 0, 1, 1)
    stores = []

    def store(src, dst, sem):
        stores.append(pltpu.make_async_copy(src, dst, sem))
        stores[-1].start()

    for t in range(hi - 1):
        for i in first:
            step(i, t)
        if t == min(1, hi - 2):
            for i in later:
                for c in loads[i]:
                    c.wait()
                start(i)
            store(wo_buf, wos_ref.at[f], store_sem.at[0])
            store(wu_buf, wus_ref.at[f], store_sem.at[1])
    for c in loads[5] + loads[6]:
        c.wait()
    store(toks_full.at[0], toks_ref.at[0], chunk_sem.at[0, 0])
    store(grad_buf, grads_ref.at[0], store_sem.at[2])
    for i in first:
        arrive(i)
    store(wq_full, wqs_ref, store_sem.at[3])
    gas_ref[...] = jnp.concatenate([ga_full[n] for n in range(fsdp)], axis=1).astype(f32)
    gms_ref[...] = jnp.concatenate([gm_full[n] for n in range(fsdp)], axis=1).astype(f32)
    gain = gas_ref[...]

    def project(j):
        if j:
            store(toks_full.at[j], toks_ref.at[j], chunk_sem.at[0, j])

        @pl.loop(0, rows // 256)
        def _(n):
            at = pl.ds(pl.multiple_of(n * 256, 256), 256)
            into = pl.ds(pl.multiple_of(j * rows + n * 256, 256), 256)
            x = toks_full[j, at].astype(f32)
            rho = lax.rsqrt(jnp.mean(x * x, axis=-1, keepdims=True) + EPSILON)
            normed = (x * rho * gain).astype(bf16)
            normed_buf[into] = normed
            qkv_buf[into] = dot(normed, wq_full[...].reshape(dim, 3 * width)).astype(bf16)

        at = pl.ds(j * rows, rows)
        store(normed_buf.at[at], normed_ref.at[at], chunk_sem.at[1, j])
        store(qkv_buf.at[at], qkv_ref.at[at], chunk_sem.at[2, j])

    hop = [0]

    def advance():
        if hop[0] < hi - 1:
            for i in later:
                step(i, hop[0])
            hop[0] += 1

    project(0)
    advance()
    have = [0]
    for n, bit in enumerate(high):
        if n:
            for j in have:
                send(0, j, j ^ bit, bit)
        for j in have:
            seq_copy(0, 0, j ^ bit, bit).wait_recv()
            send(0, j ^ bit, j ^ bit ^ 1, 1)
        have += [j ^ bit for j in have]
    for j in have:
        if j:
            project(j)
            advance()
        if seq > 1:
            seq_copy(0, 0, j ^ 1, 1).wait_recv()
            project(j ^ 1)
            advance()
    while hop[0] < hi - 1:
        advance()
    have = [0]
    for n, bit in enumerate(high):
        if n:
            for j in have:
                send(1, j, j ^ bit, bit)
        for j in have:
            seq_copy(1, 0, j ^ bit, bit).wait_recv()
            send(1, j ^ bit, j ^ bit ^ 1, 1)
        have += [j ^ bit for j in have]
    if seq > 1:
        for j in have:
            seq_copy(1, 0, j ^ 1, 1).wait_recv()
    for i in later:
        arrive(i)
    for i in first + later:
        drain(i)
    for c in sends:
        c.wait_send()
    for c in stores:
        c.wait()


def gather_start(tokens, grads, w_qkv, gain_a, gain_m, w_out, w_up, seq, fsdp):
    lo = 2
    hi = fsdp // lo
    dim_rows, hidden = w_up.shape
    share = hidden // (seq * fsdp)
    if share % 128:
        w_up = lax.dynamic_slice_in_dim(w_up.reshape(dim_rows, fsdp, seq, share), lax.axis_index("seq"), 1, axis=2)
        w_up = w_up.reshape(dim_rows, fsdp * share)
    rows, dim = tokens.shape
    width3 = w_qkv.shape[1] // seq
    anywhere = pl.BlockSpec(memory_space=pl.ANY)
    vmem = pl.BlockSpec(memory_space=pltpu.VMEM)
    dma = pltpu.SemaphoreType.DMA

    def like(*shape):
        return jax.ShapeDtypeStruct(shape, bf16)

    def buf(*shape):
        return pltpu.VMEM(shape, bf16)

    return pl.pallas_call(
        functools.partial(gather_kernel, seq, hi, lo),
        out_shape=(
            like(seq, rows, dim),
            like(seq, rows, dim),
            like(fsdp, dim_rows, width3),
            jax.ShapeDtypeStruct((1, dim), f32),
            jax.ShapeDtypeStruct((1, dim), f32),
            like(fsdp, *w_out.shape[1:]),
            like(fsdp, dim_rows, hidden // seq),
            like(seq * rows, dim),
            like(seq * rows, width3),
        ),
        in_specs=[anywhere] * 7,
        out_specs=(anywhere,) * 3 + (vmem,) * 2 + (anywhere,) * 4,
        scratch_shapes=[
            buf(seq, rows, dim),
            buf(rows, dim),
            buf(fsdp, dim_rows, width3),
            buf(fsdp, *gain_a.shape),
            buf(fsdp, *gain_m.shape),
            buf(*w_out.shape[1:]),
            buf(dim_rows, hidden // seq),
            buf(seq * rows, dim),
            buf(seq * rows, width3),
            dma((7, max(fsdp, 3))),
            dma((4,)),
            dma((2, seq)),
            dma((2, seq)),
            dma((3, seq)),
        ]
        + line_sems(5, hi),
        compiler_params=pltpu.CompilerParams(collective_id=0, has_side_effects=True, vmem_limit_bytes=48 << 20),
        name="gather_start",
    )(tokens, grads, w_qkv, gain_a, gain_m, w_out, w_up)


def finish_kernel(seq, hi, lo, inside, *refs):
    refs = list(refs)

    def take(count):
        taken = refs[:count]
        del refs[:count]
        return taken

    dqkv_hbm, wqkv_hbm, normed_hbm, down_ref, small_ref, mlp_gain_ref, tok_hbm, dmid_hbm, gain_ref = take(9)
    gq_in = None if inside else take(1)[0]
    tg_ref, rq_ref, rd_ref, dquery_ref, gate_ref, table_ref, again_ref, mgain_ref = take(8)
    dqkv_ref, wqkv_ref, normed_ref, tok_ref, dmid_ref = take(5)
    low, into, acc, gq_buf, tq, td, yq, zq, zd, xq, sy, sz, gains, gy, gz, gs = take(16)
    dn_send, dn_recv, z_send, z_recv, y_send, y_recv, x_send, x_recv, s_send, s_recv, g_send, g_recv = take(12)
    load_sem, dqkv_sem, tg_sem = take(3)
    gq_ref = gq_buf if inside else gq_in

    me = lax.axis_index("seq")
    f = lax.axis_index("fsdp")
    z, y = f // lo, f % lo
    peer = z * lo + 1 - y
    rows, dim = tok_ref.shape
    width = xq.shape[2] // 3
    bits, slots = seq_levels(seq)

    loads = [
        pltpu.make_async_copy(src, dst, load_sem.at[i])
        for i, (src, dst) in enumerate(
            (
                (wqkv_hbm, wqkv_ref),
                (down_ref, td),
                (normed_hbm, normed_ref),
                (tok_hbm, tok_ref),
                (dmid_hbm, dmid_ref),
            )
        )
    ]
    dqkv_loads = {
        j: pltpu.make_async_copy(
            dqkv_hbm.at[pl.ds(j * rows, rows)], dqkv_ref.at[pl.ds(j * rows, rows)], dqkv_sem.at[j]
        )
        for j in range(seq)
    }
    loads[0].start()
    for j in reversed(range(seq)):
        dqkv_loads[j].start()
    for c in loads[1:]:
        c.start()

    barrier = pltpu.get_barrier_semaphore()
    for k in range(1, seq):
        pl.semaphore_signal(barrier, inc=1, device_id={"seq": me ^ k}, device_id_type=MESH)
    for k in range(1, hi):
        pl.semaphore_signal(barrier, inc=1, device_id={"fsdp": lax.rem(z + k, hi) * lo + y}, device_id_type=MESH)
    pl.semaphore_signal(barrier, inc=1, device_id={"fsdp": peer}, device_id_type=MESH)
    pl.semaphore_wait(barrier, seq + hi - 1)

    def remote(src, dst, send, recv, axis, target):
        return pltpu.make_async_remote_copy(
            src_ref=src, dst_ref=dst, send_sem=send, recv_sem=recv, device_id={axis: target}, device_id_type=MESH
        )

    def dn_copy(bit, j):
        slot = slots[bit, j]
        return remote(low.at[j ^ bit], into.at[slot], dn_send.at[slot], dn_recv.at[slot], "seq", me ^ bit)

    start, combine, zsend, zrecv, drain_y, drain_z = line_reduce(
        hi,
        lo,
        lambda i, target: gq_ref.at[:, target],
        (tq, td),
        (yq,),
        (zq, zd),
        z_send,
        z_recv,
        y_send,
        y_recv,
    )

    def exchange(k, sending):
        return remote(
            tq.at[z, me ^ k] if sending else tq.at[z, me],
            xq.at[me] if sending else xq.at[me ^ k],
            x_send.at[k],
            x_recv.at[k],
            "seq",
            me ^ k if sending else me,
        )

    small_y = remote(small_ref, sy, s_send.at[0], s_recv.at[0], "fsdp", peer)
    small_y.start()
    loads[0].wait()
    if not inside:
        start(0)

    def dn_part(j):
        part = dot_t(dqkv_ref[j * rows : (j + 1) * rows], wqkv_ref[...])
        if j % 2:
            low[j] = part.astype(bf16)
            dn_copy(1, j ^ 1).start()
        else:
            acc[...] = part

    def dn_sum(j):
        for bit in bits:
            if j & bit:
                low[j] = acc[...].astype(bf16)
                dn_copy(bit, j ^ bit).start()
                break
            dn_copy(bit, j).wait_recv()
            acc[...] += into[slots[bit, j]].astype(f32)

    for j in reversed(range(2, seq)):
        dqkv_loads[j].wait()
        dn_part(j)
        if j == seq - 1:
            loads[1].wait()
            zsend(1, 0)
        if j % 2 == 0:
            dn_sum(j)
    for j in range(min(2, seq)):
        dqkv_loads[j].wait()
    loads[2].wait()
    if inside:
        for k in range(seq):
            cols = slice(k * (dim // seq), (k + 1) * (dim // seq))
            part = t_dot(normed_ref[:, cols], dqkv_ref[...]).astype(bf16)
            gq_buf[k] = part.reshape(gq_buf.shape[1:])
        start(0)
    def zstep(i, t):
        if t < hi - 1:
            zrecv(i, t)
            if t + 1 < hi - 1:
                zsend(i, t + 1)

    zstep(1, 0)
    small_y.wait_recv()
    sz[z] = small_ref[...] + sy[...]
    small_z = []
    for k in range(1, hi):
        small_z.append(
            remote(sz.at[z], sz.at[z], s_send.at[k], s_recv.at[k], "fsdp", lax.rem(z + k, hi) * lo + y)
        )
        small_z[-1].start()
    for j in reversed(range(min(2, seq))):
        dn_part(j)
    zstep(1, 1)
    for c in loads[3:]:
        c.wait()
    combine(0)
    zsend(0, 0)
    zstep(1, 2)
    for t in range(3, hi - 1):
        zstep(1, t)
    for bit in bits:
        dn_copy(bit, 0).wait_recv()
    gain = gain_ref[...]
    part = jnp.zeros((8, dim), f32)
    step = 128
    for r in range(0, rows, step):
        at = slice(r, r + step)
        dn = acc[at]
        for bit in bits:
            dn = dn + into[slots[bit, 0], at].astype(f32)
        x = tok_ref[at].astype(f32)
        rho = lax.rsqrt(jnp.mean(x * x, axis=-1, keepdims=True) + EPSILON)
        scaled = gain * dn
        mean = jnp.mean(x * scaled, axis=-1, keepdims=True)
        dmid_ref[at] += rho * scaled - x * (rho * rho * rho * mean)
        prod = dn * x * rho
        part += functools.reduce(jnp.add, [prod[n : n + 8] for n in range(0, step, 8)])
    tg_store = pltpu.make_async_copy(dmid_ref, tg_ref, tg_sem)
    tg_store.start()
    gains[0:8] = mlp_gain_ref[...]
    gains[8:16] = part
    gain_y = remote(gains, gy, g_send.at[0], g_recv.at[0], "fsdp", peer)
    gain_y.start()
    zrecv(0, 0)
    if hi > 2:
        zsend(0, 1)
    gain_y.wait_recv()
    gz[z] = gains[...] + gy[...]
    gain_z = []
    for k in range(1, hi):
        gain_z.append(
            remote(gz.at[z], gz.at[z], g_send.at[k], g_recv.at[k], "fsdp", lax.rem(z + k, hi) * lo + y)
        )
        gain_z[-1].start()
    for t in range(1, hi - 1):
        zrecv(0, t)
        if t + 1 < hi - 1:
            zsend(0, t + 1)
    for k in range(1, seq):
        exchange(k, True).start()
    for k in range(1, hi):
        source = lax.rem(z + hi - k, hi)
        remote(gz.at[source], gz.at[source], g_send.at[k], g_recv.at[k], "fsdp", f).wait_recv()
        remote(sz.at[source], sz.at[source], s_send.at[k], s_recv.at[k], "fsdp", f).wait_recv()
    gs[me] = functools.reduce(jnp.add, [gz[d] for d in range(hi)])
    gain_x = []
    for k in range(1, seq):
        gain_x.append(remote(gs.at[me], gs.at[me], g_send.at[hi + k], g_recv.at[hi + k], "seq", me ^ k))
        gain_x[-1].start()
    rd_ref[...] = td[z].astype(f32)
    total = functools.reduce(jnp.add, [sz[d] for d in range(hi)])
    cut, heads = dquery_ref.shape[0], gate_ref.shape[0]
    dquery_ref[...] = total[:cut]
    gate_ref[...] = total[cut : cut + heads]
    table_ref[...] = total[cut + heads : cut + 2 * heads, :BUCKETS]
    xq[me] = tq[z, me]
    for k in range(1, seq):
        exchange(k, False).wait_recv()
    write_parts(rq_ref, xq, seq, width)
    for k in range(1, seq):
        remote(gs.at[me ^ k], gs.at[me ^ k], g_send.at[hi + k], g_recv.at[hi + k], "seq", me).wait_recv()
    total = functools.reduce(jnp.add, [gs[k] for k in range(seq)])
    piece = again_ref.shape[1]
    total = pltpu.roll(total, lax.rem(dim - (me * hi * lo + f) * piece, dim), 1)[:, :DH]
    mgain_ref[...] = jnp.sum(total[0:8], axis=0, keepdims=True)[:, :piece]
    again_ref[...] = jnp.sum(total[8:16], axis=0, keepdims=True)[:, :piece]

    for bit in bits:
        for j in range(0, seq, 2 * bit):
            dn_copy(bit, j).wait_send()
    drain_y(0)
    for i in range(2):
        drain_z(i)
    for k in range(1, seq):
        exchange(k, True).wait_send()
    for c in [small_y, gain_y] + small_z + gain_z + gain_x:
        c.wait_send()
    tg_store.wait()


def finish(dqkv, wqkv, normed, down, small, mlp_gain, tok, dmid, gain, seq, fsdp):
    lo = 2
    hi = fsdp // lo
    rows, dim = tok.shape
    width3 = dqkv.shape[1]
    piece = dim // (seq * fsdp)
    inside = piece % 16 == 0
    heads = width3 // (3 * DH)
    vmem = pl.BlockSpec(memory_space=pltpu.VMEM)
    anywhere = pl.BlockSpec(memory_space=pl.ANY)
    dma = pltpu.SemaphoreType.DMA

    def buf(*shape):
        return pltpu.VMEM(shape, bf16)

    extra = []
    if not inside:
        extra.append(t_dot(normed, dqkv).astype(bf16).reshape(seq, fsdp, piece, width3))
    scratch = [
        buf(*dqkv.shape),
        buf(*wqkv.shape),
        buf(*normed.shape),
        buf(rows, dim),
        pltpu.VMEM((rows, dim), f32),
        buf(seq, rows, dim),
        buf(max(seq - 1, 1), rows, dim),
        pltpu.VMEM((rows, dim), f32),
        buf(seq, fsdp, piece, width3) if inside else buf(16, 128),
        buf(hi, seq, piece, width3),
        buf(*down.shape),
        buf(hi, seq, piece, width3),
        buf(2, max(hi - 1, 1), seq, piece, width3),
        buf(2, max(hi - 1, 1), *down.shape[1:]),
        buf(seq, piece, width3),
        pltpu.VMEM(small.shape, f32),
        pltpu.VMEM((hi,) + small.shape, f32),
        pltpu.VMEM((16, dim), f32),
        pltpu.VMEM((16, dim), f32),
        pltpu.VMEM((hi, 16, dim), f32),
        pltpu.VMEM((seq, 16, dim), f32),
        dma((seq,)),
        dma((seq,)),
        dma((2, 2, hi)),
        dma((2, 2, hi)),
        dma((1, hi)),
        dma((1, hi)),
        dma((seq,)),
        dma((seq,)),
        dma((hi,)),
        dma((hi,)),
        dma((hi + seq,)),
        dma((hi + seq,)),
        dma((5,)),
        dma((seq,)),
        dma,
    ]
    return pl.pallas_call(
        functools.partial(finish_kernel, seq, hi, lo, inside),
        out_shape=(
            jax.ShapeDtypeStruct((rows, dim), f32),
            jax.ShapeDtypeStruct((piece, seq * width3), f32),
            jax.ShapeDtypeStruct(down.shape[1:], f32),
            jax.ShapeDtypeStruct((heads * DH, DH), f32),
            jax.ShapeDtypeStruct((heads, DH), f32),
            jax.ShapeDtypeStruct((heads, BUCKETS), f32),
            jax.ShapeDtypeStruct((1, piece), f32),
            jax.ShapeDtypeStruct((1, piece), f32),
        ),
        in_specs=[anywhere] * 4 + [vmem] * 2 + [anywhere] * 2 + [vmem] * (1 + len(extra)),
        out_specs=(anywhere,) + (vmem,) * 7,
        scratch_shapes=scratch,
        compiler_params=pltpu.CompilerParams(
            collective_id=1, has_side_effects=True, vmem_limit_bytes=60 << 20
        ),
        name="finish",
    )(dqkv, wqkv, normed, down, small, mlp_gain, tok, dmid, gain, *extra)


GELU_P = 0.24
GELU_C = (
    0.08951261885080208,
    0.15562094398234086,
    -0.15437154502074169,
    0.6261054138112487,
    -0.6465313024138201,
    0.5547927291245551,
    -0.125128858665134,
)


def gelu_parts(x):
    size = jnp.abs(x)
    t = 1.0 / (1.0 + GELU_P * size)
    poly = GELU_C[-1] * t
    for c in GELU_C[-2::-1]:
        poly = (poly + c) * t
    bell = jnp.exp2(x * x * (-0.5 * LOG2E))
    tail = poly * bell
    cdf = jnp.where(x < 0.0, tail, 1.0 - tail)
    return x * cdf, cdf + x * bell * (1.0 / math.sqrt(2.0 * math.pi))


def mlp_kernel(seq, hi, lo, sub, length_ref, *refs):
    refs = list(refs)

    def take(count):
        taken = refs[:count]
        del refs[:count]
        return taken

    own_ref, others_ref, tok_ref, grads_ref, wo_hbm, wu_hbm, wd_hbm, gain_ref = take(8)
    mid_out, dmid_out, gsum_ref, db_ref, mo_ref, ug_out, dg_out = take(7)
    staged = len(ug_out.shape) == 4
    att_refs = [own_ref] + [others_ref.at[k] for k in range(1, seq)]
    att_buf, tok_buf, wo_ref, wu_ref, wd_ref, gm, nm, hid, dpre, low, into, acc, mid_ref, ug_ref, dg_ref = take(15)
    load_sem, w_sem, gm_sem, dn_send, dn_recv, db_send, db_recv, mo_sem, own_sem = take(9)
    if staged:
        tu, yu, y_send, y_recv = take(4)
    dbv = low.at[0]
    depth = att_buf.shape[0]

    me = lax.axis_index("seq")
    length = length_ref[0]
    dim = wo_ref.shape[0]
    width = dim // seq
    rows = tok_ref.shape[1]
    share = wu_ref.shape[1]
    subs = rows // sub
    bits, slots = seq_levels(seq)
    order = list(reversed(range(seq)))

    def chunk_loads(j):
        slot = j % depth
        copies = [
            pltpu.make_async_copy(att_refs[k].at[pl.ds(j * rows, rows)], att_buf.at[slot, k], load_sem.at[slot, k])
            for k in range(seq)
        ]
        copies.append(pltpu.make_async_copy(tok_ref.at[j], tok_buf.at[slot], load_sem.at[slot, seq]))
        return copies

    gm_loads = {
        j: pltpu.make_async_copy(grads_ref.at[j], gm.at[pl.ds(j * rows, rows)], gm_sem.at[j]) for j in order
    }
    weights = [
        pltpu.make_async_copy(src, dst, w_sem.at[i])
        for i, (src, dst) in enumerate(((wo_hbm, wo_ref), (wu_hbm, wu_ref), (wd_hbm, wd_ref)))
    ]
    for c in chunk_loads(order[0]) + weights[:1] + (chunk_loads(order[1]) if seq > 1 else []) + weights[1:]:
        c.start()
    for j in order:
        gm_loads[j].start()
    if depth == seq:
        for j in order[2:]:
            for c in chunk_loads(j):
                c.start()

    greet(bits, hi, lo)

    def dn_copy(bit, j, s):
        slot = slots[bit, j]
        at = pl.ds(pl.multiple_of(s * sub, sub), sub)
        return pltpu.make_async_remote_copy(
            src_ref=low.at[j ^ bit, at],
            dst_ref=into.at[slot, at],
            send_sem=dn_send.at[slot, s],
            recv_sem=dn_recv.at[slot, s],
            device_id={"seq": me ^ bit},
            device_id_type=MESH,
        )

    gain = gain_ref[...]

    def forward(j, s):
        slot = j % depth
        at = pl.ds(pl.multiple_of(s * sub, sub), sub)
        here = pl.ds(pl.multiple_of(j * rows + s * sub, sub), sub)
        position = (j ^ me) * rows + s * sub + lax.broadcasted_iota(jnp.int32, (sub, 1), 0)
        live = jnp.where(position < length, 1.0, 0.0)
        masked = (gm[here].astype(f32) * live).astype(bf16)
        gm[here] = masked
        mid = tok_buf[slot, at].astype(f32)
        for k in range(seq):
            own = pl.ds(pl.multiple_of((me ^ k) * width, width), width)
            mid = mid + dot(att_buf[slot, k, at], wo_ref[own])
        rho = lax.rsqrt(jnp.mean(mid * mid, axis=-1, keepdims=True) + EPSILON)
        normed = (mid * rho * gain).astype(bf16)
        nm[here] = normed
        if j == 0:
            mid_ref[at] = mid
        for c in range(0, share, 256):
            cols = slice(c, c + 256)
            value, slope = gelu_parts(dot(normed, wu_ref[:, cols]))
            hid[here, cols] = value.astype(bf16)
            dpre[here, cols] = (dot_t(masked, wd_ref[cols]) * slope).astype(bf16)
        part = dot_t(dpre[here], wu_ref[...])
        if j % 2:
            low[j, at] = part.astype(bf16)
            dn_copy(1, j ^ 1, s).start()
        else:
            acc[at] = part

    def settle(j, s):
        at = pl.ds(pl.multiple_of(s * sub, sub), sub)
        for bit in bits:
            if j & bit:
                low[j, at] = acc[at].astype(bf16)
                dn_copy(bit, j ^ bit, s).start()
                break
            dn_copy(bit, j, s).wait_recv()
            acc[at] += into[slots[bit, j], at].astype(f32)

    for c in weights:
        c.wait()
    for n in range(0, seq, 2):
        pair = order[n : n + 2]
        if n and depth < seq:
            for j in pair:
                for c in chunk_loads(j):
                    c.start()
        for j in pair:
            for c in chunk_loads(j):
                c.wait()
            gm_loads[j].wait()

        @pl.loop(0, subs)
        def _(s):
            for j in pair:
                forward(j, s)
            if pair[-1]:
                settle(pair[-1], s)

    stores = [pltpu.make_async_copy(mid_ref, mid_out, own_sem.at[1])]
    stores[0].start()
    if staged:
        for k in range(seq):
            cols = slice(k * (dim // seq), (k + 1) * (dim // seq))
            ug_ref[k] = t_dot(nm[:, cols], dpre[...]).astype(bf16).reshape(ug_ref.shape[1:])
        start, combine, _, _, drain_y, _ = line_reduce(
            hi, lo, lambda i, target: ug_ref.at[:, target], (tu,), (yu,), (), None, None, y_send, y_recv
        )
        start(0)
    else:
        for c in range(0, dim, 256):
            ug_ref[c : c + 256] = t_dot(nm[:, c : c + 256], dpre[...]).astype(bf16)
        stores.append(pltpu.make_async_copy(ug_ref, ug_out, own_sem.at[2]))
        stores[-1].start()

    def db_copy(source, target, bit, s):
        at = pl.ds(s * sub, sub)
        return pltpu.make_async_remote_copy(
            src_ref=db_ref.at[source, at] if source else dbv.at[at],
            dst_ref=db_ref.at[target, at],
            send_sem=db_send.at[target, s],
            recv_sem=db_recv.at[target, s],
            device_id={"seq": me ^ bit},
            device_id_type=MESH,
        )

    sends = []
    high = [bit for bit in reversed(bits) if bit > 1]

    def send(source, target, bit, s):
        sends.append(db_copy(source, target, bit, s))
        sends[-1].start()

    step = 128
    part = jnp.zeros((8, dim), f32)
    for s in range(subs):
        for bit in bits:
            dn_copy(bit, 0, s).wait_recv()
        for r in range(s * sub, (s + 1) * sub, step):
            at = slice(r, r + step)
            dn = acc[at]
            for bit in bits:
                dn = dn + into[slots[bit, 0], at].astype(f32)
            mid = mid_ref[at]
            rho = lax.rsqrt(jnp.mean(mid * mid, axis=-1, keepdims=True) + EPSILON)
            scaled = gain * dn
            mean = jnp.mean(mid * scaled, axis=-1, keepdims=True)
            dmid = gm[at].astype(f32) + rho * scaled - mid * (rho * rho * rho * mean)
            acc[at] = dmid
            dbv[at] = dmid.astype(bf16)
            prod = dn * mid * rho
            part += functools.reduce(jnp.add, [prod[i : i + 8] for i in range(0, step, 8)])
        if high:
            send(0, high[0], high[0], s)
        if seq > 1:
            send(0, 1, 1, s)
    gsum_ref[...] = part
    stores.append(pltpu.make_async_copy(dbv, db_ref.at[0], own_sem.at[0]))
    stores[-1].start()
    stores.append(pltpu.make_async_copy(acc, dmid_out, own_sem.at[3]))
    stores[-1].start()
    for c in range(0, share, 256):
        dg_ref[c : c + 256] = t_dot(hid[:, c : c + 256], gm[...]).astype(bf16)
    stores.append(pltpu.make_async_copy(dg_ref, dg_out, own_sem.at[4]))
    stores[-1].start()
    for j in range(seq):
        at = slice(j * rows, (j + 1) * rows)
        nm[at] = dot(hid[at], wd_ref[...]).astype(bf16)
        stores.append(pltpu.make_async_copy(nm.at[pl.ds(j * rows, rows)], mo_ref.at[j], mo_sem.at[j]))
        stores[-1].start()
    have = [0]
    for n, bit in enumerate(high):
        if n:
            for j in have:
                for s in range(subs):
                    send(j, j ^ bit, bit, s)
        for j in have:
            for s in range(subs):
                db_copy(0, j ^ bit, bit, s).wait_recv()
                send(j ^ bit, j ^ bit ^ 1, 1, s)
        have += [j ^ bit for j in have]
    if seq > 1:
        for j in have:
            for s in range(subs):
                db_copy(0, j ^ 1, 1, s).wait_recv()
    if staged:
        combine(0)
        stores.append(pltpu.make_async_copy(tu, ug_out, own_sem.at[2]))
        stores[-1].start()
        drain_y(0)
    for c in sends:
        c.wait_send()
    for c in stores:
        c.wait()
    for bit in bits:
        for j in range(0, seq, 2 * bit):
            for s in range(subs):
                dn_copy(bit, j, s).wait_send()


def mlp(length, own, others, tok, grads, wo, wu, wd, gain, fsdp):
    seq, rows, dim = tok.shape
    share = wu.shape[1]
    lo = 2
    hi = fsdp // lo
    piece = dim // (seq * fsdp)
    staged = piece % 16 == 0
    up_shape = (hi, seq, piece, share) if staged else (dim, share)
    sub = 256
    depth = seq if seq <= 4 else 2
    anywhere = pl.BlockSpec(memory_space=pl.ANY)
    vmem = pl.BlockSpec(memory_space=pltpu.VMEM)
    dma = pltpu.SemaphoreType.DMA

    def buf(*shape):
        return pltpu.VMEM(shape, bf16)

    return pl.pallas_call(
        functools.partial(mlp_kernel, seq, hi, lo, sub),
        out_shape=(
            jax.ShapeDtypeStruct((rows, dim), f32),
            jax.ShapeDtypeStruct((rows, dim), f32),
            jax.ShapeDtypeStruct((8, dim), f32),
            jax.ShapeDtypeStruct((seq, rows, dim), bf16),
            jax.ShapeDtypeStruct((seq, rows, dim), bf16),
            jax.ShapeDtypeStruct(up_shape, bf16),
            jax.ShapeDtypeStruct((share, dim), bf16),
        ),
        in_specs=[pl.BlockSpec(memory_space=pltpu.SMEM)] + [anywhere] * 7 + [vmem],
        out_specs=(anywhere, anywhere, vmem, anywhere, anywhere, anywhere, anywhere),
        scratch_shapes=[
            buf(depth, seq, rows, dim // seq),
            buf(depth, rows, dim),
            buf(dim, dim),
            buf(dim, share),
            buf(share, dim),
            buf(seq * rows, dim),
            buf(seq * rows, dim),
            buf(seq * rows, share),
            buf(seq * rows, share),
            buf(seq, rows, dim),
            buf(max(seq - 1, 1), rows, dim),
            pltpu.VMEM((rows, dim), f32),
            pltpu.VMEM((rows, dim), f32),
            buf(seq, fsdp, piece, share) if staged else buf(dim, share),
            buf(share, dim),
            dma((depth, seq + 1)),
            dma((3,)),
            dma((seq,)),
            dma((seq, rows // sub)),
            dma((seq, rows // sub)),
            dma((seq, rows // sub)),
            dma((seq, rows // sub)),
            dma((seq,)),
            dma((5,)),
        ]
        + ([buf(*up_shape), buf(*up_shape), dma((1, hi)), dma((1, hi))] if staged else []),
        compiler_params=pltpu.CompilerParams(collective_id=2, has_side_effects=True, vmem_limit_bytes=62 << 20),
        cost_estimate=pl.CostEstimate(
            flops=2 * rows * seq * dim * (dim + 6 * share), bytes_accessed=32 << 20, transcendentals=rows * seq * share
        ),
        name="mlp",
    )(length, own, others, tok, grads, wo, wu, wd, gain)


def body(
    tokens,
    lengths,
    state_init,
    w_qkv,
    w_out,
    w_up,
    w_down,
    norm_attn,
    norm_mlp,
    rel_bias,
    state_query,
    gate_bias,
    out_grad,
    state_grad,
):
    seq_count = lax.axis_size("seq")
    fsdp_count = lax.axis_size("fsdp")
    seq_at = lax.axis_index("seq")
    heads = H // seq_count
    width = heads * DH
    tok_rows, dim = tokens.shape[1:]
    rows = tok_rows * seq_count
    hidden_all = w_up.shape[1]
    share = hidden_all // (seq_count * fsdp_count)

    piece = dim // (seq_count * fsdp_count)
    all_tokens, all_grad, qkv_w, gain_attn, gain_mlp, own_out, up_w, normed, qkv = gather_start(
        tokens[0],
        out_grad[0],
        w_qkv,
        norm_attn.reshape(1, -1),
        norm_mlp.reshape(1, -1),
        w_out.reshape(2, w_out.shape[0] // 2, dim),
        w_up,
        seq_count,
        fsdp_count,
    )
    qkv_w = qkv_w.reshape(dim, 3 * width)
    up_w = up_w.reshape(dim, hidden_all // seq_count)
    own_down = lax.dynamic_slice_in_dim(w_down, seq_at * share, share, axis=0)

    bias = bias_vector(rel_bias)
    forget = jax.nn.sigmoid(gate_bias)
    forget_row = forget.reshape(1, width)

    attended, others, out_w, down_w, final_memory, mem, upd, lse, slse = attend(
        qkv,
        state_init[0],
        lengths,
        state_query,
        forget_row,
        bias,
        own_out,
        own_down,
        heads,
        seq_count,
        fsdp_count,
    )
    out_w = out_w.reshape(dim, dim)
    down_w = down_w.reshape(fsdp_count * share, dim)
    mid_here, dmid, mlp_gain_grad, dbranch, mlp_parts, up_grad, down_grad = mlp(
        lengths, attended, others, all_tokens, all_grad, out_w, up_w, down_w, gain_mlp, fsdp_count
    )
    span = fsdp_count // seq_count
    if up_grad.ndim == 2:
        up_grad = up_grad.reshape(seq_count, fsdp_count, piece, hidden_all // seq_count)
    dqkv, small, up_part, down_total, out_part, output = attend_back(
        qkv,
        dbranch.reshape(rows, dim),
        out_w,
        attended,
        mem,
        upd,
        lse,
        slse,
        state_grad[0],
        lengths,
        state_query,
        forget_row,
        bias,
        up_grad,
        down_grad.reshape(seq_count, span * share, dim),
        mlp_parts,
        mid_here,
        seq_count,
        fsdp_count,
    )
    tokens_grad, qkv_part, down_part, dquery, grad_gate, grad_table, attn_gain_grad, mlp_gain_grad = finish(
        dqkv,
        qkv_w,
        normed,
        down_total,
        small,
        mlp_gain_grad,
        tokens[0],
        dmid,
        gain_attn,
        seq_count,
        fsdp_count,
    )
    output = output[None]
    tokens_grad = tokens_grad[None]
    dquery = dquery.reshape(heads, DH, DH)
    attn_gain_grad = attn_gain_grad.reshape(piece)
    mlp_gain_grad = mlp_gain_grad.reshape(piece)
    if up_part.ndim == 3:
        up_part = up_part.reshape(seq_count, piece, fsdp_count, share)
        up_part = jnp.transpose(up_part, (1, 2, 0, 3)).reshape(piece, hidden_all)
    return (
        output,
        final_memory[None],
        tokens_grad,
        qkv_part,
        out_part,
        up_part,
        down_part,
        attn_gain_grad,
        mlp_gain_grad,
        grad_table,
        dquery,
        grad_gate,
    )


def solution(mesh):
    placed = (
        P("fsdp", "seq", None),
        P("fsdp"),
        P("fsdp", None, "seq"),
        P("fsdp", None),
        P("fsdp", None),
        P("fsdp", None),
        P("fsdp", None),
        P("fsdp"),
        P("fsdp"),
        P("seq", None),
        P("seq", None, None),
        P("seq", None),
        P("fsdp", "seq", None),
        P("fsdp", None, "seq"),
    )
    return jax.shard_map(
        body,
        mesh=mesh,
        in_specs=placed,
        out_specs=(
            P("fsdp", "seq", None),
            P("fsdp", None, "seq"),
            P("fsdp", "seq", None),
            P(("seq", "fsdp"), None),
            P(("seq", "fsdp"), None),
            P(("seq", "fsdp"), None),
            P(("seq", "fsdp"), None),
            P(("seq", "fsdp")),
            P(("seq", "fsdp")),
            P("seq", None),
            P("seq", None, None),
            P("seq", None),
        ),
        check_vma=False,
    )
```

```python
import functools
import math

import jax
import jax.numpy as jnp
import numpy as np
from jax import lax
from jax.experimental import pallas as pl
from jax.experimental.pallas import tpu as pltpu
from jax.sharding import PartitionSpec as P

H = 8
DH = 128
BLOCK = 512
STATE_VECTORS = 512
QTILE = 256
SPAN = BLOCK + QTILE

EPSILON = 1e-06
BUCKET_EDGES = (19, 21, 24, 27, 31, 35, 40, 46, 52, 59, 67, 77, 87, 99, 113)
BUCKETS = 32
LOG2E = math.log2(math.e)
SCALE = DH ** (-0.5)
NEAR = 384

f32 = jnp.float32
bf16 = jnp.bfloat16
MESH = pl.DeviceIdType.MESH


def bucket_of(distance):
    return np.minimum(distance, 16) + (distance[..., None] >= np.array(BUCKET_EDGES)).sum(-1)


def tile_distance():
    rows = np.arange(QTILE)[:, None]
    cols = np.arange(SPAN)[None, :]
    return rows + BLOCK - cols


def bias_vector(table):
    distance = BLOCK - np.arange(2 * BLOCK)
    inside = (distance >= 0) & (distance < BLOCK)
    bucket = np.where(inside, bucket_of(np.clip(distance, 0, BLOCK)), BUCKETS)
    member = jnp.asarray((np.arange(BUCKETS)[:, None] == bucket[None]).astype(np.float32))
    total = jnp.dot(table, member, precision=lax.Precision.HIGHEST, preferred_element_type=f32)
    return jnp.where(jnp.asarray(inside)[None], total * LOG2E, -jnp.inf)


def tile_bias(vector_ref, head):
    wide = jnp.broadcast_to(vector_ref[head : head + 1, :], (QTILE, 2 * BLOCK))
    return pltpu.roll(wide, 0, 1, stride=1, stride_axis=0)[:, :SPAN]


def dot(a, b):
    return jnp.dot(a, b, preferred_element_type=f32)


def dot_t(a, b):
    return lax.dot_general(a, b, (((1,), (1,)), ((), ())), preferred_element_type=f32)


def t_dot(a, b):
    return lax.dot_general(a, b, (((0,), (0,)), ((), ())), preferred_element_type=f32)


def to_row(column):
    wide = jnp.broadcast_to(column, (column.shape[0], 128))
    return wide.T[0:1, :]


def context_pieces(tile):
    start = tile * QTILE
    pieces = []
    if start < BLOCK:
        pieces.append((0, start, BLOCK, 0))
    pieces.append((1, 0, start + QTILE, BLOCK - start))
    return pieces


def softmax_parts(scores):
    top = functools.reduce(jnp.maximum, [jnp.max(s, axis=-1, keepdims=True) for s in scores])
    raised = [jnp.exp2(s - top) for s in scores]
    total = functools.reduce(jnp.add, [jnp.sum(e, axis=-1, keepdims=True) for e in raised])
    return raised, total, top + jnp.log2(total)


def line_gather(hi, lo, slot, own, z_send, z_recv, y_send, y_recv):
    f = lax.axis_index("fsdp")
    z, y = f // lo, f % lo

    def copy(i, origin, target, send, recv, first=False):
        ref = slot(i, origin)
        return pltpu.make_async_remote_copy(
            src_ref=own(i) if first else ref,
            dst_ref=ref,
            send_sem=send,
            recv_sem=recv,
            device_id={"fsdp": target},
            device_id_type=MESH,
        )

    def right(i, t):
        return copy(i, (z - t) * lo + y, (z + 1) * lo + y, z_send.at[i, 0, t], z_recv.at[i, 0, t], t == 0)

    def left(i, t):
        return copy(i, (z + t) * lo + y, (z - 1) * lo + y, z_send.at[i, 1, t], z_recv.at[i, 1, t], t == 0)

    def across(i, d):
        return copy(
            i, (z + d) * lo + y, z * lo + 1 - y, y_send.at[i, d + hi - 1], y_recv.at[i, d + hi - 1], d == 0
        )

    def start(i):
        pl.when(z + 1 < hi)(lambda: right(i, 0).start())
        pl.when(z >= 1)(lambda: left(i, 0).start())
        across(i, 0).start()

    def step(i, t):
        @pl.when(z - 1 - t >= 0)
        def _():
            copy(i, (z - 1 - t) * lo + y, f, z_send.at[i, 0, t], z_recv.at[i, 0, t]).wait_recv()
            if t + 1 < hi - 1:
                pl.when(z + 1 < hi)(lambda: right(i, t + 1).start())
            across(i, -1 - t).start()

        @pl.when(z + 1 + t < hi)
        def _():
            copy(i, (z + 1 + t) * lo + y, f, z_send.at[i, 1, t], z_recv.at[i, 1, t]).wait_recv()
            if t + 1 < hi - 1:
                pl.when(z >= 1)(lambda: left(i, t + 1).start())
            across(i, 1 + t).start()

    def arrive(i):
        for d in range(1 - hi, hi):

            @pl.when((z + d >= 0) & (z + d < hi))
            def _():
                copy(
                    i, (z + d) * lo + 1 - y, f, y_send.at[i, d + hi - 1], y_recv.at[i, d + hi - 1]
                ).wait_recv()

    def drain(i):
        for d in range(1 - hi, hi):

            @pl.when((z + d >= 0) & (z + d < hi))
            def _():
                across(i, d).wait_send()

        for t in range(hi - 1):

            @pl.when((z + 1 < hi) & (z - t >= 0))
            def _():
                right(i, t).wait_send()

            @pl.when((z >= 1) & (z + t < hi))
            def _():
                left(i, t).wait_send()

    return start, step, arrive, drain


def line_sems(count, hi):
    dma = pltpu.SemaphoreType.DMA
    return [dma((count, 2, hi)), dma((count, 2, hi)), dma((count, 2 * hi)), dma((count, 2 * hi))]


def greet(seq_targets, hi, lo):
    me = lax.axis_index("seq")
    f = lax.axis_index("fsdp")
    z, y = f // lo, f % lo
    barrier = pltpu.get_barrier_semaphore()
    for k in seq_targets:
        pl.semaphore_signal(barrier, inc=1, device_id={"seq": me ^ k}, device_id_type=MESH)
    near = (lax.rem(z + 1, hi) * lo + y, lax.rem(z + hi - 1, hi) * lo + y, z * lo + 1 - y)
    for target in near:
        pl.semaphore_signal(barrier, inc=1, device_id={"fsdp": target}, device_id_type=MESH)
    pl.semaphore_wait(barrier, len(seq_targets) + len(near))


def attend_kernel(
    heads,
    seq,
    hi,
    lo,
    length_ref,
    qkv_ref,
    init_ref,
    query_ref,
    forget_ref,
    vector_ref,
    own_out_ref,
    own_down_ref,
    att_out,
    others_ref,
    outs_ref,
    downs_ref,
    final_ref,
    mem_out,
    upd_out,
    lse_ref,
    slse_ref,
    memory_ref,
    bias_ref,
    att_ref,
    mem_ref,
    upd_ref,
    store_sem,
    own_sem,
    att_send,
    att_recv,
    out_send,
    out_recv,
    z_send,
    z_recv,
    y_send,
    y_recv,
):
    me = lax.axis_index("seq")
    f = lax.axis_index("fsdp")
    length = length_ref[0]
    width = heads * DH
    scale2 = SCALE * LOG2E
    blocks = seq
    bits = [1 << i for i in range(seq.bit_length() - 1)]
    greet(bits, hi, lo)

    own_copies = [
        pltpu.make_async_copy(own_down_ref, downs_ref.at[f], own_sem.at[0]),
        pltpu.make_async_copy(own_out_ref, outs_ref.at[:, me % 2], own_sem.at[1]),
    ]
    for c in own_copies:
        c.start()

    def lowest(k):
        return k & -k

    def out_copy(sending):
        half = me % 2 if sending else 1 - me % 2
        return pltpu.make_async_remote_copy(
            src_ref=own_out_ref,
            dst_ref=outs_ref.at[:, half],
            send_sem=out_send,
            recv_sem=out_recv,
            device_id={"seq": me ^ 1},
            device_id_type=MESH,
        )

    def att_copy(k, b):
        bit = lowest(k)
        came = k ^ bit
        here = pl.ds(pl.multiple_of((b ^ me) * BLOCK, BLOCK), BLOCK)
        there = pl.ds(pl.multiple_of((b ^ me ^ bit) * BLOCK, BLOCK), BLOCK)
        src = others_ref.at[came, here] if came else att_ref.at[here]
        return pltpu.make_async_remote_copy(
            src_ref=src,
            dst_ref=others_ref.at[k, there],
            send_sem=att_send.at[k, b],
            recv_sem=att_recv.at[k, b],
            device_id={"seq": me ^ bit},
            device_id_type=MESH,
        )

    def att_arrival(k, b):
        here = pl.ds(pl.multiple_of((b ^ me) * BLOCK, BLOCK), BLOCK)
        return pltpu.make_async_remote_copy(
            src_ref=others_ref.at[k, here],
            dst_ref=others_ref.at[k, here],
            send_sem=att_send.at[k, b],
            recv_sem=att_recv.at[k, b],
            device_id={"seq": me},
            device_id_type=MESH,
        )

    passing = sorted([k for k in range(2, seq, 2)], key=lambda k: (bin(k).count("1"), -k))

    def onward(k, send):
        for bit in reversed(bits):
            if bit < lowest(k):
                send(k | bit)

    start, step, arrive, drain = line_gather(
        hi, lo, lambda i, origin: downs_ref.at[origin], lambda i: own_down_ref, z_send, z_recv, y_send, y_recv
    )

    start(0)
    out_copy(True).start()
    memory_ref[...] = init_ref[...].astype(f32)
    for head in range(heads):
        bias_ref[head] = tile_bias(vector_ref, head)

    def block_stores(block):
        at = pl.ds(pl.multiple_of((block ^ me) * BLOCK, BLOCK), BLOCK)
        pairs = (
            (att_ref.at[at], att_out.at[at]),
            (mem_ref.at[block], mem_out.at[block]),
            (upd_ref.at[block], upd_out.at[block]),
        )
        return [pltpu.make_async_copy(a, b, store_sem.at[i, block]) for i, (a, b) in enumerate(pairs)]

    @pl.loop(0, blocks)
    def _(block):
        cur_at = pl.multiple_of((block ^ me) * BLOCK, BLOCK)
        prev_at = pl.multiple_of((jnp.maximum(block - 1, 0) ^ me) * BLOCK, BLOCK)
        cur_ref = qkv_ref.at[pl.ds(cur_at, BLOCK)]
        prev_ref = qkv_ref.at[pl.ds(prev_at, BLOCK)]
        for t in range(min(hi - 1, blocks - 1)):
            pl.when(block == t + 1)(lambda t=t: step(0, t))

        live_block = block * BLOCK < length
        for head in range(heads):
            own = slice(head * DH, (head + 1) * DH)
            memory = memory_ref[:, own]
            low = memory.astype(bf16)
            mem_ref[block, :, own] = memory
            refs = (prev_ref, cur_ref)
            key_cols = slice(width + head * DH, width + (head + 1) * DH)
            value_cols = slice(2 * width + head * DH, 2 * width + (head + 1) * DH)
            for tile in range(BLOCK // QTILE):
                rows = slice(tile * QTILE, (tile + 1) * QTILE)
                query = cur_ref[rows, own]
                scores, values = [], []
                for which, at, end, col in context_pieces(tile):
                    s = dot_t(query, refs[which][at:end, key_cols])
                    position = (block - 1 + which) * BLOCK + at + lax.broadcasted_iota(jnp.int32, (1, end - at), 1)
                    live = (position >= 0) & (position < length)
                    s = s * scale2 + bias_ref[head, :, col : col + end - at]
                    scores.append(jnp.where(live, s, -jnp.inf))
                    values.append(refs[which][at:end, value_cols])
                scores.append(dot_t(query, low) * scale2)
                values.append(low)
                raised, total, lse = softmax_parts(scores)
                out = functools.reduce(jnp.add, [dot(e.astype(bf16), v) for e, v in zip(raised, values)])
                att_ref[pl.ds(cur_at + tile * QTILE, QTILE), own] = (out / total).astype(bf16)
                lse_ref[head : head + 1, pl.ds(pl.multiple_of(block * BLOCK, BLOCK) + tile * QTILE, QTILE)] = to_row(lse)
            own_key = cur_ref[:, key_cols]
            own_value = cur_ref[:, value_cols]
            squeries = dot(low, query_ref[head]).astype(bf16)
            position = block * BLOCK + lax.broadcasted_iota(jnp.int32, (1, BLOCK), 1)
            for tile in range(STATE_VECTORS // QTILE):
                rows = slice(tile * QTILE, (tile + 1) * QTILE)
                squery = squeries[rows]
                scores = [
                    dot_t(squery, low) * scale2,
                    jnp.where(position < length, dot_t(squery, own_key) * scale2, -jnp.inf),
                ]
                raised, total, lse = softmax_parts(scores)
                update = dot(raised[0].astype(bf16), low) + dot(raised[1].astype(bf16), own_value)
                update = update / total
                upd_ref[block, rows, own] = update
                slse_ref[head : head + 1, pl.ds(pl.multiple_of(block * BLOCK, BLOCK) + tile * QTILE, QTILE)] = to_row(
                    lse
                )
                forget = forget_ref[:, own]
                old = memory[rows]
                memory_ref[rows, own] = jnp.where(live_block, forget * old + (1.0 - forget) * update, old)

        for bit in reversed(bits):
            att_copy(bit, block).start()
        for c in block_stores(block):
            c.start()

        @pl.when(block >= 1)
        def _():
            for k in passing:
                att_arrival(k, block - 1).wait_recv()
                onward(k, lambda target: att_copy(target, block - 1).start())

    final_ref[...] = memory_ref[...]
    for t in range(min(hi - 1, blocks - 1), hi - 1):
        step(0, t)
    for k in passing:
        att_arrival(k, blocks - 1).wait_recv()
        onward(k, lambda target: att_copy(target, blocks - 1).start())
    arrive(0)
    out_copy(False).wait_recv()
    for k in range(1, seq, 2):
        for b in range(blocks):
            att_arrival(k, b).wait_recv()
    for c in own_copies:
        c.wait()
    drain(0)
    for b in range(blocks):
        for c in block_stores(b):
            c.wait()
    out_copy(True).wait_send()
    for k in range(1, seq):
        for b in range(blocks):
            att_copy(k, b).wait_send()


def attend(qkv, init, length, state_query, forget, bias, own_out, own_down, heads, seq, fsdp):
    rows, width3 = qkv.shape
    width = heads * DH
    blocks = rows // BLOCK
    lo = 2
    hi = fsdp // lo
    dim = own_down.shape[1]
    anywhere = pl.BlockSpec(memory_space=pl.ANY)
    vmem = pl.BlockSpec(memory_space=pltpu.VMEM)
    dma = pltpu.SemaphoreType.DMA
    return pl.pallas_call(
        functools.partial(attend_kernel, heads, seq, hi, lo),
        out_shape=(
            jax.ShapeDtypeStruct((rows, width), bf16),
            jax.ShapeDtypeStruct((seq, rows, width), bf16),
            jax.ShapeDtypeStruct((fsdp, 2) + own_out.shape[1:], bf16),
            jax.ShapeDtypeStruct((fsdp,) + own_down.shape, bf16),
            jax.ShapeDtypeStruct((STATE_VECTORS, width), f32),
            jax.ShapeDtypeStruct((blocks, STATE_VECTORS, width), f32),
            jax.ShapeDtypeStruct((blocks, STATE_VECTORS, width), f32),
            jax.ShapeDtypeStruct((heads, rows), f32),
            jax.ShapeDtypeStruct((heads, blocks * STATE_VECTORS), f32),
        ),
        in_specs=[pl.BlockSpec(memory_space=pltpu.SMEM)] + [vmem] * 7,
        out_specs=(anywhere, anywhere, anywhere, anywhere, vmem, anywhere, anywhere, vmem, vmem),
        scratch_shapes=[
            pltpu.VMEM((STATE_VECTORS, width), f32),
            pltpu.VMEM((heads, QTILE, SPAN), f32),
            pltpu.VMEM((rows, width), bf16),
            pltpu.VMEM((blocks, STATE_VECTORS, width), f32),
            pltpu.VMEM((blocks, STATE_VECTORS, width), f32),
            dma((3, blocks)),
            dma((2,)),
            dma((seq, blocks)),
            dma((seq, blocks)),
            dma,
            dma,
        ]
        + line_sems(1, hi),
        compiler_params=pltpu.CompilerParams(collective_id=3, has_side_effects=True, vmem_limit_bytes=62 << 20),
        cost_estimate=pl.CostEstimate(
            flops=blocks * heads * 512 * 2400 * 128 * 4, bytes_accessed=16 << 20, transcendentals=10 << 20
        ),
        name="attend",
    )(length, qkv, init, state_query, forget, bias, own_out, own_down)


def line_reduce(hi, lo, block, total, from_y, from_z, z_send, z_recv, y_send, y_recv, loads=None):
    loads = loads or {}
    f = lax.axis_index("fsdp")
    z, y = f // lo, f % lo

    def remote(src, dst, send, recv, target):
        return pltpu.make_async_remote_copy(
            src_ref=src, dst_ref=dst, send_sem=send, recv_sem=recv, device_id={"fsdp": target}, device_id_type=MESH
        )

    def across(i, d):
        return remote(
            block(i, d * lo + 1 - y), from_y[i].at[d], y_send.at[i, d], y_recv.at[i, d], z * lo + 1 - y
        )

    def start(i):
        for d in range(hi):
            across(i, d).start()

    def combine(i):
        for d in range(hi):
            across(i, d).wait_recv()
            if i in loads:
                loads[i][d].wait()
                own = total[i].at[d]
            else:
                own = block(i, d * lo + y)
            total[i][d] = (own[...].astype(f32) + from_y[i][d].astype(f32)).astype(bf16)

    def hop(i, side, t, at, target):
        return remote(
            total[i].at[jnp.clip(at, 0, hi - 1)],
            from_z[i].at[side, t],
            z_send.at[i, side, t],
            z_recv.at[i, side, t],
            target,
        )

    def sending(t):
        d = t - (hi - 1 - z)
        m = hi - 1 - (t - z)
        return ((0, d, (d >= 0) & (d < z), z - 1), (1, m, (m > z) & (m < hi), z + 1))

    def zsend(i, t):
        for side, at, cond, target in sending(t):
            pl.when(cond)(lambda: hop(i, side, t, at, target * lo + y).start())

    def zrecv(i, t):
        d = t - (hi - 2 - z)
        m = hi - 1 - (t - (z - 1))
        for side, at, cond in ((0, d, (z + 1 < hi) & (d >= 0)), (1, m, (z > 0) & (m < hi))):

            @pl.when(cond)
            def _():
                hop(i, side, t, at, f).wait_recv()
                slot = jnp.clip(at, 0, hi - 1)
                total[i][slot] = (total[i][slot].astype(f32) + from_z[i][side, t].astype(f32)).astype(bf16)

    def drain_y(i):
        for d in range(hi):
            across(i, d).wait_send()

    def drain_z(i):
        for t in range(hi - 1):
            for side, at, cond, target in sending(t):
                pl.when(cond)(lambda: hop(i, side, t, at, f).wait_send())

    return start, combine, zsend, zrecv, drain_y, drain_z


def seq_levels(seq):
    bits = [1 << i for i in range(seq.bit_length() - 1)]
    slots = {}
    for bit in bits:
        for j in range(0, seq, 2 * bit):
            slots[bit, j] = len(slots)
    return bits, slots


def diagonal_sums(tile):
    rows, lanes = tile.shape
    wide = jnp.concatenate([tile, jnp.zeros((rows, lanes), f32)], axis=1)
    row = lax.broadcasted_iota(jnp.int32, wide.shape, 0)
    bit = 1
    while bit < rows:
        wide = jnp.where((row & bit) != 0, pltpu.roll(wide, 2 * lanes - bit, 1), wide)
        bit *= 2
    return jnp.sum(wide, axis=0, keepdims=True)


def attend_back_kernel(heads, seq, hi, lo, inside, length_ref, *refs):
    refs = list(refs)

    def take(count):
        taken = refs[:count]
        del refs[:count]
        return taken

    qkv_hbm, db_hbm, wout_hbm, att_hbm, mem_hbm, upd_hbm, lse_ref, slse_ref = take(8)
    sgrad_ref, query_ref, forget_ref, vector_ref, up_ref, down_ref, mo_ref, mid_hbm = take(8)
    ow_in = None if inside else take(1)[0]
    dqkv_out, small_ref, upart_ref, dtotal_ref, opart_ref, output_ref = take(6)
    qkv_ref, db_ref, att_ref, mem_ref, upd_ref, mid_ref, dqkv_ref, wout_ref = take(8)
    dmem_ref, dnext_ref, dctx_ref, bias_ref, near_ref, far_ref, dout_ref, ow_buf = take(8)
    moved, to, tu, yo, yu, yd, zo, zu, xu, mo_low, mo_in = take(11)
    z_send, z_recv, y_send, y_recv, m_send, m_recv, e_send, e_recv, x_send, x_recv = take(10)
    load_sem, block_sem, up_sem, mo_sem, out_sem = take(5)
    ow_ref = ow_buf if inside else ow_in

    me = lax.axis_index("seq")
    f = lax.axis_index("fsdp")
    z, y = f // lo, f % lo
    blocks = seq
    length = length_ref[0]
    width = heads * DH
    scale2 = SCALE * LOG2E
    tok_rows = mid_ref.shape[0]
    share = dtotal_ref.shape[1]
    bits, slots = seq_levels(seq)

    def chunk_at(block):
        return pl.ds(pl.multiple_of((block ^ me) * BLOCK, BLOCK), BLOCK)

    def block_loads(block):
        at = chunk_at(block)
        pairs = (
            (qkv_hbm.at[at], qkv_ref.at[at]),
            (mem_hbm.at[block], mem_ref.at[block]),
            (upd_hbm.at[block], upd_ref.at[block]),
        )
        return [pltpu.make_async_copy(a, b, block_sem.at[i, block]) for i, (a, b) in enumerate(pairs)]

    loads = [
        pltpu.make_async_copy(att_hbm, att_ref, load_sem.at[0]),
        pltpu.make_async_copy(db_hbm, db_ref, load_sem.at[1]),
        pltpu.make_async_copy(down_ref.at[me], moved.at[me], load_sem.at[2]),
        pltpu.make_async_copy(mid_hbm, mid_ref, load_sem.at[3]),
        pltpu.make_async_copy(
            wout_hbm.at[pl.ds(pl.multiple_of(me * width, width), width)], wout_ref, load_sem.at[4]
        ),
    ]
    up_loads = [
        pltpu.make_async_copy(up_ref.at[d] if inside else up_ref.at[:, d * lo + y], tu.at[d], up_sem.at[d])
        for d in range(hi)
    ]
    mo_loads = [pltpu.make_async_copy(mo_ref.at[j], mo_low.at[j // 2], mo_sem.at[j // 2]) for j in range(0, seq, 2)]
    for c in up_loads + loads[:2] + loads[4:] + block_loads(blocks - 1) + mo_loads:
        c.start()
    for b in reversed(range(blocks - 1)):
        for c in block_loads(b):
            c.start()
    for c in loads[2:4]:
        c.start()
    greet(list(range(1, seq)), hi, lo)

    def mo_copy(bit, j):
        slot = slots[bit, j]
        return pltpu.make_async_remote_copy(
            src_ref=mo_ref.at[j ^ bit] if bit == 1 else mo_low.at[(j ^ bit) // 2],
            dst_ref=mo_in.at[slot],
            send_sem=m_send.at[slot],
            recv_sem=m_recv.at[slot],
            device_id={"seq": me ^ bit},
            device_id_type=MESH,
        )

    def move_copy(k):
        return pltpu.make_async_remote_copy(
            src_ref=down_ref.at[me ^ k],
            dst_ref=moved.at[me],
            send_sem=e_send.at[k],
            recv_sem=e_recv.at[k],
            device_id={"seq": me ^ k},
            device_id_type=MESH,
        )

    def move_arrival(k):
        return pltpu.make_async_remote_copy(
            src_ref=down_ref.at[me],
            dst_ref=moved.at[me ^ k],
            send_sem=e_send.at[k],
            recv_sem=e_recv.at[k],
            device_id={"seq": me},
            device_id_type=MESH,
        )

    def block_of(i, target):
        if i == 0:
            return ow_ref.at[target]
        if i == 1:
            return up_ref.at[:, target]
        return moved.at[target % seq, pl.ds(pl.multiple_of((target // seq) * share, share), share)]

    start, combine, zsend, zrecv, drain_y, drain_z = line_reduce(
        hi,
        lo,
        block_of,
        (to, tu, dtotal_ref),
        (yo, yu, yd),
        (zo, zu),
        z_send,
        z_recv,
        y_send,
        y_recv,
        {1: up_loads},
    )

    def exchange(k, sending):
        return pltpu.make_async_remote_copy(
            src_ref=tu.at[z, me ^ k] if sending else tu.at[z, me],
            dst_ref=xu.at[me] if sending else xu.at[me ^ k],
            send_sem=x_send.at[k],
            recv_sem=x_recv.at[k],
            device_id={"seq": me ^ k if sending else me},
            device_id_type=MESH,
        )

    if not inside:
        start(1)
    for k in reversed(range(1, seq)):
        move_copy(k).start()
    for j in range(seq - 1, 0, -2):
        mo_copy(1, j ^ 1).start()
    if inside:
        for c in up_loads:
            c.wait()
        zsend(1, 0)
    dmem_ref[...] = sgrad_ref[...].astype(f32)
    dnext_ref[...] = jnp.zeros_like(dnext_ref)
    small_ref[...] = jnp.zeros_like(small_ref)
    near_ref[...] = jnp.zeros_like(near_ref)
    far_ref[...] = jnp.zeros_like(far_ref)
    for head in range(heads):
        bias_ref[head] = tile_bias(vector_ref, head).T
    for c in loads[:2] + loads[4:]:
        c.wait()
    if inside:
        full = t_dot(att_ref[...], db_ref[...]).astype(bf16)
        ow_buf[...] = full.reshape(ow_buf.shape)
    start(0)

    def mo_step(j):
        mo_loads[j // 2].wait()
        for bit in bits:
            if j & bit:
                mo_copy(bit, j ^ bit).start()
                break
            mo_copy(bit, j).wait_recv()
            own = mo_low[j // 2].astype(f32)
            mo_low[j // 2] = (own + mo_in[slots[bit, j]].astype(f32)).astype(bf16)

    def down_ready():
        for k in range(1, seq):
            move_arrival(k).wait_recv()
        loads[2].wait()
        start(2)

    def up_done():
        for k in range(1, seq):
            exchange(k, True).start()

    def zstep(i, t):
        zrecv(i, t)
        if t + 1 < hi - 1:
            zsend(i, t + 1)

    jobs = [lambda j=j: mo_step(j) for j in range(seq - 2, 0, -2)]
    if not inside:
        jobs.append(lambda: (combine(1), zsend(1, 0)))
    jobs.append(lambda: (zstep(1, 0), combine(0), zsend(0, 0)))
    for t in range(1, hi - 1):
        jobs.append(lambda t=t: zstep(1, t))
        if t == 1:
            jobs.append(lambda: down_ready())
    jobs.append(lambda: up_done())
    jobs += [lambda t=t: zstep(0, t) for t in range(hi - 1)]
    points = blocks * heads - 1

    dq_row = heads * DH
    block_loads(blocks - 1)[0].wait()

    @pl.loop(0, blocks)
    def _(step):
        block = blocks - 1 - step
        pl.when(block >= 1)(lambda: block_loads(jnp.maximum(block - 1, 0))[0].wait())
        for c in block_loads(block)[1:]:
            c.wait()
        cur_at = pl.multiple_of((block ^ me) * BLOCK, BLOCK)
        prev_at = pl.multiple_of((jnp.maximum(block - 1, 0) ^ me) * BLOCK, BLOCK)
        base = pl.multiple_of(block * BLOCK, BLOCK)
        cur_ref = qkv_ref.at[pl.ds(cur_at, BLOCK)]
        prev_ref = qkv_ref.at[pl.ds(prev_at, BLOCK)]
        live_block = block * BLOCK < length
        refs = (prev_ref, cur_ref)
        dout_ref[...] = dot_t(db_ref[pl.ds(cur_at, BLOCK)], wout_ref[...]).astype(bf16)
        for head in range(heads):
            for n, job in enumerate(jobs[:points]):
                if (n + 1) % heads == head:
                    pl.when(step == (n + 1) // heads)(lambda job=job: (job(), None)[1])
            own = slice(head * DH, (head + 1) * DH)
            key_cols = slice(width + head * DH, width + (head + 1) * DH)
            value_cols = slice(2 * width + head * DH, 2 * width + (head + 1) * DH)
            memory = mem_ref[block, :, own]
            update = upd_ref[block, :, own]
            low = memory.astype(bf16)
            forget = forget_ref[:, own]
            dmem = dmem_ref[:, own]
            dupd = jnp.where(live_block, (1.0 - forget) * dmem, 0.0).astype(bf16)
            gone = jnp.where(live_block, dmem * (memory - update), 0.0)
            small_ref[dq_row + head : dq_row + head + 1, :] += jnp.sum(gone, axis=0, keepdims=True)
            dmem_new = jnp.where(live_block, forget * dmem, dmem)
            own_key = cur_ref[:, key_cols]
            own_value = cur_ref[:, value_cols]
            squeries = dot(low, query_ref[head]).astype(bf16)
            sdelta = jnp.sum((dupd.astype(f32) * update).T, axis=0, keepdims=True)
            slse = slse_ref[head : head + 1, pl.ds(base, BLOCK)]
            dsquery = jnp.zeros((STATE_VECTORS, DH), f32)
            dkey = []
            dvalue = []
            for part in range(2 * STATE_VECTORS // QTILE):
                own_part = part >= STATE_VECTORS // QTILE
                at = (part % (STATE_VECTORS // QTILE)) * QTILE
                keys = (own_key if own_part else low)[at : at + QTILE]
                values = (own_value if own_part else low)[at : at + QTILE]
                s = dot_t(keys, squeries) * scale2 - slse
                if own_part:
                    position = block * BLOCK + at + lax.broadcasted_iota(jnp.int32, (QTILE, 1), 0)
                    s = jnp.where(position < length, s, -jnp.inf)
                p = jnp.exp2(s)
                dp = dot_t(values, dupd)
                ds = (p * (dp - sdelta)).astype(bf16)
                dvalue.append(dot(p.astype(bf16), dupd))
                dkey.append(dot(ds, squeries))
                dsquery += t_dot(ds, keys)
            half = STATE_VECTORS // QTILE
            dlow = [dvalue[i] + dkey[i] * SCALE for i in range(half)]
            dctx_ref[0, 0:BLOCK] = jnp.zeros((BLOCK, DH), f32)
            dctx_ref[1, 0:BLOCK] = jnp.zeros((BLOCK, DH), f32)
            for i in range(half):
                rows = slice(BLOCK + i * QTILE, BLOCK + (i + 1) * QTILE)
                old = slice(i * QTILE, (i + 1) * QTILE)
                dctx_ref[0, rows] = dkey[half + i] * SCALE + dnext_ref[0, old, own]
                dctx_ref[1, rows] = dvalue[half + i] + dnext_ref[1, old, own]
            dsq = (dsquery * SCALE).astype(bf16)
            small_ref[head * DH : (head + 1) * DH, :] += t_dot(low, dsq)
            dmem_ref[:, own] = dmem_new + dot_t(dsq, query_ref[head])
            for tile in range(BLOCK // QTILE):
                rows = slice(tile * QTILE, (tile + 1) * QTILE)
                here = pl.ds(cur_at + tile * QTILE, QTILE)
                query = cur_ref[rows, own]
                dout = dout_ref[rows, own]
                lse = lse_ref[head : head + 1, pl.ds(base + tile * QTILE, QTILE)]
                delta = jnp.sum((dout.astype(f32) * att_ref[here, own].astype(f32)).T, axis=0, keepdims=True)
                dq = jnp.zeros((QTILE, DH), f32)
                for which, first, end, col in context_pieces(tile):
                    for at in range(first, end, QTILE):
                        keys = refs[which][at : at + QTILE, key_cols]
                        values = refs[which][at : at + QTILE, value_cols]
                        band = col + at - first
                        position = (block - 1 + which) * BLOCK + at + lax.broadcasted_iota(jnp.int32, (QTILE, 1), 0)
                        live = (position >= 0) & (position < length)
                        s = dot_t(keys, query) * scale2 + bias_ref[head, band : band + QTILE, :] - lse
                        p = jnp.exp2(jnp.where(live, s, -jnp.inf))
                        dp = dot_t(values, dout)
                        ds = (p * (dp - delta)).astype(bf16)
                        wide = ds.astype(f32)
                        edge = min(max(SPAN - NEAR - band, 0), QTILE)
                        if edge:
                            far_ref[head] += functools.reduce(jnp.add, [wide[i : i + 8] for i in range(0, edge, 8)])
                        if edge < QTILE:
                            at_near = band + edge - (SPAN - NEAR)
                            near_ref[head, at_near : at_near + QTILE - edge] += wide[edge:]
                        into = slice(which * BLOCK + at, which * BLOCK + at + QTILE)
                        dctx_ref[1, into] += dot(p.astype(bf16), dout)
                        dctx_ref[0, into] += dot(ds, query) * SCALE
                        dq += t_dot(ds, keys)
                for part in range(half):
                    keys = low[part * QTILE : (part + 1) * QTILE]
                    s = dot_t(keys, query) * scale2 - lse
                    p = jnp.exp2(s)
                    dp = dot_t(keys, dout)
                    ds = (p * (dp - delta)).astype(bf16)
                    dlow[part] += dot(p.astype(bf16), dout) + dot(ds, query) * SCALE
                    dq += t_dot(ds, keys)
                dqkv_ref[here, own] = (dq * SCALE).astype(bf16)
            for part in range(half):
                dmem_ref[part * QTILE : (part + 1) * QTILE, own] += dlow[part]
            dnext_ref[0, :, own] = dctx_ref[0, 0:BLOCK]
            dnext_ref[1, :, own] = dctx_ref[1, 0:BLOCK]
            dqkv_ref[pl.ds(cur_at, BLOCK), key_cols] = dctx_ref[0, BLOCK:].astype(bf16)
            dqkv_ref[pl.ds(cur_at, BLOCK), value_cols] = dctx_ref[1, BLOCK:].astype(bf16)

    dqkv_store = pltpu.make_async_copy(dqkv_ref, dqkv_out, out_sem)
    dqkv_store.start()
    for job in jobs[points:]:
        job()
    member = bucket_members()
    lane = lax.broadcasted_iota(jnp.int32, (1, DH), 1)
    for head in range(heads):
        sums = jnp.broadcast_to(diagonal_sums(near_ref[head]), (8, 2 * QTILE))
        table = jnp.dot(sums, member, precision=lax.Precision.HIGHEST, preferred_element_type=f32)[0:1]
        total = jnp.sum(jnp.sum(far_ref[head], axis=0, keepdims=True), axis=1, keepdims=True)
        row = dq_row + heads + head
        small_ref[row : row + 1, :] = table + jnp.where(lane == BUCKETS - 1, total, 0.0)
        row = dq_row + head
        forget = forget_ref[:, head * DH : (head + 1) * DH]
        small_ref[row : row + 1, :] = small_ref[row : row + 1, :] * forget * (1.0 - forget)
    loads[3].wait()
    mo_loads[0].wait()
    for bit in bits:
        mo_copy(bit, 0).wait_recv()
    step = 128
    for r in range(0, tok_rows, step):
        at = slice(r, r + step)
        value = mid_ref[at] + mo_low[0, at].astype(f32)
        for bit in bits:
            value = value + mo_in[slots[bit, 0], at].astype(f32)
        position = me * tok_rows + r + lax.broadcasted_iota(jnp.int32, (step, 1), 0)
        output_ref[at] = (value * jnp.where(position < length, 1.0, 0.0)).astype(bf16)
    combine(2)
    opart_ref[...] = to[z].astype(f32)
    for k in range(1, seq):
        exchange(k, False).wait_recv()
    xu[me] = tu[z, me]
    write_parts(upart_ref, xu, seq, share)
    for i in (0, 2) if inside else (0, 1, 2):
        drain_y(i)
    for i in range(2):
        drain_z(i)
    for bit in bits:
        for j in range(0, seq, 2 * bit):
            mo_copy(bit, j).wait_send()
    for k in range(1, seq):
        move_copy(k).wait_send()
        exchange(k, True).wait_send()
    dqkv_store.wait()


def bucket_members():
    shape = (2 * QTILE, DH)
    row = lax.broadcasted_iota(jnp.int32, shape, 0)
    lane = lax.broadcasted_iota(jnp.int32, shape, 1)
    distance = jnp.where(row < QTILE, row, row - 2 * QTILE) + NEAR - QTILE
    bucket = jnp.minimum(distance, 16)
    for edge in BUCKET_EDGES:
        bucket = bucket + jnp.where(distance >= edge, 1, 0)
    inside = (distance >= 0) & (distance < BLOCK) & (bucket == lane)
    return jnp.where(inside, 1.0, 0.0)


def write_parts(out_ref, pieces, seq, unit):
    if len(out_ref.shape) == 3:
        out_ref[...] = pieces[...].astype(f32)
        return
    count = pieces.shape[2] // unit
    for k in range(seq):
        for c in range(count):
            at = (c * seq + k) * unit
            out_ref[:, at : at + unit] = pieces[k, :, c * unit : (c + 1) * unit].astype(f32)


def attend_back(
    qkv, db, wout, att, mem, upd, lse, slse, sgrad, length, state_query, forget, bias, up, down, mo, mid, seq, fsdp
):
    rows, width3 = qkv.shape
    width = width3 // 3
    heads = width // DH
    dim = db.shape[1]
    lo = 2
    hi = fsdp // lo
    piece, hidden = up.shape[2:]
    share = hidden // fsdp
    tok_rows = mid.shape[0]
    inside = piece % 16 == 0
    blocks = (piece, dim), (seq, piece, hidden), (share, dim)
    small_rows = heads * (DH + 2)
    small_rows += -small_rows % 8
    vmem = pl.BlockSpec(memory_space=pltpu.VMEM)
    anywhere = pl.BlockSpec(memory_space=pl.ANY)
    dma = pltpu.SemaphoreType.DMA

    def buf(*shape):
        return pltpu.VMEM(shape, bf16)

    extra = []
    if not inside:
        extra.append(t_dot(att, db).astype(bf16).reshape(fsdp, piece, dim))
    upart = (piece, hidden * seq) if share % 128 == 0 else (seq, piece, hidden)
    return pl.pallas_call(
        functools.partial(attend_back_kernel, heads, seq, hi, lo, inside),
        out_shape=(
            jax.ShapeDtypeStruct((rows, width3), bf16),
            jax.ShapeDtypeStruct((small_rows, DH), f32),
            jax.ShapeDtypeStruct(upart, f32),
            jax.ShapeDtypeStruct((hi, share, dim), bf16),
            jax.ShapeDtypeStruct((piece, dim), f32),
            jax.ShapeDtypeStruct((tok_rows, dim), bf16),
        ),
        in_specs=[pl.BlockSpec(memory_space=pltpu.SMEM), anywhere, anywhere, anywhere]
        + [anywhere] * 3
        + [vmem] * 6
        + [anywhere] * 4
        + [vmem] * len(extra),
        out_specs=(anywhere,) + (vmem,) * 5,
        scratch_shapes=[
            buf(rows, width3),
            buf(rows, dim),
            buf(rows, width),
            pltpu.VMEM(mem.shape, f32),
            pltpu.VMEM(upd.shape, f32),
            pltpu.VMEM((tok_rows, dim), f32),
            buf(rows, width3),
            buf(width, dim),
            pltpu.VMEM((STATE_VECTORS, width), f32),
            pltpu.VMEM((2, BLOCK, width), f32),
            pltpu.VMEM((2, 2 * BLOCK, DH), f32),
            pltpu.VMEM((heads, SPAN, QTILE), f32),
            pltpu.VMEM((heads, NEAR, QTILE), f32),
            pltpu.VMEM((heads, 8, QTILE), f32),
            buf(BLOCK, width),
            buf(fsdp, piece, dim),
            buf(*down.shape),
            buf(hi, *blocks[0]),
            buf(hi, *blocks[1]),
            buf(hi, *blocks[0]),
            buf(16, 128) if inside else buf(hi, *blocks[1]),
            buf(hi, *blocks[2]),
            buf(2, max(hi - 1, 1), *blocks[0]),
            buf(2, max(hi - 1, 1), *blocks[1]),
            buf(*blocks[1]),
            buf(max(seq // 2, 1), tok_rows, dim),
            buf(max(seq - 1, 1), tok_rows, dim),
            dma((2, 2, hi)),
            dma((2, 2, hi)),
            dma((3, hi)),
            dma((3, hi)),
            dma((seq,)),
            dma((seq,)),
            dma((seq,)),
            dma((seq,)),
            dma((seq,)),
            dma((seq,)),
            dma((5,)),
            dma((3, seq)),
            dma((hi,)),
            dma((seq,)),
            dma,
        ],
        compiler_params=pltpu.CompilerParams(collective_id=4, has_side_effects=True, vmem_limit_bytes=62 << 20),
        cost_estimate=pl.CostEstimate(
            flops=seq * heads * 512 * 2400 * 128 * 10, bytes_accessed=20 << 20, transcendentals=10 << 20
        ),
        name="attend_back",
    )(
        length, qkv, db, wout, att, mem, upd, lse, slse, sgrad, state_query, forget, bias, up, down, mo, mid, *extra
    )


def gather_kernel(seq, hi, lo, *refs):
    refs = list(refs)

    def take(count):
        taken = refs[:count]
        del refs[:count]
        return taken

    tok_ref, grad_ref, wq_ref, ga_ref, gm_ref, wo_ref, wu_ref = take(7)
    toks_ref, grads_ref, wqs_ref, gas_ref, gms_ref, wos_ref, wus_ref, normed_ref, qkv_ref = take(9)
    toks_full, grad_buf, wq_full, ga_full, gm_full, wo_buf, wu_buf, normed_buf, qkv_buf = take(9)
    own_sem, store_sem, seq_send, seq_recv, chunk_sem, z_send, z_recv, y_send, y_recv = take(9)

    me = lax.axis_index("seq")
    f = lax.axis_index("fsdp")
    fsdp = hi * lo
    bits = [1 << i for i in range(seq.bit_length() - 1)]
    high = [bit for bit in reversed(bits) if bit > 1]
    rows, dim = tok_ref.shape
    width = wq_full.shape[2] // 3
    share = wus_ref.shape[2] // fsdp
    every = wq_ref.shape[1] // 3
    loads = [[] for _ in range(7)]

    def load(i, src, dst):
        loads[i].append(pltpu.make_async_copy(src, dst, own_sem.at[i, len(loads[i])]))
        loads[i][-1].start()

    for c in range(3):
        cols = pl.ds(pl.multiple_of(c * every + me * width, width), width)
        load(0, wq_ref.at[:, cols], wq_full.at[f, :, pl.ds(c * width, width)])
    load(1, ga_ref, ga_full.at[f])
    load(2, gm_ref, gm_full.at[f])
    load(3, wo_ref.at[me % 2], wo_buf)
    if wu_ref.shape[1] == wus_ref.shape[2]:
        load(4, wu_ref, wu_buf)
    else:
        for c in range(fsdp):
            cols = pl.ds(pl.multiple_of((c * seq + me) * share, share), share)
            load(4, wu_ref.at[:, cols], wu_buf.at[:, pl.ds(c * share, share)])
    load(5, tok_ref, toks_full.at[0])
    load(6, grad_ref, grad_buf)
    greet(bits, hi, lo)

    pairs = ((tok_ref, toks_full), (grad_ref, grads_ref))

    def seq_copy(i, source, slot, bit):
        src, out = pairs[i]
        return pltpu.make_async_remote_copy(
            src_ref=out.at[source] if source else src,
            dst_ref=out.at[slot],
            send_sem=seq_send.at[i, slot],
            recv_sem=seq_recv.at[i, slot],
            device_id={"seq": me ^ bit},
            device_id_type=MESH,
        )

    sends = []

    def send(i, source, slot, bit):
        sends.append(seq_copy(i, source, slot, bit))
        sends[-1].start()

    fulls = (wq_full, ga_full, gm_full, wos_ref, wus_ref)
    bufs = (None, None, None, wo_buf, wu_buf)
    start, step, arrive, drain = line_gather(
        hi,
        lo,
        lambda i, origin: fulls[i].at[origin],
        lambda i: fulls[i].at[f] if i < 3 else bufs[i],
        z_send,
        z_recv,
        y_send,
        y_recv,
    )
    first, later = (0, 1, 2), (3, 4)
    if high:
        send(0, 0, high[0], high[0])
    if seq > 1:
        send(0, 0, 1, 1)
    for i in first:
        for c in loads[i]:
            c.wait()
        start(i)
    if high:
        send(1, 0, high[0], high[0])
    if seq > 1:
        send(1, 0, 1, 1)
    stores = []

    def store(src, dst, sem):
        stores.append(pltpu.make_async_copy(src, dst, sem))
        stores[-1].start()

    for t in range(hi - 1):
        for i in first:
            step(i, t)
        if t == min(1, hi - 2):
            for i in later:
                for c in loads[i]:
                    c.wait()
                start(i)
            store(wo_buf, wos_ref.at[f], store_sem.at[0])
            store(wu_buf, wus_ref.at[f], store_sem.at[1])
    for c in loads[5] + loads[6]:
        c.wait()
    store(toks_full.at[0], toks_ref.at[0], chunk_sem.at[0, 0])
    store(grad_buf, grads_ref.at[0], store_sem.at[2])
    for i in first:
        arrive(i)
    store(wq_full, wqs_ref, store_sem.at[3])
    gas_ref[...] = jnp.concatenate([ga_full[n] for n in range(fsdp)], axis=1).astype(f32)
    gms_ref[...] = jnp.concatenate([gm_full[n] for n in range(fsdp)], axis=1).astype(f32)
    gain = gas_ref[...]

    def project(j):
        if j:
            store(toks_full.at[j], toks_ref.at[j], chunk_sem.at[0, j])

        @pl.loop(0, rows // 256)
        def _(n):
            at = pl.ds(pl.multiple_of(n * 256, 256), 256)
            into = pl.ds(pl.multiple_of(j * rows + n * 256, 256), 256)
            x = toks_full[j, at].astype(f32)
            rho = lax.rsqrt(jnp.mean(x * x, axis=-1, keepdims=True) + EPSILON)
            normed = (x * rho * gain).astype(bf16)
            normed_buf[into] = normed
            qkv_buf[into] = dot(normed, wq_full[...].reshape(dim, 3 * width)).astype(bf16)

        at = pl.ds(j * rows, rows)
        store(normed_buf.at[at], normed_ref.at[at], chunk_sem.at[1, j])
        store(qkv_buf.at[at], qkv_ref.at[at], chunk_sem.at[2, j])

    hop = [0]

    def advance():
        if hop[0] < hi - 1:
            for i in later:
                step(i, hop[0])
            hop[0] += 1

    project(0)
    advance()
    have = [0]
    for n, bit in enumerate(high):
        if n:
            for j in have:
                send(0, j, j ^ bit, bit)
        for j in have:
            seq_copy(0, 0, j ^ bit, bit).wait_recv()
            send(0, j ^ bit, j ^ bit ^ 1, 1)
        have += [j ^ bit for j in have]
    for j in have:
        if j:
            project(j)
            advance()
        if seq > 1:
            seq_copy(0, 0, j ^ 1, 1).wait_recv()
            project(j ^ 1)
            advance()
    while hop[0] < hi - 1:
        advance()
    have = [0]
    for n, bit in enumerate(high):
        if n:
            for j in have:
                send(1, j, j ^ bit, bit)
        for j in have:
            seq_copy(1, 0, j ^ bit, bit).wait_recv()
            send(1, j ^ bit, j ^ bit ^ 1, 1)
        have += [j ^ bit for j in have]
    if seq > 1:
        for j in have:
            seq_copy(1, 0, j ^ 1, 1).wait_recv()
    for i in later:
        arrive(i)
    for i in first + later:
        drain(i)
    for c in sends:
        c.wait_send()
    for c in stores:
        c.wait()


def gather_start(tokens, grads, w_qkv, gain_a, gain_m, w_out, w_up, seq, fsdp):
    lo = 2
    hi = fsdp // lo
    dim_rows, hidden = w_up.shape
    share = hidden // (seq * fsdp)
    if share % 128:
        w_up = lax.dynamic_slice_in_dim(w_up.reshape(dim_rows, fsdp, seq, share), lax.axis_index("seq"), 1, axis=2)
        w_up = w_up.reshape(dim_rows, fsdp * share)
    rows, dim = tokens.shape
    width3 = w_qkv.shape[1] // seq
    anywhere = pl.BlockSpec(memory_space=pl.ANY)
    vmem = pl.BlockSpec(memory_space=pltpu.VMEM)
    dma = pltpu.SemaphoreType.DMA

    def like(*shape):
        return jax.ShapeDtypeStruct(shape, bf16)

    def buf(*shape):
        return pltpu.VMEM(shape, bf16)

    return pl.pallas_call(
        functools.partial(gather_kernel, seq, hi, lo),
        out_shape=(
            like(seq, rows, dim),
            like(seq, rows, dim),
            like(fsdp, dim_rows, width3),
            jax.ShapeDtypeStruct((1, dim), f32),
            jax.ShapeDtypeStruct((1, dim), f32),
            like(fsdp, *w_out.shape[1:]),
            like(fsdp, dim_rows, hidden // seq),
            like(seq * rows, dim),
            like(seq * rows, width3),
        ),
        in_specs=[anywhere] * 7,
        out_specs=(anywhere,) * 3 + (vmem,) * 2 + (anywhere,) * 4,
        scratch_shapes=[
            buf(seq, rows, dim),
            buf(rows, dim),
            buf(fsdp, dim_rows, width3),
            buf(fsdp, *gain_a.shape),
            buf(fsdp, *gain_m.shape),
            buf(*w_out.shape[1:]),
            buf(dim_rows, hidden // seq),
            buf(seq * rows, dim),
            buf(seq * rows, width3),
            dma((7, max(fsdp, 3))),
            dma((4,)),
            dma((2, seq)),
            dma((2, seq)),
            dma((3, seq)),
        ]
        + line_sems(5, hi),
        compiler_params=pltpu.CompilerParams(collective_id=0, has_side_effects=True, vmem_limit_bytes=62 << 20),
        name="gather_start",
    )(tokens, grads, w_qkv, gain_a, gain_m, w_out, w_up)


def finish_kernel(seq, hi, lo, inside, *refs):
    refs = list(refs)

    def take(count):
        taken = refs[:count]
        del refs[:count]
        return taken

    dqkv_hbm, wqkv_hbm, normed_hbm, down_ref, small_ref, mlp_gain_ref, tok_hbm, dmid_hbm, gain_ref = take(9)
    gq_in = None if inside else take(1)[0]
    tg_ref, rq_ref, rd_ref, dquery_ref, gate_ref, table_ref, again_ref, mgain_ref = take(8)
    dqkv_ref, wqkv_ref, normed_ref, tok_ref, dmid_ref = take(5)
    low, into, acc, gq_buf, tq, td, yq, zq, zd, xq, sy, sz, gains, gy, gz, gs = take(16)
    dn_send, dn_recv, z_send, z_recv, y_send, y_recv, x_send, x_recv, s_send, s_recv, g_send, g_recv = take(12)
    load_sem, dqkv_sem, tg_sem = take(3)
    gq_ref = gq_buf if inside else gq_in

    me = lax.axis_index("seq")
    f = lax.axis_index("fsdp")
    z, y = f // lo, f % lo
    peer = z * lo + 1 - y
    rows, dim = tok_ref.shape
    width = xq.shape[2] // 3
    part_seq = seq // 2
    bits, slots = seq_levels(seq)

    loads = [
        pltpu.make_async_copy(src, dst, load_sem.at[i])
        for i, (src, dst) in enumerate(
            (
                (normed_hbm, normed_ref),
                (wqkv_hbm, wqkv_ref),
                (down_ref, td),
                (tok_hbm, tok_ref),
                (dmid_hbm, dmid_ref),
            )
        )
    ]
    dqkv_loads = {
        j: pltpu.make_async_copy(
            dqkv_hbm.at[pl.ds(j * rows, rows)], dqkv_ref.at[pl.ds(j * rows, rows)], dqkv_sem.at[j]
        )
        for j in range(seq)
    }
    loads[0].start()
    for j in reversed(range(seq)):
        dqkv_loads[j].start()
    for c in loads[1:]:
        c.start()

    barrier = pltpu.get_barrier_semaphore()
    for k in range(1, seq):
        pl.semaphore_signal(barrier, inc=1, device_id={"seq": me ^ k}, device_id_type=MESH)
    for k in range(1, hi):
        pl.semaphore_signal(barrier, inc=1, device_id={"fsdp": lax.rem(z + k, hi) * lo + y}, device_id_type=MESH)
    pl.semaphore_signal(barrier, inc=1, device_id={"fsdp": peer}, device_id_type=MESH)
    pl.semaphore_wait(barrier, seq + hi - 1)

    def remote(src, dst, send, recv, axis, target):
        return pltpu.make_async_remote_copy(
            src_ref=src, dst_ref=dst, send_sem=send, recv_sem=recv, device_id={axis: target}, device_id_type=MESH
        )

    def dn_copy(bit, j):
        slot = slots[bit, j]
        return remote(low.at[j ^ bit], into.at[slot], dn_send.at[slot], dn_recv.at[slot], "seq", me ^ bit)

    start, combine, zsend, zrecv, drain_y, drain_z = line_reduce(
        hi,
        lo,
        lambda i, target: gq_ref.at[pl.ds((i // 2) * part_seq, part_seq), target],
        (tq.at[:, pl.ds(0, part_seq)], td, tq.at[:, pl.ds(part_seq, part_seq)]),
        (yq.at[:, pl.ds(0, part_seq)], None, yq.at[:, pl.ds(part_seq, part_seq)]),
        (zq.at[:, :, pl.ds(0, part_seq)], zd, zq.at[:, :, pl.ds(part_seq, part_seq)]),
        z_send,
        z_recv,
        y_send,
        y_recv,
    )

    def exchange(k, sending):
        return remote(
            tq.at[z, me ^ k] if sending else tq.at[z, me],
            xq.at[me] if sending else xq.at[me ^ k],
            x_send.at[k],
            x_recv.at[k],
            "seq",
            me ^ k if sending else me,
        )

    small_y = remote(small_ref, sy, s_send.at[0], s_recv.at[0], "fsdp", peer)
    small_y.start()
    def dn_part(j):
        part = dot_t(dqkv_ref[j * rows : (j + 1) * rows], wqkv_ref[...])
        if j % 2:
            low[j] = part.astype(bf16)
            dn_copy(1, j ^ 1).start()
        else:
            acc[...] = part

    def dn_sum(j):
        for bit in bits:
            if j & bit:
                low[j] = acc[...].astype(bf16)
                dn_copy(bit, j ^ bit).start()
                break
            dn_copy(bit, j).wait_recv()
            acc[...] += into[slots[bit, j]].astype(f32)

    def make_part(k):
        cols = slice(k * (dim // seq), (k + 1) * (dim // seq))
        part = t_dot(normed_ref[:, cols], dqkv_ref[...]).astype(bf16)
        gq_buf[k] = part.reshape(gq_buf.shape[1:])

    for j in reversed(range(seq)):
        dqkv_loads[j].wait()
    loads[1].wait()
    for j in reversed(range(2, seq)):
        dn_part(j)
        if j % 2 == 0:
            dn_sum(j)
    loads[2].wait()
    zsend(1, 0)
    loads[0].wait()
    for k in range(seq) if inside else ():
        make_part(k)
        if k == part_seq - 1:
            start(0)
    if not inside:
        start(0)
    start(2)

    def zstep(i, t):
        if t < hi - 1:
            zrecv(i, t)
            if t + 1 < hi - 1:
                zsend(i, t + 1)

    zstep(1, 0)
    small_y.wait_recv()
    sz[z] = small_ref[...] + sy[...]
    small_z = []
    for k in range(1, hi):
        small_z.append(
            remote(sz.at[z], sz.at[z], s_send.at[k], s_recv.at[k], "fsdp", lax.rem(z + k, hi) * lo + y)
        )
        small_z[-1].start()
    for j in reversed(range(min(2, seq))):
        dn_part(j)
    zstep(1, 1)
    for c in loads[3:]:
        c.wait()
    combine(0)
    zsend(0, 0)
    for t in range(2, hi - 1):
        zstep(1, t)
    zstep(0, 0)
    zstep(0, 1)
    combine(2)
    zsend(2, 0)
    for t in range(2, hi - 1):
        zstep(0, t)
    for bit in bits:
        dn_copy(bit, 0).wait_recv()
    gain = gain_ref[...]
    part = jnp.zeros((8, dim), f32)
    step = 128
    for r in range(0, rows, step):
        at = slice(r, r + step)
        dn = acc[at]
        for bit in bits:
            dn = dn + into[slots[bit, 0], at].astype(f32)
        x = tok_ref[at].astype(f32)
        rho = lax.rsqrt(jnp.mean(x * x, axis=-1, keepdims=True) + EPSILON)
        scaled = gain * dn
        mean = jnp.mean(x * scaled, axis=-1, keepdims=True)
        dmid_ref[at] += rho * scaled - x * (rho * rho * rho * mean)
        prod = dn * x * rho
        part += functools.reduce(jnp.add, [prod[n : n + 8] for n in range(0, step, 8)])
    tg_store = pltpu.make_async_copy(dmid_ref, tg_ref, tg_sem)
    tg_store.start()
    gains[0:8] = mlp_gain_ref[...]
    gains[8:16] = part
    gain_y = remote(gains, gy, g_send.at[0], g_recv.at[0], "fsdp", peer)
    gain_y.start()
    zstep(2, 0)
    gain_y.wait_recv()
    gz[z] = gains[...] + gy[...]
    gain_z = []
    for k in range(1, hi):
        gain_z.append(
            remote(gz.at[z], gz.at[z], g_send.at[k], g_recv.at[k], "fsdp", lax.rem(z + k, hi) * lo + y)
        )
        gain_z[-1].start()
    for t in range(1, hi - 1):
        zstep(2, t)
    for k in range(1, seq):
        exchange(k, True).start()
    for k in range(1, hi):
        source = lax.rem(z + hi - k, hi)
        remote(gz.at[source], gz.at[source], g_send.at[k], g_recv.at[k], "fsdp", f).wait_recv()
        remote(sz.at[source], sz.at[source], s_send.at[k], s_recv.at[k], "fsdp", f).wait_recv()
    gs[me] = functools.reduce(jnp.add, [gz[d] for d in range(hi)])
    gain_x = []
    for k in range(1, seq):
        gain_x.append(remote(gs.at[me], gs.at[me], g_send.at[hi + k], g_recv.at[hi + k], "seq", me ^ k))
        gain_x[-1].start()
    rd_ref[...] = td[z].astype(f32)
    total = functools.reduce(jnp.add, [sz[d] for d in range(hi)])
    cut, heads = dquery_ref.shape[0], gate_ref.shape[0]
    dquery_ref[...] = total[:cut]
    gate_ref[...] = total[cut : cut + heads]
    table_ref[...] = total[cut + heads : cut + 2 * heads, :BUCKETS]
    xq[me] = tq[z, me]
    for k in range(1, seq):
        exchange(k, False).wait_recv()
    write_parts(rq_ref, xq, seq, width)
    for k in range(1, seq):
        remote(gs.at[me ^ k], gs.at[me ^ k], g_send.at[hi + k], g_recv.at[hi + k], "seq", me).wait_recv()
    total = functools.reduce(jnp.add, [gs[k] for k in range(seq)])
    piece = again_ref.shape[1]
    total = pltpu.roll(total, lax.rem(dim - (me * hi * lo + f) * piece, dim), 1)[:, :DH]
    mgain_ref[...] = jnp.sum(total[0:8], axis=0, keepdims=True)[:, :piece]
    again_ref[...] = jnp.sum(total[8:16], axis=0, keepdims=True)[:, :piece]

    for bit in bits:
        for j in range(0, seq, 2 * bit):
            dn_copy(bit, j).wait_send()
    for i in (0, 2):
        drain_y(i)
    for i in range(3):
        drain_z(i)
    for k in range(1, seq):
        exchange(k, True).wait_send()
    for c in [small_y, gain_y] + small_z + gain_z + gain_x:
        c.wait_send()
    tg_store.wait()


def finish(dqkv, wqkv, normed, down, small, mlp_gain, tok, dmid, gain, seq, fsdp):
    lo = 2
    hi = fsdp // lo
    rows, dim = tok.shape
    width3 = dqkv.shape[1]
    piece = dim // (seq * fsdp)
    inside = piece % 16 == 0
    heads = width3 // (3 * DH)
    vmem = pl.BlockSpec(memory_space=pltpu.VMEM)
    anywhere = pl.BlockSpec(memory_space=pl.ANY)
    dma = pltpu.SemaphoreType.DMA

    def buf(*shape):
        return pltpu.VMEM(shape, bf16)

    extra = []
    if not inside:
        extra.append(t_dot(normed, dqkv).astype(bf16).reshape(seq, fsdp, piece, width3))
    scratch = [
        buf(*dqkv.shape),
        buf(*wqkv.shape),
        buf(*normed.shape),
        buf(rows, dim),
        pltpu.VMEM((rows, dim), f32),
        buf(seq, rows, dim),
        buf(max(seq - 1, 1), rows, dim),
        pltpu.VMEM((rows, dim), f32),
        buf(seq, fsdp, piece, width3) if inside else buf(16, 128),
        buf(hi, seq, piece, width3),
        buf(*down.shape),
        buf(hi, seq, piece, width3),
        buf(2, max(hi - 1, 1), seq, piece, width3),
        buf(2, max(hi - 1, 1), *down.shape[1:]),
        buf(seq, piece, width3),
        pltpu.VMEM(small.shape, f32),
        pltpu.VMEM((hi,) + small.shape, f32),
        pltpu.VMEM((16, dim), f32),
        pltpu.VMEM((16, dim), f32),
        pltpu.VMEM((hi, 16, dim), f32),
        pltpu.VMEM((seq, 16, dim), f32),
        dma((seq,)),
        dma((seq,)),
        dma((3, 2, hi)),
        dma((3, 2, hi)),
        dma((3, hi)),
        dma((3, hi)),
        dma((seq,)),
        dma((seq,)),
        dma((hi,)),
        dma((hi,)),
        dma((hi + seq,)),
        dma((hi + seq,)),
        dma((5,)),
        dma((seq,)),
        dma,
    ]
    return pl.pallas_call(
        functools.partial(finish_kernel, seq, hi, lo, inside),
        out_shape=(
            jax.ShapeDtypeStruct((rows, dim), f32),
            jax.ShapeDtypeStruct((piece, seq * width3), f32),
            jax.ShapeDtypeStruct(down.shape[1:], f32),
            jax.ShapeDtypeStruct((heads * DH, DH), f32),
            jax.ShapeDtypeStruct((heads, DH), f32),
            jax.ShapeDtypeStruct((heads, BUCKETS), f32),
            jax.ShapeDtypeStruct((1, piece), f32),
            jax.ShapeDtypeStruct((1, piece), f32),
        ),
        in_specs=[anywhere] * 4 + [vmem] * 2 + [anywhere] * 2 + [vmem] * (1 + len(extra)),
        out_specs=(anywhere,) + (vmem,) * 7,
        scratch_shapes=scratch,
        compiler_params=pltpu.CompilerParams(
            collective_id=1, has_side_effects=True, vmem_limit_bytes=60 << 20
        ),
        name="finish",
    )(dqkv, wqkv, normed, down, small, mlp_gain, tok, dmid, gain, *extra)


GELU_P = 0.24
GELU_C = (
    0.08951261885080208,
    0.15562094398234086,
    -0.15437154502074169,
    0.6261054138112487,
    -0.6465313024138201,
    0.5547927291245551,
    -0.125128858665134,
)


def gelu_parts(x):
    size = jnp.abs(x)
    t = 1.0 / (1.0 + GELU_P * size)
    poly = GELU_C[-1] * t
    for c in GELU_C[-2::-1]:
        poly = (poly + c) * t
    bell = jnp.exp2(x * x * (-0.5 * LOG2E))
    tail = poly * bell
    cdf = jnp.where(x < 0.0, tail, 1.0 - tail)
    return x * cdf, cdf + x * bell * (1.0 / math.sqrt(2.0 * math.pi))


def mlp_kernel(seq, hi, lo, sub, length_ref, *refs):
    refs = list(refs)

    def take(count):
        taken = refs[:count]
        del refs[:count]
        return taken

    own_ref, others_ref, tok_ref, grads_ref, wo_hbm, wu_hbm, wd_hbm, gain_ref = take(8)
    mid_out, dmid_out, gsum_ref, db_ref, mo_ref, ug_out, dg_out = take(7)
    staged = len(ug_out.shape) == 4
    att_refs = [own_ref] + [others_ref.at[k] for k in range(1, seq)]
    att_buf, tok_buf, wo_ref, wu_ref, wd_ref, gm, nm, hid, dpre, low, into, acc, mid_ref, ug_ref, dg_ref = take(15)
    load_sem, w_sem, gm_sem, dn_send, dn_recv, db_send, db_recv, mo_sem, own_sem = take(9)
    if staged:
        tu, yu, y_send, y_recv = take(4)
    dbv = low.at[0]
    depth = att_buf.shape[0]

    me = lax.axis_index("seq")
    length = length_ref[0]
    dim = wo_ref.shape[0]
    width = dim // seq
    rows = tok_ref.shape[1]
    share = wu_ref.shape[1]
    subs = rows // sub
    bits, slots = seq_levels(seq)
    order = list(reversed(range(seq)))

    def chunk_loads(j):
        slot = j % depth
        copies = [
            pltpu.make_async_copy(att_refs[k].at[pl.ds(j * rows, rows)], att_buf.at[slot, k], load_sem.at[slot, k])
            for k in range(seq)
        ]
        copies.append(pltpu.make_async_copy(tok_ref.at[j], tok_buf.at[slot], load_sem.at[slot, seq]))
        return copies

    gm_loads = {
        j: pltpu.make_async_copy(grads_ref.at[j], gm.at[pl.ds(j * rows, rows)], gm_sem.at[j]) for j in order
    }
    weights = [
        pltpu.make_async_copy(src, dst, w_sem.at[i])
        for i, (src, dst) in enumerate(((wo_hbm, wo_ref), (wu_hbm, wu_ref), (wd_hbm, wd_ref)))
    ]
    for c in chunk_loads(order[0]) + weights[:1] + (chunk_loads(order[1]) if seq > 1 else []) + weights[1:]:
        c.start()
    for j in order:
        gm_loads[j].start()
    if depth == seq:
        for j in order[2:]:
            for c in chunk_loads(j):
                c.start()

    greet(bits, hi, lo)

    def dn_copy(bit, j, s):
        slot = slots[bit, j]
        at = pl.ds(pl.multiple_of(s * sub, sub), sub)
        return pltpu.make_async_remote_copy(
            src_ref=low.at[j ^ bit, at],
            dst_ref=into.at[slot, at],
            send_sem=dn_send.at[slot, s],
            recv_sem=dn_recv.at[slot, s],
            device_id={"seq": me ^ bit},
            device_id_type=MESH,
        )

    gain = gain_ref[...]

    def forward(j, s):
        slot = j % depth
        at = pl.ds(pl.multiple_of(s * sub, sub), sub)
        here = pl.ds(pl.multiple_of(j * rows + s * sub, sub), sub)
        position = (j ^ me) * rows + s * sub + lax.broadcasted_iota(jnp.int32, (sub, 1), 0)
        live = jnp.where(position < length, 1.0, 0.0)
        masked = (gm[here].astype(f32) * live).astype(bf16)
        gm[here] = masked
        mid = tok_buf[slot, at].astype(f32)
        for k in range(seq):
            own = pl.ds(pl.multiple_of((me ^ k) * width, width), width)
            mid = mid + dot(att_buf[slot, k, at], wo_ref[own])
        rho = lax.rsqrt(jnp.mean(mid * mid, axis=-1, keepdims=True) + EPSILON)
        normed = (mid * rho * gain).astype(bf16)
        nm[here] = normed
        if j == 0:
            mid_ref[at] = mid
        for c in range(0, share, 256):
            cols = slice(c, c + 256)
            value, slope = gelu_parts(dot(normed, wu_ref[:, cols]))
            hid[here, cols] = value.astype(bf16)
            dpre[here, cols] = (dot_t(masked, wd_ref[cols]) * slope).astype(bf16)
        part = dot_t(dpre[here], wu_ref[...])
        if j % 2:
            low[j, at] = part.astype(bf16)
            dn_copy(1, j ^ 1, s).start()
        else:
            acc[at] = part

    def settle(j, s):
        at = pl.ds(pl.multiple_of(s * sub, sub), sub)
        for bit in bits:
            if j & bit:
                low[j, at] = acc[at].astype(bf16)
                dn_copy(bit, j ^ bit, s).start()
                break
            dn_copy(bit, j, s).wait_recv()
            acc[at] += into[slots[bit, j], at].astype(f32)

    for c in weights:
        c.wait()
    for n in range(0, seq, 2):
        pair = order[n : n + 2]
        if n and depth < seq:
            for j in pair:
                for c in chunk_loads(j):
                    c.start()
        for j in pair:
            for c in chunk_loads(j):
                c.wait()
            gm_loads[j].wait()

        @pl.loop(0, subs)
        def _(s):
            for j in pair:
                forward(j, s)
            if pair[-1]:
                settle(pair[-1], s)

    stores = [pltpu.make_async_copy(mid_ref, mid_out, own_sem.at[1])]
    stores[0].start()
    if staged:
        for k in range(seq):
            cols = slice(k * (dim // seq), (k + 1) * (dim // seq))
            ug_ref[k] = t_dot(nm[:, cols], dpre[...]).astype(bf16).reshape(ug_ref.shape[1:])
        start, combine, _, _, drain_y, _ = line_reduce(
            hi, lo, lambda i, target: ug_ref.at[:, target], (tu,), (yu,), (), None, None, y_send, y_recv
        )
        start(0)
    else:
        for c in range(0, dim, 256):
            ug_ref[c : c + 256] = t_dot(nm[:, c : c + 256], dpre[...]).astype(bf16)
        stores.append(pltpu.make_async_copy(ug_ref, ug_out, own_sem.at[2]))
        stores[-1].start()

    def db_copy(source, target, bit, s):
        at = pl.ds(s * sub, sub)
        return pltpu.make_async_remote_copy(
            src_ref=db_ref.at[source, at] if source else dbv.at[at],
            dst_ref=db_ref.at[target, at],
            send_sem=db_send.at[target, s],
            recv_sem=db_recv.at[target, s],
            device_id={"seq": me ^ bit},
            device_id_type=MESH,
        )

    sends = []
    high = [bit for bit in reversed(bits) if bit > 1]

    def send(source, target, bit, s):
        sends.append(db_copy(source, target, bit, s))
        sends[-1].start()

    step = 128
    part = jnp.zeros((8, dim), f32)
    for s in range(subs):
        for bit in bits:
            dn_copy(bit, 0, s).wait_recv()
        for r in range(s * sub, (s + 1) * sub, step):
            at = slice(r, r + step)
            dn = acc[at]
            for bit in bits:
                dn = dn + into[slots[bit, 0], at].astype(f32)
            mid = mid_ref[at]
            rho = lax.rsqrt(jnp.mean(mid * mid, axis=-1, keepdims=True) + EPSILON)
            scaled = gain * dn
            mean = jnp.mean(mid * scaled, axis=-1, keepdims=True)
            dmid = gm[at].astype(f32) + rho * scaled - mid * (rho * rho * rho * mean)
            acc[at] = dmid
            dbv[at] = dmid.astype(bf16)
            prod = dn * mid * rho
            part += functools.reduce(jnp.add, [prod[i : i + 8] for i in range(0, step, 8)])
        if high:
            send(0, high[0], high[0], s)
        if seq > 1:
            send(0, 1, 1, s)
    gsum_ref[...] = part
    stores.append(pltpu.make_async_copy(dbv, db_ref.at[0], own_sem.at[0]))
    stores[-1].start()
    stores.append(pltpu.make_async_copy(acc, dmid_out, own_sem.at[3]))
    stores[-1].start()
    for c in range(0, share, 256):
        dg_ref[c : c + 256] = t_dot(hid[:, c : c + 256], gm[...]).astype(bf16)
    stores.append(pltpu.make_async_copy(dg_ref, dg_out, own_sem.at[4]))
    stores[-1].start()
    for j in range(seq):
        at = slice(j * rows, (j + 1) * rows)
        nm[at] = dot(hid[at], wd_ref[...]).astype(bf16)
        stores.append(pltpu.make_async_copy(nm.at[pl.ds(j * rows, rows)], mo_ref.at[j], mo_sem.at[j]))
        stores[-1].start()
    have = [0]
    for n, bit in enumerate(high):
        if n:
            for j in have:
                for s in range(subs):
                    send(j, j ^ bit, bit, s)
        for j in have:
            for s in range(subs):
                db_copy(0, j ^ bit, bit, s).wait_recv()
                send(j ^ bit, j ^ bit ^ 1, 1, s)
        have += [j ^ bit for j in have]
    if seq > 1:
        for j in have:
            for s in range(subs):
                db_copy(0, j ^ 1, 1, s).wait_recv()
    if staged:
        combine(0)
        stores.append(pltpu.make_async_copy(tu, ug_out, own_sem.at[2]))
        stores[-1].start()
        drain_y(0)
    for c in sends:
        c.wait_send()
    for c in stores:
        c.wait()
    for bit in bits:
        for j in range(0, seq, 2 * bit):
            for s in range(subs):
                dn_copy(bit, j, s).wait_send()


def mlp(length, own, others, tok, grads, wo, wu, wd, gain, fsdp):
    seq, rows, dim = tok.shape
    share = wu.shape[1]
    lo = 2
    hi = fsdp // lo
    piece = dim // (seq * fsdp)
    staged = piece % 16 == 0
    up_shape = (hi, seq, piece, share) if staged else (dim, share)
    sub = 256
    depth = seq if seq <= 4 else 2
    anywhere = pl.BlockSpec(memory_space=pl.ANY)
    vmem = pl.BlockSpec(memory_space=pltpu.VMEM)
    dma = pltpu.SemaphoreType.DMA

    def buf(*shape):
        return pltpu.VMEM(shape, bf16)

    return pl.pallas_call(
        functools.partial(mlp_kernel, seq, hi, lo, sub),
        out_shape=(
            jax.ShapeDtypeStruct((rows, dim), f32),
            jax.ShapeDtypeStruct((rows, dim), f32),
            jax.ShapeDtypeStruct((8, dim), f32),
            jax.ShapeDtypeStruct((seq, rows, dim), bf16),
            jax.ShapeDtypeStruct((seq, rows, dim), bf16),
            jax.ShapeDtypeStruct(up_shape, bf16),
            jax.ShapeDtypeStruct((share, dim), bf16),
        ),
        in_specs=[pl.BlockSpec(memory_space=pltpu.SMEM)] + [anywhere] * 7 + [vmem],
        out_specs=(anywhere, anywhere, vmem, anywhere, anywhere, anywhere, anywhere),
        scratch_shapes=[
            buf(depth, seq, rows, dim // seq),
            buf(depth, rows, dim),
            buf(dim, dim),
            buf(dim, share),
            buf(share, dim),
            buf(seq * rows, dim),
            buf(seq * rows, dim),
            buf(seq * rows, share),
            buf(seq * rows, share),
            buf(seq, rows, dim),
            buf(max(seq - 1, 1), rows, dim),
            pltpu.VMEM((rows, dim), f32),
            pltpu.VMEM((rows, dim), f32),
            buf(seq, fsdp, piece, share) if staged else buf(dim, share),
            buf(share, dim),
            dma((depth, seq + 1)),
            dma((3,)),
            dma((seq,)),
            dma((seq, rows // sub)),
            dma((seq, rows // sub)),
            dma((seq, rows // sub)),
            dma((seq, rows // sub)),
            dma((seq,)),
            dma((5,)),
        ]
        + ([buf(*up_shape), buf(*up_shape), dma((1, hi)), dma((1, hi))] if staged else []),
        compiler_params=pltpu.CompilerParams(collective_id=2, has_side_effects=True, vmem_limit_bytes=62 << 20),
        cost_estimate=pl.CostEstimate(
            flops=2 * rows * seq * dim * (dim + 6 * share), bytes_accessed=32 << 20, transcendentals=rows * seq * share
        ),
        name="mlp",
    )(length, own, others, tok, grads, wo, wu, wd, gain)


def emit_kernel(*refs):
    count = len(refs) // 3
    ins, outs, bufs = refs[:count], refs[count : 2 * count], refs[2 * count : 3 * count]
    sems = refs[3 * count]
    reads = [pltpu.make_async_copy(a, b, sems.at[0, i]) for i, (a, b) in enumerate(zip(ins, bufs))]
    writes = [pltpu.make_async_copy(a, b, sems.at[1, i]) for i, (a, b) in enumerate(zip(bufs, outs))]
    for c in reads:
        c.start()
    for read, write in zip(reads, writes):
        read.wait()
        write.start()
    for c in writes:
        c.wait()


def emit(*values):
    count = len(values)
    anywhere = pl.BlockSpec(memory_space=pl.ANY)
    return pl.pallas_call(
        emit_kernel,
        out_shape=tuple(jax.ShapeDtypeStruct(v.shape, v.dtype) for v in values),
        in_specs=[anywhere] * count,
        out_specs=(anywhere,) * count,
        scratch_shapes=[pltpu.VMEM(v.shape, v.dtype) for v in values] + [pltpu.SemaphoreType.DMA((2, count))],
        compiler_params=pltpu.CompilerParams(vmem_limit_bytes=62 << 20),
        name="emit",
    )(*values)


def body(
    tokens,
    lengths,
    state_init,
    w_qkv,
    w_out,
    w_up,
    w_down,
    norm_attn,
    norm_mlp,
    rel_bias,
    state_query,
    gate_bias,
    out_grad,
    state_grad,
):
    seq_count = lax.axis_size("seq")
    fsdp_count = lax.axis_size("fsdp")
    seq_at = lax.axis_index("seq")
    heads = H // seq_count
    width = heads * DH
    tok_rows, dim = tokens.shape[1:]
    rows = tok_rows * seq_count
    hidden_all = w_up.shape[1]
    share = hidden_all // (seq_count * fsdp_count)

    piece = dim // (seq_count * fsdp_count)
    all_tokens, all_grad, qkv_w, gain_attn, gain_mlp, own_out, up_w, normed, qkv = gather_start(
        tokens[0],
        out_grad[0],
        w_qkv,
        norm_attn.reshape(1, -1),
        norm_mlp.reshape(1, -1),
        w_out.reshape(2, w_out.shape[0] // 2, dim),
        w_up,
        seq_count,
        fsdp_count,
    )
    qkv_w = qkv_w.reshape(dim, 3 * width)
    up_w = up_w.reshape(dim, hidden_all // seq_count)
    own_down = lax.dynamic_slice_in_dim(w_down, seq_at * share, share, axis=0)

    bias = bias_vector(rel_bias)
    forget = jax.nn.sigmoid(gate_bias)
    forget_row = forget.reshape(1, width)

    attended, others, out_w, down_w, final_memory, mem, upd, lse, slse = attend(
        qkv,
        state_init[0],
        lengths,
        state_query,
        forget_row,
        bias,
        own_out,
        own_down,
        heads,
        seq_count,
        fsdp_count,
    )
    out_w = out_w.reshape(dim, dim)
    down_w = down_w.reshape(fsdp_count * share, dim)
    mid_here, dmid, mlp_gain_grad, dbranch, mlp_parts, up_grad, down_grad = mlp(
        lengths, attended, others, all_tokens, all_grad, out_w, up_w, down_w, gain_mlp, fsdp_count
    )
    span = fsdp_count // seq_count
    if up_grad.ndim == 2:
        up_grad = up_grad.reshape(seq_count, fsdp_count, piece, hidden_all // seq_count)
    dqkv, small, up_part, down_total, out_part, output = attend_back(
        qkv,
        dbranch.reshape(rows, dim),
        out_w,
        attended,
        mem,
        upd,
        lse,
        slse,
        state_grad[0],
        lengths,
        state_query,
        forget_row,
        bias,
        up_grad,
        down_grad.reshape(seq_count, span * share, dim),
        mlp_parts,
        mid_here,
        seq_count,
        fsdp_count,
    )
    tokens_grad, qkv_part, down_part, dquery, grad_gate, grad_table, attn_gain_grad, mlp_gain_grad = finish(
        dqkv,
        qkv_w,
        normed,
        down_total,
        small,
        mlp_gain_grad,
        tokens[0],
        dmid,
        gain_attn,
        seq_count,
        fsdp_count,
    )
    big = (output, final_memory, tokens_grad, qkv_part, out_part, up_part, down_part)
    little = (dquery, grad_gate, grad_table, attn_gain_grad, mlp_gain_grad)
    output, final_memory, tokens_grad, qkv_part, out_part, up_part, down_part, *little = emit(*big, *little)
    dquery, grad_gate, grad_table, attn_gain_grad, mlp_gain_grad = little
    output = output[None]
    tokens_grad = tokens_grad[None]
    if up_part.ndim == 3:
        up_part = up_part.reshape(seq_count, piece, fsdp_count, share)
        up_part = jnp.transpose(up_part, (1, 2, 0, 3)).reshape(piece, hidden_all)
    dquery = dquery.reshape(heads, DH, DH)
    attn_gain_grad = attn_gain_grad.reshape(piece)
    mlp_gain_grad = mlp_gain_grad.reshape(piece)
    return (
        output,
        final_memory[None],
        tokens_grad,
        qkv_part,
        out_part,
        up_part,
        down_part,
        attn_gain_grad,
        mlp_gain_grad,
        grad_table,
        dquery,
        grad_gate,
    )


def solution(mesh):
    placed = (
        P("fsdp", "seq", None),
        P("fsdp"),
        P("fsdp", None, "seq"),
        P("fsdp", None),
        P("fsdp", None),
        P("fsdp", None),
        P("fsdp", None),
        P("fsdp"),
        P("fsdp"),
        P("seq", None),
        P("seq", None, None),
        P("seq", None),
        P("fsdp", "seq", None),
        P("fsdp", None, "seq"),
    )
    return jax.shard_map(
        body,
        mesh=mesh,
        in_specs=placed,
        out_specs=(
            P("fsdp", "seq", None),
            P("fsdp", None, "seq"),
            P("fsdp", "seq", None),
            P(("seq", "fsdp"), None),
            P(("seq", "fsdp"), None),
            P(("seq", "fsdp"), None),
            P(("seq", "fsdp"), None),
            P(("seq", "fsdp")),
            P(("seq", "fsdp")),
            P("seq", None),
            P("seq", None, None),
            P("seq", None),
        ),
        check_vma=False,
    )
```

```python
import functools
import math

import jax
import jax.numpy as jnp
import numpy as np
from jax import lax
from jax.experimental import pallas as pl
from jax.experimental.pallas import tpu as pltpu
from jax.sharding import PartitionSpec as P

H = 8
DH = 128
BLOCK = 512
STATE_VECTORS = 512
QTILE = 256
SPAN = BLOCK + QTILE

EPSILON = 1e-06
BUCKET_EDGES = (19, 21, 24, 27, 31, 35, 40, 46, 52, 59, 67, 77, 87, 99, 113)
BUCKETS = 32
LOG2E = math.log2(math.e)
SCALE = DH ** (-0.5)
NEAR = 384

f32 = jnp.float32
bf16 = jnp.bfloat16
MESH = pl.DeviceIdType.MESH


def bucket_of(distance):
    return np.minimum(distance, 16) + (distance[..., None] >= np.array(BUCKET_EDGES)).sum(-1)


def tile_distance():
    rows = np.arange(QTILE)[:, None]
    cols = np.arange(SPAN)[None, :]
    return rows + BLOCK - cols


def bias_vector(table):
    distance = BLOCK - np.arange(2 * BLOCK)
    inside = (distance >= 0) & (distance < BLOCK)
    bucket = np.where(inside, bucket_of(np.clip(distance, 0, BLOCK)), BUCKETS)
    member = jnp.asarray((np.arange(BUCKETS)[:, None] == bucket[None]).astype(np.float32))
    total = jnp.dot(table, member, precision=lax.Precision.HIGHEST, preferred_element_type=f32)
    return jnp.where(jnp.asarray(inside)[None], total * LOG2E, -jnp.inf)


def tile_bias(vector_ref, head):
    wide = jnp.broadcast_to(vector_ref[head : head + 1, :], (QTILE, 2 * BLOCK))
    return pltpu.roll(wide, 0, 1, stride=1, stride_axis=0)[:, :SPAN]


def dot(a, b):
    return jnp.dot(a, b, preferred_element_type=f32)


def dot_t(a, b):
    return lax.dot_general(a, b, (((1,), (1,)), ((), ())), preferred_element_type=f32)


def t_dot(a, b):
    return lax.dot_general(a, b, (((0,), (0,)), ((), ())), preferred_element_type=f32)


def to_row(column):
    wide = jnp.broadcast_to(column, (column.shape[0], 128))
    return wide.T[0:1, :]


def context_pieces(tile):
    start = tile * QTILE
    pieces = []
    if start < BLOCK:
        pieces.append((0, start, BLOCK, 0))
    pieces.append((1, 0, start + QTILE, BLOCK - start))
    return pieces


def softmax_parts(scores):
    top = functools.reduce(jnp.maximum, [jnp.max(s, axis=-1, keepdims=True) for s in scores])
    raised = [jnp.exp2(s - top) for s in scores]
    total = functools.reduce(jnp.add, [jnp.sum(e, axis=-1, keepdims=True) for e in raised])
    return raised, total, top + jnp.log2(total)


def line_gather(hi, lo, slot, own, z_send, z_recv, y_send, y_recv):
    f = lax.axis_index("fsdp")
    z, y = f // lo, f % lo

    def copy(i, origin, target, send, recv, first=False):
        ref = slot(i, origin)
        return pltpu.make_async_remote_copy(
            src_ref=own(i) if first else ref,
            dst_ref=ref,
            send_sem=send,
            recv_sem=recv,
            device_id={"fsdp": target},
            device_id_type=MESH,
        )

    def right(i, t):
        return copy(i, (z - t) * lo + y, (z + 1) * lo + y, z_send.at[i, 0, t], z_recv.at[i, 0, t], t == 0)

    def left(i, t):
        return copy(i, (z + t) * lo + y, (z - 1) * lo + y, z_send.at[i, 1, t], z_recv.at[i, 1, t], t == 0)

    def across(i, d):
        return copy(
            i, (z + d) * lo + y, z * lo + 1 - y, y_send.at[i, d + hi - 1], y_recv.at[i, d + hi - 1], d == 0
        )

    def start(i):
        pl.when(z + 1 < hi)(lambda: right(i, 0).start())
        pl.when(z >= 1)(lambda: left(i, 0).start())
        across(i, 0).start()

    def step(i, t):
        @pl.when(z - 1 - t >= 0)
        def _():
            copy(i, (z - 1 - t) * lo + y, f, z_send.at[i, 0, t], z_recv.at[i, 0, t]).wait_recv()
            if t + 1 < hi - 1:
                pl.when(z + 1 < hi)(lambda: right(i, t + 1).start())
            across(i, -1 - t).start()

        @pl.when(z + 1 + t < hi)
        def _():
            copy(i, (z + 1 + t) * lo + y, f, z_send.at[i, 1, t], z_recv.at[i, 1, t]).wait_recv()
            if t + 1 < hi - 1:
                pl.when(z >= 1)(lambda: left(i, t + 1).start())
            across(i, 1 + t).start()

    def arrive(i):
        for d in range(1 - hi, hi):

            @pl.when((z + d >= 0) & (z + d < hi))
            def _():
                copy(
                    i, (z + d) * lo + 1 - y, f, y_send.at[i, d + hi - 1], y_recv.at[i, d + hi - 1]
                ).wait_recv()

    def drain(i):
        for d in range(1 - hi, hi):

            @pl.when((z + d >= 0) & (z + d < hi))
            def _():
                across(i, d).wait_send()

        for t in range(hi - 1):

            @pl.when((z + 1 < hi) & (z - t >= 0))
            def _():
                right(i, t).wait_send()

            @pl.when((z >= 1) & (z + t < hi))
            def _():
                left(i, t).wait_send()

    return start, step, arrive, drain


def line_sems(count, hi):
    dma = pltpu.SemaphoreType.DMA
    return [dma((count, 2, hi)), dma((count, 2, hi)), dma((count, 2 * hi)), dma((count, 2 * hi))]


def greet(seq_targets, hi, lo):
    me = lax.axis_index("seq")
    f = lax.axis_index("fsdp")
    z, y = f // lo, f % lo
    barrier = pltpu.get_barrier_semaphore()
    for k in seq_targets:
        pl.semaphore_signal(barrier, inc=1, device_id={"seq": me ^ k}, device_id_type=MESH)
    near = (lax.rem(z + 1, hi) * lo + y, lax.rem(z + hi - 1, hi) * lo + y, z * lo + 1 - y)
    for target in near:
        pl.semaphore_signal(barrier, inc=1, device_id={"fsdp": target}, device_id_type=MESH)
    pl.semaphore_wait(barrier, len(seq_targets) + len(near))


def attend_kernel(
    heads,
    seq,
    hi,
    lo,
    length_ref,
    qkv_ref,
    init_ref,
    query_ref,
    forget_ref,
    vector_ref,
    own_out_ref,
    own_down_ref,
    att_out,
    others_ref,
    outs_ref,
    downs_ref,
    final_ref,
    mem_out,
    upd_out,
    lse_ref,
    slse_ref,
    memory_ref,
    bias_ref,
    att_ref,
    mem_ref,
    upd_ref,
    store_sem,
    own_sem,
    att_send,
    att_recv,
    out_send,
    out_recv,
    z_send,
    z_recv,
    y_send,
    y_recv,
):
    me = lax.axis_index("seq")
    f = lax.axis_index("fsdp")
    length = length_ref[0]
    width = heads * DH
    scale2 = SCALE * LOG2E
    blocks = seq
    bits = [1 << i for i in range(seq.bit_length() - 1)]
    greet(bits, hi, lo)

    own_copies = [
        pltpu.make_async_copy(own_down_ref, downs_ref.at[f], own_sem.at[0]),
        pltpu.make_async_copy(own_out_ref, outs_ref.at[:, me % 2], own_sem.at[1]),
    ]
    for c in own_copies:
        c.start()

    def lowest(k):
        return k & -k

    def out_copy(sending):
        half = me % 2 if sending else 1 - me % 2
        return pltpu.make_async_remote_copy(
            src_ref=own_out_ref,
            dst_ref=outs_ref.at[:, half],
            send_sem=out_send,
            recv_sem=out_recv,
            device_id={"seq": me ^ 1},
            device_id_type=MESH,
        )

    def att_copy(k, b):
        bit = lowest(k)
        came = k ^ bit
        here = pl.ds(pl.multiple_of((b ^ me) * BLOCK, BLOCK), BLOCK)
        there = pl.ds(pl.multiple_of((b ^ me ^ bit) * BLOCK, BLOCK), BLOCK)
        src = others_ref.at[came, here] if came else att_ref.at[here]
        return pltpu.make_async_remote_copy(
            src_ref=src,
            dst_ref=others_ref.at[k, there],
            send_sem=att_send.at[k, b],
            recv_sem=att_recv.at[k, b],
            device_id={"seq": me ^ bit},
            device_id_type=MESH,
        )

    def att_arrival(k, b):
        here = pl.ds(pl.multiple_of((b ^ me) * BLOCK, BLOCK), BLOCK)
        return pltpu.make_async_remote_copy(
            src_ref=others_ref.at[k, here],
            dst_ref=others_ref.at[k, here],
            send_sem=att_send.at[k, b],
            recv_sem=att_recv.at[k, b],
            device_id={"seq": me},
            device_id_type=MESH,
        )

    passing = sorted([k for k in range(2, seq, 2)], key=lambda k: (bin(k).count("1"), -k))

    def onward(k, send):
        for bit in reversed(bits):
            if bit < lowest(k):
                send(k | bit)

    start, step, arrive, drain = line_gather(
        hi, lo, lambda i, origin: downs_ref.at[origin], lambda i: own_down_ref, z_send, z_recv, y_send, y_recv
    )

    start(0)
    out_copy(True).start()
    memory_ref[...] = init_ref[...].astype(f32)
    for head in range(heads):
        bias_ref[head] = tile_bias(vector_ref, head)

    def block_stores(block):
        at = pl.ds(pl.multiple_of((block ^ me) * BLOCK, BLOCK), BLOCK)
        pairs = (
            (att_ref.at[at], att_out.at[at]),
            (mem_ref.at[block], mem_out.at[block]),
            (upd_ref.at[block], upd_out.at[block]),
        )
        return [pltpu.make_async_copy(a, b, store_sem.at[i, block]) for i, (a, b) in enumerate(pairs)]

    @pl.loop(0, blocks)
    def _(block):
        cur_at = pl.multiple_of((block ^ me) * BLOCK, BLOCK)
        prev_at = pl.multiple_of((jnp.maximum(block - 1, 0) ^ me) * BLOCK, BLOCK)
        cur_ref = qkv_ref.at[pl.ds(cur_at, BLOCK)]
        prev_ref = qkv_ref.at[pl.ds(prev_at, BLOCK)]
        for t in range(min(hi - 1, blocks - 1)):
            pl.when(block == t + 1)(lambda t=t: step(0, t))

        live_block = block * BLOCK < length
        for head in range(heads):
            own = slice(head * DH, (head + 1) * DH)
            memory = memory_ref[:, own]
            low = memory.astype(bf16)
            mem_ref[block, :, own] = memory
            refs = (prev_ref, cur_ref)
            key_cols = slice(width + head * DH, width + (head + 1) * DH)
            value_cols = slice(2 * width + head * DH, 2 * width + (head + 1) * DH)
            for tile in range(BLOCK // QTILE):
                rows = slice(tile * QTILE, (tile + 1) * QTILE)
                query = cur_ref[rows, own]
                scores, values = [], []
                for which, at, end, col in context_pieces(tile):
                    s = dot_t(query, refs[which][at:end, key_cols])
                    position = (block - 1 + which) * BLOCK + at + lax.broadcasted_iota(jnp.int32, (1, end - at), 1)
                    live = (position >= 0) & (position < length)
                    s = s * scale2 + bias_ref[head, :, col : col + end - at]
                    scores.append(jnp.where(live, s, -jnp.inf))
                    values.append(refs[which][at:end, value_cols])
                scores.append(dot_t(query, low) * scale2)
                values.append(low)
                raised, total, lse = softmax_parts(scores)
                out = functools.reduce(jnp.add, [dot(e.astype(bf16), v) for e, v in zip(raised, values)])
                att_ref[pl.ds(cur_at + tile * QTILE, QTILE), own] = (out / total).astype(bf16)
                lse_ref[head : head + 1, pl.ds(pl.multiple_of(block * BLOCK, BLOCK) + tile * QTILE, QTILE)] = to_row(lse)
            own_key = cur_ref[:, key_cols]
            own_value = cur_ref[:, value_cols]
            squeries = dot(low, query_ref[head]).astype(bf16)
            position = block * BLOCK + lax.broadcasted_iota(jnp.int32, (1, BLOCK), 1)
            for tile in range(STATE_VECTORS // QTILE):
                rows = slice(tile * QTILE, (tile + 1) * QTILE)
                squery = squeries[rows]
                scores = [
                    dot_t(squery, low) * scale2,
                    jnp.where(position < length, dot_t(squery, own_key) * scale2, -jnp.inf),
                ]
                raised, total, lse = softmax_parts(scores)
                update = dot(raised[0].astype(bf16), low) + dot(raised[1].astype(bf16), own_value)
                update = update / total
                upd_ref[block, rows, own] = update
                slse_ref[head : head + 1, pl.ds(pl.multiple_of(block * BLOCK, BLOCK) + tile * QTILE, QTILE)] = to_row(
                    lse
                )
                forget = forget_ref[:, own]
                old = memory[rows]
                memory_ref[rows, own] = jnp.where(live_block, forget * old + (1.0 - forget) * update, old)

        for bit in reversed(bits):
            att_copy(bit, block).start()
        for c in block_stores(block):
            c.start()

        @pl.when(block >= 1)
        def _():
            for k in passing:
                att_arrival(k, block - 1).wait_recv()
                onward(k, lambda target: att_copy(target, block - 1).start())

    final_ref[...] = memory_ref[...]
    for t in range(min(hi - 1, blocks - 1), hi - 1):
        step(0, t)
    for k in passing:
        att_arrival(k, blocks - 1).wait_recv()
        onward(k, lambda target: att_copy(target, blocks - 1).start())
    arrive(0)
    out_copy(False).wait_recv()
    for k in range(1, seq, 2):
        for b in range(blocks):
            att_arrival(k, b).wait_recv()
    for c in own_copies:
        c.wait()
    drain(0)
    for b in range(blocks):
        for c in block_stores(b):
            c.wait()
    out_copy(True).wait_send()
    for k in range(1, seq):
        for b in range(blocks):
            att_copy(k, b).wait_send()


def attend(qkv, init, length, state_query, forget, bias, own_out, own_down, heads, seq, fsdp):
    rows, width3 = qkv.shape
    width = heads * DH
    blocks = rows // BLOCK
    lo = 2
    hi = fsdp // lo
    dim = own_down.shape[1]
    anywhere = pl.BlockSpec(memory_space=pl.ANY)
    vmem = pl.BlockSpec(memory_space=pltpu.VMEM)
    dma = pltpu.SemaphoreType.DMA
    return pl.pallas_call(
        functools.partial(attend_kernel, heads, seq, hi, lo),
        out_shape=(
            jax.ShapeDtypeStruct((rows, width), bf16),
            jax.ShapeDtypeStruct((seq, rows, width), bf16),
            jax.ShapeDtypeStruct((fsdp, 2) + own_out.shape[1:], bf16),
            jax.ShapeDtypeStruct((fsdp,) + own_down.shape, bf16),
            jax.ShapeDtypeStruct((STATE_VECTORS, width), f32),
            jax.ShapeDtypeStruct((blocks, STATE_VECTORS, width), f32),
            jax.ShapeDtypeStruct((blocks, STATE_VECTORS, width), f32),
            jax.ShapeDtypeStruct((heads, rows), f32),
            jax.ShapeDtypeStruct((heads, blocks * STATE_VECTORS), f32),
        ),
        in_specs=[pl.BlockSpec(memory_space=pltpu.SMEM)] + [vmem] * 7,
        out_specs=(anywhere, anywhere, anywhere, anywhere, vmem, anywhere, anywhere, vmem, vmem),
        scratch_shapes=[
            pltpu.VMEM((STATE_VECTORS, width), f32),
            pltpu.VMEM((heads, QTILE, SPAN), f32),
            pltpu.VMEM((rows, width), bf16),
            pltpu.VMEM((blocks, STATE_VECTORS, width), f32),
            pltpu.VMEM((blocks, STATE_VECTORS, width), f32),
            dma((3, blocks)),
            dma((2,)),
            dma((seq, blocks)),
            dma((seq, blocks)),
            dma,
            dma,
        ]
        + line_sems(1, hi),
        compiler_params=pltpu.CompilerParams(collective_id=3, has_side_effects=True, vmem_limit_bytes=62 << 20),
        cost_estimate=pl.CostEstimate(
            flops=blocks * heads * 512 * 2400 * 128 * 4, bytes_accessed=16 << 20, transcendentals=10 << 20
        ),
        name="attend",
    )(length, qkv, init, state_query, forget, bias, own_out, own_down)


def line_reduce(hi, lo, block, total, from_y, from_z, z_send, z_recv, y_send, y_recv, loads=None):
    loads = loads or {}
    f = lax.axis_index("fsdp")
    z, y = f // lo, f % lo

    def remote(src, dst, send, recv, target):
        return pltpu.make_async_remote_copy(
            src_ref=src, dst_ref=dst, send_sem=send, recv_sem=recv, device_id={"fsdp": target}, device_id_type=MESH
        )

    def across(i, d):
        return remote(
            block(i, d * lo + 1 - y), from_y[i].at[d], y_send.at[i, d], y_recv.at[i, d], z * lo + 1 - y
        )

    def start(i):
        for d in range(hi):
            across(i, d).start()

    def combine(i):
        for d in range(hi):
            across(i, d).wait_recv()
            if i in loads:
                loads[i][d].wait()
                own = total[i].at[d]
            else:
                own = block(i, d * lo + y)
            total[i][d] = (own[...].astype(f32) + from_y[i][d].astype(f32)).astype(bf16)

    def hop(i, side, t, at, target):
        return remote(
            total[i].at[jnp.clip(at, 0, hi - 1)],
            from_z[i].at[side, t],
            z_send.at[i, side, t],
            z_recv.at[i, side, t],
            target,
        )

    def sending(t):
        d = t - (hi - 1 - z)
        m = hi - 1 - (t - z)
        return ((0, d, (d >= 0) & (d < z), z - 1), (1, m, (m > z) & (m < hi), z + 1))

    def zsend(i, t):
        for side, at, cond, target in sending(t):
            pl.when(cond)(lambda: hop(i, side, t, at, target * lo + y).start())

    def zrecv(i, t):
        d = t - (hi - 2 - z)
        m = hi - 1 - (t - (z - 1))
        for side, at, cond in ((0, d, (z + 1 < hi) & (d >= 0)), (1, m, (z > 0) & (m < hi))):

            @pl.when(cond)
            def _():
                hop(i, side, t, at, f).wait_recv()
                slot = jnp.clip(at, 0, hi - 1)
                total[i][slot] = (total[i][slot].astype(f32) + from_z[i][side, t].astype(f32)).astype(bf16)

    def drain_y(i):
        for d in range(hi):
            across(i, d).wait_send()

    def drain_z(i):
        for t in range(hi - 1):
            for side, at, cond, target in sending(t):
                pl.when(cond)(lambda: hop(i, side, t, at, f).wait_send())

    return start, combine, zsend, zrecv, drain_y, drain_z


def seq_levels(seq):
    bits = [1 << i for i in range(seq.bit_length() - 1)]
    slots = {}
    for bit in bits:
        for j in range(0, seq, 2 * bit):
            slots[bit, j] = len(slots)
    return bits, slots


def diagonal_sums(tile):
    rows, lanes = tile.shape
    wide = jnp.concatenate([tile, jnp.zeros((rows, lanes), f32)], axis=1)
    row = lax.broadcasted_iota(jnp.int32, wide.shape, 0)
    bit = 1
    while bit < rows:
        wide = jnp.where((row & bit) != 0, pltpu.roll(wide, 2 * lanes - bit, 1), wide)
        bit *= 2
    return jnp.sum(wide, axis=0, keepdims=True)


def attend_back_kernel(heads, seq, hi, lo, inside, length_ref, *refs):
    refs = list(refs)

    def take(count):
        taken = refs[:count]
        del refs[:count]
        return taken

    qkv_hbm, db_hbm, wout_hbm, att_hbm, mem_hbm, upd_hbm, lse_ref, slse_ref = take(8)
    sgrad_ref, query_ref, forget_ref, vector_ref, up_ref, down_ref, mo_ref, mid_hbm = take(8)
    ow_in = None if inside else take(1)[0]
    dqkv_out, small_ref, upart_ref, dtotal_ref, opart_ref, output_ref = take(6)
    qkv_ref, db_ref, att_ref, mem_ref, upd_ref, mid_ref, dqkv_ref, wout_ref = take(8)
    dmem_ref, dnext_ref, dctx_ref, bias_ref, near_ref, far_ref, dout_ref, ow_buf = take(8)
    moved, to, tu, yo, yu, yd, zo, zu, xu, mo_low, mo_in = take(11)
    z_send, z_recv, y_send, y_recv, m_send, m_recv, e_send, e_recv, x_send, x_recv = take(10)
    load_sem, block_sem, up_sem, mo_sem, out_sem = take(5)
    ow_ref = ow_buf if inside else ow_in

    me = lax.axis_index("seq")
    f = lax.axis_index("fsdp")
    z, y = f // lo, f % lo
    blocks = seq
    length = length_ref[0]
    width = heads * DH
    scale2 = SCALE * LOG2E
    tok_rows = mid_ref.shape[0]
    share = dtotal_ref.shape[1]
    bits, slots = seq_levels(seq)

    def chunk_at(block):
        return pl.ds(pl.multiple_of((block ^ me) * BLOCK, BLOCK), BLOCK)

    def block_loads(block):
        at = chunk_at(block)
        pairs = (
            (qkv_hbm.at[at], qkv_ref.at[at]),
            (mem_hbm.at[block], mem_ref.at[block]),
            (upd_hbm.at[block], upd_ref.at[block]),
        )
        return [pltpu.make_async_copy(a, b, block_sem.at[i, block]) for i, (a, b) in enumerate(pairs)]

    loads = [
        pltpu.make_async_copy(att_hbm, att_ref, load_sem.at[0]),
        pltpu.make_async_copy(db_hbm, db_ref, load_sem.at[1]),
        pltpu.make_async_copy(down_ref.at[me], moved.at[me], load_sem.at[2]),
        pltpu.make_async_copy(mid_hbm, mid_ref, load_sem.at[3]),
        pltpu.make_async_copy(
            wout_hbm.at[pl.ds(pl.multiple_of(me * width, width), width)], wout_ref, load_sem.at[4]
        ),
    ]
    up_loads = [
        pltpu.make_async_copy(up_ref.at[d] if inside else up_ref.at[:, d * lo + y], tu.at[d], up_sem.at[d])
        for d in range(hi)
    ]
    mo_loads = [pltpu.make_async_copy(mo_ref.at[j], mo_low.at[j // 2], mo_sem.at[j // 2]) for j in range(0, seq, 2)]
    for c in up_loads + loads[:2] + loads[4:] + block_loads(blocks - 1) + mo_loads:
        c.start()
    for b in reversed(range(blocks - 1)):
        for c in block_loads(b):
            c.start()
    for c in loads[2:4]:
        c.start()
    greet(list(range(1, seq)), hi, lo)

    def mo_copy(bit, j):
        slot = slots[bit, j]
        return pltpu.make_async_remote_copy(
            src_ref=mo_ref.at[j ^ bit] if bit == 1 else mo_low.at[(j ^ bit) // 2],
            dst_ref=mo_in.at[slot],
            send_sem=m_send.at[slot],
            recv_sem=m_recv.at[slot],
            device_id={"seq": me ^ bit},
            device_id_type=MESH,
        )

    def move_copy(k):
        return pltpu.make_async_remote_copy(
            src_ref=down_ref.at[me ^ k],
            dst_ref=moved.at[me],
            send_sem=e_send.at[k],
            recv_sem=e_recv.at[k],
            device_id={"seq": me ^ k},
            device_id_type=MESH,
        )

    def move_arrival(k):
        return pltpu.make_async_remote_copy(
            src_ref=down_ref.at[me],
            dst_ref=moved.at[me ^ k],
            send_sem=e_send.at[k],
            recv_sem=e_recv.at[k],
            device_id={"seq": me},
            device_id_type=MESH,
        )

    def block_of(i, target):
        if i == 0:
            return ow_ref.at[target]
        if i == 1:
            return up_ref.at[:, target]
        return moved.at[target % seq, pl.ds(pl.multiple_of((target // seq) * share, share), share)]

    start, combine, zsend, zrecv, drain_y, drain_z = line_reduce(
        hi,
        lo,
        block_of,
        (to, tu, dtotal_ref),
        (yo, yu, yd),
        (zo, zu),
        z_send,
        z_recv,
        y_send,
        y_recv,
        {1: up_loads},
    )

    def exchange(k, sending):
        return pltpu.make_async_remote_copy(
            src_ref=tu.at[z, me ^ k] if sending else tu.at[z, me],
            dst_ref=xu.at[me] if sending else xu.at[me ^ k],
            send_sem=x_send.at[k],
            recv_sem=x_recv.at[k],
            device_id={"seq": me ^ k if sending else me},
            device_id_type=MESH,
        )

    if not inside:
        start(1)
    for k in reversed(range(1, seq)):
        move_copy(k).start()
    for j in range(seq - 1, 0, -2):
        mo_copy(1, j ^ 1).start()
    if inside:
        for c in up_loads:
            c.wait()
        zsend(1, 0)
    dmem_ref[...] = sgrad_ref[...].astype(f32)
    dnext_ref[...] = jnp.zeros_like(dnext_ref)
    small_ref[...] = jnp.zeros_like(small_ref)
    near_ref[...] = jnp.zeros_like(near_ref)
    far_ref[...] = jnp.zeros_like(far_ref)
    for head in range(heads):
        bias_ref[head] = tile_bias(vector_ref, head).T
    for c in loads[:2] + loads[4:]:
        c.wait()
    if inside:
        full = t_dot(att_ref[...], db_ref[...]).astype(bf16)
        ow_buf[...] = full.reshape(ow_buf.shape)
    start(0)

    def mo_step(j):
        mo_loads[j // 2].wait()
        for bit in bits:
            if j & bit:
                mo_copy(bit, j ^ bit).start()
                break
            mo_copy(bit, j).wait_recv()
            own = mo_low[j // 2].astype(f32)
            mo_low[j // 2] = (own + mo_in[slots[bit, j]].astype(f32)).astype(bf16)

    def down_ready():
        for k in range(1, seq):
            move_arrival(k).wait_recv()
        loads[2].wait()
        start(2)

    def up_done():
        for k in range(1, seq):
            exchange(k, True).start()

    def zstep(i, t):
        zrecv(i, t)
        if t + 1 < hi - 1:
            zsend(i, t + 1)

    jobs = [lambda j=j: mo_step(j) for j in range(seq - 2, 0, -2)]
    if not inside:
        jobs.append(lambda: (combine(1), zsend(1, 0)))
    jobs.append(lambda: (zstep(1, 0), combine(0), zsend(0, 0)))
    for t in range(1, hi - 1):
        jobs.append(lambda t=t: zstep(1, t))
        if t == 1:
            jobs.append(lambda: down_ready())
    jobs.append(lambda: up_done())
    jobs += [lambda t=t: zstep(0, t) for t in range(hi - 1)]
    points = blocks * heads - 1

    dq_row = heads * DH
    block_loads(blocks - 1)[0].wait()

    @pl.loop(0, blocks)
    def _(step):
        block = blocks - 1 - step
        pl.when(block >= 1)(lambda: block_loads(jnp.maximum(block - 1, 0))[0].wait())
        for c in block_loads(block)[1:]:
            c.wait()
        cur_at = pl.multiple_of((block ^ me) * BLOCK, BLOCK)
        prev_at = pl.multiple_of((jnp.maximum(block - 1, 0) ^ me) * BLOCK, BLOCK)
        base = pl.multiple_of(block * BLOCK, BLOCK)
        cur_ref = qkv_ref.at[pl.ds(cur_at, BLOCK)]
        prev_ref = qkv_ref.at[pl.ds(prev_at, BLOCK)]
        live_block = block * BLOCK < length
        refs = (prev_ref, cur_ref)
        dout_ref[...] = dot_t(db_ref[pl.ds(cur_at, BLOCK)], wout_ref[...]).astype(bf16)
        for head in range(heads):
            for n, job in enumerate(jobs[:points]):
                if (n + 1) % heads == head:
                    pl.when(step == (n + 1) // heads)(lambda job=job: (job(), None)[1])
            own = slice(head * DH, (head + 1) * DH)
            key_cols = slice(width + head * DH, width + (head + 1) * DH)
            value_cols = slice(2 * width + head * DH, 2 * width + (head + 1) * DH)
            memory = mem_ref[block, :, own]
            update = upd_ref[block, :, own]
            low = memory.astype(bf16)
            forget = forget_ref[:, own]
            dmem = dmem_ref[:, own]
            dupd = jnp.where(live_block, (1.0 - forget) * dmem, 0.0).astype(bf16)
            gone = jnp.where(live_block, dmem * (memory - update), 0.0)
            small_ref[dq_row + head : dq_row + head + 1, :] += jnp.sum(gone, axis=0, keepdims=True)
            dmem_new = jnp.where(live_block, forget * dmem, dmem)
            own_key = cur_ref[:, key_cols]
            own_value = cur_ref[:, value_cols]
            squeries = dot(low, query_ref[head]).astype(bf16)
            sdelta = jnp.sum((dupd.astype(f32) * update).T, axis=0, keepdims=True)
            slse = slse_ref[head : head + 1, pl.ds(base, BLOCK)]
            dsquery = jnp.zeros((STATE_VECTORS, DH), f32)
            dkey = []
            dvalue = []
            for part in range(2 * STATE_VECTORS // QTILE):
                own_part = part >= STATE_VECTORS // QTILE
                at = (part % (STATE_VECTORS // QTILE)) * QTILE
                keys = (own_key if own_part else low)[at : at + QTILE]
                values = (own_value if own_part else low)[at : at + QTILE]
                s = dot_t(keys, squeries) * scale2 - slse
                if own_part:
                    position = block * BLOCK + at + lax.broadcasted_iota(jnp.int32, (QTILE, 1), 0)
                    s = jnp.where(position < length, s, -jnp.inf)
                p = jnp.exp2(s)
                dp = dot_t(values, dupd)
                ds = (p * (dp - sdelta)).astype(bf16)
                dvalue.append(dot(p.astype(bf16), dupd))
                dkey.append(dot(ds, squeries))
                dsquery += t_dot(ds, keys)
            half = STATE_VECTORS // QTILE
            dlow = [dvalue[i] + dkey[i] * SCALE for i in range(half)]
            dctx_ref[0, 0:BLOCK] = jnp.zeros((BLOCK, DH), f32)
            dctx_ref[1, 0:BLOCK] = jnp.zeros((BLOCK, DH), f32)
            for i in range(half):
                rows = slice(BLOCK + i * QTILE, BLOCK + (i + 1) * QTILE)
                old = slice(i * QTILE, (i + 1) * QTILE)
                dctx_ref[0, rows] = dkey[half + i] * SCALE + dnext_ref[0, old, own]
                dctx_ref[1, rows] = dvalue[half + i] + dnext_ref[1, old, own]
            dsq = (dsquery * SCALE).astype(bf16)
            small_ref[head * DH : (head + 1) * DH, :] += t_dot(low, dsq)
            dmem_ref[:, own] = dmem_new + dot_t(dsq, query_ref[head])
            for tile in range(BLOCK // QTILE):
                rows = slice(tile * QTILE, (tile + 1) * QTILE)
                here = pl.ds(cur_at + tile * QTILE, QTILE)
                query = cur_ref[rows, own]
                dout = dout_ref[rows, own]
                lse = lse_ref[head : head + 1, pl.ds(base + tile * QTILE, QTILE)]
                delta = jnp.sum((dout.astype(f32) * att_ref[here, own].astype(f32)).T, axis=0, keepdims=True)
                dq = jnp.zeros((QTILE, DH), f32)
                for which, first, end, col in context_pieces(tile):
                    for at in range(first, end, QTILE):
                        keys = refs[which][at : at + QTILE, key_cols]
                        values = refs[which][at : at + QTILE, value_cols]
                        band = col + at - first
                        position = (block - 1 + which) * BLOCK + at + lax.broadcasted_iota(jnp.int32, (QTILE, 1), 0)
                        live = (position >= 0) & (position < length)
                        s = dot_t(keys, query) * scale2 + bias_ref[head, band : band + QTILE, :] - lse
                        p = jnp.exp2(jnp.where(live, s, -jnp.inf))
                        dp = dot_t(values, dout)
                        ds = (p * (dp - delta)).astype(bf16)
                        wide = ds.astype(f32)
                        edge = min(max(SPAN - NEAR - band, 0), QTILE)
                        if edge:
                            far_ref[head] += functools.reduce(jnp.add, [wide[i : i + 8] for i in range(0, edge, 8)])
                        if edge < QTILE:
                            at_near = band + edge - (SPAN - NEAR)
                            near_ref[head, at_near : at_near + QTILE - edge] += wide[edge:]
                        into = slice(which * BLOCK + at, which * BLOCK + at + QTILE)
                        dctx_ref[1, into] += dot(p.astype(bf16), dout)
                        dctx_ref[0, into] += dot(ds, query) * SCALE
                        dq += t_dot(ds, keys)
                for part in range(half):
                    keys = low[part * QTILE : (part + 1) * QTILE]
                    s = dot_t(keys, query) * scale2 - lse
                    p = jnp.exp2(s)
                    dp = dot_t(keys, dout)
                    ds = (p * (dp - delta)).astype(bf16)
                    dlow[part] += dot(p.astype(bf16), dout) + dot(ds, query) * SCALE
                    dq += t_dot(ds, keys)
                dqkv_ref[here, own] = (dq * SCALE).astype(bf16)
            for part in range(half):
                dmem_ref[part * QTILE : (part + 1) * QTILE, own] += dlow[part]
            dnext_ref[0, :, own] = dctx_ref[0, 0:BLOCK]
            dnext_ref[1, :, own] = dctx_ref[1, 0:BLOCK]
            dqkv_ref[pl.ds(cur_at, BLOCK), key_cols] = dctx_ref[0, BLOCK:].astype(bf16)
            dqkv_ref[pl.ds(cur_at, BLOCK), value_cols] = dctx_ref[1, BLOCK:].astype(bf16)

    dqkv_store = pltpu.make_async_copy(dqkv_ref, dqkv_out, out_sem)
    dqkv_store.start()
    for job in jobs[points:]:
        job()
    member = bucket_members()
    lane = lax.broadcasted_iota(jnp.int32, (1, DH), 1)
    for head in range(heads):
        sums = jnp.broadcast_to(diagonal_sums(near_ref[head]), (8, 2 * QTILE))
        table = jnp.dot(sums, member, precision=lax.Precision.HIGHEST, preferred_element_type=f32)[0:1]
        total = jnp.sum(jnp.sum(far_ref[head], axis=0, keepdims=True), axis=1, keepdims=True)
        row = dq_row + heads + head
        small_ref[row : row + 1, :] = table + jnp.where(lane == BUCKETS - 1, total, 0.0)
        row = dq_row + head
        forget = forget_ref[:, head * DH : (head + 1) * DH]
        small_ref[row : row + 1, :] = small_ref[row : row + 1, :] * forget * (1.0 - forget)
    loads[3].wait()
    mo_loads[0].wait()
    for bit in bits:
        mo_copy(bit, 0).wait_recv()
    step = 128
    for r in range(0, tok_rows, step):
        at = slice(r, r + step)
        value = mid_ref[at] + mo_low[0, at].astype(f32)
        for bit in bits:
            value = value + mo_in[slots[bit, 0], at].astype(f32)
        position = me * tok_rows + r + lax.broadcasted_iota(jnp.int32, (step, 1), 0)
        output_ref[at] = (value * jnp.where(position < length, 1.0, 0.0)).astype(bf16)
    combine(2)
    opart_ref[...] = to[z].astype(f32)
    for k in range(1, seq):
        exchange(k, False).wait_recv()
    xu[me] = tu[z, me]
    write_parts(upart_ref, xu, seq, share)
    for i in (0, 2) if inside else (0, 1, 2):
        drain_y(i)
    for i in range(2):
        drain_z(i)
    for bit in bits:
        for j in range(0, seq, 2 * bit):
            mo_copy(bit, j).wait_send()
    for k in range(1, seq):
        move_copy(k).wait_send()
        exchange(k, True).wait_send()
    dqkv_store.wait()


def bucket_members():
    shape = (2 * QTILE, DH)
    row = lax.broadcasted_iota(jnp.int32, shape, 0)
    lane = lax.broadcasted_iota(jnp.int32, shape, 1)
    distance = jnp.where(row < QTILE, row, row - 2 * QTILE) + NEAR - QTILE
    bucket = jnp.minimum(distance, 16)
    for edge in BUCKET_EDGES:
        bucket = bucket + jnp.where(distance >= edge, 1, 0)
    inside = (distance >= 0) & (distance < BLOCK) & (bucket == lane)
    return jnp.where(inside, 1.0, 0.0)


def write_parts(out_ref, pieces, seq, unit):
    if len(out_ref.shape) == 3:
        out_ref[...] = pieces[...].astype(f32)
        return
    count = pieces.shape[2] // unit
    for k in range(seq):
        for c in range(count):
            at = (c * seq + k) * unit
            out_ref[:, at : at + unit] = pieces[k, :, c * unit : (c + 1) * unit].astype(f32)


def attend_back(
    qkv, db, wout, att, mem, upd, lse, slse, sgrad, length, state_query, forget, bias, up, down, mo, mid, seq, fsdp
):
    rows, width3 = qkv.shape
    width = width3 // 3
    heads = width // DH
    dim = db.shape[1]
    lo = 2
    hi = fsdp // lo
    piece, hidden = up.shape[2:]
    share = hidden // fsdp
    tok_rows = mid.shape[0]
    inside = piece % 16 == 0
    blocks = (piece, dim), (seq, piece, hidden), (share, dim)
    small_rows = heads * (DH + 2)
    small_rows += -small_rows % 8
    vmem = pl.BlockSpec(memory_space=pltpu.VMEM)
    anywhere = pl.BlockSpec(memory_space=pl.ANY)
    dma = pltpu.SemaphoreType.DMA

    def buf(*shape):
        return pltpu.VMEM(shape, bf16)

    extra = []
    if not inside:
        extra.append(t_dot(att, db).astype(bf16).reshape(fsdp, piece, dim))
    upart = (piece, hidden * seq) if share % 128 == 0 else (seq, piece, hidden)
    return pl.pallas_call(
        functools.partial(attend_back_kernel, heads, seq, hi, lo, inside),
        out_shape=(
            jax.ShapeDtypeStruct((rows, width3), bf16),
            jax.ShapeDtypeStruct((small_rows, DH), f32),
            jax.ShapeDtypeStruct(upart, f32),
            jax.ShapeDtypeStruct((hi, share, dim), bf16),
            jax.ShapeDtypeStruct((piece, dim), f32),
            jax.ShapeDtypeStruct((tok_rows, dim), bf16),
        ),
        in_specs=[pl.BlockSpec(memory_space=pltpu.SMEM), anywhere, anywhere, anywhere]
        + [anywhere] * 3
        + [vmem] * 6
        + [anywhere] * 4
        + [vmem] * len(extra),
        out_specs=(anywhere,) + (vmem,) * 5,
        scratch_shapes=[
            buf(rows, width3),
            buf(rows, dim),
            buf(rows, width),
            pltpu.VMEM(mem.shape, f32),
            pltpu.VMEM(upd.shape, f32),
            pltpu.VMEM((tok_rows, dim), f32),
            buf(rows, width3),
            buf(width, dim),
            pltpu.VMEM((STATE_VECTORS, width), f32),
            pltpu.VMEM((2, BLOCK, width), f32),
            pltpu.VMEM((2, 2 * BLOCK, DH), f32),
            pltpu.VMEM((heads, SPAN, QTILE), f32),
            pltpu.VMEM((heads, NEAR, QTILE), f32),
            pltpu.VMEM((heads, 8, QTILE), f32),
            buf(BLOCK, width),
            buf(fsdp, piece, dim),
            buf(*down.shape),
            buf(hi, *blocks[0]),
            buf(hi, *blocks[1]),
            buf(hi, *blocks[0]),
            buf(16, 128) if inside else buf(hi, *blocks[1]),
            buf(hi, *blocks[2]),
            buf(2, max(hi - 1, 1), *blocks[0]),
            buf(2, max(hi - 1, 1), *blocks[1]),
            buf(*blocks[1]),
            buf(max(seq // 2, 1), tok_rows, dim),
            buf(max(seq - 1, 1), tok_rows, dim),
            dma((2, 2, hi)),
            dma((2, 2, hi)),
            dma((3, hi)),
            dma((3, hi)),
            dma((seq,)),
            dma((seq,)),
            dma((seq,)),
            dma((seq,)),
            dma((seq,)),
            dma((seq,)),
            dma((5,)),
            dma((3, seq)),
            dma((hi,)),
            dma((seq,)),
            dma,
        ],
        compiler_params=pltpu.CompilerParams(collective_id=4, has_side_effects=True, vmem_limit_bytes=62 << 20),
        cost_estimate=pl.CostEstimate(
            flops=seq * heads * 512 * 2400 * 128 * 10, bytes_accessed=20 << 20, transcendentals=10 << 20
        ),
        name="attend_back",
    )(
        length, qkv, db, wout, att, mem, upd, lse, slse, sgrad, state_query, forget, bias, up, down, mo, mid, *extra
    )


def gather_kernel(seq, hi, lo, *refs):
    refs = list(refs)

    def take(count):
        taken = refs[:count]
        del refs[:count]
        return taken

    tok_ref, grad_ref, wq_ref, ga_ref, gm_ref, wo_ref, wu_ref = take(7)
    toks_ref, grads_ref, wqs_ref, gas_ref, gms_ref, wos_ref, wus_ref, normed_ref, qkv_ref = take(9)
    toks_full, grad_buf, wq_full, ga_full, gm_full, wo_buf, wu_buf, normed_buf, qkv_buf = take(9)
    own_sem, store_sem, seq_send, seq_recv, chunk_sem, z_send, z_recv, y_send, y_recv = take(9)

    me = lax.axis_index("seq")
    f = lax.axis_index("fsdp")
    fsdp = hi * lo
    bits = [1 << i for i in range(seq.bit_length() - 1)]
    high = [bit for bit in reversed(bits) if bit > 1]
    rows, dim = tok_ref.shape
    width = wq_full.shape[2] // 3
    share = wus_ref.shape[2] // fsdp
    every = wq_ref.shape[1] // 3
    loads = [[] for _ in range(7)]

    def load(i, src, dst):
        loads[i].append(pltpu.make_async_copy(src, dst, own_sem.at[i, len(loads[i])]))
        loads[i][-1].start()

    for c in range(3):
        cols = pl.ds(pl.multiple_of(c * every + me * width, width), width)
        load(0, wq_ref.at[:, cols], wq_full.at[f, :, pl.ds(c * width, width)])
    load(1, ga_ref, ga_full.at[f])
    load(2, gm_ref, gm_full.at[f])
    load(3, wo_ref.at[me % 2], wo_buf)
    if wu_ref.shape[1] == wus_ref.shape[2]:
        load(4, wu_ref, wu_buf)
    else:
        for c in range(fsdp):
            cols = pl.ds(pl.multiple_of((c * seq + me) * share, share), share)
            load(4, wu_ref.at[:, cols], wu_buf.at[:, pl.ds(c * share, share)])
    load(5, tok_ref, toks_full.at[0])
    load(6, grad_ref, grad_buf)
    greet(bits, hi, lo)

    pairs = ((tok_ref, toks_full), (grad_ref, grads_ref))

    def seq_copy(i, source, slot, bit):
        src, out = pairs[i]
        return pltpu.make_async_remote_copy(
            src_ref=out.at[source] if source else src,
            dst_ref=out.at[slot],
            send_sem=seq_send.at[i, slot],
            recv_sem=seq_recv.at[i, slot],
            device_id={"seq": me ^ bit},
            device_id_type=MESH,
        )

    sends = []

    def send(i, source, slot, bit):
        sends.append(seq_copy(i, source, slot, bit))
        sends[-1].start()

    fulls = (wq_full, ga_full, gm_full, wos_ref, wus_ref)
    bufs = (None, None, None, wo_buf, wu_buf)
    start, step, arrive, drain = line_gather(
        hi,
        lo,
        lambda i, origin: fulls[i].at[origin],
        lambda i: fulls[i].at[f] if i < 3 else bufs[i],
        z_send,
        z_recv,
        y_send,
        y_recv,
    )
    first, later = (0, 1, 2), (3, 4)
    if high:
        send(0, 0, high[0], high[0])
    if seq > 1:
        send(0, 0, 1, 1)
    for i in first:
        for c in loads[i]:
            c.wait()
        start(i)
    if high:
        send(1, 0, high[0], high[0])
    if seq > 1:
        send(1, 0, 1, 1)
    stores = []

    def store(src, dst, sem):
        stores.append(pltpu.make_async_copy(src, dst, sem))
        stores[-1].start()

    for t in range(hi - 1):
        for i in first:
            step(i, t)
        if t == min(1, hi - 2):
            for i in later:
                for c in loads[i]:
                    c.wait()
                start(i)
            store(wo_buf, wos_ref.at[f], store_sem.at[0])
            store(wu_buf, wus_ref.at[f], store_sem.at[1])
    for c in loads[5] + loads[6]:
        c.wait()
    store(toks_full.at[0], toks_ref.at[0], chunk_sem.at[0, 0])
    store(grad_buf, grads_ref.at[0], store_sem.at[2])
    for i in first:
        arrive(i)
    store(wq_full, wqs_ref, store_sem.at[3])
    gas_ref[...] = jnp.concatenate([ga_full[n] for n in range(fsdp)], axis=1).astype(f32)
    gms_ref[...] = jnp.concatenate([gm_full[n] for n in range(fsdp)], axis=1).astype(f32)
    gain = gas_ref[...]

    def project(j):
        if j:
            store(toks_full.at[j], toks_ref.at[j], chunk_sem.at[0, j])

        @pl.loop(0, rows // 256)
        def _(n):
            at = pl.ds(pl.multiple_of(n * 256, 256), 256)
            into = pl.ds(pl.multiple_of(j * rows + n * 256, 256), 256)
            x = toks_full[j, at].astype(f32)
            rho = lax.rsqrt(jnp.mean(x * x, axis=-1, keepdims=True) + EPSILON)
            normed = (x * rho * gain).astype(bf16)
            normed_buf[into] = normed
            qkv_buf[into] = dot(normed, wq_full[...].reshape(dim, 3 * width)).astype(bf16)

        at = pl.ds(j * rows, rows)
        store(normed_buf.at[at], normed_ref.at[at], chunk_sem.at[1, j])
        store(qkv_buf.at[at], qkv_ref.at[at], chunk_sem.at[2, j])

    hop = [0]

    def advance():
        if hop[0] < hi - 1:
            for i in later:
                step(i, hop[0])
            hop[0] += 1

    project(0)
    advance()
    have = [0]
    for n, bit in enumerate(high):
        if n:
            for j in have:
                send(0, j, j ^ bit, bit)
        for j in have:
            seq_copy(0, 0, j ^ bit, bit).wait_recv()
            send(0, j ^ bit, j ^ bit ^ 1, 1)
        have += [j ^ bit for j in have]
    for j in have:
        if j:
            project(j)
            advance()
        if seq > 1:
            seq_copy(0, 0, j ^ 1, 1).wait_recv()
            project(j ^ 1)
            advance()
    while hop[0] < hi - 1:
        advance()
    have = [0]
    for n, bit in enumerate(high):
        if n:
            for j in have:
                send(1, j, j ^ bit, bit)
        for j in have:
            seq_copy(1, 0, j ^ bit, bit).wait_recv()
            send(1, j ^ bit, j ^ bit ^ 1, 1)
        have += [j ^ bit for j in have]
    if seq > 1:
        for j in have:
            seq_copy(1, 0, j ^ 1, 1).wait_recv()
    for i in later:
        arrive(i)
    for i in first + later:
        drain(i)
    for c in sends:
        c.wait_send()
    for c in stores:
        c.wait()


def gather_start(tokens, grads, w_qkv, gain_a, gain_m, w_out, w_up, seq, fsdp):
    lo = 2
    hi = fsdp // lo
    dim_rows, hidden = w_up.shape
    share = hidden // (seq * fsdp)
    if share % 128:
        w_up = lax.dynamic_slice_in_dim(w_up.reshape(dim_rows, fsdp, seq, share), lax.axis_index("seq"), 1, axis=2)
        w_up = w_up.reshape(dim_rows, fsdp * share)
    rows, dim = tokens.shape
    width3 = w_qkv.shape[1] // seq
    anywhere = pl.BlockSpec(memory_space=pl.ANY)
    vmem = pl.BlockSpec(memory_space=pltpu.VMEM)
    dma = pltpu.SemaphoreType.DMA

    def like(*shape):
        return jax.ShapeDtypeStruct(shape, bf16)

    def buf(*shape):
        return pltpu.VMEM(shape, bf16)

    return pl.pallas_call(
        functools.partial(gather_kernel, seq, hi, lo),
        out_shape=(
            like(seq, rows, dim),
            like(seq, rows, dim),
            like(fsdp, dim_rows, width3),
            jax.ShapeDtypeStruct((1, dim), f32),
            jax.ShapeDtypeStruct((1, dim), f32),
            like(fsdp, *w_out.shape[1:]),
            like(fsdp, dim_rows, hidden // seq),
            like(seq * rows, dim),
            like(seq * rows, width3),
        ),
        in_specs=[anywhere] * 7,
        out_specs=(anywhere,) * 3 + (vmem,) * 2 + (anywhere,) * 4,
        scratch_shapes=[
            buf(seq, rows, dim),
            buf(rows, dim),
            buf(fsdp, dim_rows, width3),
            buf(fsdp, *gain_a.shape),
            buf(fsdp, *gain_m.shape),
            buf(*w_out.shape[1:]),
            buf(dim_rows, hidden // seq),
            buf(seq * rows, dim),
            buf(seq * rows, width3),
            dma((7, max(fsdp, 3))),
            dma((4,)),
            dma((2, seq)),
            dma((2, seq)),
            dma((3, seq)),
        ]
        + line_sems(5, hi),
        compiler_params=pltpu.CompilerParams(collective_id=0, has_side_effects=True, vmem_limit_bytes=62 << 20),
        name="gather_start",
    )(tokens, grads, w_qkv, gain_a, gain_m, w_out, w_up)


def finish_kernel(seq, hi, lo, inside, *refs):
    refs = list(refs)

    def take(count):
        taken = refs[:count]
        del refs[:count]
        return taken

    dqkv_hbm, wqkv_hbm, normed_hbm, down_ref, small_ref, mlp_gain_ref, tok_hbm, dmid_hbm, gain_ref = take(9)
    gq_in = None if inside else take(1)[0]
    tg_ref, rq_ref, rd_ref, dquery_ref, gate_ref, table_ref, again_ref, mgain_ref = take(8)
    dqkv_ref, wqkv_ref, normed_ref, tok_ref, dmid_ref = take(5)
    low, into, acc, gq_buf, tq, td, yq, zq, zd, xq, sy, sz, gains, gy, gz, gs = take(16)
    dn_send, dn_recv, z_send, z_recv, y_send, y_recv, x_send, x_recv, s_send, s_recv, g_send, g_recv = take(12)
    load_sem, dqkv_sem, tg_sem = take(3)
    gq_ref = gq_buf if inside else gq_in

    me = lax.axis_index("seq")
    f = lax.axis_index("fsdp")
    z, y = f // lo, f % lo
    peer = z * lo + 1 - y
    rows, dim = tok_ref.shape
    width = xq.shape[2] // 3
    bits, slots = seq_levels(seq)

    loads = [
        pltpu.make_async_copy(src, dst, load_sem.at[i])
        for i, (src, dst) in enumerate(
            (
                (wqkv_hbm, wqkv_ref),
                (down_ref, td),
                (normed_hbm, normed_ref),
                (tok_hbm, tok_ref),
                (dmid_hbm, dmid_ref),
            )
        )
    ]
    dqkv_loads = {
        j: pltpu.make_async_copy(
            dqkv_hbm.at[pl.ds(j * rows, rows)], dqkv_ref.at[pl.ds(j * rows, rows)], dqkv_sem.at[j]
        )
        for j in range(seq)
    }
    loads[0].start()
    for j in reversed(range(seq)):
        dqkv_loads[j].start()
    for c in loads[1:]:
        c.start()

    barrier = pltpu.get_barrier_semaphore()
    for k in range(1, seq):
        pl.semaphore_signal(barrier, inc=1, device_id={"seq": me ^ k}, device_id_type=MESH)
    for k in range(1, hi):
        pl.semaphore_signal(barrier, inc=1, device_id={"fsdp": lax.rem(z + k, hi) * lo + y}, device_id_type=MESH)
    pl.semaphore_signal(barrier, inc=1, device_id={"fsdp": peer}, device_id_type=MESH)
    pl.semaphore_wait(barrier, seq + hi - 1)

    def remote(src, dst, send, recv, axis, target):
        return pltpu.make_async_remote_copy(
            src_ref=src, dst_ref=dst, send_sem=send, recv_sem=recv, device_id={axis: target}, device_id_type=MESH
        )

    def dn_copy(bit, j):
        slot = slots[bit, j]
        return remote(low.at[j ^ bit], into.at[slot], dn_send.at[slot], dn_recv.at[slot], "seq", me ^ bit)

    start, combine, zsend, zrecv, drain_y, drain_z = line_reduce(
        hi,
        lo,
        lambda i, target: gq_ref.at[:, target],
        (tq, td),
        (yq,),
        (zq, zd),
        z_send,
        z_recv,
        y_send,
        y_recv,
    )

    def exchange(k, sending):
        return remote(
            tq.at[z, me ^ k] if sending else tq.at[z, me],
            xq.at[me] if sending else xq.at[me ^ k],
            x_send.at[k],
            x_recv.at[k],
            "seq",
            me ^ k if sending else me,
        )

    small_y = remote(small_ref, sy, s_send.at[0], s_recv.at[0], "fsdp", peer)
    small_y.start()
    loads[0].wait()
    if not inside:
        start(0)

    def dn_part(j):
        part = dot_t(dqkv_ref[j * rows : (j + 1) * rows], wqkv_ref[...])
        if j % 2:
            low[j] = part.astype(bf16)
            dn_copy(1, j ^ 1).start()
        else:
            acc[...] = part

    def dn_sum(j):
        for bit in bits:
            if j & bit:
                low[j] = acc[...].astype(bf16)
                dn_copy(bit, j ^ bit).start()
                break
            dn_copy(bit, j).wait_recv()
            acc[...] += into[slots[bit, j]].astype(f32)

    for j in reversed(range(2, seq)):
        dqkv_loads[j].wait()
        dn_part(j)
        if j == seq - 1:
            loads[1].wait()
            zsend(1, 0)
        if j % 2 == 0:
            dn_sum(j)
    for j in range(min(2, seq)):
        dqkv_loads[j].wait()
    loads[2].wait()
    if inside:
        for k in range(seq):
            cols = slice(k * (dim // seq), (k + 1) * (dim // seq))
            part = t_dot(normed_ref[:, cols], dqkv_ref[...]).astype(bf16)
            gq_buf[k] = part.reshape(gq_buf.shape[1:])
        start(0)
    def zstep(i, t):
        if t < hi - 1:
            zrecv(i, t)
            if t + 1 < hi - 1:
                zsend(i, t + 1)

    zstep(1, 0)
    small_y.wait_recv()
    sz[z] = small_ref[...] + sy[...]
    small_z = []
    for k in range(1, hi):
        small_z.append(
            remote(sz.at[z], sz.at[z], s_send.at[k], s_recv.at[k], "fsdp", lax.rem(z + k, hi) * lo + y)
        )
        small_z[-1].start()
    for j in reversed(range(min(2, seq))):
        dn_part(j)
    zstep(1, 1)
    for c in loads[3:]:
        c.wait()
    combine(0)
    zsend(0, 0)
    zstep(1, 2)
    for t in range(3, hi - 1):
        zstep(1, t)
    for bit in bits:
        dn_copy(bit, 0).wait_recv()
    gain = gain_ref[...]
    part = jnp.zeros((8, dim), f32)
    step = 128
    for r in range(0, rows, step):
        at = slice(r, r + step)
        dn = acc[at]
        for bit in bits:
            dn = dn + into[slots[bit, 0], at].astype(f32)
        x = tok_ref[at].astype(f32)
        rho = lax.rsqrt(jnp.mean(x * x, axis=-1, keepdims=True) + EPSILON)
        scaled = gain * dn
        mean = jnp.mean(x * scaled, axis=-1, keepdims=True)
        dmid_ref[at] += rho * scaled - x * (rho * rho * rho * mean)
        prod = dn * x * rho
        part += functools.reduce(jnp.add, [prod[n : n + 8] for n in range(0, step, 8)])
    tg_store = pltpu.make_async_copy(dmid_ref, tg_ref, tg_sem)
    tg_store.start()
    gains[0:8] = mlp_gain_ref[...]
    gains[8:16] = part
    gain_y = remote(gains, gy, g_send.at[0], g_recv.at[0], "fsdp", peer)
    gain_y.start()
    zrecv(0, 0)
    if hi > 2:
        zsend(0, 1)
    gain_y.wait_recv()
    gz[z] = gains[...] + gy[...]
    gain_z = []
    for k in range(1, hi):
        gain_z.append(
            remote(gz.at[z], gz.at[z], g_send.at[k], g_recv.at[k], "fsdp", lax.rem(z + k, hi) * lo + y)
        )
        gain_z[-1].start()
    for t in range(1, hi - 1):
        zrecv(0, t)
        if t + 1 < hi - 1:
            zsend(0, t + 1)
    for k in range(1, seq):
        exchange(k, True).start()
    for k in range(1, hi):
        source = lax.rem(z + hi - k, hi)
        remote(gz.at[source], gz.at[source], g_send.at[k], g_recv.at[k], "fsdp", f).wait_recv()
        remote(sz.at[source], sz.at[source], s_send.at[k], s_recv.at[k], "fsdp", f).wait_recv()
    gs[me] = functools.reduce(jnp.add, [gz[d] for d in range(hi)])
    gain_x = []
    for k in range(1, seq):
        gain_x.append(remote(gs.at[me], gs.at[me], g_send.at[hi + k], g_recv.at[hi + k], "seq", me ^ k))
        gain_x[-1].start()
    rd_ref[...] = td[z].astype(f32)
    total = functools.reduce(jnp.add, [sz[d] for d in range(hi)])
    cut, heads = dquery_ref.shape[0], gate_ref.shape[0]
    dquery_ref[...] = total[:cut]
    gate_ref[...] = total[cut : cut + heads]
    table_ref[...] = total[cut + heads : cut + 2 * heads, :BUCKETS]
    xq[me] = tq[z, me]
    for k in range(1, seq):
        exchange(k, False).wait_recv()
    write_parts(rq_ref, xq, seq, width)
    for k in range(1, seq):
        remote(gs.at[me ^ k], gs.at[me ^ k], g_send.at[hi + k], g_recv.at[hi + k], "seq", me).wait_recv()
    total = functools.reduce(jnp.add, [gs[k] for k in range(seq)])
    piece = again_ref.shape[1]
    total = pltpu.roll(total, lax.rem(dim - (me * hi * lo + f) * piece, dim), 1)[:, :DH]
    mgain_ref[...] = jnp.sum(total[0:8], axis=0, keepdims=True)[:, :piece]
    again_ref[...] = jnp.sum(total[8:16], axis=0, keepdims=True)[:, :piece]

    for bit in bits:
        for j in range(0, seq, 2 * bit):
            dn_copy(bit, j).wait_send()
    drain_y(0)
    for i in range(2):
        drain_z(i)
    for k in range(1, seq):
        exchange(k, True).wait_send()
    for c in [small_y, gain_y] + small_z + gain_z + gain_x:
        c.wait_send()
    tg_store.wait()


def finish(dqkv, wqkv, normed, down, small, mlp_gain, tok, dmid, gain, seq, fsdp):
    lo = 2
    hi = fsdp // lo
    rows, dim = tok.shape
    width3 = dqkv.shape[1]
    piece = dim // (seq * fsdp)
    inside = piece % 16 == 0
    heads = width3 // (3 * DH)
    vmem = pl.BlockSpec(memory_space=pltpu.VMEM)
    anywhere = pl.BlockSpec(memory_space=pl.ANY)
    dma = pltpu.SemaphoreType.DMA

    def buf(*shape):
        return pltpu.VMEM(shape, bf16)

    extra = []
    if not inside:
        extra.append(t_dot(normed, dqkv).astype(bf16).reshape(seq, fsdp, piece, width3))
    scratch = [
        buf(*dqkv.shape),
        buf(*wqkv.shape),
        buf(*normed.shape),
        buf(rows, dim),
        pltpu.VMEM((rows, dim), f32),
        buf(seq, rows, dim),
        buf(max(seq - 1, 1), rows, dim),
        pltpu.VMEM((rows, dim), f32),
        buf(seq, fsdp, piece, width3) if inside else buf(16, 128),
        buf(hi, seq, piece, width3),
        buf(*down.shape),
        buf(hi, seq, piece, width3),
        buf(2, max(hi - 1, 1), seq, piece, width3),
        buf(2, max(hi - 1, 1), *down.shape[1:]),
        buf(seq, piece, width3),
        pltpu.VMEM(small.shape, f32),
        pltpu.VMEM((hi,) + small.shape, f32),
        pltpu.VMEM((16, dim), f32),
        pltpu.VMEM((16, dim), f32),
        pltpu.VMEM((hi, 16, dim), f32),
        pltpu.VMEM((seq, 16, dim), f32),
        dma((seq,)),
        dma((seq,)),
        dma((2, 2, hi)),
        dma((2, 2, hi)),
        dma((1, hi)),
        dma((1, hi)),
        dma((seq,)),
        dma((seq,)),
        dma((hi,)),
        dma((hi,)),
        dma((hi + seq,)),
        dma((hi + seq,)),
        dma((5,)),
        dma((seq,)),
        dma,
    ]
    return pl.pallas_call(
        functools.partial(finish_kernel, seq, hi, lo, inside),
        out_shape=(
            jax.ShapeDtypeStruct((rows, dim), f32),
            jax.ShapeDtypeStruct((piece, seq * width3), f32),
            jax.ShapeDtypeStruct(down.shape[1:], f32),
            jax.ShapeDtypeStruct((heads * DH, DH), f32),
            jax.ShapeDtypeStruct((heads, DH), f32),
            jax.ShapeDtypeStruct((heads, BUCKETS), f32),
            jax.ShapeDtypeStruct((1, piece), f32),
            jax.ShapeDtypeStruct((1, piece), f32),
        ),
        in_specs=[anywhere] * 4 + [vmem] * 2 + [anywhere] * 2 + [vmem] * (1 + len(extra)),
        out_specs=(anywhere,) + (vmem,) * 7,
        scratch_shapes=scratch,
        compiler_params=pltpu.CompilerParams(
            collective_id=1, has_side_effects=True, vmem_limit_bytes=60 << 20
        ),
        name="finish",
    )(dqkv, wqkv, normed, down, small, mlp_gain, tok, dmid, gain, *extra)


GELU_P = 0.24
GELU_C = (
    0.08951261885080208,
    0.15562094398234086,
    -0.15437154502074169,
    0.6261054138112487,
    -0.6465313024138201,
    0.5547927291245551,
    -0.125128858665134,
)


def gelu_parts(x):
    size = jnp.abs(x)
    t = 1.0 / (1.0 + GELU_P * size)
    poly = GELU_C[-1] * t
    for c in GELU_C[-2::-1]:
        poly = (poly + c) * t
    bell = jnp.exp2(x * x * (-0.5 * LOG2E))
    tail = poly * bell
    cdf = jnp.where(x < 0.0, tail, 1.0 - tail)
    return x * cdf, cdf + x * bell * (1.0 / math.sqrt(2.0 * math.pi))


def mlp_kernel(seq, hi, lo, sub, length_ref, *refs):
    refs = list(refs)

    def take(count):
        taken = refs[:count]
        del refs[:count]
        return taken

    own_ref, others_ref, tok_ref, grads_ref, wo_hbm, wu_hbm, wd_hbm, gain_ref = take(8)
    mid_out, dmid_out, gsum_ref, db_ref, mo_ref, ug_out, dg_out = take(7)
    staged = len(ug_out.shape) == 4
    att_refs = [own_ref] + [others_ref.at[k] for k in range(1, seq)]
    att_buf, tok_buf, wo_ref, wu_ref, wd_ref, gm, nm, hid, dpre, low, into, acc, mid_ref, ug_ref, dg_ref = take(15)
    load_sem, w_sem, gm_sem, dn_send, dn_recv, db_send, db_recv, mo_sem, own_sem = take(9)
    if staged:
        tu, yu, y_send, y_recv = take(4)
    dbv = low.at[0]
    depth = att_buf.shape[0]

    me = lax.axis_index("seq")
    length = length_ref[0]
    dim = wo_ref.shape[0]
    width = dim // seq
    rows = tok_ref.shape[1]
    share = wu_ref.shape[1]
    subs = rows // sub
    bits, slots = seq_levels(seq)
    order = list(reversed(range(seq)))

    def chunk_loads(j):
        slot = j % depth
        copies = [
            pltpu.make_async_copy(att_refs[k].at[pl.ds(j * rows, rows)], att_buf.at[slot, k], load_sem.at[slot, k])
            for k in range(seq)
        ]
        copies.append(pltpu.make_async_copy(tok_ref.at[j], tok_buf.at[slot], load_sem.at[slot, seq]))
        return copies

    gm_loads = {
        j: pltpu.make_async_copy(grads_ref.at[j], gm.at[pl.ds(j * rows, rows)], gm_sem.at[j]) for j in order
    }
    weights = [
        pltpu.make_async_copy(src, dst, w_sem.at[i])
        for i, (src, dst) in enumerate(((wo_hbm, wo_ref), (wu_hbm, wu_ref), (wd_hbm, wd_ref)))
    ]
    for c in chunk_loads(order[0]) + weights[:1] + (chunk_loads(order[1]) if seq > 1 else []) + weights[1:]:
        c.start()
    for j in order:
        gm_loads[j].start()
    if depth == seq:
        for j in order[2:]:
            for c in chunk_loads(j):
                c.start()

    greet(bits, hi, lo)

    def dn_copy(bit, j, s):
        slot = slots[bit, j]
        at = pl.ds(pl.multiple_of(s * sub, sub), sub)
        return pltpu.make_async_remote_copy(
            src_ref=low.at[j ^ bit, at],
            dst_ref=into.at[slot, at],
            send_sem=dn_send.at[slot, s],
            recv_sem=dn_recv.at[slot, s],
            device_id={"seq": me ^ bit},
            device_id_type=MESH,
        )

    gain = gain_ref[...]

    def forward(j, s):
        slot = j % depth
        at = pl.ds(pl.multiple_of(s * sub, sub), sub)
        here = pl.ds(pl.multiple_of(j * rows + s * sub, sub), sub)
        position = (j ^ me) * rows + s * sub + lax.broadcasted_iota(jnp.int32, (sub, 1), 0)
        live = jnp.where(position < length, 1.0, 0.0)
        masked = (gm[here].astype(f32) * live).astype(bf16)
        gm[here] = masked
        mid = tok_buf[slot, at].astype(f32)
        for k in range(seq):
            own = pl.ds(pl.multiple_of((me ^ k) * width, width), width)
            mid = mid + dot(att_buf[slot, k, at], wo_ref[own])
        rho = lax.rsqrt(jnp.mean(mid * mid, axis=-1, keepdims=True) + EPSILON)
        normed = (mid * rho * gain).astype(bf16)
        nm[here] = normed
        if j == 0:
            mid_ref[at] = mid
        for c in range(0, share, 256):
            cols = slice(c, c + 256)
            value, slope = gelu_parts(dot(normed, wu_ref[:, cols]))
            hid[here, cols] = value.astype(bf16)
            dpre[here, cols] = (dot_t(masked, wd_ref[cols]) * slope).astype(bf16)
        part = dot_t(dpre[here], wu_ref[...])
        if j % 2:
            low[j, at] = part.astype(bf16)
            dn_copy(1, j ^ 1, s).start()
        else:
            acc[at] = part

    def settle(j, s):
        at = pl.ds(pl.multiple_of(s * sub, sub), sub)
        for bit in bits:
            if j & bit:
                low[j, at] = acc[at].astype(bf16)
                dn_copy(bit, j ^ bit, s).start()
                break
            dn_copy(bit, j, s).wait_recv()
            acc[at] += into[slots[bit, j], at].astype(f32)

    for c in weights:
        c.wait()
    for n in range(0, seq, 2):
        pair = order[n : n + 2]
        if n and depth < seq:
            for j in pair:
                for c in chunk_loads(j):
                    c.start()
        for j in pair:
            for c in chunk_loads(j):
                c.wait()
            gm_loads[j].wait()

        @pl.loop(0, subs)
        def _(s):
            for j in pair:
                forward(j, s)
            if pair[-1]:
                settle(pair[-1], s)

    stores = [pltpu.make_async_copy(mid_ref, mid_out, own_sem.at[1])]
    stores[0].start()
    half = seq // 2
    if staged:
        start, combine, _, _, drain_y, _ = line_reduce(
            hi,
            lo,
            lambda i, target: ug_ref.at[pl.ds(i * half, half), target],
            tuple(tu.at[:, pl.ds(i * half, half)] for i in range(2)),
            tuple(yu.at[:, pl.ds(i * half, half)] for i in range(2)),
            (),
            None,
            None,
            y_send,
            y_recv,
        )

    def up_half(i):
        for k in range(i * half, (i + 1) * half):
            cols = slice(k * (dim // seq), (k + 1) * (dim // seq))
            ug_ref[k] = t_dot(nm[:, cols], dpre[...]).astype(bf16).reshape(ug_ref.shape[1:])
        start(i)

    if staged:
        up_half(0)
    else:
        for c in range(0, dim, 256):
            ug_ref[c : c + 256] = t_dot(nm[:, c : c + 256], dpre[...]).astype(bf16)
        stores.append(pltpu.make_async_copy(ug_ref, ug_out, own_sem.at[2]))
        stores[-1].start()

    def db_copy(source, target, bit, s):
        at = pl.ds(s * sub, sub)
        return pltpu.make_async_remote_copy(
            src_ref=db_ref.at[source, at] if source else dbv.at[at],
            dst_ref=db_ref.at[target, at],
            send_sem=db_send.at[target, s],
            recv_sem=db_recv.at[target, s],
            device_id={"seq": me ^ bit},
            device_id_type=MESH,
        )

    sends = []
    high = [bit for bit in reversed(bits) if bit > 1]

    def send(source, target, bit, s):
        sends.append(db_copy(source, target, bit, s))
        sends[-1].start()

    step = 128
    part = jnp.zeros((8, dim), f32)
    for s in range(subs):
        for bit in bits:
            dn_copy(bit, 0, s).wait_recv()
        for r in range(s * sub, (s + 1) * sub, step):
            at = slice(r, r + step)
            dn = acc[at]
            for bit in bits:
                dn = dn + into[slots[bit, 0], at].astype(f32)
            mid = mid_ref[at]
            rho = lax.rsqrt(jnp.mean(mid * mid, axis=-1, keepdims=True) + EPSILON)
            scaled = gain * dn
            mean = jnp.mean(mid * scaled, axis=-1, keepdims=True)
            dmid = gm[at].astype(f32) + rho * scaled - mid * (rho * rho * rho * mean)
            acc[at] = dmid
            dbv[at] = dmid.astype(bf16)
            prod = dn * mid * rho
            part += functools.reduce(jnp.add, [prod[i : i + 8] for i in range(0, step, 8)])
        if high:
            send(0, high[0], high[0], s)
        if seq > 1:
            send(0, 1, 1, s)
    gsum_ref[...] = part
    stores.append(pltpu.make_async_copy(dbv, db_ref.at[0], own_sem.at[0]))
    stores[-1].start()
    stores.append(pltpu.make_async_copy(acc, dmid_out, own_sem.at[3]))
    stores[-1].start()
    if staged:
        up_half(1)
    for c in range(0, share, 256):
        dg_ref[c : c + 256] = t_dot(hid[:, c : c + 256], gm[...]).astype(bf16)
    stores.append(pltpu.make_async_copy(dg_ref, dg_out, own_sem.at[4]))
    stores[-1].start()
    for j in range(seq):
        at = slice(j * rows, (j + 1) * rows)
        nm[at] = dot(hid[at], wd_ref[...]).astype(bf16)
        stores.append(pltpu.make_async_copy(nm.at[pl.ds(j * rows, rows)], mo_ref.at[j], mo_sem.at[j]))
        stores[-1].start()
    have = [0]
    for n, bit in enumerate(high):
        if n:
            for j in have:
                for s in range(subs):
                    send(j, j ^ bit, bit, s)
        for j in have:
            for s in range(subs):
                db_copy(0, j ^ bit, bit, s).wait_recv()
                send(j ^ bit, j ^ bit ^ 1, 1, s)
        have += [j ^ bit for j in have]
    if seq > 1:
        for j in have:
            for s in range(subs):
                db_copy(0, j ^ 1, 1, s).wait_recv()
    if staged:
        for i in range(2):
            combine(i)
        stores.append(pltpu.make_async_copy(tu, ug_out, own_sem.at[2]))
        stores[-1].start()
        for i in range(2):
            drain_y(i)
    for c in sends:
        c.wait_send()
    for c in stores:
        c.wait()
    for bit in bits:
        for j in range(0, seq, 2 * bit):
            for s in range(subs):
                dn_copy(bit, j, s).wait_send()


def mlp(length, own, others, tok, grads, wo, wu, wd, gain, fsdp):
    seq, rows, dim = tok.shape
    share = wu.shape[1]
    lo = 2
    hi = fsdp // lo
    piece = dim // (seq * fsdp)
    staged = piece % 16 == 0
    up_shape = (hi, seq, piece, share) if staged else (dim, share)
    sub = 256
    depth = seq if seq <= 4 else 2
    anywhere = pl.BlockSpec(memory_space=pl.ANY)
    vmem = pl.BlockSpec(memory_space=pltpu.VMEM)
    dma = pltpu.SemaphoreType.DMA

    def buf(*shape):
        return pltpu.VMEM(shape, bf16)

    return pl.pallas_call(
        functools.partial(mlp_kernel, seq, hi, lo, sub),
        out_shape=(
            jax.ShapeDtypeStruct((rows, dim), f32),
            jax.ShapeDtypeStruct((rows, dim), f32),
            jax.ShapeDtypeStruct((8, dim), f32),
            jax.ShapeDtypeStruct((seq, rows, dim), bf16),
            jax.ShapeDtypeStruct((seq, rows, dim), bf16),
            jax.ShapeDtypeStruct(up_shape, bf16),
            jax.ShapeDtypeStruct((share, dim), bf16),
        ),
        in_specs=[pl.BlockSpec(memory_space=pltpu.SMEM)] + [anywhere] * 7 + [vmem],
        out_specs=(anywhere, anywhere, vmem, anywhere, anywhere, anywhere, anywhere),
        scratch_shapes=[
            buf(depth, seq, rows, dim // seq),
            buf(depth, rows, dim),
            buf(dim, dim),
            buf(dim, share),
            buf(share, dim),
            buf(seq * rows, dim),
            buf(seq * rows, dim),
            buf(seq * rows, share),
            buf(seq * rows, share),
            buf(seq, rows, dim),
            buf(max(seq - 1, 1), rows, dim),
            pltpu.VMEM((rows, dim), f32),
            pltpu.VMEM((rows, dim), f32),
            buf(seq, fsdp, piece, share) if staged else buf(dim, share),
            buf(share, dim),
            dma((depth, seq + 1)),
            dma((3,)),
            dma((seq,)),
            dma((seq, rows // sub)),
            dma((seq, rows // sub)),
            dma((seq, rows // sub)),
            dma((seq, rows // sub)),
            dma((seq,)),
            dma((5,)),
        ]
        + ([buf(*up_shape), buf(*up_shape), dma((2, hi)), dma((2, hi))] if staged else []),
        compiler_params=pltpu.CompilerParams(collective_id=2, has_side_effects=True, vmem_limit_bytes=62 << 20),
        cost_estimate=pl.CostEstimate(
            flops=2 * rows * seq * dim * (dim + 6 * share), bytes_accessed=32 << 20, transcendentals=rows * seq * share
        ),
        name="mlp",
    )(length, own, others, tok, grads, wo, wu, wd, gain)


def emit_kernel(*refs):
    count = len(refs) // 3
    ins, outs, bufs = refs[:count], refs[count : 2 * count], refs[2 * count : 3 * count]
    sems = refs[3 * count]
    reads = [pltpu.make_async_copy(a, b, sems.at[0, i]) for i, (a, b) in enumerate(zip(ins, bufs))]
    writes = [pltpu.make_async_copy(a, b, sems.at[1, i]) for i, (a, b) in enumerate(zip(bufs, outs))]
    for c in reads:
        c.start()
    for read, write in zip(reads, writes):
        read.wait()
        write.start()
    for c in writes:
        c.wait()


def emit(*values):
    count = len(values)
    anywhere = pl.BlockSpec(memory_space=pl.ANY)
    return pl.pallas_call(
        emit_kernel,
        out_shape=tuple(jax.ShapeDtypeStruct(v.shape, v.dtype) for v in values),
        in_specs=[anywhere] * count,
        out_specs=(anywhere,) * count,
        scratch_shapes=[pltpu.VMEM(v.shape, v.dtype) for v in values] + [pltpu.SemaphoreType.DMA((2, count))],
        compiler_params=pltpu.CompilerParams(vmem_limit_bytes=62 << 20),
        name="emit",
    )(*values)


def body(
    tokens,
    lengths,
    state_init,
    w_qkv,
    w_out,
    w_up,
    w_down,
    norm_attn,
    norm_mlp,
    rel_bias,
    state_query,
    gate_bias,
    out_grad,
    state_grad,
):
    seq_count = lax.axis_size("seq")
    fsdp_count = lax.axis_size("fsdp")
    seq_at = lax.axis_index("seq")
    heads = H // seq_count
    width = heads * DH
    tok_rows, dim = tokens.shape[1:]
    rows = tok_rows * seq_count
    hidden_all = w_up.shape[1]
    share = hidden_all // (seq_count * fsdp_count)

    piece = dim // (seq_count * fsdp_count)
    all_tokens, all_grad, qkv_w, gain_attn, gain_mlp, own_out, up_w, normed, qkv = gather_start(
        tokens[0],
        out_grad[0],
        w_qkv,
        norm_attn.reshape(1, -1),
        norm_mlp.reshape(1, -1),
        w_out.reshape(2, w_out.shape[0] // 2, dim),
        w_up,
        seq_count,
        fsdp_count,
    )
    qkv_w = qkv_w.reshape(dim, 3 * width)
    up_w = up_w.reshape(dim, hidden_all // seq_count)
    own_down = lax.dynamic_slice_in_dim(w_down, seq_at * share, share, axis=0)

    bias = bias_vector(rel_bias)
    forget = jax.nn.sigmoid(gate_bias)
    forget_row = forget.reshape(1, width)

    attended, others, out_w, down_w, final_memory, mem, upd, lse, slse = attend(
        qkv,
        state_init[0],
        lengths,
        state_query,
        forget_row,
        bias,
        own_out,
        own_down,
        heads,
        seq_count,
        fsdp_count,
    )
    out_w = out_w.reshape(dim, dim)
    down_w = down_w.reshape(fsdp_count * share, dim)
    mid_here, dmid, mlp_gain_grad, dbranch, mlp_parts, up_grad, down_grad = mlp(
        lengths, attended, others, all_tokens, all_grad, out_w, up_w, down_w, gain_mlp, fsdp_count
    )
    span = fsdp_count // seq_count
    if up_grad.ndim == 2:
        up_grad = up_grad.reshape(seq_count, fsdp_count, piece, hidden_all // seq_count)
    dqkv, small, up_part, down_total, out_part, output = attend_back(
        qkv,
        dbranch.reshape(rows, dim),
        out_w,
        attended,
        mem,
        upd,
        lse,
        slse,
        state_grad[0],
        lengths,
        state_query,
        forget_row,
        bias,
        up_grad,
        down_grad.reshape(seq_count, span * share, dim),
        mlp_parts,
        mid_here,
        seq_count,
        fsdp_count,
    )
    tokens_grad, qkv_part, down_part, dquery, grad_gate, grad_table, attn_gain_grad, mlp_gain_grad = finish(
        dqkv,
        qkv_w,
        normed,
        down_total,
        small,
        mlp_gain_grad,
        tokens[0],
        dmid,
        gain_attn,
        seq_count,
        fsdp_count,
    )
    big = (output, final_memory, tokens_grad, qkv_part, out_part, up_part, down_part)
    little = (dquery, grad_gate, grad_table, attn_gain_grad, mlp_gain_grad)
    output, final_memory, tokens_grad, qkv_part, out_part, up_part, down_part, *little = emit(*big, *little)
    dquery, grad_gate, grad_table, attn_gain_grad, mlp_gain_grad = little
    output = output[None]
    tokens_grad = tokens_grad[None]
    if up_part.ndim == 3:
        up_part = up_part.reshape(seq_count, piece, fsdp_count, share)
        up_part = jnp.transpose(up_part, (1, 2, 0, 3)).reshape(piece, hidden_all)
    dquery = dquery.reshape(heads, DH, DH)
    attn_gain_grad = attn_gain_grad.reshape(piece)
    mlp_gain_grad = mlp_gain_grad.reshape(piece)
    return (
        output,
        final_memory[None],
        tokens_grad,
        qkv_part,
        out_part,
        up_part,
        down_part,
        attn_gain_grad,
        mlp_gain_grad,
        grad_table,
        dquery,
        grad_gate,
    )


def solution(mesh):
    placed = (
        P("fsdp", "seq", None),
        P("fsdp"),
        P("fsdp", None, "seq"),
        P("fsdp", None),
        P("fsdp", None),
        P("fsdp", None),
        P("fsdp", None),
        P("fsdp"),
        P("fsdp"),
        P("seq", None),
        P("seq", None, None),
        P("seq", None),
        P("fsdp", "seq", None),
        P("fsdp", None, "seq"),
    )
    return jax.shard_map(
        body,
        mesh=mesh,
        in_specs=placed,
        out_specs=(
            P("fsdp", "seq", None),
            P("fsdp", None, "seq"),
            P("fsdp", "seq", None),
            P(("seq", "fsdp"), None),
            P(("seq", "fsdp"), None),
            P(("seq", "fsdp"), None),
            P(("seq", "fsdp"), None),
            P(("seq", "fsdp")),
            P(("seq", "fsdp")),
            P("seq", None),
            P("seq", None, None),
            P("seq", None),
        ),
        check_vma=False,
    )
```

```python
import functools
import math

import jax
import jax.numpy as jnp
import numpy as np
from jax import lax
from jax.experimental import pallas as pl
from jax.experimental.pallas import tpu as pltpu
from jax.sharding import PartitionSpec as P

H = 8
DH = 128
BLOCK = 512
STATE_VECTORS = 512
QTILE = 256
SPAN = BLOCK + QTILE

EPSILON = 1e-06
BUCKET_EDGES = (19, 21, 24, 27, 31, 35, 40, 46, 52, 59, 67, 77, 87, 99, 113)
BUCKETS = 32
LOG2E = math.log2(math.e)
SCALE = DH ** (-0.5)
NEAR = 384

f32 = jnp.float32
bf16 = jnp.bfloat16
MESH = pl.DeviceIdType.MESH


def bucket_of(distance):
    return np.minimum(distance, 16) + (distance[..., None] >= np.array(BUCKET_EDGES)).sum(-1)


def tile_distance():
    rows = np.arange(QTILE)[:, None]
    cols = np.arange(SPAN)[None, :]
    return rows + BLOCK - cols


def bias_vector(table):
    distance = BLOCK - np.arange(2 * BLOCK)
    inside = (distance >= 0) & (distance < BLOCK)
    bucket = np.where(inside, bucket_of(np.clip(distance, 0, BLOCK)), BUCKETS)
    member = jnp.asarray((np.arange(BUCKETS)[:, None] == bucket[None]).astype(np.float32))
    total = jnp.dot(table, member, precision=lax.Precision.HIGHEST, preferred_element_type=f32)
    return jnp.where(jnp.asarray(inside)[None], total * LOG2E, -jnp.inf)


def tile_bias(vector_ref, head):
    wide = jnp.broadcast_to(vector_ref[head : head + 1, :], (QTILE, 2 * BLOCK))
    return pltpu.roll(wide, 0, 1, stride=1, stride_axis=0)[:, :SPAN]


def dot(a, b):
    return jnp.dot(a, b, preferred_element_type=f32)


def dot_t(a, b):
    return lax.dot_general(a, b, (((1,), (1,)), ((), ())), preferred_element_type=f32)


def t_dot(a, b):
    return lax.dot_general(a, b, (((0,), (0,)), ((), ())), preferred_element_type=f32)


def to_row(column):
    wide = jnp.broadcast_to(column, (column.shape[0], 128))
    return wide.T[0:1, :]


def context_pieces(tile):
    start = tile * QTILE
    pieces = []
    if start < BLOCK:
        pieces.append((0, start, BLOCK, 0))
    pieces.append((1, 0, start + QTILE, BLOCK - start))
    return pieces


def softmax_parts(scores):
    top = functools.reduce(jnp.maximum, [jnp.max(s, axis=-1, keepdims=True) for s in scores])
    raised = [jnp.exp2(s - top) for s in scores]
    total = functools.reduce(jnp.add, [jnp.sum(e, axis=-1, keepdims=True) for e in raised])
    return raised, total, top + jnp.log2(total)


def line_gather(hi, lo, slot, own, z_send, z_recv, y_send, y_recv):
    f = lax.axis_index("fsdp")
    z, y = f // lo, f % lo

    def copy(i, origin, target, send, recv, first=False):
        ref = slot(i, origin)
        return pltpu.make_async_remote_copy(
            src_ref=own(i) if first else ref,
            dst_ref=ref,
            send_sem=send,
            recv_sem=recv,
            device_id={"fsdp": target},
            device_id_type=MESH,
        )

    def right(i, t):
        return copy(i, (z - t) * lo + y, (z + 1) * lo + y, z_send.at[i, 0, t], z_recv.at[i, 0, t], t == 0)

    def left(i, t):
        return copy(i, (z + t) * lo + y, (z - 1) * lo + y, z_send.at[i, 1, t], z_recv.at[i, 1, t], t == 0)

    def across(i, d):
        return copy(
            i, (z + d) * lo + y, z * lo + 1 - y, y_send.at[i, d + hi - 1], y_recv.at[i, d + hi - 1], d == 0
        )

    def start(i):
        pl.when(z + 1 < hi)(lambda: right(i, 0).start())
        pl.when(z >= 1)(lambda: left(i, 0).start())
        across(i, 0).start()

    def step(i, t):
        @pl.when(z - 1 - t >= 0)
        def _():
            copy(i, (z - 1 - t) * lo + y, f, z_send.at[i, 0, t], z_recv.at[i, 0, t]).wait_recv()
            if t + 1 < hi - 1:
                pl.when(z + 1 < hi)(lambda: right(i, t + 1).start())
            across(i, -1 - t).start()

        @pl.when(z + 1 + t < hi)
        def _():
            copy(i, (z + 1 + t) * lo + y, f, z_send.at[i, 1, t], z_recv.at[i, 1, t]).wait_recv()
            if t + 1 < hi - 1:
                pl.when(z >= 1)(lambda: left(i, t + 1).start())
            across(i, 1 + t).start()

    def arrive(i):
        for d in range(1 - hi, hi):

            @pl.when((z + d >= 0) & (z + d < hi))
            def _():
                copy(
                    i, (z + d) * lo + 1 - y, f, y_send.at[i, d + hi - 1], y_recv.at[i, d + hi - 1]
                ).wait_recv()

    def drain(i):
        for d in range(1 - hi, hi):

            @pl.when((z + d >= 0) & (z + d < hi))
            def _():
                across(i, d).wait_send()

        for t in range(hi - 1):

            @pl.when((z + 1 < hi) & (z - t >= 0))
            def _():
                right(i, t).wait_send()

            @pl.when((z >= 1) & (z + t < hi))
            def _():
                left(i, t).wait_send()

    return start, step, arrive, drain


def line_sems(count, hi):
    dma = pltpu.SemaphoreType.DMA
    return [dma((count, 2, hi)), dma((count, 2, hi)), dma((count, 2 * hi)), dma((count, 2 * hi))]


def greet(seq_targets, hi, lo):
    me = lax.axis_index("seq")
    f = lax.axis_index("fsdp")
    z, y = f // lo, f % lo
    barrier = pltpu.get_barrier_semaphore()
    for k in seq_targets:
        pl.semaphore_signal(barrier, inc=1, device_id={"seq": me ^ k}, device_id_type=MESH)
    near = (lax.rem(z + 1, hi) * lo + y, lax.rem(z + hi - 1, hi) * lo + y, z * lo + 1 - y)
    for target in near:
        pl.semaphore_signal(barrier, inc=1, device_id={"fsdp": target}, device_id_type=MESH)
    pl.semaphore_wait(barrier, len(seq_targets) + len(near))


def attend_kernel(
    heads,
    seq,
    hi,
    lo,
    length_ref,
    qkv_ref,
    init_ref,
    query_ref,
    gate_ref,
    vector_ref,
    own_out_ref,
    down_hbm,
    att_out,
    others_ref,
    outs_ref,
    downs_ref,
    final_ref,
    mem_out,
    upd_out,
    lse_ref,
    slse_ref,
    memory_ref,
    bias_ref,
    att_ref,
    mem_ref,
    upd_ref,
    own_down_ref,
    store_sem,
    own_sem,
    att_send,
    att_recv,
    out_send,
    out_recv,
    z_send,
    z_recv,
    y_send,
    y_recv,
):
    me = lax.axis_index("seq")
    f = lax.axis_index("fsdp")
    length = length_ref[0]
    width = heads * DH
    scale2 = SCALE * LOG2E
    blocks = seq
    bits = [1 << i for i in range(seq.bit_length() - 1)]
    held = own_down_ref.shape[0]
    down_load = pltpu.make_async_copy(
        down_hbm.at[pl.ds(pl.multiple_of(me * held, held), held)], own_down_ref, own_sem.at[2]
    )
    down_load.start()
    greet(bits, hi, lo)
    down_load.wait()

    own_copies = [
        pltpu.make_async_copy(own_down_ref, downs_ref.at[f], own_sem.at[0]),
        pltpu.make_async_copy(own_out_ref, outs_ref.at[:, me % 2], own_sem.at[1]),
    ]
    for c in own_copies:
        c.start()

    def lowest(k):
        return k & -k

    def out_copy(sending):
        half = me % 2 if sending else 1 - me % 2
        return pltpu.make_async_remote_copy(
            src_ref=own_out_ref,
            dst_ref=outs_ref.at[:, half],
            send_sem=out_send,
            recv_sem=out_recv,
            device_id={"seq": me ^ 1},
            device_id_type=MESH,
        )

    def att_copy(k, b):
        bit = lowest(k)
        came = k ^ bit
        here = pl.ds(pl.multiple_of((b ^ me) * BLOCK, BLOCK), BLOCK)
        there = pl.ds(pl.multiple_of((b ^ me ^ bit) * BLOCK, BLOCK), BLOCK)
        src = others_ref.at[came, here] if came else att_ref.at[here]
        return pltpu.make_async_remote_copy(
            src_ref=src,
            dst_ref=others_ref.at[k, there],
            send_sem=att_send.at[k, b],
            recv_sem=att_recv.at[k, b],
            device_id={"seq": me ^ bit},
            device_id_type=MESH,
        )

    def att_arrival(k, b):
        here = pl.ds(pl.multiple_of((b ^ me) * BLOCK, BLOCK), BLOCK)
        return pltpu.make_async_remote_copy(
            src_ref=others_ref.at[k, here],
            dst_ref=others_ref.at[k, here],
            send_sem=att_send.at[k, b],
            recv_sem=att_recv.at[k, b],
            device_id={"seq": me},
            device_id_type=MESH,
        )

    passing = sorted([k for k in range(2, seq, 2)], key=lambda k: (bin(k).count("1"), -k))

    def onward(k, send):
        for bit in reversed(bits):
            if bit < lowest(k):
                send(k | bit)

    start, step, arrive, drain = line_gather(
        hi, lo, lambda i, origin: downs_ref.at[origin], lambda i: own_down_ref, z_send, z_recv, y_send, y_recv
    )

    start(0)
    out_copy(True).start()
    memory_ref[...] = init_ref[...].astype(f32)
    for head in range(heads):
        bias_ref[head] = tile_bias(vector_ref, head)

    def block_stores(block):
        at = pl.ds(pl.multiple_of((block ^ me) * BLOCK, BLOCK), BLOCK)
        pairs = (
            (att_ref.at[at], att_out.at[at]),
            (mem_ref.at[block], mem_out.at[block]),
            (upd_ref.at[block], upd_out.at[block]),
        )
        return [pltpu.make_async_copy(a, b, store_sem.at[i, block]) for i, (a, b) in enumerate(pairs)]

    @pl.loop(0, blocks)
    def _(block):
        cur_at = pl.multiple_of((block ^ me) * BLOCK, BLOCK)
        prev_at = pl.multiple_of((jnp.maximum(block - 1, 0) ^ me) * BLOCK, BLOCK)
        cur_ref = qkv_ref.at[pl.ds(cur_at, BLOCK)]
        prev_ref = qkv_ref.at[pl.ds(prev_at, BLOCK)]
        for t in range(min(hi - 1, blocks - 1)):
            pl.when(block == t + 1)(lambda t=t: step(0, t))

        live_block = block * BLOCK < length
        for head in range(heads):
            own = slice(head * DH, (head + 1) * DH)
            memory = memory_ref[:, own]
            low = memory.astype(bf16)
            mem_ref[block, :, own] = memory
            refs = (prev_ref, cur_ref)
            key_cols = slice(width + head * DH, width + (head + 1) * DH)
            value_cols = slice(2 * width + head * DH, 2 * width + (head + 1) * DH)
            for tile in range(BLOCK // QTILE):
                rows = slice(tile * QTILE, (tile + 1) * QTILE)
                query = cur_ref[rows, own]
                scores, values = [], []
                for which, at, end, col in context_pieces(tile):
                    s = dot_t(query, refs[which][at:end, key_cols])
                    position = (block - 1 + which) * BLOCK + at + lax.broadcasted_iota(jnp.int32, (1, end - at), 1)
                    live = (position >= 0) & (position < length)
                    s = s * scale2 + bias_ref[head, :, col : col + end - at]
                    scores.append(jnp.where(live, s, -jnp.inf))
                    values.append(refs[which][at:end, value_cols])
                scores.append(dot_t(query, low) * scale2)
                values.append(low)
                raised, total, lse = softmax_parts(scores)
                out = functools.reduce(jnp.add, [dot(e.astype(bf16), v) for e, v in zip(raised, values)])
                att_ref[pl.ds(cur_at + tile * QTILE, QTILE), own] = (out / total).astype(bf16)
                lse_ref[head : head + 1, pl.ds(pl.multiple_of(block * BLOCK, BLOCK) + tile * QTILE, QTILE)] = to_row(lse)
            own_key = cur_ref[:, key_cols]
            own_value = cur_ref[:, value_cols]
            squeries = dot(low, query_ref[head]).astype(bf16)
            position = block * BLOCK + lax.broadcasted_iota(jnp.int32, (1, BLOCK), 1)
            for tile in range(STATE_VECTORS // QTILE):
                rows = slice(tile * QTILE, (tile + 1) * QTILE)
                squery = squeries[rows]
                scores = [
                    dot_t(squery, low) * scale2,
                    jnp.where(position < length, dot_t(squery, own_key) * scale2, -jnp.inf),
                ]
                raised, total, lse = softmax_parts(scores)
                update = dot(raised[0].astype(bf16), low) + dot(raised[1].astype(bf16), own_value)
                update = update / total
                upd_ref[block, rows, own] = update
                slse_ref[head : head + 1, pl.ds(pl.multiple_of(block * BLOCK, BLOCK) + tile * QTILE, QTILE)] = to_row(
                    lse
                )
                forget = jax.nn.sigmoid(gate_ref[head : head + 1, :])
                old = memory[rows]
                memory_ref[rows, own] = jnp.where(live_block, forget * old + (1.0 - forget) * update, old)

        for bit in reversed(bits):
            att_copy(bit, block).start()
        for c in block_stores(block):
            c.start()

        @pl.when(block >= 1)
        def _():
            for k in passing:
                att_arrival(k, block - 1).wait_recv()
                onward(k, lambda target: att_copy(target, block - 1).start())

    final_ref[...] = memory_ref[...]
    for t in range(min(hi - 1, blocks - 1), hi - 1):
        step(0, t)
    for k in passing:
        att_arrival(k, blocks - 1).wait_recv()
        onward(k, lambda target: att_copy(target, blocks - 1).start())
    arrive(0)
    out_copy(False).wait_recv()
    for k in range(1, seq, 2):
        for b in range(blocks):
            att_arrival(k, b).wait_recv()
    for c in own_copies:
        c.wait()
    drain(0)
    for b in range(blocks):
        for c in block_stores(b):
            c.wait()
    out_copy(True).wait_send()
    for k in range(1, seq):
        for b in range(blocks):
            att_copy(k, b).wait_send()


def attend(qkv, init, length, state_query, gate, bias, own_out, w_down, heads, seq, fsdp):
    rows, width3 = qkv.shape
    width = heads * DH
    blocks = rows // BLOCK
    lo = 2
    hi = fsdp // lo
    dim = w_down.shape[1]
    held = w_down.shape[0] // seq
    anywhere = pl.BlockSpec(memory_space=pl.ANY)
    vmem = pl.BlockSpec(memory_space=pltpu.VMEM)
    dma = pltpu.SemaphoreType.DMA
    return pl.pallas_call(
        functools.partial(attend_kernel, heads, seq, hi, lo),
        out_shape=(
            jax.ShapeDtypeStruct((rows, width), bf16),
            jax.ShapeDtypeStruct((seq, rows, width), bf16),
            jax.ShapeDtypeStruct((fsdp, 2) + own_out.shape[1:], bf16),
            jax.ShapeDtypeStruct((fsdp, held, dim), bf16),
            jax.ShapeDtypeStruct((STATE_VECTORS, width), f32),
            jax.ShapeDtypeStruct((blocks, STATE_VECTORS, width), f32),
            jax.ShapeDtypeStruct((blocks, STATE_VECTORS, width), f32),
            jax.ShapeDtypeStruct((heads, rows), f32),
            jax.ShapeDtypeStruct((heads, blocks * STATE_VECTORS), f32),
        ),
        in_specs=[pl.BlockSpec(memory_space=pltpu.SMEM)] + [vmem] * 6 + [anywhere],
        out_specs=(anywhere, anywhere, anywhere, anywhere, vmem, anywhere, anywhere, vmem, vmem),
        scratch_shapes=[
            pltpu.VMEM((STATE_VECTORS, width), f32),
            pltpu.VMEM((heads, QTILE, SPAN), f32),
            pltpu.VMEM((rows, width), bf16),
            pltpu.VMEM((blocks, STATE_VECTORS, width), f32),
            pltpu.VMEM((blocks, STATE_VECTORS, width), f32),
            pltpu.VMEM((held, dim), bf16),
            dma((3, blocks)),
            dma((3,)),
            dma((seq, blocks)),
            dma((seq, blocks)),
            dma,
            dma,
        ]
        + line_sems(1, hi),
        compiler_params=pltpu.CompilerParams(collective_id=3, has_side_effects=True, vmem_limit_bytes=62 << 20),
        cost_estimate=pl.CostEstimate(
            flops=blocks * heads * 512 * 2400 * 128 * 4, bytes_accessed=16 << 20, transcendentals=10 << 20
        ),
        name="attend",
    )(length, qkv, init, state_query, gate, bias, own_out, w_down)


def line_reduce(hi, lo, block, total, from_y, from_z, z_send, z_recv, y_send, y_recv, loads=None):
    loads = loads or {}
    f = lax.axis_index("fsdp")
    z, y = f // lo, f % lo

    def remote(src, dst, send, recv, target):
        return pltpu.make_async_remote_copy(
            src_ref=src, dst_ref=dst, send_sem=send, recv_sem=recv, device_id={"fsdp": target}, device_id_type=MESH
        )

    def across(i, d):
        return remote(
            block(i, d * lo + 1 - y), from_y[i].at[d], y_send.at[i, d], y_recv.at[i, d], z * lo + 1 - y
        )

    def start(i):
        for d in range(hi):
            across(i, d).start()

    def combine(i):
        for d in range(hi):
            across(i, d).wait_recv()
            if i in loads:
                loads[i][d].wait()
                own = total[i].at[d]
            else:
                own = block(i, d * lo + y)
            total[i][d] = (own[...].astype(f32) + from_y[i][d].astype(f32)).astype(bf16)

    def hop(i, side, t, at, target):
        return remote(
            total[i].at[jnp.clip(at, 0, hi - 1)],
            from_z[i].at[side, t],
            z_send.at[i, side, t],
            z_recv.at[i, side, t],
            target,
        )

    def sending(t):
        d = t - (hi - 1 - z)
        m = hi - 1 - (t - z)
        return ((0, d, (d >= 0) & (d < z), z - 1), (1, m, (m > z) & (m < hi), z + 1))

    def zsend(i, t):
        for side, at, cond, target in sending(t):
            pl.when(cond)(lambda: hop(i, side, t, at, target * lo + y).start())

    def zrecv(i, t):
        d = t - (hi - 2 - z)
        m = hi - 1 - (t - (z - 1))
        for side, at, cond in ((0, d, (z + 1 < hi) & (d >= 0)), (1, m, (z > 0) & (m < hi))):

            @pl.when(cond)
            def _():
                hop(i, side, t, at, f).wait_recv()
                slot = jnp.clip(at, 0, hi - 1)
                total[i][slot] = (total[i][slot].astype(f32) + from_z[i][side, t].astype(f32)).astype(bf16)

    def drain_y(i):
        for d in range(hi):
            across(i, d).wait_send()

    def drain_z(i):
        for t in range(hi - 1):
            for side, at, cond, target in sending(t):
                pl.when(cond)(lambda: hop(i, side, t, at, f).wait_send())

    return start, combine, zsend, zrecv, drain_y, drain_z


def seq_levels(seq):
    bits = [1 << i for i in range(seq.bit_length() - 1)]
    slots = {}
    for bit in bits:
        for j in range(0, seq, 2 * bit):
            slots[bit, j] = len(slots)
    return bits, slots


def diagonal_sums(tile):
    rows, lanes = tile.shape
    wide = jnp.concatenate([tile, jnp.zeros((rows, lanes), f32)], axis=1)
    row = lax.broadcasted_iota(jnp.int32, wide.shape, 0)
    bit = 1
    while bit < rows:
        wide = jnp.where((row & bit) != 0, pltpu.roll(wide, 2 * lanes - bit, 1), wide)
        bit *= 2
    return jnp.sum(wide, axis=0, keepdims=True)


def attend_back_kernel(heads, seq, hi, lo, inside, length_ref, *refs):
    refs = list(refs)

    def take(count):
        taken = refs[:count]
        del refs[:count]
        return taken

    qkv_hbm, db_hbm, wout_hbm, att_hbm, mem_hbm, upd_hbm, lse_ref, slse_ref = take(8)
    sgrad_ref, query_ref, gate_ref, vector_ref, up_ref, down_ref, mo_ref, mid_hbm = take(8)
    ow_in = None if inside else take(1)[0]
    dqkv_out, small_ref, upart_ref, dtotal_ref, opart_ref, output_ref = take(6)
    qkv_ref, db_ref, att_ref, mem_ref, upd_ref, mid_ref, dqkv_ref, wout_ref = take(8)
    dmem_ref, dnext_ref, dctx_ref, bias_ref, near_ref, far_ref, dout_ref, ow_buf = take(8)
    moved, to, tu, yo, yu, yd, zo, zu, xu, mo_low, mo_in = take(11)
    z_send, z_recv, y_send, y_recv, m_send, m_recv, e_send, e_recv, x_send, x_recv = take(10)
    load_sem, block_sem, up_sem, mo_sem, out_sem = take(5)
    ow_ref = ow_buf if inside else ow_in

    me = lax.axis_index("seq")
    f = lax.axis_index("fsdp")
    z, y = f // lo, f % lo
    blocks = seq
    length = length_ref[0]
    width = heads * DH
    scale2 = SCALE * LOG2E
    tok_rows = mid_ref.shape[0]
    share = dtotal_ref.shape[1]
    bits, slots = seq_levels(seq)

    def chunk_at(block):
        return pl.ds(pl.multiple_of((block ^ me) * BLOCK, BLOCK), BLOCK)

    def block_loads(block):
        at = chunk_at(block)
        pairs = (
            (qkv_hbm.at[at], qkv_ref.at[at]),
            (mem_hbm.at[block], mem_ref.at[block]),
            (upd_hbm.at[block], upd_ref.at[block]),
        )
        return [pltpu.make_async_copy(a, b, block_sem.at[i, block]) for i, (a, b) in enumerate(pairs)]

    loads = [
        pltpu.make_async_copy(att_hbm, att_ref, load_sem.at[0]),
        pltpu.make_async_copy(db_hbm, db_ref, load_sem.at[1]),
        pltpu.make_async_copy(down_ref.at[me], moved.at[me], load_sem.at[2]),
        pltpu.make_async_copy(mid_hbm, mid_ref, load_sem.at[3]),
        pltpu.make_async_copy(
            wout_hbm.at[pl.ds(pl.multiple_of(me * width, width), width)], wout_ref, load_sem.at[4]
        ),
    ]
    up_loads = [
        pltpu.make_async_copy(up_ref.at[d] if inside else up_ref.at[:, d * lo + y], tu.at[d], up_sem.at[d])
        for d in range(hi)
    ]
    mo_loads = [pltpu.make_async_copy(mo_ref.at[j], mo_low.at[j // 2], mo_sem.at[j // 2]) for j in range(0, seq, 2)]
    for c in up_loads + loads[:2] + loads[4:] + block_loads(blocks - 1) + mo_loads:
        c.start()
    for b in reversed(range(blocks - 1)):
        for c in block_loads(b):
            c.start()
    for c in loads[2:4]:
        c.start()
    greet(list(range(1, seq)), hi, lo)

    def mo_copy(bit, j):
        slot = slots[bit, j]
        return pltpu.make_async_remote_copy(
            src_ref=mo_ref.at[j ^ bit] if bit == 1 else mo_low.at[(j ^ bit) // 2],
            dst_ref=mo_in.at[slot],
            send_sem=m_send.at[slot],
            recv_sem=m_recv.at[slot],
            device_id={"seq": me ^ bit},
            device_id_type=MESH,
        )

    def move_copy(k):
        return pltpu.make_async_remote_copy(
            src_ref=down_ref.at[me ^ k],
            dst_ref=moved.at[me],
            send_sem=e_send.at[k],
            recv_sem=e_recv.at[k],
            device_id={"seq": me ^ k},
            device_id_type=MESH,
        )

    def move_arrival(k):
        return pltpu.make_async_remote_copy(
            src_ref=down_ref.at[me],
            dst_ref=moved.at[me ^ k],
            send_sem=e_send.at[k],
            recv_sem=e_recv.at[k],
            device_id={"seq": me},
            device_id_type=MESH,
        )

    def block_of(i, target):
        if i == 0:
            return ow_ref.at[target]
        if i == 1:
            return up_ref.at[:, target]
        return moved.at[target % seq, pl.ds(pl.multiple_of((target // seq) * share, share), share)]

    start, combine, zsend, zrecv, drain_y, drain_z = line_reduce(
        hi,
        lo,
        block_of,
        (to, tu, dtotal_ref),
        (yo, yu, yd),
        (zo, zu),
        z_send,
        z_recv,
        y_send,
        y_recv,
        {1: up_loads},
    )

    def exchange(k, sending):
        return pltpu.make_async_remote_copy(
            src_ref=tu.at[z, me ^ k] if sending else tu.at[z, me],
            dst_ref=xu.at[me] if sending else xu.at[me ^ k],
            send_sem=x_send.at[k],
            recv_sem=x_recv.at[k],
            device_id={"seq": me ^ k if sending else me},
            device_id_type=MESH,
        )

    if not inside:
        start(1)
    for k in reversed(range(1, seq)):
        move_copy(k).start()
    for j in range(seq - 1, 0, -2):
        mo_copy(1, j ^ 1).start()
    if inside:
        for c in up_loads:
            c.wait()
        zsend(1, 0)
    dmem_ref[...] = sgrad_ref[...].astype(f32)
    dnext_ref[...] = jnp.zeros_like(dnext_ref)
    small_ref[...] = jnp.zeros_like(small_ref)
    near_ref[...] = jnp.zeros_like(near_ref)
    far_ref[...] = jnp.zeros_like(far_ref)
    for head in range(heads):
        bias_ref[head] = tile_bias(vector_ref, head).T
    for c in loads[:2] + loads[4:]:
        c.wait()
    if inside:
        full = t_dot(att_ref[...], db_ref[...]).astype(bf16)
        ow_buf[...] = full.reshape(ow_buf.shape)
    start(0)

    def mo_step(j):
        mo_loads[j // 2].wait()
        for bit in bits:
            if j & bit:
                mo_copy(bit, j ^ bit).start()
                break
            mo_copy(bit, j).wait_recv()
            own = mo_low[j // 2].astype(f32)
            mo_low[j // 2] = (own + mo_in[slots[bit, j]].astype(f32)).astype(bf16)

    def down_ready():
        for k in range(1, seq):
            move_arrival(k).wait_recv()
        loads[2].wait()
        start(2)

    def up_done():
        for k in range(1, seq):
            exchange(k, True).start()

    def zstep(i, t):
        zrecv(i, t)
        if t + 1 < hi - 1:
            zsend(i, t + 1)

    jobs = [lambda j=j: mo_step(j) for j in range(seq - 2, 0, -2)]
    if not inside:
        jobs.append(lambda: (combine(1), zsend(1, 0)))
    jobs.append(lambda: (zstep(1, 0), combine(0), zsend(0, 0)))
    for t in range(1, hi - 1):
        jobs.append(lambda t=t: zstep(1, t))
        if t == 1:
            jobs.append(lambda: down_ready())
    jobs.append(lambda: up_done())
    jobs += [lambda t=t: zstep(0, t) for t in range(hi - 1)]
    points = blocks * heads - 1

    dq_row = heads * DH
    block_loads(blocks - 1)[0].wait()

    @pl.loop(0, blocks)
    def _(step):
        block = blocks - 1 - step
        pl.when(block >= 1)(lambda: block_loads(jnp.maximum(block - 1, 0))[0].wait())
        for c in block_loads(block)[1:]:
            c.wait()
        cur_at = pl.multiple_of((block ^ me) * BLOCK, BLOCK)
        prev_at = pl.multiple_of((jnp.maximum(block - 1, 0) ^ me) * BLOCK, BLOCK)
        base = pl.multiple_of(block * BLOCK, BLOCK)
        cur_ref = qkv_ref.at[pl.ds(cur_at, BLOCK)]
        prev_ref = qkv_ref.at[pl.ds(prev_at, BLOCK)]
        live_block = block * BLOCK < length
        refs = (prev_ref, cur_ref)
        dout_ref[...] = dot_t(db_ref[pl.ds(cur_at, BLOCK)], wout_ref[...]).astype(bf16)
        for head in range(heads):
            for n, job in enumerate(jobs[:points]):
                if (n + 1) % heads == head:
                    pl.when(step == (n + 1) // heads)(lambda job=job: (job(), None)[1])
            own = slice(head * DH, (head + 1) * DH)
            key_cols = slice(width + head * DH, width + (head + 1) * DH)
            value_cols = slice(2 * width + head * DH, 2 * width + (head + 1) * DH)
            memory = mem_ref[block, :, own]
            update = upd_ref[block, :, own]
            low = memory.astype(bf16)
            forget = jax.nn.sigmoid(gate_ref[head : head + 1, :])
            dmem = dmem_ref[:, own]
            dupd = jnp.where(live_block, (1.0 - forget) * dmem, 0.0).astype(bf16)
            gone = jnp.where(live_block, dmem * (memory - update), 0.0)
            small_ref[dq_row + head : dq_row + head + 1, :] += jnp.sum(gone, axis=0, keepdims=True)
            dmem_new = jnp.where(live_block, forget * dmem, dmem)
            own_key = cur_ref[:, key_cols]
            own_value = cur_ref[:, value_cols]
            squeries = dot(low, query_ref[head]).astype(bf16)
            sdelta = jnp.sum((dupd.astype(f32) * update).T, axis=0, keepdims=True)
            slse = slse_ref[head : head + 1, pl.ds(base, BLOCK)]
            dsquery = jnp.zeros((STATE_VECTORS, DH), f32)
            dkey = []
            dvalue = []
            for part in range(2 * STATE_VECTORS // QTILE):
                own_part = part >= STATE_VECTORS // QTILE
                at = (part % (STATE_VECTORS // QTILE)) * QTILE
                keys = (own_key if own_part else low)[at : at + QTILE]
                values = (own_value if own_part else low)[at : at + QTILE]
                s = dot_t(keys, squeries) * scale2 - slse
                if own_part:
                    position = block * BLOCK + at + lax.broadcasted_iota(jnp.int32, (QTILE, 1), 0)
                    s = jnp.where(position < length, s, -jnp.inf)
                p = jnp.exp2(s)
                dp = dot_t(values, dupd)
                ds = (p * (dp - sdelta)).astype(bf16)
                dvalue.append(dot(p.astype(bf16), dupd))
                dkey.append(dot(ds, squeries))
                dsquery += t_dot(ds, keys)
            half = STATE_VECTORS // QTILE
            dlow = [dvalue[i] + dkey[i] * SCALE for i in range(half)]
            dctx_ref[0, 0:BLOCK] = jnp.zeros((BLOCK, DH), f32)
            dctx_ref[1, 0:BLOCK] = jnp.zeros((BLOCK, DH), f32)
            for i in range(half):
                rows = slice(BLOCK + i * QTILE, BLOCK + (i + 1) * QTILE)
                old = slice(i * QTILE, (i + 1) * QTILE)
                dctx_ref[0, rows] = dkey[half + i] * SCALE + dnext_ref[0, old, own]
                dctx_ref[1, rows] = dvalue[half + i] + dnext_ref[1, old, own]
            dsq = (dsquery * SCALE).astype(bf16)
            small_ref[head * DH : (head + 1) * DH, :] += t_dot(low, dsq)
            dmem_ref[:, own] = dmem_new + dot_t(dsq, query_ref[head])
            for tile in range(BLOCK // QTILE):
                rows = slice(tile * QTILE, (tile + 1) * QTILE)
                here = pl.ds(cur_at + tile * QTILE, QTILE)
                query = cur_ref[rows, own]
                dout = dout_ref[rows, own]
                lse = lse_ref[head : head + 1, pl.ds(base + tile * QTILE, QTILE)]
                delta = jnp.sum((dout.astype(f32) * att_ref[here, own].astype(f32)).T, axis=0, keepdims=True)
                dq = jnp.zeros((QTILE, DH), f32)
                for which, first, end, col in context_pieces(tile):
                    for at in range(first, end, QTILE):
                        keys = refs[which][at : at + QTILE, key_cols]
                        values = refs[which][at : at + QTILE, value_cols]
                        band = col + at - first
                        position = (block - 1 + which) * BLOCK + at + lax.broadcasted_iota(jnp.int32, (QTILE, 1), 0)
                        live = (position >= 0) & (position < length)
                        s = dot_t(keys, query) * scale2 + bias_ref[head, band : band + QTILE, :] - lse
                        p = jnp.exp2(jnp.where(live, s, -jnp.inf))
                        dp = dot_t(values, dout)
                        ds = (p * (dp - delta)).astype(bf16)
                        wide = ds.astype(f32)
                        edge = min(max(SPAN - NEAR - band, 0), QTILE)
                        if edge:
                            far_ref[head] += functools.reduce(jnp.add, [wide[i : i + 8] for i in range(0, edge, 8)])
                        if edge < QTILE:
                            at_near = band + edge - (SPAN - NEAR)
                            near_ref[head, at_near : at_near + QTILE - edge] += wide[edge:]
                        into = slice(which * BLOCK + at, which * BLOCK + at + QTILE)
                        dctx_ref[1, into] += dot(p.astype(bf16), dout)
                        dctx_ref[0, into] += dot(ds, query) * SCALE
                        dq += t_dot(ds, keys)
                for part in range(half):
                    keys = low[part * QTILE : (part + 1) * QTILE]
                    s = dot_t(keys, query) * scale2 - lse
                    p = jnp.exp2(s)
                    dp = dot_t(keys, dout)
                    ds = (p * (dp - delta)).astype(bf16)
                    dlow[part] += dot(p.astype(bf16), dout) + dot(ds, query) * SCALE
                    dq += t_dot(ds, keys)
                dqkv_ref[here, own] = (dq * SCALE).astype(bf16)
            for part in range(half):
                dmem_ref[part * QTILE : (part + 1) * QTILE, own] += dlow[part]
            dnext_ref[0, :, own] = dctx_ref[0, 0:BLOCK]
            dnext_ref[1, :, own] = dctx_ref[1, 0:BLOCK]
            dqkv_ref[pl.ds(cur_at, BLOCK), key_cols] = dctx_ref[0, BLOCK:].astype(bf16)
            dqkv_ref[pl.ds(cur_at, BLOCK), value_cols] = dctx_ref[1, BLOCK:].astype(bf16)

    dqkv_store = pltpu.make_async_copy(dqkv_ref, dqkv_out, out_sem)
    dqkv_store.start()
    for job in jobs[points:]:
        job()
    member = bucket_members()
    lane = lax.broadcasted_iota(jnp.int32, (1, DH), 1)
    for head in range(heads):
        sums = jnp.broadcast_to(diagonal_sums(near_ref[head]), (8, 2 * QTILE))
        table = jnp.dot(sums, member, precision=lax.Precision.HIGHEST, preferred_element_type=f32)[0:1]
        total = jnp.sum(jnp.sum(far_ref[head], axis=0, keepdims=True), axis=1, keepdims=True)
        row = dq_row + heads + head
        small_ref[row : row + 1, :] = table + jnp.where(lane == BUCKETS - 1, total, 0.0)
        row = dq_row + head
        forget = jax.nn.sigmoid(gate_ref[head : head + 1, :])
        small_ref[row : row + 1, :] = small_ref[row : row + 1, :] * forget * (1.0 - forget)
    loads[3].wait()
    mo_loads[0].wait()
    for bit in bits:
        mo_copy(bit, 0).wait_recv()
    step = 128
    for r in range(0, tok_rows, step):
        at = slice(r, r + step)
        value = mid_ref[at] + mo_low[0, at].astype(f32)
        for bit in bits:
            value = value + mo_in[slots[bit, 0], at].astype(f32)
        position = me * tok_rows + r + lax.broadcasted_iota(jnp.int32, (step, 1), 0)
        output_ref[at] = (value * jnp.where(position < length, 1.0, 0.0)).astype(bf16)
    combine(2)
    opart_ref[...] = to[z].astype(f32)
    for k in range(1, seq):
        exchange(k, False).wait_recv()
    xu[me] = tu[z, me]
    write_parts(upart_ref, xu, seq, share)
    for i in (0, 2) if inside else (0, 1, 2):
        drain_y(i)
    for i in range(2):
        drain_z(i)
    for bit in bits:
        for j in range(0, seq, 2 * bit):
            mo_copy(bit, j).wait_send()
    for k in range(1, seq):
        move_copy(k).wait_send()
        exchange(k, True).wait_send()
    dqkv_store.wait()


def bucket_members():
    shape = (2 * QTILE, DH)
    row = lax.broadcasted_iota(jnp.int32, shape, 0)
    lane = lax.broadcasted_iota(jnp.int32, shape, 1)
    distance = jnp.where(row < QTILE, row, row - 2 * QTILE) + NEAR - QTILE
    bucket = jnp.minimum(distance, 16)
    for edge in BUCKET_EDGES:
        bucket = bucket + jnp.where(distance >= edge, 1, 0)
    inside = (distance >= 0) & (distance < BLOCK) & (bucket == lane)
    return jnp.where(inside, 1.0, 0.0)


def write_parts(out_ref, pieces, seq, unit):
    if len(out_ref.shape) == 3:
        out_ref[...] = pieces[...].astype(f32)
        return
    count = pieces.shape[2] // unit
    for k in range(seq):
        for c in range(count):
            at = (c * seq + k) * unit
            out_ref[:, at : at + unit] = pieces[k, :, c * unit : (c + 1) * unit].astype(f32)


def attend_back(
    qkv, db, wout, att, mem, upd, lse, slse, sgrad, length, state_query, forget, bias, up, down, mo, mid, seq, fsdp
):
    rows, width3 = qkv.shape
    width = width3 // 3
    heads = width // DH
    dim = db.shape[1]
    lo = 2
    hi = fsdp // lo
    piece, hidden = up.shape[2:]
    share = hidden // fsdp
    tok_rows = mid.shape[0]
    inside = piece % 16 == 0
    blocks = (piece, dim), (seq, piece, hidden), (share, dim)
    small_rows = heads * (DH + 2)
    small_rows += -small_rows % 8
    vmem = pl.BlockSpec(memory_space=pltpu.VMEM)
    anywhere = pl.BlockSpec(memory_space=pl.ANY)
    dma = pltpu.SemaphoreType.DMA

    def buf(*shape):
        return pltpu.VMEM(shape, bf16)

    extra = []
    if not inside:
        extra.append(t_dot(att, db).astype(bf16).reshape(fsdp, piece, dim))
    upart = (piece, hidden * seq) if share % 128 == 0 else (seq, piece, hidden)
    return pl.pallas_call(
        functools.partial(attend_back_kernel, heads, seq, hi, lo, inside),
        out_shape=(
            jax.ShapeDtypeStruct((rows, width3), bf16),
            jax.ShapeDtypeStruct((small_rows, DH), f32),
            jax.ShapeDtypeStruct(upart, f32),
            jax.ShapeDtypeStruct((hi, share, dim), bf16),
            jax.ShapeDtypeStruct((piece, dim), f32),
            jax.ShapeDtypeStruct((tok_rows, dim), bf16),
        ),
        in_specs=[pl.BlockSpec(memory_space=pltpu.SMEM), anywhere, anywhere, anywhere]
        + [anywhere] * 3
        + [vmem] * 6
        + [anywhere] * 4
        + [vmem] * len(extra),
        out_specs=(anywhere,) + (vmem,) * 5,
        scratch_shapes=[
            buf(rows, width3),
            buf(rows, dim),
            buf(rows, width),
            pltpu.VMEM(mem.shape, f32),
            pltpu.VMEM(upd.shape, f32),
            pltpu.VMEM((tok_rows, dim), f32),
            buf(rows, width3),
            buf(width, dim),
            pltpu.VMEM((STATE_VECTORS, width), f32),
            pltpu.VMEM((2, BLOCK, width), f32),
            pltpu.VMEM((2, 2 * BLOCK, DH), f32),
            pltpu.VMEM((heads, SPAN, QTILE), f32),
            pltpu.VMEM((heads, NEAR, QTILE), f32),
            pltpu.VMEM((heads, 8, QTILE), f32),
            buf(BLOCK, width),
            buf(fsdp, piece, dim),
            buf(*down.shape),
            buf(hi, *blocks[0]),
            buf(hi, *blocks[1]),
            buf(hi, *blocks[0]),
            buf(16, 128) if inside else buf(hi, *blocks[1]),
            buf(hi, *blocks[2]),
            buf(2, max(hi - 1, 1), *blocks[0]),
            buf(2, max(hi - 1, 1), *blocks[1]),
            buf(*blocks[1]),
            buf(max(seq // 2, 1), tok_rows, dim),
            buf(max(seq - 1, 1), tok_rows, dim),
            dma((2, 2, hi)),
            dma((2, 2, hi)),
            dma((3, hi)),
            dma((3, hi)),
            dma((seq,)),
            dma((seq,)),
            dma((seq,)),
            dma((seq,)),
            dma((seq,)),
            dma((seq,)),
            dma((5,)),
            dma((3, seq)),
            dma((hi,)),
            dma((seq,)),
            dma,
        ],
        compiler_params=pltpu.CompilerParams(collective_id=4, has_side_effects=True, vmem_limit_bytes=62 << 20),
        cost_estimate=pl.CostEstimate(
            flops=seq * heads * 512 * 2400 * 128 * 10, bytes_accessed=20 << 20, transcendentals=10 << 20
        ),
        name="attend_back",
    )(
        length, qkv, db, wout, att, mem, upd, lse, slse, sgrad, state_query, forget, bias, up, down, mo, mid, *extra
    )


def gather_kernel(seq, hi, lo, *refs):
    refs = list(refs)

    def take(count):
        taken = refs[:count]
        del refs[:count]
        return taken

    tok_ref, grad_ref, wq_ref, ga_ref, gm_ref, wo_ref, wu_ref = take(7)
    toks_ref, grads_ref, wqs_ref, gas_ref, gms_ref, wos_ref, wus_ref, normed_ref, qkv_ref = take(9)
    toks_full, grad_buf, wq_full, ga_full, gm_full, wo_buf, wu_buf, normed_buf, qkv_buf = take(9)
    own_sem, store_sem, seq_send, seq_recv, chunk_sem, z_send, z_recv, y_send, y_recv = take(9)

    me = lax.axis_index("seq")
    f = lax.axis_index("fsdp")
    fsdp = hi * lo
    bits = [1 << i for i in range(seq.bit_length() - 1)]
    high = [bit for bit in reversed(bits) if bit > 1]
    rows, dim = tok_ref.shape
    width = wq_full.shape[2] // 3
    share = wus_ref.shape[2] // fsdp
    every = wq_ref.shape[1] // 3
    loads = [[] for _ in range(7)]

    def load(i, src, dst):
        loads[i].append(pltpu.make_async_copy(src, dst, own_sem.at[i, len(loads[i])]))
        loads[i][-1].start()

    for c in range(3):
        cols = pl.ds(pl.multiple_of(c * every + me * width, width), width)
        load(0, wq_ref.at[:, cols], wq_full.at[f, :, pl.ds(c * width, width)])
    load(1, ga_ref, ga_full.at[f])
    load(2, gm_ref, gm_full.at[f])
    load(3, wo_ref.at[me % 2], wo_buf)
    if wu_ref.shape[1] == wus_ref.shape[2]:
        load(4, wu_ref, wu_buf)
    else:
        for c in range(fsdp):
            cols = pl.ds(pl.multiple_of((c * seq + me) * share, share), share)
            load(4, wu_ref.at[:, cols], wu_buf.at[:, pl.ds(c * share, share)])
    load(5, tok_ref, toks_full.at[0])
    load(6, grad_ref, grad_buf)
    greet(bits, hi, lo)

    pairs = ((tok_ref, toks_full), (grad_ref, grads_ref))

    def seq_copy(i, source, slot, bit):
        src, out = pairs[i]
        return pltpu.make_async_remote_copy(
            src_ref=out.at[source] if source else src,
            dst_ref=out.at[slot],
            send_sem=seq_send.at[i, slot],
            recv_sem=seq_recv.at[i, slot],
            device_id={"seq": me ^ bit},
            device_id_type=MESH,
        )

    sends = []

    def send(i, source, slot, bit):
        sends.append(seq_copy(i, source, slot, bit))
        sends[-1].start()

    fulls = (wq_full, ga_full, gm_full, wos_ref, wus_ref)
    bufs = (None, None, None, wo_buf, wu_buf)
    start, step, arrive, drain = line_gather(
        hi,
        lo,
        lambda i, origin: fulls[i].at[origin],
        lambda i: fulls[i].at[f] if i < 3 else bufs[i],
        z_send,
        z_recv,
        y_send,
        y_recv,
    )
    first, later = (0, 1, 2), (3, 4)
    if high:
        send(0, 0, high[0], high[0])
    if seq > 1:
        send(0, 0, 1, 1)
    for i in first:
        for c in loads[i]:
            c.wait()
        start(i)
    if high:
        send(1, 0, high[0], high[0])
    if seq > 1:
        send(1, 0, 1, 1)
    stores = []

    def store(src, dst, sem):
        stores.append(pltpu.make_async_copy(src, dst, sem))
        stores[-1].start()

    for t in range(hi - 1):
        for i in first:
            step(i, t)
        if t == min(1, hi - 2):
            for i in later:
                for c in loads[i]:
                    c.wait()
                start(i)
            store(wo_buf, wos_ref.at[f], store_sem.at[0])
            store(wu_buf, wus_ref.at[f], store_sem.at[1])
    for c in loads[5] + loads[6]:
        c.wait()
    store(toks_full.at[0], toks_ref.at[0], chunk_sem.at[0, 0])
    store(grad_buf, grads_ref.at[0], store_sem.at[2])
    for i in first:
        arrive(i)
    store(wq_full, wqs_ref, store_sem.at[3])
    gas_ref[...] = jnp.concatenate([ga_full[n] for n in range(fsdp)], axis=1).astype(f32)
    gms_ref[...] = jnp.concatenate([gm_full[n] for n in range(fsdp)], axis=1).astype(f32)
    gain = gas_ref[...]

    def project(j):
        if j:
            store(toks_full.at[j], toks_ref.at[j], chunk_sem.at[0, j])

        @pl.loop(0, rows // 256)
        def _(n):
            at = pl.ds(pl.multiple_of(n * 256, 256), 256)
            into = pl.ds(pl.multiple_of(j * rows + n * 256, 256), 256)
            x = toks_full[j, at].astype(f32)
            rho = lax.rsqrt(jnp.mean(x * x, axis=-1, keepdims=True) + EPSILON)
            normed = (x * rho * gain).astype(bf16)
            normed_buf[into] = normed
            qkv_buf[into] = dot(normed, wq_full[...].reshape(dim, 3 * width)).astype(bf16)

        at = pl.ds(j * rows, rows)
        store(normed_buf.at[at], normed_ref.at[at], chunk_sem.at[1, j])
        store(qkv_buf.at[at], qkv_ref.at[at], chunk_sem.at[2, j])

    hop = [0]

    def advance():
        if hop[0] < hi - 1:
            for i in later:
                step(i, hop[0])
            hop[0] += 1

    project(0)
    advance()
    have = [0]
    for n, bit in enumerate(high):
        if n:
            for j in have:
                send(0, j, j ^ bit, bit)
        for j in have:
            seq_copy(0, 0, j ^ bit, bit).wait_recv()
            send(0, j ^ bit, j ^ bit ^ 1, 1)
        have += [j ^ bit for j in have]
    for j in have:
        if j:
            project(j)
            advance()
        if seq > 1:
            seq_copy(0, 0, j ^ 1, 1).wait_recv()
            project(j ^ 1)
            advance()
    while hop[0] < hi - 1:
        advance()
    have = [0]
    for n, bit in enumerate(high):
        if n:
            for j in have:
                send(1, j, j ^ bit, bit)
        for j in have:
            seq_copy(1, 0, j ^ bit, bit).wait_recv()
            send(1, j ^ bit, j ^ bit ^ 1, 1)
        have += [j ^ bit for j in have]
    if seq > 1:
        for j in have:
            seq_copy(1, 0, j ^ 1, 1).wait_recv()
    for i in later:
        arrive(i)
    for i in first + later:
        drain(i)
    for c in sends:
        c.wait_send()
    for c in stores:
        c.wait()


def gather_start(tokens, grads, w_qkv, gain_a, gain_m, w_out, w_up, seq, fsdp):
    lo = 2
    hi = fsdp // lo
    dim_rows, hidden = w_up.shape
    share = hidden // (seq * fsdp)
    if share % 128:
        w_up = lax.dynamic_slice_in_dim(w_up.reshape(dim_rows, fsdp, seq, share), lax.axis_index("seq"), 1, axis=2)
        w_up = w_up.reshape(dim_rows, fsdp * share)
    rows, dim = tokens.shape
    width3 = w_qkv.shape[1] // seq
    anywhere = pl.BlockSpec(memory_space=pl.ANY)
    vmem = pl.BlockSpec(memory_space=pltpu.VMEM)
    dma = pltpu.SemaphoreType.DMA

    def like(*shape):
        return jax.ShapeDtypeStruct(shape, bf16)

    def buf(*shape):
        return pltpu.VMEM(shape, bf16)

    return pl.pallas_call(
        functools.partial(gather_kernel, seq, hi, lo),
        out_shape=(
            like(seq, rows, dim),
            like(seq, rows, dim),
            like(fsdp, dim_rows, width3),
            jax.ShapeDtypeStruct((1, dim), f32),
            jax.ShapeDtypeStruct((1, dim), f32),
            like(fsdp, *w_out.shape[1:]),
            like(fsdp, dim_rows, hidden // seq),
            like(seq * rows, dim),
            like(seq * rows, width3),
        ),
        in_specs=[anywhere] * 7,
        out_specs=(anywhere,) * 3 + (vmem,) * 2 + (anywhere,) * 4,
        scratch_shapes=[
            buf(seq, rows, dim),
            buf(rows, dim),
            buf(fsdp, dim_rows, width3),
            buf(fsdp, *gain_a.shape),
            buf(fsdp, *gain_m.shape),
            buf(*w_out.shape[1:]),
            buf(dim_rows, hidden // seq),
            buf(seq * rows, dim),
            buf(seq * rows, width3),
            dma((7, max(fsdp, 3))),
            dma((4,)),
            dma((2, seq)),
            dma((2, seq)),
            dma((3, seq)),
        ]
        + line_sems(5, hi),
        compiler_params=pltpu.CompilerParams(collective_id=0, has_side_effects=True, vmem_limit_bytes=62 << 20),
        name="gather_start",
    )(tokens, grads, w_qkv, gain_a, gain_m, w_out, w_up)


def finish_kernel(seq, hi, lo, inside, *refs):
    refs = list(refs)

    def take(count):
        taken = refs[:count]
        del refs[:count]
        return taken

    dqkv_hbm, wqkv_hbm, normed_hbm, down_ref, small_ref, mlp_gain_ref, tok_hbm, dmid_hbm, gain_ref = take(9)
    gq_in = None if inside else take(1)[0]
    tg_ref, rq_ref, rd_ref, dquery_ref, gate_ref, table_ref, again_ref, mgain_ref = take(8)
    dqkv_ref, wqkv_ref, normed_ref, tok_ref, dmid_ref = take(5)
    low, into, acc, gq_buf, tq, td, yq, zq, zd, xq, sy, sz, gains, gy, gz, gs = take(16)
    dn_send, dn_recv, z_send, z_recv, y_send, y_recv, x_send, x_recv, s_send, s_recv, g_send, g_recv = take(12)
    load_sem, dqkv_sem, tg_sem = take(3)
    gq_ref = gq_buf if inside else gq_in

    me = lax.axis_index("seq")
    f = lax.axis_index("fsdp")
    z, y = f // lo, f % lo
    peer = z * lo + 1 - y
    rows, dim = tok_ref.shape
    width = xq.shape[2] // 3
    bits, slots = seq_levels(seq)

    loads = [
        pltpu.make_async_copy(src, dst, load_sem.at[i])
        for i, (src, dst) in enumerate(
            (
                (wqkv_hbm, wqkv_ref),
                (down_ref, td),
                (normed_hbm, normed_ref),
                (tok_hbm, tok_ref),
                (dmid_hbm, dmid_ref),
            )
        )
    ]
    dqkv_loads = {
        j: pltpu.make_async_copy(
            dqkv_hbm.at[pl.ds(j * rows, rows)], dqkv_ref.at[pl.ds(j * rows, rows)], dqkv_sem.at[j]
        )
        for j in range(seq)
    }
    loads[0].start()
    for j in reversed(range(seq)):
        dqkv_loads[j].start()
    for c in loads[1:]:
        c.start()

    barrier = pltpu.get_barrier_semaphore()
    for k in range(1, seq):
        pl.semaphore_signal(barrier, inc=1, device_id={"seq": me ^ k}, device_id_type=MESH)
    for k in range(1, hi):
        pl.semaphore_signal(barrier, inc=1, device_id={"fsdp": lax.rem(z + k, hi) * lo + y}, device_id_type=MESH)
    pl.semaphore_signal(barrier, inc=1, device_id={"fsdp": peer}, device_id_type=MESH)
    pl.semaphore_wait(barrier, seq + hi - 1)

    def remote(src, dst, send, recv, axis, target):
        return pltpu.make_async_remote_copy(
            src_ref=src, dst_ref=dst, send_sem=send, recv_sem=recv, device_id={axis: target}, device_id_type=MESH
        )

    def dn_copy(bit, j):
        slot = slots[bit, j]
        return remote(low.at[j ^ bit], into.at[slot], dn_send.at[slot], dn_recv.at[slot], "seq", me ^ bit)

    _, _, zsend, zrecv, _, drain_z = line_reduce(
        hi,
        lo,
        lambda i, target: gq_ref.at[:, target],
        (tq, td),
        (yq,),
        (zq, zd),
        z_send,
        z_recv,
        y_send,
        y_recv,
    )
    half = seq // 2
    start, combine, _, _, drain_y, _ = line_reduce(
        hi,
        lo,
        lambda i, target: gq_ref.at[pl.ds(i * half, half), target],
        tuple(tq.at[:, pl.ds(i * half, half)] for i in range(2)),
        tuple(yq.at[:, pl.ds(i * half, half)] for i in range(2)),
        (),
        None,
        None,
        y_send,
        y_recv,
    )

    def exchange(k, sending):
        return remote(
            tq.at[z, me ^ k] if sending else tq.at[z, me],
            xq.at[me] if sending else xq.at[me ^ k],
            x_send.at[k],
            x_recv.at[k],
            "seq",
            me ^ k if sending else me,
        )

    small_y = remote(small_ref, sy, s_send.at[0], s_recv.at[0], "fsdp", peer)
    small_y.start()
    loads[0].wait()
    if not inside:
        start(0)
        start(1)

    def dn_part(j):
        part = dot_t(dqkv_ref[j * rows : (j + 1) * rows], wqkv_ref[...])
        if j % 2:
            low[j] = part.astype(bf16)
            dn_copy(1, j ^ 1).start()
        else:
            acc[...] = part

    def dn_sum(j):
        for bit in bits:
            if j & bit:
                low[j] = acc[...].astype(bf16)
                dn_copy(bit, j ^ bit).start()
                break
            dn_copy(bit, j).wait_recv()
            acc[...] += into[slots[bit, j]].astype(f32)

    for j in reversed(range(2, seq)):
        dqkv_loads[j].wait()
        dn_part(j)
        if j == seq - 1:
            loads[1].wait()
            zsend(1, 0)
        if j % 2 == 0:
            dn_sum(j)
    for j in range(min(2, seq)):
        dqkv_loads[j].wait()
    loads[2].wait()
    if inside:
        for k in range(seq):
            cols = slice(k * (dim // seq), (k + 1) * (dim // seq))
            part = t_dot(normed_ref[:, cols], dqkv_ref[...]).astype(bf16)
            gq_buf[k] = part.reshape(gq_buf.shape[1:])
            if (k + 1) % half == 0:
                start(k // half)
    def zstep(i, t):
        if t < hi - 1:
            zrecv(i, t)
            if t + 1 < hi - 1:
                zsend(i, t + 1)

    zstep(1, 0)
    small_y.wait_recv()
    sz[z] = small_ref[...] + sy[...]
    small_z = []
    for k in range(1, hi):
        small_z.append(
            remote(sz.at[z], sz.at[z], s_send.at[k], s_recv.at[k], "fsdp", lax.rem(z + k, hi) * lo + y)
        )
        small_z[-1].start()
    for j in reversed(range(min(2, seq))):
        dn_part(j)
    zstep(1, 1)
    for c in loads[3:]:
        c.wait()
    combine(0)
    combine(1)
    zsend(0, 0)
    zstep(1, 2)
    for t in range(3, hi - 1):
        zstep(1, t)
    for bit in bits:
        dn_copy(bit, 0).wait_recv()
    gain = gain_ref[...]
    part = jnp.zeros((8, dim), f32)
    step = 128
    for r in range(0, rows, step):
        at = slice(r, r + step)
        dn = acc[at]
        for bit in bits:
            dn = dn + into[slots[bit, 0], at].astype(f32)
        x = tok_ref[at].astype(f32)
        rho = lax.rsqrt(jnp.mean(x * x, axis=-1, keepdims=True) + EPSILON)
        scaled = gain * dn
        mean = jnp.mean(x * scaled, axis=-1, keepdims=True)
        dmid_ref[at] += rho * scaled - x * (rho * rho * rho * mean)
        prod = dn * x * rho
        part += functools.reduce(jnp.add, [prod[n : n + 8] for n in range(0, step, 8)])
    tg_store = pltpu.make_async_copy(dmid_ref, tg_ref, tg_sem)
    tg_store.start()
    gains[0:8] = mlp_gain_ref[...]
    gains[8:16] = part
    gain_y = remote(gains, gy, g_send.at[0], g_recv.at[0], "fsdp", peer)
    gain_y.start()
    zrecv(0, 0)
    if hi > 2:
        zsend(0, 1)
    gain_y.wait_recv()
    gz[z] = gains[...] + gy[...]
    gain_z = []
    for k in range(1, hi):
        gain_z.append(
            remote(gz.at[z], gz.at[z], g_send.at[k], g_recv.at[k], "fsdp", lax.rem(z + k, hi) * lo + y)
        )
        gain_z[-1].start()
    for t in range(1, hi - 1):
        zrecv(0, t)
        if t + 1 < hi - 1:
            zsend(0, t + 1)
    for k in range(1, seq):
        exchange(k, True).start()
    for k in range(1, hi):
        source = lax.rem(z + hi - k, hi)
        remote(gz.at[source], gz.at[source], g_send.at[k], g_recv.at[k], "fsdp", f).wait_recv()
        remote(sz.at[source], sz.at[source], s_send.at[k], s_recv.at[k], "fsdp", f).wait_recv()
    gs[me] = functools.reduce(jnp.add, [gz[d] for d in range(hi)])
    gain_x = []
    for k in range(1, seq):
        gain_x.append(remote(gs.at[me], gs.at[me], g_send.at[hi + k], g_recv.at[hi + k], "seq", me ^ k))
        gain_x[-1].start()
    rd_ref[...] = td[z].astype(f32)
    total = functools.reduce(jnp.add, [sz[d] for d in range(hi)])
    cut, heads = dquery_ref.shape[0], gate_ref.shape[0]
    dquery_ref[...] = total[:cut]
    gate_ref[...] = total[cut : cut + heads]
    table_ref[...] = total[cut + heads : cut + 2 * heads, :BUCKETS]
    xq[me] = tq[z, me]
    for k in range(1, seq):
        exchange(k, False).wait_recv()
    write_parts(rq_ref, xq, seq, width)
    for k in range(1, seq):
        remote(gs.at[me ^ k], gs.at[me ^ k], g_send.at[hi + k], g_recv.at[hi + k], "seq", me).wait_recv()
    total = functools.reduce(jnp.add, [gs[k] for k in range(seq)])
    piece = again_ref.shape[1]
    total = pltpu.roll(total, lax.rem(dim - (me * hi * lo + f) * piece, dim), 1)[:, :DH]
    mgain_ref[...] = jnp.sum(total[0:8], axis=0, keepdims=True)[:, :piece]
    again_ref[...] = jnp.sum(total[8:16], axis=0, keepdims=True)[:, :piece]

    for bit in bits:
        for j in range(0, seq, 2 * bit):
            dn_copy(bit, j).wait_send()
    drain_y(0)
    drain_y(1)
    for i in range(2):
        drain_z(i)
    for k in range(1, seq):
        exchange(k, True).wait_send()
    for c in [small_y, gain_y] + small_z + gain_z + gain_x:
        c.wait_send()
    tg_store.wait()


def finish(dqkv, wqkv, normed, down, small, mlp_gain, tok, dmid, gain, seq, fsdp):
    lo = 2
    hi = fsdp // lo
    rows, dim = tok.shape
    width3 = dqkv.shape[1]
    piece = dim // (seq * fsdp)
    inside = piece % 16 == 0
    heads = width3 // (3 * DH)
    vmem = pl.BlockSpec(memory_space=pltpu.VMEM)
    anywhere = pl.BlockSpec(memory_space=pl.ANY)
    dma = pltpu.SemaphoreType.DMA

    def buf(*shape):
        return pltpu.VMEM(shape, bf16)

    extra = []
    if not inside:
        extra.append(t_dot(normed, dqkv).astype(bf16).reshape(seq, fsdp, piece, width3))
    scratch = [
        buf(*dqkv.shape),
        buf(*wqkv.shape),
        buf(*normed.shape),
        buf(rows, dim),
        pltpu.VMEM((rows, dim), f32),
        buf(seq, rows, dim),
        buf(max(seq - 1, 1), rows, dim),
        pltpu.VMEM((rows, dim), f32),
        buf(seq, fsdp, piece, width3) if inside else buf(16, 128),
        buf(hi, seq, piece, width3),
        buf(*down.shape),
        buf(hi, seq, piece, width3),
        buf(2, max(hi - 1, 1), seq, piece, width3),
        buf(2, max(hi - 1, 1), *down.shape[1:]),
        buf(seq, piece, width3),
        pltpu.VMEM(small.shape, f32),
        pltpu.VMEM((hi,) + small.shape, f32),
        pltpu.VMEM((16, dim), f32),
        pltpu.VMEM((16, dim), f32),
        pltpu.VMEM((hi, 16, dim), f32),
        pltpu.VMEM((seq, 16, dim), f32),
        dma((seq,)),
        dma((seq,)),
        dma((2, 2, hi)),
        dma((2, 2, hi)),
        dma((2, hi)),
        dma((2, hi)),
        dma((seq,)),
        dma((seq,)),
        dma((hi,)),
        dma((hi,)),
        dma((hi + seq,)),
        dma((hi + seq,)),
        dma((5,)),
        dma((seq,)),
        dma,
    ]
    return pl.pallas_call(
        functools.partial(finish_kernel, seq, hi, lo, inside),
        out_shape=(
            jax.ShapeDtypeStruct((rows, dim), f32),
            jax.ShapeDtypeStruct((piece, seq * width3), f32),
            jax.ShapeDtypeStruct(down.shape[1:], f32),
            jax.ShapeDtypeStruct((heads * DH, DH), f32),
            jax.ShapeDtypeStruct((heads, DH), f32),
            jax.ShapeDtypeStruct((heads, BUCKETS), f32),
            jax.ShapeDtypeStruct((1, piece), f32),
            jax.ShapeDtypeStruct((1, piece), f32),
        ),
        in_specs=[anywhere] * 4 + [vmem] * 2 + [anywhere] * 2 + [vmem] * (1 + len(extra)),
        out_specs=(anywhere,) + (vmem,) * 7,
        scratch_shapes=scratch,
        compiler_params=pltpu.CompilerParams(
            collective_id=1, has_side_effects=True, vmem_limit_bytes=60 << 20
        ),
        name="finish",
    )(dqkv, wqkv, normed, down, small, mlp_gain, tok, dmid, gain, *extra)


GELU_P = 0.24
GELU_C = (
    0.08951261885080208,
    0.15562094398234086,
    -0.15437154502074169,
    0.6261054138112487,
    -0.6465313024138201,
    0.5547927291245551,
    -0.125128858665134,
)


def gelu_parts(x):
    size = jnp.abs(x)
    t = 1.0 / (1.0 + GELU_P * size)
    poly = GELU_C[-1] * t
    for c in GELU_C[-2::-1]:
        poly = (poly + c) * t
    bell = jnp.exp2(x * x * (-0.5 * LOG2E))
    tail = poly * bell
    cdf = jnp.where(x < 0.0, tail, 1.0 - tail)
    return x * cdf, cdf + x * bell * (1.0 / math.sqrt(2.0 * math.pi))


def mlp_kernel(seq, hi, lo, sub, length_ref, *refs):
    refs = list(refs)

    def take(count):
        taken = refs[:count]
        del refs[:count]
        return taken

    own_ref, others_ref, tok_ref, grads_ref, wo_hbm, wu_hbm, wd_hbm, gain_ref = take(8)
    mid_out, dmid_out, gsum_ref, db_ref, mo_ref, ug_out, dg_out = take(7)
    staged = len(ug_out.shape) == 4
    att_refs = [own_ref] + [others_ref.at[k] for k in range(1, seq)]
    att_buf, tok_buf, wo_ref, wu_ref, wd_ref, gm, nm, hid, dpre, low, into, acc, mid_ref, ug_ref, dg_ref = take(15)
    load_sem, w_sem, gm_sem, dn_send, dn_recv, db_send, db_recv, mo_sem, own_sem = take(9)
    if staged:
        tu, yu, y_send, y_recv = take(4)
    dbv = low.at[0]
    depth = att_buf.shape[0]

    me = lax.axis_index("seq")
    length = length_ref[0]
    dim = wo_ref.shape[0]
    width = dim // seq
    rows = tok_ref.shape[1]
    share = wu_ref.shape[1]
    subs = rows // sub
    bits, slots = seq_levels(seq)
    order = list(reversed(range(seq)))

    def chunk_loads(j):
        slot = j % depth
        copies = [
            pltpu.make_async_copy(att_refs[k].at[pl.ds(j * rows, rows)], att_buf.at[slot, k], load_sem.at[slot, k])
            for k in range(seq)
        ]
        copies.append(pltpu.make_async_copy(tok_ref.at[j], tok_buf.at[slot], load_sem.at[slot, seq]))
        return copies

    gm_loads = {
        j: pltpu.make_async_copy(grads_ref.at[j], gm.at[pl.ds(j * rows, rows)], gm_sem.at[j]) for j in order
    }
    weights = [
        pltpu.make_async_copy(src, dst, w_sem.at[i])
        for i, (src, dst) in enumerate(((wo_hbm, wo_ref), (wu_hbm, wu_ref), (wd_hbm, wd_ref)))
    ]
    for c in chunk_loads(order[0]) + weights[:1] + (chunk_loads(order[1]) if seq > 1 else []) + weights[1:]:
        c.start()
    for j in order:
        gm_loads[j].start()
    if depth == seq:
        for j in order[2:]:
            for c in chunk_loads(j):
                c.start()

    greet(bits, hi, lo)

    def dn_copy(bit, j, s):
        slot = slots[bit, j]
        at = pl.ds(pl.multiple_of(s * sub, sub), sub)
        return pltpu.make_async_remote_copy(
            src_ref=low.at[j ^ bit, at],
            dst_ref=into.at[slot, at],
            send_sem=dn_send.at[slot, s],
            recv_sem=dn_recv.at[slot, s],
            device_id={"seq": me ^ bit},
            device_id_type=MESH,
        )

    gain = gain_ref[...]

    def forward(j, s):
        slot = j % depth
        at = pl.ds(pl.multiple_of(s * sub, sub), sub)
        here = pl.ds(pl.multiple_of(j * rows + s * sub, sub), sub)
        position = (j ^ me) * rows + s * sub + lax.broadcasted_iota(jnp.int32, (sub, 1), 0)
        live = jnp.where(position < length, 1.0, 0.0)
        masked = (gm[here].astype(f32) * live).astype(bf16)
        gm[here] = masked
        mid = tok_buf[slot, at].astype(f32)
        for k in range(seq):
            own = pl.ds(pl.multiple_of((me ^ k) * width, width), width)
            mid = mid + dot(att_buf[slot, k, at], wo_ref[own])
        rho = lax.rsqrt(jnp.mean(mid * mid, axis=-1, keepdims=True) + EPSILON)
        normed = (mid * rho * gain).astype(bf16)
        nm[here] = normed
        if j == 0:
            mid_ref[at] = mid
        for c in range(0, share, 256):
            cols = slice(c, c + 256)
            value, slope = gelu_parts(dot(normed, wu_ref[:, cols]))
            hid[here, cols] = value.astype(bf16)
            dpre[here, cols] = (dot_t(masked, wd_ref[cols]) * slope).astype(bf16)
        part = dot_t(dpre[here], wu_ref[...])
        if j % 2:
            low[j, at] = part.astype(bf16)
            dn_copy(1, j ^ 1, s).start()
        else:
            acc[at] = part

    def settle(j, s):
        at = pl.ds(pl.multiple_of(s * sub, sub), sub)
        for bit in bits:
            if j & bit:
                low[j, at] = acc[at].astype(bf16)
                dn_copy(bit, j ^ bit, s).start()
                break
            dn_copy(bit, j, s).wait_recv()
            acc[at] += into[slots[bit, j], at].astype(f32)

    for c in weights:
        c.wait()
    for n in range(0, seq, 2):
        pair = order[n : n + 2]
        if n and depth < seq:
            for j in pair:
                for c in chunk_loads(j):
                    c.start()
        for j in pair:
            for c in chunk_loads(j):
                c.wait()
            gm_loads[j].wait()

        @pl.loop(0, subs)
        def _(s):
            for j in pair:
                forward(j, s)
            if pair[-1]:
                settle(pair[-1], s)

    stores = [pltpu.make_async_copy(mid_ref, mid_out, own_sem.at[1])]
    stores[0].start()
    half = seq // 2
    if staged:
        start, combine, _, _, drain_y, _ = line_reduce(
            hi,
            lo,
            lambda i, target: ug_ref.at[pl.ds(i * half, half), target],
            tuple(tu.at[:, pl.ds(i * half, half)] for i in range(2)),
            tuple(yu.at[:, pl.ds(i * half, half)] for i in range(2)),
            (),
            None,
            None,
            y_send,
            y_recv,
        )

    def up_half(i):
        for k in range(i * half, (i + 1) * half):
            cols = slice(k * (dim // seq), (k + 1) * (dim // seq))
            ug_ref[k] = t_dot(nm[:, cols], dpre[...]).astype(bf16).reshape(ug_ref.shape[1:])
        start(i)

    if staged:
        up_half(0)
    else:
        for c in range(0, dim, 256):
            ug_ref[c : c + 256] = t_dot(nm[:, c : c + 256], dpre[...]).astype(bf16)
        stores.append(pltpu.make_async_copy(ug_ref, ug_out, own_sem.at[2]))
        stores[-1].start()

    def db_copy(source, target, bit, s):
        at = pl.ds(s * sub, sub)
        return pltpu.make_async_remote_copy(
            src_ref=db_ref.at[source, at] if source else dbv.at[at],
            dst_ref=db_ref.at[target, at],
            send_sem=db_send.at[target, s],
            recv_sem=db_recv.at[target, s],
            device_id={"seq": me ^ bit},
            device_id_type=MESH,
        )

    sends = []
    high = [bit for bit in reversed(bits) if bit > 1]

    def send(source, target, bit, s):
        sends.append(db_copy(source, target, bit, s))
        sends[-1].start()

    step = 128
    part = jnp.zeros((8, dim), f32)
    for s in range(subs):
        for bit in bits:
            dn_copy(bit, 0, s).wait_recv()
        for r in range(s * sub, (s + 1) * sub, step):
            at = slice(r, r + step)
            dn = acc[at]
            for bit in bits:
                dn = dn + into[slots[bit, 0], at].astype(f32)
            mid = mid_ref[at]
            rho = lax.rsqrt(jnp.mean(mid * mid, axis=-1, keepdims=True) + EPSILON)
            scaled = gain * dn
            mean = jnp.mean(mid * scaled, axis=-1, keepdims=True)
            dmid = gm[at].astype(f32) + rho * scaled - mid * (rho * rho * rho * mean)
            acc[at] = dmid
            dbv[at] = dmid.astype(bf16)
            prod = dn * mid * rho
            part += functools.reduce(jnp.add, [prod[i : i + 8] for i in range(0, step, 8)])
        if high:
            send(0, high[0], high[0], s)
        if seq > 1:
            send(0, 1, 1, s)
    gsum_ref[...] = part
    stores.append(pltpu.make_async_copy(dbv, db_ref.at[0], own_sem.at[0]))
    stores[-1].start()
    stores.append(pltpu.make_async_copy(acc, dmid_out, own_sem.at[3]))
    stores[-1].start()
    if staged:
        up_half(1)
    for c in range(0, share, 256):
        dg_ref[c : c + 256] = t_dot(hid[:, c : c + 256], gm[...]).astype(bf16)
    stores.append(pltpu.make_async_copy(dg_ref, dg_out, own_sem.at[4]))
    stores[-1].start()
    for j in range(seq):
        at = slice(j * rows, (j + 1) * rows)
        nm[at] = dot(hid[at], wd_ref[...]).astype(bf16)
        stores.append(pltpu.make_async_copy(nm.at[pl.ds(j * rows, rows)], mo_ref.at[j], mo_sem.at[j]))
        stores[-1].start()
    have = [0]
    for n, bit in enumerate(high):
        if n:
            for j in have:
                for s in range(subs):
                    send(j, j ^ bit, bit, s)
        for j in have:
            for s in range(subs):
                db_copy(0, j ^ bit, bit, s).wait_recv()
                send(j ^ bit, j ^ bit ^ 1, 1, s)
        have += [j ^ bit for j in have]
    if seq > 1:
        for j in have:
            for s in range(subs):
                db_copy(0, j ^ 1, 1, s).wait_recv()
    if staged:
        for i in range(2):
            combine(i)
        stores.append(pltpu.make_async_copy(tu, ug_out, own_sem.at[2]))
        stores[-1].start()
        for i in range(2):
            drain_y(i)
    for c in sends:
        c.wait_send()
    for c in stores:
        c.wait()
    for bit in bits:
        for j in range(0, seq, 2 * bit):
            for s in range(subs):
                dn_copy(bit, j, s).wait_send()


def mlp(length, own, others, tok, grads, wo, wu, wd, gain, fsdp):
    seq, rows, dim = tok.shape
    share = wu.shape[1]
    lo = 2
    hi = fsdp // lo
    piece = dim // (seq * fsdp)
    staged = piece % 16 == 0
    up_shape = (hi, seq, piece, share) if staged else (dim, share)
    sub = 256
    depth = seq if seq <= 4 else 2
    anywhere = pl.BlockSpec(memory_space=pl.ANY)
    vmem = pl.BlockSpec(memory_space=pltpu.VMEM)
    dma = pltpu.SemaphoreType.DMA

    def buf(*shape):
        return pltpu.VMEM(shape, bf16)

    return pl.pallas_call(
        functools.partial(mlp_kernel, seq, hi, lo, sub),
        out_shape=(
            jax.ShapeDtypeStruct((rows, dim), f32),
            jax.ShapeDtypeStruct((rows, dim), f32),
            jax.ShapeDtypeStruct((8, dim), f32),
            jax.ShapeDtypeStruct((seq, rows, dim), bf16),
            jax.ShapeDtypeStruct((seq, rows, dim), bf16),
            jax.ShapeDtypeStruct(up_shape, bf16),
            jax.ShapeDtypeStruct((share, dim), bf16),
        ),
        in_specs=[pl.BlockSpec(memory_space=pltpu.SMEM)] + [anywhere] * 7 + [vmem],
        out_specs=(anywhere, anywhere, vmem, anywhere, anywhere, anywhere, anywhere),
        scratch_shapes=[
            buf(depth, seq, rows, dim // seq),
            buf(depth, rows, dim),
            buf(dim, dim),
            buf(dim, share),
            buf(share, dim),
            buf(seq * rows, dim),
            buf(seq * rows, dim),
            buf(seq * rows, share),
            buf(seq * rows, share),
            buf(seq, rows, dim),
            buf(max(seq - 1, 1), rows, dim),
            pltpu.VMEM((rows, dim), f32),
            pltpu.VMEM((rows, dim), f32),
            buf(seq, fsdp, piece, share) if staged else buf(dim, share),
            buf(share, dim),
            dma((depth, seq + 1)),
            dma((3,)),
            dma((seq,)),
            dma((seq, rows // sub)),
            dma((seq, rows // sub)),
            dma((seq, rows // sub)),
            dma((seq, rows // sub)),
            dma((seq,)),
            dma((5,)),
        ]
        + ([buf(*up_shape), buf(*up_shape), dma((2, hi)), dma((2, hi))] if staged else []),
        compiler_params=pltpu.CompilerParams(collective_id=2, has_side_effects=True, vmem_limit_bytes=62 << 20),
        cost_estimate=pl.CostEstimate(
            flops=2 * rows * seq * dim * (dim + 6 * share), bytes_accessed=32 << 20, transcendentals=rows * seq * share
        ),
        name="mlp",
    )(length, own, others, tok, grads, wo, wu, wd, gain)


def emit_kernel(*refs):
    count = len(refs) // 3
    ins, outs, bufs = refs[:count], refs[count : 2 * count], refs[2 * count : 3 * count]
    sems = refs[3 * count]
    reads = [pltpu.make_async_copy(a, b, sems.at[0, i]) for i, (a, b) in enumerate(zip(ins, bufs))]
    writes = [pltpu.make_async_copy(a, b, sems.at[1, i]) for i, (a, b) in enumerate(zip(bufs, outs))]
    for c in reads:
        c.start()
    for read, write in zip(reads, writes):
        read.wait()
        write.start()
    for c in writes:
        c.wait()


def emit(*values):
    count = len(values)
    anywhere = pl.BlockSpec(memory_space=pl.ANY)
    return pl.pallas_call(
        emit_kernel,
        out_shape=tuple(jax.ShapeDtypeStruct(v.shape, v.dtype) for v in values),
        in_specs=[anywhere] * count,
        out_specs=(anywhere,) * count,
        scratch_shapes=[pltpu.VMEM(v.shape, v.dtype) for v in values] + [pltpu.SemaphoreType.DMA((2, count))],
        compiler_params=pltpu.CompilerParams(vmem_limit_bytes=62 << 20),
        name="emit",
    )(*values)


def body(
    tokens,
    lengths,
    state_init,
    w_qkv,
    w_out,
    w_up,
    w_down,
    norm_attn,
    norm_mlp,
    rel_bias,
    state_query,
    gate_bias,
    out_grad,
    state_grad,
):
    seq_count = lax.axis_size("seq")
    fsdp_count = lax.axis_size("fsdp")
    seq_at = lax.axis_index("seq")
    heads = H // seq_count
    width = heads * DH
    tok_rows, dim = tokens.shape[1:]
    rows = tok_rows * seq_count
    hidden_all = w_up.shape[1]
    share = hidden_all // (seq_count * fsdp_count)

    piece = dim // (seq_count * fsdp_count)
    all_tokens, all_grad, qkv_w, gain_attn, gain_mlp, own_out, up_w, normed, qkv = gather_start(
        tokens[0],
        out_grad[0],
        w_qkv,
        norm_attn.reshape(1, -1),
        norm_mlp.reshape(1, -1),
        w_out.reshape(2, w_out.shape[0] // 2, dim),
        w_up,
        seq_count,
        fsdp_count,
    )
    qkv_w = qkv_w.reshape(dim, 3 * width)
    up_w = up_w.reshape(dim, hidden_all // seq_count)

    bias = bias_vector(rel_bias)

    attended, others, out_w, down_w, final_memory, mem, upd, lse, slse = attend(
        qkv,
        state_init[0],
        lengths,
        state_query,
        gate_bias,
        bias,
        own_out,
        w_down,
        heads,
        seq_count,
        fsdp_count,
    )
    out_w = out_w.reshape(dim, dim)
    down_w = down_w.reshape(fsdp_count * share, dim)
    mid_here, dmid, mlp_gain_grad, dbranch, mlp_parts, up_grad, down_grad = mlp(
        lengths, attended, others, all_tokens, all_grad, out_w, up_w, down_w, gain_mlp, fsdp_count
    )
    span = fsdp_count // seq_count
    if up_grad.ndim == 2:
        up_grad = up_grad.reshape(seq_count, fsdp_count, piece, hidden_all // seq_count)
    dqkv, small, up_part, down_total, out_part, output = attend_back(
        qkv,
        dbranch.reshape(rows, dim),
        out_w,
        attended,
        mem,
        upd,
        lse,
        slse,
        state_grad[0],
        lengths,
        state_query,
        gate_bias,
        bias,
        up_grad,
        down_grad.reshape(seq_count, span * share, dim),
        mlp_parts,
        mid_here,
        seq_count,
        fsdp_count,
    )
    tokens_grad, qkv_part, down_part, dquery, grad_gate, grad_table, attn_gain_grad, mlp_gain_grad = finish(
        dqkv,
        qkv_w,
        normed,
        down_total,
        small,
        mlp_gain_grad,
        tokens[0],
        dmid,
        gain_attn,
        seq_count,
        fsdp_count,
    )
    big = (output, final_memory, tokens_grad, qkv_part, out_part, up_part, down_part)
    little = (dquery, grad_gate, grad_table, attn_gain_grad, mlp_gain_grad)
    output, final_memory, tokens_grad, qkv_part, out_part, up_part, down_part, *little = emit(*big, *little)
    dquery, grad_gate, grad_table, attn_gain_grad, mlp_gain_grad = little
    output = output[None]
    tokens_grad = tokens_grad[None]
    if up_part.ndim == 3:
        up_part = up_part.reshape(seq_count, piece, fsdp_count, share)
        up_part = jnp.transpose(up_part, (1, 2, 0, 3)).reshape(piece, hidden_all)
    dquery = dquery.reshape(heads, DH, DH)
    attn_gain_grad = attn_gain_grad.reshape(piece)
    mlp_gain_grad = mlp_gain_grad.reshape(piece)
    return (
        output,
        final_memory[None],
        tokens_grad,
        qkv_part,
        out_part,
        up_part,
        down_part,
        attn_gain_grad,
        mlp_gain_grad,
        grad_table,
        dquery,
        grad_gate,
    )


def solution(mesh):
    placed = (
        P("fsdp", "seq", None),
        P("fsdp"),
        P("fsdp", None, "seq"),
        P("fsdp", None),
        P("fsdp", None),
        P("fsdp", None),
        P("fsdp", None),
        P("fsdp"),
        P("fsdp"),
        P("seq", None),
        P("seq", None, None),
        P("seq", None),
        P("fsdp", "seq", None),
        P("fsdp", None, "seq"),
    )
    return jax.shard_map(
        body,
        mesh=mesh,
        in_specs=placed,
        out_specs=(
            P("fsdp", "seq", None),
            P("fsdp", None, "seq"),
            P("fsdp", "seq", None),
            P(("seq", "fsdp"), None),
            P(("seq", "fsdp"), None),
            P(("seq", "fsdp"), None),
            P(("seq", "fsdp"), None),
            P(("seq", "fsdp")),
            P(("seq", "fsdp")),
            P("seq", None),
            P("seq", None, None),
            P("seq", None),
        ),
        check_vma=False,
    )
```

```python
import functools
import math

import jax
import jax.numpy as jnp
import numpy as np
from jax import lax
from jax.experimental import pallas as pl
from jax.experimental.pallas import tpu as pltpu
from jax.sharding import PartitionSpec as P

H = 8
DH = 128
BLOCK = 512
STATE_VECTORS = 512
QTILE = 256
SPAN = BLOCK + QTILE

EPSILON = 1e-06
BUCKET_EDGES = (19, 21, 24, 27, 31, 35, 40, 46, 52, 59, 67, 77, 87, 99, 113)
BUCKETS = 32
LOG2E = math.log2(math.e)
SCALE = DH ** (-0.5)
NEAR = 384

f32 = jnp.float32
bf16 = jnp.bfloat16
MESH = pl.DeviceIdType.MESH


def bucket_of(distance):
    return np.minimum(distance, 16) + (distance[..., None] >= np.array(BUCKET_EDGES)).sum(-1)


def tile_distance():
    rows = np.arange(QTILE)[:, None]
    cols = np.arange(SPAN)[None, :]
    return rows + BLOCK - cols


def bias_vector(table):
    distance = BLOCK - np.arange(2 * BLOCK)
    inside = (distance >= 0) & (distance < BLOCK)
    bucket = np.where(inside, bucket_of(np.clip(distance, 0, BLOCK)), BUCKETS)
    member = jnp.asarray((np.arange(BUCKETS)[:, None] == bucket[None]).astype(np.float32))
    total = jnp.dot(table, member, precision=lax.Precision.HIGHEST, preferred_element_type=f32)
    return jnp.where(jnp.asarray(inside)[None], total * LOG2E, -jnp.inf)


def tile_bias(vector_ref, head):
    wide = jnp.broadcast_to(vector_ref[head : head + 1, :], (QTILE, 2 * BLOCK))
    return pltpu.roll(wide, 0, 1, stride=1, stride_axis=0)[:, :SPAN]


def dot(a, b):
    return jnp.dot(a, b, preferred_element_type=f32)


def dot_t(a, b):
    return lax.dot_general(a, b, (((1,), (1,)), ((), ())), preferred_element_type=f32)


def t_dot(a, b):
    return lax.dot_general(a, b, (((0,), (0,)), ((), ())), preferred_element_type=f32)


def to_row(column):
    wide = jnp.broadcast_to(column, (column.shape[0], 128))
    return wide.T[0:1, :]


def context_pieces(tile):
    start = tile * QTILE
    pieces = []
    if start < BLOCK:
        pieces.append((0, start, BLOCK, 0))
    pieces.append((1, 0, start + QTILE, BLOCK - start))
    return pieces


def softmax_parts(scores):
    top = functools.reduce(jnp.maximum, [jnp.max(s, axis=-1, keepdims=True) for s in scores])
    raised = [jnp.exp2(s - top) for s in scores]
    total = functools.reduce(jnp.add, [jnp.sum(e, axis=-1, keepdims=True) for e in raised])
    return raised, total, top + jnp.log2(total)


def line_gather(hi, lo, slot, own, z_send, z_recv, y_send, y_recv):
    f = lax.axis_index("fsdp")
    z, y = f // lo, f % lo

    def copy(i, origin, target, send, recv, first=False):
        ref = slot(i, origin)
        return pltpu.make_async_remote_copy(
            src_ref=own(i) if first else ref,
            dst_ref=ref,
            send_sem=send,
            recv_sem=recv,
            device_id={"fsdp": target},
            device_id_type=MESH,
        )

    def right(i, t):
        return copy(i, (z - t) * lo + y, (z + 1) * lo + y, z_send.at[i, 0, t], z_recv.at[i, 0, t], t == 0)

    def left(i, t):
        return copy(i, (z + t) * lo + y, (z - 1) * lo + y, z_send.at[i, 1, t], z_recv.at[i, 1, t], t == 0)

    def across(i, d):
        return copy(
            i, (z + d) * lo + y, z * lo + 1 - y, y_send.at[i, d + hi - 1], y_recv.at[i, d + hi - 1], d == 0
        )

    def start(i):
        pl.when(z + 1 < hi)(lambda: right(i, 0).start())
        pl.when(z >= 1)(lambda: left(i, 0).start())
        across(i, 0).start()

    def step(i, t):
        @pl.when(z - 1 - t >= 0)
        def _():
            copy(i, (z - 1 - t) * lo + y, f, z_send.at[i, 0, t], z_recv.at[i, 0, t]).wait_recv()
            if t + 1 < hi - 1:
                pl.when(z + 1 < hi)(lambda: right(i, t + 1).start())
            across(i, -1 - t).start()

        @pl.when(z + 1 + t < hi)
        def _():
            copy(i, (z + 1 + t) * lo + y, f, z_send.at[i, 1, t], z_recv.at[i, 1, t]).wait_recv()
            if t + 1 < hi - 1:
                pl.when(z >= 1)(lambda: left(i, t + 1).start())
            across(i, 1 + t).start()

    def arrive(i):
        for d in range(1 - hi, hi):

            @pl.when((z + d >= 0) & (z + d < hi))
            def _():
                copy(
                    i, (z + d) * lo + 1 - y, f, y_send.at[i, d + hi - 1], y_recv.at[i, d + hi - 1]
                ).wait_recv()

    def drain(i):
        for d in range(1 - hi, hi):

            @pl.when((z + d >= 0) & (z + d < hi))
            def _():
                across(i, d).wait_send()

        for t in range(hi - 1):

            @pl.when((z + 1 < hi) & (z - t >= 0))
            def _():
                right(i, t).wait_send()

            @pl.when((z >= 1) & (z + t < hi))
            def _():
                left(i, t).wait_send()

    return start, step, arrive, drain


def line_sems(count, hi):
    dma = pltpu.SemaphoreType.DMA
    return [dma((count, 2, hi)), dma((count, 2, hi)), dma((count, 2 * hi)), dma((count, 2 * hi))]


def greet(seq_targets, hi, lo):
    me = lax.axis_index("seq")
    f = lax.axis_index("fsdp")
    z, y = f // lo, f % lo
    barrier = pltpu.get_barrier_semaphore()
    for k in seq_targets:
        pl.semaphore_signal(barrier, inc=1, device_id={"seq": me ^ k}, device_id_type=MESH)
    near = (lax.rem(z + 1, hi) * lo + y, lax.rem(z + hi - 1, hi) * lo + y, z * lo + 1 - y)
    for target in near:
        pl.semaphore_signal(barrier, inc=1, device_id={"fsdp": target}, device_id_type=MESH)
    pl.semaphore_wait(barrier, len(seq_targets) + len(near))


def attend_kernel(
    heads,
    seq,
    hi,
    lo,
    length_ref,
    qkv_ref,
    init_ref,
    query_ref,
    gate_ref,
    vector_ref,
    own_out_ref,
    down_hbm,
    att_out,
    others_ref,
    outs_ref,
    downs_ref,
    final_ref,
    mem_out,
    upd_out,
    lse_ref,
    slse_ref,
    memory_ref,
    bias_ref,
    att_ref,
    mem_ref,
    upd_ref,
    own_down_ref,
    store_sem,
    own_sem,
    att_send,
    att_recv,
    out_send,
    out_recv,
    z_send,
    z_recv,
    y_send,
    y_recv,
):
    me = lax.axis_index("seq")
    f = lax.axis_index("fsdp")
    length = length_ref[0]
    width = heads * DH
    scale2 = SCALE * LOG2E
    blocks = seq
    bits = [1 << i for i in range(seq.bit_length() - 1)]
    held = own_down_ref.shape[0]
    down_load = pltpu.make_async_copy(
        down_hbm.at[pl.ds(pl.multiple_of(me * held, held), held)], own_down_ref, own_sem.at[2]
    )
    down_load.start()
    greet(bits, hi, lo)
    down_load.wait()

    own_copies = [
        pltpu.make_async_copy(own_down_ref, downs_ref.at[f], own_sem.at[0]),
        pltpu.make_async_copy(own_out_ref, outs_ref.at[:, me % 2], own_sem.at[1]),
    ]
    for c in own_copies:
        c.start()

    def lowest(k):
        return k & -k

    def out_copy(sending):
        half = me % 2 if sending else 1 - me % 2
        return pltpu.make_async_remote_copy(
            src_ref=own_out_ref,
            dst_ref=outs_ref.at[:, half],
            send_sem=out_send,
            recv_sem=out_recv,
            device_id={"seq": me ^ 1},
            device_id_type=MESH,
        )

    def att_copy(k, b):
        bit = lowest(k)
        came = k ^ bit
        here = pl.ds(pl.multiple_of((b ^ me) * BLOCK, BLOCK), BLOCK)
        there = pl.ds(pl.multiple_of((b ^ me ^ bit) * BLOCK, BLOCK), BLOCK)
        src = others_ref.at[came, here] if came else att_ref.at[here]
        return pltpu.make_async_remote_copy(
            src_ref=src,
            dst_ref=others_ref.at[k, there],
            send_sem=att_send.at[k, b],
            recv_sem=att_recv.at[k, b],
            device_id={"seq": me ^ bit},
            device_id_type=MESH,
        )

    def att_arrival(k, b):
        here = pl.ds(pl.multiple_of((b ^ me) * BLOCK, BLOCK), BLOCK)
        return pltpu.make_async_remote_copy(
            src_ref=others_ref.at[k, here],
            dst_ref=others_ref.at[k, here],
            send_sem=att_send.at[k, b],
            recv_sem=att_recv.at[k, b],
            device_id={"seq": me},
            device_id_type=MESH,
        )

    passing = sorted([k for k in range(2, seq, 2)], key=lambda k: (bin(k).count("1"), -k))

    def onward(k, send):
        for bit in reversed(bits):
            if bit < lowest(k):
                send(k | bit)

    start, step, arrive, drain = line_gather(
        hi, lo, lambda i, origin: downs_ref.at[origin], lambda i: own_down_ref, z_send, z_recv, y_send, y_recv
    )

    start(0)
    out_copy(True).start()
    memory_ref[...] = init_ref[...].astype(f32)
    for head in range(heads):
        bias_ref[head] = tile_bias(vector_ref, head)

    def block_stores(block):
        at = pl.ds(pl.multiple_of((block ^ me) * BLOCK, BLOCK), BLOCK)
        pairs = (
            (att_ref.at[at], att_out.at[at]),
            (mem_ref.at[block], mem_out.at[block]),
            (upd_ref.at[block], upd_out.at[block]),
        )
        return [pltpu.make_async_copy(a, b, store_sem.at[i, block]) for i, (a, b) in enumerate(pairs)]

    @pl.loop(0, blocks)
    def _(block):
        cur_at = pl.multiple_of((block ^ me) * BLOCK, BLOCK)
        prev_at = pl.multiple_of((jnp.maximum(block - 1, 0) ^ me) * BLOCK, BLOCK)
        cur_ref = qkv_ref.at[pl.ds(cur_at, BLOCK)]
        prev_ref = qkv_ref.at[pl.ds(prev_at, BLOCK)]
        for t in range(min(hi - 1, blocks - 1)):
            pl.when(block == t + 1)(lambda t=t: step(0, t))

        live_block = block * BLOCK < length
        for head in range(heads):
            own = slice(head * DH, (head + 1) * DH)
            memory = memory_ref[:, own]
            low = memory.astype(bf16)
            mem_ref[block, :, own] = memory
            refs = (prev_ref, cur_ref)
            key_cols = slice(width + head * DH, width + (head + 1) * DH)
            value_cols = slice(2 * width + head * DH, 2 * width + (head + 1) * DH)
            for tile in range(BLOCK // QTILE):
                rows = slice(tile * QTILE, (tile + 1) * QTILE)
                query = cur_ref[rows, own]
                scores, values = [], []
                for which, at, end, col in context_pieces(tile):
                    s = dot_t(query, refs[which][at:end, key_cols])
                    position = (block - 1 + which) * BLOCK + at + lax.broadcasted_iota(jnp.int32, (1, end - at), 1)
                    live = (position >= 0) & (position < length)
                    s = s * scale2 + bias_ref[head, :, col : col + end - at]
                    scores.append(jnp.where(live, s, -jnp.inf))
                    values.append(refs[which][at:end, value_cols])
                scores.append(dot_t(query, low) * scale2)
                values.append(low)
                raised, total, lse = softmax_parts(scores)
                out = functools.reduce(jnp.add, [dot(e.astype(bf16), v) for e, v in zip(raised, values)])
                att_ref[pl.ds(cur_at + tile * QTILE, QTILE), own] = (out / total).astype(bf16)
                lse_ref[head : head + 1, pl.ds(pl.multiple_of(block * BLOCK, BLOCK) + tile * QTILE, QTILE)] = to_row(lse)
            own_key = cur_ref[:, key_cols]
            own_value = cur_ref[:, value_cols]
            squeries = dot(low, query_ref[head]).astype(bf16)
            position = block * BLOCK + lax.broadcasted_iota(jnp.int32, (1, BLOCK), 1)
            for tile in range(STATE_VECTORS // QTILE):
                rows = slice(tile * QTILE, (tile + 1) * QTILE)
                squery = squeries[rows]
                scores = [
                    dot_t(squery, low) * scale2,
                    jnp.where(position < length, dot_t(squery, own_key) * scale2, -jnp.inf),
                ]
                raised, total, lse = softmax_parts(scores)
                update = dot(raised[0].astype(bf16), low) + dot(raised[1].astype(bf16), own_value)
                update = update / total
                upd_ref[block, rows, own] = update
                slse_ref[head : head + 1, pl.ds(pl.multiple_of(block * BLOCK, BLOCK) + tile * QTILE, QTILE)] = to_row(
                    lse
                )
                forget = jax.nn.sigmoid(gate_ref[head : head + 1, :])
                old = memory[rows]
                memory_ref[rows, own] = jnp.where(live_block, forget * old + (1.0 - forget) * update, old)

        for bit in reversed(bits):
            att_copy(bit, block).start()
        for c in block_stores(block):
            c.start()

        @pl.when(block >= 1)
        def _():
            for k in passing:
                att_arrival(k, block - 1).wait_recv()
                onward(k, lambda target: att_copy(target, block - 1).start())

    final_ref[...] = memory_ref[...]
    for t in range(min(hi - 1, blocks - 1), hi - 1):
        step(0, t)
    for k in passing:
        att_arrival(k, blocks - 1).wait_recv()
        onward(k, lambda target: att_copy(target, blocks - 1).start())
    arrive(0)
    out_copy(False).wait_recv()
    for k in range(1, seq, 2):
        for b in range(blocks):
            att_arrival(k, b).wait_recv()
    for c in own_copies:
        c.wait()
    drain(0)
    for b in range(blocks):
        for c in block_stores(b):
            c.wait()
    out_copy(True).wait_send()
    for k in range(1, seq):
        for b in range(blocks):
            att_copy(k, b).wait_send()


def attend(qkv, init, length, state_query, gate, bias, own_out, w_down, heads, seq, fsdp):
    rows, width3 = qkv.shape
    width = heads * DH
    blocks = rows // BLOCK
    lo = 2
    hi = fsdp // lo
    dim = w_down.shape[1]
    held = w_down.shape[0] // seq
    anywhere = pl.BlockSpec(memory_space=pl.ANY)
    vmem = pl.BlockSpec(memory_space=pltpu.VMEM)
    dma = pltpu.SemaphoreType.DMA
    return pl.pallas_call(
        functools.partial(attend_kernel, heads, seq, hi, lo),
        out_shape=(
            jax.ShapeDtypeStruct((rows, width), bf16),
            jax.ShapeDtypeStruct((seq, rows, width), bf16),
            jax.ShapeDtypeStruct((fsdp, 2) + own_out.shape[1:], bf16),
            jax.ShapeDtypeStruct((fsdp, held, dim), bf16),
            jax.ShapeDtypeStruct((STATE_VECTORS, width), f32),
            jax.ShapeDtypeStruct((blocks, STATE_VECTORS, width), f32),
            jax.ShapeDtypeStruct((blocks, STATE_VECTORS, width), f32),
            jax.ShapeDtypeStruct((heads, rows), f32),
            jax.ShapeDtypeStruct((heads, blocks * STATE_VECTORS), f32),
        ),
        in_specs=[pl.BlockSpec(memory_space=pltpu.SMEM)] + [vmem] * 6 + [anywhere],
        out_specs=(anywhere, anywhere, anywhere, anywhere, vmem, anywhere, anywhere, vmem, vmem),
        scratch_shapes=[
            pltpu.VMEM((STATE_VECTORS, width), f32),
            pltpu.VMEM((heads, QTILE, SPAN), f32),
            pltpu.VMEM((rows, width), bf16),
            pltpu.VMEM((blocks, STATE_VECTORS, width), f32),
            pltpu.VMEM((blocks, STATE_VECTORS, width), f32),
            pltpu.VMEM((held, dim), bf16),
            dma((3, blocks)),
            dma((3,)),
            dma((seq, blocks)),
            dma((seq, blocks)),
            dma,
            dma,
        ]
        + line_sems(1, hi),
        compiler_params=pltpu.CompilerParams(collective_id=3, has_side_effects=True, vmem_limit_bytes=62 << 20),
        cost_estimate=pl.CostEstimate(
            flops=blocks * heads * 512 * 2400 * 128 * 4, bytes_accessed=16 << 20, transcendentals=10 << 20
        ),
        name="attend",
    )(length, qkv, init, state_query, gate, bias, own_out, w_down)


def line_reduce(hi, lo, block, total, from_y, from_z, z_send, z_recv, y_send, y_recv, loads=None):
    loads = loads or {}
    f = lax.axis_index("fsdp")
    z, y = f // lo, f % lo

    def remote(src, dst, send, recv, target):
        return pltpu.make_async_remote_copy(
            src_ref=src, dst_ref=dst, send_sem=send, recv_sem=recv, device_id={"fsdp": target}, device_id_type=MESH
        )

    def across(i, d):
        return remote(
            block(i, d * lo + 1 - y), from_y[i].at[d], y_send.at[i, d], y_recv.at[i, d], z * lo + 1 - y
        )

    def start(i):
        for d in range(hi):
            across(i, d).start()

    def combine(i):
        for d in range(hi):
            across(i, d).wait_recv()
            if i in loads:
                loads[i][d].wait()
                own = total[i].at[d]
            else:
                own = block(i, d * lo + y)
            total[i][d] = (own[...].astype(f32) + from_y[i][d].astype(f32)).astype(bf16)

    def hop(i, side, t, at, target):
        return remote(
            total[i].at[jnp.clip(at, 0, hi - 1)],
            from_z[i].at[side, t],
            z_send.at[i, side, t],
            z_recv.at[i, side, t],
            target,
        )

    def sending(t):
        d = t - (hi - 1 - z)
        m = hi - 1 - (t - z)
        return ((0, d, (d >= 0) & (d < z), z - 1), (1, m, (m > z) & (m < hi), z + 1))

    def zsend(i, t):
        for side, at, cond, target in sending(t):
            pl.when(cond)(lambda: hop(i, side, t, at, target * lo + y).start())

    def zrecv(i, t):
        d = t - (hi - 2 - z)
        m = hi - 1 - (t - (z - 1))
        for side, at, cond in ((0, d, (z + 1 < hi) & (d >= 0)), (1, m, (z > 0) & (m < hi))):

            @pl.when(cond)
            def _():
                hop(i, side, t, at, f).wait_recv()
                slot = jnp.clip(at, 0, hi - 1)
                total[i][slot] = (total[i][slot].astype(f32) + from_z[i][side, t].astype(f32)).astype(bf16)

    def drain_y(i):
        for d in range(hi):
            across(i, d).wait_send()

    def drain_z(i):
        for t in range(hi - 1):
            for side, at, cond, target in sending(t):
                pl.when(cond)(lambda: hop(i, side, t, at, f).wait_send())

    return start, combine, zsend, zrecv, drain_y, drain_z


def seq_levels(seq):
    bits = [1 << i for i in range(seq.bit_length() - 1)]
    slots = {}
    for bit in bits:
        for j in range(0, seq, 2 * bit):
            slots[bit, j] = len(slots)
    return bits, slots


def diagonal_sums(tile):
    rows, lanes = tile.shape
    wide = jnp.concatenate([tile, jnp.zeros((rows, lanes), f32)], axis=1)
    row = lax.broadcasted_iota(jnp.int32, wide.shape, 0)
    bit = 1
    while bit < rows:
        wide = jnp.where((row & bit) != 0, pltpu.roll(wide, 2 * lanes - bit, 1), wide)
        bit *= 2
    return jnp.sum(wide, axis=0, keepdims=True)


def attend_back_kernel(heads, seq, hi, lo, inside, length_ref, *refs):
    refs = list(refs)

    def take(count):
        taken = refs[:count]
        del refs[:count]
        return taken

    qkv_hbm, db_hbm, wout_hbm, att_hbm, mem_hbm, upd_hbm, lse_ref, slse_ref = take(8)
    sgrad_ref, query_ref, gate_ref, vector_ref, up_ref, down_ref, mo_ref, mid_hbm = take(8)
    ow_in = None if inside else take(1)[0]
    dqkv_out, small_ref, upart_ref, dtotal_ref, opart_ref, output_ref = take(6)
    qkv_ref, db_ref, att_ref, mem_ref, upd_ref, mid_ref, dqkv_ref, wout_ref = take(8)
    dmem_ref, dnext_ref, dctx_ref, bias_ref, near_ref, far_ref, dout_ref, ow_buf = take(8)
    moved, to, tu, yo, yu, yd, zo, zu, xu, mo_low, mo_in = take(11)
    z_send, z_recv, y_send, y_recv, m_send, m_recv, e_send, e_recv, x_send, x_recv = take(10)
    load_sem, block_sem, up_sem, mo_sem, out_sem = take(5)
    ow_ref = ow_buf if inside else ow_in

    me = lax.axis_index("seq")
    f = lax.axis_index("fsdp")
    z, y = f // lo, f % lo
    blocks = seq
    length = length_ref[0]
    width = heads * DH
    scale2 = SCALE * LOG2E
    tok_rows = mid_ref.shape[0]
    share = dtotal_ref.shape[1]
    bits, slots = seq_levels(seq)

    def chunk_at(block):
        return pl.ds(pl.multiple_of((block ^ me) * BLOCK, BLOCK), BLOCK)

    def block_loads(block):
        at = chunk_at(block)
        pairs = (
            (qkv_hbm.at[at], qkv_ref.at[at]),
            (mem_hbm.at[block], mem_ref.at[block]),
            (upd_hbm.at[block], upd_ref.at[block]),
        )
        return [pltpu.make_async_copy(a, b, block_sem.at[i, block]) for i, (a, b) in enumerate(pairs)]

    loads = [
        pltpu.make_async_copy(att_hbm, att_ref, load_sem.at[0]),
        pltpu.make_async_copy(db_hbm, db_ref, load_sem.at[1]),
        pltpu.make_async_copy(down_ref.at[me], moved.at[me], load_sem.at[2]),
        pltpu.make_async_copy(mid_hbm, mid_ref, load_sem.at[3]),
        pltpu.make_async_copy(
            wout_hbm.at[pl.ds(pl.multiple_of(me * width, width), width)], wout_ref, load_sem.at[4]
        ),
    ]
    up_loads = [
        pltpu.make_async_copy(up_ref.at[d] if inside else up_ref.at[:, d * lo + y], tu.at[d], up_sem.at[d])
        for d in range(hi)
    ]
    mo_loads = [pltpu.make_async_copy(mo_ref.at[j], mo_low.at[j // 2], mo_sem.at[j // 2]) for j in range(0, seq, 2)]
    for c in up_loads + loads[:2] + loads[4:] + block_loads(blocks - 1) + mo_loads:
        c.start()
    for b in reversed(range(blocks - 1)):
        for c in block_loads(b):
            c.start()
    for c in loads[2:4]:
        c.start()
    greet(list(range(1, seq)), hi, lo)

    def mo_copy(bit, j):
        slot = slots[bit, j]
        return pltpu.make_async_remote_copy(
            src_ref=mo_ref.at[j ^ bit] if bit == 1 else mo_low.at[(j ^ bit) // 2],
            dst_ref=mo_in.at[slot],
            send_sem=m_send.at[slot],
            recv_sem=m_recv.at[slot],
            device_id={"seq": me ^ bit},
            device_id_type=MESH,
        )

    def move_copy(k):
        return pltpu.make_async_remote_copy(
            src_ref=down_ref.at[me ^ k],
            dst_ref=moved.at[me],
            send_sem=e_send.at[k],
            recv_sem=e_recv.at[k],
            device_id={"seq": me ^ k},
            device_id_type=MESH,
        )

    def move_arrival(k):
        return pltpu.make_async_remote_copy(
            src_ref=down_ref.at[me],
            dst_ref=moved.at[me ^ k],
            send_sem=e_send.at[k],
            recv_sem=e_recv.at[k],
            device_id={"seq": me},
            device_id_type=MESH,
        )

    def block_of(i, target):
        if i == 0:
            return ow_ref.at[target]
        if i == 1:
            return up_ref.at[:, target]
        return moved.at[target % seq, pl.ds(pl.multiple_of((target // seq) * share, share), share)]

    start, combine, zsend, zrecv, drain_y, drain_z = line_reduce(
        hi,
        lo,
        block_of,
        (to, tu, dtotal_ref),
        (yo, yu, yd),
        (zo, zu),
        z_send,
        z_recv,
        y_send,
        y_recv,
        {1: up_loads},
    )

    def exchange(k, sending):
        return pltpu.make_async_remote_copy(
            src_ref=tu.at[z, me ^ k] if sending else tu.at[z, me],
            dst_ref=xu.at[me] if sending else xu.at[me ^ k],
            send_sem=x_send.at[k],
            recv_sem=x_recv.at[k],
            device_id={"seq": me ^ k if sending else me},
            device_id_type=MESH,
        )

    if not inside:
        start(1)
    for k in reversed(range(1, seq)):
        move_copy(k).start()
    for j in range(seq - 1, 0, -2):
        mo_copy(1, j ^ 1).start()
    if inside:
        for c in up_loads:
            c.wait()
        zsend(1, 0)
    dmem_ref[...] = sgrad_ref[...].astype(f32)
    dnext_ref[...] = jnp.zeros_like(dnext_ref)
    small_ref[...] = jnp.zeros_like(small_ref)
    near_ref[...] = jnp.zeros_like(near_ref)
    far_ref[...] = jnp.zeros_like(far_ref)
    for head in range(heads):
        bias_ref[head] = tile_bias(vector_ref, head).T
    for c in loads[:2] + loads[4:]:
        c.wait()
    if inside:
        full = t_dot(att_ref[...], db_ref[...]).astype(bf16)
        ow_buf[...] = full.reshape(ow_buf.shape)
    start(0)

    def mo_step(j):
        mo_loads[j // 2].wait()
        for bit in bits:
            if j & bit:
                mo_copy(bit, j ^ bit).start()
                break
            mo_copy(bit, j).wait_recv()
            own = mo_low[j // 2].astype(f32)
            mo_low[j // 2] = (own + mo_in[slots[bit, j]].astype(f32)).astype(bf16)

    def down_ready():
        for k in range(1, seq):
            move_arrival(k).wait_recv()
        loads[2].wait()
        start(2)

    def up_done():
        for k in range(1, seq):
            exchange(k, True).start()

    def zstep(i, t):
        zrecv(i, t)
        if t + 1 < hi - 1:
            zsend(i, t + 1)

    jobs = [lambda j=j: mo_step(j) for j in range(seq - 2, 0, -2)]
    if not inside:
        jobs.append(lambda: (combine(1), zsend(1, 0)))
    jobs.append(lambda: (zstep(1, 0), combine(0), zsend(0, 0)))
    for t in range(1, hi - 1):
        jobs.append(lambda t=t: zstep(1, t))
        if t == 1:
            jobs.append(lambda: down_ready())
    jobs.append(lambda: up_done())
    jobs += [lambda t=t: zstep(0, t) for t in range(hi - 1)]
    points = blocks * heads - 1

    dq_row = heads * DH
    block_loads(blocks - 1)[0].wait()

    @pl.loop(0, blocks)
    def _(step):
        block = blocks - 1 - step
        pl.when(block >= 1)(lambda: block_loads(jnp.maximum(block - 1, 0))[0].wait())
        for c in block_loads(block)[1:]:
            c.wait()
        cur_at = pl.multiple_of((block ^ me) * BLOCK, BLOCK)
        prev_at = pl.multiple_of((jnp.maximum(block - 1, 0) ^ me) * BLOCK, BLOCK)
        base = pl.multiple_of(block * BLOCK, BLOCK)
        cur_ref = qkv_ref.at[pl.ds(cur_at, BLOCK)]
        prev_ref = qkv_ref.at[pl.ds(prev_at, BLOCK)]
        live_block = block * BLOCK < length
        refs = (prev_ref, cur_ref)
        dout_ref[...] = dot_t(db_ref[pl.ds(cur_at, BLOCK)], wout_ref[...]).astype(bf16)
        for head in range(heads):
            for n, job in enumerate(jobs[:points]):
                if (n + 1) % heads == head:
                    pl.when(step == (n + 1) // heads)(lambda job=job: (job(), None)[1])
            own = slice(head * DH, (head + 1) * DH)
            key_cols = slice(width + head * DH, width + (head + 1) * DH)
            value_cols = slice(2 * width + head * DH, 2 * width + (head + 1) * DH)
            memory = mem_ref[block, :, own]
            update = upd_ref[block, :, own]
            low = memory.astype(bf16)
            forget = jax.nn.sigmoid(gate_ref[head : head + 1, :])
            dmem = dmem_ref[:, own]
            dupd = jnp.where(live_block, (1.0 - forget) * dmem, 0.0).astype(bf16)
            gone = jnp.where(live_block, dmem * (memory - update), 0.0)
            small_ref[dq_row + head : dq_row + head + 1, :] += jnp.sum(gone, axis=0, keepdims=True)
            dmem_new = jnp.where(live_block, forget * dmem, dmem)
            own_key = cur_ref[:, key_cols]
            own_value = cur_ref[:, value_cols]
            squeries = dot(low, query_ref[head]).astype(bf16)
            sdelta = jnp.sum((dupd.astype(f32) * update).T, axis=0, keepdims=True)
            slse = slse_ref[head : head + 1, pl.ds(base, BLOCK)]
            dsquery = jnp.zeros((STATE_VECTORS, DH), f32)
            dkey = []
            dvalue = []
            for part in range(2 * STATE_VECTORS // QTILE):
                own_part = part >= STATE_VECTORS // QTILE
                at = (part % (STATE_VECTORS // QTILE)) * QTILE
                keys = (own_key if own_part else low)[at : at + QTILE]
                values = (own_value if own_part else low)[at : at + QTILE]
                s = dot_t(keys, squeries) * scale2 - slse
                if own_part:
                    position = block * BLOCK + at + lax.broadcasted_iota(jnp.int32, (QTILE, 1), 0)
                    s = jnp.where(position < length, s, -jnp.inf)
                p = jnp.exp2(s)
                dp = dot_t(values, dupd)
                ds = (p * (dp - sdelta)).astype(bf16)
                dvalue.append(dot(p.astype(bf16), dupd))
                dkey.append(dot(ds, squeries))
                dsquery += t_dot(ds, keys)
            half = STATE_VECTORS // QTILE
            dlow = [dvalue[i] + dkey[i] * SCALE for i in range(half)]
            dctx_ref[0, 0:BLOCK] = jnp.zeros((BLOCK, DH), f32)
            dctx_ref[1, 0:BLOCK] = jnp.zeros((BLOCK, DH), f32)
            for i in range(half):
                rows = slice(BLOCK + i * QTILE, BLOCK + (i + 1) * QTILE)
                old = slice(i * QTILE, (i + 1) * QTILE)
                dctx_ref[0, rows] = dkey[half + i] * SCALE + dnext_ref[0, old, own]
                dctx_ref[1, rows] = dvalue[half + i] + dnext_ref[1, old, own]
            dsq = (dsquery * SCALE).astype(bf16)
            small_ref[head * DH : (head + 1) * DH, :] += t_dot(low, dsq)
            dmem_ref[:, own] = dmem_new + dot_t(dsq, query_ref[head])
            for tile in range(BLOCK // QTILE):
                rows = slice(tile * QTILE, (tile + 1) * QTILE)
                here = pl.ds(cur_at + tile * QTILE, QTILE)
                query = cur_ref[rows, own]
                dout = dout_ref[rows, own]
                lse = lse_ref[head : head + 1, pl.ds(base + tile * QTILE, QTILE)]
                delta = jnp.sum((dout.astype(f32) * att_ref[here, own].astype(f32)).T, axis=0, keepdims=True)
                dq = jnp.zeros((QTILE, DH), f32)
                for which, first, end, col in context_pieces(tile):
                    for at in range(first, end, QTILE):
                        keys = refs[which][at : at + QTILE, key_cols]
                        values = refs[which][at : at + QTILE, value_cols]
                        band = col + at - first
                        position = (block - 1 + which) * BLOCK + at + lax.broadcasted_iota(jnp.int32, (QTILE, 1), 0)
                        live = (position >= 0) & (position < length)
                        s = dot_t(keys, query) * scale2 + bias_ref[head, band : band + QTILE, :] - lse
                        p = jnp.exp2(jnp.where(live, s, -jnp.inf))
                        dp = dot_t(values, dout)
                        ds = (p * (dp - delta)).astype(bf16)
                        wide = ds.astype(f32)
                        edge = min(max(SPAN - NEAR - band, 0), QTILE)
                        if edge:
                            far_ref[head] += functools.reduce(jnp.add, [wide[i : i + 8] for i in range(0, edge, 8)])
                        if edge < QTILE:
                            at_near = band + edge - (SPAN - NEAR)
                            near_ref[head, at_near : at_near + QTILE - edge] += wide[edge:]
                        into = slice(which * BLOCK + at, which * BLOCK + at + QTILE)
                        dctx_ref[1, into] += dot(p.astype(bf16), dout)
                        dctx_ref[0, into] += dot(ds, query) * SCALE
                        dq += t_dot(ds, keys)
                for part in range(half):
                    keys = low[part * QTILE : (part + 1) * QTILE]
                    s = dot_t(keys, query) * scale2 - lse
                    p = jnp.exp2(s)
                    dp = dot_t(keys, dout)
                    ds = (p * (dp - delta)).astype(bf16)
                    dlow[part] += dot(p.astype(bf16), dout) + dot(ds, query) * SCALE
                    dq += t_dot(ds, keys)
                dqkv_ref[here, own] = (dq * SCALE).astype(bf16)
            for part in range(half):
                dmem_ref[part * QTILE : (part + 1) * QTILE, own] += dlow[part]
            dnext_ref[0, :, own] = dctx_ref[0, 0:BLOCK]
            dnext_ref[1, :, own] = dctx_ref[1, 0:BLOCK]
            dqkv_ref[pl.ds(cur_at, BLOCK), key_cols] = dctx_ref[0, BLOCK:].astype(bf16)
            dqkv_ref[pl.ds(cur_at, BLOCK), value_cols] = dctx_ref[1, BLOCK:].astype(bf16)

    dqkv_store = pltpu.make_async_copy(dqkv_ref, dqkv_out, out_sem)
    dqkv_store.start()
    for job in jobs[points:]:
        job()
    member = bucket_members()
    lane = lax.broadcasted_iota(jnp.int32, (1, DH), 1)
    for head in range(heads):
        sums = jnp.broadcast_to(diagonal_sums(near_ref[head]), (8, 2 * QTILE))
        table = jnp.dot(sums, member, precision=lax.Precision.HIGHEST, preferred_element_type=f32)[0:1]
        total = jnp.sum(jnp.sum(far_ref[head], axis=0, keepdims=True), axis=1, keepdims=True)
        row = dq_row + heads + head
        small_ref[row : row + 1, :] = table + jnp.where(lane == BUCKETS - 1, total, 0.0)
        row = dq_row + head
        forget = jax.nn.sigmoid(gate_ref[head : head + 1, :])
        small_ref[row : row + 1, :] = small_ref[row : row + 1, :] * forget * (1.0 - forget)
    loads[3].wait()
    mo_loads[0].wait()
    for bit in bits:
        mo_copy(bit, 0).wait_recv()
    step = 128
    for r in range(0, tok_rows, step):
        at = slice(r, r + step)
        value = mid_ref[at] + mo_low[0, at].astype(f32)
        for bit in bits:
            value = value + mo_in[slots[bit, 0], at].astype(f32)
        position = me * tok_rows + r + lax.broadcasted_iota(jnp.int32, (step, 1), 0)
        output_ref[at] = (value * jnp.where(position < length, 1.0, 0.0)).astype(bf16)
    combine(2)
    opart_ref[...] = to[z].astype(f32)
    for k in range(1, seq):
        exchange(k, False).wait_recv()
    xu[me] = tu[z, me]
    write_parts(upart_ref, xu, seq, share)
    for i in (0, 2) if inside else (0, 1, 2):
        drain_y(i)
    for i in range(2):
        drain_z(i)
    for bit in bits:
        for j in range(0, seq, 2 * bit):
            mo_copy(bit, j).wait_send()
    for k in range(1, seq):
        move_copy(k).wait_send()
        exchange(k, True).wait_send()
    dqkv_store.wait()


def bucket_members():
    shape = (2 * QTILE, DH)
    row = lax.broadcasted_iota(jnp.int32, shape, 0)
    lane = lax.broadcasted_iota(jnp.int32, shape, 1)
    distance = jnp.where(row < QTILE, row, row - 2 * QTILE) + NEAR - QTILE
    bucket = jnp.minimum(distance, 16)
    for edge in BUCKET_EDGES:
        bucket = bucket + jnp.where(distance >= edge, 1, 0)
    inside = (distance >= 0) & (distance < BLOCK) & (bucket == lane)
    return jnp.where(inside, 1.0, 0.0)


def write_parts(out_ref, pieces, seq, unit):
    if len(out_ref.shape) == 3:
        out_ref[...] = pieces[...].astype(f32)
        return
    count = pieces.shape[2] // unit
    for k in range(seq):
        for c in range(count):
            at = (c * seq + k) * unit
            out_ref[:, at : at + unit] = pieces[k, :, c * unit : (c + 1) * unit].astype(f32)


def attend_back(
    qkv, db, wout, att, mem, upd, lse, slse, sgrad, length, state_query, forget, bias, up, down, mo, mid, seq, fsdp
):
    rows, width3 = qkv.shape
    width = width3 // 3
    heads = width // DH
    dim = db.shape[1]
    lo = 2
    hi = fsdp // lo
    piece, hidden = up.shape[2:]
    share = hidden // fsdp
    tok_rows = mid.shape[0]
    inside = piece % 16 == 0
    blocks = (piece, dim), (seq, piece, hidden), (share, dim)
    small_rows = heads * (DH + 2)
    small_rows += -small_rows % 8
    vmem = pl.BlockSpec(memory_space=pltpu.VMEM)
    anywhere = pl.BlockSpec(memory_space=pl.ANY)
    dma = pltpu.SemaphoreType.DMA

    def buf(*shape):
        return pltpu.VMEM(shape, bf16)

    extra = []
    if not inside:
        extra.append(t_dot(att, db).astype(bf16).reshape(fsdp, piece, dim))
    upart = (piece, hidden * seq) if share % 128 == 0 else (seq, piece, hidden)
    return pl.pallas_call(
        functools.partial(attend_back_kernel, heads, seq, hi, lo, inside),
        out_shape=(
            jax.ShapeDtypeStruct((rows, width3), bf16),
            jax.ShapeDtypeStruct((small_rows, DH), f32),
            jax.ShapeDtypeStruct(upart, f32),
            jax.ShapeDtypeStruct((hi, share, dim), bf16),
            jax.ShapeDtypeStruct((piece, dim), f32),
            jax.ShapeDtypeStruct((tok_rows, dim), bf16),
        ),
        in_specs=[pl.BlockSpec(memory_space=pltpu.SMEM), anywhere, anywhere, anywhere]
        + [anywhere] * 3
        + [vmem] * 6
        + [anywhere] * 4
        + [vmem] * len(extra),
        out_specs=(anywhere,) + (vmem,) * 5,
        scratch_shapes=[
            buf(rows, width3),
            buf(rows, dim),
            buf(rows, width),
            pltpu.VMEM(mem.shape, f32),
            pltpu.VMEM(upd.shape, f32),
            pltpu.VMEM((tok_rows, dim), f32),
            buf(rows, width3),
            buf(width, dim),
            pltpu.VMEM((STATE_VECTORS, width), f32),
            pltpu.VMEM((2, BLOCK, width), f32),
            pltpu.VMEM((2, 2 * BLOCK, DH), f32),
            pltpu.VMEM((heads, SPAN, QTILE), f32),
            pltpu.VMEM((heads, NEAR, QTILE), f32),
            pltpu.VMEM((heads, 8, QTILE), f32),
            buf(BLOCK, width),
            buf(fsdp, piece, dim),
            buf(*down.shape),
            buf(hi, *blocks[0]),
            buf(hi, *blocks[1]),
            buf(hi, *blocks[0]),
            buf(16, 128) if inside else buf(hi, *blocks[1]),
            buf(hi, *blocks[2]),
            buf(2, max(hi - 1, 1), *blocks[0]),
            buf(2, max(hi - 1, 1), *blocks[1]),
            buf(*blocks[1]),
            buf(max(seq // 2, 1), tok_rows, dim),
            buf(max(seq - 1, 1), tok_rows, dim),
            dma((2, 2, hi)),
            dma((2, 2, hi)),
            dma((3, hi)),
            dma((3, hi)),
            dma((seq,)),
            dma((seq,)),
            dma((seq,)),
            dma((seq,)),
            dma((seq,)),
            dma((seq,)),
            dma((5,)),
            dma((3, seq)),
            dma((hi,)),
            dma((seq,)),
            dma,
        ],
        compiler_params=pltpu.CompilerParams(collective_id=4, has_side_effects=True, vmem_limit_bytes=62 << 20),
        cost_estimate=pl.CostEstimate(
            flops=seq * heads * 512 * 2400 * 128 * 10, bytes_accessed=20 << 20, transcendentals=10 << 20
        ),
        name="attend_back",
    )(
        length, qkv, db, wout, att, mem, upd, lse, slse, sgrad, state_query, forget, bias, up, down, mo, mid, *extra
    )


def gather_kernel(seq, hi, lo, *refs):
    refs = list(refs)

    def take(count):
        taken = refs[:count]
        del refs[:count]
        return taken

    tok_ref, grad_ref, wq_ref, ga_ref, gm_ref, wo_ref, wu_ref = take(7)
    toks_ref, grads_ref, wqs_ref, gas_ref, gms_ref, wos_ref, wus_ref, normed_ref, qkv_ref = take(9)
    toks_full, grad_buf, wq_full, ga_full, gm_full, wo_buf, wu_buf, normed_buf, qkv_buf = take(9)
    own_sem, store_sem, seq_send, seq_recv, chunk_sem, z_send, z_recv, y_send, y_recv = take(9)

    me = lax.axis_index("seq")
    f = lax.axis_index("fsdp")
    fsdp = hi * lo
    bits = [1 << i for i in range(seq.bit_length() - 1)]
    high = [bit for bit in reversed(bits) if bit > 1]
    rows, dim = tok_ref.shape
    width = wq_full.shape[2] // 3
    share = wus_ref.shape[2] // fsdp
    every = wq_ref.shape[1] // 3
    loads = [[] for _ in range(7)]

    def load(i, src, dst):
        loads[i].append(pltpu.make_async_copy(src, dst, own_sem.at[i, len(loads[i])]))
        loads[i][-1].start()

    for c in range(3):
        cols = pl.ds(pl.multiple_of(c * every + me * width, width), width)
        load(0, wq_ref.at[:, cols], wq_full.at[f, :, pl.ds(c * width, width)])
    load(1, ga_ref, ga_full.at[f])
    load(2, gm_ref, gm_full.at[f])
    load(3, wo_ref.at[me % 2], wo_buf)
    if wu_ref.shape[1] == wus_ref.shape[2]:
        load(4, wu_ref, wu_buf)
    else:
        for c in range(fsdp):
            cols = pl.ds(pl.multiple_of((c * seq + me) * share, share), share)
            load(4, wu_ref.at[:, cols], wu_buf.at[:, pl.ds(c * share, share)])
    load(5, tok_ref, toks_full.at[0])
    load(6, grad_ref, grad_buf)
    greet(bits, hi, lo)

    pairs = ((tok_ref, toks_full), (grad_ref, grads_ref))

    def seq_copy(i, source, slot, bit):
        src, out = pairs[i]
        return pltpu.make_async_remote_copy(
            src_ref=out.at[source] if source else src,
            dst_ref=out.at[slot],
            send_sem=seq_send.at[i, slot],
            recv_sem=seq_recv.at[i, slot],
            device_id={"seq": me ^ bit},
            device_id_type=MESH,
        )

    sends = []

    def send(i, source, slot, bit):
        sends.append(seq_copy(i, source, slot, bit))
        sends[-1].start()

    fulls = (wq_full, ga_full, gm_full, wos_ref, wus_ref)
    bufs = (None, None, None, wo_buf, wu_buf)
    start, step, arrive, drain = line_gather(
        hi,
        lo,
        lambda i, origin: fulls[i].at[origin],
        lambda i: fulls[i].at[f] if i < 3 else bufs[i],
        z_send,
        z_recv,
        y_send,
        y_recv,
    )
    first, later = (0, 1, 2), (3, 4)
    if high:
        send(0, 0, high[0], high[0])
    if seq > 1:
        send(0, 0, 1, 1)
    for i in first:
        for c in loads[i]:
            c.wait()
        start(i)
    if high:
        send(1, 0, high[0], high[0])
    if seq > 1:
        send(1, 0, 1, 1)
    stores = []

    def store(src, dst, sem):
        stores.append(pltpu.make_async_copy(src, dst, sem))
        stores[-1].start()

    for t in range(hi - 1):
        for i in first:
            step(i, t)
        if t == 0:
            for i in later:
                for c in loads[i]:
                    c.wait()
                start(i)
            store(wo_buf, wos_ref.at[f], store_sem.at[0])
            store(wu_buf, wus_ref.at[f], store_sem.at[1])
    for c in loads[5] + loads[6]:
        c.wait()
    store(toks_full.at[0], toks_ref.at[0], chunk_sem.at[0, 0])
    store(grad_buf, grads_ref.at[0], store_sem.at[2])
    for i in first:
        arrive(i)
    store(wq_full, wqs_ref, store_sem.at[3])
    gas_ref[...] = jnp.concatenate([ga_full[n] for n in range(fsdp)], axis=1).astype(f32)
    gms_ref[...] = jnp.concatenate([gm_full[n] for n in range(fsdp)], axis=1).astype(f32)
    gain = gas_ref[...]

    def project(j):
        if j:
            store(toks_full.at[j], toks_ref.at[j], chunk_sem.at[0, j])

        @pl.loop(0, rows // 256)
        def _(n):
            at = pl.ds(pl.multiple_of(n * 256, 256), 256)
            into = pl.ds(pl.multiple_of(j * rows + n * 256, 256), 256)
            x = toks_full[j, at].astype(f32)
            rho = lax.rsqrt(jnp.mean(x * x, axis=-1, keepdims=True) + EPSILON)
            normed = (x * rho * gain).astype(bf16)
            normed_buf[into] = normed
            qkv_buf[into] = dot(normed, wq_full[...].reshape(dim, 3 * width)).astype(bf16)

        at = pl.ds(j * rows, rows)
        store(normed_buf.at[at], normed_ref.at[at], chunk_sem.at[1, j])
        store(qkv_buf.at[at], qkv_ref.at[at], chunk_sem.at[2, j])

    hop = [0]

    def advance():
        if hop[0] < hi - 1:
            for i in later:
                step(i, hop[0])
            hop[0] += 1

    project(0)
    advance()
    have = [0]
    for n, bit in enumerate(high):
        if n:
            for j in have:
                send(0, j, j ^ bit, bit)
        for j in have:
            seq_copy(0, 0, j ^ bit, bit).wait_recv()
            send(0, j ^ bit, j ^ bit ^ 1, 1)
        have += [j ^ bit for j in have]
    for j in have:
        if j:
            project(j)
            advance()
        if seq > 1:
            seq_copy(0, 0, j ^ 1, 1).wait_recv()
            project(j ^ 1)
            advance()
    while hop[0] < hi - 1:
        advance()
    have = [0]
    for n, bit in enumerate(high):
        if n:
            for j in have:
                send(1, j, j ^ bit, bit)
        for j in have:
            seq_copy(1, 0, j ^ bit, bit).wait_recv()
            send(1, j ^ bit, j ^ bit ^ 1, 1)
        have += [j ^ bit for j in have]
    if seq > 1:
        for j in have:
            seq_copy(1, 0, j ^ 1, 1).wait_recv()
    for i in later:
        arrive(i)
    for i in first + later:
        drain(i)
    for c in sends:
        c.wait_send()
    for c in stores:
        c.wait()


def gather_start(tokens, grads, w_qkv, gain_a, gain_m, w_out, w_up, seq, fsdp):
    lo = 2
    hi = fsdp // lo
    dim_rows, hidden = w_up.shape
    share = hidden // (seq * fsdp)
    if share % 128:
        w_up = lax.dynamic_slice_in_dim(w_up.reshape(dim_rows, fsdp, seq, share), lax.axis_index("seq"), 1, axis=2)
        w_up = w_up.reshape(dim_rows, fsdp * share)
    rows, dim = tokens.shape
    width3 = w_qkv.shape[1] // seq
    anywhere = pl.BlockSpec(memory_space=pl.ANY)
    vmem = pl.BlockSpec(memory_space=pltpu.VMEM)
    dma = pltpu.SemaphoreType.DMA

    def like(*shape):
        return jax.ShapeDtypeStruct(shape, bf16)

    def buf(*shape):
        return pltpu.VMEM(shape, bf16)

    return pl.pallas_call(
        functools.partial(gather_kernel, seq, hi, lo),
        out_shape=(
            like(seq, rows, dim),
            like(seq, rows, dim),
            like(fsdp, dim_rows, width3),
            jax.ShapeDtypeStruct((1, dim), f32),
            jax.ShapeDtypeStruct((1, dim), f32),
            like(fsdp, *w_out.shape[1:]),
            like(fsdp, dim_rows, hidden // seq),
            like(seq * rows, dim),
            like(seq * rows, width3),
        ),
        in_specs=[anywhere] * 7,
        out_specs=(anywhere,) * 3 + (vmem,) * 2 + (anywhere,) * 4,
        scratch_shapes=[
            buf(seq, rows, dim),
            buf(rows, dim),
            buf(fsdp, dim_rows, width3),
            buf(fsdp, *gain_a.shape),
            buf(fsdp, *gain_m.shape),
            buf(*w_out.shape[1:]),
            buf(dim_rows, hidden // seq),
            buf(seq * rows, dim),
            buf(seq * rows, width3),
            dma((7, max(fsdp, 3))),
            dma((4,)),
            dma((2, seq)),
            dma((2, seq)),
            dma((3, seq)),
        ]
        + line_sems(5, hi),
        compiler_params=pltpu.CompilerParams(collective_id=0, has_side_effects=True, vmem_limit_bytes=62 << 20),
        name="gather_start",
    )(tokens, grads, w_qkv, gain_a, gain_m, w_out, w_up)


def finish_kernel(seq, hi, lo, inside, *refs):
    refs = list(refs)

    def take(count):
        taken = refs[:count]
        del refs[:count]
        return taken

    dqkv_hbm, wqkv_hbm, normed_hbm, down_ref, small_ref, mlp_gain_ref, tok_hbm, dmid_hbm, gain_ref = take(9)
    gq_in = None if inside else take(1)[0]
    tg_ref, rq_ref, rd_ref, dquery_ref, gate_ref, table_ref, again_ref, mgain_ref = take(8)
    dqkv_ref, wqkv_ref, normed_ref, tok_ref, dmid_ref = take(5)
    low, into, acc, gq_buf, tq, td, yq, zq, zd, xq, sy, sz, gains, gy, gz, gs = take(16)
    dn_send, dn_recv, z_send, z_recv, y_send, y_recv, x_send, x_recv, s_send, s_recv, g_send, g_recv = take(12)
    load_sem, dqkv_sem, tg_sem = take(3)
    gq_ref = gq_buf if inside else gq_in

    me = lax.axis_index("seq")
    f = lax.axis_index("fsdp")
    z, y = f // lo, f % lo
    peer = z * lo + 1 - y
    rows, dim = tok_ref.shape
    width = xq.shape[2] // 3
    bits, slots = seq_levels(seq)

    loads = [
        pltpu.make_async_copy(src, dst, load_sem.at[i])
        for i, (src, dst) in enumerate(
            (
                (wqkv_hbm, wqkv_ref),
                (down_ref, td),
                (normed_hbm, normed_ref),
                (tok_hbm, tok_ref),
                (dmid_hbm, dmid_ref),
            )
        )
    ]
    dqkv_loads = {
        j: pltpu.make_async_copy(
            dqkv_hbm.at[pl.ds(j * rows, rows)], dqkv_ref.at[pl.ds(j * rows, rows)], dqkv_sem.at[j]
        )
        for j in range(seq)
    }
    loads[0].start()
    for j in reversed(range(seq)):
        dqkv_loads[j].start()
    for c in loads[1:]:
        c.start()

    barrier = pltpu.get_barrier_semaphore()
    for k in range(1, seq):
        pl.semaphore_signal(barrier, inc=1, device_id={"seq": me ^ k}, device_id_type=MESH)
    for k in range(1, hi):
        pl.semaphore_signal(barrier, inc=1, device_id={"fsdp": lax.rem(z + k, hi) * lo + y}, device_id_type=MESH)
    pl.semaphore_signal(barrier, inc=1, device_id={"fsdp": peer}, device_id_type=MESH)
    pl.semaphore_wait(barrier, seq + hi - 1)

    def remote(src, dst, send, recv, axis, target):
        return pltpu.make_async_remote_copy(
            src_ref=src, dst_ref=dst, send_sem=send, recv_sem=recv, device_id={axis: target}, device_id_type=MESH
        )

    def dn_copy(bit, j):
        slot = slots[bit, j]
        return remote(low.at[j ^ bit], into.at[slot], dn_send.at[slot], dn_recv.at[slot], "seq", me ^ bit)

    _, _, zsend, zrecv, _, drain_z = line_reduce(
        hi,
        lo,
        lambda i, target: gq_ref.at[:, target],
        (tq, td),
        (yq,),
        (zq, zd),
        z_send,
        z_recv,
        y_send,
        y_recv,
    )
    half = seq // 2
    start, combine, _, _, drain_y, _ = line_reduce(
        hi,
        lo,
        lambda i, target: gq_ref.at[pl.ds(i * half, half), target],
        tuple(tq.at[:, pl.ds(i * half, half)] for i in range(2)),
        tuple(yq.at[:, pl.ds(i * half, half)] for i in range(2)),
        (),
        None,
        None,
        y_send,
        y_recv,
    )

    def exchange(k, sending):
        return remote(
            tq.at[z, me ^ k] if sending else tq.at[z, me],
            xq.at[me] if sending else xq.at[me ^ k],
            x_send.at[k],
            x_recv.at[k],
            "seq",
            me ^ k if sending else me,
        )

    small_y = remote(small_ref, sy, s_send.at[0], s_recv.at[0], "fsdp", peer)
    small_y.start()
    loads[0].wait()
    if not inside:
        start(0)
        start(1)

    def dn_part(j):
        part = dot_t(dqkv_ref[j * rows : (j + 1) * rows], wqkv_ref[...])
        if j % 2:
            low[j] = part.astype(bf16)
            dn_copy(1, j ^ 1).start()
        else:
            acc[...] = part

    def dn_sum(j):
        for bit in bits:
            if j & bit:
                low[j] = acc[...].astype(bf16)
                dn_copy(bit, j ^ bit).start()
                break
            dn_copy(bit, j).wait_recv()
            acc[...] += into[slots[bit, j]].astype(f32)

    for j in reversed(range(2, seq)):
        dqkv_loads[j].wait()
        dn_part(j)
        if j == seq - 1:
            loads[1].wait()
            zsend(1, 0)
        if j % 2 == 0:
            dn_sum(j)
    for j in range(min(2, seq)):
        dqkv_loads[j].wait()
    loads[2].wait()
    if inside:
        for k in range(seq):
            cols = slice(k * (dim // seq), (k + 1) * (dim // seq))
            part = t_dot(normed_ref[:, cols], dqkv_ref[...]).astype(bf16)
            gq_buf[k] = part.reshape(gq_buf.shape[1:])
            if (k + 1) % half == 0:
                start(k // half)
    def zstep(i, t):
        if t < hi - 1:
            zrecv(i, t)
            if t + 1 < hi - 1:
                zsend(i, t + 1)

    zstep(1, 0)
    small_y.wait_recv()
    sz[z] = small_ref[...] + sy[...]
    small_z = []
    for k in range(1, hi):
        small_z.append(
            remote(sz.at[z], sz.at[z], s_send.at[k], s_recv.at[k], "fsdp", lax.rem(z + k, hi) * lo + y)
        )
        small_z[-1].start()
    for j in reversed(range(min(2, seq))):
        dn_part(j)
    zstep(1, 1)
    for c in loads[3:]:
        c.wait()
    combine(0)
    combine(1)
    zsend(0, 0)
    zstep(1, 2)
    for t in range(3, hi - 1):
        zstep(1, t)
    for bit in bits:
        dn_copy(bit, 0).wait_recv()
    gain = gain_ref[...]
    part = jnp.zeros((8, dim), f32)
    step = 128
    for r in range(0, rows, step):
        at = slice(r, r + step)
        dn = acc[at]
        for bit in bits:
            dn = dn + into[slots[bit, 0], at].astype(f32)
        x = tok_ref[at].astype(f32)
        rho = lax.rsqrt(jnp.mean(x * x, axis=-1, keepdims=True) + EPSILON)
        scaled = gain * dn
        mean = jnp.mean(x * scaled, axis=-1, keepdims=True)
        dmid_ref[at] += rho * scaled - x * (rho * rho * rho * mean)
        prod = dn * x * rho
        part += functools.reduce(jnp.add, [prod[n : n + 8] for n in range(0, step, 8)])
    tg_store = pltpu.make_async_copy(dmid_ref, tg_ref, tg_sem)
    tg_store.start()
    gains[0:8] = mlp_gain_ref[...]
    gains[8:16] = part
    gain_y = remote(gains, gy, g_send.at[0], g_recv.at[0], "fsdp", peer)
    gain_y.start()
    zrecv(0, 0)
    if hi > 2:
        zsend(0, 1)
    gain_y.wait_recv()
    gz[z] = gains[...] + gy[...]
    gain_z = []
    for k in range(1, hi):
        gain_z.append(
            remote(gz.at[z], gz.at[z], g_send.at[k], g_recv.at[k], "fsdp", lax.rem(z + k, hi) * lo + y)
        )
        gain_z[-1].start()
    for t in range(1, hi - 1):
        zrecv(0, t)
        if t + 1 < hi - 1:
            zsend(0, t + 1)
    for k in range(1, seq):
        exchange(k, True).start()
    for k in range(1, hi):
        source = lax.rem(z + hi - k, hi)
        remote(gz.at[source], gz.at[source], g_send.at[k], g_recv.at[k], "fsdp", f).wait_recv()
        remote(sz.at[source], sz.at[source], s_send.at[k], s_recv.at[k], "fsdp", f).wait_recv()
    gs[me] = functools.reduce(jnp.add, [gz[d] for d in range(hi)])
    gain_x = []
    for k in range(1, seq):
        gain_x.append(remote(gs.at[me], gs.at[me], g_send.at[hi + k], g_recv.at[hi + k], "seq", me ^ k))
        gain_x[-1].start()
    rd_ref[...] = td[z].astype(f32)
    total = functools.reduce(jnp.add, [sz[d] for d in range(hi)])
    cut, heads = dquery_ref.shape[0], gate_ref.shape[0]
    dquery_ref[...] = total[:cut]
    gate_ref[...] = total[cut : cut + heads]
    table_ref[...] = total[cut + heads : cut + 2 * heads, :BUCKETS]
    xq[me] = tq[z, me]
    for k in range(1, seq):
        exchange(k, False).wait_recv()
    write_parts(rq_ref, xq, seq, width)
    for k in range(1, seq):
        remote(gs.at[me ^ k], gs.at[me ^ k], g_send.at[hi + k], g_recv.at[hi + k], "seq", me).wait_recv()
    total = functools.reduce(jnp.add, [gs[k] for k in range(seq)])
    piece = again_ref.shape[1]
    total = pltpu.roll(total, lax.rem(dim - (me * hi * lo + f) * piece, dim), 1)[:, :DH]
    mgain_ref[...] = jnp.sum(total[0:8], axis=0, keepdims=True)[:, :piece]
    again_ref[...] = jnp.sum(total[8:16], axis=0, keepdims=True)[:, :piece]

    for bit in bits:
        for j in range(0, seq, 2 * bit):
            dn_copy(bit, j).wait_send()
    drain_y(0)
    drain_y(1)
    for i in range(2):
        drain_z(i)
    for k in range(1, seq):
        exchange(k, True).wait_send()
    for c in [small_y, gain_y] + small_z + gain_z + gain_x:
        c.wait_send()
    tg_store.wait()


def finish(dqkv, wqkv, normed, down, small, mlp_gain, tok, dmid, gain, seq, fsdp):
    lo = 2
    hi = fsdp // lo
    rows, dim = tok.shape
    width3 = dqkv.shape[1]
    piece = dim // (seq * fsdp)
    inside = piece % 16 == 0
    heads = width3 // (3 * DH)
    vmem = pl.BlockSpec(memory_space=pltpu.VMEM)
    anywhere = pl.BlockSpec(memory_space=pl.ANY)
    dma = pltpu.SemaphoreType.DMA

    def buf(*shape):
        return pltpu.VMEM(shape, bf16)

    extra = []
    if not inside:
        extra.append(t_dot(normed, dqkv).astype(bf16).reshape(seq, fsdp, piece, width3))
    scratch = [
        buf(*dqkv.shape),
        buf(*wqkv.shape),
        buf(*normed.shape),
        buf(rows, dim),
        pltpu.VMEM((rows, dim), f32),
        buf(seq, rows, dim),
        buf(max(seq - 1, 1), rows, dim),
        pltpu.VMEM((rows, dim), f32),
        buf(seq, fsdp, piece, width3) if inside else buf(16, 128),
        buf(hi, seq, piece, width3),
        buf(*down.shape),
        buf(hi, seq, piece, width3),
        buf(2, max(hi - 1, 1), seq, piece, width3),
        buf(2, max(hi - 1, 1), *down.shape[1:]),
        buf(seq, piece, width3),
        pltpu.VMEM(small.shape, f32),
        pltpu.VMEM((hi,) + small.shape, f32),
        pltpu.VMEM((16, dim), f32),
        pltpu.VMEM((16, dim), f32),
        pltpu.VMEM((hi, 16, dim), f32),
        pltpu.VMEM((seq, 16, dim), f32),
        dma((seq,)),
        dma((seq,)),
        dma((2, 2, hi)),
        dma((2, 2, hi)),
        dma((2, hi)),
        dma((2, hi)),
        dma((seq,)),
        dma((seq,)),
        dma((hi,)),
        dma((hi,)),
        dma((hi + seq,)),
        dma((hi + seq,)),
        dma((5,)),
        dma((seq,)),
        dma,
    ]
    return pl.pallas_call(
        functools.partial(finish_kernel, seq, hi, lo, inside),
        out_shape=(
            jax.ShapeDtypeStruct((rows, dim), f32),
            jax.ShapeDtypeStruct((piece, seq * width3), f32),
            jax.ShapeDtypeStruct(down.shape[1:], f32),
            jax.ShapeDtypeStruct((heads * DH, DH), f32),
            jax.ShapeDtypeStruct((heads, DH), f32),
            jax.ShapeDtypeStruct((heads, BUCKETS), f32),
            jax.ShapeDtypeStruct((1, piece), f32),
            jax.ShapeDtypeStruct((1, piece), f32),
        ),
        in_specs=[anywhere] * 4 + [vmem] * 2 + [anywhere] * 2 + [vmem] * (1 + len(extra)),
        out_specs=(anywhere,) + (vmem,) * 7,
        scratch_shapes=scratch,
        compiler_params=pltpu.CompilerParams(
            collective_id=1, has_side_effects=True, vmem_limit_bytes=60 << 20
        ),
        name="finish",
    )(dqkv, wqkv, normed, down, small, mlp_gain, tok, dmid, gain, *extra)


GELU_P = 0.24
GELU_C = (
    0.08951261885080208,
    0.15562094398234086,
    -0.15437154502074169,
    0.6261054138112487,
    -0.6465313024138201,
    0.5547927291245551,
    -0.125128858665134,
)


def gelu_parts(x):
    size = jnp.abs(x)
    t = 1.0 / (1.0 + GELU_P * size)
    poly = GELU_C[-1] * t
    for c in GELU_C[-2::-1]:
        poly = (poly + c) * t
    bell = jnp.exp2(x * x * (-0.5 * LOG2E))
    tail = poly * bell
    cdf = jnp.where(x < 0.0, tail, 1.0 - tail)
    return x * cdf, cdf + x * bell * (1.0 / math.sqrt(2.0 * math.pi))


def mlp_kernel(seq, hi, lo, sub, length_ref, *refs):
    refs = list(refs)

    def take(count):
        taken = refs[:count]
        del refs[:count]
        return taken

    own_ref, others_ref, tok_ref, grads_ref, wo_hbm, wu_hbm, wd_hbm, gain_ref = take(8)
    mid_out, dmid_out, gsum_ref, db_ref, mo_ref, ug_out, dg_out = take(7)
    staged = len(ug_out.shape) == 4
    att_refs = [own_ref] + [others_ref.at[k] for k in range(1, seq)]
    att_buf, tok_buf, wo_ref, wu_ref, wd_ref, gm, nm, hid, dpre, low, into, acc, mid_ref, ug_ref, dg_ref = take(15)
    load_sem, w_sem, gm_sem, dn_send, dn_recv, db_send, db_recv, mo_sem, own_sem = take(9)
    if staged:
        tu, yu, y_send, y_recv = take(4)
    dbv = low.at[0]
    depth = att_buf.shape[0]

    me = lax.axis_index("seq")
    length = length_ref[0]
    dim = wo_ref.shape[0]
    width = dim // seq
    rows = tok_ref.shape[1]
    share = wu_ref.shape[1]
    subs = rows // sub
    bits, slots = seq_levels(seq)
    order = list(reversed(range(seq)))

    def chunk_loads(j):
        slot = j % depth
        copies = [
            pltpu.make_async_copy(att_refs[k].at[pl.ds(j * rows, rows)], att_buf.at[slot, k], load_sem.at[slot, k])
            for k in range(seq)
        ]
        copies.append(pltpu.make_async_copy(tok_ref.at[j], tok_buf.at[slot], load_sem.at[slot, seq]))
        return copies

    gm_loads = {
        j: pltpu.make_async_copy(grads_ref.at[j], gm.at[pl.ds(j * rows, rows)], gm_sem.at[j]) for j in order
    }
    weights = [
        pltpu.make_async_copy(src, dst, w_sem.at[i])
        for i, (src, dst) in enumerate(((wo_hbm, wo_ref), (wu_hbm, wu_ref), (wd_hbm, wd_ref)))
    ]
    for c in chunk_loads(order[0]) + weights[:1] + (chunk_loads(order[1]) if seq > 1 else []) + weights[1:]:
        c.start()
    for j in order:
        gm_loads[j].start()
    if depth == seq:
        for j in order[2:]:
            for c in chunk_loads(j):
                c.start()

    greet(bits, hi, lo)

    def dn_copy(bit, j, s):
        slot = slots[bit, j]
        at = pl.ds(pl.multiple_of(s * sub, sub), sub)
        return pltpu.make_async_remote_copy(
            src_ref=low.at[j ^ bit, at],
            dst_ref=into.at[slot, at],
            send_sem=dn_send.at[slot, s],
            recv_sem=dn_recv.at[slot, s],
            device_id={"seq": me ^ bit},
            device_id_type=MESH,
        )

    gain = gain_ref[...]

    def forward(j, s):
        slot = j % depth
        at = pl.ds(pl.multiple_of(s * sub, sub), sub)
        here = pl.ds(pl.multiple_of(j * rows + s * sub, sub), sub)
        position = (j ^ me) * rows + s * sub + lax.broadcasted_iota(jnp.int32, (sub, 1), 0)
        live = jnp.where(position < length, 1.0, 0.0)
        masked = (gm[here].astype(f32) * live).astype(bf16)
        gm[here] = masked
        mid = tok_buf[slot, at].astype(f32)
        for k in range(seq):
            own = pl.ds(pl.multiple_of((me ^ k) * width, width), width)
            mid = mid + dot(att_buf[slot, k, at], wo_ref[own])
        rho = lax.rsqrt(jnp.mean(mid * mid, axis=-1, keepdims=True) + EPSILON)
        normed = (mid * rho * gain).astype(bf16)
        nm[here] = normed
        if j == 0:
            mid_ref[at] = mid
        for c in range(0, share, 256):
            cols = slice(c, c + 256)
            value, slope = gelu_parts(dot(normed, wu_ref[:, cols]))
            hid[here, cols] = value.astype(bf16)
            dpre[here, cols] = (dot_t(masked, wd_ref[cols]) * slope).astype(bf16)
        part = dot_t(dpre[here], wu_ref[...])
        if j % 2:
            low[j, at] = part.astype(bf16)
            dn_copy(1, j ^ 1, s).start()
        else:
            acc[at] = part

    def settle(j, s):
        at = pl.ds(pl.multiple_of(s * sub, sub), sub)
        for bit in bits:
            if j & bit:
                low[j, at] = acc[at].astype(bf16)
                dn_copy(bit, j ^ bit, s).start()
                break
            dn_copy(bit, j, s).wait_recv()
            acc[at] += into[slots[bit, j], at].astype(f32)

    for c in weights:
        c.wait()
    for n in range(0, seq, 2):
        pair = order[n : n + 2]
        if n and depth < seq:
            for j in pair:
                for c in chunk_loads(j):
                    c.start()
        for j in pair:
            for c in chunk_loads(j):
                c.wait()
            gm_loads[j].wait()

        @pl.loop(0, subs)
        def _(s):
            for j in pair:
                forward(j, s)
            if pair[-1]:
                settle(pair[-1], s)

    stores = [pltpu.make_async_copy(mid_ref, mid_out, own_sem.at[1])]
    stores[0].start()
    half = seq // 2
    if staged:
        start, combine, _, _, drain_y, _ = line_reduce(
            hi,
            lo,
            lambda i, target: ug_ref.at[pl.ds(i * half, half), target],
            tuple(tu.at[:, pl.ds(i * half, half)] for i in range(2)),
            tuple(yu.at[:, pl.ds(i * half, half)] for i in range(2)),
            (),
            None,
            None,
            y_send,
            y_recv,
        )

    def up_half(i):
        for k in range(i * half, (i + 1) * half):
            cols = slice(k * (dim // seq), (k + 1) * (dim // seq))
            ug_ref[k] = t_dot(nm[:, cols], dpre[...]).astype(bf16).reshape(ug_ref.shape[1:])
        start(i)

    if staged:
        up_half(0)
    else:
        for c in range(0, dim, 256):
            ug_ref[c : c + 256] = t_dot(nm[:, c : c + 256], dpre[...]).astype(bf16)
        stores.append(pltpu.make_async_copy(ug_ref, ug_out, own_sem.at[2]))
        stores[-1].start()

    def db_copy(source, target, bit, s):
        at = pl.ds(s * sub, sub)
        return pltpu.make_async_remote_copy(
            src_ref=db_ref.at[source, at] if source else dbv.at[at],
            dst_ref=db_ref.at[target, at],
            send_sem=db_send.at[target, s],
            recv_sem=db_recv.at[target, s],
            device_id={"seq": me ^ bit},
            device_id_type=MESH,
        )

    sends = []
    high = [bit for bit in reversed(bits) if bit > 1]

    def send(source, target, bit, s):
        sends.append(db_copy(source, target, bit, s))
        sends[-1].start()

    step = 128
    part = jnp.zeros((8, dim), f32)
    for s in range(subs):
        for bit in bits:
            dn_copy(bit, 0, s).wait_recv()
        for r in range(s * sub, (s + 1) * sub, step):
            at = slice(r, r + step)
            dn = acc[at]
            for bit in bits:
                dn = dn + into[slots[bit, 0], at].astype(f32)
            mid = mid_ref[at]
            rho = lax.rsqrt(jnp.mean(mid * mid, axis=-1, keepdims=True) + EPSILON)
            scaled = gain * dn
            mean = jnp.mean(mid * scaled, axis=-1, keepdims=True)
            dmid = gm[at].astype(f32) + rho * scaled - mid * (rho * rho * rho * mean)
            acc[at] = dmid
            dbv[at] = dmid.astype(bf16)
            prod = dn * mid * rho
            part += functools.reduce(jnp.add, [prod[i : i + 8] for i in range(0, step, 8)])
        if high:
            send(0, high[0], high[0], s)
        if seq > 1:
            send(0, 1, 1, s)
    gsum_ref[...] = part
    stores.append(pltpu.make_async_copy(dbv, db_ref.at[0], own_sem.at[0]))
    stores[-1].start()
    stores.append(pltpu.make_async_copy(acc, dmid_out, own_sem.at[3]))
    stores[-1].start()
    if staged:
        up_half(1)
    for c in range(0, share, 256):
        dg_ref[c : c + 256] = t_dot(hid[:, c : c + 256], gm[...]).astype(bf16)
    stores.append(pltpu.make_async_copy(dg_ref, dg_out, own_sem.at[4]))
    stores[-1].start()
    for j in range(seq):
        at = slice(j * rows, (j + 1) * rows)
        nm[at] = dot(hid[at], wd_ref[...]).astype(bf16)
        stores.append(pltpu.make_async_copy(nm.at[pl.ds(j * rows, rows)], mo_ref.at[j], mo_sem.at[j]))
        stores[-1].start()
    have = [0]
    for n, bit in enumerate(high):
        if n:
            for j in have:
                for s in range(subs):
                    send(j, j ^ bit, bit, s)
        for j in have:
            for s in range(subs):
                db_copy(0, j ^ bit, bit, s).wait_recv()
                send(j ^ bit, j ^ bit ^ 1, 1, s)
        have += [j ^ bit for j in have]
    if seq > 1:
        for j in have:
            for s in range(subs):
                db_copy(0, j ^ 1, 1, s).wait_recv()
    if staged:
        for i in range(2):
            combine(i)
        stores.append(pltpu.make_async_copy(tu, ug_out, own_sem.at[2]))
        stores[-1].start()
        for i in range(2):
            drain_y(i)
    for c in sends:
        c.wait_send()
    for c in stores:
        c.wait()
    for bit in bits:
        for j in range(0, seq, 2 * bit):
            for s in range(subs):
                dn_copy(bit, j, s).wait_send()


def mlp(length, own, others, tok, grads, wo, wu, wd, gain, fsdp):
    seq, rows, dim = tok.shape
    share = wu.shape[1]
    lo = 2
    hi = fsdp // lo
    piece = dim // (seq * fsdp)
    staged = piece % 16 == 0
    up_shape = (hi, seq, piece, share) if staged else (dim, share)
    sub = 256
    depth = seq if seq <= 4 else 2
    anywhere = pl.BlockSpec(memory_space=pl.ANY)
    vmem = pl.BlockSpec(memory_space=pltpu.VMEM)
    dma = pltpu.SemaphoreType.DMA

    def buf(*shape):
        return pltpu.VMEM(shape, bf16)

    return pl.pallas_call(
        functools.partial(mlp_kernel, seq, hi, lo, sub),
        out_shape=(
            jax.ShapeDtypeStruct((rows, dim), f32),
            jax.ShapeDtypeStruct((rows, dim), f32),
            jax.ShapeDtypeStruct((8, dim), f32),
            jax.ShapeDtypeStruct((seq, rows, dim), bf16),
            jax.ShapeDtypeStruct((seq, rows, dim), bf16),
            jax.ShapeDtypeStruct(up_shape, bf16),
            jax.ShapeDtypeStruct((share, dim), bf16),
        ),
        in_specs=[pl.BlockSpec(memory_space=pltpu.SMEM)] + [anywhere] * 7 + [vmem],
        out_specs=(anywhere, anywhere, vmem, anywhere, anywhere, anywhere, anywhere),
        scratch_shapes=[
            buf(depth, seq, rows, dim // seq),
            buf(depth, rows, dim),
            buf(dim, dim),
            buf(dim, share),
            buf(share, dim),
            buf(seq * rows, dim),
            buf(seq * rows, dim),
            buf(seq * rows, share),
            buf(seq * rows, share),
            buf(seq, rows, dim),
            buf(max(seq - 1, 1), rows, dim),
            pltpu.VMEM((rows, dim), f32),
            pltpu.VMEM((rows, dim), f32),
            buf(seq, fsdp, piece, share) if staged else buf(dim, share),
            buf(share, dim),
            dma((depth, seq + 1)),
            dma((3,)),
            dma((seq,)),
            dma((seq, rows // sub)),
            dma((seq, rows // sub)),
            dma((seq, rows // sub)),
            dma((seq, rows // sub)),
            dma((seq,)),
            dma((5,)),
        ]
        + ([buf(*up_shape), buf(*up_shape), dma((2, hi)), dma((2, hi))] if staged else []),
        compiler_params=pltpu.CompilerParams(collective_id=2, has_side_effects=True, vmem_limit_bytes=62 << 20),
        cost_estimate=pl.CostEstimate(
            flops=2 * rows * seq * dim * (dim + 6 * share), bytes_accessed=32 << 20, transcendentals=rows * seq * share
        ),
        name="mlp",
    )(length, own, others, tok, grads, wo, wu, wd, gain)


def emit_kernel(*refs):
    count = len(refs) // 3
    ins, outs, bufs = refs[:count], refs[count : 2 * count], refs[2 * count : 3 * count]
    sems = refs[3 * count]
    reads = [pltpu.make_async_copy(a, b, sems.at[0, i]) for i, (a, b) in enumerate(zip(ins, bufs))]
    writes = [pltpu.make_async_copy(a, b, sems.at[1, i]) for i, (a, b) in enumerate(zip(bufs, outs))]
    for c in reads:
        c.start()
    for read, write in zip(reads, writes):
        read.wait()
        write.start()
    for c in writes:
        c.wait()


def emit(*values):
    count = len(values)
    anywhere = pl.BlockSpec(memory_space=pl.ANY)
    return pl.pallas_call(
        emit_kernel,
        out_shape=tuple(jax.ShapeDtypeStruct(v.shape, v.dtype) for v in values),
        in_specs=[anywhere] * count,
        out_specs=(anywhere,) * count,
        scratch_shapes=[pltpu.VMEM(v.shape, v.dtype) for v in values] + [pltpu.SemaphoreType.DMA((2, count))],
        compiler_params=pltpu.CompilerParams(vmem_limit_bytes=62 << 20),
        name="emit",
    )(*values)


def body(
    tokens,
    lengths,
    state_init,
    w_qkv,
    w_out,
    w_up,
    w_down,
    norm_attn,
    norm_mlp,
    rel_bias,
    state_query,
    gate_bias,
    out_grad,
    state_grad,
):
    seq_count = lax.axis_size("seq")
    fsdp_count = lax.axis_size("fsdp")
    seq_at = lax.axis_index("seq")
    heads = H // seq_count
    width = heads * DH
    tok_rows, dim = tokens.shape[1:]
    rows = tok_rows * seq_count
    hidden_all = w_up.shape[1]
    share = hidden_all // (seq_count * fsdp_count)

    piece = dim // (seq_count * fsdp_count)
    all_tokens, all_grad, qkv_w, gain_attn, gain_mlp, own_out, up_w, normed, qkv = gather_start(
        tokens[0],
        out_grad[0],
        w_qkv,
        norm_attn.reshape(1, -1),
        norm_mlp.reshape(1, -1),
        w_out.reshape(2, w_out.shape[0] // 2, dim),
        w_up,
        seq_count,
        fsdp_count,
    )
    qkv_w = qkv_w.reshape(dim, 3 * width)
    up_w = up_w.reshape(dim, hidden_all // seq_count)

    bias = bias_vector(rel_bias)

    attended, others, out_w, down_w, final_memory, mem, upd, lse, slse = attend(
        qkv,
        state_init[0],
        lengths,
        state_query,
        gate_bias,
        bias,
        own_out,
        w_down,
        heads,
        seq_count,
        fsdp_count,
    )
    out_w = out_w.reshape(dim, dim)
    down_w = down_w.reshape(fsdp_count * share, dim)
    mid_here, dmid, mlp_gain_grad, dbranch, mlp_parts, up_grad, down_grad = mlp(
        lengths, attended, others, all_tokens, all_grad, out_w, up_w, down_w, gain_mlp, fsdp_count
    )
    span = fsdp_count // seq_count
    if up_grad.ndim == 2:
        up_grad = up_grad.reshape(seq_count, fsdp_count, piece, hidden_all // seq_count)
    dqkv, small, up_part, down_total, out_part, output = attend_back(
        qkv,
        dbranch.reshape(rows, dim),
        out_w,
        attended,
        mem,
        upd,
        lse,
        slse,
        state_grad[0],
        lengths,
        state_query,
        gate_bias,
        bias,
        up_grad,
        down_grad.reshape(seq_count, span * share, dim),
        mlp_parts,
        mid_here,
        seq_count,
        fsdp_count,
    )
    tokens_grad, qkv_part, down_part, dquery, grad_gate, grad_table, attn_gain_grad, mlp_gain_grad = finish(
        dqkv,
        qkv_w,
        normed,
        down_total,
        small,
        mlp_gain_grad,
        tokens[0],
        dmid,
        gain_attn,
        seq_count,
        fsdp_count,
    )
    big = (output, final_memory, tokens_grad, qkv_part, out_part, up_part, down_part)
    little = (dquery, grad_gate, grad_table, attn_gain_grad, mlp_gain_grad)
    output, final_memory, tokens_grad, qkv_part, out_part, up_part, down_part, *little = emit(*big, *little)
    dquery, grad_gate, grad_table, attn_gain_grad, mlp_gain_grad = little
    output = output[None]
    tokens_grad = tokens_grad[None]
    if up_part.ndim == 3:
        up_part = up_part.reshape(seq_count, piece, fsdp_count, share)
        up_part = jnp.transpose(up_part, (1, 2, 0, 3)).reshape(piece, hidden_all)
    dquery = dquery.reshape(heads, DH, DH)
    attn_gain_grad = attn_gain_grad.reshape(piece)
    mlp_gain_grad = mlp_gain_grad.reshape(piece)
    return (
        output,
        final_memory[None],
        tokens_grad,
        qkv_part,
        out_part,
        up_part,
        down_part,
        attn_gain_grad,
        mlp_gain_grad,
        grad_table,
        dquery,
        grad_gate,
    )


def solution(mesh):
    placed = (
        P("fsdp", "seq", None),
        P("fsdp"),
        P("fsdp", None, "seq"),
        P("fsdp", None),
        P("fsdp", None),
        P("fsdp", None),
        P("fsdp", None),
        P("fsdp"),
        P("fsdp"),
        P("seq", None),
        P("seq", None, None),
        P("seq", None),
        P("fsdp", "seq", None),
        P("fsdp", None, "seq"),
    )
    return jax.shard_map(
        body,
        mesh=mesh,
        in_specs=placed,
        out_specs=(
            P("fsdp", "seq", None),
            P("fsdp", None, "seq"),
            P("fsdp", "seq", None),
            P(("seq", "fsdp"), None),
            P(("seq", "fsdp"), None),
            P(("seq", "fsdp"), None),
            P(("seq", "fsdp"), None),
            P(("seq", "fsdp")),
            P(("seq", "fsdp")),
            P("seq", None),
            P("seq", None, None),
            P("seq", None),
        ),
        check_vma=False,
    )
```
